32 devices in a mesh: clip: 8 (over z, x), band: 4 (over y, core).
Axes of the slice: x: 2, y: 2, z: 4, core: 2. Of those that a mesh axis runs over, the one named last changes fastest.
Arguments:
- latents: float32 [8, 5, 32, 16, 8], P('clip', None, 'band'), may hold values from -6 to 6
- noise_field: float32 [8, 5, 32, 16, 8], P('clip', None, 'band'), may hold values from -6 to 6
- timesteps: int32 [8], P('clip'), may hold values from 0 to 999
- null_flags: int32 [8], P('clip'), may hold values 0 or 1
- frame_mask: int32 [8, 5], P('clip'), may hold values from 0 to 1, as said below
- context: bfloat16 [8, 77, 4096], P('clip'), may hold values from -6 to 6
- w_wide: float32 [1024, 30720], P('clip')
- m_wide: float32 [1024, 30720], P('clip'), may hold values from -8.940697e-08 to 8.940697e-08
- v_wide: float32 [1024, 30720], P('clip'), may hold values from 1.0983557e-15 to 4.3519752e-15
- w_deep: float32 [4096, 4096], P('clip'), may hold values from -0.09375 to 0.09375
- m_deep: float32 [4096, 4096], P('clip'), may hold values from -8.940697e-08 to 8.940697e-08
- v_deep: float32 [4096, 4096], P('clip'), may hold values from 1.0983557e-15 to 4.3519752e-15
- w_small: float32 [19, 1024], replicated
- m_small: float32 [19, 1024], replicated, may hold values from -8.940697e-08 to 8.940697e-08
- v_small: float32 [19, 1024], replicated, may hold values from 1.0983557e-15 to 4.3519752e-15
Outputs:
- loss: float32 [], replicated
- grad_norm: float32 [], replicated
- new_w_wide: float32 [1024, 30720], P('clip')
- new_m_wide: float32 [1024, 30720], P('clip')
- new_v_wide: float32 [1024, 30720], P('clip')
- new_w_deep: float32 [4096, 4096], P('clip')
- new_m_deep: float32 [4096, 4096], P('clip')
- new_v_deep: float32 [4096, 4096], P('clip')
- new_w_small: float32 [19, 1024], replicated
- new_m_small: float32 [19, 1024], replicated
- new_v_small: float32 [19, 1024], replicated
The draws below stay inside these ranges and needn't reach their ends.
Inputs may be any that keep to these rules, and one draw needn't show every extreme that they name: `frame_mask`: every clip counts at least one frame.
All inputs are finite; a program needn't handle non-finite values. No bound on the sum of `null_flags` on one device may be relied on, other than what follows from the above.
Results may differ from the reference program's by a relative error of at most 0.0024.
The reference program's roundings to bfloat16 on the way count: a program that leaves them out, or rounds other values in their place, can miss the bound.
Values may be sent and summed in bfloat16 or wider, within the bound.
A program may use at most 640 MiB of HBM per device.

```python
import math
import jax
import jax.numpy as jnp
from jax import lax

D = 1024
HEADS = 16
HEAD_DIM = 64
FF = 4096
CH = 8
CTX_DIM = 4096
CTX_LEN = 77
FRAMES = 5
COLS = 16
SPACE = 16
WIN = 8
SHIFT = 4
TMAX = 1000
STEP = 10
HEIGHT = 32
CLIPS = 8
PARAMS = 48253952


def draw_w_wide(key, part):
    col_scale = jnp.concatenate([jnp.full((12 * D,), 3.0, jnp.float32), jnp.full((6 * D,), 1.0, jnp.float32), jnp.full((2 * D,), 4.0, jnp.float32), jnp.full((D,), 1.5, jnp.float32), jnp.full((D,), 4.0, jnp.float32), jnp.full((2 * FF,), 1.0, jnp.float32)]) * D ** (-0.5)
    base_draw = jax.random.normal(key, (D, 22 * D + 2 * FF), jnp.float32)
    return base_draw * col_scale[None, :]


def draw_w_small(key, part):
    row_scale = jnp.concatenate([jnp.full((CH,), CH ** (-0.5), jnp.float32), jnp.full((CH,), D ** (-0.5), jnp.float32), jnp.full((1,), 0.3, jnp.float32), jnp.full((2,), 0.1, jnp.float32)])
    row_offset = jnp.concatenate([jnp.zeros((2 * CH + 1,), jnp.float32), jnp.ones((2,), jnp.float32)])
    base_draw = jax.random.normal(key, (2 * CH + 3, D), jnp.float32)
    return base_draw * row_scale[:, None] + row_offset[:, None]


def draw_frame_mask(key, part):
    random_bits = jax.random.randint(key, (CLIPS, FRAMES), 0, 2)
    chosen = jax.random.randint(jax.random.fold_in(key, 7), (CLIPS, 1), 0, FRAMES)
    forced = (jnp.arange(FRAMES)[None, :] == chosen).astype(jnp.int32)
    return jnp.maximum(random_bits, forced).astype(jnp.int32)


def set_ends(drawn, rng, least, largest):
    index_at = [jax.random.randint(jax.random.fold_in(rng, axis), (), 0, length) for axis, length in enumerate(drawn.shape)]
    widest = drawn.shape.index(max(drawn.shape))
    neighbour = index_at[:widest] + [(index_at[widest] + 1) % drawn.shape[widest]] + index_at[widest + 1:]
    return drawn.at[tuple(index_at)].set(least).at[tuple(neighbour)].set(largest)


def block_scale(rng, shape, shards, least, top_value):
    loudness = 1.0
    for axis_at, shards_of in shards:
        draws = jax.random.uniform(jax.random.fold_in(jax.random.fold_in(rng, 6), axis_at), (shards_of,), jnp.float32, least / len(shards), top_value / len(shards))
        loudness = loudness * jnp.repeat(jnp.exp(draws), shape[axis_at] // shards_of).reshape((-1,) + (1,) * (len(shape) - 1 - axis_at))
    return loudness


def noise(stream_key, shape, scale, limit, cuts=(), kind=jnp.bfloat16):
    drawn = scale * jax.random.normal(stream_key, shape, jnp.float32)
    if cuts:
        drawn = drawn * block_scale(stream_key, shape, cuts, -0.22, 0.18)
    return jnp.clip(drawn, -limit, limit).astype(kind)


def setup_inputs(seed: int = 0) -> dict:
    keys = jax.random.split(jax.random.key(seed), 16)
    latents = noise(keys[0], (CLIPS, FRAMES, HEIGHT, COLS, CH), 1.0, 6.0, ((0, 8), (2, 4)), jnp.float32)
    noise_field = noise(keys[1], (CLIPS, FRAMES, HEIGHT, COLS, CH), 1.0, 6.0, ((0, 8), (2, 4)), jnp.float32)
    timesteps = set_ends(jax.random.randint(keys[2], (CLIPS,), 0, TMAX), jax.random.fold_in(keys[2], 1), 0, TMAX - 1).astype(jnp.int32)
    null_flags = set_ends((jax.random.randint(keys[3], (CLIPS,), 0, 4) < 1).astype(jnp.int32), jax.random.fold_in(keys[3], 1), 0, 1)
    frame_mask = draw_frame_mask(jax.random.fold_in(keys[15], 71), 0)
    context = noise(keys[5], (CLIPS, CTX_LEN, CTX_DIM), 1.0, 6.0, ((0, 8),))
    w_wide = draw_w_wide(jax.random.fold_in(keys[15], 71), 0)
    m_wide = noise(keys[7], (D, 22 * D + 2 * FF), (0.00011 / PARAMS ** 0.5), 8.940696716308594e-08, ((0, 8),), jnp.float32)
    v_wide = jnp.clip(jnp.exp(math.log(4.35197523837908e-15) - 1.3768156 * jax.random.uniform(keys[8], (D, 22 * D + 2 * FF), jnp.float32) ** block_scale(keys[8], (D, 22 * D + 2 * FF), ((0, 8),), -0.2, 0.2)), 1.0983556695176502e-15, 4.35197523837908e-15)
    w_deep = noise(keys[9], (FF, 4 * D), FF ** -0.5, 0.09375, ((0, 8),), jnp.float32)
    m_deep = noise(keys[10], (FF, 4 * D), (0.00011 / PARAMS ** 0.5), 8.940696716308594e-08, ((0, 8),), jnp.float32)
    v_deep = jnp.clip(jnp.exp(math.log(4.35197523837908e-15) - 1.3768156 * jax.random.uniform(keys[11], (FF, 4 * D), jnp.float32) ** block_scale(keys[11], (FF, 4 * D), ((0, 8),), -0.2, 0.2)), 1.0983556695176502e-15, 4.35197523837908e-15)
    w_small = draw_w_small(jax.random.fold_in(keys[15], 71), 0)
    m_small = noise(keys[13], (2 * CH + 3, D), (0.00011 / PARAMS ** 0.5), 8.940696716308594e-08, (), jnp.float32)
    v_small = jnp.clip(jnp.exp(jax.random.uniform(keys[14], (2 * CH + 3, D), jnp.float32, math.log(1.0983556695176502e-15), math.log(4.35197523837908e-15))), 1.0983556695176502e-15, 4.35197523837908e-15)
    return {"latents": latents, "noise_field": noise_field, "timesteps": timesteps, "null_flags": null_flags, "frame_mask": frame_mask, "context": context, "w_wide": w_wide, "m_wide": m_wide, "v_wide": v_wide, "w_deep": w_deep, "m_deep": m_deep, "v_deep": v_deep, "w_small": w_small, "m_small": m_small, "v_small": v_small}


@jax.custom_vjp
def low(v):
    return lax.optimization_barrier(v.astype(jnp.bfloat16)).astype(jnp.float32)

@jax.custom_vjp
def low_back(v):
    return v

def low_keep(v):
    return (low(v), None)

def low_pass(kept, grad):
    return (grad,)

def back_keep(v):
    return (v, None)

def back_low(kept, grad):
    return (low(grad),)
low.defvjp(low_keep, low_pass)
low_back.defvjp(back_keep, back_low)
HIGH = lax.Precision.HIGHEST
EPS_NORM = 1e-06
CLIP_MAX = 0.001
BETA_ONE = 0.9
BETA_TWO = 0.95
ADAM_EPS = 1e-08
DECAY = 0.1
RATES = (0.15, 0.05, 0.5)

def matmul(left_op, right_op):
    return jnp.dot(left_op, right_op, precision=HIGH, preferred_element_type=jnp.float32)

def layer_norm(field_in):
    average = lax.optimization_barrier(jnp.mean(field_in, -1, keepdims=True))
    centred = field_in - average
    return centred * lax.rsqrt(lax.optimization_barrier(jnp.mean(centred * centred, -1, keepdims=True)) + EPS_NORM)

def time_features(time_value):
    half_width = D // 2
    frequency = jnp.exp(-math.log(10000.0) * jnp.arange(half_width, dtype=jnp.float32) / half_width)
    angles = time_value[..., None] * frequency
    return jnp.concatenate([jnp.cos(angles), jnp.sin(angles)], -1)

def to_windows(token_grid, shape_win):
    num_frames, num_rows, num_cols, feat_dim = token_grid.shape
    win_frames, win_rows, win_cols = shape_win
    shaped = token_grid.reshape(num_frames // win_frames, win_frames, num_rows // win_rows, win_rows, num_cols // win_cols, win_cols, feat_dim)
    return shaped.transpose(0, 2, 4, 1, 3, 5, 6).reshape(-1, win_frames * win_rows * win_cols, feat_dim)

def from_windows(blocks, grid_shape, shape_win):
    num_frames, num_rows, num_cols = grid_shape
    win_frames, win_rows, win_cols = shape_win
    feat_dim = blocks.shape[-1]
    shaped = blocks.reshape(num_frames // win_frames, num_rows // win_rows, num_cols // win_cols, win_frames, win_rows, win_cols, feat_dim)
    return shaped.transpose(0, 3, 1, 4, 2, 5, 6).reshape(num_frames, num_rows, num_cols, feat_dim)

def heads_of(field_in):
    return field_in.reshape(field_in.shape[:-1] + (HEADS, HEAD_DIM))

def window_attention(qkv_blocks):
    queries = heads_of(qkv_blocks[..., :D])
    key_heads = heads_of(qkv_blocks[..., D:2 * D])
    value_heads = heads_of(qkv_blocks[..., 2 * D:])
    scores = low_back(jnp.einsum('wqhd,wkhd->whqk', queries, key_heads, precision=HIGH) * HEAD_DIM ** (-0.5))
    probabilities = jax.nn.softmax(scores, -1)
    attended = jnp.einsum('whqk,wkhd->wqhd', low(probabilities), value_heads, precision=HIGH)
    return attended.reshape(qkv_blocks.shape[0], qkv_blocks.shape[1], D)

def cross_attention(query_proj, keyval):
    queries = heads_of(query_proj)
    key_heads = heads_of(keyval[:, :D])
    value_heads = heads_of(keyval[:, D:])
    scores = low_back(jnp.einsum('qhd,khd->hqk', queries, key_heads, precision=HIGH) * HEAD_DIM ** (-0.5))
    probabilities = jax.nn.softmax(scores, -1)
    attended = jnp.einsum('hqk,khd->qhd', low(probabilities), value_heads, precision=HIGH)
    return attended.reshape(query_proj.shape[0], D)

def window_branch(stream, modul, qkv_weight, out_weight, shape_win, shift_rows):
    normed = low(layer_norm(stream) * (1.0 + modul[1]) + modul[0])
    token_grid = jnp.roll(normed.reshape(FRAMES, HEIGHT, COLS, D), -shift_rows, axis=1)
    qkv_val = low(low_back(matmul(token_grid.reshape(-1, D), qkv_weight)))
    blocks = window_attention(to_windows(qkv_val.reshape(FRAMES, HEIGHT, COLS, 3 * D), shape_win))
    attended = jnp.roll(from_windows(blocks, (FRAMES, HEIGHT, COLS), shape_win), shift_rows, axis=1).reshape(-1, D)
    attended = low(low_back(attended))
    return stream + modul[2] * low_back(matmul(attended, out_weight))

def mlp_branch(stream, modul, up_weight, down_weight):
    mlp_in = low(layer_norm(stream) * (1.0 + modul[4]) + modul[3])
    up_proj = low_back(matmul(mlp_in, up_weight))
    gelu_low = low(jax.nn.gelu(up_proj, approximate=False))
    return stream + modul[5] * low_back(matmul(gelu_low, down_weight))

def clip_loss(weight_packs, clip_in):
    wide_pack, deep_pack, small_pack = weight_packs
    latent, noise_clip, time_step, null_flag, mask_row, context_clip = clip_in
    time_value = time_step.astype(jnp.float32)
    noise_angle = 0.5 * math.pi * time_value / TMAX
    signal, spread = (jnp.cos(noise_angle), jnp.sin(noise_angle))
    noisy_tok = signal * latent + spread * noise_clip
    target = (signal * noise_clip - spread * latent).reshape(-1, CH)
    time_low = low(jax.nn.silu(time_features(time_value)))[None]
    modulation = matmul(time_low, wide_pack[:, :12 * D]).reshape(12, D)
    mod_a, mod_b = (modulation[:6], modulation[6:])
    stream = matmul(low(noisy_tok).reshape(-1, CH), small_pack[:CH]) + small_pack[2 * CH]
    stream = window_branch(stream, mod_a, wide_pack[:, 12 * D:15 * D], wide_pack[:, 18 * D:19 * D], (1, SPACE, SPACE), 0)
    stream = mlp_branch(stream, mod_a, wide_pack[:, 22 * D:22 * D + FF], deep_pack[:, :D])
    stream = window_branch(stream, mod_b, wide_pack[:, 15 * D:18 * D], wide_pack[:, 19 * D:20 * D], (FRAMES, WIN, WIN), SHIFT)
    cross_in = low(layer_norm(stream) * small_pack[2 * CH + 1])
    query_proj = low(low_back(matmul(cross_in, wide_pack[:, 20 * D:21 * D])))
    kept_text = context_clip * (1 - null_flag).astype(jnp.float32)
    keyval = low(matmul(kept_text, deep_pack[:, D:3 * D]))
    crossed = low(low_back(cross_attention(query_proj, keyval)))
    stream = stream + low_back(matmul(crossed, wide_pack[:, 21 * D:22 * D]))
    stream = mlp_branch(stream, mod_b, wide_pack[:, 22 * D + FF:], deep_pack[:, 3 * D:])
    final_in = low(layer_norm(stream) * small_pack[2 * CH + 2])
    predicted = low_back(matmul(final_in, small_pack[CH:2 * CH].T))
    weight_row = jnp.repeat(mask_row.astype(jnp.float32), HEIGHT * COLS)[:, None]
    pred_error = predicted - target
    return jnp.sum(weight_row * pred_error * pred_error)

def adam_update(weight, first_mom, second_mom, grad_val, learn_rate):
    first_mom = BETA_ONE * first_mom + (1.0 - BETA_ONE) * grad_val
    second_mom = BETA_TWO * second_mom + (1.0 - BETA_TWO) * grad_val * grad_val
    first_hat = first_mom / (1.0 - BETA_ONE ** STEP)
    second_hat = second_mom / (1.0 - BETA_TWO ** STEP)
    weight = weight - learn_rate * (first_hat / (jnp.sqrt(second_hat) + ADAM_EPS) + DECAY * weight)
    return (weight, first_mom, second_mom)

def reference(latents, noise_field, timesteps, null_flags, frame_mask, context, w_wide, m_wide, v_wide, w_deep, m_deep, v_deep, w_small, m_small, v_small):
    global_count = jnp.sum(frame_mask).astype(jnp.float32) * (HEIGHT * COLS * CH)
    inputs = (latents, noise_field, timesteps, null_flags, frame_mask, context.astype(jnp.float32))

    def total_loss(wide_pack, deep_pack, small_pack):
        weight_packs = (low(wide_pack), low(deep_pack), low(small_pack))

        def step_fn(running, clip_in):
            return (running + jax.checkpoint(clip_loss)(weight_packs, clip_in), None)
        summed, unused = lax.scan(step_fn, jnp.zeros((), jnp.float32), inputs)
        return summed / global_count
    loss, pullback = jax.vjp(total_loss, w_wide, w_deep, w_small)
    gradients = pullback(jnp.ones((), jnp.float32))
    grad_norm = jnp.sqrt(sum((jnp.sum(grad_val * grad_val) for grad_val in gradients)))
    factor = CLIP_MAX / jnp.maximum(grad_norm, CLIP_MAX)
    results = [loss, grad_norm]
    states = ((w_wide, m_wide, v_wide), (w_deep, m_deep, v_deep), (w_small, m_small, v_small))
    for state, grad_val, learn_rate in zip(states, gradients, RATES):
        results.extend(adam_update(state[0], state[1], state[2], grad_val * factor, learn_rate))
    return (results[0], results[1], results[2], results[3], results[4], results[5], results[6], results[7], results[8], results[9], results[10])
```

```python
from functools import partial
import math

import jax
import jax.numpy as jnp
from jax import lax
from jax.experimental import pallas as pl
from jax.experimental.pallas import tpu as pltpu
from jax.sharding import PartitionSpec as P

D = 1024
HEADS = 16
HEAD_DIM = 64
FF = 4096
CH = 8
SPACE = 16
WIN = 8
SHIFT = 4
TMAX = 1000
STEP = 10


EPS_NORM = 1e-06
CLIP_MAX = 0.001
BETA_ONE = 0.9
BETA_TWO = 0.95
ADAM_EPS = 1e-08
DECAY = 0.1
SELF_FORMS = ("wqhd,wkhd->whqk", "whqk,wkhd->wqhd", "whqk,wqhd->wkhd", "whqk,wkhd->wqhd")
CROSS_FORMS = ("qhd,khd->hqk", "hqk,khd->qhd", "hqk,qhd->khd", "hqk,khd->qhd")


def from_partner(block, axis, distance):
    count = lax.axis_size(axis)
    route = []
    for low in range(count):
        high = low | 1 << distance
        if high != low and high < count:
            route += [(low, high), (high, low)]
    return lax.ppermute(block, axis, route)


def shifted(value, axis, by):
    length = lax.axis_size(axis)
    return lax.ppermute(value, axis, [(i, (i + by) % length) for i in range(length)])


def matmul(left_op, right_op):
    return jnp.dot(left_op, right_op, preferred_element_type=jnp.float32)


def matmul_tn(left_op, right_op, precision=None):
    return lax.dot_general(
        left_op,
        right_op,
        (((0,), (0,)), ((), ())),
        precision=precision,
        preferred_element_type=jnp.float32,
    )


def matmul_nt(left_op, right_op):
    return lax.dot_general(
        left_op, right_op, (((1,), (1,)), ((), ())), preferred_element_type=jnp.float32
    )


def layer_norm(field_in):
    average = jnp.mean(field_in, -1, keepdims=True)
    centred = field_in - average
    return centred * lax.rsqrt(jnp.mean(centred * centred, -1, keepdims=True) + EPS_NORM)


def norm_modulated(field_in, shift_vec, scale_vec):
    return layer_norm(field_in) * (1.0 + scale_vec) + shift_vec


def norm_gained(field_in, gain_vec):
    return layer_norm(field_in) * gain_vec


def time_features(time_value):
    half_width = D // 2
    frequency = jnp.exp(-math.log(10000.0) * jnp.arange(half_width, dtype=jnp.float32) / half_width)
    angles = time_value[..., None] * frequency
    return jnp.concatenate([jnp.cos(angles), jnp.sin(angles)], -1)


def to_windows(token_grid, shape_win):
    num_frames, num_rows, num_cols, feat_dim = token_grid.shape
    win_frames, win_rows, win_cols = shape_win
    shaped = token_grid.reshape(
        num_frames // win_frames,
        win_frames,
        num_rows // win_rows,
        win_rows,
        num_cols // win_cols,
        win_cols,
        feat_dim,
    )
    return shaped.transpose(0, 2, 4, 1, 3, 5, 6).reshape(
        -1, win_frames * win_rows * win_cols, feat_dim
    )


def from_windows(blocks, grid_shape, shape_win):
    num_frames, num_rows, num_cols = grid_shape
    win_frames, win_rows, win_cols = shape_win
    feat_dim = blocks.shape[-1]
    shaped = blocks.reshape(
        num_frames // win_frames,
        num_rows // win_rows,
        num_cols // win_cols,
        win_frames,
        win_rows,
        win_cols,
        feat_dim,
    )
    return shaped.transpose(0, 3, 1, 4, 2, 5, 6).reshape(num_frames, num_rows, num_cols, feat_dim)


def split_heads(field_in):
    return field_in.reshape(field_in.shape[:-1] + (HEADS, HEAD_DIM))


def merge_heads(field_in):
    return field_in.reshape(field_in.shape[:-2] + (D,))


def attend_forward(queries, key_heads, value_heads, einsum_forms):
    scores = jnp.einsum(
        einsum_forms[0], queries, key_heads, preferred_element_type=jnp.float32
    ) * HEAD_DIM ** (-0.5)
    log_total = jax.nn.logsumexp(scores, axis=-1, keepdims=True)
    probabilities = jnp.exp(scores - log_total)
    attended = jnp.einsum(
        einsum_forms[1],
        probabilities.astype(jnp.bfloat16),
        value_heads,
        preferred_element_type=jnp.float32,
    )
    return (attended, log_total)


def attend_backward(queries, key_heads, value_heads, log_total, grad_out, einsum_forms):
    scores = jnp.einsum(
        einsum_forms[0], queries, key_heads, preferred_element_type=jnp.float32
    ) * HEAD_DIM ** (-0.5)
    probabilities = jnp.exp(scores - log_total)
    grad_values = jnp.einsum(
        einsum_forms[2],
        probabilities.astype(jnp.bfloat16),
        grad_out,
        preferred_element_type=jnp.float32,
    )
    grad_probs = jnp.einsum(
        einsum_forms[0], grad_out, value_heads, preferred_element_type=jnp.float32
    )
    inner_sum = jnp.sum(probabilities * grad_probs, -1, keepdims=True)
    grad_scores = (probabilities * (grad_probs - inner_sum)).astype(jnp.bfloat16)
    grad_queries = jnp.einsum(
        einsum_forms[3], grad_scores, key_heads, preferred_element_type=jnp.float32
    ) * HEAD_DIM ** (-0.5)
    grad_keys = jnp.einsum(
        einsum_forms[2], grad_scores, queries, preferred_element_type=jnp.float32
    ) * HEAD_DIM ** (-0.5)
    return (grad_queries, grad_keys, grad_values)


def mlp_forward(stream, modul, up_weight, down_weight):
    mlp_val, norm_back = jax.vjp(norm_modulated, stream, modul[3], modul[4])
    mlp_in = mlp_val.astype(jnp.bfloat16)
    up_proj = matmul(mlp_in, up_weight)
    gelu_val, gelu_back = jax.vjp(partial(jax.nn.gelu, approximate=False), up_proj)
    gelu_low = gelu_val.astype(jnp.bfloat16)
    down_proj = matmul(gelu_low, down_weight)
    return (stream + modul[5] * down_proj, (norm_back, mlp_in, gelu_back, gelu_low, down_proj))


def mlp_backward(grad_stream, modul, up_weight, down_weight, saved):
    norm_back, mlp_in, gelu_back, gelu_low, down_proj = saved
    grad_down = (modul[5] * grad_stream).astype(jnp.bfloat16)
    grad_gate = jnp.sum(grad_stream * down_proj, 0)
    grad_w_down = matmul_tn(gelu_low, grad_down)
    grad_up = gelu_back(matmul_nt(grad_down, down_weight))[0].astype(jnp.bfloat16)
    grad_w_up = matmul_tn(mlp_in, grad_up)
    grad_part, grad_shift, grad_scale = norm_back(matmul_nt(grad_up, up_weight))
    return (grad_stream + grad_part, grad_w_up, grad_w_down, (grad_shift, grad_scale, grad_gate))


def adam_update(weight, first_mom, second_mom, grad_val, learn_rate):
    first_mom = BETA_ONE * first_mom + (1.0 - BETA_ONE) * grad_val
    second_mom = BETA_TWO * second_mom + (1.0 - BETA_TWO) * grad_val * grad_val
    first_hat = first_mom / (1.0 - BETA_ONE**STEP)
    second_hat = second_mom / (1.0 - BETA_TWO**STEP)
    weight = weight - learn_rate * (first_hat / (jnp.sqrt(second_hat) + ADAM_EPS) + DECAY * weight)
    return (weight, first_mom, second_mom)

MESH = pl.DeviceIdType.MESH
ANY = pl.BlockSpec(memory_space=pl.ANY)
TEXT_PAD = 80


def ring_place(clip, count):
    half = clip // 2
    odd = clip % 2
    return half + odd * (count - 1 - 2 * half)


def ring_clip(place, count):
    far = place // (count // 2)
    return (1 - far) * 2 * place + far * (2 * (count - 1 - place) + 1)


def greet(peers):
    barrier = pltpu.get_barrier_semaphore()
    for peer in peers:
        pl.semaphore_signal(barrier, inc=1, device_id=peer, device_id_type=MESH)
    pl.semaphore_wait(barrier, len(peers))


def exchange_kernel(count, facts_ref, text_ref, facts_out, text_out, send, recv, local):
    me = lax.axis_index("clip")
    band = lax.axis_index("band")
    peers = [((me + step) % count, band) for step in range(1, count)]
    greet(peers)
    own = [
        pltpu.make_async_copy(facts_ref, facts_out.at[me], local.at[0]),
        pltpu.make_async_copy(text_ref.at[me], text_out.at[me], local.at[1]),
    ]
    for copy in own:
        copy.start()
    sent = []
    for step, peer in enumerate(peers):
        sent += [
            pltpu.make_async_remote_copy(
                facts_ref, facts_out.at[me], send.at[0, step], recv.at[0, step], peer, MESH
            ),
            pltpu.make_async_remote_copy(
                text_ref.at[peer[0]], text_out.at[me], send.at[1, step], recv.at[1, step], peer, MESH
            ),
        ]
    for copy in sent:
        copy.start()
    for copy in own + sent:
        copy.wait()


def exchange_facts(facts, text):
    count = lax.axis_size("clip")
    return pl.pallas_call(
        partial(exchange_kernel, count),
        out_shape=(
            jax.ShapeDtypeStruct((count,) + facts.shape, facts.dtype),
            jax.ShapeDtypeStruct(text.shape, text.dtype),
        ),
        in_specs=[ANY] * 2,
        out_specs=(ANY,) * 2,
        scratch_shapes=[
            pltpu.SemaphoreType.DMA((2, count - 1)),
            pltpu.SemaphoreType.DMA((2, count - 1)),
            pltpu.SemaphoreType.DMA((2,)),
        ],
        compiler_params=pltpu.CompilerParams(collective_id=0, has_side_effects=True),
    )(facts, text)


def gather_kernel(count, shapes, *refs):
    num = len(shapes)
    shards, (vec_ref, text_ref) = refs[:num], refs[num : num + 2]
    full, (vec_out, text_out) = refs[num + 2 : 2 * num + 2], refs[2 * num + 2 : 2 * num + 4]
    ring_send, ring_recv, pair_send, pair_recv, own_sem, part_send, part_recv, part_own = refs[
        2 * num + 4 :
    ]
    me = lax.axis_index("clip")
    band = lax.axis_index("band")
    core = band % 2
    place = ring_place(me, count)
    onward = 1 - 2 * core
    following = (ring_clip((place + onward + count) % count, count), band)
    partner = (me, band + 1 - 2 * core)
    peers = [((me + step) % count, band) for step in range(1, count)]
    greet(peers + [partner])

    def block(ref, group, owner):
        rows, cols = shapes[group]
        return ref.at[
            pl.ds(pl.multiple_of(owner * rows, rows), rows),
            pl.ds(pl.multiple_of(core * (cols // 2), 128), cols // 2),
        ]

    def ring_copy(group, step):
        owner = ring_clip((place - onward * step + 2 * count) % count, count)
        there = block(full[group], group, owner)
        return pltpu.make_async_remote_copy(
            there, there, ring_send.at[step, group], ring_recv.at[step, group], following, MESH
        )

    def pair_copy(group, step):
        owner = ring_clip((place - onward * (step + 1) + 2 * count) % count, count)
        there = block(full[group], group, owner)
        return pltpu.make_async_remote_copy(
            there, there, pair_send.at[step, group], pair_recv.at[step, group], partner, MESH
        )

    def own_copy(group):
        rows, cols = shapes[group]
        return pltpu.make_async_copy(
            shards[group],
            full[group].at[pl.ds(pl.multiple_of(me * rows, rows), rows), :],
            own_sem.at[group],
        )

    parts = []
    for step, peer in enumerate(peers):
        for which, (src, dst) in enumerate(((vec_ref, vec_out), (text_ref, text_out))):
            parts.append(
                pltpu.make_async_remote_copy(
                    src.at[peer[0]],
                    dst.at[me],
                    part_send.at[which, step],
                    part_recv.at[which, step],
                    peer,
                    MESH,
                )
            )
    parts_own = [
        pltpu.make_async_copy(src.at[me], dst.at[me], part_own.at[which])
        for which, (src, dst) in enumerate(((vec_ref, vec_out), (text_ref, text_out)))
    ]
    for group in range(num):
        rows, cols = shapes[group]
        own_copy(group).start()
        pltpu.make_async_remote_copy(
            shards[group].at[:, pl.ds(pl.multiple_of(core * (cols // 2), 128), cols // 2)],
            block(full[group], group, me),
            ring_send.at[0, group],
            ring_recv.at[0, group],
            following,
            MESH,
        ).start()
    for copy in parts_own + parts:
        copy.start()

    @pl.loop(1, count - 1)
    def _(step):
        for group in range(num):
            ring_copy(group, step - 1).wait_recv()
            ring_copy(group, step).start()
            pair_copy(group, step - 1).start()

    for group in range(num):
        ring_copy(group, count - 2).wait_recv()
        pair_copy(group, count - 2).start()
    for copy in parts_own + parts:
        copy.wait()
    for group in range(num):
        own_copy(group).wait()

    @pl.loop(0, count - 1)
    def _(step):
        for group in range(num):
            ring_copy(group, step).wait_send()
            pair_copy(group, step).wait()


def gather_weights(shards, vectors, texts):
    count = lax.axis_size("clip")
    num = len(shards)
    steps = pltpu.SemaphoreType.DMA((count - 1, num))
    out = pl.pallas_call(
        partial(gather_kernel, count, [shard.shape for shard in shards]),
        out_shape=tuple(
            jax.ShapeDtypeStruct((count * s.shape[0], s.shape[1]), s.dtype) for s in shards
        )
        + tuple(jax.ShapeDtypeStruct(v.shape, v.dtype) for v in (vectors, texts)),
        in_specs=[ANY] * (num + 2),
        out_specs=(ANY,) * (num + 2),
        scratch_shapes=[
            steps,
            steps,
            steps,
            steps,
            pltpu.SemaphoreType.DMA((num,)),
            pltpu.SemaphoreType.DMA((2, count - 1)),
            pltpu.SemaphoreType.DMA((2, count - 1)),
            pltpu.SemaphoreType.DMA((2,)),
        ],
        compiler_params=pltpu.CompilerParams(collective_id=1, has_side_effects=True),
    )(*shards, vectors, texts)
    return out[:num], out[num], out[num + 1]


def per_device(
    latents,
    noise_field,
    timesteps,
    null_flags,
    frame_mask,
    context,
    w_wide,
    m_wide,
    v_wide,
    w_deep,
    m_deep,
    v_deep,
    w_small,
    m_small,
    v_small,
):
    clip_count = lax.axis_size("clip")
    band_count = lax.axis_size("band")
    clip_at = lax.axis_index("clip")
    band_at = lax.axis_index("band")
    wide_rows = w_wide.shape[0]
    deep_rows = w_deep.shape[0]
    text_len, text_dim = context.shape[1:]
    facts = jnp.pad(
        jnp.concatenate([timesteps, frame_mask[0]])[None],
        ((0, 7), (0, 127 - frame_mask.shape[1])),
    )
    kept_text = context[0] * (1 - null_flags[0]).astype(jnp.bfloat16)
    text_cols = jnp.pad(
        kept_text.reshape(text_len, clip_count, deep_rows).transpose(1, 0, 2),
        ((0, 0), (0, TEXT_PAD - text_len), (0, 0)),
    )
    all_facts, all_text = exchange_facts(facts, text_cols)
    all_times = all_facts[:, 0, 0].astype(jnp.float32)
    all_time_low = jax.nn.silu(time_features(all_times)).astype(jnp.bfloat16)
    time_rows = lax.dynamic_slice(
        all_time_low, (0, clip_at * wide_rows), (clip_count, wide_rows)
    )
    part_modul = matmul(time_rows, w_wide[:, : 12 * D].astype(jnp.bfloat16))
    kv_cols = 2 * D // band_count
    kv_weight = lax.dynamic_slice(
        w_deep, (0, D + band_at * kv_cols), (deep_rows, kv_cols)
    ).astype(jnp.bfloat16)
    part_kv = matmul(all_text.reshape(clip_count * TEXT_PAD, deep_rows), kv_weight)
    edges = (12 * D, 15 * D, 18 * D, 19 * D, 20 * D, 21 * D, 22 * D, 22 * D + FF, 22 * D + 2 * FF)
    shards = [w_wide[:, low:high].astype(jnp.bfloat16) for low, high in zip(edges, edges[1:])]
    shards += [w_deep[:, :D].astype(jnp.bfloat16), w_deep[:, 3 * D :].astype(jnp.bfloat16)]
    gathered, all_modul, all_kv = gather_weights(
        shards,
        part_modul.reshape(clip_count, 12 * D // 128, 128),
        part_kv.reshape(clip_count, TEXT_PAD, kv_cols),
    )
    (
        qkv_a_w,
        qkv_b_w,
        out_a_w,
        out_b_w,
        query_w,
        cross_out_w,
        up_a_w,
        up_b_w,
        down_a_w,
        down_b_w,
    ) = gathered
    keyval = lax.all_gather(jnp.sum(all_kv, 0).astype(jnp.bfloat16), "band", axis=1, tiled=True)
    keyval = keyval[:text_len]
    small_low = w_small.astype(jnp.bfloat16)
    small_val = small_low.astype(jnp.float32)
    num_frames, num_rows, num_cols = (latents.shape[1], latents.shape[2], latents.shape[3])
    grid_shape = (num_frames, num_rows, num_cols)
    tok_count = num_frames * num_rows * num_cols
    all_mask = all_facts[:, 0, 1 : 1 + num_frames]
    global_count = jnp.sum(all_mask).astype(jnp.float32) * (num_rows * num_cols * CH * band_count)
    time_value = timesteps[0].astype(jnp.float32)
    noise_angle = 0.5 * math.pi * time_value / TMAX
    signal, spread = (jnp.cos(noise_angle), jnp.sin(noise_angle))
    clean_tok = latents[0].reshape(tok_count, CH)
    noise_tok = noise_field[0].reshape(tok_count, CH)
    noisy_low = (signal * clean_tok + spread * noise_tok).astype(jnp.bfloat16)
    target = signal * noise_tok - spread * clean_tok
    modulation = jnp.sum(all_modul, 0).reshape(12, D)
    mod_a, mod_b = (modulation[:6], modulation[6:])
    stream_zero = matmul(noisy_low, small_low[:CH]) + small_val[2 * CH]
    normed_a, back_a = jax.vjp(norm_modulated, stream_zero, mod_a[0], mod_a[1])
    in_a = normed_a.astype(jnp.bfloat16)
    spatial = (1, num_rows, SPACE)
    qkv_a = (
        matmul(in_a, qkv_a_w).astype(jnp.bfloat16).reshape(num_frames, num_rows, num_cols, 3 * D)
    )
    blocks_a = to_windows(qkv_a, spatial)
    partner = from_partner(blocks_a[..., D:], "band", 0)
    keys_all = jnp.concatenate([blocks_a[..., D:], partner], 1)
    space_q = split_heads(blocks_a[..., :D])
    space_k = split_heads(keys_all[..., :D])
    space_v = split_heads(keys_all[..., D:])
    space_out, space_total = attend_forward(space_q, space_k, space_v, SELF_FORMS)
    att_a = from_windows(merge_heads(space_out.astype(jnp.bfloat16)), grid_shape, spatial).reshape(
        tok_count, D
    )
    proj_a = matmul(att_a, out_a_w)
    stream_one = stream_zero + mod_a[2] * proj_a
    stream_two, saved_a = mlp_forward(stream_one, mod_a, up_a_w, down_a_w)
    normed_b, back_b = jax.vjp(norm_modulated, stream_two, mod_b[0], mod_b[1])
    token_grid = normed_b.astype(jnp.bfloat16).reshape(num_frames, num_rows, num_cols, D)
    arrived = shifted(token_grid[:, :SHIFT], "band", -1)
    rolled = jnp.concatenate([token_grid[:, SHIFT:], arrived], 1).reshape(tok_count, D)
    temporal = (num_frames, WIN, WIN)
    qkv_b = matmul(rolled, qkv_b_w).astype(jnp.bfloat16)
    blocks_b = to_windows(qkv_b.reshape(num_frames, num_rows, num_cols, 3 * D), temporal)
    win_q = split_heads(blocks_b[..., :D])
    win_k = split_heads(blocks_b[..., D : 2 * D])
    win_v = split_heads(blocks_b[..., 2 * D :])
    win_out, win_total = attend_forward(win_q, win_k, win_v, SELF_FORMS)
    out_grid = from_windows(merge_heads(win_out.astype(jnp.bfloat16)), grid_shape, temporal)
    returned = shifted(out_grid[:, num_rows - SHIFT :], "band", 1)
    att_b = jnp.concatenate([returned, out_grid[:, : num_rows - SHIFT]], 1).reshape(tok_count, D)
    proj_b = matmul(att_b, out_b_w)
    stream_three = stream_two + mod_b[2] * proj_b
    cross_val, cross_back = jax.vjp(norm_gained, stream_three, small_val[2 * CH + 1])
    cross_in = cross_val.astype(jnp.bfloat16)
    query_proj = matmul(cross_in, query_w).astype(jnp.bfloat16)
    cross_q = split_heads(query_proj)
    cross_k = split_heads(keyval[:, :D])
    cross_v = split_heads(keyval[:, D:])
    cross_out, cross_total = attend_forward(cross_q, cross_k, cross_v, CROSS_FORMS)
    crossed = merge_heads(cross_out.astype(jnp.bfloat16))
    stream_four = stream_three + matmul(crossed, cross_out_w)
    stream_five, saved_b = mlp_forward(stream_four, mod_b, up_b_w, down_b_w)
    final_val, final_back = jax.vjp(norm_gained, stream_five, small_val[2 * CH + 2])
    final_low = final_val.astype(jnp.bfloat16)
    head_low = small_low[CH : 2 * CH]
    predicted = matmul_nt(final_low, head_low)
    weight_row = jnp.repeat(frame_mask[0].astype(jnp.float32), num_rows * num_cols)[:, None]
    pred_error = predicted - target
    loss_part = jnp.sum(weight_row * pred_error * pred_error)
    grad_pred = (weight_row * pred_error * (2.0 / global_count)).astype(jnp.bfloat16)
    grad_head = matmul_tn(grad_pred, final_low)
    grad_stream, grad_gain_f = final_back(matmul(grad_pred, head_low))
    grad_stream, grad_up_b, grad_down_b, extra_b = mlp_backward(
        grad_stream, mod_b, up_b_w, down_b_w, saved_b
    )
    grad_cross = grad_stream.astype(jnp.bfloat16)
    grad_w_co = matmul_tn(crossed, grad_cross)
    grad_crossed = split_heads(matmul_nt(grad_cross, cross_out_w).astype(jnp.bfloat16))
    cq_grad, ck_grad, cv_grad = attend_backward(
        cross_q, cross_k, cross_v, cross_total, grad_crossed, CROSS_FORMS
    )
    grad_query = merge_heads(cq_grad).astype(jnp.bfloat16)
    grad_w_cq = matmul_tn(cross_in, grad_query)
    grad_part, grad_gain_c = cross_back(matmul_nt(grad_query, query_w))
    grad_keyval = jnp.concatenate([merge_heads(ck_grad), merge_heads(cv_grad)], 1)
    grad_keyval = jnp.pad(grad_keyval, ((0, TEXT_PAD - text_len), (0, 0)))
    grad_keyval = lax.psum_scatter(grad_keyval, "band", scatter_dimension=1, tiled=True)
    grad_keyval = lax.all_gather(grad_keyval, "clip", axis=0, tiled=True)
    grad_w_ckv = matmul_tn(
        all_text.reshape(clip_count * TEXT_PAD, deep_rows).astype(jnp.float32),
        grad_keyval,
        lax.Precision.HIGHEST,
    )
    grad_w_ckv = lax.all_gather(grad_w_ckv, "band", axis=1, tiled=True)
    grad_stream = grad_stream + grad_part
    grad_proj = (mod_b[2] * grad_stream).astype(jnp.bfloat16)
    grad_gate_b = jnp.sum(grad_stream * proj_b, 0)
    grad_w_ob = matmul_tn(att_b, grad_proj)
    grad_att = (
        matmul_nt(grad_proj, out_b_w)
        .astype(jnp.bfloat16)
        .reshape(num_frames, num_rows, num_cols, D)
    )
    fetched = shifted(grad_att[:, :SHIFT], "band", -1)
    grad_rolled = jnp.concatenate([grad_att[:, SHIFT:], fetched], 1)
    grad_win = split_heads(to_windows(grad_rolled, temporal))
    wq_grad, wk_grad, wv_grad = attend_backward(
        win_q, win_k, win_v, win_total, grad_win, SELF_FORMS
    )
    grad_blocks = jnp.concatenate(
        [merge_heads(wq_grad), merge_heads(wk_grad), merge_heads(wv_grad)], -1
    )
    grad_qkv = (
        from_windows(grad_blocks, grid_shape, temporal)
        .reshape(tok_count, 3 * D)
        .astype(jnp.bfloat16)
    )
    grad_w_qkvb = matmul_tn(rolled, grad_qkv)
    grad_in_roll = matmul_nt(grad_qkv, qkv_b_w).reshape(num_frames, num_rows, num_cols, D)
    sent_back = shifted(grad_in_roll[:, num_rows - SHIFT :], "band", 1)
    grad_normed = jnp.concatenate([sent_back, grad_in_roll[:, : num_rows - SHIFT]], 1).reshape(
        tok_count, D
    )
    grad_part, grad_shift_b, grad_scale_b = back_b(grad_normed)
    grad_stream = grad_stream + grad_part
    grad_stream, grad_up_a, grad_down_a, extra_a = mlp_backward(
        grad_stream, mod_a, up_a_w, down_a_w, saved_a
    )
    grad_proj = (mod_a[2] * grad_stream).astype(jnp.bfloat16)
    grad_gate_a = jnp.sum(grad_stream * proj_a, 0)
    grad_w_oa = matmul_tn(att_a, grad_proj)
    grad_att = (
        matmul_nt(grad_proj, out_a_w)
        .astype(jnp.bfloat16)
        .reshape(num_frames, num_rows, num_cols, D)
    )
    grad_space = split_heads(to_windows(grad_att, spatial))
    sq_grad, sk_grad, sv_grad = attend_backward(
        space_q, space_k, space_v, space_total, grad_space, SELF_FORMS
    )
    half_len = space_q.shape[1]
    key_grads = merge_heads(sk_grad)
    value_grads = merge_heads(sv_grad)
    back_keys, back_values = from_partner(
        (key_grads[:, half_len:], value_grads[:, half_len:]), "band", 0
    )
    grad_blocks = jnp.concatenate(
        [
            merge_heads(sq_grad),
            key_grads[:, :half_len] + back_keys,
            value_grads[:, :half_len] + back_values,
        ],
        -1,
    )
    grad_qkv = (
        from_windows(grad_blocks, grid_shape, spatial)
        .reshape(tok_count, 3 * D)
        .astype(jnp.bfloat16)
    )
    grad_w_qkva = matmul_tn(in_a, grad_qkv)
    grad_part, grad_shift_a, grad_scale_a = back_a(matmul_nt(grad_qkv, qkv_a_w))
    grad_stream = grad_stream + grad_part
    grad_patch = matmul_tn(noisy_low.astype(jnp.float32), grad_stream, lax.Precision.HIGHEST)
    grad_bias = jnp.sum(grad_stream, 0)
    grad_modul = jnp.stack(
        [
            grad_shift_a,
            grad_scale_a,
            grad_gate_a,
            extra_a[0],
            extra_a[1],
            extra_a[2],
            grad_shift_b,
            grad_scale_b,
            grad_gate_b,
            extra_b[0],
            extra_b[1],
            extra_b[2],
        ]
    ).reshape(1, 12 * D)
    grad_small = jnp.concatenate(
        [grad_patch, grad_head, grad_bias[None], grad_gain_c[None], grad_gain_f[None]], 0
    )
    all_grad_modul = lax.all_gather(lax.psum(grad_modul, "band"), "clip", axis=0, tiled=True)
    grad_w_ada = matmul_tn(time_rows.astype(jnp.float32), all_grad_modul, lax.Precision.HIGHEST)
    members = (
        grad_w_qkva,
        grad_w_qkvb,
        grad_w_oa,
        grad_w_ob,
        grad_w_cq,
        grad_w_co,
        grad_up_a,
        grad_up_b,
        grad_down_a,
        grad_down_b,
    )
    summed = []
    for member in members:
        rows, cols = member.shape
        member = member.reshape(rows, band_count, cols // band_count).transpose(1, 0, 2)
        member = member.reshape(band_count, clip_count, rows // clip_count, cols // band_count)
        member = member.transpose(1, 0, 2, 3).reshape(-1, cols // band_count)
        member = lax.psum_scatter(member, ("clip", "band"), scatter_dimension=0, tiled=True)
        summed.append(lax.all_gather(member, "band", axis=1, tiled=True))
    wide_sum = jnp.concatenate([grad_w_ada] + summed[:8], 1)
    deep_sum = jnp.concatenate([summed[8], grad_w_ckv, summed[9]], 1)
    square_part = (jnp.sum(wide_sum * wide_sum) + jnp.sum(deep_sum * deep_sum)) / lax.axis_size(
        "band"
    )
    loss_sum, square_sum, small_sum = lax.psum(
        (loss_part, square_part, grad_small), ("clip", "band")
    )
    grad_norm = jnp.sqrt(square_sum + jnp.sum(small_sum * small_sum))
    factor = CLIP_MAX / jnp.maximum(grad_norm, CLIP_MAX)
    new_wide = adam_update(w_wide, m_wide, v_wide, wide_sum * factor, 0.15)
    new_deep = adam_update(w_deep, m_deep, v_deep, deep_sum * factor, 0.05)
    new_small = adam_update(w_small, m_small, v_small, small_sum * factor, 0.5)
    loss = loss_sum / global_count
    return (
        loss,
        grad_norm,
        new_wide[0],
        new_wide[1],
        new_wide[2],
        new_deep[0],
        new_deep[1],
        new_deep[2],
        new_small[0],
        new_small[1],
        new_small[2],
    )


def solution(mesh):
    in_specs = (
        P("clip", None, "band", None, None),
        P("clip", None, "band", None, None),
        P("clip"),
        P("clip"),
        P("clip", None),
        P("clip", None, None),
        P("clip", None),
        P("clip", None),
        P("clip", None),
        P("clip", None),
        P("clip", None),
        P("clip", None),
        P(),
        P(),
        P(),
    )
    out_specs = (
        P(),
        P(),
        P("clip", None),
        P("clip", None),
        P("clip", None),
        P("clip", None),
        P("clip", None),
        P("clip", None),
        P(),
        P(),
        P(),
    )
    return jax.shard_map(
        per_device, mesh=mesh, in_specs=in_specs, out_specs=out_specs, check_vma=False
    )
```

```python
from functools import partial
import math

import jax
import jax.numpy as jnp
from jax import lax
from jax.experimental import pallas as pl
from jax.experimental.pallas import tpu as pltpu
from jax.sharding import PartitionSpec as P

D = 1024
HEADS = 16
HEAD_DIM = 64
FF = 4096
CH = 8
SPACE = 16
WIN = 8
SHIFT = 4
TMAX = 1000
STEP = 10


EPS_NORM = 1e-06
CLIP_MAX = 0.001
BETA_ONE = 0.9
BETA_TWO = 0.95
ADAM_EPS = 1e-08
DECAY = 0.1
SELF_FORMS = ("wqhd,wkhd->whqk", "whqk,wkhd->wqhd", "whqk,wqhd->wkhd", "whqk,wkhd->wqhd")
CROSS_FORMS = ("qhd,khd->hqk", "hqk,khd->qhd", "hqk,qhd->khd", "hqk,khd->qhd")


def from_partner(block, axis, distance):
    count = lax.axis_size(axis)
    route = []
    for low in range(count):
        high = low | 1 << distance
        if high != low and high < count:
            route += [(low, high), (high, low)]
    return lax.ppermute(block, axis, route)


def shifted(value, axis, by):
    length = lax.axis_size(axis)
    return lax.ppermute(value, axis, [(i, (i + by) % length) for i in range(length)])


def matmul(left_op, right_op):
    return jnp.dot(left_op, right_op, preferred_element_type=jnp.float32)


def matmul_tn(left_op, right_op, precision=None):
    return lax.dot_general(
        left_op,
        right_op,
        (((0,), (0,)), ((), ())),
        precision=precision,
        preferred_element_type=jnp.float32,
    )


def matmul_nt(left_op, right_op):
    return lax.dot_general(
        left_op, right_op, (((1,), (1,)), ((), ())), preferred_element_type=jnp.float32
    )


def layer_norm(field_in):
    average = jnp.mean(field_in, -1, keepdims=True)
    centred = field_in - average
    return centred * lax.rsqrt(jnp.mean(centred * centred, -1, keepdims=True) + EPS_NORM)


def norm_modulated(field_in, shift_vec, scale_vec):
    return layer_norm(field_in) * (1.0 + scale_vec) + shift_vec


def norm_gained(field_in, gain_vec):
    return layer_norm(field_in) * gain_vec


def time_features(time_value):
    half_width = D // 2
    frequency = jnp.exp(-math.log(10000.0) * jnp.arange(half_width, dtype=jnp.float32) / half_width)
    angles = time_value[..., None] * frequency
    return jnp.concatenate([jnp.cos(angles), jnp.sin(angles)], -1)


def to_windows(token_grid, shape_win):
    num_frames, num_rows, num_cols, feat_dim = token_grid.shape
    win_frames, win_rows, win_cols = shape_win
    shaped = token_grid.reshape(
        num_frames // win_frames,
        win_frames,
        num_rows // win_rows,
        win_rows,
        num_cols // win_cols,
        win_cols,
        feat_dim,
    )
    return shaped.transpose(0, 2, 4, 1, 3, 5, 6).reshape(
        -1, win_frames * win_rows * win_cols, feat_dim
    )


def from_windows(blocks, grid_shape, shape_win):
    num_frames, num_rows, num_cols = grid_shape
    win_frames, win_rows, win_cols = shape_win
    feat_dim = blocks.shape[-1]
    shaped = blocks.reshape(
        num_frames // win_frames,
        num_rows // win_rows,
        num_cols // win_cols,
        win_frames,
        win_rows,
        win_cols,
        feat_dim,
    )
    return shaped.transpose(0, 3, 1, 4, 2, 5, 6).reshape(num_frames, num_rows, num_cols, feat_dim)


def split_heads(field_in):
    return field_in.reshape(field_in.shape[:-1] + (HEADS, HEAD_DIM))


def merge_heads(field_in):
    return field_in.reshape(field_in.shape[:-2] + (D,))


def attend_forward(queries, key_heads, value_heads, einsum_forms):
    scores = jnp.einsum(
        einsum_forms[0], queries, key_heads, preferred_element_type=jnp.float32
    ) * HEAD_DIM ** (-0.5)
    log_total = jax.nn.logsumexp(scores, axis=-1, keepdims=True)
    probabilities = jnp.exp(scores - log_total)
    attended = jnp.einsum(
        einsum_forms[1],
        probabilities.astype(jnp.bfloat16),
        value_heads,
        preferred_element_type=jnp.float32,
    )
    return (attended, log_total)


def attend_backward(queries, key_heads, value_heads, log_total, grad_out, einsum_forms):
    scores = jnp.einsum(
        einsum_forms[0], queries, key_heads, preferred_element_type=jnp.float32
    ) * HEAD_DIM ** (-0.5)
    probabilities = jnp.exp(scores - log_total)
    grad_values = jnp.einsum(
        einsum_forms[2],
        probabilities.astype(jnp.bfloat16),
        grad_out,
        preferred_element_type=jnp.float32,
    )
    grad_probs = jnp.einsum(
        einsum_forms[0], grad_out, value_heads, preferred_element_type=jnp.float32
    )
    inner_sum = jnp.sum(probabilities * grad_probs, -1, keepdims=True)
    grad_scores = (probabilities * (grad_probs - inner_sum)).astype(jnp.bfloat16)
    grad_queries = jnp.einsum(
        einsum_forms[3], grad_scores, key_heads, preferred_element_type=jnp.float32
    ) * HEAD_DIM ** (-0.5)
    grad_keys = jnp.einsum(
        einsum_forms[2], grad_scores, queries, preferred_element_type=jnp.float32
    ) * HEAD_DIM ** (-0.5)
    return (grad_queries, grad_keys, grad_values)


def mlp_forward(stream, modul, up_weight, down_weight):
    mlp_val, norm_back = jax.vjp(norm_modulated, stream, modul[3], modul[4])
    mlp_in = mlp_val.astype(jnp.bfloat16)
    up_proj = matmul(mlp_in, up_weight)
    gelu_val, gelu_back = jax.vjp(partial(jax.nn.gelu, approximate=False), up_proj)
    gelu_low = gelu_val.astype(jnp.bfloat16)
    down_proj = matmul(gelu_low, down_weight)
    return (stream + modul[5] * down_proj, (norm_back, mlp_in, gelu_back, gelu_low, down_proj))


def mlp_backward(grad_stream, modul, up_weight, down_weight, saved):
    norm_back, mlp_in, gelu_back, gelu_low, down_proj = saved
    grad_down = (modul[5] * grad_stream).astype(jnp.bfloat16)
    grad_gate = jnp.sum(grad_stream * down_proj, 0)
    grad_up = gelu_back(matmul_nt(grad_down, down_weight))[0].astype(jnp.bfloat16)
    grad_part, grad_shift, grad_scale = norm_back(matmul_nt(grad_up, up_weight))
    factors = ((gelu_low, grad_down), (mlp_in, grad_up))
    return (grad_stream + grad_part, factors, (grad_shift, grad_scale, grad_gate))


def adam_update(weight, first_mom, second_mom, grad_val, learn_rate):
    first_mom = BETA_ONE * first_mom + (1.0 - BETA_ONE) * grad_val
    second_mom = BETA_TWO * second_mom + (1.0 - BETA_TWO) * grad_val * grad_val
    first_hat = first_mom / (1.0 - BETA_ONE**STEP)
    second_hat = second_mom / (1.0 - BETA_TWO**STEP)
    weight = weight - learn_rate * (first_hat / (jnp.sqrt(second_hat) + ADAM_EPS) + DECAY * weight)
    return (weight, first_mom, second_mom)

MESH = pl.DeviceIdType.MESH
ANY = pl.BlockSpec(memory_space=pl.ANY)
TEXT_PAD = 80


def ring_place(clip, count):
    half = clip // 2
    odd = clip % 2
    return half + odd * (count - 1 - 2 * half)


def ring_clip(place, count):
    far = place // (count // 2)
    return (1 - far) * 2 * place + far * (2 * (count - 1 - place) + 1)


def greet(peers):
    barrier = pltpu.get_barrier_semaphore()
    for peer in peers:
        pl.semaphore_signal(barrier, inc=1, device_id=peer, device_id_type=MESH)
    pl.semaphore_wait(barrier, len(peers))


def exchange_kernel(count, facts_ref, text_ref, facts_out, text_out, send, recv, local):
    me = lax.axis_index("clip")
    band = lax.axis_index("band")
    peers = [((me + step) % count, band) for step in range(1, count)]
    greet(peers)
    own = [
        pltpu.make_async_copy(facts_ref, facts_out.at[me], local.at[0]),
        pltpu.make_async_copy(text_ref.at[me], text_out.at[me], local.at[1]),
    ]
    for copy in own:
        copy.start()
    sent = []
    for step, peer in enumerate(peers):
        sent += [
            pltpu.make_async_remote_copy(
                facts_ref, facts_out.at[me], send.at[0, step], recv.at[0, step], peer, MESH
            ),
            pltpu.make_async_remote_copy(
                text_ref.at[peer[0]], text_out.at[me], send.at[1, step], recv.at[1, step], peer, MESH
            ),
        ]
    for copy in sent:
        copy.start()
    for copy in own + sent:
        copy.wait()


def exchange_facts(facts, text):
    count = lax.axis_size("clip")
    return pl.pallas_call(
        partial(exchange_kernel, count),
        out_shape=(
            jax.ShapeDtypeStruct((count,) + facts.shape, facts.dtype),
            jax.ShapeDtypeStruct(text.shape, text.dtype),
        ),
        in_specs=[ANY] * 2,
        out_specs=(ANY,) * 2,
        scratch_shapes=[
            pltpu.SemaphoreType.DMA((2, count - 1)),
            pltpu.SemaphoreType.DMA((2, count - 1)),
            pltpu.SemaphoreType.DMA((2,)),
        ],
        compiler_params=pltpu.CompilerParams(collective_id=0, has_side_effects=True),
    )(facts, text)


def gather_kernel(count, shapes, *refs):
    num = len(shapes)
    shards, (vec_ref, text_ref) = refs[:num], refs[num : num + 2]
    full, (vec_out, text_out) = refs[num + 2 : 2 * num + 2], refs[2 * num + 2 : 2 * num + 4]
    ring_send, ring_recv, pair_send, pair_recv, own_sem, part_send, part_recv, part_own = refs[
        2 * num + 4 :
    ]
    me = lax.axis_index("clip")
    band = lax.axis_index("band")
    core = band % 2
    place = ring_place(me, count)
    onward = 1 - 2 * core
    following = (ring_clip((place + onward + count) % count, count), band)
    partner = (me, band + 1 - 2 * core)
    peers = [((me + step) % count, band) for step in range(1, count)]
    greet(peers + [partner])

    def block(ref, group, owner):
        rows, cols = shapes[group]
        return ref.at[
            pl.ds(pl.multiple_of(owner * rows, rows), rows),
            pl.ds(pl.multiple_of(core * (cols // 2), 128), cols // 2),
        ]

    def ring_copy(group, step):
        owner = ring_clip((place - onward * step + 2 * count) % count, count)
        there = block(full[group], group, owner)
        return pltpu.make_async_remote_copy(
            there, there, ring_send.at[step, group], ring_recv.at[step, group], following, MESH
        )

    def pair_copy(group, step):
        owner = ring_clip((place - onward * (step + 1) + 2 * count) % count, count)
        there = block(full[group], group, owner)
        return pltpu.make_async_remote_copy(
            there, there, pair_send.at[step, group], pair_recv.at[step, group], partner, MESH
        )

    def own_copy(group):
        rows, cols = shapes[group]
        return pltpu.make_async_copy(
            shards[group],
            full[group].at[pl.ds(pl.multiple_of(me * rows, rows), rows), :],
            own_sem.at[group],
        )

    parts = []
    for step, peer in enumerate(peers):
        for which, (src, dst) in enumerate(((vec_ref, vec_out), (text_ref, text_out))):
            parts.append(
                pltpu.make_async_remote_copy(
                    src.at[peer[0]],
                    dst.at[me],
                    part_send.at[which, step],
                    part_recv.at[which, step],
                    peer,
                    MESH,
                )
            )
    parts_own = [
        pltpu.make_async_copy(src.at[me], dst.at[me], part_own.at[which])
        for which, (src, dst) in enumerate(((vec_ref, vec_out), (text_ref, text_out)))
    ]
    for group in range(num):
        rows, cols = shapes[group]
        own_copy(group).start()
        pltpu.make_async_remote_copy(
            shards[group].at[:, pl.ds(pl.multiple_of(core * (cols // 2), 128), cols // 2)],
            block(full[group], group, me),
            ring_send.at[0, group],
            ring_recv.at[0, group],
            following,
            MESH,
        ).start()
    for copy in parts_own + parts:
        copy.start()

    @pl.loop(1, count - 1)
    def _(step):
        for group in range(num):
            ring_copy(group, step - 1).wait_recv()
            ring_copy(group, step).start()
            pair_copy(group, step - 1).start()

    for group in range(num):
        ring_copy(group, count - 2).wait_recv()
        pair_copy(group, count - 2).start()
    for copy in parts_own + parts:
        copy.wait()
    for group in range(num):
        own_copy(group).wait()

    @pl.loop(0, count - 1)
    def _(step):
        for group in range(num):
            ring_copy(group, step).wait_send()
            pair_copy(group, step).wait()


def gather_weights(shards, vectors, texts):
    count = lax.axis_size("clip")
    num = len(shards)
    steps = pltpu.SemaphoreType.DMA((count - 1, num))
    out = pl.pallas_call(
        partial(gather_kernel, count, [shard.shape for shard in shards]),
        out_shape=tuple(
            jax.ShapeDtypeStruct((count * s.shape[0], s.shape[1]), s.dtype) for s in shards
        )
        + tuple(jax.ShapeDtypeStruct(v.shape, v.dtype) for v in (vectors, texts)),
        in_specs=[ANY] * (num + 2),
        out_specs=(ANY,) * (num + 2),
        scratch_shapes=[
            steps,
            steps,
            steps,
            steps,
            pltpu.SemaphoreType.DMA((num,)),
            pltpu.SemaphoreType.DMA((2, count - 1)),
            pltpu.SemaphoreType.DMA((2, count - 1)),
            pltpu.SemaphoreType.DMA((2,)),
        ],
        compiler_params=pltpu.CompilerParams(collective_id=1, has_side_effects=True),
    )(*shards, vectors, texts)
    return out[:num], out[num], out[num + 1]


WIRE_MAX = 32767.0
WIRE_LEAST = 1e-30
UNIT = (128, 512)


def unit_parts(kind, first):
    if kind == 0:
        return ((0, 4, lambda u: u, lambda u: 0), (4, 4, lambda u: 4, lambda u: u - 3))
    return ((first, 3 - first, lambda u: u, lambda u: u), (3, 3, lambda u: 3, lambda u: u))


def reduce_kernel(count, tokens, phases, *refs):
    num = sum(len(phase["lefts"]) for phase in phases)
    lefts, rights = refs[:num], refs[num : 2 * num]
    wide_out, deep_out, square_out = refs[2 * num : 2 * num + 3]
    left_far, right_far = refs[2 * num + 3 : 3 * num + 3], refs[3 * num + 3 : 4 * num + 3]
    scratch = refs[4 * num + 3 :]
    left_buf, right_buf, got_low, got_scale, put_low, put_scale, plane_put = (
        scratch[2 * i : 2 * i + 2] for i in range(7)
    )
    plane_got = scratch[14 : 14 + len(phases)]
    (
        square_buf,
        left_sem,
        right_sem,
        pair_send,
        pair_recv,
        half_send,
        half_recv,
        ring_send,
        ring_recv,
        credit,
        plane_send,
        plane_recv,
        out_sem,
        out_send,
        out_recv,
    ) = scratch[14 + len(phases) :]
    me = lax.axis_index("clip")
    band = lax.axis_index("band")
    core = band % 2
    plane = band // 2
    place = ring_place(me, count)
    onward = 1 - 2 * core
    following = (ring_clip((place + onward + count) % count, count), band)
    preceding = (ring_clip((place - onward + count) % count, count), band)
    partner = (me, band + 1 - 2 * core)
    mirror = (me, band + 2 - 4 * plane)
    greet([following, preceding, partner, mirror])

    def owner_at(step, way):
        return ring_clip((place - way * (step + 1) + 2 * count) % count, count)

    def left_blocks(at):
        phase = phases[at]
        if phase["kind"] == 0:
            return [(b, phase["lefts"][0], b, 4) for b in range(4)] + [(4, phase["lefts"][1], 0, 1)]
        first = phase["first"]
        return [(first + i, left, 0, 1) for i, left in enumerate(phase["lefts"])]

    def right_blocks(at):
        phase = phases[at]
        if phase["kind"] == 0:
            return [(0, phase["lefts"][0], 0)] + [(1 + i, phase["lefts"][1], i) for i in range(4)]
        first = phase["first"]
        return [(first + i, phase["lefts"][i], 0) for i in range(3 - first)] + [
            (3 + i, phase["lefts"][-1], i) for i in range(3)
        ]

    def left_cols(step, way, which, many):
        width = lefts_width // count if many == 1 else deep_width // count
        start = owner_at(step, way) * width + which * 128
        return pl.ds(pl.multiple_of(start, 128), 128)

    lefts_width = lefts[phases[1]["lefts"][0]].shape[1]
    deep_width = lefts[phases[0]["lefts"][0]].shape[1]

    def pair_left(at, step):
        out = []
        for block, operand, which, many in left_blocks(at):
            cols = left_cols(step, -onward, which, many)
            out.append(
                pltpu.make_async_remote_copy(
                    lefts[operand].at[:, cols],
                    left_far[operand].at[:, cols],
                    pair_send.at[at, block, step],
                    pair_recv.at[at, block, step],
                    partner,
                    MESH,
                )
            )
        return out

    def pair_right(at):
        out = []
        for i, operand in enumerate(phases[at]["lefts"]):
            half = rights[operand].shape[1] // 2
            out.append(
                pltpu.make_async_remote_copy(
                    rights[operand].at[:, pl.ds(pl.multiple_of((1 - core) * half, 128), half)],
                    right_far[operand],
                    half_send.at[operand],
                    half_recv.at[operand],
                    partner,
                    MESH,
                )
            )
        return out

    def load_left(at, step, slot, far):
        kind = phases[at]["kind"]
        out = []
        for block, operand, which, many in left_blocks(at):
            cols = left_cols(step, onward, which, many)
            source = left_far if far else lefts
            out.append(
                pltpu.make_async_copy(
                    source[operand].at[:, cols],
                    left_buf[kind].at[slot, block, pl.ds(far * tokens, tokens), :],
                    left_sem.at[kind, slot, block, far],
                )
            )
        return out

    def load_right(at, far):
        kind = phases[at]["kind"]
        out = []
        for block, operand, which in right_blocks(at):
            if far:
                source = right_far[operand].at[:, pl.ds(which * UNIT[1], UNIT[1])]
            else:
                half = rights[operand].shape[1] // 2
                start = pl.multiple_of(core * half + which * UNIT[1], 128)
                source = rights[operand].at[:, pl.ds(start, UNIT[1])]
            out.append(
                pltpu.make_async_copy(
                    source,
                    right_buf[kind].at[block, pl.ds(far * tokens, tokens), :],
                    right_sem.at[kind, block, far],
                )
            )
        return out

    def ring_copies(at, part, slot):
        kind = phases[at]["kind"]
        start, many = unit_parts(kind, phases[at]["first"])[part][:2]
        units = pl.ds(start, many)
        return [
            pltpu.make_async_remote_copy(
                put.at[slot, units],
                got.at[slot, units],
                ring_send.at[kind, slot, part, i],
                ring_recv.at[kind, slot, part, i],
                following,
                MESH,
            )
            for i, (put, got) in enumerate(
                ((put_low[kind], got_low[kind]), (put_scale[kind], got_scale[kind]))
            )
        ]

    def plane_copy(at, part):
        kind = phases[at]["kind"]
        start, many = unit_parts(kind, phases[at]["first"])[part][:2]
        units = pl.ds(start, many)
        return pltpu.make_async_remote_copy(
            plane_put[kind].at[units],
            plane_got[at].at[units],
            plane_send.at[at, part],
            plane_recv.at[at, part],
            mirror,
            MESH,
        )

    def out_copies(at, unit):
        phase = phases[at]
        if phase["kind"] == 0 and unit < 4:
            half = UNIT[1]
            rows = deep_out.shape[0] // 4
            there = deep_out.at[
                pl.ds(unit * rows, rows),
                pl.ds(pl.multiple_of(phase["cols"][0] + core * half, 128), half),
            ]
        else:
            which, col = (1, unit - 4) if phase["kind"] == 0 else (unit - phase["first"], 0)
            if phase["kind"] and unit >= 3:
                which, col = len(phase["lefts"]) - 1, unit - 3
            half = rights[phase["lefts"][which]].shape[1] // 2
            start = phase["cols"][which] + core * half + col * UNIT[1]
            there = wide_out.at[:, pl.ds(pl.multiple_of(start, 128), UNIT[1])]
        here = plane_got[at].at[unit]
        return (
            pltpu.make_async_copy(here, there, out_sem.at[at, unit]),
            pltpu.make_async_remote_copy(
                here, there, out_send.at[at, unit], out_recv.at[at, unit], partner, MESH
            ),
        )

    def product(kind, slot, left, right):
        return lax.dot_general(
            left_buf[kind][slot, left],
            right_buf[kind][right],
            (((0,), (0,)), ((), ())),
            preferred_element_type=jnp.float32,
        )

    def start(copies):
        for copy in copies:
            copy.start()

    def finish(copies):
        for copy in copies:
            copy.wait()

    def take_step(at, step, first, last):
        phase = phases[at]
        kind = phase["kind"]
        slot = step % 2
        before = (step + 1) % 2
        for far in range(2):
            finish(load_left(at, step, slot, far))
        if not last:
            for copy in pair_left(at, step + 1):
                copy.wait_recv()
            for far in range(2):
                start(load_left(at, step + 1, before, far))
        for part, (low, many, left_of, right_of) in enumerate(unit_parts(kind, phase["first"])):
            if not first:
                for copy in ring_copies(at, part, before):
                    copy.wait_recv()
            if not (first or last):

                @pl.when(step >= 2)
                def _(part=part):
                    for copy in ring_copies(at, part, slot):
                        copy.wait_send()
                    pl.semaphore_wait(credit.at[kind, part], 1)

            @pl.loop(low, low + many)
            def _(unit, left_of=left_of, right_of=right_of):
                term = product(kind, slot, left_of(unit), right_of(unit))
                if not first:
                    came = got_low[kind][before, unit].astype(jnp.float32)
                    term = term + came * got_scale[kind][before, unit]
                if last:
                    plane_put[kind][unit] = term
                else:
                    largest = jnp.max(jnp.abs(term), axis=0, keepdims=True)
                    largest = jnp.maximum(largest, WIRE_LEAST)
                    factor = WIRE_MAX / largest
                    put_low[kind][slot, unit] = jnp.round(term * factor).astype(jnp.int16)
                    put_scale[kind][slot, unit] = largest * (1.0 / WIRE_MAX)

            if last:
                plane_copy(at, part).start()
            else:
                start(ring_copies(at, part, slot))
            if not (first or last):

                @pl.when(step < count - 2)
                def _(part=part):
                    pl.semaphore_signal(
                        credit.at[kind, part], inc=1, device_id=preceding, device_id_type=MESH
                    )

    def close(at):
        kind = phases[at]["kind"]
        for part, (low, many, _, _) in enumerate(unit_parts(kind, phases[at]["first"])):
            plane_copy(at, part).wait()

            @pl.loop(low, low + many)
            def _(unit):
                total = plane_put[kind][unit] + plane_got[at][unit]
                plane_got[at][unit] = total
                square_buf[...] += jnp.sum(
                    (total * total).reshape(UNIT[0] // 8, 8, UNIT[1]), axis=0
                )

            for unit in range(low, low + many):
                start(out_copies(at, unit))

    square_buf[...] = jnp.zeros_like(square_buf)
    start(load_right(0, 0))
    start(pair_right(0))

    @pl.loop(0, count)
    def _(step):
        start(pair_left(0, step))

    start(load_left(0, 0, 0, 0))
    for at in range(len(phases)):
        if at == 0:
            for copy in pair_right(0):
                copy.wait_recv()
            start(load_right(0, 1))
            for copy in pair_left(0, 0):
                copy.wait_recv()
            start(load_left(0, 0, 0, 1))
        for far in range(2):
            finish(load_right(at, far))
        more = at + 1 < len(phases)
        if more:
            start(pair_right(at + 1))
            start(load_right(at + 1, 0))
        take_step(at, 0, True, False)
        if more:
            start(pair_left(at + 1, 0))

        @pl.loop(1, count - 1)
        def _(step, at=at, more=more):
            take_step(at, step, False, False)
            if more:
                start(pair_left(at + 1, step))

        if more:
            start(pair_left(at + 1, count - 1))
            for copy in pair_right(at + 1):
                copy.wait_recv()
            start(load_right(at + 1, 1))
            for copy in pair_left(at + 1, 0):
                copy.wait_recv()
            for far in range(2):
                start(load_left(at + 1, 0, 0, far))
        take_step(at, count - 1, False, True)
        for part in range(2):
            for slot in range(2):
                for copy in ring_copies(at, part, slot):
                    copy.wait_send()
        if at:
            close(at - 1)
    close(len(phases) - 1)
    square_out[...] = square_buf[...]
    for at, phase in enumerate(phases):
        for copy in pair_right(at):
            copy.wait_send()

        @pl.loop(0, count)
        def _(step, at=at):
            for copy in pair_left(at, step):
                copy.wait_send()

        for unit in range(phase["first"], 8 if phase["kind"] == 0 else 6):
            finish(out_copies(at, unit))


def reduce_gradients(phases, lefts, rights, wide_cols, deep_cols):
    count = lax.axis_size("clip")
    tokens = lefts[0].shape[0]
    wide_rows = lefts[1].shape[1] // count
    deep_rows = lefts[0].shape[1] // count
    num = len(lefts)
    dma = pltpu.SemaphoreType.DMA
    units, lefts_of, rights_of = (8, 6), (5, 4), (5, 6)
    scratch = [pltpu.VMEM((2, lefts_of[k], 2 * tokens, 128), jnp.bfloat16) for k in range(2)]
    scratch += [pltpu.VMEM((rights_of[k], 2 * tokens, UNIT[1]), jnp.bfloat16) for k in range(2)]
    for _ in range(2):
        scratch += [pltpu.VMEM((2, units[k]) + UNIT, jnp.int16) for k in range(2)]
        scratch += [pltpu.VMEM((2, units[k], 1, UNIT[1]), jnp.float32) for k in range(2)]
    scratch += [pltpu.VMEM((units[k],) + UNIT, jnp.float32) for k in range(2)]
    scratch += [pltpu.VMEM((units[p["kind"]],) + UNIT, jnp.float32) for p in phases]
    scratch += [
        pltpu.VMEM((8, UNIT[1]), jnp.float32),
        dma((2, 2, 5, 2)),
        dma((2, 6, 2)),
        dma((len(phases), 5, count)),
        dma((len(phases), 5, count)),
        dma((num,)),
        dma((num,)),
        dma((2, 2, 2, 2)),
        dma((2, 2, 2, 2)),
        pltpu.SemaphoreType.REGULAR((2, 2)),
        dma((len(phases), 2)),
        dma((len(phases), 2)),
        dma((len(phases), 8)),
        dma((len(phases), 8)),
        dma((len(phases), 8)),
    ]
    out = pl.pallas_call(
        partial(reduce_kernel, count, tokens, phases),
        out_shape=(
            jax.ShapeDtypeStruct((wide_rows, wide_cols), jnp.float32),
            jax.ShapeDtypeStruct((deep_rows, deep_cols), jnp.float32),
            jax.ShapeDtypeStruct((8, UNIT[1]), jnp.float32),
        )
        + tuple(jax.ShapeDtypeStruct(x.shape, x.dtype) for x in lefts)
        + tuple(jax.ShapeDtypeStruct((tokens, x.shape[1] // 2), x.dtype) for x in rights),
        in_specs=[ANY] * (2 * num),
        out_specs=(ANY, ANY, pl.BlockSpec(memory_space=pltpu.VMEM)) + (ANY,) * (2 * num),
        scratch_shapes=scratch,
        compiler_params=pltpu.CompilerParams(
            collective_id=2, has_side_effects=True, vmem_limit_bytes=58 << 20
        ),
    )(*lefts, *rights)
    return out[:3]


def per_device(
    latents,
    noise_field,
    timesteps,
    null_flags,
    frame_mask,
    context,
    w_wide,
    m_wide,
    v_wide,
    w_deep,
    m_deep,
    v_deep,
    w_small,
    m_small,
    v_small,
):
    clip_count = lax.axis_size("clip")
    band_count = lax.axis_size("band")
    clip_at = lax.axis_index("clip")
    band_at = lax.axis_index("band")
    wide_rows = w_wide.shape[0]
    deep_rows = w_deep.shape[0]
    text_len, text_dim = context.shape[1:]
    facts = jnp.pad(
        jnp.concatenate([timesteps, frame_mask[0]])[None],
        ((0, 7), (0, 127 - frame_mask.shape[1])),
    )
    kept_text = context[0] * (1 - null_flags[0]).astype(jnp.bfloat16)
    text_cols = jnp.pad(
        kept_text.reshape(text_len, clip_count, deep_rows).transpose(1, 0, 2),
        ((0, 0), (0, TEXT_PAD - text_len), (0, 0)),
    )
    all_facts, all_text = exchange_facts(facts, text_cols)
    all_times = all_facts[:, 0, 0].astype(jnp.float32)
    all_time_low = jax.nn.silu(time_features(all_times)).astype(jnp.bfloat16)
    time_rows = lax.dynamic_slice(
        all_time_low, (0, clip_at * wide_rows), (clip_count, wide_rows)
    )
    part_modul = matmul(time_rows, w_wide[:, : 12 * D].astype(jnp.bfloat16))
    kv_cols = 2 * D // band_count
    kv_weight = lax.dynamic_slice(
        w_deep, (0, D + band_at * kv_cols), (deep_rows, kv_cols)
    ).astype(jnp.bfloat16)
    part_kv = matmul(all_text.reshape(clip_count * TEXT_PAD, deep_rows), kv_weight)
    edges = (12 * D, 15 * D, 18 * D, 19 * D, 20 * D, 21 * D, 22 * D, 22 * D + FF, 22 * D + 2 * FF)
    shards = [w_wide[:, low:high].astype(jnp.bfloat16) for low, high in zip(edges, edges[1:])]
    shards += [w_deep[:, :D].astype(jnp.bfloat16), w_deep[:, 3 * D :].astype(jnp.bfloat16)]
    gathered, all_modul, all_kv = gather_weights(
        shards,
        part_modul.reshape(clip_count, 12 * D // 128, 128),
        part_kv.reshape(clip_count, TEXT_PAD, kv_cols),
    )
    (
        qkv_a_w,
        qkv_b_w,
        out_a_w,
        out_b_w,
        query_w,
        cross_out_w,
        up_a_w,
        up_b_w,
        down_a_w,
        down_b_w,
    ) = gathered
    keyval = lax.all_gather(jnp.sum(all_kv, 0).astype(jnp.bfloat16), "band", axis=1, tiled=True)
    keyval = keyval[:text_len]
    small_low = w_small.astype(jnp.bfloat16)
    small_val = small_low.astype(jnp.float32)
    num_frames, num_rows, num_cols = (latents.shape[1], latents.shape[2], latents.shape[3])
    grid_shape = (num_frames, num_rows, num_cols)
    tok_count = num_frames * num_rows * num_cols
    all_mask = all_facts[:, 0, 1 : 1 + num_frames]
    global_count = jnp.sum(all_mask).astype(jnp.float32) * (num_rows * num_cols * CH * band_count)
    time_value = timesteps[0].astype(jnp.float32)
    noise_angle = 0.5 * math.pi * time_value / TMAX
    signal, spread = (jnp.cos(noise_angle), jnp.sin(noise_angle))
    clean_tok = latents[0].reshape(tok_count, CH)
    noise_tok = noise_field[0].reshape(tok_count, CH)
    noisy_low = (signal * clean_tok + spread * noise_tok).astype(jnp.bfloat16)
    target = signal * noise_tok - spread * clean_tok
    modulation = jnp.sum(all_modul, 0).reshape(12, D)
    mod_a, mod_b = (modulation[:6], modulation[6:])
    stream_zero = matmul(noisy_low, small_low[:CH]) + small_val[2 * CH]
    normed_a, back_a = jax.vjp(norm_modulated, stream_zero, mod_a[0], mod_a[1])
    in_a = normed_a.astype(jnp.bfloat16)
    spatial = (1, num_rows, SPACE)
    qkv_a = (
        matmul(in_a, qkv_a_w).astype(jnp.bfloat16).reshape(num_frames, num_rows, num_cols, 3 * D)
    )
    blocks_a = to_windows(qkv_a, spatial)
    partner = from_partner(blocks_a[..., D:], "band", 0)
    keys_all = jnp.concatenate([blocks_a[..., D:], partner], 1)
    space_q = split_heads(blocks_a[..., :D])
    space_k = split_heads(keys_all[..., :D])
    space_v = split_heads(keys_all[..., D:])
    space_out, space_total = attend_forward(space_q, space_k, space_v, SELF_FORMS)
    att_a = from_windows(merge_heads(space_out.astype(jnp.bfloat16)), grid_shape, spatial).reshape(
        tok_count, D
    )
    proj_a = matmul(att_a, out_a_w)
    stream_one = stream_zero + mod_a[2] * proj_a
    stream_two, saved_a = mlp_forward(stream_one, mod_a, up_a_w, down_a_w)
    normed_b, back_b = jax.vjp(norm_modulated, stream_two, mod_b[0], mod_b[1])
    token_grid = normed_b.astype(jnp.bfloat16).reshape(num_frames, num_rows, num_cols, D)
    arrived = shifted(token_grid[:, :SHIFT], "band", -1)
    rolled = jnp.concatenate([token_grid[:, SHIFT:], arrived], 1).reshape(tok_count, D)
    temporal = (num_frames, WIN, WIN)
    qkv_b = matmul(rolled, qkv_b_w).astype(jnp.bfloat16)
    blocks_b = to_windows(qkv_b.reshape(num_frames, num_rows, num_cols, 3 * D), temporal)
    win_q = split_heads(blocks_b[..., :D])
    win_k = split_heads(blocks_b[..., D : 2 * D])
    win_v = split_heads(blocks_b[..., 2 * D :])
    win_out, win_total = attend_forward(win_q, win_k, win_v, SELF_FORMS)
    out_grid = from_windows(merge_heads(win_out.astype(jnp.bfloat16)), grid_shape, temporal)
    returned = shifted(out_grid[:, num_rows - SHIFT :], "band", 1)
    att_b = jnp.concatenate([returned, out_grid[:, : num_rows - SHIFT]], 1).reshape(tok_count, D)
    proj_b = matmul(att_b, out_b_w)
    stream_three = stream_two + mod_b[2] * proj_b
    cross_val, cross_back = jax.vjp(norm_gained, stream_three, small_val[2 * CH + 1])
    cross_in = cross_val.astype(jnp.bfloat16)
    query_proj = matmul(cross_in, query_w).astype(jnp.bfloat16)
    cross_q = split_heads(query_proj)
    cross_k = split_heads(keyval[:, :D])
    cross_v = split_heads(keyval[:, D:])
    cross_out, cross_total = attend_forward(cross_q, cross_k, cross_v, CROSS_FORMS)
    crossed = merge_heads(cross_out.astype(jnp.bfloat16))
    stream_four = stream_three + matmul(crossed, cross_out_w)
    stream_five, saved_b = mlp_forward(stream_four, mod_b, up_b_w, down_b_w)
    final_val, final_back = jax.vjp(norm_gained, stream_five, small_val[2 * CH + 2])
    final_low = final_val.astype(jnp.bfloat16)
    head_low = small_low[CH : 2 * CH]
    predicted = matmul_nt(final_low, head_low)
    weight_row = jnp.repeat(frame_mask[0].astype(jnp.float32), num_rows * num_cols)[:, None]
    pred_error = predicted - target
    loss_part = jnp.sum(weight_row * pred_error * pred_error)
    grad_pred = (weight_row * pred_error * (2.0 / global_count)).astype(jnp.bfloat16)
    grad_head = matmul_tn(grad_pred, final_low)
    grad_stream, grad_gain_f = final_back(matmul(grad_pred, head_low))
    grad_stream, mlp_factors_b, extra_b = mlp_backward(
        grad_stream, mod_b, up_b_w, down_b_w, saved_b
    )
    grad_cross = grad_stream.astype(jnp.bfloat16)
    grad_crossed = split_heads(matmul_nt(grad_cross, cross_out_w).astype(jnp.bfloat16))
    cq_grad, ck_grad, cv_grad = attend_backward(
        cross_q, cross_k, cross_v, cross_total, grad_crossed, CROSS_FORMS
    )
    grad_query = merge_heads(cq_grad).astype(jnp.bfloat16)
    grad_part, grad_gain_c = cross_back(matmul_nt(grad_query, query_w))
    grad_keyval = jnp.concatenate([merge_heads(ck_grad), merge_heads(cv_grad)], 1)
    grad_keyval = jnp.pad(grad_keyval, ((0, TEXT_PAD - text_len), (0, 0)))
    grad_keyval = lax.psum_scatter(grad_keyval, "band", scatter_dimension=1, tiled=True)
    grad_keyval = lax.all_gather(grad_keyval, "clip", axis=0, tiled=True)
    grad_w_ckv = matmul_tn(
        all_text.reshape(clip_count * TEXT_PAD, deep_rows).astype(jnp.float32),
        grad_keyval,
        lax.Precision.HIGHEST,
    )
    grad_w_ckv = lax.all_gather(grad_w_ckv, "band", axis=1, tiled=True)
    grad_stream = grad_stream + grad_part
    grad_proj = (mod_b[2] * grad_stream).astype(jnp.bfloat16)
    grad_gate_b = jnp.sum(grad_stream * proj_b, 0)
    factors_ob = (att_b, grad_proj)
    grad_att = (
        matmul_nt(grad_proj, out_b_w)
        .astype(jnp.bfloat16)
        .reshape(num_frames, num_rows, num_cols, D)
    )
    fetched = shifted(grad_att[:, :SHIFT], "band", -1)
    grad_rolled = jnp.concatenate([grad_att[:, SHIFT:], fetched], 1)
    grad_win = split_heads(to_windows(grad_rolled, temporal))
    wq_grad, wk_grad, wv_grad = attend_backward(
        win_q, win_k, win_v, win_total, grad_win, SELF_FORMS
    )
    grad_blocks = jnp.concatenate(
        [merge_heads(wq_grad), merge_heads(wk_grad), merge_heads(wv_grad)], -1
    )
    grad_qkv = (
        from_windows(grad_blocks, grid_shape, temporal)
        .reshape(tok_count, 3 * D)
        .astype(jnp.bfloat16)
    )
    factors_qkvb = (rolled, grad_qkv)
    grad_in_roll = matmul_nt(grad_qkv, qkv_b_w).reshape(num_frames, num_rows, num_cols, D)
    sent_back = shifted(grad_in_roll[:, num_rows - SHIFT :], "band", 1)
    grad_normed = jnp.concatenate([sent_back, grad_in_roll[:, : num_rows - SHIFT]], 1).reshape(
        tok_count, D
    )
    grad_part, grad_shift_b, grad_scale_b = back_b(grad_normed)
    grad_stream = grad_stream + grad_part
    grad_stream, mlp_factors_a, extra_a = mlp_backward(
        grad_stream, mod_a, up_a_w, down_a_w, saved_a
    )
    grad_proj = (mod_a[2] * grad_stream).astype(jnp.bfloat16)
    grad_gate_a = jnp.sum(grad_stream * proj_a, 0)
    factors_oa = (att_a, grad_proj)
    grad_att = (
        matmul_nt(grad_proj, out_a_w)
        .astype(jnp.bfloat16)
        .reshape(num_frames, num_rows, num_cols, D)
    )
    grad_space = split_heads(to_windows(grad_att, spatial))
    sq_grad, sk_grad, sv_grad = attend_backward(
        space_q, space_k, space_v, space_total, grad_space, SELF_FORMS
    )
    half_len = space_q.shape[1]
    key_grads = merge_heads(sk_grad)
    value_grads = merge_heads(sv_grad)
    back_keys, back_values = from_partner(
        (key_grads[:, half_len:], value_grads[:, half_len:]), "band", 0
    )
    grad_blocks = jnp.concatenate(
        [
            merge_heads(sq_grad),
            key_grads[:, :half_len] + back_keys,
            value_grads[:, :half_len] + back_values,
        ],
        -1,
    )
    grad_qkv = (
        from_windows(grad_blocks, grid_shape, spatial)
        .reshape(tok_count, 3 * D)
        .astype(jnp.bfloat16)
    )
    factors_qkva = (in_a, grad_qkv)
    grad_part, grad_shift_a, grad_scale_a = back_a(matmul_nt(grad_qkv, qkv_a_w))
    grad_stream = grad_stream + grad_part
    grad_patch = matmul_tn(noisy_low.astype(jnp.float32), grad_stream, lax.Precision.HIGHEST)
    grad_bias = jnp.sum(grad_stream, 0)
    grad_modul = jnp.stack(
        [
            grad_shift_a,
            grad_scale_a,
            grad_gate_a,
            extra_a[0],
            extra_a[1],
            extra_a[2],
            grad_shift_b,
            grad_scale_b,
            grad_gate_b,
            extra_b[0],
            extra_b[1],
            extra_b[2],
        ]
    ).reshape(1, 12 * D)
    grad_small = jnp.concatenate(
        [grad_patch, grad_head, grad_bias[None], grad_gain_c[None], grad_gain_f[None]], 0
    )
    all_grad_modul = lax.all_gather(lax.psum(grad_modul, "band"), "clip", axis=0, tiled=True)
    grad_w_ada = matmul_tn(time_rows.astype(jnp.float32), all_grad_modul, lax.Precision.HIGHEST)
    factors = mlp_factors_b + (
        (crossed, grad_cross),
        (cross_in, grad_query),
        factors_ob,
        factors_qkvb,
    )
    factors += mlp_factors_a + (factors_oa, factors_qkva)
    if wide_rows == 128 and deep_rows == 512:
        phases = (
            {"kind": 0, "first": 0, "lefts": (0, 1), "cols": (D, 10 * D + FF)},
            {"kind": 1, "first": 0, "lefts": (2, 3, 4, 5), "cols": (9 * D, 8 * D, 7 * D, 3 * D)},
            {"kind": 0, "first": 0, "lefts": (6, 7), "cols": (0, 10 * D)},
            {"kind": 1, "first": 2, "lefts": (8, 9), "cols": (6 * D, 0)},
        )
        wide_rest, deep_rest, squares = reduce_gradients(
            phases, [f[0] for f in factors], [f[1] for f in factors], 10 * D + 2 * FF, 2 * D
        )
        square_part = jnp.sum(squares) / (band_count // 2)
    else:
        summed = []
        for left, right in factors:
            member = matmul_tn(left, right)
            rows, cols = member.shape
            member = member.reshape(rows, band_count, cols // band_count).transpose(1, 0, 2)
            member = member.reshape(band_count, clip_count, rows // clip_count, cols // band_count)
            member = member.transpose(1, 0, 2, 3).reshape(-1, cols // band_count)
            member = lax.psum_scatter(member, ("clip", "band"), scatter_dimension=0, tiled=True)
            summed.append(lax.all_gather(member, "band", axis=1, tiled=True))
        wide_rest = jnp.concatenate([summed[i] for i in (9, 5, 8, 4, 3, 2, 7, 1)], 1)
        deep_rest = jnp.concatenate([summed[6], summed[0]], 1)
        square_part = (jnp.sum(wide_rest**2) + jnp.sum(deep_rest**2)) / band_count
    wide_sum = jnp.concatenate([grad_w_ada, wide_rest], 1)
    deep_sum = jnp.concatenate([deep_rest[:, :D], grad_w_ckv, deep_rest[:, D:]], 1)
    square_part += (jnp.sum(grad_w_ada**2) + jnp.sum(grad_w_ckv**2)) / band_count
    loss_sum, square_sum, small_sum = lax.psum(
        (loss_part, square_part, grad_small), ("clip", "band")
    )
    grad_norm = jnp.sqrt(square_sum + jnp.sum(small_sum * small_sum))
    factor = CLIP_MAX / jnp.maximum(grad_norm, CLIP_MAX)
    new_wide = adam_update(w_wide, m_wide, v_wide, wide_sum * factor, 0.15)
    new_deep = adam_update(w_deep, m_deep, v_deep, deep_sum * factor, 0.05)
    new_small = adam_update(w_small, m_small, v_small, small_sum * factor, 0.5)
    loss = loss_sum / global_count
    return (
        loss,
        grad_norm,
        new_wide[0],
        new_wide[1],
        new_wide[2],
        new_deep[0],
        new_deep[1],
        new_deep[2],
        new_small[0],
        new_small[1],
        new_small[2],
    )


def solution(mesh):
    in_specs = (
        P("clip", None, "band", None, None),
        P("clip", None, "band", None, None),
        P("clip"),
        P("clip"),
        P("clip", None),
        P("clip", None, None),
        P("clip", None),
        P("clip", None),
        P("clip", None),
        P("clip", None),
        P("clip", None),
        P("clip", None),
        P(),
        P(),
        P(),
    )
    out_specs = (
        P(),
        P(),
        P("clip", None),
        P("clip", None),
        P("clip", None),
        P("clip", None),
        P("clip", None),
        P("clip", None),
        P(),
        P(),
        P(),
    )
    return jax.shard_map(
        per_device, mesh=mesh, in_specs=in_specs, out_specs=out_specs, check_vma=False
    )
```

```python
from functools import partial
import math

import jax
import jax.numpy as jnp
from jax import lax
from jax.experimental import pallas as pl
from jax.experimental.pallas import tpu as pltpu
from jax.sharding import PartitionSpec as P

D = 1024
HEADS = 16
HEAD_DIM = 64
FF = 4096
CH = 8
SPACE = 16
WIN = 8
SHIFT = 4
TMAX = 1000
STEP = 10


EPS_NORM = 1e-06
CLIP_MAX = 0.001
BETA_ONE = 0.9
BETA_TWO = 0.95
ADAM_EPS = 1e-08
DECAY = 0.1
SELF_FORMS = ("wqhd,wkhd->whqk", "whqk,wkhd->wqhd", "whqk,wqhd->wkhd", "whqk,wkhd->wqhd")
CROSS_FORMS = ("qhd,khd->hqk", "hqk,khd->qhd", "hqk,qhd->khd", "hqk,khd->qhd")


def from_partner(block, axis, distance):
    count = lax.axis_size(axis)
    route = []
    for low in range(count):
        high = low | 1 << distance
        if high != low and high < count:
            route += [(low, high), (high, low)]
    return lax.ppermute(block, axis, route)


def shifted(value, axis, by):
    length = lax.axis_size(axis)
    return lax.ppermute(value, axis, [(i, (i + by) % length) for i in range(length)])


def matmul(left_op, right_op):
    return jnp.dot(left_op, right_op, preferred_element_type=jnp.float32)


def matmul_tn(left_op, right_op, precision=None):
    return lax.dot_general(
        left_op,
        right_op,
        (((0,), (0,)), ((), ())),
        precision=precision,
        preferred_element_type=jnp.float32,
    )


def matmul_nt(left_op, right_op):
    return lax.dot_general(
        left_op, right_op, (((1,), (1,)), ((), ())), preferred_element_type=jnp.float32
    )


def layer_norm(field_in):
    average = jnp.mean(field_in, -1, keepdims=True)
    centred = field_in - average
    return centred * lax.rsqrt(jnp.mean(centred * centred, -1, keepdims=True) + EPS_NORM)


def norm_modulated(field_in, shift_vec, scale_vec):
    return layer_norm(field_in) * (1.0 + scale_vec) + shift_vec


def norm_gained(field_in, gain_vec):
    return layer_norm(field_in) * gain_vec


def time_features(time_value):
    half_width = D // 2
    frequency = jnp.exp(-math.log(10000.0) * jnp.arange(half_width, dtype=jnp.float32) / half_width)
    angles = time_value[..., None] * frequency
    return jnp.concatenate([jnp.cos(angles), jnp.sin(angles)], -1)


def to_windows(token_grid, shape_win):
    num_frames, num_rows, num_cols, feat_dim = token_grid.shape
    win_frames, win_rows, win_cols = shape_win
    shaped = token_grid.reshape(
        num_frames // win_frames,
        win_frames,
        num_rows // win_rows,
        win_rows,
        num_cols // win_cols,
        win_cols,
        feat_dim,
    )
    return shaped.transpose(0, 2, 4, 1, 3, 5, 6).reshape(
        -1, win_frames * win_rows * win_cols, feat_dim
    )


def from_windows(blocks, grid_shape, shape_win):
    num_frames, num_rows, num_cols = grid_shape
    win_frames, win_rows, win_cols = shape_win
    feat_dim = blocks.shape[-1]
    shaped = blocks.reshape(
        num_frames // win_frames,
        num_rows // win_rows,
        num_cols // win_cols,
        win_frames,
        win_rows,
        win_cols,
        feat_dim,
    )
    return shaped.transpose(0, 3, 1, 4, 2, 5, 6).reshape(num_frames, num_rows, num_cols, feat_dim)


def split_heads(field_in):
    return field_in.reshape(field_in.shape[:-1] + (HEADS, HEAD_DIM))


def merge_heads(field_in):
    return field_in.reshape(field_in.shape[:-2] + (D,))


def attend_forward(queries, key_heads, value_heads, einsum_forms):
    scores = jnp.einsum(
        einsum_forms[0], queries, key_heads, preferred_element_type=jnp.float32
    ) * HEAD_DIM ** (-0.5)
    log_total = jax.nn.logsumexp(scores, axis=-1, keepdims=True)
    probabilities = jnp.exp(scores - log_total)
    attended = jnp.einsum(
        einsum_forms[1],
        probabilities.astype(jnp.bfloat16),
        value_heads,
        preferred_element_type=jnp.float32,
    )
    return (attended, log_total)


def attend_backward(queries, key_heads, value_heads, log_total, grad_out, einsum_forms):
    scores = jnp.einsum(
        einsum_forms[0], queries, key_heads, preferred_element_type=jnp.float32
    ) * HEAD_DIM ** (-0.5)
    probabilities = jnp.exp(scores - log_total)
    grad_values = jnp.einsum(
        einsum_forms[2],
        probabilities.astype(jnp.bfloat16),
        grad_out,
        preferred_element_type=jnp.float32,
    )
    grad_probs = jnp.einsum(
        einsum_forms[0], grad_out, value_heads, preferred_element_type=jnp.float32
    )
    inner_sum = jnp.sum(probabilities * grad_probs, -1, keepdims=True)
    grad_scores = (probabilities * (grad_probs - inner_sum)).astype(jnp.bfloat16)
    grad_queries = jnp.einsum(
        einsum_forms[3], grad_scores, key_heads, preferred_element_type=jnp.float32
    ) * HEAD_DIM ** (-0.5)
    grad_keys = jnp.einsum(
        einsum_forms[2], grad_scores, queries, preferred_element_type=jnp.float32
    ) * HEAD_DIM ** (-0.5)
    return (grad_queries, grad_keys, grad_values)


def mlp_forward(stream, modul, up_weight, down_weight):
    mlp_val, norm_back = jax.vjp(norm_modulated, stream, modul[3], modul[4])
    mlp_in = mlp_val.astype(jnp.bfloat16)
    up_proj = matmul(mlp_in, up_weight)
    gelu_val, gelu_back = jax.vjp(partial(jax.nn.gelu, approximate=False), up_proj)
    gelu_low = gelu_val.astype(jnp.bfloat16)
    down_proj = matmul(gelu_low, down_weight)
    return (stream + modul[5] * down_proj, (norm_back, mlp_in, gelu_back, gelu_low, down_proj))


def mlp_backward(grad_stream, modul, up_weight, down_weight, saved):
    norm_back, mlp_in, gelu_back, gelu_low, down_proj = saved
    grad_down = (modul[5] * grad_stream).astype(jnp.bfloat16)
    grad_gate = jnp.sum(grad_stream * down_proj, 0)
    grad_up = gelu_back(matmul_nt(grad_down, down_weight))[0].astype(jnp.bfloat16)
    grad_part, grad_shift, grad_scale = norm_back(matmul_nt(grad_up, up_weight))
    factors = ((gelu_low, grad_down), (mlp_in, grad_up))
    return (grad_stream + grad_part, factors, (grad_shift, grad_scale, grad_gate))


def adam_update(weight, first_mom, second_mom, grad_val, learn_rate):
    first_mom = BETA_ONE * first_mom + (1.0 - BETA_ONE) * grad_val
    second_mom = BETA_TWO * second_mom + (1.0 - BETA_TWO) * grad_val * grad_val
    first_hat = first_mom / (1.0 - BETA_ONE**STEP)
    second_hat = second_mom / (1.0 - BETA_TWO**STEP)
    weight = weight - learn_rate * (first_hat / (jnp.sqrt(second_hat) + ADAM_EPS) + DECAY * weight)
    return (weight, first_mom, second_mom)

MESH = pl.DeviceIdType.MESH
ANY = pl.BlockSpec(memory_space=pl.ANY)
TEXT_PAD = 80


def ring_place(clip, count):
    half = clip // 2
    odd = clip % 2
    return half + odd * (count - 1 - 2 * half)


def ring_clip(place, count):
    far = place // (count // 2)
    return (1 - far) * 2 * place + far * (2 * (count - 1 - place) + 1)


def greet(peers):
    barrier = pltpu.get_barrier_semaphore()
    for peer in peers:
        pl.semaphore_signal(barrier, inc=1, device_id=peer, device_id_type=MESH)
    pl.semaphore_wait(barrier, len(peers))


def exchange_kernel(count, facts_ref, text_ref, facts_out, text_out, send, recv, local):
    me = lax.axis_index("clip")
    band = lax.axis_index("band")
    peers = [((me + step) % count, band) for step in range(1, count)]
    greet(peers)
    own = [
        pltpu.make_async_copy(facts_ref, facts_out.at[me], local.at[0]),
        pltpu.make_async_copy(text_ref.at[me], text_out.at[me], local.at[1]),
    ]
    for copy in own:
        copy.start()
    sent = []
    for step, peer in enumerate(peers):
        sent += [
            pltpu.make_async_remote_copy(
                facts_ref, facts_out.at[me], send.at[0, step], recv.at[0, step], peer, MESH
            ),
            pltpu.make_async_remote_copy(
                text_ref.at[peer[0]], text_out.at[me], send.at[1, step], recv.at[1, step], peer, MESH
            ),
        ]
    for copy in sent:
        copy.start()
    for copy in own + sent:
        copy.wait()


def exchange_facts(facts, text):
    count = lax.axis_size("clip")
    return pl.pallas_call(
        partial(exchange_kernel, count),
        out_shape=(
            jax.ShapeDtypeStruct((count,) + facts.shape, facts.dtype),
            jax.ShapeDtypeStruct(text.shape, text.dtype),
        ),
        in_specs=[ANY] * 2,
        out_specs=(ANY,) * 2,
        scratch_shapes=[
            pltpu.SemaphoreType.DMA((2, count - 1)),
            pltpu.SemaphoreType.DMA((2, count - 1)),
            pltpu.SemaphoreType.DMA((2,)),
        ],
        compiler_params=pltpu.CompilerParams(collective_id=0, has_side_effects=True),
    )(facts, text)


def gather_kernel(count, shapes, *refs):
    num = len(shapes)
    shards, (vec_ref, text_ref) = refs[:num], refs[num : num + 2]
    full, (vec_out, text_out) = refs[num + 2 : 2 * num + 2], refs[2 * num + 2 : 2 * num + 4]
    ring_send, ring_recv, pair_send, pair_recv, own_sem, part_send, part_recv, part_own = refs[
        2 * num + 4 :
    ]
    me = lax.axis_index("clip")
    band = lax.axis_index("band")
    core = band % 2
    place = ring_place(me, count)
    onward = 1 - 2 * core
    following = (ring_clip((place + onward + count) % count, count), band)
    partner = (me, band + 1 - 2 * core)
    peers = [((me + step) % count, band) for step in range(1, count)]
    greet(peers + [partner])

    def block(ref, group, owner):
        rows, cols = shapes[group]
        return ref.at[
            pl.ds(pl.multiple_of(owner * rows, rows), rows),
            pl.ds(pl.multiple_of(core * (cols // 2), 128), cols // 2),
        ]

    def ring_copy(group, step):
        owner = ring_clip((place - onward * step + 2 * count) % count, count)
        there = block(full[group], group, owner)
        return pltpu.make_async_remote_copy(
            there, there, ring_send.at[step, group], ring_recv.at[step, group], following, MESH
        )

    def pair_copy(group, step):
        owner = ring_clip((place - onward * (step + 1) + 2 * count) % count, count)
        there = block(full[group], group, owner)
        return pltpu.make_async_remote_copy(
            there, there, pair_send.at[step, group], pair_recv.at[step, group], partner, MESH
        )

    def own_copy(group):
        rows, cols = shapes[group]
        return pltpu.make_async_copy(
            shards[group],
            full[group].at[pl.ds(pl.multiple_of(me * rows, rows), rows), :],
            own_sem.at[group],
        )

    parts = []
    for step, peer in enumerate(peers):
        for which, (src, dst) in enumerate(((vec_ref, vec_out), (text_ref, text_out))):
            parts.append(
                pltpu.make_async_remote_copy(
                    src.at[peer[0]],
                    dst.at[me],
                    part_send.at[which, step],
                    part_recv.at[which, step],
                    peer,
                    MESH,
                )
            )
    parts_own = [
        pltpu.make_async_copy(src.at[me], dst.at[me], part_own.at[which])
        for which, (src, dst) in enumerate(((vec_ref, vec_out), (text_ref, text_out)))
    ]
    for group in range(num):
        rows, cols = shapes[group]
        own_copy(group).start()
        pltpu.make_async_remote_copy(
            shards[group].at[:, pl.ds(pl.multiple_of(core * (cols // 2), 128), cols // 2)],
            block(full[group], group, me),
            ring_send.at[0, group],
            ring_recv.at[0, group],
            following,
            MESH,
        ).start()
    for copy in parts_own + parts:
        copy.start()

    @pl.loop(1, count - 1)
    def _(step):
        for group in range(num):
            ring_copy(group, step - 1).wait_recv()
            ring_copy(group, step).start()
            pair_copy(group, step - 1).start()

    for group in range(num):
        ring_copy(group, count - 2).wait_recv()
        pair_copy(group, count - 2).start()
    for copy in parts_own + parts:
        copy.wait()
    for group in range(num):
        own_copy(group).wait()

    @pl.loop(0, count - 1)
    def _(step):
        for group in range(num):
            ring_copy(group, step).wait_send()
            pair_copy(group, step).wait()


def gather_quarters(shard):
    band_count = lax.axis_size("band")
    rows = shard.shape[0] // band_count
    own = lax.dynamic_slice_in_dim(shard, lax.axis_index("band") * rows, rows, 0)
    return lax.all_gather(own.astype(jnp.bfloat16), ("clip", "band"), axis=0, tiled=True)


def sum_rows(left, right):
    part = lax.psum_scatter(
        matmul_tn(left, right), ("clip", "band"), scatter_dimension=0, tiled=True
    )
    return lax.all_gather(part, "band", axis=0, tiled=True)


def gather_weights(shards, vectors, texts):
    count = lax.axis_size("clip")
    num = len(shards)
    steps = pltpu.SemaphoreType.DMA((count - 1, num))
    out = pl.pallas_call(
        partial(gather_kernel, count, [shard.shape for shard in shards]),
        out_shape=tuple(
            jax.ShapeDtypeStruct((count * s.shape[0], s.shape[1]), s.dtype) for s in shards
        )
        + tuple(jax.ShapeDtypeStruct(v.shape, v.dtype) for v in (vectors, texts)),
        in_specs=[ANY] * (num + 2),
        out_specs=(ANY,) * (num + 2),
        scratch_shapes=[
            steps,
            steps,
            steps,
            steps,
            pltpu.SemaphoreType.DMA((num,)),
            pltpu.SemaphoreType.DMA((2, count - 1)),
            pltpu.SemaphoreType.DMA((2, count - 1)),
            pltpu.SemaphoreType.DMA((2,)),
        ],
        compiler_params=pltpu.CompilerParams(collective_id=1, has_side_effects=True),
        cost_estimate=pl.CostEstimate(flops=2 * 10**11, bytes_accessed=6 * 10**8, transcendentals=0),
    )(*shards, vectors, texts)
    return out[:num], out[num], out[num + 1]


WIRE_MAX = 32767.0
WIRE_LEAST = 1e-30
UNIT = (128, 512)


def unit_parts(kind, first):
    if kind == 0:
        return ((0, 4, lambda u: u, lambda u: 0), (4, 4, lambda u: 4, lambda u: u - 3))
    return ((first, 3 - first, lambda u: u, lambda u: u), (3, 3, lambda u: 3, lambda u: u))


def reduce_kernel(count, tokens, phases, *refs):
    num = sum(len(phase["lefts"]) for phase in phases)
    lefts, rights = refs[:num], refs[num : 2 * num]
    wide_out, deep_out, square_out = refs[2 * num : 2 * num + 3]
    left_far, right_far = refs[2 * num + 3 : 3 * num + 3], refs[3 * num + 3 : 4 * num + 3]
    scratch = refs[4 * num + 3 :]
    left_buf, right_buf, got_low, got_scale, put_low, put_scale, plane_put = (
        scratch[2 * i : 2 * i + 2] for i in range(7)
    )
    plane_got = scratch[14 : 14 + len(phases)]
    (
        square_buf,
        left_sem,
        right_sem,
        pair_send,
        pair_recv,
        half_send,
        half_recv,
        ring_send,
        ring_recv,
        credit,
        plane_send,
        plane_recv,
        out_sem,
        out_send,
        out_recv,
    ) = scratch[14 + len(phases) :]
    me = lax.axis_index("clip")
    band = lax.axis_index("band")
    core = band % 2
    plane = band // 2
    place = ring_place(me, count)
    onward = 1 - 2 * core
    following = (ring_clip((place + onward + count) % count, count), band)
    preceding = (ring_clip((place - onward + count) % count, count), band)
    partner = (me, band + 1 - 2 * core)
    mirror = (me, band + 2 - 4 * plane)
    greet([following, preceding, partner, mirror])

    def owner_at(step, way):
        return ring_clip((place - way * (step + 1) + 2 * count) % count, count)

    def left_blocks(at):
        phase = phases[at]
        if phase["kind"] == 0:
            return [(b, phase["lefts"][0], b, 4) for b in range(4)] + [(4, phase["lefts"][1], 0, 1)]
        first = phase["first"]
        return [(first + i, left, 0, 1) for i, left in enumerate(phase["lefts"])]

    def right_blocks(at):
        phase = phases[at]
        if phase["kind"] == 0:
            return [(0, phase["lefts"][0], 0)] + [(1 + i, phase["lefts"][1], i) for i in range(4)]
        first = phase["first"]
        return [(first + i, phase["lefts"][i], 0) for i in range(3 - first)] + [
            (3 + i, phase["lefts"][-1], i) for i in range(3)
        ]

    def left_cols(step, way, which, many):
        width = lefts_width // count if many == 1 else deep_width // count
        start = owner_at(step, way) * width + which * 128
        return pl.ds(pl.multiple_of(start, 128), 128)

    lefts_width = wide_out.shape[0] * count
    deep_width = deep_out.shape[0] * count

    def pair_left(at, step):
        out = []
        for block, operand, which, many in left_blocks(at):
            cols = left_cols(step, -onward, which, many)
            out.append(
                pltpu.make_async_remote_copy(
                    lefts[operand].at[:, cols],
                    left_far[operand].at[:, cols],
                    pair_send.at[at, block, step],
                    pair_recv.at[at, block, step],
                    partner,
                    MESH,
                )
            )
        return out

    def pair_right(at):
        out = []
        for i, operand in enumerate(phases[at]["lefts"]):
            half = rights[operand].shape[1] // 2
            out.append(
                pltpu.make_async_remote_copy(
                    rights[operand].at[:, pl.ds(pl.multiple_of((1 - core) * half, 128), half)],
                    right_far[operand],
                    half_send.at[operand],
                    half_recv.at[operand],
                    partner,
                    MESH,
                )
            )
        return out

    def load_left(at, step, slot, far):
        kind = phases[at]["kind"]
        out = []
        for block, operand, which, many in left_blocks(at):
            cols = left_cols(step, onward, which, many)
            source = left_far if far else lefts
            out.append(
                pltpu.make_async_copy(
                    source[operand].at[:, cols],
                    left_buf[kind].at[slot, block, pl.ds(far * tokens, tokens), :],
                    left_sem.at[kind, slot, block, far],
                )
            )
        return out

    def load_right(at, far):
        kind = phases[at]["kind"]
        out = []
        for block, operand, which in right_blocks(at):
            if far:
                source = right_far[operand].at[:, pl.ds(which * UNIT[1], UNIT[1])]
            else:
                half = rights[operand].shape[1] // 2
                start = pl.multiple_of(core * half + which * UNIT[1], 128)
                source = rights[operand].at[:, pl.ds(start, UNIT[1])]
            out.append(
                pltpu.make_async_copy(
                    source,
                    right_buf[kind].at[block, pl.ds(far * tokens, tokens), :],
                    right_sem.at[kind, block, far],
                )
            )
        return out

    def ring_copies(at, part, slot):
        kind = phases[at]["kind"]
        start, many = unit_parts(kind, phases[at]["first"])[part][:2]
        units = pl.ds(start, many)
        return [
            pltpu.make_async_remote_copy(
                put.at[slot, units],
                got.at[slot, units],
                ring_send.at[kind, slot, part, i],
                ring_recv.at[kind, slot, part, i],
                following,
                MESH,
            )
            for i, (put, got) in enumerate(
                ((put_low[kind], got_low[kind]), (put_scale[kind], got_scale[kind]))
            )
        ]

    def plane_copy(at, part):
        kind = phases[at]["kind"]
        start, many = unit_parts(kind, phases[at]["first"])[part][:2]
        units = pl.ds(start, many)
        return pltpu.make_async_remote_copy(
            plane_put[kind].at[units],
            plane_got[at].at[units],
            plane_send.at[at, part],
            plane_recv.at[at, part],
            mirror,
            MESH,
        )

    def out_copies(at, unit):
        phase = phases[at]
        if phase["kind"] == 0 and unit < 4:
            half = UNIT[1]
            rows = deep_out.shape[0] // 4
            there = deep_out.at[
                pl.ds(unit * rows, rows),
                pl.ds(pl.multiple_of(phase["cols"][0] + core * half, 128), half),
            ]
        else:
            which, col = (1, unit - 4) if phase["kind"] == 0 else (unit - phase["first"], 0)
            if phase["kind"] and unit >= 3:
                which, col = len(phase["lefts"]) - 1, unit - 3
            half = rights[phase["lefts"][which]].shape[1] // 2
            start = phase["cols"][which] + core * half + col * UNIT[1]
            there = wide_out.at[:, pl.ds(pl.multiple_of(start, 128), UNIT[1])]
        here = plane_got[at].at[unit]
        return (
            pltpu.make_async_copy(here, there, out_sem.at[at, unit]),
            pltpu.make_async_remote_copy(
                here, there, out_send.at[at, unit], out_recv.at[at, unit], partner, MESH
            ),
        )

    def product(kind, slot, left, right):
        return lax.dot_general(
            left_buf[kind][slot, left],
            right_buf[kind][right],
            (((0,), (0,)), ((), ())),
            preferred_element_type=jnp.float32,
        )

    def start(copies):
        for copy in copies:
            copy.start()

    def finish(copies):
        for copy in copies:
            copy.wait()

    def take_step(at, step, first, last):
        phase = phases[at]
        kind = phase["kind"]
        slot = step % 2
        before = (step + 1) % 2
        for far in range(2):
            finish(load_left(at, step, slot, far))
        if not last:
            for copy in pair_left(at, step + 1):
                copy.wait_recv()
            for far in range(2):
                start(load_left(at, step + 1, before, far))
        for part, (low, many, left_of, right_of) in enumerate(unit_parts(kind, phase["first"])):
            if not first:
                for copy in ring_copies(at, part, before):
                    copy.wait_recv()
            if not (first or last):

                @pl.when(step >= 2)
                def _(part=part):
                    for copy in ring_copies(at, part, slot):
                        copy.wait_send()
                    pl.semaphore_wait(credit.at[kind, part], 1)

            @pl.loop(low, low + many)
            def _(unit, left_of=left_of, right_of=right_of):
                term = product(kind, slot, left_of(unit), right_of(unit))
                if not first:
                    came = got_low[kind][before, unit].astype(jnp.float32)
                    term = term + came * got_scale[kind][before, unit]
                if last:
                    plane_put[kind][unit] = term
                else:
                    largest = jnp.max(jnp.abs(term), axis=0, keepdims=True)
                    largest = jnp.maximum(largest, WIRE_LEAST)
                    factor = WIRE_MAX / largest
                    put_low[kind][slot, unit] = jnp.round(term * factor).astype(jnp.int16)
                    put_scale[kind][slot, unit] = largest * (1.0 / WIRE_MAX)

            if last:
                plane_copy(at, part).start()
            else:
                start(ring_copies(at, part, slot))
            if not (first or last):

                @pl.when(step < count - 2)
                def _(part=part):
                    pl.semaphore_signal(
                        credit.at[kind, part], inc=1, device_id=preceding, device_id_type=MESH
                    )

    def close(at):
        kind = phases[at]["kind"]
        for part, (low, many, _, _) in enumerate(unit_parts(kind, phases[at]["first"])):
            plane_copy(at, part).wait()

            @pl.loop(low, low + many)
            def _(unit):
                total = plane_put[kind][unit] + plane_got[at][unit]
                plane_got[at][unit] = total
                square_buf[...] += jnp.sum(
                    (total * total).reshape(UNIT[0] // 8, 8, UNIT[1]), axis=0
                )

            for unit in range(low, low + many):
                start(out_copies(at, unit))

    square_buf[...] = jnp.zeros_like(square_buf)
    start(load_right(0, 0))
    start(pair_right(0))

    @pl.loop(0, count)
    def _(step):
        start(pair_left(0, step))

    start(load_left(0, 0, 0, 0))
    for at in range(len(phases)):
        if at == 0:
            for copy in pair_right(0):
                copy.wait_recv()
            start(load_right(0, 1))
            for copy in pair_left(0, 0):
                copy.wait_recv()
            start(load_left(0, 0, 0, 1))
        for far in range(2):
            finish(load_right(at, far))
        more = at + 1 < len(phases)
        if more:
            start(pair_right(at + 1))
            start(load_right(at + 1, 0))
        take_step(at, 0, True, False)
        if more:
            start(pair_left(at + 1, 0))

        @pl.loop(1, count - 1)
        def _(step, at=at, more=more):
            take_step(at, step, False, False)
            if more:
                start(pair_left(at + 1, step))

        if more:
            start(pair_left(at + 1, count - 1))
            for copy in pair_right(at + 1):
                copy.wait_recv()
            start(load_right(at + 1, 1))
            for copy in pair_left(at + 1, 0):
                copy.wait_recv()
            for far in range(2):
                start(load_left(at + 1, 0, 0, far))
        take_step(at, count - 1, False, True)
        for part in range(2):
            for slot in range(2):
                for copy in ring_copies(at, part, slot):
                    copy.wait_send()
        if at:
            close(at - 1)
    close(len(phases) - 1)
    square_out[...] = square_buf[...]
    for at, phase in enumerate(phases):
        for copy in pair_right(at):
            copy.wait_send()

        @pl.loop(0, count)
        def _(step, at=at):
            for copy in pair_left(at, step):
                copy.wait_send()

        for unit in range(phase["first"], 8 if phase["kind"] == 0 else 6):
            finish(out_copies(at, unit))


def reduce_gradients(phases, lefts, rights, wide_shape, deep_shape):
    count = lax.axis_size("clip")
    tokens = lefts[0].shape[0]
    num = len(lefts)
    dma = pltpu.SemaphoreType.DMA
    units, lefts_of, rights_of = (8, 6), (5, 4), (5, 6)
    scratch = [pltpu.VMEM((2, lefts_of[k], 2 * tokens, 128), jnp.bfloat16) for k in range(2)]
    scratch += [pltpu.VMEM((rights_of[k], 2 * tokens, UNIT[1]), jnp.bfloat16) for k in range(2)]
    for _ in range(2):
        scratch += [pltpu.VMEM((2, units[k]) + UNIT, jnp.int16) for k in range(2)]
        scratch += [pltpu.VMEM((2, units[k], 1, UNIT[1]), jnp.float32) for k in range(2)]
    scratch += [pltpu.VMEM((units[k],) + UNIT, jnp.float32) for k in range(2)]
    scratch += [pltpu.VMEM((units[p["kind"]],) + UNIT, jnp.float32) for p in phases]
    scratch += [
        pltpu.VMEM((8, UNIT[1]), jnp.float32),
        dma((2, 2, 5, 2)),
        dma((2, 6, 2)),
        dma((len(phases), 5, count)),
        dma((len(phases), 5, count)),
        dma((num,)),
        dma((num,)),
        dma((2, 2, 2, 2)),
        dma((2, 2, 2, 2)),
        pltpu.SemaphoreType.REGULAR((2, 2)),
        dma((len(phases), 2)),
        dma((len(phases), 2)),
        dma((len(phases), 8)),
        dma((len(phases), 8)),
        dma((len(phases), 8)),
    ]
    out = pl.pallas_call(
        partial(reduce_kernel, count, tokens, phases),
        out_shape=(
            jax.ShapeDtypeStruct(wide_shape, jnp.float32),
            jax.ShapeDtypeStruct(deep_shape, jnp.float32),
            jax.ShapeDtypeStruct((8, UNIT[1]), jnp.float32),
        )
        + tuple(jax.ShapeDtypeStruct(x.shape, x.dtype) for x in lefts)
        + tuple(jax.ShapeDtypeStruct((tokens, x.shape[1] // 2), x.dtype) for x in rights),
        in_specs=[ANY] * (2 * num),
        out_specs=(ANY, ANY, pl.BlockSpec(memory_space=pltpu.VMEM)) + (ANY,) * (2 * num),
        scratch_shapes=scratch,
        compiler_params=pltpu.CompilerParams(
            collective_id=2, has_side_effects=True, vmem_limit_bytes=58 << 20
        ),
        cost_estimate=pl.CostEstimate(flops=3 * 10**11, bytes_accessed=8 * 10**8, transcendentals=0),
    )(*lefts, *rights)
    return out[:3]


def per_device(
    latents,
    noise_field,
    timesteps,
    null_flags,
    frame_mask,
    context,
    w_wide,
    m_wide,
    v_wide,
    w_deep,
    m_deep,
    v_deep,
    w_small,
    m_small,
    v_small,
):
    clip_count = lax.axis_size("clip")
    band_count = lax.axis_size("band")
    clip_at = lax.axis_index("clip")
    band_at = lax.axis_index("band")
    wide_rows = w_wide.shape[0]
    deep_rows = w_deep.shape[0]
    text_len, text_dim = context.shape[1:]
    facts = jnp.pad(
        jnp.concatenate([timesteps, frame_mask[0]])[None],
        ((0, 7), (0, 127 - frame_mask.shape[1])),
    )
    kept_text = context[0] * (1 - null_flags[0]).astype(jnp.bfloat16)
    text_cols = jnp.pad(
        kept_text.reshape(text_len, clip_count, deep_rows).transpose(1, 0, 2),
        ((0, 0), (0, TEXT_PAD - text_len), (0, 0)),
    )
    all_facts, all_text = exchange_facts(facts, text_cols)
    all_times = all_facts[:, 0, 0].astype(jnp.float32)
    all_time_low = jax.nn.silu(time_features(all_times)).astype(jnp.bfloat16)
    time_rows = lax.dynamic_slice(
        all_time_low, (0, clip_at * wide_rows), (clip_count, wide_rows)
    )
    part_modul = matmul(time_rows, w_wide[:, : 12 * D].astype(jnp.bfloat16))
    kv_cols = 2 * D // band_count
    kv_weight = lax.dynamic_slice(
        w_deep, (0, D + band_at * kv_cols), (deep_rows, kv_cols)
    ).astype(jnp.bfloat16)
    part_kv = matmul(all_text.reshape(clip_count * TEXT_PAD, deep_rows), kv_weight)
    edges = (12 * D, 15 * D, 18 * D, 19 * D, 20 * D, 21 * D, 22 * D, 22 * D + FF)
    shards = [w_wide[:, low:high].astype(jnp.bfloat16) for low, high in zip(edges, edges[1:])]
    shards += [w_deep[:, :D].astype(jnp.bfloat16)]
    up_b_w = gather_quarters(w_wide[:, 22 * D + FF :])
    down_b_w = gather_quarters(w_deep[:, 3 * D :])
    gathered, all_modul, all_kv = gather_weights(
        shards,
        part_modul.reshape(clip_count, 12 * D // 128, 128),
        part_kv.reshape(clip_count, TEXT_PAD, kv_cols),
    )
    (
        qkv_a_w,
        qkv_b_w,
        out_a_w,
        out_b_w,
        query_w,
        cross_out_w,
        up_a_w,
        down_a_w,
    ) = gathered
    keyval = lax.all_gather(jnp.sum(all_kv, 0).astype(jnp.bfloat16), "band", axis=1, tiled=True)
    keyval = keyval[:text_len]
    small_low = w_small.astype(jnp.bfloat16)
    small_val = small_low.astype(jnp.float32)
    num_frames, num_rows, num_cols = (latents.shape[1], latents.shape[2], latents.shape[3])
    grid_shape = (num_frames, num_rows, num_cols)
    tok_count = num_frames * num_rows * num_cols
    all_mask = all_facts[:, 0, 1 : 1 + num_frames]
    global_count = jnp.sum(all_mask).astype(jnp.float32) * (num_rows * num_cols * CH * band_count)
    time_value = timesteps[0].astype(jnp.float32)
    noise_angle = 0.5 * math.pi * time_value / TMAX
    signal, spread = (jnp.cos(noise_angle), jnp.sin(noise_angle))
    clean_tok = latents[0].reshape(tok_count, CH)
    noise_tok = noise_field[0].reshape(tok_count, CH)
    noisy_low = (signal * clean_tok + spread * noise_tok).astype(jnp.bfloat16)
    target = signal * noise_tok - spread * clean_tok
    modulation = jnp.sum(all_modul, 0).reshape(12, D)
    mod_a, mod_b = (modulation[:6], modulation[6:])
    stream_zero = matmul(noisy_low, small_low[:CH]) + small_val[2 * CH]
    normed_a, back_a = jax.vjp(norm_modulated, stream_zero, mod_a[0], mod_a[1])
    in_a = normed_a.astype(jnp.bfloat16)
    spatial = (1, num_rows, SPACE)
    qkv_a = (
        matmul(in_a, qkv_a_w).astype(jnp.bfloat16).reshape(num_frames, num_rows, num_cols, 3 * D)
    )
    blocks_a = to_windows(qkv_a, spatial)
    partner = from_partner(blocks_a[..., D:], "band", 0)
    keys_all = jnp.concatenate([blocks_a[..., D:], partner], 1)
    space_q = split_heads(blocks_a[..., :D])
    space_k = split_heads(keys_all[..., :D])
    space_v = split_heads(keys_all[..., D:])
    space_out, space_total = attend_forward(space_q, space_k, space_v, SELF_FORMS)
    att_a = from_windows(merge_heads(space_out.astype(jnp.bfloat16)), grid_shape, spatial).reshape(
        tok_count, D
    )
    proj_a = matmul(att_a, out_a_w)
    stream_one = stream_zero + mod_a[2] * proj_a
    stream_two, saved_a = mlp_forward(stream_one, mod_a, up_a_w, down_a_w)
    normed_b, back_b = jax.vjp(norm_modulated, stream_two, mod_b[0], mod_b[1])
    token_grid = normed_b.astype(jnp.bfloat16).reshape(num_frames, num_rows, num_cols, D)
    arrived = shifted(token_grid[:, :SHIFT], "band", -1)
    rolled = jnp.concatenate([token_grid[:, SHIFT:], arrived], 1).reshape(tok_count, D)
    temporal = (num_frames, WIN, WIN)
    qkv_b = matmul(rolled, qkv_b_w).astype(jnp.bfloat16)
    blocks_b = to_windows(qkv_b.reshape(num_frames, num_rows, num_cols, 3 * D), temporal)
    win_q = split_heads(blocks_b[..., :D])
    win_k = split_heads(blocks_b[..., D : 2 * D])
    win_v = split_heads(blocks_b[..., 2 * D :])
    win_out, win_total = attend_forward(win_q, win_k, win_v, SELF_FORMS)
    out_grid = from_windows(merge_heads(win_out.astype(jnp.bfloat16)), grid_shape, temporal)
    returned = shifted(out_grid[:, num_rows - SHIFT :], "band", 1)
    att_b = jnp.concatenate([returned, out_grid[:, : num_rows - SHIFT]], 1).reshape(tok_count, D)
    proj_b = matmul(att_b, out_b_w)
    stream_three = stream_two + mod_b[2] * proj_b
    cross_val, cross_back = jax.vjp(norm_gained, stream_three, small_val[2 * CH + 1])
    cross_in = cross_val.astype(jnp.bfloat16)
    query_proj = matmul(cross_in, query_w).astype(jnp.bfloat16)
    cross_q = split_heads(query_proj)
    cross_k = split_heads(keyval[:, :D])
    cross_v = split_heads(keyval[:, D:])
    cross_out, cross_total = attend_forward(cross_q, cross_k, cross_v, CROSS_FORMS)
    crossed = merge_heads(cross_out.astype(jnp.bfloat16))
    stream_four = stream_three + matmul(crossed, cross_out_w)
    stream_five, saved_b = mlp_forward(stream_four, mod_b, up_b_w, down_b_w)
    final_val, final_back = jax.vjp(norm_gained, stream_five, small_val[2 * CH + 2])
    final_low = final_val.astype(jnp.bfloat16)
    head_low = small_low[CH : 2 * CH]
    predicted = matmul_nt(final_low, head_low)
    weight_row = jnp.repeat(frame_mask[0].astype(jnp.float32), num_rows * num_cols)[:, None]
    pred_error = predicted - target
    loss_part = jnp.sum(weight_row * pred_error * pred_error)
    grad_pred = (weight_row * pred_error * (2.0 / global_count)).astype(jnp.bfloat16)
    grad_head = matmul_tn(grad_pred, final_low)
    grad_stream, grad_gain_f = final_back(matmul(grad_pred, head_low))
    grad_stream, mlp_factors_b, extra_b = mlp_backward(
        grad_stream, mod_b, up_b_w, down_b_w, saved_b
    )
    grad_cross = grad_stream.astype(jnp.bfloat16)
    grad_crossed = split_heads(matmul_nt(grad_cross, cross_out_w).astype(jnp.bfloat16))
    cq_grad, ck_grad, cv_grad = attend_backward(
        cross_q, cross_k, cross_v, cross_total, grad_crossed, CROSS_FORMS
    )
    grad_query = merge_heads(cq_grad).astype(jnp.bfloat16)
    grad_part, grad_gain_c = cross_back(matmul_nt(grad_query, query_w))
    grad_keyval = jnp.concatenate([merge_heads(ck_grad), merge_heads(cv_grad)], 1)
    grad_keyval = jnp.pad(grad_keyval, ((0, TEXT_PAD - text_len), (0, 0)))
    grad_keyval = lax.psum_scatter(grad_keyval, "band", scatter_dimension=1, tiled=True)
    grad_keyval = lax.all_gather(grad_keyval, "clip", axis=0, tiled=True)
    grad_w_ckv = matmul_tn(
        all_text.reshape(clip_count * TEXT_PAD, deep_rows).astype(jnp.float32),
        grad_keyval,
        lax.Precision.HIGHEST,
    )
    grad_w_ckv = lax.all_gather(grad_w_ckv, "band", axis=1, tiled=True)
    grad_stream = grad_stream + grad_part
    grad_proj = (mod_b[2] * grad_stream).astype(jnp.bfloat16)
    grad_gate_b = jnp.sum(grad_stream * proj_b, 0)
    factors_ob = (att_b, grad_proj)
    grad_att = (
        matmul_nt(grad_proj, out_b_w)
        .astype(jnp.bfloat16)
        .reshape(num_frames, num_rows, num_cols, D)
    )
    fetched = shifted(grad_att[:, :SHIFT], "band", -1)
    grad_rolled = jnp.concatenate([grad_att[:, SHIFT:], fetched], 1)
    grad_win = split_heads(to_windows(grad_rolled, temporal))
    wq_grad, wk_grad, wv_grad = attend_backward(
        win_q, win_k, win_v, win_total, grad_win, SELF_FORMS
    )
    grad_blocks = jnp.concatenate(
        [merge_heads(wq_grad), merge_heads(wk_grad), merge_heads(wv_grad)], -1
    )
    grad_qkv = (
        from_windows(grad_blocks, grid_shape, temporal)
        .reshape(tok_count, 3 * D)
        .astype(jnp.bfloat16)
    )
    factors_qkvb = (rolled, grad_qkv)
    grad_in_roll = matmul_nt(grad_qkv, qkv_b_w).reshape(num_frames, num_rows, num_cols, D)
    sent_back = shifted(grad_in_roll[:, num_rows - SHIFT :], "band", 1)
    grad_normed = jnp.concatenate([sent_back, grad_in_roll[:, : num_rows - SHIFT]], 1).reshape(
        tok_count, D
    )
    grad_part, grad_shift_b, grad_scale_b = back_b(grad_normed)
    grad_stream = grad_stream + grad_part
    grad_stream, mlp_factors_a, extra_a = mlp_backward(
        grad_stream, mod_a, up_a_w, down_a_w, saved_a
    )
    grad_proj = (mod_a[2] * grad_stream).astype(jnp.bfloat16)
    grad_gate_a = jnp.sum(grad_stream * proj_a, 0)
    factors_oa = (att_a, grad_proj)
    grad_att = (
        matmul_nt(grad_proj, out_a_w)
        .astype(jnp.bfloat16)
        .reshape(num_frames, num_rows, num_cols, D)
    )
    grad_space = split_heads(to_windows(grad_att, spatial))
    sq_grad, sk_grad, sv_grad = attend_backward(
        space_q, space_k, space_v, space_total, grad_space, SELF_FORMS
    )
    half_len = space_q.shape[1]
    key_grads = merge_heads(sk_grad)
    value_grads = merge_heads(sv_grad)
    back_keys, back_values = from_partner(
        (key_grads[:, half_len:], value_grads[:, half_len:]), "band", 0
    )
    grad_blocks = jnp.concatenate(
        [
            merge_heads(sq_grad),
            key_grads[:, :half_len] + back_keys,
            value_grads[:, :half_len] + back_values,
        ],
        -1,
    )
    grad_qkv = (
        from_windows(grad_blocks, grid_shape, spatial)
        .reshape(tok_count, 3 * D)
        .astype(jnp.bfloat16)
    )
    factors_qkva = (in_a, grad_qkv)
    grad_part, grad_shift_a, grad_scale_a = back_a(matmul_nt(grad_qkv, qkv_a_w))
    grad_stream = grad_stream + grad_part
    grad_patch = matmul_tn(noisy_low.astype(jnp.float32), grad_stream, lax.Precision.HIGHEST)
    grad_bias = jnp.sum(grad_stream, 0)
    grad_modul = jnp.stack(
        [
            grad_shift_a,
            grad_scale_a,
            grad_gate_a,
            extra_a[0],
            extra_a[1],
            extra_a[2],
            grad_shift_b,
            grad_scale_b,
            grad_gate_b,
            extra_b[0],
            extra_b[1],
            extra_b[2],
        ]
    ).reshape(1, 12 * D)
    grad_small = jnp.concatenate(
        [grad_patch, grad_head, grad_bias[None], grad_gain_c[None], grad_gain_f[None]], 0
    )
    all_grad_modul = lax.all_gather(lax.psum(grad_modul, "band"), "clip", axis=0, tiled=True)
    grad_w_ada = matmul_tn(time_rows.astype(jnp.float32), all_grad_modul, lax.Precision.HIGHEST)
    down_b_sum, up_b_sum = (sum_rows(*pair) for pair in mlp_factors_b)
    factors = ((crossed, grad_cross), (cross_in, grad_query), factors_ob, factors_qkvb)
    factors += mlp_factors_a + (factors_oa, factors_qkva)
    square_part = (jnp.sum(down_b_sum**2) + jnp.sum(up_b_sum**2)) / band_count
    if wide_rows == 128 and deep_rows == 512:
        phases = (
            {"kind": 1, "first": 0, "lefts": (0, 1, 2, 3), "cols": (9 * D, 8 * D, 7 * D, 3 * D)},
            {"kind": 0, "first": 0, "lefts": (4, 5), "cols": (0, 10 * D)},
            {"kind": 1, "first": 2, "lefts": (6, 7), "cols": (6 * D, 0)},
        )
        wide_rest, down_a_sum, squares = reduce_gradients(
            phases,
            [f[0] for f in factors],
            [f[1] for f in factors],
            (wide_rows, 10 * D + FF),
            (deep_rows, D),
        )
        square_part += jnp.sum(squares) / (band_count // 2)
    else:
        summed = [sum_rows(*pair) for pair in factors]
        wide_rest = jnp.concatenate([summed[i] for i in (7, 3, 6, 2, 1, 0, 5)], 1)
        down_a_sum = summed[4]
        square_part += (jnp.sum(wide_rest**2) + jnp.sum(down_a_sum**2)) / band_count
    wide_sum = jnp.concatenate([grad_w_ada, wide_rest, up_b_sum], 1)
    deep_sum = jnp.concatenate([down_a_sum, grad_w_ckv, down_b_sum], 1)
    square_part += (jnp.sum(grad_w_ada**2) + jnp.sum(grad_w_ckv**2)) / band_count
    loss_sum, square_sum, small_sum = lax.psum(
        (loss_part, square_part, grad_small), ("clip", "band")
    )
    grad_norm = jnp.sqrt(square_sum + jnp.sum(small_sum * small_sum))
    factor = CLIP_MAX / jnp.maximum(grad_norm, CLIP_MAX)
    new_wide = adam_update(w_wide, m_wide, v_wide, wide_sum * factor, 0.15)
    new_deep = adam_update(w_deep, m_deep, v_deep, deep_sum * factor, 0.05)
    new_small = adam_update(w_small, m_small, v_small, small_sum * factor, 0.5)
    loss = loss_sum / global_count
    return (
        loss,
        grad_norm,
        new_wide[0],
        new_wide[1],
        new_wide[2],
        new_deep[0],
        new_deep[1],
        new_deep[2],
        new_small[0],
        new_small[1],
        new_small[2],
    )


def solution(mesh):
    in_specs = (
        P("clip", None, "band", None, None),
        P("clip", None, "band", None, None),
        P("clip"),
        P("clip"),
        P("clip", None),
        P("clip", None, None),
        P("clip", None),
        P("clip", None),
        P("clip", None),
        P("clip", None),
        P("clip", None),
        P("clip", None),
        P(),
        P(),
        P(),
    )
    out_specs = (
        P(),
        P(),
        P("clip", None),
        P("clip", None),
        P("clip", None),
        P("clip", None),
        P("clip", None),
        P("clip", None),
        P(),
        P(),
        P(),
    )
    return jax.shard_map(
        per_device, mesh=mesh, in_specs=in_specs, out_specs=out_specs, check_vma=False
    )
```

```python
from functools import partial
import math

import jax
import jax.numpy as jnp
from jax import lax
from jax.experimental import pallas as pl
from jax.experimental.pallas import tpu as pltpu
from jax.sharding import PartitionSpec as P

D = 1024
HEADS = 16
HEAD_DIM = 64
FF = 4096
CH = 8
SPACE = 16
WIN = 8
SHIFT = 4
TMAX = 1000
STEP = 10


EPS_NORM = 1e-06
CLIP_MAX = 0.001
BETA_ONE = 0.9
BETA_TWO = 0.95
ADAM_EPS = 1e-08
DECAY = 0.1


def from_partner(block, axis, distance):
    count = lax.axis_size(axis)
    route = []
    for low in range(count):
        high = low | 1 << distance
        if high != low and high < count:
            route += [(low, high), (high, low)]
    return lax.ppermute(block, axis, route)


def shifted(value, axis, by):
    length = lax.axis_size(axis)
    return lax.ppermute(value, axis, [(i, (i + by) % length) for i in range(length)])


def matmul(left_op, right_op):
    return jnp.dot(left_op, right_op, preferred_element_type=jnp.float32)


def matmul_tn(left_op, right_op, precision=None):
    return lax.dot_general(
        left_op,
        right_op,
        (((0,), (0,)), ((), ())),
        precision=precision,
        preferred_element_type=jnp.float32,
    )


def matmul_nt(left_op, right_op):
    return lax.dot_general(
        left_op, right_op, (((1,), (1,)), ((), ())), preferred_element_type=jnp.float32
    )


def layer_norm(field_in):
    average = jnp.mean(field_in, -1, keepdims=True)
    centred = field_in - average
    return centred * lax.rsqrt(jnp.mean(centred * centred, -1, keepdims=True) + EPS_NORM)


def norm_modulated(field_in, shift_vec, scale_vec):
    return layer_norm(field_in) * (1.0 + scale_vec) + shift_vec


def norm_gained(field_in, gain_vec):
    return layer_norm(field_in) * gain_vec


def time_features(time_value):
    half_width = D // 2
    frequency = jnp.exp(-math.log(10000.0) * jnp.arange(half_width, dtype=jnp.float32) / half_width)
    angles = time_value[..., None] * frequency
    return jnp.concatenate([jnp.cos(angles), jnp.sin(angles)], -1)


def token_order(grid):
    frames, rows, cols, width = grid.shape
    halves = grid.reshape(frames, rows, cols // WIN, WIN, width).transpose(2, 0, 1, 3, 4)
    return halves.reshape(frames * rows * cols, width)


def with_rows(tokens, first_rows, run):
    width = tokens.shape[1]
    runs = tokens.reshape(-1, run, width)
    return jnp.concatenate([first_rows, runs[:, first_rows.shape[1] :]], 1).reshape(-1, width)


def first_rows(tokens, run, part):
    return tokens.reshape(-1, run, tokens.shape[1])[:, :part]


def attend_pieces(tokens, frames, keys):
    if keys == "frame":
        run = tokens // (2 * frames)
        return [((f * run, run), (tokens // 2 + f * run, run)) for f in range(frames)]
    if keys == "half":
        return [((half * (tokens // 2), tokens // 2),) for half in range(2)]
    return [((0, tokens),)]


def take(ref, runs):
    pieces = [ref[low : low + many, :] for low, many in runs]
    return pieces[0] if len(pieces) == 1 else jnp.concatenate(pieces, 0)


def put(ref, cols, runs, value):
    done = 0
    for low, many in runs:
        ref[low : low + many, cols] = value[done : done + many].astype(ref.dtype)
        done += many


def softmax_rows(queries, keys, text_len):
    scores = matmul_nt(queries, keys)
    if text_len:
        place = lax.broadcasted_iota(jnp.int32, scores.shape, 1)
        scores = jnp.where(place < text_len, scores, -1e30)
    weight = jnp.exp(scores - jnp.max(scores, -1, keepdims=True))
    return weight / jnp.sum(weight, -1, keepdims=True)


def lanes_of(head, shape):
    lane = lax.broadcasted_iota(jnp.int32, shape, 1)
    return lane < HEAD_DIM if head == 0 else lane >= HEAD_DIM


def only(head, value):
    return jnp.where(lanes_of(head, value.shape), value, jnp.zeros_like(value))


def key_sets(key_refs, runs, text_len):
    if text_len:
        return key_refs[0][...]
    pieces = [take(ref, runs) for ref in key_refs]
    return pieces[0] if len(pieces) == 1 else jnp.concatenate(pieces, 0)


def attend_kernel(windows, text_len, sets, *refs):
    q_ref, k_refs, v_refs, out_ref = refs[0], refs[1 : 1 + sets], refs[1 + sets : 1 + 2 * sets], refs[-1]
    for runs in windows:
        queries = take(q_ref, runs) * HEAD_DIM ** (-0.5)
        keys, values = key_sets(k_refs, runs, text_len), key_sets(v_refs, runs, text_len)
        outs = []
        for head in range(2):
            probs = softmax_rows(only(head, queries), keys, text_len)
            outs.append(matmul(probs.astype(jnp.bfloat16), values))
        put(out_ref, slice(None), runs, jnp.where(lanes_of(0, outs[0].shape), *outs))


def attend_back_kernel(windows, text_len, sets, *refs):
    q_ref, k_refs, v_refs = refs[0], refs[1 : 1 + sets], refs[1 + sets : 1 + 2 * sets]
    grad_ref = refs[1 + 2 * sets]
    dq_ref = refs[2 + 2 * sets]
    own_ref = refs[3 + 2 * sets] if len(refs) > 3 + 2 * sets else None
    far_ref = refs[4 + 2 * sets] if sets == 2 else None
    pair = pl.program_id(0)
    cols = [pl.ds(pl.multiple_of(i * D + pair * 2 * HEAD_DIM, 128), 2 * HEAD_DIM) for i in range(3)]
    merged = dq_ref.shape[1] == 3 * D
    for runs in windows:
        queries = take(q_ref, runs) * HEAD_DIM ** (-0.5)
        keys, values = key_sets(k_refs, runs, text_len), key_sets(v_refs, runs, text_len)
        grad_out = take(grad_ref, runs)
        dq, dk, dv = [], [], []
        for head in range(2):
            probs = softmax_rows(only(head, queries), keys, text_len)
            dprobs = matmul_nt(only(head, grad_out), values)
            dv.append(matmul_tn(probs.astype(jnp.bfloat16), grad_out))
            inner = jnp.sum(probs * dprobs, -1, keepdims=True)
            dscores = (probs * (dprobs - inner)).astype(jnp.bfloat16)
            dq.append(matmul(dscores, keys))
            dk.append(matmul_tn(dscores, queries))
        dq, dk, dv = (jnp.where(lanes_of(0, x[0].shape), *x) for x in (dq, dk, dv))
        put(dq_ref, cols[0], runs, dq * HEAD_DIM ** (-0.5))
        if merged:
            put(dq_ref, cols[1], runs, dk)
            put(dq_ref, cols[2], runs, dv)
        elif text_len:
            own_ref[:, cols[0]] = dk
            own_ref[:, cols[1]] = dv
        else:
            half = dk.shape[0] // 2
            put(own_ref, cols[0], runs, dk[:half])
            put(own_ref, cols[1], runs, dv[:half])
            put(far_ref, cols[0], runs, dk[half:])
            put(far_ref, cols[1], runs, dv[half:])


def head_cols(array, first):
    return array, pl.BlockSpec((array.shape[0], 2 * HEAD_DIM), lambda h: (0, first + h))


def attention_operands(queries, key_values):
    ins = [head_cols(queries, 0)]
    ins += [head_cols(array, first) for array, first, _ in key_values]
    return ins + [head_cols(array, second) for array, _, second in key_values]


def attention_cost(tokens, keys, products):
    flops = 2 * products * tokens * keys * D * 2
    return pl.CostEstimate(
        flops=flops, bytes_accessed=tokens * D * 2 * 8, transcendentals=tokens * keys * HEADS
    )


def attend(queries, key_values, windows, text_len=0):
    tokens = queries.shape[0]
    ins = attention_operands(queries, key_values)
    return pl.pallas_call(
        partial(attend_kernel, windows, text_len, len(key_values)),
        grid=(HEADS // 2,),
        in_specs=[spec for _, spec in ins],
        out_specs=pl.BlockSpec((tokens, 2 * HEAD_DIM), lambda h: (0, h)),
        out_shape=jax.ShapeDtypeStruct((tokens, D), jnp.bfloat16),
        compiler_params=pltpu.CompilerParams(vmem_limit_bytes=40 << 20),
        cost_estimate=attention_cost(tokens, 320, 2),
    )(*[array for array, _ in ins])


def attend_back(queries, key_values, grad_out, windows, text_len=0):
    tokens = queries.shape[0]
    ins = attention_operands(queries, key_values) + [head_cols(grad_out, 0)]
    sets = len(key_values)
    whole = lambda rows, cols: pl.BlockSpec((rows, cols), lambda h: (0, 0))
    if sets == 1 and not text_len:
        outs = [((tokens, 3 * D), jnp.bfloat16)]
    else:
        rows = key_values[0][0].shape[0]
        outs = [((tokens, D), jnp.bfloat16)] + [((rows, 2 * D), jnp.float32)] * sets
    return pl.pallas_call(
        partial(attend_back_kernel, windows, text_len, sets),
        grid=(HEADS // 2,),
        in_specs=[spec for _, spec in ins],
        out_specs=[whole(*shape) for shape, _ in outs],
        out_shape=[jax.ShapeDtypeStruct(*out) for out in outs],
        compiler_params=pltpu.CompilerParams(vmem_limit_bytes=50 << 20),
        cost_estimate=attention_cost(tokens, 320, 5),
    )(*[array for array, _ in ins])


def mlp_forward(stream, modul, up_weight, down_weight):
    mlp_val, norm_back = jax.vjp(norm_modulated, stream, modul[3], modul[4])
    mlp_in = mlp_val.astype(jnp.bfloat16)
    up_proj = matmul(mlp_in, up_weight)
    gelu_val, gelu_back = jax.vjp(partial(jax.nn.gelu, approximate=False), up_proj)
    gelu_low = gelu_val.astype(jnp.bfloat16)
    down_proj = matmul(gelu_low, down_weight)
    return (stream + modul[5] * down_proj, (norm_back, mlp_in, gelu_back, gelu_low, down_proj))


def mlp_backward(grad_stream, modul, up_weight, down_weight, saved):
    norm_back, mlp_in, gelu_back, gelu_low, down_proj = saved
    grad_down = (modul[5] * grad_stream).astype(jnp.bfloat16)
    grad_gate = jnp.sum(grad_stream * down_proj, 0)
    grad_up = gelu_back(matmul_nt(grad_down, down_weight))[0].astype(jnp.bfloat16)
    grad_part, grad_shift, grad_scale = norm_back(matmul_nt(grad_up, up_weight))
    factors = ((gelu_low, grad_down), (mlp_in, grad_up))
    return (grad_stream + grad_part, factors, (grad_shift, grad_scale, grad_gate))


def adam_update(weight, first_mom, second_mom, grad_val, learn_rate):
    first_mom = BETA_ONE * first_mom + (1.0 - BETA_ONE) * grad_val
    second_mom = BETA_TWO * second_mom + (1.0 - BETA_TWO) * grad_val * grad_val
    first_hat = first_mom / (1.0 - BETA_ONE**STEP)
    second_hat = second_mom / (1.0 - BETA_TWO**STEP)
    weight = weight - learn_rate * (first_hat / (jnp.sqrt(second_hat) + ADAM_EPS) + DECAY * weight)
    return (weight, first_mom, second_mom)

MESH = pl.DeviceIdType.MESH
ANY = pl.BlockSpec(memory_space=pl.ANY)
TEXT_PAD = 80


def ring_place(clip, count):
    half = clip // 2
    odd = clip % 2
    return half + odd * (count - 1 - 2 * half)


def ring_clip(place, count):
    far = place // (count // 2)
    return (1 - far) * 2 * place + far * (2 * (count - 1 - place) + 1)


def greet(peers):
    barrier = pltpu.get_barrier_semaphore()
    for peer in peers:
        pl.semaphore_signal(barrier, inc=1, device_id=peer, device_id_type=MESH)
    pl.semaphore_wait(barrier, len(peers))


def exchange_kernel(count, facts_ref, text_ref, facts_out, text_out, send, recv, local):
    me = lax.axis_index("clip")
    band = lax.axis_index("band")
    peers = [((me + step) % count, band) for step in range(1, count)]
    greet(peers)
    own = [
        pltpu.make_async_copy(facts_ref, facts_out.at[me], local.at[0]),
        pltpu.make_async_copy(text_ref.at[me], text_out.at[me], local.at[1]),
    ]
    for copy in own:
        copy.start()
    sent = []
    for step, peer in enumerate(peers):
        sent += [
            pltpu.make_async_remote_copy(
                facts_ref, facts_out.at[me], send.at[0, step], recv.at[0, step], peer, MESH
            ),
            pltpu.make_async_remote_copy(
                text_ref.at[peer[0]], text_out.at[me], send.at[1, step], recv.at[1, step], peer, MESH
            ),
        ]
    for copy in sent:
        copy.start()
    for copy in own + sent:
        copy.wait()


def exchange_facts(facts, text):
    count = lax.axis_size("clip")
    return pl.pallas_call(
        partial(exchange_kernel, count),
        out_shape=(
            jax.ShapeDtypeStruct((count,) + facts.shape, facts.dtype),
            jax.ShapeDtypeStruct(text.shape, text.dtype),
        ),
        in_specs=[ANY] * 2,
        out_specs=(ANY,) * 2,
        scratch_shapes=[
            pltpu.SemaphoreType.DMA((2, count - 1)),
            pltpu.SemaphoreType.DMA((2, count - 1)),
            pltpu.SemaphoreType.DMA((2,)),
        ],
        compiler_params=pltpu.CompilerParams(collective_id=0, has_side_effects=True),
    )(facts, text)


def gather_kernel(count, shapes, sides, *refs):
    num = len(shapes)
    shards, (vec_ref, text_ref) = refs[:num], refs[num : num + 2]
    full, (vec_out, text_out) = refs[num + 2 : 2 * num + 2], refs[2 * num + 2 : 2 * num + 4]
    ring_send, ring_recv, pair_send, pair_recv, cross_send, cross_recv = refs[
        2 * num + 4 : 2 * num + 10
    ]
    own_sem, part_send, part_recv, part_own = refs[2 * num + 10 :]
    me = lax.axis_index("clip")
    band = lax.axis_index("band")
    core = band % 2
    place = ring_place(me, count)
    onward = 1 - 2 * core
    following = (ring_clip((place + onward + count) % count, count), band)
    plane = band // 2
    partner = (me, band + 1 - 2 * core)
    mirror = (me, band + 2 - 4 * plane)
    peers = [((me + step) % count, band) for step in range(1, count)]
    greet(peers + [partner, mirror])

    def block(ref, group, owner):
        rows, cols = shapes[group]
        return ref.at[
            pl.ds(pl.multiple_of(owner * rows, rows), rows),
            pl.ds(pl.multiple_of(core * (cols // 2), 128), cols // 2),
        ]

    def ring_copy(group, step):
        owner = ring_clip((place - onward * step + 2 * count) % count, count)
        there = block(full[group], group, owner)
        return pltpu.make_async_remote_copy(
            there, there, ring_send.at[step, group], ring_recv.at[step, group], following, MESH
        )

    def handed(group, step, send, recv, peer):
        owner = ring_clip((place - onward * (step + 1) + 2 * count) % count, count)
        there = block(full[group], group, owner)
        return pltpu.make_async_remote_copy(
            there, there, send.at[step, group], recv.at[step, group], peer, MESH
        )

    def pair_copy(group, step):
        return handed(group, step, pair_send, pair_recv, partner)

    def cross_copy(group, step):
        return handed(group, step, cross_send, cross_recv, mirror)

    def in_ring(group):
        def decorate(body):
            if sides[group]:
                pl.when(plane == sides[group] - 1)(body)
            else:
                body()

        return decorate

    def off_ring(group, also=None):
        def decorate(body):
            if sides[group]:
                off = plane != sides[group] - 1
                pl.when(off if also is None else jnp.logical_and(off, also))(body)

        return decorate

    def ring_arrival(group, step, onto):
        ring_copy(group, step).wait_recv()
        if onto:
            ring_copy(group, step + 1).start()
        pair_copy(group, step).start()
        if sides[group]:
            cross_copy(group, step).start()

    def cross_arrival(group, step):
        cross_copy(group, step).wait_recv()
        pair_copy(group, step).start()

    def own_copy(group):
        rows, cols = shapes[group]
        return pltpu.make_async_copy(
            shards[group],
            full[group].at[pl.ds(pl.multiple_of(me * rows, rows), rows), :],
            own_sem.at[group],
        )

    parts = []
    for step, peer in enumerate(peers):
        for which, (src, dst) in enumerate(((vec_ref, vec_out), (text_ref, text_out))):
            parts.append(
                pltpu.make_async_remote_copy(
                    src.at[peer[0]],
                    dst.at[me],
                    part_send.at[which, step],
                    part_recv.at[which, step],
                    peer,
                    MESH,
                )
            )
    parts_own = [
        pltpu.make_async_copy(src.at[me], dst.at[me], part_own.at[which])
        for which, (src, dst) in enumerate(((vec_ref, vec_out), (text_ref, text_out)))
    ]
    for group in range(num):
        rows, cols = shapes[group]
        own_copy(group).start()

        @in_ring(group)
        def _(group=group, rows=rows, cols=cols):
            pltpu.make_async_remote_copy(
                shards[group].at[:, pl.ds(pl.multiple_of(core * (cols // 2), 128), cols // 2)],
                block(full[group], group, me),
                ring_send.at[0, group],
                ring_recv.at[0, group],
                following,
                MESH,
            ).start()

    for copy in parts_own + parts:
        copy.start()

    @pl.loop(1, count - 1)
    def _(step):
        for group in range(num):

            @in_ring(group)
            def _(group=group):
                ring_arrival(group, step - 1, True)

        for group in range(num):

            @off_ring(group, step >= 2)
            def _(group=group):
                cross_arrival(group, step - 2)

    for group in range(num):

        @in_ring(group)
        def _(group=group):
            ring_arrival(group, count - 2, False)

    for late in (count - 3, count - 2):
        for group in range(num):

            @off_ring(group)
            def _(group=group, late=late):
                cross_arrival(group, late)

    for copy in parts_own + parts:
        copy.wait()
    for group in range(num):
        own_copy(group).wait()

    @pl.loop(0, count - 1)
    def _(step):
        for group in range(num):

            @in_ring(group)
            def _(group=group):
                ring_copy(group, step).wait_send()
                if sides[group]:
                    cross_copy(group, step).wait_send()

            pair_copy(group, step).wait()


def gather_quarters(shard):
    band_count = lax.axis_size("band")
    rows = shard.shape[0] // band_count
    own = lax.dynamic_slice_in_dim(shard, lax.axis_index("band") * rows, rows, 0)
    return lax.all_gather(own.astype(jnp.bfloat16), ("clip", "band"), axis=0, tiled=True)


def sum_rows(left, right):
    part = lax.psum_scatter(
        matmul_tn(left, right), ("clip", "band"), scatter_dimension=0, tiled=True
    )
    return lax.all_gather(part, "band", axis=0, tiled=True)


def gather_weights(shards, sides, vectors, texts):
    count = lax.axis_size("clip")
    num = len(shards)
    steps = pltpu.SemaphoreType.DMA((count - 1, num))
    out = pl.pallas_call(
        partial(gather_kernel, count, [shard.shape for shard in shards], sides),
        out_shape=tuple(
            jax.ShapeDtypeStruct((count * s.shape[0], s.shape[1]), s.dtype) for s in shards
        )
        + tuple(jax.ShapeDtypeStruct(v.shape, v.dtype) for v in (vectors, texts)),
        in_specs=[ANY] * (num + 2),
        out_specs=(ANY,) * (num + 2),
        scratch_shapes=[
            *[steps] * 6,
            pltpu.SemaphoreType.DMA((num,)),
            pltpu.SemaphoreType.DMA((2, count - 1)),
            pltpu.SemaphoreType.DMA((2, count - 1)),
            pltpu.SemaphoreType.DMA((2,)),
        ],
        compiler_params=pltpu.CompilerParams(collective_id=1, has_side_effects=True),
        cost_estimate=pl.CostEstimate(flops=2 * 10**11, bytes_accessed=6 * 10**8, transcendentals=0),
    )(*shards, vectors, texts)
    return out[:num], out[num], out[num + 1]


WIRE_MAX = 32767.0
WIRE_LEAST = 1e-30
UNIT = (128, 512)


def unit_parts(kind, first):
    if kind == 0:
        return ((0, 4, lambda u: u, lambda u: 0), (4, 4, lambda u: 4, lambda u: u - 3))
    return ((first, 3 - first, lambda u: u, lambda u: u), (3, 3, lambda u: 3, lambda u: u))


def reduce_kernel(count, tokens, phases, *refs):
    num = sum(len(phase["lefts"]) for phase in phases)
    lefts, rights = refs[:num], refs[num : 2 * num]
    wide_out, deep_out, square_out = refs[2 * num : 2 * num + 3]
    left_far, right_far = refs[2 * num + 3 : 3 * num + 3], refs[3 * num + 3 : 4 * num + 3]
    scratch = refs[4 * num + 3 :]
    left_buf, right_buf, got_low, got_scale, put_low, put_scale, plane_put = (
        scratch[2 * i : 2 * i + 2] for i in range(7)
    )
    plane_got = scratch[14 : 14 + len(phases)]
    (
        square_buf,
        left_sem,
        right_sem,
        pair_send,
        pair_recv,
        half_send,
        half_recv,
        ring_send,
        ring_recv,
        credit,
        plane_send,
        plane_recv,
        out_sem,
        out_send,
        out_recv,
    ) = scratch[14 + len(phases) :]
    me = lax.axis_index("clip")
    band = lax.axis_index("band")
    core = band % 2
    plane = band // 2
    place = ring_place(me, count)
    onward = 1 - 2 * core
    following = (ring_clip((place + onward + count) % count, count), band)
    preceding = (ring_clip((place - onward + count) % count, count), band)
    partner = (me, band + 1 - 2 * core)
    mirror = (me, band + 2 - 4 * plane)
    greet([following, preceding, partner, mirror])

    def owner_at(step, way):
        return ring_clip((place - way * (step + 1) + 2 * count) % count, count)

    def left_blocks(at):
        phase = phases[at]
        if phase["kind"] == 0:
            return [(b, phase["lefts"][0], b, 4) for b in range(4)] + [(4, phase["lefts"][1], 0, 1)]
        first = phase["first"]
        return [(first + i, left, 0, 1) for i, left in enumerate(phase["lefts"])]

    def right_blocks(at):
        phase = phases[at]
        if phase["kind"] == 0:
            return [(0, phase["lefts"][0], 0)] + [(1 + i, phase["lefts"][1], i) for i in range(4)]
        first = phase["first"]
        return [(first + i, phase["lefts"][i], 0) for i in range(3 - first)] + [
            (3 + i, phase["lefts"][-1], i) for i in range(3)
        ]

    def left_cols(step, way, which, many):
        width = lefts_width // count if many == 1 else deep_width // count
        start = owner_at(step, way) * width + which * 128
        return pl.ds(pl.multiple_of(start, 128), 128)

    lefts_width = lefts[phases[1]["lefts"][0]].shape[1]
    deep_width = lefts[phases[0]["lefts"][0]].shape[1]

    def pair_left(at, step):
        out = []
        for block, operand, which, many in left_blocks(at):
            cols = left_cols(step, -onward, which, many)
            out.append(
                pltpu.make_async_remote_copy(
                    lefts[operand].at[:, cols],
                    left_far[operand].at[:, cols],
                    pair_send.at[at, block, step],
                    pair_recv.at[at, block, step],
                    partner,
                    MESH,
                )
            )
        return out

    def pair_right(at):
        out = []
        for i, operand in enumerate(phases[at]["lefts"]):
            half = rights[operand].shape[1] // 2
            out.append(
                pltpu.make_async_remote_copy(
                    rights[operand].at[:, pl.ds(pl.multiple_of((1 - core) * half, 128), half)],
                    right_far[operand],
                    half_send.at[operand],
                    half_recv.at[operand],
                    partner,
                    MESH,
                )
            )
        return out

    def load_left(at, step, slot, far):
        kind = phases[at]["kind"]
        out = []
        for block, operand, which, many in left_blocks(at):
            cols = left_cols(step, onward, which, many)
            source = left_far if far else lefts
            out.append(
                pltpu.make_async_copy(
                    source[operand].at[:, cols],
                    left_buf[kind].at[slot, block, pl.ds(far * tokens, tokens), :],
                    left_sem.at[kind, slot, block, far],
                )
            )
        return out

    def load_right(at, far):
        kind = phases[at]["kind"]
        out = []
        for block, operand, which in right_blocks(at):
            if far:
                source = right_far[operand].at[:, pl.ds(which * UNIT[1], UNIT[1])]
            else:
                half = rights[operand].shape[1] // 2
                start = pl.multiple_of(core * half + which * UNIT[1], 128)
                source = rights[operand].at[:, pl.ds(start, UNIT[1])]
            out.append(
                pltpu.make_async_copy(
                    source,
                    right_buf[kind].at[block, pl.ds(far * tokens, tokens), :],
                    right_sem.at[kind, block, far],
                )
            )
        return out

    def ring_copies(at, part, slot):
        kind = phases[at]["kind"]
        start, many = unit_parts(kind, phases[at]["first"])[part][:2]
        units = pl.ds(start, many)
        return [
            pltpu.make_async_remote_copy(
                put.at[slot, units],
                got.at[slot, units],
                ring_send.at[kind, slot, part, i],
                ring_recv.at[kind, slot, part, i],
                following,
                MESH,
            )
            for i, (put, got) in enumerate(
                ((put_low[kind], got_low[kind]), (put_scale[kind], got_scale[kind]))
            )
        ]

    def plane_copy(at, part):
        kind = phases[at]["kind"]
        start, many = unit_parts(kind, phases[at]["first"])[part][:2]
        units = pl.ds(start, many)
        return pltpu.make_async_remote_copy(
            plane_put[kind].at[units],
            plane_got[at].at[units],
            plane_send.at[at, part],
            plane_recv.at[at, part],
            mirror,
            MESH,
        )

    def out_copies(at, unit):
        phase = phases[at]
        if phase["kind"] == 0 and unit < 4:
            half = UNIT[1]
            rows = deep_out.shape[0] // 4
            there = deep_out.at[
                pl.ds(unit * rows, rows),
                pl.ds(pl.multiple_of(phase["cols"][0] + core * half, 128), half),
            ]
        else:
            which, col = (1, unit - 4) if phase["kind"] == 0 else (unit - phase["first"], 0)
            if phase["kind"] and unit >= 3:
                which, col = len(phase["lefts"]) - 1, unit - 3
            half = rights[phase["lefts"][which]].shape[1] // 2
            start = phase["cols"][which] + core * half + col * UNIT[1]
            there = wide_out.at[:, pl.ds(pl.multiple_of(start, 128), UNIT[1])]
        here = plane_got[at].at[unit]
        return (
            pltpu.make_async_copy(here, there, out_sem.at[at, unit]),
            pltpu.make_async_remote_copy(
                here, there, out_send.at[at, unit], out_recv.at[at, unit], partner, MESH
            ),
        )

    def product(kind, slot, left, right):
        return lax.dot_general(
            left_buf[kind][slot, left],
            right_buf[kind][right],
            (((0,), (0,)), ((), ())),
            preferred_element_type=jnp.float32,
        )

    def start(copies):
        for copy in copies:
            copy.start()

    def finish(copies):
        for copy in copies:
            copy.wait()

    def take_step(at, step, first, last):
        phase = phases[at]
        kind = phase["kind"]
        slot = step % 2
        before = (step + 1) % 2
        for far in range(2):
            finish(load_left(at, step, slot, far))
        if not last:
            for copy in pair_left(at, step + 1):
                copy.wait_recv()
            for far in range(2):
                start(load_left(at, step + 1, before, far))
        for part, (low, many, left_of, right_of) in enumerate(unit_parts(kind, phase["first"])):
            if not first:
                for copy in ring_copies(at, part, before):
                    copy.wait_recv()
            if not (first or last):

                @pl.when(step >= 2)
                def _(part=part):
                    for copy in ring_copies(at, part, slot):
                        copy.wait_send()
                    pl.semaphore_wait(credit.at[kind, part], 1)

            @pl.loop(low, low + many)
            def _(unit, left_of=left_of, right_of=right_of):
                term = product(kind, slot, left_of(unit), right_of(unit))
                if not first:
                    came = got_low[kind][before, unit].astype(jnp.float32)
                    term = term + came * got_scale[kind][before, unit]
                if last:
                    plane_put[kind][unit] = term
                else:
                    largest = jnp.max(jnp.abs(term), axis=0, keepdims=True)
                    largest = jnp.maximum(largest, WIRE_LEAST)
                    factor = WIRE_MAX / largest
                    put_low[kind][slot, unit] = jnp.round(term * factor).astype(jnp.int16)
                    put_scale[kind][slot, unit] = largest * (1.0 / WIRE_MAX)

            if last:
                plane_copy(at, part).start()
            else:
                start(ring_copies(at, part, slot))
            if not (first or last):

                @pl.when(step < count - 2)
                def _(part=part):
                    pl.semaphore_signal(
                        credit.at[kind, part], inc=1, device_id=preceding, device_id_type=MESH
                    )

    def close(at):
        kind = phases[at]["kind"]
        for part, (low, many, _, _) in enumerate(unit_parts(kind, phases[at]["first"])):
            plane_copy(at, part).wait()

            @pl.loop(low, low + many)
            def _(unit):
                total = plane_put[kind][unit] + plane_got[at][unit]
                plane_got[at][unit] = total
                square_buf[...] += jnp.sum(
                    (total * total).reshape(UNIT[0] // 8, 8, UNIT[1]), axis=0
                )

            for unit in range(low, low + many):
                start(out_copies(at, unit))

    square_buf[...] = jnp.zeros_like(square_buf)
    start(load_right(0, 0))
    start(pair_right(0))

    @pl.loop(0, count)
    def _(step):
        start(pair_left(0, step))

    start(load_left(0, 0, 0, 0))
    for at in range(len(phases)):
        if at == 0:
            for copy in pair_right(0):
                copy.wait_recv()
            start(load_right(0, 1))
            for copy in pair_left(0, 0):
                copy.wait_recv()
            start(load_left(0, 0, 0, 1))
        for far in range(2):
            finish(load_right(at, far))
        more = at + 1 < len(phases)
        if more:
            start(pair_right(at + 1))
            start(load_right(at + 1, 0))
        take_step(at, 0, True, False)
        if more:
            start(pair_left(at + 1, 0))

        @pl.loop(1, count - 1)
        def _(step, at=at, more=more):
            take_step(at, step, False, False)
            if more:
                start(pair_left(at + 1, step))

        if more:
            start(pair_left(at + 1, count - 1))
            for copy in pair_right(at + 1):
                copy.wait_recv()
            start(load_right(at + 1, 1))
            for copy in pair_left(at + 1, 0):
                copy.wait_recv()
            for far in range(2):
                start(load_left(at + 1, 0, 0, far))
        take_step(at, count - 1, False, True)
        for part in range(2):
            for slot in range(2):
                for copy in ring_copies(at, part, slot):
                    copy.wait_send()
        if at:
            close(at - 1)
    close(len(phases) - 1)
    square_out[...] = square_buf[...]
    for at, phase in enumerate(phases):
        for copy in pair_right(at):
            copy.wait_send()

        @pl.loop(0, count)
        def _(step, at=at):
            for copy in pair_left(at, step):
                copy.wait_send()

        for unit in range(phase["first"], 8 if phase["kind"] == 0 else 6):
            finish(out_copies(at, unit))


def reduce_gradients(phases, lefts, rights, wide_cols, deep_cols):
    count = lax.axis_size("clip")
    tokens = lefts[0].shape[0]
    wide_rows = lefts[1].shape[1] // count
    deep_rows = lefts[0].shape[1] // count
    num = len(lefts)
    dma = pltpu.SemaphoreType.DMA
    units, lefts_of, rights_of = (8, 6), (5, 4), (5, 6)
    scratch = [pltpu.VMEM((2, lefts_of[k], 2 * tokens, 128), jnp.bfloat16) for k in range(2)]
    scratch += [pltpu.VMEM((rights_of[k], 2 * tokens, UNIT[1]), jnp.bfloat16) for k in range(2)]
    for _ in range(2):
        scratch += [pltpu.VMEM((2, units[k]) + UNIT, jnp.int16) for k in range(2)]
        scratch += [pltpu.VMEM((2, units[k], 1, UNIT[1]), jnp.float32) for k in range(2)]
    scratch += [pltpu.VMEM((units[k],) + UNIT, jnp.float32) for k in range(2)]
    scratch += [pltpu.VMEM((units[p["kind"]],) + UNIT, jnp.float32) for p in phases]
    scratch += [
        pltpu.VMEM((8, UNIT[1]), jnp.float32),
        dma((2, 2, 5, 2)),
        dma((2, 6, 2)),
        dma((len(phases), 5, count)),
        dma((len(phases), 5, count)),
        dma((num,)),
        dma((num,)),
        dma((2, 2, 2, 2)),
        dma((2, 2, 2, 2)),
        pltpu.SemaphoreType.REGULAR((2, 2)),
        dma((len(phases), 2)),
        dma((len(phases), 2)),
        dma((len(phases), 8)),
        dma((len(phases), 8)),
        dma((len(phases), 8)),
    ]
    out = pl.pallas_call(
        partial(reduce_kernel, count, tokens, phases),
        out_shape=(
            jax.ShapeDtypeStruct((wide_rows, wide_cols), jnp.float32),
            jax.ShapeDtypeStruct((deep_rows, deep_cols), jnp.float32),
            jax.ShapeDtypeStruct((8, UNIT[1]), jnp.float32),
        )
        + tuple(jax.ShapeDtypeStruct(x.shape, x.dtype) for x in lefts)
        + tuple(jax.ShapeDtypeStruct((tokens, x.shape[1] // 2), x.dtype) for x in rights),
        in_specs=[ANY] * (2 * num),
        out_specs=(ANY, ANY, pl.BlockSpec(memory_space=pltpu.VMEM)) + (ANY,) * (2 * num),
        scratch_shapes=scratch,
        compiler_params=pltpu.CompilerParams(
            collective_id=2, has_side_effects=True, vmem_limit_bytes=58 << 20
        ),
        cost_estimate=pl.CostEstimate(flops=3 * 10**11, bytes_accessed=8 * 10**8, transcendentals=0),
    )(*lefts, *rights)
    return out[:3]


def per_device(
    latents,
    noise_field,
    timesteps,
    null_flags,
    frame_mask,
    context,
    w_wide,
    m_wide,
    v_wide,
    w_deep,
    m_deep,
    v_deep,
    w_small,
    m_small,
    v_small,
):
    clip_count = lax.axis_size("clip")
    band_count = lax.axis_size("band")
    clip_at = lax.axis_index("clip")
    band_at = lax.axis_index("band")
    wide_rows = w_wide.shape[0]
    deep_rows = w_deep.shape[0]
    text_len, text_dim = context.shape[1:]
    facts = jnp.pad(
        jnp.concatenate([timesteps, frame_mask[0]])[None],
        ((0, 7), (0, 127 - frame_mask.shape[1])),
    )
    kept_text = context[0] * (1 - null_flags[0]).astype(jnp.bfloat16)
    text_cols = jnp.pad(
        kept_text.reshape(text_len, clip_count, deep_rows).transpose(1, 0, 2),
        ((0, 0), (0, TEXT_PAD - text_len), (0, 0)),
    )
    all_facts, all_text = exchange_facts(facts, text_cols)
    all_times = all_facts[:, 0, 0].astype(jnp.float32)
    all_time_low = jax.nn.silu(time_features(all_times)).astype(jnp.bfloat16)
    time_rows = lax.dynamic_slice(
        all_time_low, (0, clip_at * wide_rows), (clip_count, wide_rows)
    )
    part_modul = matmul(time_rows, w_wide[:, : 12 * D].astype(jnp.bfloat16))
    kv_cols = 2 * D // band_count
    kv_weight = lax.dynamic_slice(
        w_deep, (0, D + band_at * kv_cols), (deep_rows, kv_cols)
    ).astype(jnp.bfloat16)
    part_kv = matmul(all_text.reshape(clip_count * TEXT_PAD, deep_rows), kv_weight)
    edges = (12 * D, 15 * D, 18 * D, 19 * D, 20 * D, 21 * D, 22 * D, 22 * D + FF)
    shards = [w_wide[:, low:high].astype(jnp.bfloat16) for low, high in zip(edges, edges[1:])]
    shards += [w_deep[:, :D].astype(jnp.bfloat16)]
    up_b_w = gather_quarters(w_wide[:, 22 * D + FF :])
    down_b_w = gather_quarters(w_deep[:, 3 * D :])
    gathered, all_modul, all_kv = gather_weights(
        shards,
        (0, 0, 1, 2, 1, 2, 1, 2),
        part_modul.reshape(clip_count, 12 * D // 128, 128),
        part_kv.reshape(clip_count, TEXT_PAD, kv_cols),
    )
    (
        qkv_a_w,
        qkv_b_w,
        out_a_w,
        out_b_w,
        query_w,
        cross_out_w,
        up_a_w,
        down_a_w,
    ) = gathered
    keyval = lax.all_gather(jnp.sum(all_kv, 0).astype(jnp.bfloat16), "band", axis=1, tiled=True)
    small_low = w_small.astype(jnp.bfloat16)
    small_val = small_low.astype(jnp.float32)
    num_frames, num_rows, num_cols = (latents.shape[1], latents.shape[2], latents.shape[3])
    tok_count = num_frames * num_rows * num_cols
    all_mask = all_facts[:, 0, 1 : 1 + num_frames]
    global_count = jnp.sum(all_mask).astype(jnp.float32) * (num_rows * num_cols * CH * band_count)
    time_value = timesteps[0].astype(jnp.float32)
    noise_angle = 0.5 * math.pi * time_value / TMAX
    signal, spread = (jnp.cos(noise_angle), jnp.sin(noise_angle))
    clean_tok = token_order(latents[0])
    noise_tok = token_order(noise_field[0])
    run = num_rows * WIN
    part = SHIFT * WIN
    frame_windows = attend_pieces(tok_count, num_frames, "frame")
    half_windows = attend_pieces(tok_count, num_frames, "half")
    text_windows = attend_pieces(tok_count, num_frames, "text")
    noisy_low = (signal * clean_tok + spread * noise_tok).astype(jnp.bfloat16)
    target = signal * noise_tok - spread * clean_tok
    modulation = jnp.sum(all_modul, 0).reshape(12, D)
    mod_a, mod_b = (modulation[:6], modulation[6:])
    stream_zero = matmul(noisy_low, small_low[:CH]) + small_val[2 * CH]
    normed_a, back_a = jax.vjp(norm_modulated, stream_zero, mod_a[0], mod_a[1])
    in_a = normed_a.astype(jnp.bfloat16)
    qkv_a = matmul(in_a, qkv_a_w).astype(jnp.bfloat16)
    far_kv = from_partner(qkv_a[:, D:], "band", 0)
    space_kv = [(qkv_a, HEADS // 2, HEADS), (far_kv, 0, HEADS // 2)]
    att_a = attend(qkv_a, space_kv, frame_windows)
    proj_a = matmul(att_a, out_a_w)
    stream_one = stream_zero + mod_a[2] * proj_a
    stream_two, saved_a = mlp_forward(stream_one, mod_a, up_a_w, down_a_w)
    normed_b, back_b = jax.vjp(norm_modulated, stream_two, mod_b[0], mod_b[1])
    low_b = normed_b.astype(jnp.bfloat16)
    rolled = with_rows(low_b, shifted(first_rows(low_b, run, part), "band", -1), run)
    qkv_b = matmul(rolled, qkv_b_w).astype(jnp.bfloat16)
    win_kv = [(qkv_b, HEADS // 2, HEADS)]
    win_out = attend(qkv_b, win_kv, half_windows)
    att_b = with_rows(win_out, shifted(first_rows(win_out, run, part), "band", 1), run)
    proj_b = matmul(att_b, out_b_w)
    stream_three = stream_two + mod_b[2] * proj_b
    cross_val, cross_back = jax.vjp(norm_gained, stream_three, small_val[2 * CH + 1])
    cross_in = cross_val.astype(jnp.bfloat16)
    query_proj = matmul(cross_in, query_w).astype(jnp.bfloat16)
    text_kv = [(keyval, 0, HEADS // 2)]
    crossed = attend(query_proj, text_kv, text_windows, text_len)
    stream_four = stream_three + matmul(crossed, cross_out_w)
    stream_five, saved_b = mlp_forward(stream_four, mod_b, up_b_w, down_b_w)
    final_val, final_back = jax.vjp(norm_gained, stream_five, small_val[2 * CH + 2])
    final_low = final_val.astype(jnp.bfloat16)
    head_low = small_low[CH : 2 * CH]
    predicted = matmul_nt(final_low, head_low)
    weight_row = jnp.repeat(frame_mask[0].astype(jnp.float32), run)
    weight_row = jnp.tile(weight_row, num_cols // WIN)[:, None]
    pred_error = predicted - target
    loss_part = jnp.sum(weight_row * pred_error * pred_error)
    grad_pred = (weight_row * pred_error * (2.0 / global_count)).astype(jnp.bfloat16)
    grad_head = matmul_tn(grad_pred, final_low)
    grad_stream, grad_gain_f = final_back(matmul(grad_pred, head_low))
    grad_stream, mlp_factors_b, extra_b = mlp_backward(
        grad_stream, mod_b, up_b_w, down_b_w, saved_b
    )
    grad_cross = grad_stream.astype(jnp.bfloat16)
    grad_crossed = matmul_nt(grad_cross, cross_out_w).astype(jnp.bfloat16)
    grad_query, grad_keyval = attend_back(
        query_proj, text_kv, grad_crossed, text_windows, text_len
    )
    grad_part, grad_gain_c = cross_back(matmul_nt(grad_query, query_w))
    grad_keyval = lax.psum_scatter(grad_keyval, "band", scatter_dimension=1, tiled=True)
    grad_keyval = lax.all_gather(grad_keyval, "clip", axis=0, tiled=True)
    grad_w_ckv = matmul_tn(
        all_text.reshape(clip_count * TEXT_PAD, deep_rows).astype(jnp.float32),
        grad_keyval,
        lax.Precision.HIGHEST,
    )
    grad_w_ckv = lax.all_gather(grad_w_ckv, "band", axis=1, tiled=True)
    grad_stream = grad_stream + grad_part
    grad_proj = (mod_b[2] * grad_stream).astype(jnp.bfloat16)
    grad_gate_b = jnp.sum(grad_stream * proj_b, 0)
    factors_ob = (att_b, grad_proj)
    grad_att = matmul_nt(grad_proj, out_b_w).astype(jnp.bfloat16)
    grad_win = with_rows(grad_att, shifted(first_rows(grad_att, run, part), "band", -1), run)
    grad_qkv = attend_back(qkv_b, win_kv, grad_win, half_windows)[0]
    factors_qkvb = (rolled, grad_qkv)
    grad_in_roll = matmul_nt(grad_qkv, qkv_b_w)
    sent_back = shifted(first_rows(grad_in_roll, run, part), "band", 1)
    grad_normed = with_rows(grad_in_roll, sent_back, run)
    grad_part, grad_shift_b, grad_scale_b = back_b(grad_normed)
    grad_stream = grad_stream + grad_part
    grad_stream, mlp_factors_a, extra_a = mlp_backward(
        grad_stream, mod_a, up_a_w, down_a_w, saved_a
    )
    grad_proj = (mod_a[2] * grad_stream).astype(jnp.bfloat16)
    grad_gate_a = jnp.sum(grad_stream * proj_a, 0)
    factors_oa = (att_a, grad_proj)
    grad_att = matmul_nt(grad_proj, out_a_w).astype(jnp.bfloat16)
    grad_q, grad_own, grad_far = attend_back(qkv_a, space_kv, grad_att, frame_windows)
    grad_kv = grad_own + from_partner(grad_far, "band", 0)
    grad_qkv = jnp.concatenate([grad_q, grad_kv.astype(jnp.bfloat16)], 1)
    factors_qkva = (in_a, grad_qkv)
    grad_part, grad_shift_a, grad_scale_a = back_a(matmul_nt(grad_qkv, qkv_a_w))
    grad_stream = grad_stream + grad_part
    grad_patch = matmul_tn(noisy_low.astype(jnp.float32), grad_stream, lax.Precision.HIGHEST)
    grad_bias = jnp.sum(grad_stream, 0)
    grad_modul = jnp.stack(
        [
            grad_shift_a,
            grad_scale_a,
            grad_gate_a,
            extra_a[0],
            extra_a[1],
            extra_a[2],
            grad_shift_b,
            grad_scale_b,
            grad_gate_b,
            extra_b[0],
            extra_b[1],
            extra_b[2],
        ]
    ).reshape(1, 12 * D)
    grad_small = jnp.concatenate(
        [grad_patch, grad_head, grad_bias[None], grad_gain_c[None], grad_gain_f[None]], 0
    )
    all_grad_modul = lax.all_gather(lax.psum(grad_modul, "band"), "clip", axis=0, tiled=True)
    grad_w_ada = matmul_tn(time_rows.astype(jnp.float32), all_grad_modul, lax.Precision.HIGHEST)
    factors = mlp_factors_b + (
        (crossed, grad_cross),
        (cross_in, grad_query),
        factors_ob,
        factors_qkvb,
    )
    factors += mlp_factors_a + (factors_oa, factors_qkva)
    if wide_rows == 128 and deep_rows == 512:
        phases = (
            {"kind": 0, "first": 0, "lefts": (0, 1), "cols": (D, 10 * D + FF)},
            {"kind": 1, "first": 0, "lefts": (2, 3, 4, 5), "cols": (9 * D, 8 * D, 7 * D, 3 * D)},
            {"kind": 0, "first": 0, "lefts": (6, 7), "cols": (0, 10 * D)},
            {"kind": 1, "first": 2, "lefts": (8, 9), "cols": (6 * D, 0)},
        )
        wide_rest, deep_rest, squares = reduce_gradients(
            phases, [f[0] for f in factors], [f[1] for f in factors], 10 * D + 2 * FF, 2 * D
        )
        square_part = jnp.sum(squares) / (band_count // 2)
    else:
        summed = [sum_rows(*pair) for pair in factors]
        wide_rest = jnp.concatenate([summed[i] for i in (9, 5, 8, 4, 3, 2, 7, 1)], 1)
        deep_rest = jnp.concatenate([summed[6], summed[0]], 1)
        square_part = (jnp.sum(wide_rest**2) + jnp.sum(deep_rest**2)) / band_count
    wide_sum = jnp.concatenate([grad_w_ada, wide_rest], 1)
    deep_sum = jnp.concatenate([deep_rest[:, :D], grad_w_ckv, deep_rest[:, D:]], 1)
    square_part += (jnp.sum(grad_w_ada**2) + jnp.sum(grad_w_ckv**2)) / band_count
    loss_sum, square_sum, small_sum = lax.psum(
        (loss_part, square_part, grad_small), ("clip", "band")
    )
    grad_norm = jnp.sqrt(square_sum + jnp.sum(small_sum * small_sum))
    factor = CLIP_MAX / jnp.maximum(grad_norm, CLIP_MAX)
    new_wide = adam_update(w_wide, m_wide, v_wide, wide_sum * factor, 0.15)
    new_deep = adam_update(w_deep, m_deep, v_deep, deep_sum * factor, 0.05)
    new_small = adam_update(w_small, m_small, v_small, small_sum * factor, 0.5)
    loss = loss_sum / global_count
    return (
        loss,
        grad_norm,
        new_wide[0],
        new_wide[1],
        new_wide[2],
        new_deep[0],
        new_deep[1],
        new_deep[2],
        new_small[0],
        new_small[1],
        new_small[2],
    )


def solution(mesh):
    in_specs = (
        P("clip", None, "band", None, None),
        P("clip", None, "band", None, None),
        P("clip"),
        P("clip"),
        P("clip", None),
        P("clip", None, None),
        P("clip", None),
        P("clip", None),
        P("clip", None),
        P("clip", None),
        P("clip", None),
        P("clip", None),
        P(),
        P(),
        P(),
    )
    out_specs = (
        P(),
        P(),
        P("clip", None),
        P("clip", None),
        P("clip", None),
        P("clip", None),
        P("clip", None),
        P("clip", None),
        P(),
        P(),
        P(),
    )
    return jax.shard_map(
        per_device, mesh=mesh, in_specs=in_specs, out_specs=out_specs, check_vma=False
    )
```

```python
from functools import partial
import math

import jax
import jax.numpy as jnp
from jax import lax
from jax.experimental import pallas as pl
from jax.experimental.pallas import tpu as pltpu
from jax.sharding import PartitionSpec as P

D = 1024
HEADS = 16
HEAD_DIM = 64
FF = 4096
CH = 8
SPACE = 16
WIN = 8
SHIFT = 4
TMAX = 1000
STEP = 10


EPS_NORM = 1e-06
CLIP_MAX = 0.001
BETA_ONE = 0.9
BETA_TWO = 0.95
ADAM_EPS = 1e-08
DECAY = 0.1


def from_partner(block, axis, distance):
    count = lax.axis_size(axis)
    route = []
    for low in range(count):
        high = low | 1 << distance
        if high != low and high < count:
            route += [(low, high), (high, low)]
    return lax.ppermute(block, axis, route)


def shifted(value, axis, by):
    length = lax.axis_size(axis)
    return lax.ppermute(value, axis, [(i, (i + by) % length) for i in range(length)])


def matmul(left_op, right_op):
    return jnp.dot(left_op, right_op, preferred_element_type=jnp.float32)


def matmul_tn(left_op, right_op, precision=None):
    return lax.dot_general(
        left_op,
        right_op,
        (((0,), (0,)), ((), ())),
        precision=precision,
        preferred_element_type=jnp.float32,
    )


def matmul_nt(left_op, right_op):
    return lax.dot_general(
        left_op, right_op, (((1,), (1,)), ((), ())), preferred_element_type=jnp.float32
    )


def layer_norm(field_in):
    average = jnp.mean(field_in, -1, keepdims=True)
    centred = field_in - average
    return centred * lax.rsqrt(jnp.mean(centred * centred, -1, keepdims=True) + EPS_NORM)


def norm_modulated(field_in, shift_vec, scale_vec):
    return layer_norm(field_in) * (1.0 + scale_vec) + shift_vec


def norm_gained(field_in, gain_vec):
    return layer_norm(field_in) * gain_vec


def time_features(time_value):
    half_width = D // 2
    frequency = jnp.exp(-math.log(10000.0) * jnp.arange(half_width, dtype=jnp.float32) / half_width)
    angles = time_value[..., None] * frequency
    return jnp.concatenate([jnp.cos(angles), jnp.sin(angles)], -1)


def token_order(grid):
    frames, rows, cols, width = grid.shape
    halves = grid.reshape(frames, rows, cols // WIN, WIN, width).transpose(2, 0, 1, 3, 4)
    return halves.reshape(frames * rows * cols, width)


def with_rows(tokens, first_rows, run):
    width = tokens.shape[1]
    runs = tokens.reshape(-1, run, width)
    return jnp.concatenate([first_rows, runs[:, first_rows.shape[1] :]], 1).reshape(-1, width)


def first_rows(tokens, run, part):
    return tokens.reshape(-1, run, tokens.shape[1])[:, :part]


def attend_pieces(tokens, frames, keys):
    if keys == "frame":
        run = tokens // (2 * frames)
        return [((f * run, run), (tokens // 2 + f * run, run)) for f in range(frames)]
    if keys == "half":
        return [((half * (tokens // 2), tokens // 2),) for half in range(2)]
    return [((0, tokens),)]


def take(ref, runs):
    pieces = [ref[low : low + many, :] for low, many in runs]
    return pieces[0] if len(pieces) == 1 else jnp.concatenate(pieces, 0)


def put(ref, cols, runs, value):
    done = 0
    for low, many in runs:
        ref[low : low + many, cols] = value[done : done + many].astype(ref.dtype)
        done += many


def softmax_rows(queries, keys, text_len):
    scores = matmul_nt(queries, keys)
    if text_len:
        place = lax.broadcasted_iota(jnp.int32, scores.shape, 1)
        scores = jnp.where(place < text_len, scores, -1e30)
    weight = jnp.exp(scores - jnp.max(scores, -1, keepdims=True))
    return weight / jnp.sum(weight, -1, keepdims=True)


def lanes_of(head, shape):
    lane = lax.broadcasted_iota(jnp.int32, shape, 1)
    return lane < HEAD_DIM if head == 0 else lane >= HEAD_DIM


def only(head, value):
    return jnp.where(lanes_of(head, value.shape), value, jnp.zeros_like(value))


def key_sets(key_refs, runs, text_len):
    if text_len:
        return key_refs[0][...]
    pieces = [take(ref, runs) for ref in key_refs]
    return pieces[0] if len(pieces) == 1 else jnp.concatenate(pieces, 0)


def attend_kernel(windows, text_len, sets, *refs):
    q_ref, k_refs, v_refs, out_ref = refs[0], refs[1 : 1 + sets], refs[1 + sets : 1 + 2 * sets], refs[-1]
    for runs in windows:
        queries = take(q_ref, runs) * HEAD_DIM ** (-0.5)
        keys, values = key_sets(k_refs, runs, text_len), key_sets(v_refs, runs, text_len)
        outs = []
        for head in range(2):
            probs = softmax_rows(only(head, queries), keys, text_len)
            outs.append(matmul(probs.astype(jnp.bfloat16), values))
        put(out_ref, slice(None), runs, jnp.where(lanes_of(0, outs[0].shape), *outs))


def attend_back_kernel(windows, text_len, sets, *refs):
    q_ref, k_refs, v_refs = refs[0], refs[1 : 1 + sets], refs[1 + sets : 1 + 2 * sets]
    grad_ref = refs[1 + 2 * sets]
    dq_ref = refs[2 + 2 * sets]
    own_ref = refs[3 + 2 * sets] if len(refs) > 3 + 2 * sets else None
    far_ref = refs[4 + 2 * sets] if sets == 2 else None
    pair = pl.program_id(0)
    cols = [pl.ds(pl.multiple_of(i * D + pair * 2 * HEAD_DIM, 128), 2 * HEAD_DIM) for i in range(3)]
    merged = dq_ref.shape[1] == 3 * D
    for runs in windows:
        queries = take(q_ref, runs) * HEAD_DIM ** (-0.5)
        keys, values = key_sets(k_refs, runs, text_len), key_sets(v_refs, runs, text_len)
        grad_out = take(grad_ref, runs)
        dq, dk, dv = [], [], []
        for head in range(2):
            probs = softmax_rows(only(head, queries), keys, text_len)
            dprobs = matmul_nt(only(head, grad_out), values)
            dv.append(matmul_tn(probs.astype(jnp.bfloat16), grad_out))
            inner = jnp.sum(probs * dprobs, -1, keepdims=True)
            dscores = (probs * (dprobs - inner)).astype(jnp.bfloat16)
            dq.append(matmul(dscores, keys))
            dk.append(matmul_tn(dscores, queries))
        dq, dk, dv = (jnp.where(lanes_of(0, x[0].shape), *x) for x in (dq, dk, dv))
        put(dq_ref, cols[0], runs, dq * HEAD_DIM ** (-0.5))
        if merged:
            put(dq_ref, cols[1], runs, dk)
            put(dq_ref, cols[2], runs, dv)
        elif text_len:
            own_ref[:, cols[0]] = dk
            own_ref[:, cols[1]] = dv
        else:
            half = dk.shape[0] // 2
            put(own_ref, cols[0], runs, dk[:half])
            put(own_ref, cols[1], runs, dv[:half])
            put(far_ref, cols[0], runs, dk[half:])
            put(far_ref, cols[1], runs, dv[half:])


def head_cols(array, first):
    return array, pl.BlockSpec((array.shape[0], 2 * HEAD_DIM), lambda h: (0, first + h))


def attention_operands(queries, key_values):
    ins = [head_cols(queries, 0)]
    ins += [head_cols(array, first) for array, first, _ in key_values]
    return ins + [head_cols(array, second) for array, _, second in key_values]


def attention_cost(tokens, keys, products):
    flops = 2 * products * tokens * keys * D * 2
    return pl.CostEstimate(
        flops=flops, bytes_accessed=tokens * D * 2 * 8, transcendentals=tokens * keys * HEADS
    )


def attend(queries, key_values, windows, text_len=0):
    tokens = queries.shape[0]
    ins = attention_operands(queries, key_values)
    return pl.pallas_call(
        partial(attend_kernel, windows, text_len, len(key_values)),
        grid=(HEADS // 2,),
        in_specs=[spec for _, spec in ins],
        out_specs=pl.BlockSpec((tokens, 2 * HEAD_DIM), lambda h: (0, h)),
        out_shape=jax.ShapeDtypeStruct((tokens, D), jnp.bfloat16),
        compiler_params=pltpu.CompilerParams(vmem_limit_bytes=40 << 20),
        cost_estimate=attention_cost(tokens, 320, 2),
    )(*[array for array, _ in ins])


def attend_back(queries, key_values, grad_out, windows, text_len=0):
    tokens = queries.shape[0]
    ins = attention_operands(queries, key_values) + [head_cols(grad_out, 0)]
    sets = len(key_values)
    whole = lambda rows, cols: pl.BlockSpec((rows, cols), lambda h: (0, 0))
    if sets == 1 and not text_len:
        outs = [((tokens, 3 * D), jnp.bfloat16)]
    else:
        rows = key_values[0][0].shape[0]
        outs = [((tokens, D), jnp.bfloat16)] + [((rows, 2 * D), jnp.float32)] * sets
    return pl.pallas_call(
        partial(attend_back_kernel, windows, text_len, sets),
        grid=(HEADS // 2,),
        in_specs=[spec for _, spec in ins],
        out_specs=[whole(*shape) for shape, _ in outs],
        out_shape=[jax.ShapeDtypeStruct(*out) for out in outs],
        compiler_params=pltpu.CompilerParams(vmem_limit_bytes=50 << 20),
        cost_estimate=attention_cost(tokens, 320, 5),
    )(*[array for array, _ in ins])


def mlp_forward(stream, modul, up_weight, down_weight):
    mlp_val, norm_back = jax.vjp(norm_modulated, stream, modul[3], modul[4])
    mlp_in = mlp_val.astype(jnp.bfloat16)
    up_proj = matmul(mlp_in, up_weight)
    gelu_val, gelu_back = jax.vjp(partial(jax.nn.gelu, approximate=False), up_proj)
    gelu_low = gelu_val.astype(jnp.bfloat16)
    down_proj = matmul(gelu_low, down_weight)
    return (stream + modul[5] * down_proj, (norm_back, mlp_in, gelu_back, gelu_low, down_proj))


def mlp_backward(grad_stream, modul, up_weight, down_weight, saved):
    norm_back, mlp_in, gelu_back, gelu_low, down_proj = saved
    grad_down = (modul[5] * grad_stream).astype(jnp.bfloat16)
    grad_gate = jnp.sum(grad_stream * down_proj, 0)
    grad_up = gelu_back(matmul_nt(grad_down, down_weight))[0].astype(jnp.bfloat16)
    grad_part, grad_shift, grad_scale = norm_back(matmul_nt(grad_up, up_weight))
    factors = ((gelu_low, grad_down), (mlp_in, grad_up))
    return (grad_stream + grad_part, factors, (grad_shift, grad_scale, grad_gate))


def adam_update(weight, first_mom, second_mom, grad_val, learn_rate):
    first_mom = BETA_ONE * first_mom + (1.0 - BETA_ONE) * grad_val
    second_mom = BETA_TWO * second_mom + (1.0 - BETA_TWO) * grad_val * grad_val
    first_hat = first_mom / (1.0 - BETA_ONE**STEP)
    second_hat = second_mom / (1.0 - BETA_TWO**STEP)
    weight = weight - learn_rate * (first_hat / (jnp.sqrt(second_hat) + ADAM_EPS) + DECAY * weight)
    return (weight, first_mom, second_mom)

MESH = pl.DeviceIdType.MESH
ANY = pl.BlockSpec(memory_space=pl.ANY)
IN_VMEM = pl.BlockSpec(memory_space=pltpu.VMEM)
TEXT_PAD = 80


def ring_place(clip, count):
    half = clip // 2
    odd = clip % 2
    return half + odd * (count - 1 - 2 * half)


def ring_clip(place, count):
    far = place // (count // 2)
    return (1 - far) * 2 * place + far * (2 * (count - 1 - place) + 1)


def greet(peers):
    barrier = pltpu.get_barrier_semaphore()
    for peer in peers:
        pl.semaphore_signal(barrier, inc=1, device_id=peer, device_id_type=MESH)
    pl.semaphore_wait(barrier, len(peers))


def exchange_kernel(count, facts_ref, text_ref, facts_out, text_out, send, recv, local):
    me = lax.axis_index("clip")
    band = lax.axis_index("band")
    peers = [((me + step) % count, band) for step in range(1, count)]
    greet(peers)
    own = [
        pltpu.make_async_copy(facts_ref, facts_out.at[me], local.at[0]),
        pltpu.make_async_copy(text_ref.at[me], text_out.at[me], local.at[1]),
    ]
    for copy in own:
        copy.start()
    sent = []
    for step, peer in enumerate(peers):
        sent += [
            pltpu.make_async_remote_copy(
                facts_ref, facts_out.at[me], send.at[0, step], recv.at[0, step], peer, MESH
            ),
            pltpu.make_async_remote_copy(
                text_ref.at[peer[0]], text_out.at[me], send.at[1, step], recv.at[1, step], peer, MESH
            ),
        ]
    for copy in sent:
        copy.start()
    for copy in own + sent:
        copy.wait()


def exchange_facts(facts, text):
    count = lax.axis_size("clip")
    return pl.pallas_call(
        partial(exchange_kernel, count),
        out_shape=(
            jax.ShapeDtypeStruct((count,) + facts.shape, facts.dtype),
            jax.ShapeDtypeStruct(text.shape, text.dtype),
        ),
        in_specs=[ANY] * 2,
        out_specs=(ANY,) * 2,
        scratch_shapes=[
            pltpu.SemaphoreType.DMA((2, count - 1)),
            pltpu.SemaphoreType.DMA((2, count - 1)),
            pltpu.SemaphoreType.DMA((2,)),
        ],
        compiler_params=pltpu.CompilerParams(collective_id=0, has_side_effects=True),
    )(facts, text)


def gather_kernel(count, shapes, sides, *refs):
    num = len(shapes)
    shards, (vec_ref, text_ref) = refs[:num], refs[num : num + 2]
    full, (vec_out, text_out) = refs[num + 2 : 2 * num + 2], refs[2 * num + 2 : 2 * num + 4]
    ring_send, ring_recv, pair_send, pair_recv, cross_send, cross_recv = refs[
        2 * num + 4 : 2 * num + 10
    ]
    own_sem, part_send, part_recv, part_own = refs[2 * num + 10 :]
    me = lax.axis_index("clip")
    band = lax.axis_index("band")
    core = band % 2
    place = ring_place(me, count)
    onward = 1 - 2 * core
    following = (ring_clip((place + onward + count) % count, count), band)
    plane = band // 2
    partner = (me, band + 1 - 2 * core)
    mirror = (me, band + 2 - 4 * plane)
    peers = [((me + step) % count, band) for step in range(1, count)]
    greet(peers + [partner, mirror])

    def block(ref, group, owner):
        rows, cols = shapes[group]
        return ref.at[
            pl.ds(pl.multiple_of(owner * rows, rows), rows),
            pl.ds(pl.multiple_of(core * (cols // 2), 128), cols // 2),
        ]

    def ring_copy(group, step):
        owner = ring_clip((place - onward * step + 2 * count) % count, count)
        there = block(full[group], group, owner)
        return pltpu.make_async_remote_copy(
            there, there, ring_send.at[step, group], ring_recv.at[step, group], following, MESH
        )

    def handed(group, step, send, recv, peer):
        owner = ring_clip((place - onward * (step + 1) + 2 * count) % count, count)
        there = block(full[group], group, owner)
        return pltpu.make_async_remote_copy(
            there, there, send.at[step, group], recv.at[step, group], peer, MESH
        )

    def pair_copy(group, step):
        return handed(group, step, pair_send, pair_recv, partner)

    def cross_copy(group, step):
        return handed(group, step, cross_send, cross_recv, mirror)

    def in_ring(group):
        def decorate(body):
            if sides[group]:
                pl.when(plane == sides[group] - 1)(body)
            else:
                body()

        return decorate

    def off_ring(group, also=None):
        def decorate(body):
            if sides[group]:
                off = plane != sides[group] - 1
                pl.when(off if also is None else jnp.logical_and(off, also))(body)

        return decorate

    def ring_arrival(group, step, onto):
        ring_copy(group, step).wait_recv()
        if onto:
            ring_copy(group, step + 1).start()
        pair_copy(group, step).start()
        if sides[group]:
            cross_copy(group, step).start()

    def cross_arrival(group, step):
        cross_copy(group, step).wait_recv()
        pair_copy(group, step).start()

    def own_copy(group):
        rows, cols = shapes[group]
        return pltpu.make_async_copy(
            shards[group],
            full[group].at[pl.ds(pl.multiple_of(me * rows, rows), rows), :],
            own_sem.at[group],
        )

    parts = []
    for step, peer in enumerate(peers):
        for which, (src, dst) in enumerate(((vec_ref, vec_out), (text_ref, text_out))):
            parts.append(
                pltpu.make_async_remote_copy(
                    src.at[peer[0]],
                    dst.at[me],
                    part_send.at[which, step],
                    part_recv.at[which, step],
                    peer,
                    MESH,
                )
            )
    parts_own = [
        pltpu.make_async_copy(src.at[me], dst.at[me], part_own.at[which])
        for which, (src, dst) in enumerate(((vec_ref, vec_out), (text_ref, text_out)))
    ]
    for group in range(num):
        rows, cols = shapes[group]
        own_copy(group).start()

        @in_ring(group)
        def _(group=group, rows=rows, cols=cols):
            pltpu.make_async_remote_copy(
                shards[group].at[:, pl.ds(pl.multiple_of(core * (cols // 2), 128), cols // 2)],
                block(full[group], group, me),
                ring_send.at[0, group],
                ring_recv.at[0, group],
                following,
                MESH,
            ).start()

    for copy in parts_own + parts:
        copy.start()

    @pl.loop(1, count - 1)
    def _(step):
        for group in range(num):

            @in_ring(group)
            def _(group=group):
                ring_arrival(group, step - 1, True)

        for group in range(num):

            @off_ring(group, step >= 2)
            def _(group=group):
                cross_arrival(group, step - 2)

    for group in range(num):

        @in_ring(group)
        def _(group=group):
            ring_arrival(group, count - 2, False)

    for late in (count - 3, count - 2):
        for group in range(num):

            @off_ring(group)
            def _(group=group, late=late):
                cross_arrival(group, late)

    for copy in parts_own + parts:
        copy.wait()
    for group in range(num):
        own_copy(group).wait()

    @pl.loop(0, count - 1)
    def _(step):
        for group in range(num):

            @in_ring(group)
            def _(group=group):
                ring_copy(group, step).wait_send()
                if sides[group]:
                    cross_copy(group, step).wait_send()

            pair_copy(group, step).wait()


def gather_quarters(shard):
    band_count = lax.axis_size("band")
    rows = shard.shape[0] // band_count
    own = lax.dynamic_slice_in_dim(shard, lax.axis_index("band") * rows, rows, 0)
    return lax.all_gather(own.astype(jnp.bfloat16), ("clip", "band"), axis=0, tiled=True)


def sum_rows(left, right):
    part = lax.psum_scatter(
        matmul_tn(left, right), ("clip", "band"), scatter_dimension=0, tiled=True
    )
    return lax.all_gather(part, "band", axis=0, tiled=True)


def gather_weights(shards, sides, vectors, texts):
    count = lax.axis_size("clip")
    num = len(shards)
    steps = pltpu.SemaphoreType.DMA((count - 1, num))
    out = pl.pallas_call(
        partial(gather_kernel, count, [shard.shape for shard in shards], sides),
        out_shape=tuple(
            jax.ShapeDtypeStruct((count * s.shape[0], s.shape[1]), s.dtype) for s in shards
        )
        + tuple(jax.ShapeDtypeStruct(v.shape, v.dtype) for v in (vectors, texts)),
        in_specs=[ANY] * (num + 2),
        out_specs=(ANY,) * (num + 2),
        scratch_shapes=[
            *[steps] * 6,
            pltpu.SemaphoreType.DMA((num,)),
            pltpu.SemaphoreType.DMA((2, count - 1)),
            pltpu.SemaphoreType.DMA((2, count - 1)),
            pltpu.SemaphoreType.DMA((2,)),
        ],
        compiler_params=pltpu.CompilerParams(collective_id=1, has_side_effects=True),
        cost_estimate=pl.CostEstimate(flops=2 * 10**11, bytes_accessed=6 * 10**8, transcendentals=0),
    )(*shards, vectors, texts)
    return out[:num], out[num], out[num + 1]


WIRE_MAX = 32767.0
WIRE_LEAST = 1e-30
UNIT = (128, 512)


def unit_parts(kind, first):
    if kind == 0:
        return ((0, 4, lambda u: u, lambda u: 0), (4, 2, lambda u: 4, lambda u: u - 3))
    return ((first, 3 - first, lambda u: u, lambda u: u), (3, 1, lambda u: 3, lambda u: u))


def carried(parts, part):
    return pl.ds(parts[part][0], parts[part][1] + part)


def reduce_kernel(count, tokens, phases, *refs):
    num = sum(len(phase["lefts"]) for phase in phases)
    lefts, rights = refs[:num], refs[num : 2 * num]
    vec_ref, kv_ref, text_ref = refs[2 * num : 2 * num + 3]
    refs = refs[2 * num + 3 :]
    wide_out, deep_out, square_out, all_vec, kv_out, kv_square = refs[:6]
    left_far, right_far = refs[6 : 6 + num], refs[6 + num : 6 + 2 * num]
    scratch = refs[6 + 2 * num :]
    left_buf, right_buf, got_low, got_scale, put_low, put_scale, plane_put = (
        scratch[2 * i : 2 * i + 2] for i in range(7)
    )
    plane_got = scratch[14 : 14 + len(phases)]
    (
        square_buf,
        left_sem,
        right_sem,
        pair_send,
        pair_recv,
        half_send,
        half_recv,
        ring_send,
        ring_recv,
        credit,
        plane_send,
        plane_recv,
        out_sem,
        out_send,
        out_recv,
        cross_put,
        cross_put_scale,
        cross_got,
        cross_got_scale,
        cross_send,
        cross_recv,
        cross_credit,
        vec_got,
        kv_got,
        vec_sum,
        all_kv,
        text_buf,
        kv_grad,
        side_own,
        side_send,
        side_recv,
        vec_send,
        vec_recv,
        vec_pair_send,
        vec_pair_recv,
        kv_own,
        kv_send,
        kv_recv,
    ) = scratch[14 + len(phases) :]
    me = lax.axis_index("clip")
    band = lax.axis_index("band")
    core = band % 2
    plane = band // 2
    place = ring_place(me, count)
    onward = 1 - 2 * core
    following = (ring_clip((place + onward + count) % count, count), band)
    preceding = (ring_clip((place - onward + count) % count, count), band)
    partner = (me, band + 1 - 2 * core)
    mirror = (me, band + 2 - 4 * plane)
    band_count = vec_got.shape[0]
    band_peers = [(me, (band + step) % band_count) for step in range(1, band_count)]
    greet([following, preceding] + band_peers)

    def owner_at(step, way):
        return ring_clip((place - way * (step + 1) + 2 * count) % count, count)

    def left_blocks(at):
        phase = phases[at]
        if phase["kind"] == 0:
            return [(b, phase["lefts"][0], b, 4) for b in range(4)] + [(4, phase["lefts"][1], 0, 1)]
        first = phase["first"]
        return [(first + i, left, 0, 1) for i, left in enumerate(phase["lefts"])]

    def right_blocks(at):
        phase = phases[at]
        if phase["kind"] == 0:
            return [(0, phase["lefts"][0], 0)] + [(1 + i, phase["lefts"][1], i) for i in range(4)]
        first = phase["first"]
        return [(first + i, phase["lefts"][i], 0) for i in range(3 - first)] + [
            (3 + i, phase["lefts"][-1], i) for i in range(3)
        ]

    def left_cols(step, way, which, many):
        width = lefts_width // count if many == 1 else deep_width // count
        start = owner_at(step, way) * width + which * 128
        return pl.ds(pl.multiple_of(start, 128), 128)

    lefts_width = lefts[phases[1]["lefts"][0]].shape[1]
    deep_width = lefts[phases[0]["lefts"][0]].shape[1]

    def pair_left(at, step):
        out = []
        for block, operand, which, many in left_blocks(at):
            cols = left_cols(step, -onward, which, many)
            out.append(
                pltpu.make_async_remote_copy(
                    lefts[operand].at[:, cols],
                    left_far[operand].at[:, cols],
                    pair_send.at[at, block, step],
                    pair_recv.at[at, block, step],
                    partner,
                    MESH,
                )
            )
        return out

    def pair_right(at):
        out = []
        for i, operand in enumerate(phases[at]["lefts"]):
            half = rights[operand].shape[1] // 2
            out.append(
                pltpu.make_async_remote_copy(
                    rights[operand].at[:, pl.ds(pl.multiple_of((1 - core) * half, 128), half)],
                    right_far[operand],
                    half_send.at[operand],
                    half_recv.at[operand],
                    partner,
                    MESH,
                )
            )
        return out

    def load_left(at, step, slot, far):
        kind = phases[at]["kind"]
        out = []
        for block, operand, which, many in left_blocks(at):
            cols = left_cols(step, onward, which, many)
            source = left_far if far else lefts
            out.append(
                pltpu.make_async_copy(
                    source[operand].at[:, cols],
                    left_buf[kind].at[slot, block, pl.ds(far * tokens, tokens), :],
                    left_sem.at[kind, slot, block, far],
                )
            )
        return out

    def load_right(at, far):
        kind = phases[at]["kind"]
        out = []
        for block, operand, which in right_blocks(at):
            if far:
                source = right_far[operand].at[:, pl.ds(which * UNIT[1], UNIT[1])]
            else:
                half = rights[operand].shape[1] // 2
                start = pl.multiple_of(core * half + which * UNIT[1], 128)
                source = rights[operand].at[:, pl.ds(start, UNIT[1])]
            out.append(
                pltpu.make_async_copy(
                    source,
                    right_buf[kind].at[block, pl.ds(far * tokens, tokens), :],
                    right_sem.at[kind, block, far],
                )
            )
        return out

    def ring_copies(at, part, slot):
        kind = phases[at]["kind"]
        units = carried(unit_parts(kind, phases[at]["first"]), part)
        return [
            pltpu.make_async_remote_copy(
                put.at[slot, units],
                got.at[slot, units],
                ring_send.at[kind, slot, part, i],
                ring_recv.at[kind, slot, part, i],
                following,
                MESH,
            )
            for i, (put, got) in enumerate(
                ((put_low[kind], got_low[kind]), (put_scale[kind], got_scale[kind]))
            )
        ]

    def split_base(at):
        return 6 if phases[at]["kind"] == 0 else 4

    def plane_copy(at, part):
        kind = phases[at]["kind"]
        start, many = unit_parts(kind, phases[at]["first"])[part][:2]
        units = pl.ds(start, many)
        return pltpu.make_async_remote_copy(
            plane_put[kind].at[units],
            plane_got[at].at[units],
            plane_send.at[at, part],
            plane_recv.at[at, part],
            mirror,
            MESH,
        )

    def split_copy(at):
        unit = split_base(at) + plane
        return pltpu.make_async_remote_copy(
            plane_put[phases[at]["kind"]].at[unit],
            plane_got[at].at[unit],
            plane_send.at[at, 2],
            plane_recv.at[at, 2],
            mirror,
            MESH,
        )

    def split_arrival(at):
        unit = split_base(at) + 1 - plane
        here = plane_got[at].at[unit]
        return pltpu.make_async_remote_copy(
            here, here, plane_send.at[at, 2], plane_recv.at[at, 2], mirror, MESH
        )

    def cross_copies(slot):
        return [
            pltpu.make_async_remote_copy(
                put.at[slot], got.at[slot], cross_send.at[slot, i], cross_recv.at[slot, i], mirror, MESH
            )
            for i, (put, got) in enumerate(
                ((cross_put, cross_got), (cross_put_scale, cross_got_scale))
            )
        ]

    def out_copies(at, unit):
        phase = phases[at]
        if phase["kind"] == 0 and unit < 4:
            half = UNIT[1]
            rows = deep_out.shape[0] // 4
            there = deep_out.at[
                pl.ds(unit * rows, rows),
                pl.ds(pl.multiple_of(phase["cols"][0] + core * half, 128), half),
            ]
        else:
            which, col = (1, unit - 4) if phase["kind"] == 0 else (unit - phase["first"], 0)
            if phase["kind"] and unit >= 3:
                which, col = len(phase["lefts"]) - 1, unit - 3
            half = rights[phase["lefts"][which]].shape[1] // 2
            start = phase["cols"][which] + core * half + col * UNIT[1]
            there = wide_out.at[:, pl.ds(pl.multiple_of(start, 128), UNIT[1])]
        here = plane_got[at].at[unit]
        return (
            pltpu.make_async_copy(here, there, out_sem.at[at, unit]),
            pltpu.make_async_remote_copy(
                here, there, out_send.at[at, unit], out_recv.at[at, unit], partner, MESH
            ),
        )

    def product(kind, slot, left, right):
        return lax.dot_general(
            left_buf[kind][slot, left],
            right_buf[kind][right],
            (((0,), (0,)), ((), ())),
            preferred_element_type=jnp.float32,
        )

    def start(copies):
        for copy in copies:
            copy.start()

    def finish(copies):
        for copy in copies:
            copy.wait()

    def take_step(at, step, first, last):
        phase = phases[at]
        kind = phase["kind"]
        slot = step % 2
        before = (step + 1) % 2
        for far in range(2):
            finish(load_left(at, step, slot, far))
        if not last:
            for copy in pair_left(at, step + 1):
                copy.wait_recv()
            for far in range(2):
                start(load_left(at, step + 1, before, far))
        parts = unit_parts(kind, phase["first"])
        theirs = split_base(at) + 1 - plane
        ours = split_base(at) + plane

        def encode(term):
            largest = jnp.maximum(jnp.max(jnp.abs(term), axis=0, keepdims=True), WIRE_LEAST)
            low = jnp.round(term * (WIRE_MAX / largest)).astype(jnp.int16)
            return low, largest * (1.0 / WIRE_MAX)

        def spend_cross():
            for copy in cross_copies(slot):
                copy.wait_send()
            pl.semaphore_wait(cross_credit, 1)

        if at or last:
            spend_cross()
        elif not first:
            pl.when(step >= 2)(spend_cross)
        low_part, scale_part = encode(
            product(kind, slot, parts[1][2](theirs), parts[1][3](theirs))
        )
        cross_put[slot] = low_part
        cross_put_scale[slot] = scale_part
        start(cross_copies(slot))
        for part, (low, many, left_of, right_of) in enumerate(parts):
            if not first:
                for copy in ring_copies(at, part, before):
                    copy.wait_recv()
            if not (first or last):

                @pl.when(step >= 2)
                def _(part=part):
                    for copy in ring_copies(at, part, slot):
                        copy.wait_send()
                    pl.semaphore_wait(credit.at[kind, part], 1)

            def settle(position, unit, term):
                if not first:
                    came = got_low[kind][before, position].astype(jnp.float32)
                    term = term + came * got_scale[kind][before, position]
                if last:
                    plane_put[kind][unit] = term
                else:
                    low_part, scale_part = encode(term)
                    put_low[kind][slot, position] = low_part
                    put_scale[kind][slot, position] = scale_part

            @pl.loop(low, low + many)
            def _(unit, left_of=left_of, right_of=right_of):
                settle(unit, unit, product(kind, slot, left_of(unit), right_of(unit)))

            if part:
                for copy in cross_copies(slot):
                    copy.wait_recv()
                came = cross_got[slot].astype(jnp.float32) * cross_got_scale[slot]
                settle(low + many, ours, product(kind, slot, left_of(ours), right_of(ours)) + came)
                final = at + 1 == len(phases)

                def credit_cross():
                    pl.semaphore_signal(
                        cross_credit, inc=1, device_id=mirror, device_id_type=MESH
                    )

                if not final or first:
                    credit_cross()
                elif not last:
                    pl.when(step < count - 2)(credit_cross)

            if last:
                plane_copy(at, part).start()
                if part:
                    split_copy(at).start()
            else:
                start(ring_copies(at, part, slot))
            if not (first or last):

                @pl.when(step < count - 2)
                def _(part=part):
                    pl.semaphore_signal(
                        credit.at[kind, part], inc=1, device_id=preceding, device_id_type=MESH
                    )

    def close(at):
        kind = phases[at]["kind"]

        def add_square(total):
            square_buf[...] += jnp.sum((total * total).reshape(UNIT[0] // 8, 8, UNIT[1]), axis=0)

        for part, (low, many, _, _) in enumerate(unit_parts(kind, phases[at]["first"])):
            plane_copy(at, part).wait()

            @pl.loop(low, low + many)
            def _(unit):
                total = plane_put[kind][unit] + plane_got[at][unit]
                plane_got[at][unit] = total
                add_square(total)

            for unit in range(low, low + many):
                start(out_copies(at, unit))
        ours = split_base(at) + plane
        split_copy(at).wait_send()
        split_arrival(at).wait_recv()
        plane_got[at][ours] = plane_put[kind][ours]
        for unit in (split_base(at), split_base(at) + 1):
            add_square(plane_got[at][unit])
            start(out_copies(at, unit))

    half_rows = pl.ds(pl.multiple_of(core * (vec_sum.shape[0] // 2), 8), vec_sum.shape[0] // 2)
    side_local = [
        pltpu.make_async_copy(vec_ref, vec_got.at[band], side_own.at[0]),
        pltpu.make_async_copy(kv_ref.at[band], kv_got.at[band], side_own.at[1]),
        pltpu.make_async_copy(text_ref, text_buf, side_own.at[2]),
    ]
    side_remote = []
    for step, peer in enumerate(band_peers):
        side_remote += [
            pltpu.make_async_remote_copy(
                vec_ref, vec_got.at[band], side_send.at[0, step], side_recv.at[0, step], peer, MESH
            ),
            pltpu.make_async_remote_copy(
                kv_ref.at[peer[1]],
                kv_got.at[band],
                side_send.at[1, step],
                side_recv.at[1, step],
                peer,
                MESH,
            ),
        ]
    vec_own = pltpu.make_async_copy(vec_sum, all_vec.at[me], side_own.at[3])

    def vec_copies(step):
        owner = ring_clip((place - onward * step + 2 * count) % count, count)
        vec = all_vec.at[owner, half_rows]
        return [
            pltpu.make_async_remote_copy(
                here, there, vec_send.at[step, i], vec_recv.at[step, i], following, MESH
            )
            for i, (here, there) in enumerate(((vec, vec), (all_kv.at[owner], all_kv.at[owner])))
        ]

    def vec_first():
        vec = all_vec.at[me, half_rows]
        return [
            pltpu.make_async_remote_copy(
                here, there, vec_send.at[0, i], vec_recv.at[0, i], following, MESH
            )
            for i, (here, there) in enumerate(
                ((vec_sum.at[half_rows], vec), (all_kv.at[me], all_kv.at[me]))
            )
        ]

    def vec_pair(step):
        owner = ring_clip((place - onward * (step + 1) + 2 * count) % count, count)
        vec = all_vec.at[owner, half_rows]
        return pltpu.make_async_remote_copy(
            vec, vec, vec_pair_send.at[step], vec_pair_recv.at[step], partner, MESH
        )

    def kv_copies():
        width = kv_grad.shape[1]
        there = kv_out.at[:, pl.ds(pl.multiple_of(band * width, 128), width)]
        return [pltpu.make_async_copy(kv_grad, there, kv_own)] + [
            pltpu.make_async_remote_copy(
                kv_grad, there, kv_send.at[step], kv_recv.at[step], peer, MESH
            )
            for step, peer in enumerate(band_peers)
        ]

    def sum_bands():
        finish(side_local + side_remote)
        vec_sum[...] = jnp.sum(vec_got[...], 0)
        all_kv[me] = jnp.sum(kv_got[...], 0)
        vec_own.start()
        start(vec_first())

    def pass_sums(step):
        for copy in vec_copies(step - 1):
            copy.wait_recv()
        start(vec_copies(step))
        vec_pair(step - 1).start()

    def multiply_text():
        for copy in vec_copies(count - 2):
            copy.wait_recv()
        vec_pair(count - 2).start()
        grads = all_kv[...].reshape(text_buf.shape[0], -1)
        total = jnp.zeros_like(kv_grad)
        for _ in range(3):
            part = grads.astype(jnp.bfloat16)
            grads = grads - part.astype(jnp.float32)
            total = total + matmul_tn(text_buf[...], part)
        kv_grad[...] = total
        kv_square[...] = jnp.sum((total * total).reshape(-1, 8, total.shape[1]), axis=0)
        start(kv_copies())

    square_buf[...] = jnp.zeros_like(square_buf)
    start(side_local + side_remote)
    start(load_right(0, 0))
    start(pair_right(0))

    @pl.loop(0, count)
    def _(step):
        start(pair_left(0, step))

    start(load_left(0, 0, 0, 0))
    for at in range(len(phases)):
        if at == 0:
            for copy in pair_right(0):
                copy.wait_recv()
            start(load_right(0, 1))
            for copy in pair_left(0, 0):
                copy.wait_recv()
            start(load_left(0, 0, 0, 1))
        for far in range(2):
            finish(load_right(at, far))
        more = at + 1 < len(phases)
        if more:
            start(pair_right(at + 1))
            start(load_right(at + 1, 0))
        take_step(at, 0, True, False)
        if at == 0:
            sum_bands()
        if more:
            start(pair_left(at + 1, 0))

        @pl.loop(1, count - 1)
        def _(step, at=at, more=more):
            take_step(at, step, False, False)
            if at == 0:
                pass_sums(step)
            if more:
                start(pair_left(at + 1, step))

        if more:
            start(pair_left(at + 1, count - 1))
            for copy in pair_right(at + 1):
                copy.wait_recv()
            start(load_right(at + 1, 1))
            for copy in pair_left(at + 1, 0):
                copy.wait_recv()
            for far in range(2):
                start(load_left(at + 1, 0, 0, far))
        take_step(at, count - 1, False, True)
        if at == 0:
            multiply_text()
        for part in range(2):
            for slot in range(2):
                for copy in ring_copies(at, part, slot):
                    copy.wait_send()
        if at:
            close(at - 1)
    close(len(phases) - 1)
    for slot in range(2):
        for copy in cross_copies(slot):
            copy.wait_send()
    vec_own.wait()
    finish(kv_copies())

    @pl.loop(0, count - 1)
    def _(step):
        for copy in vec_copies(step):
            copy.wait_send()
        vec_pair(step).wait()

    square_out[...] = square_buf[...]
    for at, phase in enumerate(phases):
        for copy in pair_right(at):
            copy.wait_send()

        @pl.loop(0, count)
        def _(step, at=at):
            for copy in pair_left(at, step):
                copy.wait_send()

        for unit in range(phase["first"], 8 if phase["kind"] == 0 else 6):
            finish(out_copies(at, unit))


def reduce_gradients(phases, lefts, rights, vectors, keyvals, text, wide_cols, deep_cols):
    count = lax.axis_size("clip")
    tokens = lefts[0].shape[0]
    wide_rows = lefts[1].shape[1] // count
    deep_rows = lefts[0].shape[1] // count
    band_count, _, kv_cols = keyvals.shape
    num = len(lefts)
    dma = pltpu.SemaphoreType.DMA
    units, lefts_of, rights_of = (8, 6), (5, 4), (5, 6)
    scratch = [pltpu.VMEM((2, lefts_of[k], 2 * tokens, 128), jnp.bfloat16) for k in range(2)]
    scratch += [pltpu.VMEM((rights_of[k], 2 * tokens, UNIT[1]), jnp.bfloat16) for k in range(2)]
    for _ in range(2):
        scratch += [pltpu.VMEM((2, units[k]) + UNIT, jnp.int16) for k in range(2)]
        scratch += [pltpu.VMEM((2, units[k], 1, UNIT[1]), jnp.float32) for k in range(2)]
    scratch += [pltpu.VMEM((units[k],) + UNIT, jnp.float32) for k in range(2)]
    scratch += [pltpu.VMEM((units[p["kind"]],) + UNIT, jnp.float32) for p in phases]
    scratch += [
        pltpu.VMEM((8, UNIT[1]), jnp.float32),
        dma((2, 2, 5, 2)),
        dma((2, 6, 2)),
        dma((len(phases), 5, count)),
        dma((len(phases), 5, count)),
        dma((num,)),
        dma((num,)),
        dma((2, 2, 2, 2)),
        dma((2, 2, 2, 2)),
        pltpu.SemaphoreType.REGULAR((2, 2)),
        dma((len(phases), 3)),
        dma((len(phases), 3)),
        dma((len(phases), 8)),
        dma((len(phases), 8)),
        dma((len(phases), 8)),
    ]
    for _ in range(2):
        scratch += [pltpu.VMEM((2,) + UNIT, jnp.int16), pltpu.VMEM((2, 1, UNIT[1]), jnp.float32)]
    scratch += [
        dma((2, 2)),
        dma((2, 2)),
        pltpu.SemaphoreType.REGULAR,
        pltpu.VMEM((band_count,) + vectors.shape, jnp.float32),
        pltpu.VMEM(keyvals.shape, jnp.float32),
        pltpu.VMEM(vectors.shape, jnp.float32),
        pltpu.VMEM((count,) + keyvals.shape[1:], jnp.float32),
        pltpu.VMEM(text.shape, jnp.bfloat16),
        pltpu.VMEM((text.shape[1], kv_cols), jnp.float32),
        dma((4,)),
        dma((2, band_count - 1)),
        dma((2, band_count - 1)),
        dma((count - 1, 2)),
        dma((count - 1, 2)),
        dma((count - 1,)),
        dma((count - 1,)),
        dma,
        dma((band_count - 1,)),
        dma((band_count - 1,)),
    ]
    out = pl.pallas_call(
        partial(reduce_kernel, count, tokens, phases),
        out_shape=(
            jax.ShapeDtypeStruct((wide_rows, wide_cols), jnp.float32),
            jax.ShapeDtypeStruct((deep_rows, deep_cols), jnp.float32),
            jax.ShapeDtypeStruct((8, UNIT[1]), jnp.float32),
            jax.ShapeDtypeStruct((count,) + vectors.shape, jnp.float32),
            jax.ShapeDtypeStruct((deep_rows, band_count * kv_cols), jnp.float32),
            jax.ShapeDtypeStruct((8, kv_cols), jnp.float32),
        )
        + tuple(jax.ShapeDtypeStruct(x.shape, x.dtype) for x in lefts)
        + tuple(jax.ShapeDtypeStruct((tokens, x.shape[1] // 2), x.dtype) for x in rights),
        in_specs=[ANY] * (2 * num + 3),
        out_specs=(ANY, ANY, IN_VMEM, ANY, ANY, IN_VMEM) + (ANY,) * (2 * num),
        scratch_shapes=scratch,
        compiler_params=pltpu.CompilerParams(
            collective_id=2, has_side_effects=True, vmem_limit_bytes=58 << 20
        ),
        cost_estimate=pl.CostEstimate(flops=3 * 10**11, bytes_accessed=8 * 10**8, transcendentals=0),
    )(*lefts, *rights, vectors, keyvals, text)
    return out[:6]


def total_kernel(count, part_ref, out_ref, mid, band_got, clip_got, *sems):
    me = lax.axis_index("clip")
    band = lax.axis_index("band")
    band_count = band_got.shape[0]
    band_peers = [(me, (band + step) % band_count) for step in range(1, band_count)]
    clip_peers = [((me + step) % count, band) for step in range(1, count)]
    greet(band_peers + clip_peers)
    stages = (
        (part_ref, band_got, band, band_peers, mid, sems[:2]),
        (mid, clip_got, me, clip_peers, out_ref, sems[2:]),
    )
    for value, got, index, peers, result, (send, recv) in stages:
        copies = [
            pltpu.make_async_remote_copy(
                value, got.at[index], send.at[step], recv.at[step], peer, MESH
            )
            for step, peer in enumerate(peers)
        ]
        for copy in copies:
            copy.start()
        got[index] = value[...]
        for copy in copies:
            copy.wait()
        result[...] = jnp.sum(got[...], 0)


def total_over_devices(value):
    count, band_count = lax.axis_size("clip"), lax.axis_size("band")
    dma = pltpu.SemaphoreType.DMA
    tile = (8, 128)
    return pl.pallas_call(
        partial(total_kernel, count),
        out_shape=jax.ShapeDtypeStruct(tile, jnp.float32),
        in_specs=[IN_VMEM],
        out_specs=IN_VMEM,
        scratch_shapes=[
            pltpu.VMEM(tile, jnp.float32),
            pltpu.VMEM((band_count,) + tile, jnp.float32),
            pltpu.VMEM((count,) + tile, jnp.float32),
            dma((band_count - 1,)),
            dma((band_count - 1,)),
            dma((count - 1,)),
            dma((count - 1,)),
        ],
        compiler_params=pltpu.CompilerParams(collective_id=3, has_side_effects=True),
    )(jnp.broadcast_to(value, tile))[0, 0]


def per_device(
    latents,
    noise_field,
    timesteps,
    null_flags,
    frame_mask,
    context,
    w_wide,
    m_wide,
    v_wide,
    w_deep,
    m_deep,
    v_deep,
    w_small,
    m_small,
    v_small,
):
    clip_count = lax.axis_size("clip")
    band_count = lax.axis_size("band")
    clip_at = lax.axis_index("clip")
    band_at = lax.axis_index("band")
    wide_rows = w_wide.shape[0]
    deep_rows = w_deep.shape[0]
    text_len, text_dim = context.shape[1:]
    facts = jnp.pad(
        jnp.concatenate([timesteps, frame_mask[0]])[None],
        ((0, 7), (0, 127 - frame_mask.shape[1])),
    )
    kept_text = context[0] * (1 - null_flags[0]).astype(jnp.bfloat16)
    text_cols = jnp.pad(
        kept_text.reshape(text_len, clip_count, deep_rows).transpose(1, 0, 2),
        ((0, 0), (0, TEXT_PAD - text_len), (0, 0)),
    )
    all_facts, all_text = exchange_facts(facts, text_cols)
    all_times = all_facts[:, 0, 0].astype(jnp.float32)
    all_time_low = jax.nn.silu(time_features(all_times)).astype(jnp.bfloat16)
    time_rows = lax.dynamic_slice(
        all_time_low, (0, clip_at * wide_rows), (clip_count, wide_rows)
    )
    part_modul = matmul(time_rows, w_wide[:, : 12 * D].astype(jnp.bfloat16))
    kv_cols = 2 * D // band_count
    kv_weight = lax.dynamic_slice(
        w_deep, (0, D + band_at * kv_cols), (deep_rows, kv_cols)
    ).astype(jnp.bfloat16)
    part_kv = matmul(all_text.reshape(clip_count * TEXT_PAD, deep_rows), kv_weight)
    edges = (12 * D, 15 * D, 18 * D, 19 * D, 20 * D, 21 * D, 22 * D, 22 * D + FF)
    shards = [w_wide[:, low:high].astype(jnp.bfloat16) for low, high in zip(edges, edges[1:])]
    shards += [w_deep[:, :D].astype(jnp.bfloat16)]
    up_b_w = gather_quarters(w_wide[:, 22 * D + FF :])
    down_b_w = gather_quarters(w_deep[:, 3 * D :])
    gathered, all_modul, all_kv = gather_weights(
        shards,
        (0, 0, 1, 2, 1, 2, 1, 2),
        part_modul.reshape(clip_count, 12 * D // 128, 128),
        part_kv.reshape(clip_count, TEXT_PAD, kv_cols),
    )
    (
        qkv_a_w,
        qkv_b_w,
        out_a_w,
        out_b_w,
        query_w,
        cross_out_w,
        up_a_w,
        down_a_w,
    ) = gathered
    keyval = lax.all_gather(jnp.sum(all_kv, 0).astype(jnp.bfloat16), "band", axis=1, tiled=True)
    small_low = w_small.astype(jnp.bfloat16)
    small_val = small_low.astype(jnp.float32)
    num_frames, num_rows, num_cols = (latents.shape[1], latents.shape[2], latents.shape[3])
    tok_count = num_frames * num_rows * num_cols
    all_mask = all_facts[:, 0, 1 : 1 + num_frames]
    global_count = jnp.sum(all_mask).astype(jnp.float32) * (num_rows * num_cols * CH * band_count)
    time_value = timesteps[0].astype(jnp.float32)
    noise_angle = 0.5 * math.pi * time_value / TMAX
    signal, spread = (jnp.cos(noise_angle), jnp.sin(noise_angle))
    clean_tok = token_order(latents[0])
    noise_tok = token_order(noise_field[0])
    run = num_rows * WIN
    part = SHIFT * WIN
    frame_windows = attend_pieces(tok_count, num_frames, "frame")
    half_windows = attend_pieces(tok_count, num_frames, "half")
    text_windows = attend_pieces(tok_count, num_frames, "text")
    noisy_low = (signal * clean_tok + spread * noise_tok).astype(jnp.bfloat16)
    target = signal * noise_tok - spread * clean_tok
    modulation = jnp.sum(all_modul, 0).reshape(12, D)
    mod_a, mod_b = (modulation[:6], modulation[6:])
    stream_zero = matmul(noisy_low, small_low[:CH]) + small_val[2 * CH]
    normed_a, back_a = jax.vjp(norm_modulated, stream_zero, mod_a[0], mod_a[1])
    in_a = normed_a.astype(jnp.bfloat16)
    qkv_a = matmul(in_a, qkv_a_w).astype(jnp.bfloat16)
    far_kv = from_partner(qkv_a[:, D:], "band", 0)
    space_kv = [(qkv_a, HEADS // 2, HEADS), (far_kv, 0, HEADS // 2)]
    att_a = attend(qkv_a, space_kv, frame_windows)
    proj_a = matmul(att_a, out_a_w)
    stream_one = stream_zero + mod_a[2] * proj_a
    stream_two, saved_a = mlp_forward(stream_one, mod_a, up_a_w, down_a_w)
    normed_b, back_b = jax.vjp(norm_modulated, stream_two, mod_b[0], mod_b[1])
    low_b = normed_b.astype(jnp.bfloat16)
    rolled = with_rows(low_b, shifted(first_rows(low_b, run, part), "band", -1), run)
    qkv_b = matmul(rolled, qkv_b_w).astype(jnp.bfloat16)
    win_kv = [(qkv_b, HEADS // 2, HEADS)]
    win_out = attend(qkv_b, win_kv, half_windows)
    att_b = with_rows(win_out, shifted(first_rows(win_out, run, part), "band", 1), run)
    proj_b = matmul(att_b, out_b_w)
    stream_three = stream_two + mod_b[2] * proj_b
    cross_val, cross_back = jax.vjp(norm_gained, stream_three, small_val[2 * CH + 1])
    cross_in = cross_val.astype(jnp.bfloat16)
    query_proj = matmul(cross_in, query_w).astype(jnp.bfloat16)
    text_kv = [(keyval, 0, HEADS // 2)]
    crossed = attend(query_proj, text_kv, text_windows, text_len)
    stream_four = stream_three + matmul(crossed, cross_out_w)
    stream_five, saved_b = mlp_forward(stream_four, mod_b, up_b_w, down_b_w)
    final_val, final_back = jax.vjp(norm_gained, stream_five, small_val[2 * CH + 2])
    final_low = final_val.astype(jnp.bfloat16)
    head_low = small_low[CH : 2 * CH]
    predicted = matmul_nt(final_low, head_low)
    weight_row = jnp.repeat(frame_mask[0].astype(jnp.float32), run)
    weight_row = jnp.tile(weight_row, num_cols // WIN)[:, None]
    pred_error = predicted - target
    loss_part = jnp.sum(weight_row * pred_error * pred_error)
    grad_pred = (weight_row * pred_error * (2.0 / global_count)).astype(jnp.bfloat16)
    grad_head = matmul_tn(grad_pred, final_low)
    grad_stream, grad_gain_f = final_back(matmul(grad_pred, head_low))
    grad_stream, mlp_factors_b, extra_b = mlp_backward(
        grad_stream, mod_b, up_b_w, down_b_w, saved_b
    )
    grad_cross = grad_stream.astype(jnp.bfloat16)
    grad_crossed = matmul_nt(grad_cross, cross_out_w).astype(jnp.bfloat16)
    grad_query, grad_keyval = attend_back(
        query_proj, text_kv, grad_crossed, text_windows, text_len
    )
    grad_part, grad_gain_c = cross_back(matmul_nt(grad_query, query_w))
    grad_stream = grad_stream + grad_part
    grad_proj = (mod_b[2] * grad_stream).astype(jnp.bfloat16)
    grad_gate_b = jnp.sum(grad_stream * proj_b, 0)
    factors_ob = (att_b, grad_proj)
    grad_att = matmul_nt(grad_proj, out_b_w).astype(jnp.bfloat16)
    grad_win = with_rows(grad_att, shifted(first_rows(grad_att, run, part), "band", -1), run)
    grad_qkv = attend_back(qkv_b, win_kv, grad_win, half_windows)[0]
    factors_qkvb = (rolled, grad_qkv)
    grad_in_roll = matmul_nt(grad_qkv, qkv_b_w)
    sent_back = shifted(first_rows(grad_in_roll, run, part), "band", 1)
    grad_normed = with_rows(grad_in_roll, sent_back, run)
    grad_part, grad_shift_b, grad_scale_b = back_b(grad_normed)
    grad_stream = grad_stream + grad_part
    grad_stream, mlp_factors_a, extra_a = mlp_backward(
        grad_stream, mod_a, up_a_w, down_a_w, saved_a
    )
    grad_proj = (mod_a[2] * grad_stream).astype(jnp.bfloat16)
    grad_gate_a = jnp.sum(grad_stream * proj_a, 0)
    factors_oa = (att_a, grad_proj)
    grad_att = matmul_nt(grad_proj, out_a_w).astype(jnp.bfloat16)
    grad_q, grad_own, grad_far = attend_back(qkv_a, space_kv, grad_att, frame_windows)
    grad_kv = grad_own + from_partner(grad_far, "band", 0)
    grad_qkv = jnp.concatenate([grad_q, grad_kv.astype(jnp.bfloat16)], 1)
    factors_qkva = (in_a, grad_qkv)
    grad_part, grad_shift_a, grad_scale_a = back_a(matmul_nt(grad_qkv, qkv_a_w))
    grad_stream = grad_stream + grad_part
    grad_patch = matmul_tn(noisy_low.astype(jnp.float32), grad_stream, lax.Precision.HIGHEST)
    grad_bias = jnp.sum(grad_stream, 0)
    grad_modul = jnp.stack(
        [
            grad_shift_a,
            grad_scale_a,
            grad_gate_a,
            extra_a[0],
            extra_a[1],
            extra_a[2],
            grad_shift_b,
            grad_scale_b,
            grad_gate_b,
            extra_b[0],
            extra_b[1],
            extra_b[2],
        ]
    ).reshape(1, 12 * D)
    grad_small = jnp.concatenate(
        [grad_patch, grad_head, grad_bias[None], grad_gain_c[None], grad_gain_f[None]], 0
    )
    factors = mlp_factors_b + (
        (crossed, grad_cross),
        (cross_in, grad_query),
        factors_ob,
        factors_qkvb,
    )
    factors += mlp_factors_a + (factors_oa, factors_qkva)
    if wide_rows == 128 and deep_rows == 512:
        phases = (
            {"kind": 0, "first": 0, "lefts": (0, 1), "cols": (D, 10 * D + FF)},
            {"kind": 1, "first": 0, "lefts": (2, 3, 4, 5), "cols": (9 * D, 8 * D, 7 * D, 3 * D)},
            {"kind": 0, "first": 0, "lefts": (6, 7), "cols": (0, 10 * D)},
            {"kind": 1, "first": 2, "lefts": (8, 9), "cols": (6 * D, 0)},
        )
        used = 12 * D + grad_small.size
        vectors = jnp.concatenate(
            [grad_modul.reshape(-1), grad_small.reshape(-1), loss_part[None]]
        )
        vectors = jnp.pad(vectors, (0, 256 * 128 - vectors.shape[0])).reshape(256, 128)
        keyvals = grad_keyval.reshape(TEXT_PAD, band_count, kv_cols).transpose(1, 0, 2)
        wide_rest, deep_rest, squares, all_vectors, grad_w_ckv, kv_squares = reduce_gradients(
            phases,
            [f[0] for f in factors],
            [f[1] for f in factors],
            vectors,
            keyvals,
            all_text.reshape(clip_count * TEXT_PAD, deep_rows),
            10 * D + 2 * FF,
            2 * D,
        )
        all_vectors = all_vectors.reshape(clip_count, -1)
        all_grad_modul = all_vectors[:, : 12 * D]
        small_sum = jnp.sum(all_vectors[:, 12 * D : used], 0).reshape(grad_small.shape)
        loss_sum = jnp.sum(all_vectors[:, used])
        square_part = jnp.sum(squares) / (band_count // 2) + jnp.sum(kv_squares)
    else:
        summed = [sum_rows(*pair) for pair in factors]
        wide_rest = jnp.concatenate([summed[i] for i in (9, 5, 8, 4, 3, 2, 7, 1)], 1)
        deep_rest = jnp.concatenate([summed[6], summed[0]], 1)
        grad_keyval = lax.psum_scatter(grad_keyval, "band", scatter_dimension=1, tiled=True)
        grad_keyval = lax.all_gather(grad_keyval, "clip", axis=0, tiled=True)
        grad_w_ckv = matmul_tn(
            all_text.reshape(clip_count * TEXT_PAD, deep_rows).astype(jnp.float32),
            grad_keyval,
            lax.Precision.HIGHEST,
        )
        grad_w_ckv = lax.all_gather(grad_w_ckv, "band", axis=1, tiled=True)
        all_grad_modul = lax.all_gather(lax.psum(grad_modul, "band"), "clip", axis=0, tiled=True)
        loss_sum, small_sum = lax.psum((loss_part, grad_small), ("clip", "band"))
        square_part = sum(jnp.sum(x * x) for x in (wide_rest, deep_rest, grad_w_ckv)) / band_count
    grad_w_ada = matmul_tn(time_rows.astype(jnp.float32), all_grad_modul, lax.Precision.HIGHEST)
    wide_sum = jnp.concatenate([grad_w_ada, wide_rest], 1)
    deep_sum = jnp.concatenate([deep_rest[:, :D], grad_w_ckv, deep_rest[:, D:]], 1)
    square_part += jnp.sum(grad_w_ada * grad_w_ada) / band_count
    square_sum = total_over_devices(square_part)
    grad_norm = jnp.sqrt(square_sum + jnp.sum(small_sum * small_sum))
    factor = CLIP_MAX / jnp.maximum(grad_norm, CLIP_MAX)
    new_wide = adam_update(w_wide, m_wide, v_wide, wide_sum * factor, 0.15)
    new_deep = adam_update(w_deep, m_deep, v_deep, deep_sum * factor, 0.05)
    new_small = adam_update(w_small, m_small, v_small, small_sum * factor, 0.5)
    loss = loss_sum / global_count
    return (
        loss,
        grad_norm,
        new_wide[0],
        new_wide[1],
        new_wide[2],
        new_deep[0],
        new_deep[1],
        new_deep[2],
        new_small[0],
        new_small[1],
        new_small[2],
    )


def solution(mesh):
    in_specs = (
        P("clip", None, "band", None, None),
        P("clip", None, "band", None, None),
        P("clip"),
        P("clip"),
        P("clip", None),
        P("clip", None, None),
        P("clip", None),
        P("clip", None),
        P("clip", None),
        P("clip", None),
        P("clip", None),
        P("clip", None),
        P(),
        P(),
        P(),
    )
    out_specs = (
        P(),
        P(),
        P("clip", None),
        P("clip", None),
        P("clip", None),
        P("clip", None),
        P("clip", None),
        P("clip", None),
        P(),
        P(),
        P(),
    )
    return jax.shard_map(
        per_device, mesh=mesh, in_specs=in_specs, out_specs=out_specs, check_vma=False
    )
```

```python
from functools import partial
import math

import jax
import jax.numpy as jnp
from jax import lax
from jax.experimental import pallas as pl
from jax.experimental.pallas import tpu as pltpu
from jax.sharding import PartitionSpec as P

D = 1024
HEADS = 16
HEAD_DIM = 64
FF = 4096
CH = 8
SPACE = 16
WIN = 8
SHIFT = 4
TMAX = 1000
STEP = 10


EPS_NORM = 1e-06
CLIP_MAX = 0.001
BETA_ONE = 0.9
BETA_TWO = 0.95
ADAM_EPS = 1e-08
DECAY = 0.1


def from_partner(block, axis, distance):
    count = lax.axis_size(axis)
    route = []
    for low in range(count):
        high = low | 1 << distance
        if high != low and high < count:
            route += [(low, high), (high, low)]
    return lax.ppermute(block, axis, route)


def shifted(value, axis, by):
    length = lax.axis_size(axis)
    return lax.ppermute(value, axis, [(i, (i + by) % length) for i in range(length)])


def matmul(left_op, right_op):
    return jnp.dot(left_op, right_op, preferred_element_type=jnp.float32)


def matmul_tn(left_op, right_op, precision=None):
    return lax.dot_general(
        left_op,
        right_op,
        (((0,), (0,)), ((), ())),
        precision=precision,
        preferred_element_type=jnp.float32,
    )


def matmul_nt(left_op, right_op):
    return lax.dot_general(
        left_op, right_op, (((1,), (1,)), ((), ())), preferred_element_type=jnp.float32
    )


def layer_norm(field_in):
    average = jnp.mean(field_in, -1, keepdims=True)
    centred = field_in - average
    return centred * lax.rsqrt(jnp.mean(centred * centred, -1, keepdims=True) + EPS_NORM)


def norm_modulated(field_in, shift_vec, scale_vec):
    return layer_norm(field_in) * (1.0 + scale_vec) + shift_vec


def norm_gained(field_in, gain_vec):
    return layer_norm(field_in) * gain_vec


def time_features(time_value):
    half_width = D // 2
    frequency = jnp.exp(-math.log(10000.0) * jnp.arange(half_width, dtype=jnp.float32) / half_width)
    angles = time_value[..., None] * frequency
    return jnp.concatenate([jnp.cos(angles), jnp.sin(angles)], -1)


def token_order(grid):
    frames, rows, cols, width = grid.shape
    halves = grid.reshape(frames, rows, cols // WIN, WIN, width).transpose(2, 0, 1, 3, 4)
    return halves.reshape(frames * rows * cols, width)


def with_rows(tokens, first_rows, run):
    width = tokens.shape[1]
    runs = tokens.reshape(-1, run, width)
    return jnp.concatenate([first_rows, runs[:, first_rows.shape[1] :]], 1).reshape(-1, width)


def first_rows(tokens, run, part):
    return tokens.reshape(-1, run, tokens.shape[1])[:, :part]


def attend_pieces(tokens, frames, keys):
    if keys == "frame":
        run = tokens // (2 * frames)
        return [((f * run, run), (tokens // 2 + f * run, run)) for f in range(frames)]
    if keys == "half":
        return [((half * (tokens // 2), tokens // 2),) for half in range(2)]
    return [((0, tokens),)]


def take(ref, runs):
    pieces = [ref[low : low + many, :] for low, many in runs]
    return pieces[0] if len(pieces) == 1 else jnp.concatenate(pieces, 0)


def put(ref, cols, runs, value):
    done = 0
    for low, many in runs:
        ref[low : low + many, cols] = value[done : done + many].astype(ref.dtype)
        done += many


def softmax_rows(queries, keys, text_len):
    scores = matmul_nt(queries, keys)
    if text_len:
        place = lax.broadcasted_iota(jnp.int32, scores.shape, 1)
        scores = jnp.where(place < text_len, scores, -1e30)
    weight = jnp.exp(scores - jnp.max(scores, -1, keepdims=True))
    return weight / jnp.sum(weight, -1, keepdims=True)


def lanes_of(head, shape):
    lane = lax.broadcasted_iota(jnp.int32, shape, 1)
    return lane < HEAD_DIM if head == 0 else lane >= HEAD_DIM


def only(head, value):
    return jnp.where(lanes_of(head, value.shape), value, jnp.zeros_like(value))


def key_sets(key_refs, runs, text_len):
    if text_len:
        return key_refs[0][...]
    pieces = [take(ref, runs) for ref in key_refs]
    return pieces[0] if len(pieces) == 1 else jnp.concatenate(pieces, 0)


def attend_kernel(windows, text_len, sets, *refs):
    q_ref, k_refs, v_refs, out_ref = refs[0], refs[1 : 1 + sets], refs[1 + sets : 1 + 2 * sets], refs[-1]
    for runs in windows:
        queries = take(q_ref, runs) * HEAD_DIM ** (-0.5)
        keys, values = key_sets(k_refs, runs, text_len), key_sets(v_refs, runs, text_len)
        outs = []
        for head in range(2):
            probs = softmax_rows(only(head, queries), keys, text_len)
            outs.append(matmul(probs.astype(jnp.bfloat16), values))
        put(out_ref, slice(None), runs, jnp.where(lanes_of(0, outs[0].shape), *outs))


def attend_back_kernel(windows, text_len, sets, *refs):
    q_ref, k_refs, v_refs = refs[0], refs[1 : 1 + sets], refs[1 + sets : 1 + 2 * sets]
    grad_ref = refs[1 + 2 * sets]
    dq_ref = refs[2 + 2 * sets]
    own_ref = refs[3 + 2 * sets] if len(refs) > 3 + 2 * sets else None
    far_ref = refs[4 + 2 * sets] if sets == 2 else None
    pair = pl.program_id(0)
    cols = [pl.ds(pl.multiple_of(i * D + pair * 2 * HEAD_DIM, 128), 2 * HEAD_DIM) for i in range(3)]
    merged = dq_ref.shape[1] == 3 * D
    for runs in windows:
        queries = take(q_ref, runs) * HEAD_DIM ** (-0.5)
        keys, values = key_sets(k_refs, runs, text_len), key_sets(v_refs, runs, text_len)
        grad_out = take(grad_ref, runs)
        dq, dk, dv = [], [], []
        for head in range(2):
            probs = softmax_rows(only(head, queries), keys, text_len)
            dprobs = matmul_nt(only(head, grad_out), values)
            dv.append(matmul_tn(probs.astype(jnp.bfloat16), grad_out))
            inner = jnp.sum(probs * dprobs, -1, keepdims=True)
            dscores = (probs * (dprobs - inner)).astype(jnp.bfloat16)
            dq.append(matmul(dscores, keys))
            dk.append(matmul_tn(dscores, queries))
        dq, dk, dv = (jnp.where(lanes_of(0, x[0].shape), *x) for x in (dq, dk, dv))
        put(dq_ref, cols[0], runs, dq * HEAD_DIM ** (-0.5))
        if merged:
            put(dq_ref, cols[1], runs, dk)
            put(dq_ref, cols[2], runs, dv)
        elif text_len:
            own_ref[:, cols[0]] = dk
            own_ref[:, cols[1]] = dv
        else:
            half = dk.shape[0] // 2
            put(own_ref, cols[0], runs, dk[:half])
            put(own_ref, cols[1], runs, dv[:half])
            put(far_ref, cols[0], runs, dk[half:])
            put(far_ref, cols[1], runs, dv[half:])


def head_cols(array, first):
    return array, pl.BlockSpec((array.shape[0], 2 * HEAD_DIM), lambda h: (0, first + h))


def attention_operands(queries, key_values):
    ins = [head_cols(queries, 0)]
    ins += [head_cols(array, first) for array, first, _ in key_values]
    return ins + [head_cols(array, second) for array, _, second in key_values]


def attention_cost(tokens, keys, products):
    flops = 2 * products * tokens * keys * D * 2
    return pl.CostEstimate(
        flops=flops, bytes_accessed=tokens * D * 2 * 8, transcendentals=tokens * keys * HEADS
    )


def attend(queries, key_values, windows, text_len=0):
    tokens = queries.shape[0]
    ins = attention_operands(queries, key_values)
    return pl.pallas_call(
        partial(attend_kernel, windows, text_len, len(key_values)),
        grid=(HEADS // 2,),
        in_specs=[spec for _, spec in ins],
        out_specs=pl.BlockSpec((tokens, 2 * HEAD_DIM), lambda h: (0, h)),
        out_shape=jax.ShapeDtypeStruct((tokens, D), jnp.bfloat16),
        compiler_params=pltpu.CompilerParams(vmem_limit_bytes=40 << 20),
        cost_estimate=attention_cost(tokens, 320, 2),
    )(*[array for array, _ in ins])


def attend_back(queries, key_values, grad_out, windows, text_len=0):
    tokens = queries.shape[0]
    ins = attention_operands(queries, key_values) + [head_cols(grad_out, 0)]
    sets = len(key_values)
    whole = lambda rows, cols: pl.BlockSpec((rows, cols), lambda h: (0, 0))
    if sets == 1 and not text_len:
        outs = [((tokens, 3 * D), jnp.bfloat16)]
    else:
        rows = key_values[0][0].shape[0]
        outs = [((tokens, D), jnp.bfloat16)] + [((rows, 2 * D), jnp.float32)] * sets
    return pl.pallas_call(
        partial(attend_back_kernel, windows, text_len, sets),
        grid=(HEADS // 2,),
        in_specs=[spec for _, spec in ins],
        out_specs=[whole(*shape) for shape, _ in outs],
        out_shape=[jax.ShapeDtypeStruct(*out) for out in outs],
        compiler_params=pltpu.CompilerParams(vmem_limit_bytes=50 << 20),
        cost_estimate=attention_cost(tokens, 320, 5),
    )(*[array for array, _ in ins])


def mlp_forward(stream, modul, up_weight, down_weight):
    mlp_val, norm_back = jax.vjp(norm_modulated, stream, modul[3], modul[4])
    mlp_in = mlp_val.astype(jnp.bfloat16)
    up_proj = matmul(mlp_in, up_weight)
    share = 0.5 + 0.5 * lax.erf(up_proj * math.sqrt(0.5))
    gelu_val = up_proj * share
    slope = share + up_proj * (jnp.exp(-0.5 * up_proj * up_proj) / math.sqrt(2.0 * math.pi))
    gelu_low = gelu_val.astype(jnp.bfloat16)
    down_proj = matmul(gelu_low, down_weight)
    return (stream + modul[5] * down_proj, (norm_back, mlp_in, slope, gelu_low, down_proj))


def mlp_backward(grad_stream, modul, up_weight, down_weight, saved):
    norm_back, mlp_in, slope, gelu_low, down_proj = saved
    grad_down = (modul[5] * grad_stream).astype(jnp.bfloat16)
    grad_gate = jnp.sum(grad_stream * down_proj, 0)
    grad_up = (slope * matmul_nt(grad_down, down_weight)).astype(jnp.bfloat16)
    grad_part, grad_shift, grad_scale = norm_back(matmul_nt(grad_up, up_weight))
    factors = ((gelu_low, grad_down), (mlp_in, grad_up))
    return (grad_stream + grad_part, factors, (grad_shift, grad_scale, grad_gate))


def adam_update(weight, first_mom, second_mom, grad_val, learn_rate):
    first_mom = BETA_ONE * first_mom + (1.0 - BETA_ONE) * grad_val
    second_mom = BETA_TWO * second_mom + (1.0 - BETA_TWO) * grad_val * grad_val
    first_hat = first_mom / (1.0 - BETA_ONE**STEP)
    second_hat = second_mom / (1.0 - BETA_TWO**STEP)
    weight = weight - learn_rate * (first_hat / (jnp.sqrt(second_hat) + ADAM_EPS) + DECAY * weight)
    return (weight, first_mom, second_mom)

MESH = pl.DeviceIdType.MESH
ANY = pl.BlockSpec(memory_space=pl.ANY)
IN_VMEM = pl.BlockSpec(memory_space=pltpu.VMEM)
TEXT_PAD = 80


def ring_place(clip, count):
    half = clip // 2
    odd = clip % 2
    return half + odd * (count - 1 - 2 * half)


def ring_clip(place, count):
    far = place // (count // 2)
    return (1 - far) * 2 * place + far * (2 * (count - 1 - place) + 1)


def greet(peers):
    barrier = pltpu.get_barrier_semaphore()
    for peer in peers:
        pl.semaphore_signal(barrier, inc=1, device_id=peer, device_id_type=MESH)
    pl.semaphore_wait(barrier, len(peers))


def exchange_kernel(count, facts_ref, text_ref, facts_out, text_out, send, recv, local):
    me = lax.axis_index("clip")
    band = lax.axis_index("band")
    peers = [((me + step) % count, band) for step in range(1, count)]
    greet(peers)
    own = [
        pltpu.make_async_copy(facts_ref, facts_out.at[me], local.at[0]),
        pltpu.make_async_copy(text_ref.at[me], text_out.at[me], local.at[1]),
    ]
    for copy in own:
        copy.start()
    sent = []
    for step, peer in enumerate(peers):
        sent += [
            pltpu.make_async_remote_copy(
                facts_ref, facts_out.at[me], send.at[0, step], recv.at[0, step], peer, MESH
            ),
            pltpu.make_async_remote_copy(
                text_ref.at[peer[0]], text_out.at[me], send.at[1, step], recv.at[1, step], peer, MESH
            ),
        ]
    for copy in sent:
        copy.start()
    for copy in own + sent:
        copy.wait()


def exchange_facts(facts, text):
    count = lax.axis_size("clip")
    return pl.pallas_call(
        partial(exchange_kernel, count),
        out_shape=(
            jax.ShapeDtypeStruct((count,) + facts.shape, facts.dtype),
            jax.ShapeDtypeStruct(text.shape, text.dtype),
        ),
        in_specs=[ANY] * 2,
        out_specs=(ANY,) * 2,
        scratch_shapes=[
            pltpu.SemaphoreType.DMA((2, count - 1)),
            pltpu.SemaphoreType.DMA((2, count - 1)),
            pltpu.SemaphoreType.DMA((2,)),
        ],
        compiler_params=pltpu.CompilerParams(collective_id=0, has_side_effects=True),
    )(facts, text)


def gather_kernel(count, shapes, sides, *refs):
    num = len(shapes)
    shards, (vec_ref, text_ref) = refs[:num], refs[num : num + 2]
    full, (vec_out, text_out) = refs[num + 2 : 2 * num + 2], refs[2 * num + 2 : 2 * num + 4]
    ring_send, ring_recv, pair_send, pair_recv, cross_send, cross_recv = refs[
        2 * num + 4 : 2 * num + 10
    ]
    own_sem, part_send, part_recv, part_own = refs[2 * num + 10 :]
    me = lax.axis_index("clip")
    band = lax.axis_index("band")
    core = band % 2
    place = ring_place(me, count)
    onward = 1 - 2 * core
    following = (ring_clip((place + onward + count) % count, count), band)
    plane = band // 2
    partner = (me, band + 1 - 2 * core)
    mirror = (me, band + 2 - 4 * plane)
    peers = [((me + step) % count, band) for step in range(1, count)]
    greet(peers + [partner, mirror])

    def block(ref, group, owner):
        rows, cols = shapes[group]
        return ref.at[
            pl.ds(pl.multiple_of(owner * rows, rows), rows),
            pl.ds(pl.multiple_of(core * (cols // 2), 128), cols // 2),
        ]

    def ring_copy(group, step):
        owner = ring_clip((place - onward * step + 2 * count) % count, count)
        there = block(full[group], group, owner)
        return pltpu.make_async_remote_copy(
            there, there, ring_send.at[step, group], ring_recv.at[step, group], following, MESH
        )

    def handed(group, step, send, recv, peer):
        owner = ring_clip((place - onward * (step + 1) + 2 * count) % count, count)
        there = block(full[group], group, owner)
        return pltpu.make_async_remote_copy(
            there, there, send.at[step, group], recv.at[step, group], peer, MESH
        )

    def pair_copy(group, step):
        return handed(group, step, pair_send, pair_recv, partner)

    def cross_copy(group, step):
        return handed(group, step, cross_send, cross_recv, mirror)

    def in_ring(group):
        def decorate(body):
            if sides[group]:
                pl.when(plane == sides[group] - 1)(body)
            else:
                body()

        return decorate

    def off_ring(group, also=None):
        def decorate(body):
            if sides[group]:
                off = plane != sides[group] - 1
                pl.when(off if also is None else jnp.logical_and(off, also))(body)

        return decorate

    def ring_arrival(group, step, onto):
        ring_copy(group, step).wait_recv()
        if onto:
            ring_copy(group, step + 1).start()
        pair_copy(group, step).start()
        if sides[group]:
            cross_copy(group, step).start()

    def cross_arrival(group, step):
        cross_copy(group, step).wait_recv()
        pair_copy(group, step).start()

    def own_copy(group):
        rows, cols = shapes[group]
        return pltpu.make_async_copy(
            shards[group],
            full[group].at[pl.ds(pl.multiple_of(me * rows, rows), rows), :],
            own_sem.at[group],
        )

    parts = []
    for step, peer in enumerate(peers):
        for which, (src, dst) in enumerate(((vec_ref, vec_out), (text_ref, text_out))):
            parts.append(
                pltpu.make_async_remote_copy(
                    src.at[peer[0]],
                    dst.at[me],
                    part_send.at[which, step],
                    part_recv.at[which, step],
                    peer,
                    MESH,
                )
            )
    parts_own = [
        pltpu.make_async_copy(src.at[me], dst.at[me], part_own.at[which])
        for which, (src, dst) in enumerate(((vec_ref, vec_out), (text_ref, text_out)))
    ]
    for group in range(num):
        rows, cols = shapes[group]
        own_copy(group).start()

        @in_ring(group)
        def _(group=group, rows=rows, cols=cols):
            pltpu.make_async_remote_copy(
                shards[group].at[:, pl.ds(pl.multiple_of(core * (cols // 2), 128), cols // 2)],
                block(full[group], group, me),
                ring_send.at[0, group],
                ring_recv.at[0, group],
                following,
                MESH,
            ).start()

    for copy in parts_own + parts:
        copy.start()

    @pl.loop(1, count - 1)
    def _(step):
        for group in range(num):

            @in_ring(group)
            def _(group=group):
                ring_arrival(group, step - 1, True)

        for group in range(num):

            @off_ring(group, step >= 2)
            def _(group=group):
                cross_arrival(group, step - 2)

    for group in range(num):

        @in_ring(group)
        def _(group=group):
            ring_arrival(group, count - 2, False)

    for late in (count - 3, count - 2):
        for group in range(num):

            @off_ring(group)
            def _(group=group, late=late):
                cross_arrival(group, late)

    for copy in parts_own + parts:
        copy.wait()
    for group in range(num):
        own_copy(group).wait()

    @pl.loop(0, count - 1)
    def _(step):
        for group in range(num):

            @in_ring(group)
            def _(group=group):
                ring_copy(group, step).wait_send()
                if sides[group]:
                    cross_copy(group, step).wait_send()

            pair_copy(group, step).wait()


def gather_quarters(shard):
    band_count = lax.axis_size("band")
    rows = shard.shape[0] // band_count
    own = lax.dynamic_slice_in_dim(shard, lax.axis_index("band") * rows, rows, 0)
    return lax.all_gather(own.astype(jnp.bfloat16), ("clip", "band"), axis=0, tiled=True)


def sum_rows(left, right):
    part = lax.psum_scatter(
        matmul_tn(left, right), ("clip", "band"), scatter_dimension=0, tiled=True
    )
    return lax.all_gather(part, "band", axis=0, tiled=True)


def gather_weights(shards, sides, vectors, texts):
    count = lax.axis_size("clip")
    num = len(shards)
    steps = pltpu.SemaphoreType.DMA((count - 1, num))
    out = pl.pallas_call(
        partial(gather_kernel, count, [shard.shape for shard in shards], sides),
        out_shape=tuple(
            jax.ShapeDtypeStruct((count * s.shape[0], s.shape[1]), s.dtype) for s in shards
        )
        + tuple(jax.ShapeDtypeStruct(v.shape, v.dtype) for v in (vectors, texts)),
        in_specs=[ANY] * (num + 2),
        out_specs=(ANY,) * (num + 2),
        scratch_shapes=[
            *[steps] * 6,
            pltpu.SemaphoreType.DMA((num,)),
            pltpu.SemaphoreType.DMA((2, count - 1)),
            pltpu.SemaphoreType.DMA((2, count - 1)),
            pltpu.SemaphoreType.DMA((2,)),
        ],
        compiler_params=pltpu.CompilerParams(collective_id=1, has_side_effects=True),
        cost_estimate=pl.CostEstimate(flops=2 * 10**11, bytes_accessed=6 * 10**8, transcendentals=0),
    )(*shards, vectors, texts)
    return out[:num], out[num], out[num + 1]


WIRE_MAX = 32767.0
WIRE_LEAST = 1e-30
UNIT = (128, 512)


def unit_parts(kind, first):
    if kind == 0:
        return ((0, 4, lambda u: u, lambda u: 0), (4, 4, lambda u: 4, lambda u: u - 3))
    return ((first, 3 - first, lambda u: u, lambda u: u), (3, 3, lambda u: 3, lambda u: u))


def reduce_kernel(count, tokens, phases, *refs):
    num = sum(len(phase["lefts"]) for phase in phases)
    lefts, rights = refs[:num], refs[num : 2 * num]
    vec_ref, kv_ref, text_ref = refs[2 * num : 2 * num + 3]
    refs = refs[2 * num + 3 :]
    wide_out, deep_out, square_out, all_vec, kv_out, kv_square = refs[:6]
    left_far, right_far = refs[6 : 6 + num], refs[6 + num : 6 + 2 * num]
    scratch = refs[6 + 2 * num :]
    left_buf, right_buf, got_low, got_scale, put_low, put_scale, plane_put = (
        scratch[2 * i : 2 * i + 2] for i in range(7)
    )
    plane_got = scratch[14 : 14 + len(phases)]
    (
        square_buf,
        left_sem,
        right_sem,
        pair_send,
        pair_recv,
        half_send,
        half_recv,
        ring_send,
        ring_recv,
        credit,
        plane_send,
        plane_recv,
        out_sem,
        out_send,
        out_recv,
        vec_got,
        kv_got,
        vec_sum,
        all_kv,
        text_buf,
        kv_grad,
        side_own,
        side_send,
        side_recv,
        vec_send,
        vec_recv,
        vec_pair_send,
        vec_pair_recv,
        kv_own,
        kv_send,
        kv_recv,
    ) = scratch[14 + len(phases) :]
    me = lax.axis_index("clip")
    band = lax.axis_index("band")
    core = band % 2
    plane = band // 2
    place = ring_place(me, count)
    onward = 1 - 2 * core
    following = (ring_clip((place + onward + count) % count, count), band)
    preceding = (ring_clip((place - onward + count) % count, count), band)
    partner = (me, band + 1 - 2 * core)
    mirror = (me, band + 2 - 4 * plane)
    band_count = vec_got.shape[0]
    band_peers = [(me, (band + step) % band_count) for step in range(1, band_count)]
    greet([following, preceding] + band_peers)

    def owner_at(step, way):
        return ring_clip((place - way * (step + 1) + 2 * count) % count, count)

    def left_blocks(at):
        phase = phases[at]
        if phase["kind"] == 0:
            return [(b, phase["lefts"][0], b, 4) for b in range(4)] + [(4, phase["lefts"][1], 0, 1)]
        first = phase["first"]
        return [(first + i, left, 0, 1) for i, left in enumerate(phase["lefts"])]

    def right_blocks(at):
        phase = phases[at]
        if phase["kind"] == 0:
            return [(0, phase["lefts"][0], 0)] + [(1 + i, phase["lefts"][1], i) for i in range(4)]
        first = phase["first"]
        return [(first + i, phase["lefts"][i], 0) for i in range(3 - first)] + [
            (3 + i, phase["lefts"][-1], i) for i in range(3)
        ]

    def left_cols(step, way, which, many):
        width = lefts_width // count if many == 1 else deep_width // count
        start = owner_at(step, way) * width + which * 128
        return pl.ds(pl.multiple_of(start, 128), 128)

    lefts_width = lefts[phases[1]["lefts"][0]].shape[1]
    deep_width = lefts[phases[0]["lefts"][0]].shape[1]

    def pair_left(at, step):
        out = []
        for block, operand, which, many in left_blocks(at):
            cols = left_cols(step, -onward, which, many)
            out.append(
                pltpu.make_async_remote_copy(
                    lefts[operand].at[:, cols],
                    left_far[operand].at[:, cols],
                    pair_send.at[at, block, step],
                    pair_recv.at[at, block, step],
                    partner,
                    MESH,
                )
            )
        return out

    def pair_right(at):
        out = []
        for i, operand in enumerate(phases[at]["lefts"]):
            half = rights[operand].shape[1] // 2
            out.append(
                pltpu.make_async_remote_copy(
                    rights[operand].at[:, pl.ds(pl.multiple_of((1 - core) * half, 128), half)],
                    right_far[operand],
                    half_send.at[operand],
                    half_recv.at[operand],
                    partner,
                    MESH,
                )
            )
        return out

    def load_left(at, step, slot, far):
        kind = phases[at]["kind"]
        out = []
        for block, operand, which, many in left_blocks(at):
            cols = left_cols(step, onward, which, many)
            source = left_far if far else lefts
            out.append(
                pltpu.make_async_copy(
                    source[operand].at[:, cols],
                    left_buf[kind].at[slot, block, pl.ds(far * tokens, tokens), :],
                    left_sem.at[kind, slot, block, far],
                )
            )
        return out

    def load_right(at, far):
        kind = phases[at]["kind"]
        out = []
        for block, operand, which in right_blocks(at):
            if far:
                source = right_far[operand].at[:, pl.ds(which * UNIT[1], UNIT[1])]
            else:
                half = rights[operand].shape[1] // 2
                start = pl.multiple_of(core * half + which * UNIT[1], 128)
                source = rights[operand].at[:, pl.ds(start, UNIT[1])]
            out.append(
                pltpu.make_async_copy(
                    source,
                    right_buf[kind].at[block, pl.ds(far * tokens, tokens), :],
                    right_sem.at[kind, block, far],
                )
            )
        return out

    def ring_copies(at, part, slot):
        kind = phases[at]["kind"]
        units = pl.ds(*unit_parts(kind, phases[at]["first"])[part][:2])
        return [
            pltpu.make_async_remote_copy(
                put.at[slot, units],
                got.at[slot, units],
                ring_send.at[kind, slot, part, i],
                ring_recv.at[kind, slot, part, i],
                following,
                MESH,
            )
            for i, (put, got) in enumerate(
                ((put_low[kind], got_low[kind]), (put_scale[kind], got_scale[kind]))
            )
        ]

    def plane_copy(at, part):
        kind = phases[at]["kind"]
        start, many = unit_parts(kind, phases[at]["first"])[part][:2]
        units = pl.ds(start, many)
        return pltpu.make_async_remote_copy(
            plane_put[kind].at[units],
            plane_got[at].at[units],
            plane_send.at[at, part],
            plane_recv.at[at, part],
            mirror,
            MESH,
        )

    def out_copies(at, unit):
        phase = phases[at]
        if phase["kind"] == 0 and unit < 4:
            half = UNIT[1]
            rows = deep_out.shape[0] // 4
            there = deep_out.at[
                pl.ds(unit * rows, rows),
                pl.ds(pl.multiple_of(phase["cols"][0] + core * half, 128), half),
            ]
        else:
            which, col = (1, unit - 4) if phase["kind"] == 0 else (unit - phase["first"], 0)
            if phase["kind"] and unit >= 3:
                which, col = len(phase["lefts"]) - 1, unit - 3
            half = rights[phase["lefts"][which]].shape[1] // 2
            start = phase["cols"][which] + core * half + col * UNIT[1]
            there = wide_out.at[:, pl.ds(pl.multiple_of(start, 128), UNIT[1])]
        here = plane_got[at].at[unit]
        return (
            pltpu.make_async_copy(here, there, out_sem.at[at, unit]),
            pltpu.make_async_remote_copy(
                here, there, out_send.at[at, unit], out_recv.at[at, unit], partner, MESH
            ),
        )

    def product(kind, slot, left, right):
        return lax.dot_general(
            left_buf[kind][slot, left],
            right_buf[kind][right],
            (((0,), (0,)), ((), ())),
            preferred_element_type=jnp.float32,
        )

    def start(copies):
        for copy in copies:
            copy.start()

    def finish(copies):
        for copy in copies:
            copy.wait()

    def take_step(at, step, first, last):
        phase = phases[at]
        kind = phase["kind"]
        slot = step % 2
        before = (step + 1) % 2
        for far in range(2):
            finish(load_left(at, step, slot, far))
        if not last:
            for copy in pair_left(at, step + 1):
                copy.wait_recv()
            for far in range(2):
                start(load_left(at, step + 1, before, far))
        parts = unit_parts(kind, phase["first"])
        def encode(term):
            largest = jnp.maximum(jnp.max(jnp.abs(term), axis=0, keepdims=True), WIRE_LEAST)
            low = jnp.round(term * (WIRE_MAX / largest)).astype(jnp.int16)
            return low, largest * (1.0 / WIRE_MAX)

        for part, (low, many, left_of, right_of) in enumerate(parts):
            if not first:
                for copy in ring_copies(at, part, before):
                    copy.wait_recv()
            if not (first or last):

                @pl.when(step >= 2)
                def _(part=part):
                    for copy in ring_copies(at, part, slot):
                        copy.wait_send()
                    pl.semaphore_wait(credit.at[kind, part], 1)

            def settle(position, unit, term):
                if not first:
                    came = got_low[kind][before, position].astype(jnp.float32)
                    term = term + came * got_scale[kind][before, position]
                if last:
                    plane_put[kind][unit] = term
                else:
                    low_part, scale_part = encode(term)
                    put_low[kind][slot, position] = low_part
                    put_scale[kind][slot, position] = scale_part

            @pl.loop(low, low + many)
            def _(unit, left_of=left_of, right_of=right_of):
                settle(unit, unit, product(kind, slot, left_of(unit), right_of(unit)))

            if last:
                plane_copy(at, part).start()
            else:
                start(ring_copies(at, part, slot))
            if not (first or last):

                @pl.when(step < count - 2)
                def _(part=part):
                    pl.semaphore_signal(
                        credit.at[kind, part], inc=1, device_id=preceding, device_id_type=MESH
                    )

    def close(at):
        kind = phases[at]["kind"]

        def add_square(total):
            square_buf[...] += jnp.sum((total * total).reshape(UNIT[0] // 8, 8, UNIT[1]), axis=0)

        for part, (low, many, _, _) in enumerate(unit_parts(kind, phases[at]["first"])):
            plane_copy(at, part).wait()

            @pl.loop(low, low + many)
            def _(unit):
                total = plane_put[kind][unit] + plane_got[at][unit]
                plane_got[at][unit] = total
                add_square(total)

            for unit in range(low, low + many):
                start(out_copies(at, unit))

    half_rows = pl.ds(pl.multiple_of(core * (vec_sum.shape[0] // 2), 8), vec_sum.shape[0] // 2)
    side_local = [
        pltpu.make_async_copy(vec_ref, vec_got.at[band], side_own.at[0]),
        pltpu.make_async_copy(kv_ref.at[band], kv_got.at[band], side_own.at[1]),
        pltpu.make_async_copy(text_ref, text_buf, side_own.at[2]),
    ]
    side_remote = []
    for step, peer in enumerate(band_peers):
        side_remote += [
            pltpu.make_async_remote_copy(
                vec_ref, vec_got.at[band], side_send.at[0, step], side_recv.at[0, step], peer, MESH
            ),
            pltpu.make_async_remote_copy(
                kv_ref.at[peer[1]],
                kv_got.at[band],
                side_send.at[1, step],
                side_recv.at[1, step],
                peer,
                MESH,
            ),
        ]
    vec_own = pltpu.make_async_copy(vec_sum, all_vec.at[me], side_own.at[3])

    def vec_copies(step):
        owner = ring_clip((place - onward * step + 2 * count) % count, count)
        vec = all_vec.at[owner, half_rows]
        return [
            pltpu.make_async_remote_copy(
                here, there, vec_send.at[step, i], vec_recv.at[step, i], following, MESH
            )
            for i, (here, there) in enumerate(((vec, vec), (all_kv.at[owner], all_kv.at[owner])))
        ]

    def vec_first():
        vec = all_vec.at[me, half_rows]
        return [
            pltpu.make_async_remote_copy(
                here, there, vec_send.at[0, i], vec_recv.at[0, i], following, MESH
            )
            for i, (here, there) in enumerate(
                ((vec_sum.at[half_rows], vec), (all_kv.at[me], all_kv.at[me]))
            )
        ]

    def vec_pair(step):
        owner = ring_clip((place - onward * (step + 1) + 2 * count) % count, count)
        vec = all_vec.at[owner, half_rows]
        return pltpu.make_async_remote_copy(
            vec, vec, vec_pair_send.at[step], vec_pair_recv.at[step], partner, MESH
        )

    kv_width = kv_grad.shape[1]

    def kv_place(owner):
        return kv_out.at[:, pl.ds(pl.multiple_of(owner * kv_width, 128), kv_width)]

    def kv_copy(i):
        if i == 2:
            return pltpu.make_async_copy(kv_grad, kv_place(band), kv_own)
        peer = (partner, mirror)[i]
        return pltpu.make_async_remote_copy(
            kv_grad, kv_place(band), kv_send.at[i], kv_recv.at[i], peer, MESH
        )

    def kv_passed():
        there = kv_place(mirror[1])
        return pltpu.make_async_remote_copy(
            there, there, kv_send.at[2], kv_recv.at[2], partner, MESH
        )

    def sum_bands():
        finish(side_local + side_remote)
        vec_sum[...] = jnp.sum(vec_got[...], 0)
        all_kv[me] = jnp.sum(kv_got[...], 0)
        vec_own.start()
        start(vec_first())

    def pass_sums(step):
        for copy in vec_copies(step - 1):
            copy.wait_recv()
        start(vec_copies(step))
        vec_pair(step - 1).start()

    def multiply_text():
        for copy in vec_copies(count - 2):
            copy.wait_recv()
        vec_pair(count - 2).start()
        grads = all_kv[...].reshape(text_buf.shape[0], -1)
        total = jnp.zeros_like(kv_grad)
        for _ in range(3):
            part = grads.astype(jnp.bfloat16)
            grads = grads - part.astype(jnp.float32)
            total = total + matmul_tn(text_buf[...], part)
        kv_grad[...] = total
        kv_square[...] = jnp.sum((total * total).reshape(-1, 8, total.shape[1]), axis=0)
        start([kv_copy(i) for i in range(3)])

    square_buf[...] = jnp.zeros_like(square_buf)
    start(side_local + side_remote)
    start(load_right(0, 0))
    start(pair_right(0))

    @pl.loop(0, count)
    def _(step):
        start(pair_left(0, step))

    start(load_left(0, 0, 0, 0))
    for at in range(len(phases)):
        if at == 0:
            for copy in pair_right(0):
                copy.wait_recv()
            start(load_right(0, 1))
            for copy in pair_left(0, 0):
                copy.wait_recv()
            start(load_left(0, 0, 0, 1))
        for far in range(2):
            finish(load_right(at, far))
        more = at + 1 < len(phases)
        if more:
            start(pair_right(at + 1))
            start(load_right(at + 1, 0))
        take_step(at, 0, True, False)
        if at == 0:
            sum_bands()
        if more:
            start(pair_left(at + 1, 0))

        @pl.loop(1, count - 1)
        def _(step, at=at, more=more):
            take_step(at, step, False, False)
            if at == 0:
                pass_sums(step)
            if more:
                start(pair_left(at + 1, step))

        if more:
            start(pair_left(at + 1, count - 1))
            for copy in pair_right(at + 1):
                copy.wait_recv()
            start(load_right(at + 1, 1))
            for copy in pair_left(at + 1, 0):
                copy.wait_recv()
            for far in range(2):
                start(load_left(at + 1, 0, 0, far))
        take_step(at, count - 1, False, True)
        if at == 0:
            multiply_text()
        for part in range(2):
            for slot in range(2):
                for copy in ring_copies(at, part, slot):
                    copy.wait_send()
        if at == 1:
            kv_copy(1).wait_recv()
            kv_passed().start()
        if at:
            close(at - 1)
    close(len(phases) - 1)
    vec_own.wait()
    kv_passed().wait()
    kv_copy(0).wait()
    kv_copy(1).wait_send()
    kv_copy(2).wait()

    @pl.loop(0, count - 1)
    def _(step):
        for copy in vec_copies(step):
            copy.wait_send()
        vec_pair(step).wait()

    square_out[...] = square_buf[...]
    for at, phase in enumerate(phases):
        for copy in pair_right(at):
            copy.wait_send()

        @pl.loop(0, count)
        def _(step, at=at):
            for copy in pair_left(at, step):
                copy.wait_send()

        for unit in range(phase["first"], 8 if phase["kind"] == 0 else 6):
            finish(out_copies(at, unit))


def reduce_gradients(phases, lefts, rights, vectors, keyvals, text, wide_cols, deep_cols):
    count = lax.axis_size("clip")
    tokens = lefts[0].shape[0]
    wide_rows = lefts[1].shape[1] // count
    deep_rows = lefts[0].shape[1] // count
    band_count, _, kv_cols = keyvals.shape
    num = len(lefts)
    dma = pltpu.SemaphoreType.DMA
    units, lefts_of, rights_of = (8, 6), (5, 4), (5, 6)
    scratch = [pltpu.VMEM((2, lefts_of[k], 2 * tokens, 128), jnp.bfloat16) for k in range(2)]
    scratch += [pltpu.VMEM((rights_of[k], 2 * tokens, UNIT[1]), jnp.bfloat16) for k in range(2)]
    for _ in range(2):
        scratch += [pltpu.VMEM((2, units[k]) + UNIT, jnp.int16) for k in range(2)]
        scratch += [pltpu.VMEM((2, units[k], 1, UNIT[1]), jnp.float32) for k in range(2)]
    scratch += [pltpu.VMEM((units[k],) + UNIT, jnp.float32) for k in range(2)]
    scratch += [pltpu.VMEM((units[p["kind"]],) + UNIT, jnp.float32) for p in phases]
    scratch += [
        pltpu.VMEM((8, UNIT[1]), jnp.float32),
        dma((2, 2, 5, 2)),
        dma((2, 6, 2)),
        dma((len(phases), 5, count)),
        dma((len(phases), 5, count)),
        dma((num,)),
        dma((num,)),
        dma((2, 2, 2, 2)),
        dma((2, 2, 2, 2)),
        pltpu.SemaphoreType.REGULAR((2, 2)),
        dma((len(phases), 2)),
        dma((len(phases), 2)),
        dma((len(phases), 8)),
        dma((len(phases), 8)),
        dma((len(phases), 8)),
    ]
    scratch += [
        pltpu.VMEM((band_count,) + vectors.shape, jnp.float32),
        pltpu.VMEM(keyvals.shape, jnp.float32),
        pltpu.VMEM(vectors.shape, jnp.float32),
        pltpu.VMEM((count,) + keyvals.shape[1:], jnp.float32),
        pltpu.VMEM(text.shape, jnp.bfloat16),
        pltpu.VMEM((text.shape[1], kv_cols), jnp.float32),
        dma((4,)),
        dma((2, band_count - 1)),
        dma((2, band_count - 1)),
        dma((count - 1, 2)),
        dma((count - 1, 2)),
        dma((count - 1,)),
        dma((count - 1,)),
        dma,
        dma((3,)),
        dma((3,)),
    ]
    out = pl.pallas_call(
        partial(reduce_kernel, count, tokens, phases),
        out_shape=(
            jax.ShapeDtypeStruct((wide_rows, wide_cols), jnp.float32),
            jax.ShapeDtypeStruct((deep_rows, deep_cols), jnp.float32),
            jax.ShapeDtypeStruct((8, UNIT[1]), jnp.float32),
            jax.ShapeDtypeStruct((count,) + vectors.shape, jnp.float32),
            jax.ShapeDtypeStruct((deep_rows, band_count * kv_cols), jnp.float32),
            jax.ShapeDtypeStruct((8, kv_cols), jnp.float32),
        )
        + tuple(jax.ShapeDtypeStruct(x.shape, x.dtype) for x in lefts)
        + tuple(jax.ShapeDtypeStruct((tokens, x.shape[1] // 2), x.dtype) for x in rights),
        in_specs=[ANY] * (2 * num + 3),
        out_specs=(ANY, ANY, IN_VMEM, ANY, ANY, IN_VMEM) + (ANY,) * (2 * num),
        scratch_shapes=scratch,
        compiler_params=pltpu.CompilerParams(
            collective_id=2, has_side_effects=True, vmem_limit_bytes=58 << 20
        ),
        cost_estimate=pl.CostEstimate(flops=3 * 10**11, bytes_accessed=8 * 10**8, transcendentals=0),
    )(*lefts, *rights, vectors, keyvals, text)
    return out[:6]


def total_kernel(count, part_ref, out_ref, mid, band_got, clip_got, *sems):
    me = lax.axis_index("clip")
    band = lax.axis_index("band")
    band_count = band_got.shape[0]
    band_peers = [(me, (band + step) % band_count) for step in range(1, band_count)]
    clip_peers = [((me + step) % count, band) for step in range(1, count)]
    greet(band_peers + clip_peers)
    stages = (
        (part_ref, band_got, band, band_peers, mid, sems[:2]),
        (mid, clip_got, me, clip_peers, out_ref, sems[2:]),
    )
    for value, got, index, peers, result, (send, recv) in stages:
        copies = [
            pltpu.make_async_remote_copy(
                value, got.at[index], send.at[step], recv.at[step], peer, MESH
            )
            for step, peer in enumerate(peers)
        ]
        for copy in copies:
            copy.start()
        got[index] = value[...]
        for copy in copies:
            copy.wait()
        result[...] = jnp.sum(got[...], 0)


def total_over_devices(value):
    count, band_count = lax.axis_size("clip"), lax.axis_size("band")
    dma = pltpu.SemaphoreType.DMA
    tile = (8, 128)
    return pl.pallas_call(
        partial(total_kernel, count),
        out_shape=jax.ShapeDtypeStruct(tile, jnp.float32),
        in_specs=[IN_VMEM],
        out_specs=IN_VMEM,
        scratch_shapes=[
            pltpu.VMEM(tile, jnp.float32),
            pltpu.VMEM((band_count,) + tile, jnp.float32),
            pltpu.VMEM((count,) + tile, jnp.float32),
            dma((band_count - 1,)),
            dma((band_count - 1,)),
            dma((count - 1,)),
            dma((count - 1,)),
        ],
        compiler_params=pltpu.CompilerParams(collective_id=3, has_side_effects=True),
    )(jnp.broadcast_to(value, tile))[0, 0]


def per_device(
    latents,
    noise_field,
    timesteps,
    null_flags,
    frame_mask,
    context,
    w_wide,
    m_wide,
    v_wide,
    w_deep,
    m_deep,
    v_deep,
    w_small,
    m_small,
    v_small,
):
    clip_count = lax.axis_size("clip")
    band_count = lax.axis_size("band")
    clip_at = lax.axis_index("clip")
    band_at = lax.axis_index("band")
    wide_rows = w_wide.shape[0]
    deep_rows = w_deep.shape[0]
    text_len, text_dim = context.shape[1:]
    facts = jnp.pad(
        jnp.concatenate([timesteps, frame_mask[0]])[None],
        ((0, 7), (0, 127 - frame_mask.shape[1])),
    )
    kept_text = context[0] * (1 - null_flags[0]).astype(jnp.bfloat16)
    text_cols = jnp.pad(
        kept_text.reshape(text_len, clip_count, deep_rows).transpose(1, 0, 2),
        ((0, 0), (0, TEXT_PAD - text_len), (0, 0)),
    )
    all_facts, all_text = exchange_facts(facts, text_cols)
    all_times = all_facts[:, 0, 0].astype(jnp.float32)
    all_time_low = jax.nn.silu(time_features(all_times)).astype(jnp.bfloat16)
    time_rows = lax.dynamic_slice(
        all_time_low, (0, clip_at * wide_rows), (clip_count, wide_rows)
    )
    part_modul = matmul(time_rows, w_wide[:, : 12 * D].astype(jnp.bfloat16))
    kv_cols = 2 * D // band_count
    kv_weight = lax.dynamic_slice(
        w_deep, (0, D + band_at * kv_cols), (deep_rows, kv_cols)
    ).astype(jnp.bfloat16)
    part_kv = matmul(all_text.reshape(clip_count * TEXT_PAD, deep_rows), kv_weight)
    qkv_b_w = gather_quarters(w_wide[:, 15 * D : 18 * D])
    small_b_w = gather_quarters(w_wide[:, 19 * D : 22 * D])
    up_b_w = gather_quarters(w_wide[:, 22 * D + FF :])
    down_b_w = gather_quarters(w_deep[:, 3 * D :])
    out_b_w, query_w, cross_out_w = (small_b_w[:, i * D : (i + 1) * D] for i in range(3))
    shards = (
        w_wide[:, 12 * D : 15 * D].astype(jnp.bfloat16),
        w_wide[:, 18 * D : 19 * D].astype(jnp.bfloat16),
        w_wide[:, 22 * D : 22 * D + FF].astype(jnp.bfloat16),
        w_deep[:, :D].astype(jnp.bfloat16),
    )
    gathered, all_modul, all_kv = gather_weights(
        shards,
        (0, 0, 1, 2),
        part_modul.reshape(clip_count, 12 * D // 128, 128),
        part_kv.reshape(clip_count, TEXT_PAD, kv_cols),
    )
    qkv_a_w, out_a_w, up_a_w, down_a_w = gathered
    keyval = lax.all_gather(jnp.sum(all_kv, 0).astype(jnp.bfloat16), "band", axis=1, tiled=True)
    small_low = w_small.astype(jnp.bfloat16)
    small_val = small_low.astype(jnp.float32)
    num_frames, num_rows, num_cols = (latents.shape[1], latents.shape[2], latents.shape[3])
    tok_count = num_frames * num_rows * num_cols
    all_mask = all_facts[:, 0, 1 : 1 + num_frames]
    global_count = jnp.sum(all_mask).astype(jnp.float32) * (num_rows * num_cols * CH * band_count)
    time_value = timesteps[0].astype(jnp.float32)
    noise_angle = 0.5 * math.pi * time_value / TMAX
    signal, spread = (jnp.cos(noise_angle), jnp.sin(noise_angle))
    clean_tok = token_order(latents[0])
    noise_tok = token_order(noise_field[0])
    run = num_rows * WIN
    part = SHIFT * WIN
    frame_windows = attend_pieces(tok_count, num_frames, "frame")
    half_windows = attend_pieces(tok_count, num_frames, "half")
    text_windows = attend_pieces(tok_count, num_frames, "text")
    noisy_low = (signal * clean_tok + spread * noise_tok).astype(jnp.bfloat16)
    target = signal * noise_tok - spread * clean_tok
    modulation = jnp.sum(all_modul, 0).reshape(12, D)
    mod_a, mod_b = (modulation[:6], modulation[6:])
    stream_zero = matmul(noisy_low, small_low[:CH]) + small_val[2 * CH]
    normed_a, back_a = jax.vjp(norm_modulated, stream_zero, mod_a[0], mod_a[1])
    in_a = normed_a.astype(jnp.bfloat16)
    qkv_a = matmul(in_a, qkv_a_w).astype(jnp.bfloat16)
    far_kv = from_partner(qkv_a[:, D:], "band", 0)
    space_kv = [(qkv_a, HEADS // 2, HEADS), (far_kv, 0, HEADS // 2)]
    att_a = attend(qkv_a, space_kv, frame_windows)
    proj_a = matmul(att_a, out_a_w)
    stream_one = stream_zero + mod_a[2] * proj_a
    stream_two, saved_a = mlp_forward(stream_one, mod_a, up_a_w, down_a_w)
    normed_b, back_b = jax.vjp(norm_modulated, stream_two, mod_b[0], mod_b[1])
    low_b = normed_b.astype(jnp.bfloat16)
    rolled = with_rows(low_b, shifted(first_rows(low_b, run, part), "band", -1), run)
    qkv_b = matmul(rolled, qkv_b_w).astype(jnp.bfloat16)
    win_kv = [(qkv_b, HEADS // 2, HEADS)]
    win_out = attend(qkv_b, win_kv, half_windows)
    att_b = with_rows(win_out, shifted(first_rows(win_out, run, part), "band", 1), run)
    proj_b = matmul(att_b, out_b_w)
    stream_three = stream_two + mod_b[2] * proj_b
    cross_val, cross_back = jax.vjp(norm_gained, stream_three, small_val[2 * CH + 1])
    cross_in = cross_val.astype(jnp.bfloat16)
    query_proj = matmul(cross_in, query_w).astype(jnp.bfloat16)
    text_kv = [(keyval, 0, HEADS // 2)]
    crossed = attend(query_proj, text_kv, text_windows, text_len)
    stream_four = stream_three + matmul(crossed, cross_out_w)
    stream_five, saved_b = mlp_forward(stream_four, mod_b, up_b_w, down_b_w)
    final_val, final_back = jax.vjp(norm_gained, stream_five, small_val[2 * CH + 2])
    final_low = final_val.astype(jnp.bfloat16)
    head_low = small_low[CH : 2 * CH]
    predicted = matmul_nt(final_low, head_low)
    weight_row = jnp.repeat(frame_mask[0].astype(jnp.float32), run)
    weight_row = jnp.tile(weight_row, num_cols // WIN)[:, None]
    pred_error = predicted - target
    loss_part = jnp.sum(weight_row * pred_error * pred_error)
    grad_pred = (weight_row * pred_error * (2.0 / global_count)).astype(jnp.bfloat16)
    grad_head = matmul_tn(grad_pred, final_low)
    grad_stream, grad_gain_f = final_back(matmul(grad_pred, head_low))
    grad_stream, mlp_factors_b, extra_b = mlp_backward(
        grad_stream, mod_b, up_b_w, down_b_w, saved_b
    )
    grad_cross = grad_stream.astype(jnp.bfloat16)
    grad_crossed = matmul_nt(grad_cross, cross_out_w).astype(jnp.bfloat16)
    grad_query, grad_keyval = attend_back(
        query_proj, text_kv, grad_crossed, text_windows, text_len
    )
    grad_part, grad_gain_c = cross_back(matmul_nt(grad_query, query_w))
    grad_stream = grad_stream + grad_part
    grad_proj = (mod_b[2] * grad_stream).astype(jnp.bfloat16)
    grad_gate_b = jnp.sum(grad_stream * proj_b, 0)
    factors_ob = (att_b, grad_proj)
    grad_att = matmul_nt(grad_proj, out_b_w).astype(jnp.bfloat16)
    grad_win = with_rows(grad_att, shifted(first_rows(grad_att, run, part), "band", -1), run)
    grad_qkv = attend_back(qkv_b, win_kv, grad_win, half_windows)[0]
    factors_qkvb = (rolled, grad_qkv)
    grad_in_roll = matmul_nt(grad_qkv, qkv_b_w)
    sent_back = shifted(first_rows(grad_in_roll, run, part), "band", 1)
    grad_normed = with_rows(grad_in_roll, sent_back, run)
    grad_part, grad_shift_b, grad_scale_b = back_b(grad_normed)
    grad_stream = grad_stream + grad_part
    grad_stream, mlp_factors_a, extra_a = mlp_backward(
        grad_stream, mod_a, up_a_w, down_a_w, saved_a
    )
    grad_proj = (mod_a[2] * grad_stream).astype(jnp.bfloat16)
    grad_gate_a = jnp.sum(grad_stream * proj_a, 0)
    factors_oa = (att_a, grad_proj)
    grad_att = matmul_nt(grad_proj, out_a_w).astype(jnp.bfloat16)
    grad_q, grad_own, grad_far = attend_back(qkv_a, space_kv, grad_att, frame_windows)
    grad_kv = grad_own + from_partner(grad_far, "band", 0)
    grad_qkv = jnp.concatenate([grad_q, grad_kv.astype(jnp.bfloat16)], 1)
    factors_qkva = (in_a, grad_qkv)
    grad_part, grad_shift_a, grad_scale_a = back_a(matmul_nt(grad_qkv, qkv_a_w))
    grad_stream = grad_stream + grad_part
    grad_patch = matmul_tn(noisy_low.astype(jnp.float32), grad_stream, lax.Precision.HIGHEST)
    grad_bias = jnp.sum(grad_stream, 0)
    grad_modul = jnp.stack(
        [
            grad_shift_a,
            grad_scale_a,
            grad_gate_a,
            extra_a[0],
            extra_a[1],
            extra_a[2],
            grad_shift_b,
            grad_scale_b,
            grad_gate_b,
            extra_b[0],
            extra_b[1],
            extra_b[2],
        ]
    ).reshape(1, 12 * D)
    grad_small = jnp.concatenate(
        [grad_patch, grad_head, grad_bias[None], grad_gain_c[None], grad_gain_f[None]], 0
    )
    factors = mlp_factors_b + (
        (crossed, grad_cross),
        (cross_in, grad_query),
        factors_ob,
        factors_qkvb,
    )
    factors += mlp_factors_a + (factors_oa, factors_qkva)
    if wide_rows == 128 and deep_rows == 512:
        phases = (
            {"kind": 0, "first": 0, "lefts": (0, 1), "cols": (D, 10 * D + FF)},
            {"kind": 1, "first": 0, "lefts": (2, 3, 4, 5), "cols": (9 * D, 8 * D, 7 * D, 3 * D)},
            {"kind": 0, "first": 0, "lefts": (6, 7), "cols": (0, 10 * D)},
            {"kind": 1, "first": 2, "lefts": (8, 9), "cols": (6 * D, 0)},
        )
        used = 12 * D + grad_small.size
        vectors = jnp.concatenate(
            [grad_modul.reshape(-1), grad_small.reshape(-1), loss_part[None]]
        )
        vectors = jnp.pad(vectors, (0, 256 * 128 - vectors.shape[0])).reshape(256, 128)
        keyvals = grad_keyval.reshape(TEXT_PAD, band_count, kv_cols).transpose(1, 0, 2)
        wide_rest, deep_rest, squares, all_vectors, grad_w_ckv, kv_squares = reduce_gradients(
            phases,
            [f[0] for f in factors],
            [f[1] for f in factors],
            vectors,
            keyvals,
            all_text.reshape(clip_count * TEXT_PAD, deep_rows),
            10 * D + 2 * FF,
            2 * D,
        )
        all_vectors = all_vectors.reshape(clip_count, -1)
        all_grad_modul = all_vectors[:, : 12 * D]
        small_sum = jnp.sum(all_vectors[:, 12 * D : used], 0).reshape(grad_small.shape)
        loss_sum = jnp.sum(all_vectors[:, used])
        square_part = jnp.sum(squares) / (band_count // 2) + jnp.sum(kv_squares)
    else:
        summed = [sum_rows(*pair) for pair in factors]
        wide_rest = jnp.concatenate([summed[i] for i in (9, 5, 8, 4, 3, 2, 7, 1)], 1)
        deep_rest = jnp.concatenate([summed[6], summed[0]], 1)
        grad_keyval = lax.psum_scatter(grad_keyval, "band", scatter_dimension=1, tiled=True)
        grad_keyval = lax.all_gather(grad_keyval, "clip", axis=0, tiled=True)
        grad_w_ckv = matmul_tn(
            all_text.reshape(clip_count * TEXT_PAD, deep_rows).astype(jnp.float32),
            grad_keyval,
            lax.Precision.HIGHEST,
        )
        grad_w_ckv = lax.all_gather(grad_w_ckv, "band", axis=1, tiled=True)
        all_grad_modul = lax.all_gather(lax.psum(grad_modul, "band"), "clip", axis=0, tiled=True)
        loss_sum, small_sum = lax.psum((loss_part, grad_small), ("clip", "band"))
        square_part = sum(jnp.sum(x * x) for x in (wide_rest, deep_rest, grad_w_ckv)) / band_count
    grad_w_ada = matmul_tn(time_rows.astype(jnp.float32), all_grad_modul, lax.Precision.HIGHEST)
    wide_sum = jnp.concatenate([grad_w_ada, wide_rest], 1)
    deep_sum = jnp.concatenate([deep_rest[:, :D], grad_w_ckv, deep_rest[:, D:]], 1)
    square_part += jnp.sum(grad_w_ada * grad_w_ada) / band_count
    square_sum = total_over_devices(square_part)
    grad_norm = jnp.sqrt(square_sum + jnp.sum(small_sum * small_sum))
    factor = CLIP_MAX / jnp.maximum(grad_norm, CLIP_MAX)
    new_wide = adam_update(w_wide, m_wide, v_wide, wide_sum * factor, 0.15)
    new_deep = adam_update(w_deep, m_deep, v_deep, deep_sum * factor, 0.05)
    new_small = adam_update(w_small, m_small, v_small, small_sum * factor, 0.5)
    loss = loss_sum / global_count
    return (
        loss,
        grad_norm,
        new_wide[0],
        new_wide[1],
        new_wide[2],
        new_deep[0],
        new_deep[1],
        new_deep[2],
        new_small[0],
        new_small[1],
        new_small[2],
    )


def solution(mesh):
    in_specs = (
        P("clip", None, "band", None, None),
        P("clip", None, "band", None, None),
        P("clip"),
        P("clip"),
        P("clip", None),
        P("clip", None, None),
        P("clip", None),
        P("clip", None),
        P("clip", None),
        P("clip", None),
        P("clip", None),
        P("clip", None),
        P(),
        P(),
        P(),
    )
    out_specs = (
        P(),
        P(),
        P("clip", None),
        P("clip", None),
        P("clip", None),
        P("clip", None),
        P("clip", None),
        P("clip", None),
        P(),
        P(),
        P(),
    )
    return jax.shard_map(
        per_device, mesh=mesh, in_specs=in_specs, out_specs=out_specs, check_vma=False
    )
```

```python
from functools import partial
import math

import jax
import jax.numpy as jnp
from jax import lax
from jax.experimental import pallas as pl
from jax.experimental.pallas import tpu as pltpu
from jax.sharding import PartitionSpec as P

D = 1024
HEADS = 16
HEAD_DIM = 64
FF = 4096
CH = 8
SPACE = 16
WIN = 8
SHIFT = 4
TMAX = 1000
STEP = 10


EPS_NORM = 1e-06
CLIP_MAX = 0.001
BETA_ONE = 0.9
BETA_TWO = 0.95
ADAM_EPS = 1e-08
DECAY = 0.1


def from_partner(block, axis, distance):
    count = lax.axis_size(axis)
    route = []
    for low in range(count):
        high = low | 1 << distance
        if high != low and high < count:
            route += [(low, high), (high, low)]
    return lax.ppermute(block, axis, route)


def shifted(value, axis, by):
    length = lax.axis_size(axis)
    return lax.ppermute(value, axis, [(i, (i + by) % length) for i in range(length)])


def matmul(left_op, right_op):
    return jnp.dot(left_op, right_op, preferred_element_type=jnp.float32)


def matmul_tn(left_op, right_op, precision=None):
    return lax.dot_general(
        left_op,
        right_op,
        (((0,), (0,)), ((), ())),
        precision=precision,
        preferred_element_type=jnp.float32,
    )


def matmul_nt(left_op, right_op):
    return lax.dot_general(
        left_op, right_op, (((1,), (1,)), ((), ())), preferred_element_type=jnp.float32
    )


def layer_norm(field_in):
    average = jnp.mean(field_in, -1, keepdims=True)
    centred = field_in - average
    return centred * lax.rsqrt(jnp.mean(centred * centred, -1, keepdims=True) + EPS_NORM)


def norm_modulated(field_in, shift_vec, scale_vec):
    return layer_norm(field_in) * (1.0 + scale_vec) + shift_vec


def norm_gained(field_in, gain_vec):
    return layer_norm(field_in) * gain_vec


def time_features(time_value):
    half_width = D // 2
    frequency = jnp.exp(-math.log(10000.0) * jnp.arange(half_width, dtype=jnp.float32) / half_width)
    angles = time_value[..., None] * frequency
    return jnp.concatenate([jnp.cos(angles), jnp.sin(angles)], -1)


def token_order(grid):
    frames, rows, cols, width = grid.shape
    halves = grid.reshape(frames, rows, cols // WIN, WIN, width).transpose(2, 0, 1, 3, 4)
    return halves.reshape(frames * rows * cols, width)


def with_rows(tokens, first_rows, run):
    width = tokens.shape[1]
    runs = tokens.reshape(-1, run, width)
    return jnp.concatenate([first_rows, runs[:, first_rows.shape[1] :]], 1).reshape(-1, width)


def first_rows(tokens, run, part):
    return tokens.reshape(-1, run, tokens.shape[1])[:, :part]


def attend_pieces(tokens, frames, keys):
    if keys == "frame":
        run = tokens // (2 * frames)
        return [((f * run, run), (tokens // 2 + f * run, run)) for f in range(frames)]
    if keys == "half":
        return [((half * (tokens // 2), tokens // 2),) for half in range(2)]
    return [((0, tokens),)]


def take(ref, runs):
    pieces = [ref[low : low + many, :] for low, many in runs]
    return pieces[0] if len(pieces) == 1 else jnp.concatenate(pieces, 0)


def put(ref, cols, runs, value):
    done = 0
    for low, many in runs:
        ref[low : low + many, cols] = value[done : done + many].astype(ref.dtype)
        done += many


def softmax_of(scores, axis, text_len):
    if text_len:
        place = lax.broadcasted_iota(jnp.int32, scores.shape, axis)
        scores = jnp.where(place < text_len, scores, -1e30)
    weight = jnp.exp(scores - jnp.max(scores, axis, keepdims=True))
    return weight * (1.0 / jnp.sum(weight, axis, keepdims=True))


def lanes_of(head, shape):
    lane = lax.broadcasted_iota(jnp.int32, shape, 1)
    return lane < HEAD_DIM if head == 0 else lane >= HEAD_DIM


def only(head, value):
    return jnp.where(lanes_of(head, value.shape), value, jnp.zeros_like(value))


def key_sets(key_refs, runs, text_len):
    if text_len:
        return key_refs[0][...]
    pieces = [take(ref, runs) for ref in key_refs]
    return pieces[0] if len(pieces) == 1 else jnp.concatenate(pieces, 0)


def attend_kernel(windows, text_len, sets, *refs):
    q_ref, k_refs, v_refs, out_ref = refs[0], refs[1 : 1 + sets], refs[1 + sets : 1 + 2 * sets], refs[-1]
    for runs in windows:
        queries = take(q_ref, runs) * HEAD_DIM ** (-0.5)
        keys, values = key_sets(k_refs, runs, text_len), key_sets(v_refs, runs, text_len)
        outs = []
        for head in range(2):
            probs = softmax_of(matmul_nt(only(head, queries), keys), 1, text_len)
            outs.append(matmul(probs.astype(jnp.bfloat16), values))
        put(out_ref, slice(None), runs, jnp.where(lanes_of(0, outs[0].shape), *outs))


def attend_back_kernel(windows, text_len, sets, *refs):
    q_ref, k_refs, v_refs = refs[0], refs[1 : 1 + sets], refs[1 + sets : 1 + 2 * sets]
    grad_ref = refs[1 + 2 * sets]
    dq_ref = refs[2 + 2 * sets]
    own_ref = refs[3 + 2 * sets] if len(refs) > 3 + 2 * sets else None
    far_ref = refs[4 + 2 * sets] if sets == 2 else None
    pair = pl.program_id(0)
    cols = [pl.ds(pl.multiple_of(i * D + pair * 2 * HEAD_DIM, 128), 2 * HEAD_DIM) for i in range(3)]
    merged = dq_ref.shape[1] == 3 * D
    for runs in windows:
        queries = take(q_ref, runs) * HEAD_DIM ** (-0.5)
        keys, values = key_sets(k_refs, runs, text_len), key_sets(v_refs, runs, text_len)
        grad_out = take(grad_ref, runs)
        dq, dk, dv = [], [], []
        for head in range(2):
            probs = softmax_of(matmul_nt(keys, only(head, queries)), 0, text_len)
            dprobs = matmul_nt(values, only(head, grad_out))
            dv.append(matmul(probs.astype(jnp.bfloat16), grad_out))
            inner = jnp.sum(probs * dprobs, 0, keepdims=True)
            dscores = (probs * (dprobs - inner)).astype(jnp.bfloat16)
            dk.append(matmul(dscores, queries))
            dq.append(matmul_tn(dscores, keys))
        dq, dk, dv = (jnp.where(lanes_of(0, x[0].shape), *x) for x in (dq, dk, dv))
        put(dq_ref, cols[0], runs, dq * HEAD_DIM ** (-0.5))
        if merged:
            put(dq_ref, cols[1], runs, dk)
            put(dq_ref, cols[2], runs, dv)
        elif text_len:
            own_ref[:, cols[0]] = dk
            own_ref[:, cols[1]] = dv
        else:
            half = dk.shape[0] // 2
            put(own_ref, cols[0], runs, dk[:half])
            put(own_ref, cols[1], runs, dv[:half])
            put(far_ref, cols[0], runs, dk[half:])
            put(far_ref, cols[1], runs, dv[half:])


def head_cols(array, first):
    return array, pl.BlockSpec((array.shape[0], 2 * HEAD_DIM), lambda h: (0, first + h))


def attention_operands(queries, key_values):
    ins = [head_cols(queries, 0)]
    ins += [head_cols(array, first) for array, first, _ in key_values]
    return ins + [head_cols(array, second) for array, _, second in key_values]


def attention_cost(tokens, keys, products):
    flops = 2 * products * tokens * keys * D * 2
    return pl.CostEstimate(
        flops=flops, bytes_accessed=tokens * D * 2 * 8, transcendentals=tokens * keys * HEADS
    )


def attend(queries, key_values, windows, text_len=0):
    tokens = queries.shape[0]
    ins = attention_operands(queries, key_values)
    return pl.pallas_call(
        partial(attend_kernel, windows, text_len, len(key_values)),
        grid=(HEADS // 2,),
        in_specs=[spec for _, spec in ins],
        out_specs=pl.BlockSpec((tokens, 2 * HEAD_DIM), lambda h: (0, h)),
        out_shape=jax.ShapeDtypeStruct((tokens, D), jnp.bfloat16),
        compiler_params=pltpu.CompilerParams(vmem_limit_bytes=40 << 20),
        cost_estimate=attention_cost(tokens, 320, 2),
    )(*[array for array, _ in ins])


def attend_back(queries, key_values, grad_out, windows, text_len=0):
    tokens = queries.shape[0]
    ins = attention_operands(queries, key_values) + [head_cols(grad_out, 0)]
    sets = len(key_values)
    whole = lambda rows, cols: pl.BlockSpec((rows, cols), lambda h: (0, 0))
    if sets == 1 and not text_len:
        outs = [((tokens, 3 * D), jnp.bfloat16)]
    else:
        rows = key_values[0][0].shape[0]
        outs = [((tokens, D), jnp.bfloat16)] + [((rows, 2 * D), jnp.float32)] * sets
    return pl.pallas_call(
        partial(attend_back_kernel, windows, text_len, sets),
        grid=(HEADS // 2,),
        in_specs=[spec for _, spec in ins],
        out_specs=[whole(*shape) for shape, _ in outs],
        out_shape=[jax.ShapeDtypeStruct(*out) for out in outs],
        compiler_params=pltpu.CompilerParams(vmem_limit_bytes=50 << 20),
        cost_estimate=attention_cost(tokens, 320, 5),
    )(*[array for array, _ in ins])


def mlp_forward(stream, modul, up_weight, down_weight):
    mlp_val, norm_back = jax.vjp(norm_modulated, stream, modul[3], modul[4])
    mlp_in = mlp_val.astype(jnp.bfloat16)
    up_proj = matmul(mlp_in, up_weight)
    share = 0.5 + 0.5 * lax.erf(up_proj * math.sqrt(0.5))
    gelu_val = up_proj * share
    slope = share + up_proj * (jnp.exp(-0.5 * up_proj * up_proj) / math.sqrt(2.0 * math.pi))
    gelu_low = gelu_val.astype(jnp.bfloat16)
    down_proj = matmul(gelu_low, down_weight)
    return (stream + modul[5] * down_proj, (norm_back, mlp_in, slope, gelu_low, down_proj))


def mlp_backward(grad_stream, modul, up_weight, down_weight, saved):
    norm_back, mlp_in, slope, gelu_low, down_proj = saved
    grad_down = (modul[5] * grad_stream).astype(jnp.bfloat16)
    grad_gate = jnp.sum(grad_stream * down_proj, 0)
    grad_up = (slope * matmul_nt(grad_down, down_weight)).astype(jnp.bfloat16)
    grad_part, grad_shift, grad_scale = norm_back(matmul_nt(grad_up, up_weight))
    factors = ((gelu_low, grad_down), (mlp_in, grad_up))
    return (grad_stream + grad_part, factors, (grad_shift, grad_scale, grad_gate))


def adam_update(weight, first_mom, second_mom, grad_val, learn_rate):
    first_mom = BETA_ONE * first_mom + (1.0 - BETA_ONE) * grad_val
    second_mom = BETA_TWO * second_mom + (1.0 - BETA_TWO) * grad_val * grad_val
    first_hat = first_mom / (1.0 - BETA_ONE**STEP)
    second_hat = second_mom / (1.0 - BETA_TWO**STEP)
    weight = weight - learn_rate * (first_hat / (jnp.sqrt(second_hat) + ADAM_EPS) + DECAY * weight)
    return (weight, first_mom, second_mom)

MESH = pl.DeviceIdType.MESH
ANY = pl.BlockSpec(memory_space=pl.ANY)
IN_VMEM = pl.BlockSpec(memory_space=pltpu.VMEM)
TEXT_PAD = 80


def ring_place(clip, count):
    half = clip // 2
    odd = clip % 2
    return half + odd * (count - 1 - 2 * half)


def ring_clip(place, count):
    far = place // (count // 2)
    return (1 - far) * 2 * place + far * (2 * (count - 1 - place) + 1)


def greet(peers):
    barrier = pltpu.get_barrier_semaphore()
    for peer in peers:
        pl.semaphore_signal(barrier, inc=1, device_id=peer, device_id_type=MESH)
    pl.semaphore_wait(barrier, len(peers))


def exchange_kernel(count, facts_ref, text_ref, facts_out, text_out, send, recv, local):
    me = lax.axis_index("clip")
    band = lax.axis_index("band")
    peers = [((me + step) % count, band) for step in range(1, count)]
    greet(peers)
    own = [
        pltpu.make_async_copy(facts_ref, facts_out.at[me], local.at[0]),
        pltpu.make_async_copy(text_ref.at[me], text_out.at[me], local.at[1]),
    ]
    for copy in own:
        copy.start()
    sent = []
    for step, peer in enumerate(peers):
        sent += [
            pltpu.make_async_remote_copy(
                facts_ref, facts_out.at[me], send.at[0, step], recv.at[0, step], peer, MESH
            ),
            pltpu.make_async_remote_copy(
                text_ref.at[peer[0]], text_out.at[me], send.at[1, step], recv.at[1, step], peer, MESH
            ),
        ]
    for copy in sent:
        copy.start()
    for copy in own + sent:
        copy.wait()


def exchange_facts(facts, text):
    count = lax.axis_size("clip")
    return pl.pallas_call(
        partial(exchange_kernel, count),
        out_shape=(
            jax.ShapeDtypeStruct((count,) + facts.shape, facts.dtype),
            jax.ShapeDtypeStruct(text.shape, text.dtype),
        ),
        in_specs=[ANY] * 2,
        out_specs=(ANY,) * 2,
        scratch_shapes=[
            pltpu.SemaphoreType.DMA((2, count - 1)),
            pltpu.SemaphoreType.DMA((2, count - 1)),
            pltpu.SemaphoreType.DMA((2,)),
        ],
        compiler_params=pltpu.CompilerParams(collective_id=0, has_side_effects=True),
    )(facts, text)


def gather_kernel(count, shapes, sides, *refs):
    num = len(shapes)
    shards, (vec_ref, text_ref) = refs[:num], refs[num : num + 2]
    full, (vec_out, text_out) = refs[num + 2 : 2 * num + 2], refs[2 * num + 2 : 2 * num + 4]
    ring_send, ring_recv, pair_send, pair_recv, cross_send, cross_recv = refs[
        2 * num + 4 : 2 * num + 10
    ]
    own_sem, part_send, part_recv, part_own = refs[2 * num + 10 :]
    me = lax.axis_index("clip")
    band = lax.axis_index("band")
    core = band % 2
    place = ring_place(me, count)
    onward = 1 - 2 * core
    following = (ring_clip((place + onward + count) % count, count), band)
    plane = band // 2
    partner = (me, band + 1 - 2 * core)
    mirror = (me, band + 2 - 4 * plane)
    peers = [((me + step) % count, band) for step in range(1, count)]
    greet(peers + [partner, mirror])

    def block(ref, group, owner):
        rows, cols = shapes[group]
        return ref.at[
            pl.ds(pl.multiple_of(owner * rows, rows), rows),
            pl.ds(pl.multiple_of(core * (cols // 2), 128), cols // 2),
        ]

    def ring_copy(group, step):
        owner = ring_clip((place - onward * step + 2 * count) % count, count)
        there = block(full[group], group, owner)
        return pltpu.make_async_remote_copy(
            there, there, ring_send.at[step, group], ring_recv.at[step, group], following, MESH
        )

    def handed(group, step, send, recv, peer):
        owner = ring_clip((place - onward * (step + 1) + 2 * count) % count, count)
        there = block(full[group], group, owner)
        return pltpu.make_async_remote_copy(
            there, there, send.at[step, group], recv.at[step, group], peer, MESH
        )

    def pair_copy(group, step):
        return handed(group, step, pair_send, pair_recv, partner)

    def cross_copy(group, step):
        return handed(group, step, cross_send, cross_recv, mirror)

    def in_ring(group):
        def decorate(body):
            if sides[group]:
                pl.when(plane == sides[group] - 1)(body)
            else:
                body()

        return decorate

    def off_ring(group, also=None):
        def decorate(body):
            if sides[group]:
                off = plane != sides[group] - 1
                pl.when(off if also is None else jnp.logical_and(off, also))(body)

        return decorate

    def ring_arrival(group, step, onto):
        ring_copy(group, step).wait_recv()
        if onto:
            ring_copy(group, step + 1).start()
        pair_copy(group, step).start()
        if sides[group]:
            cross_copy(group, step).start()

    def cross_arrival(group, step):
        cross_copy(group, step).wait_recv()
        pair_copy(group, step).start()

    def own_copy(group):
        rows, cols = shapes[group]
        return pltpu.make_async_copy(
            shards[group],
            full[group].at[pl.ds(pl.multiple_of(me * rows, rows), rows), :],
            own_sem.at[group],
        )

    parts = []
    for step, peer in enumerate(peers):
        for which, (src, dst) in enumerate(((vec_ref, vec_out), (text_ref, text_out))):
            parts.append(
                pltpu.make_async_remote_copy(
                    src.at[peer[0]],
                    dst.at[me],
                    part_send.at[which, step],
                    part_recv.at[which, step],
                    peer,
                    MESH,
                )
            )
    parts_own = [
        pltpu.make_async_copy(src.at[me], dst.at[me], part_own.at[which])
        for which, (src, dst) in enumerate(((vec_ref, vec_out), (text_ref, text_out)))
    ]
    for group in range(num):
        rows, cols = shapes[group]
        own_copy(group).start()

        @in_ring(group)
        def _(group=group, rows=rows, cols=cols):
            pltpu.make_async_remote_copy(
                shards[group].at[:, pl.ds(pl.multiple_of(core * (cols // 2), 128), cols // 2)],
                block(full[group], group, me),
                ring_send.at[0, group],
                ring_recv.at[0, group],
                following,
                MESH,
            ).start()

    for copy in parts_own + parts:
        copy.start()

    @pl.loop(1, count - 1)
    def _(step):
        for group in range(num):

            @in_ring(group)
            def _(group=group):
                ring_arrival(group, step - 1, True)

        for group in range(num):

            @off_ring(group, step >= 2)
            def _(group=group):
                cross_arrival(group, step - 2)

    for group in range(num):

        @in_ring(group)
        def _(group=group):
            ring_arrival(group, count - 2, False)

    for late in (count - 3, count - 2):
        for group in range(num):

            @off_ring(group)
            def _(group=group, late=late):
                cross_arrival(group, late)

    for copy in parts_own + parts:
        copy.wait()
    for group in range(num):
        own_copy(group).wait()

    @pl.loop(0, count - 1)
    def _(step):
        for group in range(num):

            @in_ring(group)
            def _(group=group):
                ring_copy(group, step).wait_send()
                if sides[group]:
                    cross_copy(group, step).wait_send()

            pair_copy(group, step).wait()


def gather_quarters(shard):
    band_count = lax.axis_size("band")
    rows = shard.shape[0] // band_count
    own = lax.dynamic_slice_in_dim(shard, lax.axis_index("band") * rows, rows, 0)
    return lax.all_gather(own.astype(jnp.bfloat16), ("clip", "band"), axis=0, tiled=True)


def sum_rows(left, right):
    part = lax.psum_scatter(
        matmul_tn(left, right), ("clip", "band"), scatter_dimension=0, tiled=True
    )
    return lax.all_gather(part, "band", axis=0, tiled=True)


def gather_weights(shards, sides, vectors, texts):
    count = lax.axis_size("clip")
    num = len(shards)
    steps = pltpu.SemaphoreType.DMA((count - 1, num))
    out = pl.pallas_call(
        partial(gather_kernel, count, [shard.shape for shard in shards], sides),
        out_shape=tuple(
            jax.ShapeDtypeStruct((count * s.shape[0], s.shape[1]), s.dtype) for s in shards
        )
        + tuple(jax.ShapeDtypeStruct(v.shape, v.dtype) for v in (vectors, texts)),
        in_specs=[ANY] * (num + 2),
        out_specs=(ANY,) * (num + 2),
        scratch_shapes=[
            *[steps] * 6,
            pltpu.SemaphoreType.DMA((num,)),
            pltpu.SemaphoreType.DMA((2, count - 1)),
            pltpu.SemaphoreType.DMA((2, count - 1)),
            pltpu.SemaphoreType.DMA((2,)),
        ],
        compiler_params=pltpu.CompilerParams(collective_id=1, has_side_effects=True),
        cost_estimate=pl.CostEstimate(flops=2 * 10**11, bytes_accessed=6 * 10**8, transcendentals=0),
    )(*shards, vectors, texts)
    return out[:num], out[num], out[num + 1]


WIRE_MAX = 32767.0
WIRE_LEAST = 1e-30
UNIT = (128, 512)


def unit_parts(kind, first):
    if kind == 0:
        return ((0, 4, lambda u: u, lambda u: 0), (4, 4, lambda u: 4, lambda u: u - 3))
    if first:
        return ((2, 2, lambda u: u, lambda u: u), (4, 2, lambda u: 3, lambda u: u))
    return ((0, 3, lambda u: u, lambda u: u), (3, 3, lambda u: 3, lambda u: u))


def reduce_kernel(count, tokens, phases, *refs):
    num = sum(len(phase["lefts"]) for phase in phases)
    lefts, rights = refs[:num], refs[num : 2 * num]
    vec_ref, kv_ref, text_ref = refs[2 * num : 2 * num + 3]
    refs = refs[2 * num + 3 :]
    wide_out, deep_out, square_out, all_vec, kv_out, kv_square = refs[:6]
    left_far, right_far = refs[6 : 6 + num], refs[6 + num : 6 + 2 * num]
    scratch = refs[6 + 2 * num :]
    left_buf, right_buf, got_low, got_scale, put_low, put_scale, plane_put = (
        scratch[2 * i : 2 * i + 2] for i in range(7)
    )
    plane_got = scratch[14 : 14 + len(phases)]
    (
        square_buf,
        left_sem,
        right_sem,
        pair_send,
        pair_recv,
        half_send,
        half_recv,
        ring_send,
        ring_recv,
        credit,
        plane_send,
        plane_recv,
        out_sem,
        out_send,
        out_recv,
        last_put,
        last_put_scale,
        last_got,
        last_got_scale,
        push_send,
        push_recv,
        vec_got,
        kv_got,
        vec_sum,
        all_kv,
        text_buf,
        kv_grad,
        side_own,
        side_send,
        side_recv,
        vec_send,
        vec_recv,
        vec_pair_send,
        vec_pair_recv,
        kv_own,
        kv_send,
        kv_recv,
    ) = scratch[14 + len(phases) :]
    me = lax.axis_index("clip")
    band = lax.axis_index("band")
    core = band % 2
    plane = band // 2
    place = ring_place(me, count)
    onward = 1 - 2 * core
    following = (ring_clip((place + onward + count) % count, count), band)
    preceding = (ring_clip((place - onward + count) % count, count), band)
    partner = (me, band + 1 - 2 * core)
    mirror = (me, band + 2 - 4 * plane)
    band_count = vec_got.shape[0]
    band_peers = [(me, (band + step) % band_count) for step in range(1, band_count)]
    greet([following, preceding] + band_peers)

    def owner_at(step, way):
        return ring_clip((place - way * (step + 1) + 2 * count) % count, count)

    def left_blocks(at):
        phase = phases[at]
        if phase["kind"] == 0:
            return [(b, phase["lefts"][0], b, 4) for b in range(4)] + [(4, phase["lefts"][1], 0, 1)]
        first = phase["first"]
        return [(first + i, left, 0, 1) for i, left in enumerate(phase["lefts"])]

    def right_blocks(at):
        phase = phases[at]
        if phase["kind"] == 0:
            return [(0, phase["lefts"][0], 0)] + [(1 + i, phase["lefts"][1], i) for i in range(4)]
        first = phase["first"]
        return [(first + i, phase["lefts"][i], 0) for i in range(3 - first)] + [
            (3 + i, phase["lefts"][-1], i) for i in range(3)
        ]

    def left_cols(step, way, which, many):
        width = lefts_width // count if many == 1 else deep_width // count
        start = owner_at(step, way) * width + which * 128
        return pl.ds(pl.multiple_of(start, 128), 128)

    lefts_width = lefts[phases[1]["lefts"][0]].shape[1]
    deep_width = lefts[phases[0]["lefts"][0]].shape[1]

    def pair_left(at, step):
        out = []
        for block, operand, which, many in left_blocks(at):
            cols = left_cols(step, -onward, which, many)
            out.append(
                pltpu.make_async_remote_copy(
                    lefts[operand].at[:, cols],
                    left_far[operand].at[:, cols],
                    pair_send.at[at, block, step],
                    pair_recv.at[at, block, step],
                    partner,
                    MESH,
                )
            )
        return out

    def pair_right(at):
        out = []
        for i, operand in enumerate(phases[at]["lefts"]):
            half = rights[operand].shape[1] // 2
            out.append(
                pltpu.make_async_remote_copy(
                    rights[operand].at[:, pl.ds(pl.multiple_of((1 - core) * half, 128), half)],
                    right_far[operand],
                    half_send.at[operand],
                    half_recv.at[operand],
                    partner,
                    MESH,
                )
            )
        return out

    def load_left(at, step, slot, far):
        kind = phases[at]["kind"]
        out = []
        for block, operand, which, many in left_blocks(at):
            cols = left_cols(step, onward, which, many)
            source = left_far if far else lefts
            out.append(
                pltpu.make_async_copy(
                    source[operand].at[:, cols],
                    left_buf[kind].at[slot, block, pl.ds(far * tokens, tokens), :],
                    left_sem.at[kind, slot, block, far],
                )
            )
        return out

    def load_right(at, far):
        kind = phases[at]["kind"]
        out = []
        for block, operand, which in right_blocks(at):
            if far:
                source = right_far[operand].at[:, pl.ds(which * UNIT[1], UNIT[1])]
            else:
                half = rights[operand].shape[1] // 2
                start = pl.multiple_of(core * half + which * UNIT[1], 128)
                source = rights[operand].at[:, pl.ds(start, UNIT[1])]
            out.append(
                pltpu.make_async_copy(
                    source,
                    right_buf[kind].at[block, pl.ds(far * tokens, tokens), :],
                    right_sem.at[kind, block, far],
                )
            )
        return out

    def ring_copies(at, part, slot):
        kind = phases[at]["kind"]
        units = pl.ds(*unit_parts(kind, phases[at]["first"])[part][:2])
        return [
            pltpu.make_async_remote_copy(
                put.at[slot, units],
                got.at[slot, units],
                ring_send.at[kind, slot, part, i],
                ring_recv.at[kind, slot, part, i],
                following,
                MESH,
            )
            for i, (put, got) in enumerate(
                ((put_low[kind], got_low[kind]), (put_scale[kind], got_scale[kind]))
            )
        ]

    def plane_copies(at, part):
        kind = phases[at]["kind"]
        units = pl.ds(*unit_parts(kind, phases[at]["first"])[part][:2])
        pairs = ((plane_put[kind], plane_got[at]),)
        if at + 1 == len(phases):
            pairs = ((last_put, last_got), (last_put_scale, last_got_scale))
        return [
            pltpu.make_async_remote_copy(
                here.at[units],
                there.at[units],
                plane_send.at[at, part, i],
                plane_recv.at[at, part, i],
                mirror,
                MESH,
            )
            for i, (here, there) in enumerate(pairs)
        ]

    def push_right(block):
        operand, which = [entry[1:] for entry in right_blocks(0) if entry[0] == block][0]
        half = rights[operand].shape[1] // 2
        begin = pl.multiple_of((1 - core) * half + which * UNIT[1], 128)
        return pltpu.make_async_remote_copy(
            rights[operand].at[:, pl.ds(begin, UNIT[1])],
            right_buf[phases[0]["kind"]].at[block, pl.ds(tokens, tokens), :],
            push_send.at[block],
            push_recv.at[block],
            partner,
            MESH,
        )

    def out_copies(at, unit):
        phase = phases[at]
        if phase["kind"] == 0 and unit < 4:
            half = UNIT[1]
            rows = deep_out.shape[0] // 4
            there = deep_out.at[
                pl.ds(unit * rows, rows),
                pl.ds(pl.multiple_of(phase["cols"][0] + core * half, 128), half),
            ]
        else:
            which, col = (1, unit - 4) if phase["kind"] == 0 else (unit - phase["first"], 0)
            if phase["kind"] and unit >= 3:
                which, col = len(phase["lefts"]) - 1, unit - 3
            half = rights[phase["lefts"][which]].shape[1] // 2
            start = phase["cols"][which] + core * half + col * UNIT[1]
            there = wide_out.at[:, pl.ds(pl.multiple_of(start, 128), UNIT[1])]
        here = plane_got[at].at[unit]
        return (
            pltpu.make_async_copy(here, there, out_sem.at[at, unit]),
            pltpu.make_async_remote_copy(
                here, there, out_send.at[at, unit], out_recv.at[at, unit], partner, MESH
            ),
        )

    def product(kind, slot, left, right):
        return lax.dot_general(
            left_buf[kind][slot, left],
            right_buf[kind][right],
            (((0,), (0,)), ((), ())),
            preferred_element_type=jnp.float32,
        )

    def start(copies):
        for copy in copies:
            copy.start()

    def finish(copies):
        for copy in copies:
            copy.wait()

    def take_step(at, step, first, last):
        phase = phases[at]
        kind = phase["kind"]
        slot = step % 2
        before = (step + 1) % 2
        for far in range(2):
            finish(load_left(at, step, slot, far))

        def load_next():
            for copy in pair_left(at, step + 1):
                copy.wait_recv()
            for far in range(2):
                start(load_left(at, step + 1, before, far))

        opening = first and at == 0
        if not (last or opening):
            load_next()
        parts = unit_parts(kind, phase["first"])

        def encode(term):
            largest = jnp.maximum(jnp.max(jnp.abs(term), axis=0, keepdims=True), WIRE_LEAST)
            low = jnp.round(term * (WIRE_MAX / largest)).astype(jnp.int16)
            return low, largest * (1.0 / WIRE_MAX)

        for part, (low, many, left_of, right_of) in enumerate(parts):
            if opening:
                blocks = range(1) if part == 0 else range(1, 5)
                finish(load_right(0, 0)[blocks.start : blocks.stop])
                for block in blocks:
                    push_right(block).wait_recv()
            if not first:
                for copy in ring_copies(at, part, before):
                    copy.wait_recv()
            if not (first or last):

                @pl.when(step >= 2)
                def _(part=part):
                    for copy in ring_copies(at, part, slot):
                        copy.wait_send()
                    pl.semaphore_wait(credit.at[kind, part], 1)

            def settle(position, unit, term):
                if not first:
                    came = got_low[kind][before, position].astype(jnp.float32)
                    term = term + came * got_scale[kind][before, position]
                if last and at + 1 == len(phases):
                    last_put[unit], last_put_scale[unit] = encode(term)
                elif last:
                    plane_put[kind][unit] = term
                else:
                    low_part, scale_part = encode(term)
                    put_low[kind][slot, position] = low_part
                    put_scale[kind][slot, position] = scale_part

            @pl.loop(low, low + many)
            def _(unit, left_of=left_of, right_of=right_of):
                settle(unit, unit, product(kind, slot, left_of(unit), right_of(unit)))

            if last:
                start(plane_copies(at, part))
            else:
                start(ring_copies(at, part, slot))
            if not (first or last):

                @pl.when(step < count - 2)
                def _(part=part):
                    pl.semaphore_signal(
                        credit.at[kind, part], inc=1, device_id=preceding, device_id_type=MESH
                    )

        if opening:
            load_next()

    def close(at):
        kind = phases[at]["kind"]

        def add_square(total):
            square_buf[...] += jnp.sum((total * total).reshape(UNIT[0] // 8, 8, UNIT[1]), axis=0)

        for part, (low, many, _, _) in enumerate(unit_parts(kind, phases[at]["first"])):
            finish(plane_copies(at, part))

            @pl.loop(low, low + many)
            def _(unit):
                if at + 1 == len(phases):
                    total = last_put[unit].astype(jnp.float32) * last_put_scale[unit]
                    total += last_got[unit].astype(jnp.float32) * last_got_scale[unit]
                else:
                    total = plane_put[kind][unit] + plane_got[at][unit]
                plane_got[at][unit] = total
                add_square(total)

            for unit in range(low, low + many):
                start(out_copies(at, unit))

    half_rows = pl.ds(pl.multiple_of(core * (vec_sum.shape[0] // 2), 8), vec_sum.shape[0] // 2)
    side_local = [
        pltpu.make_async_copy(vec_ref, vec_got.at[band], side_own.at[0]),
        pltpu.make_async_copy(kv_ref.at[band], kv_got.at[band], side_own.at[1]),
        pltpu.make_async_copy(text_ref, text_buf, side_own.at[2]),
    ]
    side_remote = []
    for step, peer in enumerate(band_peers):
        side_remote += [
            pltpu.make_async_remote_copy(
                vec_ref, vec_got.at[band], side_send.at[0, step], side_recv.at[0, step], peer, MESH
            ),
            pltpu.make_async_remote_copy(
                kv_ref.at[peer[1]],
                kv_got.at[band],
                side_send.at[1, step],
                side_recv.at[1, step],
                peer,
                MESH,
            ),
        ]
    vec_own = pltpu.make_async_copy(vec_sum, all_vec.at[me], side_own.at[3])

    def vec_copies(step):
        owner = ring_clip((place - onward * step + 2 * count) % count, count)
        vec = all_vec.at[owner, half_rows]
        return [
            pltpu.make_async_remote_copy(
                here, there, vec_send.at[step, i], vec_recv.at[step, i], following, MESH
            )
            for i, (here, there) in enumerate(((vec, vec), (all_kv.at[owner], all_kv.at[owner])))
        ]

    def vec_first():
        vec = all_vec.at[me, half_rows]
        return [
            pltpu.make_async_remote_copy(
                here, there, vec_send.at[0, i], vec_recv.at[0, i], following, MESH
            )
            for i, (here, there) in enumerate(
                ((vec_sum.at[half_rows], vec), (all_kv.at[me], all_kv.at[me]))
            )
        ]

    def vec_pair(step):
        owner = ring_clip((place - onward * (step + 1) + 2 * count) % count, count)
        vec = all_vec.at[owner, half_rows]
        return pltpu.make_async_remote_copy(
            vec, vec, vec_pair_send.at[step], vec_pair_recv.at[step], partner, MESH
        )

    kv_width = kv_grad.shape[1]

    def kv_place(owner):
        return kv_out.at[:, pl.ds(pl.multiple_of(owner * kv_width, 128), kv_width)]

    def kv_copy(i):
        if i == 2:
            return pltpu.make_async_copy(kv_grad, kv_place(band), kv_own)
        peer = (partner, mirror)[i]
        return pltpu.make_async_remote_copy(
            kv_grad, kv_place(band), kv_send.at[i], kv_recv.at[i], peer, MESH
        )

    def kv_passed():
        there = kv_place(mirror[1])
        return pltpu.make_async_remote_copy(
            there, there, kv_send.at[2], kv_recv.at[2], partner, MESH
        )

    def sum_bands():
        finish(side_local + side_remote)
        vec_sum[...] = jnp.sum(vec_got[...], 0)
        all_kv[me] = jnp.sum(kv_got[...], 0)
        vec_own.start()
        start(vec_first())

    def pass_sums(step):
        for copy in vec_copies(step - 1):
            copy.wait_recv()
        start(vec_copies(step))
        vec_pair(step - 1).start()

    def multiply_text():
        for copy in vec_copies(count - 2):
            copy.wait_recv()
        vec_pair(count - 2).start()
        grads = all_kv[...].reshape(text_buf.shape[0], -1)
        total = jnp.zeros_like(kv_grad)
        for _ in range(3):
            part = grads.astype(jnp.bfloat16)
            grads = grads - part.astype(jnp.float32)
            total = total + matmul_tn(text_buf[...], part)
        kv_grad[...] = total
        kv_square[...] = jnp.sum((total * total).reshape(-1, 8, total.shape[1]), axis=0)
        start([kv_copy(i) for i in range(3)])

    square_buf[...] = jnp.zeros_like(square_buf)
    start(side_local + side_remote)
    start(load_right(0, 0))
    start(load_left(0, 0, 0, 0))
    push_right(0).start()
    start(pair_left(0, 0))
    for block in range(1, 5):
        push_right(block).start()

    @pl.loop(1, count)
    def _(step):
        start(pair_left(0, step))

    for copy in pair_left(0, 0):
        copy.wait_recv()
    start(load_left(0, 0, 0, 1))
    take_step(0, 0, True, False)
    for at in range(len(phases)):
        more = at + 1 < len(phases)
        if more:
            start(pair_right(at + 1))
            start(load_right(at + 1, 0))
            start(pair_left(at + 1, 0))
        if at == 1:
            sum_bands()

        @pl.loop(1, count - 1)
        def _(step, at=at, more=more):
            take_step(at, step, False, False)
            if at == 1:
                pass_sums(step)
            if more:
                start(pair_left(at + 1, step))

                @pl.when(step == count // 2)
                def _():
                    for copy in pair_right(at + 1):
                        copy.wait_recv()
                    start(load_right(at + 1, 1))
                    for copy in pair_left(at + 1, 0):
                        copy.wait_recv()
                    for far in range(2):
                        start(load_left(at + 1, 0, 0, far))

        if more:
            start(pair_left(at + 1, count - 1))
            for far in range(2):
                finish(load_right(at + 1, far))
            take_step(at + 1, 0, True, False)
        take_step(at, count - 1, False, True)
        if at == 1:
            multiply_text()
        for part in range(2):
            for slot in range(2):
                for copy in ring_copies(at, part, slot):
                    copy.wait_send()
        if at == 2:
            kv_copy(1).wait_recv()
            kv_passed().start()
        if at:
            close(at - 1)
    close(len(phases) - 1)
    vec_own.wait()
    kv_passed().wait()
    kv_copy(0).wait()
    kv_copy(1).wait_send()
    kv_copy(2).wait()

    @pl.loop(0, count - 1)
    def _(step):
        for copy in vec_copies(step):
            copy.wait_send()
        vec_pair(step).wait()

    square_out[...] = square_buf[...]
    for at, phase in enumerate(phases):
        for copy in pair_right(at) if at else [push_right(block) for block in range(5)]:
            copy.wait_send()

        @pl.loop(0, count)
        def _(step, at=at):
            for copy in pair_left(at, step):
                copy.wait_send()

        for unit in range(phase["first"], 8 if phase["kind"] == 0 else 6):
            finish(out_copies(at, unit))


def reduce_gradients(phases, lefts, rights, vectors, keyvals, text, wide_cols, deep_cols):
    count = lax.axis_size("clip")
    tokens = lefts[0].shape[0]
    wide_rows = lefts[1].shape[1] // count
    deep_rows = lefts[0].shape[1] // count
    band_count, _, kv_cols = keyvals.shape
    num = len(lefts)
    dma = pltpu.SemaphoreType.DMA
    units, lefts_of, rights_of = (8, 6), (5, 4), (5, 6)
    scratch = [pltpu.VMEM((2, lefts_of[k], 2 * tokens, 128), jnp.bfloat16) for k in range(2)]
    scratch += [pltpu.VMEM((rights_of[k], 2 * tokens, UNIT[1]), jnp.bfloat16) for k in range(2)]
    for _ in range(2):
        scratch += [pltpu.VMEM((2, units[k]) + UNIT, jnp.int16) for k in range(2)]
        scratch += [pltpu.VMEM((2, units[k], 1, UNIT[1]), jnp.float32) for k in range(2)]
    scratch += [pltpu.VMEM((units[k],) + UNIT, jnp.float32) for k in range(2)]
    scratch += [pltpu.VMEM((units[p["kind"]],) + UNIT, jnp.float32) for p in phases]
    scratch += [
        pltpu.VMEM((8, UNIT[1]), jnp.float32),
        dma((2, 2, 5, 2)),
        dma((2, 6, 2)),
        dma((len(phases), 5, count)),
        dma((len(phases), 5, count)),
        dma((num,)),
        dma((num,)),
        dma((2, 2, 2, 2)),
        dma((2, 2, 2, 2)),
        pltpu.SemaphoreType.REGULAR((2, 2)),
        dma((len(phases), 2, 2)),
        dma((len(phases), 2, 2)),
        dma((len(phases), 8)),
        dma((len(phases), 8)),
        dma((len(phases), 8)),
    ]
    for _ in range(2):
        scratch += [pltpu.VMEM((6,) + UNIT, jnp.int16), pltpu.VMEM((6, 1, UNIT[1]), jnp.float32)]
    scratch += [
        dma((5,)),
        dma((5,)),
        pltpu.VMEM((band_count,) + vectors.shape, jnp.float32),
        pltpu.VMEM(keyvals.shape, jnp.float32),
        pltpu.VMEM(vectors.shape, jnp.float32),
        pltpu.VMEM((count,) + keyvals.shape[1:], jnp.float32),
        pltpu.VMEM(text.shape, jnp.bfloat16),
        pltpu.VMEM((text.shape[1], kv_cols), jnp.float32),
        dma((4,)),
        dma((2, band_count - 1)),
        dma((2, band_count - 1)),
        dma((count - 1, 2)),
        dma((count - 1, 2)),
        dma((count - 1,)),
        dma((count - 1,)),
        dma,
        dma((3,)),
        dma((3,)),
    ]
    out = pl.pallas_call(
        partial(reduce_kernel, count, tokens, phases),
        out_shape=(
            jax.ShapeDtypeStruct((wide_rows, wide_cols), jnp.float32),
            jax.ShapeDtypeStruct((deep_rows, deep_cols), jnp.float32),
            jax.ShapeDtypeStruct((8, UNIT[1]), jnp.float32),
            jax.ShapeDtypeStruct((count,) + vectors.shape, jnp.float32),
            jax.ShapeDtypeStruct((deep_rows, band_count * kv_cols), jnp.float32),
            jax.ShapeDtypeStruct((8, kv_cols), jnp.float32),
        )
        + tuple(jax.ShapeDtypeStruct(x.shape, x.dtype) for x in lefts)
        + tuple(jax.ShapeDtypeStruct((tokens, x.shape[1] // 2), x.dtype) for x in rights),
        in_specs=[ANY] * (2 * num + 3),
        out_specs=(ANY, ANY, IN_VMEM, ANY, ANY, IN_VMEM) + (ANY,) * (2 * num),
        scratch_shapes=scratch,
        compiler_params=pltpu.CompilerParams(
            collective_id=2, has_side_effects=True, vmem_limit_bytes=58 << 20
        ),
        cost_estimate=pl.CostEstimate(flops=3 * 10**11, bytes_accessed=8 * 10**8, transcendentals=0),
    )(*lefts, *rights, vectors, keyvals, text)
    return out[:6]


def total_kernel(count, part_ref, out_ref, mid, band_got, clip_got, *sems):
    me = lax.axis_index("clip")
    band = lax.axis_index("band")
    band_count = band_got.shape[0]
    band_peers = [(me, (band + step) % band_count) for step in range(1, band_count)]
    clip_peers = [((me + step) % count, band) for step in range(1, count)]
    greet(band_peers + clip_peers)
    stages = (
        (part_ref, band_got, band, band_peers, mid, sems[:2]),
        (mid, clip_got, me, clip_peers, out_ref, sems[2:]),
    )
    for value, got, index, peers, result, (send, recv) in stages:
        copies = [
            pltpu.make_async_remote_copy(
                value, got.at[index], send.at[step], recv.at[step], peer, MESH
            )
            for step, peer in enumerate(peers)
        ]
        for copy in copies:
            copy.start()
        got[index] = value[...]
        for copy in copies:
            copy.wait()
        result[...] = jnp.sum(got[...], 0)


def total_over_devices(value):
    count, band_count = lax.axis_size("clip"), lax.axis_size("band")
    dma = pltpu.SemaphoreType.DMA
    tile = (8, 128)
    return pl.pallas_call(
        partial(total_kernel, count),
        out_shape=jax.ShapeDtypeStruct(tile, jnp.float32),
        in_specs=[IN_VMEM],
        out_specs=IN_VMEM,
        scratch_shapes=[
            pltpu.VMEM(tile, jnp.float32),
            pltpu.VMEM((band_count,) + tile, jnp.float32),
            pltpu.VMEM((count,) + tile, jnp.float32),
            dma((band_count - 1,)),
            dma((band_count - 1,)),
            dma((count - 1,)),
            dma((count - 1,)),
        ],
        compiler_params=pltpu.CompilerParams(collective_id=3, has_side_effects=True),
    )(jnp.broadcast_to(value, tile))[0, 0]


def per_device(
    latents,
    noise_field,
    timesteps,
    null_flags,
    frame_mask,
    context,
    w_wide,
    m_wide,
    v_wide,
    w_deep,
    m_deep,
    v_deep,
    w_small,
    m_small,
    v_small,
):
    clip_count = lax.axis_size("clip")
    band_count = lax.axis_size("band")
    clip_at = lax.axis_index("clip")
    band_at = lax.axis_index("band")
    wide_rows = w_wide.shape[0]
    deep_rows = w_deep.shape[0]
    text_len, text_dim = context.shape[1:]
    facts = jnp.pad(
        jnp.concatenate([timesteps, frame_mask[0]])[None],
        ((0, 7), (0, 127 - frame_mask.shape[1])),
    )
    kept_text = context[0] * (1 - null_flags[0]).astype(jnp.bfloat16)
    text_cols = jnp.pad(
        kept_text.reshape(text_len, clip_count, deep_rows).transpose(1, 0, 2),
        ((0, 0), (0, TEXT_PAD - text_len), (0, 0)),
    )
    all_facts, all_text = exchange_facts(facts, text_cols)
    all_times = all_facts[:, 0, 0].astype(jnp.float32)
    all_time_low = jax.nn.silu(time_features(all_times)).astype(jnp.bfloat16)
    time_rows = lax.dynamic_slice(
        all_time_low, (0, clip_at * wide_rows), (clip_count, wide_rows)
    )
    part_modul = matmul(time_rows, w_wide[:, : 12 * D].astype(jnp.bfloat16))
    kv_cols = 2 * D // band_count
    kv_weight = lax.dynamic_slice(
        w_deep, (0, D + band_at * kv_cols), (deep_rows, kv_cols)
    ).astype(jnp.bfloat16)
    part_kv = matmul(all_text.reshape(clip_count * TEXT_PAD, deep_rows), kv_weight)
    up_b_w = gather_quarters(w_wide[:, 22 * D + FF :])
    edges = (12 * D, 15 * D, 18 * D, 19 * D, 20 * D, 21 * D, 22 * D, 22 * D + FF)
    shards = [w_wide[:, low:high].astype(jnp.bfloat16) for low, high in zip(edges, edges[1:])]
    shards += [w_deep[:, :D].astype(jnp.bfloat16)]
    gathered, all_modul, all_kv = gather_weights(
        shards,
        (0, 0, 1, 2, 1, 2, 1, 2),
        part_modul.reshape(clip_count, 12 * D // 128, 128),
        part_kv.reshape(clip_count, TEXT_PAD, kv_cols),
    )
    qkv_a_w, qkv_b_w, out_a_w, out_b_w, query_w, cross_out_w, up_a_w, down_a_w = gathered
    late_down_b, all_modul = lax.optimization_barrier((w_deep[:, 3 * D :], all_modul))
    down_b_w = gather_quarters(late_down_b)
    keyval = lax.all_gather(jnp.sum(all_kv, 0).astype(jnp.bfloat16), "band", axis=1, tiled=True)
    small_low = w_small.astype(jnp.bfloat16)
    small_val = small_low.astype(jnp.float32)
    num_frames, num_rows, num_cols = (latents.shape[1], latents.shape[2], latents.shape[3])
    tok_count = num_frames * num_rows * num_cols
    all_mask = all_facts[:, 0, 1 : 1 + num_frames]
    global_count = jnp.sum(all_mask).astype(jnp.float32) * (num_rows * num_cols * CH * band_count)
    time_value = timesteps[0].astype(jnp.float32)
    noise_angle = 0.5 * math.pi * time_value / TMAX
    signal, spread = (jnp.cos(noise_angle), jnp.sin(noise_angle))
    clean_tok = token_order(latents[0])
    noise_tok = token_order(noise_field[0])
    run = num_rows * WIN
    part = SHIFT * WIN
    frame_windows = attend_pieces(tok_count, num_frames, "frame")
    half_windows = attend_pieces(tok_count, num_frames, "half")
    text_windows = attend_pieces(tok_count, num_frames, "text")
    noisy_low = (signal * clean_tok + spread * noise_tok).astype(jnp.bfloat16)
    target = signal * noise_tok - spread * clean_tok
    modulation = jnp.sum(all_modul, 0).reshape(12, D)
    mod_a, mod_b = (modulation[:6], modulation[6:])
    stream_zero = matmul(noisy_low, small_low[:CH]) + small_val[2 * CH]
    normed_a, back_a = jax.vjp(norm_modulated, stream_zero, mod_a[0], mod_a[1])
    in_a = normed_a.astype(jnp.bfloat16)
    qkv_a = matmul(in_a, qkv_a_w).astype(jnp.bfloat16)
    far_kv = from_partner(qkv_a[:, D:], "band", 0)
    space_kv = [(qkv_a, HEADS // 2, HEADS), (far_kv, 0, HEADS // 2)]
    att_a = attend(qkv_a, space_kv, frame_windows)
    proj_a = matmul(att_a, out_a_w)
    stream_one = stream_zero + mod_a[2] * proj_a
    stream_two, saved_a = mlp_forward(stream_one, mod_a, up_a_w, down_a_w)
    normed_b, back_b = jax.vjp(norm_modulated, stream_two, mod_b[0], mod_b[1])
    low_b = normed_b.astype(jnp.bfloat16)
    rolled = with_rows(low_b, shifted(first_rows(low_b, run, part), "band", -1), run)
    qkv_b = matmul(rolled, qkv_b_w).astype(jnp.bfloat16)
    win_kv = [(qkv_b, HEADS // 2, HEADS)]
    win_out = attend(qkv_b, win_kv, half_windows)
    att_b = with_rows(win_out, shifted(first_rows(win_out, run, part), "band", 1), run)
    proj_b = matmul(att_b, out_b_w)
    stream_three = stream_two + mod_b[2] * proj_b
    cross_val, cross_back = jax.vjp(norm_gained, stream_three, small_val[2 * CH + 1])
    cross_in = cross_val.astype(jnp.bfloat16)
    query_proj = matmul(cross_in, query_w).astype(jnp.bfloat16)
    text_kv = [(keyval, 0, HEADS // 2)]
    crossed = attend(query_proj, text_kv, text_windows, text_len)
    stream_four = stream_three + matmul(crossed, cross_out_w)
    stream_five, saved_b = mlp_forward(stream_four, mod_b, up_b_w, down_b_w)
    final_val, final_back = jax.vjp(norm_gained, stream_five, small_val[2 * CH + 2])
    final_low = final_val.astype(jnp.bfloat16)
    head_low = small_low[CH : 2 * CH]
    predicted = matmul_nt(final_low, head_low)
    weight_row = jnp.repeat(frame_mask[0].astype(jnp.float32), run)
    weight_row = jnp.tile(weight_row, num_cols // WIN)[:, None]
    pred_error = predicted - target
    loss_part = jnp.sum(weight_row * pred_error * pred_error)
    grad_pred = (weight_row * pred_error * (2.0 / global_count)).astype(jnp.bfloat16)
    grad_head = matmul_tn(grad_pred, final_low)
    grad_stream, grad_gain_f = final_back(matmul(grad_pred, head_low))
    grad_stream, mlp_factors_b, extra_b = mlp_backward(
        grad_stream, mod_b, up_b_w, down_b_w, saved_b
    )
    grad_cross = grad_stream.astype(jnp.bfloat16)
    grad_crossed = matmul_nt(grad_cross, cross_out_w).astype(jnp.bfloat16)
    grad_query, grad_keyval = attend_back(
        query_proj, text_kv, grad_crossed, text_windows, text_len
    )
    grad_part, grad_gain_c = cross_back(matmul_nt(grad_query, query_w))
    grad_stream = grad_stream + grad_part
    grad_proj = (mod_b[2] * grad_stream).astype(jnp.bfloat16)
    grad_gate_b = jnp.sum(grad_stream * proj_b, 0)
    factors_ob = (att_b, grad_proj)
    grad_att = matmul_nt(grad_proj, out_b_w).astype(jnp.bfloat16)
    grad_win = with_rows(grad_att, shifted(first_rows(grad_att, run, part), "band", -1), run)
    grad_qkv = attend_back(qkv_b, win_kv, grad_win, half_windows)[0]
    factors_qkvb = (rolled, grad_qkv)
    grad_in_roll = matmul_nt(grad_qkv, qkv_b_w)
    sent_back = shifted(first_rows(grad_in_roll, run, part), "band", 1)
    grad_normed = with_rows(grad_in_roll, sent_back, run)
    grad_part, grad_shift_b, grad_scale_b = back_b(grad_normed)
    grad_stream = grad_stream + grad_part
    grad_stream, mlp_factors_a, extra_a = mlp_backward(
        grad_stream, mod_a, up_a_w, down_a_w, saved_a
    )
    grad_proj = (mod_a[2] * grad_stream).astype(jnp.bfloat16)
    grad_gate_a = jnp.sum(grad_stream * proj_a, 0)
    factors_oa = (att_a, grad_proj)
    grad_att = matmul_nt(grad_proj, out_a_w).astype(jnp.bfloat16)
    grad_q, grad_own, grad_far = attend_back(qkv_a, space_kv, grad_att, frame_windows)
    grad_kv = grad_own + from_partner(grad_far, "band", 0)
    grad_qkv = jnp.concatenate([grad_q, grad_kv.astype(jnp.bfloat16)], 1)
    factors_qkva = (in_a, grad_qkv)
    grad_part, grad_shift_a, grad_scale_a = back_a(matmul_nt(grad_qkv, qkv_a_w))
    grad_stream = grad_stream + grad_part
    grad_patch = matmul_tn(noisy_low.astype(jnp.float32), grad_stream, lax.Precision.HIGHEST)
    grad_bias = jnp.sum(grad_stream, 0)
    grad_modul = jnp.stack(
        [
            grad_shift_a,
            grad_scale_a,
            grad_gate_a,
            extra_a[0],
            extra_a[1],
            extra_a[2],
            grad_shift_b,
            grad_scale_b,
            grad_gate_b,
            extra_b[0],
            extra_b[1],
            extra_b[2],
        ]
    ).reshape(1, 12 * D)
    grad_small = jnp.concatenate(
        [grad_patch, grad_head, grad_bias[None], grad_gain_c[None], grad_gain_f[None]], 0
    )
    factors = mlp_factors_b + (
        (crossed, grad_cross),
        (cross_in, grad_query),
        factors_ob,
        factors_qkvb,
    )
    factors += mlp_factors_a + (factors_oa, factors_qkva)
    if wide_rows == 128 and deep_rows == 512:
        phases = (
            {"kind": 0, "first": 0, "lefts": (0, 1), "cols": (D, 10 * D + FF)},
            {"kind": 1, "first": 0, "lefts": (2, 3, 4, 5), "cols": (9 * D, 8 * D, 7 * D, 3 * D)},
            {"kind": 0, "first": 0, "lefts": (6, 7), "cols": (0, 10 * D)},
            {"kind": 1, "first": 2, "lefts": (8, 9), "cols": (6 * D, 0)},
        )
        used = 12 * D + grad_small.size
        vectors = jnp.concatenate(
            [grad_modul.reshape(-1), grad_small.reshape(-1), loss_part[None]]
        )
        vectors = jnp.pad(vectors, (0, 256 * 128 - vectors.shape[0])).reshape(256, 128)
        keyvals = grad_keyval.reshape(TEXT_PAD, band_count, kv_cols).transpose(1, 0, 2)
        wide_rest, deep_rest, squares, all_vectors, grad_w_ckv, kv_squares = reduce_gradients(
            phases,
            [f[0] for f in factors],
            [f[1] for f in factors],
            vectors,
            keyvals,
            all_text.reshape(clip_count * TEXT_PAD, deep_rows),
            10 * D + 2 * FF,
            2 * D,
        )
        all_vectors = all_vectors.reshape(clip_count, -1)
        all_grad_modul = all_vectors[:, : 12 * D]
        small_sum = jnp.sum(all_vectors[:, 12 * D : used], 0).reshape(grad_small.shape)
        loss_sum = jnp.sum(all_vectors[:, used])
        square_part = jnp.sum(squares) / (band_count // 2) + jnp.sum(kv_squares)
    else:
        summed = [sum_rows(*pair) for pair in factors]
        wide_rest = jnp.concatenate([summed[i] for i in (9, 5, 8, 4, 3, 2, 7, 1)], 1)
        deep_rest = jnp.concatenate([summed[6], summed[0]], 1)
        grad_keyval = lax.psum_scatter(grad_keyval, "band", scatter_dimension=1, tiled=True)
        grad_keyval = lax.all_gather(grad_keyval, "clip", axis=0, tiled=True)
        grad_w_ckv = matmul_tn(
            all_text.reshape(clip_count * TEXT_PAD, deep_rows).astype(jnp.float32),
            grad_keyval,
            lax.Precision.HIGHEST,
        )
        grad_w_ckv = lax.all_gather(grad_w_ckv, "band", axis=1, tiled=True)
        all_grad_modul = lax.all_gather(lax.psum(grad_modul, "band"), "clip", axis=0, tiled=True)
        loss_sum, small_sum = lax.psum((loss_part, grad_small), ("clip", "band"))
        square_part = sum(jnp.sum(x * x) for x in (wide_rest, deep_rest, grad_w_ckv)) / band_count
    grad_w_ada = matmul_tn(time_rows.astype(jnp.float32), all_grad_modul, lax.Precision.HIGHEST)
    wide_sum = jnp.concatenate([grad_w_ada, wide_rest], 1)
    deep_sum = jnp.concatenate([deep_rest[:, :D], grad_w_ckv, deep_rest[:, D:]], 1)
    square_part += jnp.sum(grad_w_ada * grad_w_ada) / band_count
    square_sum = total_over_devices(square_part)
    grad_norm = jnp.sqrt(square_sum + jnp.sum(small_sum * small_sum))
    factor = CLIP_MAX / jnp.maximum(grad_norm, CLIP_MAX)
    new_wide = adam_update(w_wide, m_wide, v_wide, wide_sum * factor, 0.15)
    new_deep = adam_update(w_deep, m_deep, v_deep, deep_sum * factor, 0.05)
    new_small = adam_update(w_small, m_small, v_small, small_sum * factor, 0.5)
    loss = loss_sum / global_count
    return (
        loss,
        grad_norm,
        new_wide[0],
        new_wide[1],
        new_wide[2],
        new_deep[0],
        new_deep[1],
        new_deep[2],
        new_small[0],
        new_small[1],
        new_small[2],
    )


def solution(mesh):
    in_specs = (
        P("clip", None, "band", None, None),
        P("clip", None, "band", None, None),
        P("clip"),
        P("clip"),
        P("clip", None),
        P("clip", None, None),
        P("clip", None),
        P("clip", None),
        P("clip", None),
        P("clip", None),
        P("clip", None),
        P("clip", None),
        P(),
        P(),
        P(),
    )
    out_specs = (
        P(),
        P(),
        P("clip", None),
        P("clip", None),
        P("clip", None),
        P("clip", None),
        P("clip", None),
        P("clip", None),
        P(),
        P(),
        P(),
    )
    return jax.shard_map(
        per_device, mesh=mesh, in_specs=in_specs, out_specs=out_specs, check_vma=False
    )
```

```python
from functools import partial
import math

import jax
import jax.numpy as jnp
from jax import lax
from jax.experimental import pallas as pl
from jax.experimental.pallas import tpu as pltpu
from jax.sharding import PartitionSpec as P

D = 1024
HEADS = 16
HEAD_DIM = 64
FF = 4096
CH = 8
SPACE = 16
WIN = 8
SHIFT = 4
TMAX = 1000
STEP = 10


EPS_NORM = 1e-06
CLIP_MAX = 0.001
BETA_ONE = 0.9
BETA_TWO = 0.95
ADAM_EPS = 1e-08
DECAY = 0.1


def from_partner(block, axis, distance):
    count = lax.axis_size(axis)
    route = []
    for low in range(count):
        high = low | 1 << distance
        if high != low and high < count:
            route += [(low, high), (high, low)]
    return lax.ppermute(block, axis, route)


def shifted(value, axis, by):
    length = lax.axis_size(axis)
    return lax.ppermute(value, axis, [(i, (i + by) % length) for i in range(length)])


def matmul(left_op, right_op):
    return jnp.dot(left_op, right_op, preferred_element_type=jnp.float32)


def matmul_tn(left_op, right_op, precision=None):
    return lax.dot_general(
        left_op,
        right_op,
        (((0,), (0,)), ((), ())),
        precision=precision,
        preferred_element_type=jnp.float32,
    )


def matmul_nt(left_op, right_op):
    return lax.dot_general(
        left_op, right_op, (((1,), (1,)), ((), ())), preferred_element_type=jnp.float32
    )


def layer_norm(field_in):
    average = jnp.mean(field_in, -1, keepdims=True)
    centred = field_in - average
    return centred * lax.rsqrt(jnp.mean(centred * centred, -1, keepdims=True) + EPS_NORM)


def norm_modulated(field_in, shift_vec, scale_vec):
    return layer_norm(field_in) * (1.0 + scale_vec) + shift_vec


def norm_gained(field_in, gain_vec):
    return layer_norm(field_in) * gain_vec


def time_features(time_value):
    half_width = D // 2
    frequency = jnp.exp(-math.log(10000.0) * jnp.arange(half_width, dtype=jnp.float32) / half_width)
    angles = time_value[..., None] * frequency
    return jnp.concatenate([jnp.cos(angles), jnp.sin(angles)], -1)


def token_order(grid):
    frames, rows, cols, width = grid.shape
    halves = grid.reshape(frames, rows, cols // WIN, WIN, width).transpose(2, 0, 1, 3, 4)
    return halves.reshape(frames * rows * cols, width)


def with_rows(tokens, first_rows, run):
    width = tokens.shape[1]
    runs = tokens.reshape(-1, run, width)
    return jnp.concatenate([first_rows, runs[:, first_rows.shape[1] :]], 1).reshape(-1, width)


def first_rows(tokens, run, part):
    return tokens.reshape(-1, run, tokens.shape[1])[:, :part]


def attend_pieces(tokens, frames, keys):
    if keys == "frame":
        run = tokens // (2 * frames)
        return [((f * run, run), (tokens // 2 + f * run, run)) for f in range(frames)]
    if keys == "half":
        return [((half * (tokens // 2), tokens // 2),) for half in range(2)]
    return [((0, tokens),)]


def take(ref, runs):
    pieces = [ref[low : low + many, :] for low, many in runs]
    return pieces[0] if len(pieces) == 1 else jnp.concatenate(pieces, 0)


def put(ref, cols, runs, value):
    done = 0
    for low, many in runs:
        ref[low : low + many, cols] = value[done : done + many].astype(ref.dtype)
        done += many


def softmax_of(scores, axis, text_len):
    if text_len:
        place = lax.broadcasted_iota(jnp.int32, scores.shape, axis)
        scores = jnp.where(place < text_len, scores, -1e30)
    weight = jnp.exp(scores - jnp.max(scores, axis, keepdims=True))
    return weight * (1.0 / jnp.sum(weight, axis, keepdims=True))


def lanes_of(head, shape):
    lane = lax.broadcasted_iota(jnp.int32, shape, 1)
    return lane < HEAD_DIM if head == 0 else lane >= HEAD_DIM


def only(head, value):
    return jnp.where(lanes_of(head, value.shape), value, jnp.zeros_like(value))


def key_sets(key_refs, runs, text_len):
    if text_len:
        return key_refs[0][...]
    pieces = [take(ref, runs) for ref in key_refs]
    return pieces[0] if len(pieces) == 1 else jnp.concatenate(pieces, 0)


def attend_kernel(windows, text_len, sets, *refs):
    q_ref, k_refs, v_refs, out_ref = refs[0], refs[1 : 1 + sets], refs[1 + sets : 1 + 2 * sets], refs[-1]
    for runs in windows:
        queries = take(q_ref, runs) * HEAD_DIM ** (-0.5)
        keys, values = key_sets(k_refs, runs, text_len), key_sets(v_refs, runs, text_len)
        outs = []
        for head in range(2):
            probs = softmax_of(matmul_nt(only(head, queries), keys), 1, text_len)
            outs.append(matmul(probs.astype(jnp.bfloat16), values))
        put(out_ref, slice(None), runs, jnp.where(lanes_of(0, outs[0].shape), *outs))


def attend_back_kernel(windows, text_len, sets, *refs):
    q_ref, k_refs, v_refs = refs[0], refs[1 : 1 + sets], refs[1 + sets : 1 + 2 * sets]
    grad_ref = refs[1 + 2 * sets]
    dq_ref = refs[2 + 2 * sets]
    own_ref = refs[3 + 2 * sets] if len(refs) > 3 + 2 * sets else None
    far_ref = refs[4 + 2 * sets] if sets == 2 else None
    pair = pl.program_id(0)
    cols = [pl.ds(pl.multiple_of(i * D + pair * 2 * HEAD_DIM, 128), 2 * HEAD_DIM) for i in range(3)]
    merged = dq_ref.shape[1] == 3 * D
    for runs in windows:
        queries = take(q_ref, runs) * HEAD_DIM ** (-0.5)
        keys, values = key_sets(k_refs, runs, text_len), key_sets(v_refs, runs, text_len)
        grad_out = take(grad_ref, runs)
        dq, dk, dv = [], [], []
        for head in range(2):
            probs = softmax_of(matmul_nt(keys, only(head, queries)), 0, text_len)
            dprobs = matmul_nt(values, only(head, grad_out))
            dv.append(matmul(probs.astype(jnp.bfloat16), grad_out))
            inner = jnp.sum(probs * dprobs, 0, keepdims=True)
            dscores = (probs * (dprobs - inner)).astype(jnp.bfloat16)
            dk.append(matmul(dscores, queries))
            dq.append(matmul_tn(dscores, keys))
        dq, dk, dv = (jnp.where(lanes_of(0, x[0].shape), *x) for x in (dq, dk, dv))
        put(dq_ref, cols[0], runs, dq * HEAD_DIM ** (-0.5))
        if merged:
            put(dq_ref, cols[1], runs, dk)
            put(dq_ref, cols[2], runs, dv)
        elif text_len:
            own_ref[:, cols[0]] = dk
            own_ref[:, cols[1]] = dv
        else:
            half = dk.shape[0] // 2
            put(own_ref, cols[0], runs, dk[:half])
            put(own_ref, cols[1], runs, dv[:half])
            put(far_ref, cols[0], runs, dk[half:])
            put(far_ref, cols[1], runs, dv[half:])


def head_cols(array, first):
    return array, pl.BlockSpec((array.shape[0], 2 * HEAD_DIM), lambda h: (0, first + h))


def attention_operands(queries, key_values):
    ins = [head_cols(queries, 0)]
    ins += [head_cols(array, first) for array, first, _ in key_values]
    return ins + [head_cols(array, second) for array, _, second in key_values]


def attention_cost(tokens, keys, products):
    flops = 2 * products * tokens * keys * D * 2
    return pl.CostEstimate(
        flops=flops, bytes_accessed=tokens * D * 2 * 8, transcendentals=tokens * keys * HEADS
    )


def attend(queries, key_values, windows, text_len=0):
    tokens = queries.shape[0]
    ins = attention_operands(queries, key_values)
    return pl.pallas_call(
        partial(attend_kernel, windows, text_len, len(key_values)),
        grid=(HEADS // 2,),
        in_specs=[spec for _, spec in ins],
        out_specs=pl.BlockSpec((tokens, 2 * HEAD_DIM), lambda h: (0, h)),
        out_shape=jax.ShapeDtypeStruct((tokens, D), jnp.bfloat16),
        compiler_params=pltpu.CompilerParams(vmem_limit_bytes=40 << 20),
        cost_estimate=attention_cost(tokens, 320, 2),
    )(*[array for array, _ in ins])


def attend_back(queries, key_values, grad_out, windows, text_len=0):
    tokens = queries.shape[0]
    ins = attention_operands(queries, key_values) + [head_cols(grad_out, 0)]
    sets = len(key_values)
    whole = lambda rows, cols: pl.BlockSpec((rows, cols), lambda h: (0, 0))
    if sets == 1 and not text_len:
        outs = [((tokens, 3 * D), jnp.bfloat16)]
    else:
        rows = key_values[0][0].shape[0]
        outs = [((tokens, D), jnp.bfloat16)] + [((rows, 2 * D), jnp.float32)] * sets
    return pl.pallas_call(
        partial(attend_back_kernel, windows, text_len, sets),
        grid=(HEADS // 2,),
        in_specs=[spec for _, spec in ins],
        out_specs=[whole(*shape) for shape, _ in outs],
        out_shape=[jax.ShapeDtypeStruct(*out) for out in outs],
        compiler_params=pltpu.CompilerParams(vmem_limit_bytes=50 << 20),
        cost_estimate=attention_cost(tokens, 320, 5),
    )(*[array for array, _ in ins])


def mlp_forward(stream, modul, up_weight, down_weight):
    mlp_val, norm_back = jax.vjp(norm_modulated, stream, modul[3], modul[4])
    mlp_in = mlp_val.astype(jnp.bfloat16)
    up_proj = matmul(mlp_in, up_weight)
    share = 0.5 + 0.5 * lax.erf(up_proj * math.sqrt(0.5))
    gelu_val = up_proj * share
    slope = share + up_proj * (jnp.exp(-0.5 * up_proj * up_proj) / math.sqrt(2.0 * math.pi))
    gelu_low = gelu_val.astype(jnp.bfloat16)
    down_proj = matmul(gelu_low, down_weight)
    return (stream + modul[5] * down_proj, (norm_back, mlp_in, slope, gelu_low, down_proj))


def mlp_backward(grad_stream, modul, up_weight, down_weight, saved):
    norm_back, mlp_in, slope, gelu_low, down_proj = saved
    grad_down = (modul[5] * grad_stream).astype(jnp.bfloat16)
    grad_gate = jnp.sum(grad_stream * down_proj, 0)
    grad_up = (slope * matmul_nt(grad_down, down_weight)).astype(jnp.bfloat16)
    grad_part, grad_shift, grad_scale = norm_back(matmul_nt(grad_up, up_weight))
    factors = ((gelu_low, grad_down), (mlp_in, grad_up))
    return (grad_stream + grad_part, factors, (grad_shift, grad_scale, grad_gate))


def adam_update(weight, first_mom, second_mom, grad_val, learn_rate):
    first_mom = BETA_ONE * first_mom + (1.0 - BETA_ONE) * grad_val
    second_mom = BETA_TWO * second_mom + (1.0 - BETA_TWO) * grad_val * grad_val
    first_hat = first_mom / (1.0 - BETA_ONE**STEP)
    second_hat = second_mom / (1.0 - BETA_TWO**STEP)
    weight = weight - learn_rate * (first_hat / (jnp.sqrt(second_hat) + ADAM_EPS) + DECAY * weight)
    return (weight, first_mom, second_mom)

MESH = pl.DeviceIdType.MESH
ANY = pl.BlockSpec(memory_space=pl.ANY)
IN_VMEM = pl.BlockSpec(memory_space=pltpu.VMEM)
TEXT_PAD = 80


def ring_place(clip, count):
    half = clip // 2
    odd = clip % 2
    return half + odd * (count - 1 - 2 * half)


def ring_clip(place, count):
    far = place // (count // 2)
    return (1 - far) * 2 * place + far * (2 * (count - 1 - place) + 1)


def greet(peers):
    barrier = pltpu.get_barrier_semaphore()
    for peer in peers:
        pl.semaphore_signal(barrier, inc=1, device_id=peer, device_id_type=MESH)
    pl.semaphore_wait(barrier, len(peers))


def exchange_kernel(count, facts_ref, facts_out, send, recv):
    me = lax.axis_index("clip")
    band = lax.axis_index("band")
    peers = [((me + step) % count, band) for step in range(1, count)]
    greet(peers)
    sent = [
        pltpu.make_async_remote_copy(
            facts_ref, facts_out.at[me], send.at[step], recv.at[step], peer, MESH
        )
        for step, peer in enumerate(peers)
    ]
    for copy in sent:
        copy.start()
    facts_out[me] = facts_ref[...]
    for copy in sent:
        copy.wait()


def exchange_facts(facts):
    count = lax.axis_size("clip")
    return pl.pallas_call(
        partial(exchange_kernel, count),
        out_shape=jax.ShapeDtypeStruct((count,) + facts.shape, facts.dtype),
        in_specs=[IN_VMEM],
        out_specs=IN_VMEM,
        scratch_shapes=[pltpu.SemaphoreType.DMA((count - 1,))] * 2,
        compiler_params=pltpu.CompilerParams(collective_id=0, has_side_effects=True),
    )(facts)


def gather_kernel(count, picks, sides, *refs):
    num = len(picks)
    packs, vec_ref, text_ref = refs[:2], refs[2], refs[3]
    full, (vec_out, text_out), refs = refs[4 : 4 + num], refs[4 + num : 6 + num], refs[6 + num :]
    wide, shards = refs[:num], refs[num : 2 * num]
    ring_send, ring_recv, pair_send, pair_recv, cross_send, cross_recv = refs[2 * num : 2 * num + 6]
    load_sem, own_sem, part_send, part_recv, part_own = refs[2 * num + 6 :]
    shapes = [(packs[pack].shape[0], cols) for pack, _, cols in picks]
    loads = [
        pltpu.make_async_copy(
            packs[pack].at[:, pl.ds(start, cols)], wide[group], load_sem.at[group]
        )
        for group, (pack, start, cols) in enumerate(picks)
    ]
    for copy in loads:
        copy.start()
    me = lax.axis_index("clip")
    band = lax.axis_index("band")
    core = band % 2
    place = ring_place(me, count)
    onward = 1 - 2 * core
    following = (ring_clip((place + onward + count) % count, count), band)
    plane = band // 2
    partner = (me, band + 1 - 2 * core)
    mirror = (me, band + 2 - 4 * plane)
    peers = [((me + step) % count, band) for step in range(1, count)]
    greet(peers + [partner, mirror])

    def block(ref, group, owner):
        rows, cols = shapes[group]
        return ref.at[
            pl.ds(pl.multiple_of(owner * rows, rows), rows),
            pl.ds(pl.multiple_of(core * (cols // 2), 128), cols // 2),
        ]

    def ring_copy(group, step):
        owner = ring_clip((place - onward * step + 2 * count) % count, count)
        there = block(full[group], group, owner)
        return pltpu.make_async_remote_copy(
            there, there, ring_send.at[step, group], ring_recv.at[step, group], following, MESH
        )

    def handed(group, step, send, recv, peer):
        owner = ring_clip((place - onward * (step + 1) + 2 * count) % count, count)
        there = block(full[group], group, owner)
        return pltpu.make_async_remote_copy(
            there, there, send.at[step, group], recv.at[step, group], peer, MESH
        )

    def pair_copy(group, step):
        return handed(group, step, pair_send, pair_recv, partner)

    def cross_copy(group, step):
        return handed(group, step, cross_send, cross_recv, mirror)

    def in_ring(group):
        def decorate(body):
            if sides[group]:
                pl.when(plane == sides[group] - 1)(body)
            else:
                body()

        return decorate

    def off_ring(group, also=None):
        def decorate(body):
            if sides[group]:
                off = plane != sides[group] - 1
                pl.when(off if also is None else jnp.logical_and(off, also))(body)

        return decorate

    def ring_arrival(group, step, onto):
        ring_copy(group, step).wait_recv()
        if onto:
            ring_copy(group, step + 1).start()
        pair_copy(group, step).start()
        if sides[group]:
            cross_copy(group, step).start()

    def cross_arrival(group, step):
        cross_copy(group, step).wait_recv()
        pair_copy(group, step).start()

    def own_copy(group):
        rows, cols = shapes[group]
        return pltpu.make_async_copy(
            shards[group],
            full[group].at[pl.ds(pl.multiple_of(me * rows, rows), rows), :],
            own_sem.at[group],
        )

    parts = []
    for step, peer in enumerate(peers):
        for which, (src, dst) in enumerate(((vec_ref, vec_out), (text_ref, text_out))):
            parts.append(
                pltpu.make_async_remote_copy(
                    src.at[peer[0]],
                    dst.at[me],
                    part_send.at[which, step],
                    part_recv.at[which, step],
                    peer,
                    MESH,
                )
            )
    parts_own = [
        pltpu.make_async_copy(src.at[me], dst.at[me], part_own.at[which])
        for which, (src, dst) in enumerate(((vec_ref, vec_out), (text_ref, text_out)))
    ]
    for copy in parts_own + parts[::2]:
        copy.start()
    for group in range(num):
        rows, cols = shapes[group]
        loads[group].wait()
        shards[group][...] = wide[group][...].astype(jnp.bfloat16)
        own_copy(group).start()

        @in_ring(group)
        def _(group=group, rows=rows, cols=cols):
            pltpu.make_async_remote_copy(
                shards[group].at[:, pl.ds(pl.multiple_of(core * (cols // 2), 128), cols // 2)],
                block(full[group], group, me),
                ring_send.at[0, group],
                ring_recv.at[0, group],
                following,
                MESH,
            ).start()

    for copy in parts[1::2]:
        copy.start()

    @pl.loop(1, count - 1)
    def _(step):
        for group in range(num):

            @in_ring(group)
            def _(group=group):
                ring_arrival(group, step - 1, True)

        for group in range(num):

            @off_ring(group, step >= 2)
            def _(group=group):
                cross_arrival(group, step - 2)

    for group in range(num):

        @in_ring(group)
        def _(group=group):
            ring_arrival(group, count - 2, False)

    for late in (count - 3, count - 2):
        for group in range(num):

            @off_ring(group)
            def _(group=group, late=late):
                cross_arrival(group, late)

    for copy in parts_own + parts:
        copy.wait()
    for group in range(num):
        own_copy(group).wait()

    @pl.loop(0, count - 1)
    def _(step):
        for group in range(num):

            @in_ring(group)
            def _(group=group):
                ring_copy(group, step).wait_send()
                if sides[group]:
                    cross_copy(group, step).wait_send()

            pair_copy(group, step).wait()


def gather_quarters(shard):
    band_count = lax.axis_size("band")
    rows = shard.shape[0] // band_count
    own = lax.dynamic_slice_in_dim(shard, lax.axis_index("band") * rows, rows, 0)
    return lax.all_gather(own.astype(jnp.bfloat16), ("clip", "band"), axis=0, tiled=True)


def sum_rows(left, right):
    part = lax.psum_scatter(
        matmul_tn(left, right), ("clip", "band"), scatter_dimension=0, tiled=True
    )
    return lax.all_gather(part, "band", axis=0, tiled=True)


def gather_weights(packs, picks, sides, vectors, texts):
    count = lax.axis_size("clip")
    num = len(picks)
    steps = pltpu.SemaphoreType.DMA((count - 1, num))
    shapes = [(packs[pack].shape[0], cols) for pack, _, cols in picks]
    out = pl.pallas_call(
        partial(gather_kernel, count, picks, sides),
        out_shape=tuple(
            jax.ShapeDtypeStruct((count * rows, cols), jnp.bfloat16) for rows, cols in shapes
        )
        + tuple(jax.ShapeDtypeStruct(v.shape, v.dtype) for v in (vectors, texts)),
        in_specs=[ANY] * 4,
        out_specs=(ANY,) * (num + 2),
        scratch_shapes=[pltpu.VMEM(shape, jnp.float32) for shape in shapes]
        + [pltpu.VMEM(shape, jnp.bfloat16) for shape in shapes]
        + [steps] * 6
        + [
            pltpu.SemaphoreType.DMA((num,)),
            pltpu.SemaphoreType.DMA((num,)),
            pltpu.SemaphoreType.DMA((2, count - 1)),
            pltpu.SemaphoreType.DMA((2, count - 1)),
            pltpu.SemaphoreType.DMA((2,)),
        ],
        compiler_params=pltpu.CompilerParams(
            collective_id=1, has_side_effects=True, vmem_limit_bytes=32 << 20
        ),
        cost_estimate=pl.CostEstimate(flops=2 * 10**11, bytes_accessed=6 * 10**8, transcendentals=0),
    )(*packs, vectors, texts)
    return out[:num], out[num], out[num + 1]


WIRE_MAX = 32767.0
WIRE_LEAST = 1e-30
UNIT = (128, 512)


def unit_parts(kind, first):
    if kind == 0:
        return ((0, 4, lambda u: u, lambda u: 0), (4, 4, lambda u: 4, lambda u: u - 3))
    if first:
        return ((2, 2, lambda u: u, lambda u: u), (4, 2, lambda u: 3, lambda u: u))
    return ((0, 3, lambda u: u, lambda u: u), (3, 3, lambda u: 3, lambda u: u))


def reduce_kernel(count, tokens, phases, *refs):
    num = sum(len(phase["lefts"]) for phase in phases)
    lefts, rights = refs[:num], refs[num : 2 * num]
    vec_ref, kv_ref, text_ref = refs[2 * num : 2 * num + 3]
    refs = refs[2 * num + 3 :]
    wide_out, deep_out, square_out, all_vec, kv_out, kv_square = refs[:6]
    left_far, right_far = refs[6 : 6 + num], refs[6 + num : 6 + 2 * num]
    scratch = refs[6 + 2 * num :]
    left_buf, right_buf, got_low, got_scale, put_low, put_scale, plane_put = (
        scratch[2 * i : 2 * i + 2] for i in range(7)
    )
    plane_got = scratch[14 : 14 + len(phases)]
    (
        square_buf,
        left_sem,
        right_sem,
        pair_send,
        pair_recv,
        half_send,
        half_recv,
        ring_send,
        ring_recv,
        credit,
        plane_send,
        plane_recv,
        out_sem,
        out_send,
        out_recv,
        last_put,
        last_put_scale,
        last_got,
        last_got_scale,
        push_send,
        push_recv,
        vec_got,
        kv_got,
        vec_sum,
        all_kv,
        text_buf,
        kv_grad,
        side_own,
        side_send,
        side_recv,
        vec_send,
        vec_recv,
        vec_pair_send,
        vec_pair_recv,
        kv_own,
        kv_send,
        kv_recv,
    ) = scratch[14 + len(phases) :]
    me = lax.axis_index("clip")
    band = lax.axis_index("band")
    core = band % 2
    plane = band // 2
    place = ring_place(me, count)
    onward = 1 - 2 * core
    following = (ring_clip((place + onward + count) % count, count), band)
    preceding = (ring_clip((place - onward + count) % count, count), band)
    partner = (me, band + 1 - 2 * core)
    mirror = (me, band + 2 - 4 * plane)
    band_count = vec_got.shape[0]
    band_peers = [(me, (band + step) % band_count) for step in range(1, band_count)]
    greet([following, preceding] + band_peers)

    def owner_at(step, way):
        return ring_clip((place - way * (step + 1) + 2 * count) % count, count)

    def left_blocks(at):
        phase = phases[at]
        if phase["kind"] == 0:
            return [(b, phase["lefts"][0], b, 4) for b in range(4)] + [(4, phase["lefts"][1], 0, 1)]
        first = phase["first"]
        return [(first + i, left, 0, 1) for i, left in enumerate(phase["lefts"])]

    def right_blocks(at):
        phase = phases[at]
        if phase["kind"] == 0:
            return [(0, phase["lefts"][0], 0)] + [(1 + i, phase["lefts"][1], i) for i in range(4)]
        first = phase["first"]
        return [(first + i, phase["lefts"][i], 0) for i in range(3 - first)] + [
            (3 + i, phase["lefts"][-1], i) for i in range(3)
        ]

    def left_cols(step, way, which, many):
        width = lefts_width // count if many == 1 else deep_width // count
        start = owner_at(step, way) * width + which * 128
        return pl.ds(pl.multiple_of(start, 128), 128)

    lefts_width = lefts[phases[1]["lefts"][0]].shape[1]
    deep_width = lefts[phases[0]["lefts"][0]].shape[1]

    def pair_left(at, step):
        out = []
        for block, operand, which, many in left_blocks(at):
            cols = left_cols(step, -onward, which, many)
            out.append(
                pltpu.make_async_remote_copy(
                    lefts[operand].at[:, cols],
                    left_far[operand].at[:, cols],
                    pair_send.at[at, block, step],
                    pair_recv.at[at, block, step],
                    partner,
                    MESH,
                )
            )
        return out

    def pair_right(at):
        out = []
        for i, operand in enumerate(phases[at]["lefts"]):
            half = rights[operand].shape[1] // 2
            out.append(
                pltpu.make_async_remote_copy(
                    rights[operand].at[:, pl.ds(pl.multiple_of((1 - core) * half, 128), half)],
                    right_far[operand],
                    half_send.at[operand],
                    half_recv.at[operand],
                    partner,
                    MESH,
                )
            )
        return out

    def load_left(at, step, slot, far):
        kind = phases[at]["kind"]
        out = []
        for block, operand, which, many in left_blocks(at):
            cols = left_cols(step, onward, which, many)
            source = left_far if far else lefts
            out.append(
                pltpu.make_async_copy(
                    source[operand].at[:, cols],
                    left_buf[kind].at[slot, block, pl.ds(far * tokens, tokens), :],
                    left_sem.at[kind, slot, block, far],
                )
            )
        return out

    def load_right(at, far):
        kind = phases[at]["kind"]
        out = []
        for block, operand, which in right_blocks(at):
            if far:
                source = right_far[operand].at[:, pl.ds(which * UNIT[1], UNIT[1])]
            else:
                half = rights[operand].shape[1] // 2
                start = pl.multiple_of(core * half + which * UNIT[1], 128)
                source = rights[operand].at[:, pl.ds(start, UNIT[1])]
            out.append(
                pltpu.make_async_copy(
                    source,
                    right_buf[kind].at[block, pl.ds(far * tokens, tokens), :],
                    right_sem.at[kind, block, far],
                )
            )
        return out

    def ring_copies(at, part, slot):
        kind = phases[at]["kind"]
        units = pl.ds(*unit_parts(kind, phases[at]["first"])[part][:2])
        return [
            pltpu.make_async_remote_copy(
                put.at[slot, units],
                got.at[slot, units],
                ring_send.at[kind, slot, part, i],
                ring_recv.at[kind, slot, part, i],
                following,
                MESH,
            )
            for i, (put, got) in enumerate(
                ((put_low[kind], got_low[kind]), (put_scale[kind], got_scale[kind]))
            )
        ]

    def plane_copies(at, part):
        kind = phases[at]["kind"]
        units = pl.ds(*unit_parts(kind, phases[at]["first"])[part][:2])
        pairs = ((plane_put[kind], plane_got[at]),)
        if at + 1 == len(phases):
            pairs = ((last_put, last_got), (last_put_scale, last_got_scale))
        return [
            pltpu.make_async_remote_copy(
                here.at[units],
                there.at[units],
                plane_send.at[at, part, i],
                plane_recv.at[at, part, i],
                mirror,
                MESH,
            )
            for i, (here, there) in enumerate(pairs)
        ]

    def push_right(block):
        operand, which = [entry[1:] for entry in right_blocks(0) if entry[0] == block][0]
        half = rights[operand].shape[1] // 2
        begin = pl.multiple_of((1 - core) * half + which * UNIT[1], 128)
        return pltpu.make_async_remote_copy(
            rights[operand].at[:, pl.ds(begin, UNIT[1])],
            right_buf[phases[0]["kind"]].at[block, pl.ds(tokens, tokens), :],
            push_send.at[block],
            push_recv.at[block],
            partner,
            MESH,
        )

    def out_copies(at, unit):
        phase = phases[at]
        if phase["kind"] == 0 and unit < 4:
            half = UNIT[1]
            rows = deep_out.shape[0] // 4
            there = deep_out.at[
                pl.ds(unit * rows, rows),
                pl.ds(pl.multiple_of(phase["cols"][0] + core * half, 128), half),
            ]
        else:
            which, col = (1, unit - 4) if phase["kind"] == 0 else (unit - phase["first"], 0)
            if phase["kind"] and unit >= 3:
                which, col = len(phase["lefts"]) - 1, unit - 3
            half = rights[phase["lefts"][which]].shape[1] // 2
            start = phase["cols"][which] + core * half + col * UNIT[1]
            there = wide_out.at[:, pl.ds(pl.multiple_of(start, 128), UNIT[1])]
        here = plane_got[at].at[unit]
        return (
            pltpu.make_async_copy(here, there, out_sem.at[at, unit]),
            pltpu.make_async_remote_copy(
                here, there, out_send.at[at, unit], out_recv.at[at, unit], partner, MESH
            ),
        )

    def product(kind, slot, left, right):
        return lax.dot_general(
            left_buf[kind][slot, left],
            right_buf[kind][right],
            (((0,), (0,)), ((), ())),
            preferred_element_type=jnp.float32,
        )

    def start(copies):
        for copy in copies:
            copy.start()

    def finish(copies):
        for copy in copies:
            copy.wait()

    def take_step(at, step, first, last):
        phase = phases[at]
        kind = phase["kind"]
        slot = step % 2
        before = (step + 1) % 2
        for far in range(2):
            finish(load_left(at, step, slot, far))

        def load_next():
            for copy in pair_left(at, step + 1):
                copy.wait_recv()
            for far in range(2):
                start(load_left(at, step + 1, before, far))

        opening = first and at == 0
        if not (last or opening):
            load_next()
        parts = unit_parts(kind, phase["first"])

        def encode(term):
            largest = jnp.maximum(jnp.max(jnp.abs(term), axis=0, keepdims=True), WIRE_LEAST)
            low = jnp.round(term * (WIRE_MAX / largest)).astype(jnp.int16)
            return low, largest * (1.0 / WIRE_MAX)

        for part, (low, many, left_of, right_of) in enumerate(parts):
            if opening:
                blocks = range(1) if part == 0 else range(1, 5)
                finish(load_right(0, 0)[blocks.start : blocks.stop])
                for block in blocks:
                    push_right(block).wait_recv()
            if not first:
                for copy in ring_copies(at, part, before):
                    copy.wait_recv()
            if not (first or last):

                @pl.when(step >= 2)
                def _(part=part):
                    for copy in ring_copies(at, part, slot):
                        copy.wait_send()
                    pl.semaphore_wait(credit.at[kind, part], 1)

            def settle(position, unit, term):
                if not first:
                    came = got_low[kind][before, position].astype(jnp.float32)
                    term = term + came * got_scale[kind][before, position]
                if last and at + 1 == len(phases):
                    last_put[unit], last_put_scale[unit] = encode(term)
                elif last:
                    plane_put[kind][unit] = term
                else:
                    low_part, scale_part = encode(term)
                    put_low[kind][slot, position] = low_part
                    put_scale[kind][slot, position] = scale_part

            @pl.loop(low, low + many)
            def _(unit, left_of=left_of, right_of=right_of):
                settle(unit, unit, product(kind, slot, left_of(unit), right_of(unit)))

            if last:
                start(plane_copies(at, part))
            else:
                start(ring_copies(at, part, slot))
            if not (first or last):

                @pl.when(step < count - 2)
                def _(part=part):
                    pl.semaphore_signal(
                        credit.at[kind, part], inc=1, device_id=preceding, device_id_type=MESH
                    )

        if opening:
            load_next()

    def close(at):
        kind = phases[at]["kind"]

        def add_square(total):
            square_buf[...] += jnp.sum((total * total).reshape(UNIT[0] // 8, 8, UNIT[1]), axis=0)

        for part, (low, many, _, _) in enumerate(unit_parts(kind, phases[at]["first"])):
            finish(plane_copies(at, part))

            @pl.loop(low, low + many)
            def _(unit):
                if at + 1 == len(phases):
                    total = last_put[unit].astype(jnp.float32) * last_put_scale[unit]
                    total += last_got[unit].astype(jnp.float32) * last_got_scale[unit]
                else:
                    total = plane_put[kind][unit] + plane_got[at][unit]
                plane_got[at][unit] = total
                add_square(total)

            for unit in range(low, low + many):
                start(out_copies(at, unit))

    half_rows = pl.ds(pl.multiple_of(core * (vec_sum.shape[0] // 2), 8), vec_sum.shape[0] // 2)
    side_local = [
        pltpu.make_async_copy(vec_ref, vec_got.at[band], side_own.at[0]),
        pltpu.make_async_copy(kv_ref.at[band], kv_got.at[band], side_own.at[1]),
        pltpu.make_async_copy(text_ref, text_buf, side_own.at[2]),
    ]
    side_remote = []
    for step, peer in enumerate(band_peers):
        side_remote += [
            pltpu.make_async_remote_copy(
                vec_ref, vec_got.at[band], side_send.at[0, step], side_recv.at[0, step], peer, MESH
            ),
            pltpu.make_async_remote_copy(
                kv_ref.at[peer[1]],
                kv_got.at[band],
                side_send.at[1, step],
                side_recv.at[1, step],
                peer,
                MESH,
            ),
        ]
    vec_own = pltpu.make_async_copy(vec_sum, all_vec.at[me], side_own.at[3])

    def vec_copies(step):
        owner = ring_clip((place - onward * step + 2 * count) % count, count)
        vec = all_vec.at[owner, half_rows]
        return [
            pltpu.make_async_remote_copy(
                here, there, vec_send.at[step, i], vec_recv.at[step, i], following, MESH
            )
            for i, (here, there) in enumerate(((vec, vec), (all_kv.at[owner], all_kv.at[owner])))
        ]

    def vec_first():
        vec = all_vec.at[me, half_rows]
        return [
            pltpu.make_async_remote_copy(
                here, there, vec_send.at[0, i], vec_recv.at[0, i], following, MESH
            )
            for i, (here, there) in enumerate(
                ((vec_sum.at[half_rows], vec), (all_kv.at[me], all_kv.at[me]))
            )
        ]

    def vec_pair(step):
        owner = ring_clip((place - onward * (step + 1) + 2 * count) % count, count)
        vec = all_vec.at[owner, half_rows]
        return pltpu.make_async_remote_copy(
            vec, vec, vec_pair_send.at[step], vec_pair_recv.at[step], partner, MESH
        )

    kv_width = kv_grad.shape[1]

    def kv_place(owner):
        return kv_out.at[:, pl.ds(pl.multiple_of(owner * kv_width, 128), kv_width)]

    def kv_copy(i):
        if i == 2:
            return pltpu.make_async_copy(kv_grad, kv_place(band), kv_own)
        peer = (partner, mirror)[i]
        return pltpu.make_async_remote_copy(
            kv_grad, kv_place(band), kv_send.at[i], kv_recv.at[i], peer, MESH
        )

    def kv_passed():
        there = kv_place(mirror[1])
        return pltpu.make_async_remote_copy(
            there, there, kv_send.at[2], kv_recv.at[2], partner, MESH
        )

    def sum_bands():
        finish(side_local + side_remote)
        vec_sum[...] = jnp.sum(vec_got[...], 0)
        all_kv[me] = jnp.sum(kv_got[...], 0)
        vec_own.start()
        start(vec_first())

    def pass_sums(step):
        for copy in vec_copies(step - 1):
            copy.wait_recv()
        start(vec_copies(step))
        vec_pair(step - 1).start()

    def multiply_text():
        for copy in vec_copies(count - 2):
            copy.wait_recv()
        vec_pair(count - 2).start()
        grads = all_kv[...].reshape(text_buf.shape[0], -1)
        total = jnp.zeros_like(kv_grad)
        for _ in range(3):
            part = grads.astype(jnp.bfloat16)
            grads = grads - part.astype(jnp.float32)
            total = total + matmul_tn(text_buf[...], part)
        kv_grad[...] = total
        kv_square[...] = jnp.sum((total * total).reshape(-1, 8, total.shape[1]), axis=0)
        start([kv_copy(i) for i in range(3)])

    square_buf[...] = jnp.zeros_like(square_buf)
    start(side_local + side_remote)
    start(load_right(0, 0))
    start(load_left(0, 0, 0, 0))
    push_right(0).start()
    start(pair_left(0, 0))
    for block in range(1, 5):
        push_right(block).start()

    @pl.loop(1, count)
    def _(step):
        start(pair_left(0, step))

    for copy in pair_left(0, 0):
        copy.wait_recv()
    start(load_left(0, 0, 0, 1))
    take_step(0, 0, True, False)
    for at in range(len(phases)):
        more = at + 1 < len(phases)
        if more:
            start(pair_right(at + 1))
            start(load_right(at + 1, 0))
            start(pair_left(at + 1, 0))
        if at == 1:
            sum_bands()

        @pl.loop(1, count - 1)
        def _(step, at=at, more=more):
            take_step(at, step, False, False)
            if at == 1:
                pass_sums(step)
            if more:
                start(pair_left(at + 1, step))

                @pl.when(step == count // 2)
                def _():
                    for copy in pair_right(at + 1):
                        copy.wait_recv()
                    start(load_right(at + 1, 1))
                    for copy in pair_left(at + 1, 0):
                        copy.wait_recv()
                    for far in range(2):
                        start(load_left(at + 1, 0, 0, far))

        if more:
            start(pair_left(at + 1, count - 1))
            for far in range(2):
                finish(load_right(at + 1, far))
            take_step(at + 1, 0, True, False)
        take_step(at, count - 1, False, True)
        if at == 1:
            multiply_text()
        for part in range(2):
            for slot in range(2):
                for copy in ring_copies(at, part, slot):
                    copy.wait_send()
        if at == 2:
            kv_copy(1).wait_recv()
            kv_passed().start()
        if at:
            close(at - 1)
    close(len(phases) - 1)
    vec_own.wait()
    kv_passed().wait()
    kv_copy(0).wait()
    kv_copy(1).wait_send()
    kv_copy(2).wait()

    @pl.loop(0, count - 1)
    def _(step):
        for copy in vec_copies(step):
            copy.wait_send()
        vec_pair(step).wait()

    square_out[...] = square_buf[...]
    for at, phase in enumerate(phases):
        for copy in pair_right(at) if at else [push_right(block) for block in range(5)]:
            copy.wait_send()

        @pl.loop(0, count)
        def _(step, at=at):
            for copy in pair_left(at, step):
                copy.wait_send()

        for unit in range(phase["first"], 8 if phase["kind"] == 0 else 6):
            finish(out_copies(at, unit))


def reduce_gradients(phases, lefts, rights, vectors, keyvals, text, wide_cols, deep_cols):
    count = lax.axis_size("clip")
    tokens = lefts[0].shape[0]
    wide_rows = lefts[1].shape[1] // count
    deep_rows = lefts[0].shape[1] // count
    band_count, _, kv_cols = keyvals.shape
    num = len(lefts)
    dma = pltpu.SemaphoreType.DMA
    units, lefts_of, rights_of = (8, 6), (5, 4), (5, 6)
    scratch = [pltpu.VMEM((2, lefts_of[k], 2 * tokens, 128), jnp.bfloat16) for k in range(2)]
    scratch += [pltpu.VMEM((rights_of[k], 2 * tokens, UNIT[1]), jnp.bfloat16) for k in range(2)]
    for _ in range(2):
        scratch += [pltpu.VMEM((2, units[k]) + UNIT, jnp.int16) for k in range(2)]
        scratch += [pltpu.VMEM((2, units[k], 1, UNIT[1]), jnp.float32) for k in range(2)]
    scratch += [pltpu.VMEM((units[k],) + UNIT, jnp.float32) for k in range(2)]
    scratch += [pltpu.VMEM((units[p["kind"]],) + UNIT, jnp.float32) for p in phases]
    scratch += [
        pltpu.VMEM((8, UNIT[1]), jnp.float32),
        dma((2, 2, 5, 2)),
        dma((2, 6, 2)),
        dma((len(phases), 5, count)),
        dma((len(phases), 5, count)),
        dma((num,)),
        dma((num,)),
        dma((2, 2, 2, 2)),
        dma((2, 2, 2, 2)),
        pltpu.SemaphoreType.REGULAR((2, 2)),
        dma((len(phases), 2, 2)),
        dma((len(phases), 2, 2)),
        dma((len(phases), 8)),
        dma((len(phases), 8)),
        dma((len(phases), 8)),
    ]
    for _ in range(2):
        scratch += [pltpu.VMEM((6,) + UNIT, jnp.int16), pltpu.VMEM((6, 1, UNIT[1]), jnp.float32)]
    scratch += [
        dma((5,)),
        dma((5,)),
        pltpu.VMEM((band_count,) + vectors.shape, jnp.float32),
        pltpu.VMEM(keyvals.shape, jnp.float32),
        pltpu.VMEM(vectors.shape, jnp.float32),
        pltpu.VMEM((count,) + keyvals.shape[1:], jnp.float32),
        pltpu.VMEM(text.shape, jnp.bfloat16),
        pltpu.VMEM((text.shape[1], kv_cols), jnp.float32),
        dma((4,)),
        dma((2, band_count - 1)),
        dma((2, band_count - 1)),
        dma((count - 1, 2)),
        dma((count - 1, 2)),
        dma((count - 1,)),
        dma((count - 1,)),
        dma,
        dma((3,)),
        dma((3,)),
    ]
    out = pl.pallas_call(
        partial(reduce_kernel, count, tokens, phases),
        out_shape=(
            jax.ShapeDtypeStruct((wide_rows, wide_cols), jnp.float32),
            jax.ShapeDtypeStruct((deep_rows, deep_cols), jnp.float32),
            jax.ShapeDtypeStruct((8, UNIT[1]), jnp.float32),
            jax.ShapeDtypeStruct((count,) + vectors.shape, jnp.float32),
            jax.ShapeDtypeStruct((deep_rows, band_count * kv_cols), jnp.float32),
            jax.ShapeDtypeStruct((8, kv_cols), jnp.float32),
        )
        + tuple(jax.ShapeDtypeStruct(x.shape, x.dtype) for x in lefts)
        + tuple(jax.ShapeDtypeStruct((tokens, x.shape[1] // 2), x.dtype) for x in rights),
        in_specs=[ANY] * (2 * num + 3),
        out_specs=(ANY, ANY, IN_VMEM, ANY, ANY, IN_VMEM) + (ANY,) * (2 * num),
        scratch_shapes=scratch,
        compiler_params=pltpu.CompilerParams(
            collective_id=2, has_side_effects=True, vmem_limit_bytes=58 << 20
        ),
        cost_estimate=pl.CostEstimate(flops=3 * 10**11, bytes_accessed=8 * 10**8, transcendentals=0),
    )(*lefts, *rights, vectors, keyvals, text)
    return out[:6]


def total_kernel(count, part_ref, out_ref, mid, band_got, clip_got, *sems):
    me = lax.axis_index("clip")
    band = lax.axis_index("band")
    band_count = band_got.shape[0]
    band_peers = [(me, (band + step) % band_count) for step in range(1, band_count)]
    clip_peers = [((me + step) % count, band) for step in range(1, count)]
    greet(band_peers + clip_peers)
    stages = (
        (part_ref, band_got, band, band_peers, mid, sems[:2]),
        (mid, clip_got, me, clip_peers, out_ref, sems[2:]),
    )
    for value, got, index, peers, result, (send, recv) in stages:
        copies = [
            pltpu.make_async_remote_copy(
                value, got.at[index], send.at[step], recv.at[step], peer, MESH
            )
            for step, peer in enumerate(peers)
        ]
        for copy in copies:
            copy.start()
        got[index] = value[...]
        for copy in copies:
            copy.wait()
        result[...] = jnp.sum(got[...], 0)


def total_over_devices(value):
    count, band_count = lax.axis_size("clip"), lax.axis_size("band")
    dma = pltpu.SemaphoreType.DMA
    tile = (8, 128)
    return pl.pallas_call(
        partial(total_kernel, count),
        out_shape=jax.ShapeDtypeStruct(tile, jnp.float32),
        in_specs=[IN_VMEM],
        out_specs=IN_VMEM,
        scratch_shapes=[
            pltpu.VMEM(tile, jnp.float32),
            pltpu.VMEM((band_count,) + tile, jnp.float32),
            pltpu.VMEM((count,) + tile, jnp.float32),
            dma((band_count - 1,)),
            dma((band_count - 1,)),
            dma((count - 1,)),
            dma((count - 1,)),
        ],
        compiler_params=pltpu.CompilerParams(collective_id=3, has_side_effects=True),
    )(jnp.broadcast_to(value, tile))[0, 0]


def per_device(
    latents,
    noise_field,
    timesteps,
    null_flags,
    frame_mask,
    context,
    w_wide,
    m_wide,
    v_wide,
    w_deep,
    m_deep,
    v_deep,
    w_small,
    m_small,
    v_small,
):
    clip_count = lax.axis_size("clip")
    band_count = lax.axis_size("band")
    clip_at = lax.axis_index("clip")
    band_at = lax.axis_index("band")
    wide_rows = w_wide.shape[0]
    deep_rows = w_deep.shape[0]
    text_len, text_dim = context.shape[1:]
    facts = jnp.pad(
        jnp.concatenate([timesteps, frame_mask[0]])[None],
        ((0, 7), (0, 127 - frame_mask.shape[1])),
    )
    kept_text = context[0] * (1 - null_flags[0]).astype(jnp.bfloat16)
    text_cols = jnp.pad(
        kept_text.reshape(text_len, clip_count, deep_rows).transpose(1, 0, 2),
        ((0, 0), (0, TEXT_PAD - text_len), (0, 0)),
    )
    all_facts = exchange_facts(facts)
    all_times = all_facts[:, 0, 0].astype(jnp.float32)
    all_time_low = jax.nn.silu(time_features(all_times)).astype(jnp.bfloat16)
    time_rows = lax.dynamic_slice(
        all_time_low, (0, clip_at * wide_rows), (clip_count, wide_rows)
    )
    part_modul = matmul(time_rows, w_wide[:, : 12 * D].astype(jnp.bfloat16))
    kv_cols = 2 * D // band_count
    kv_weight = lax.dynamic_slice(
        w_deep, (0, D + band_at * kv_cols), (deep_rows, kv_cols)
    ).astype(jnp.bfloat16)
    up_b_w = gather_quarters(w_wide[:, 22 * D + FF :])
    gathered, all_modul, all_text = gather_weights(
        (w_wide, w_deep),
        (
            (0, 22 * D, FF),
            (1, 0, D),
            (0, 18 * D, D),
            (0, 19 * D, D),
            (0, 20 * D, D),
            (0, 21 * D, D),
            (0, 12 * D, 3 * D),
            (0, 15 * D, 3 * D),
        ),
        (1, 2, 1, 2, 1, 2, 0, 0),
        part_modul.reshape(clip_count, 12 * D // 128, 128),
        text_cols,
    )
    up_a_w, down_a_w, out_a_w, out_b_w, query_w, cross_out_w, qkv_a_w, qkv_b_w = gathered
    part_kv = matmul(all_text.reshape(clip_count * TEXT_PAD, deep_rows), kv_weight)
    keyval = lax.psum_scatter(part_kv, "clip", scatter_dimension=0, tiled=True)
    late_down_b, all_modul = lax.optimization_barrier((w_deep[:, 3 * D :], all_modul))
    down_b_w = gather_quarters(late_down_b)
    keyval = lax.all_gather(keyval.astype(jnp.bfloat16), "band", axis=1, tiled=True)
    small_low = w_small.astype(jnp.bfloat16)
    small_val = small_low.astype(jnp.float32)
    num_frames, num_rows, num_cols = (latents.shape[1], latents.shape[2], latents.shape[3])
    tok_count = num_frames * num_rows * num_cols
    all_mask = all_facts[:, 0, 1 : 1 + num_frames]
    global_count = jnp.sum(all_mask).astype(jnp.float32) * (num_rows * num_cols * CH * band_count)
    time_value = timesteps[0].astype(jnp.float32)
    noise_angle = 0.5 * math.pi * time_value / TMAX
    signal, spread = (jnp.cos(noise_angle), jnp.sin(noise_angle))
    clean_tok = token_order(latents[0])
    noise_tok = token_order(noise_field[0])
    run = num_rows * WIN
    part = SHIFT * WIN
    frame_windows = attend_pieces(tok_count, num_frames, "frame")
    half_windows = attend_pieces(tok_count, num_frames, "half")
    text_windows = attend_pieces(tok_count, num_frames, "text")
    noisy_low = (signal * clean_tok + spread * noise_tok).astype(jnp.bfloat16)
    target = signal * noise_tok - spread * clean_tok
    modulation = jnp.sum(all_modul, 0).reshape(12, D)
    mod_a, mod_b = (modulation[:6], modulation[6:])
    stream_zero = matmul(noisy_low, small_low[:CH]) + small_val[2 * CH]
    normed_a, back_a = jax.vjp(norm_modulated, stream_zero, mod_a[0], mod_a[1])
    in_a = normed_a.astype(jnp.bfloat16)
    qkv_a = matmul(in_a, qkv_a_w).astype(jnp.bfloat16)
    far_kv = from_partner(qkv_a[:, D:], "band", 0)
    space_kv = [(qkv_a, HEADS // 2, HEADS), (far_kv, 0, HEADS // 2)]
    att_a = attend(qkv_a, space_kv, frame_windows)
    proj_a = matmul(att_a, out_a_w)
    stream_one = stream_zero + mod_a[2] * proj_a
    stream_two, saved_a = mlp_forward(stream_one, mod_a, up_a_w, down_a_w)
    normed_b, back_b = jax.vjp(norm_modulated, stream_two, mod_b[0], mod_b[1])
    low_b = normed_b.astype(jnp.bfloat16)
    rolled = with_rows(low_b, shifted(first_rows(low_b, run, part), "band", -1), run)
    qkv_b = matmul(rolled, qkv_b_w).astype(jnp.bfloat16)
    win_kv = [(qkv_b, HEADS // 2, HEADS)]
    win_out = attend(qkv_b, win_kv, half_windows)
    att_b = with_rows(win_out, shifted(first_rows(win_out, run, part), "band", 1), run)
    proj_b = matmul(att_b, out_b_w)
    stream_three = stream_two + mod_b[2] * proj_b
    cross_val, cross_back = jax.vjp(norm_gained, stream_three, small_val[2 * CH + 1])
    cross_in = cross_val.astype(jnp.bfloat16)
    query_proj = matmul(cross_in, query_w).astype(jnp.bfloat16)
    text_kv = [(keyval, 0, HEADS // 2)]
    crossed = attend(query_proj, text_kv, text_windows, text_len)
    stream_four = stream_three + matmul(crossed, cross_out_w)
    stream_five, saved_b = mlp_forward(stream_four, mod_b, up_b_w, down_b_w)
    final_val, final_back = jax.vjp(norm_gained, stream_five, small_val[2 * CH + 2])
    final_low = final_val.astype(jnp.bfloat16)
    head_low = small_low[CH : 2 * CH]
    predicted = matmul_nt(final_low, head_low)
    weight_row = jnp.repeat(frame_mask[0].astype(jnp.float32), run)
    weight_row = jnp.tile(weight_row, num_cols // WIN)[:, None]
    pred_error = predicted - target
    loss_part = jnp.sum(weight_row * pred_error * pred_error)
    grad_pred = (weight_row * pred_error * (2.0 / global_count)).astype(jnp.bfloat16)
    grad_head = matmul_tn(grad_pred, final_low)
    grad_stream, grad_gain_f = final_back(matmul(grad_pred, head_low))
    grad_stream, mlp_factors_b, extra_b = mlp_backward(
        grad_stream, mod_b, up_b_w, down_b_w, saved_b
    )
    grad_cross = grad_stream.astype(jnp.bfloat16)
    grad_crossed = matmul_nt(grad_cross, cross_out_w).astype(jnp.bfloat16)
    grad_query, grad_keyval = attend_back(
        query_proj, text_kv, grad_crossed, text_windows, text_len
    )
    grad_part, grad_gain_c = cross_back(matmul_nt(grad_query, query_w))
    grad_stream = grad_stream + grad_part
    grad_proj = (mod_b[2] * grad_stream).astype(jnp.bfloat16)
    grad_gate_b = jnp.sum(grad_stream * proj_b, 0)
    factors_ob = (att_b, grad_proj)
    grad_att = matmul_nt(grad_proj, out_b_w).astype(jnp.bfloat16)
    grad_win = with_rows(grad_att, shifted(first_rows(grad_att, run, part), "band", -1), run)
    grad_qkv = attend_back(qkv_b, win_kv, grad_win, half_windows)[0]
    factors_qkvb = (rolled, grad_qkv)
    grad_in_roll = matmul_nt(grad_qkv, qkv_b_w)
    sent_back = shifted(first_rows(grad_in_roll, run, part), "band", 1)
    grad_normed = with_rows(grad_in_roll, sent_back, run)
    grad_part, grad_shift_b, grad_scale_b = back_b(grad_normed)
    grad_stream = grad_stream + grad_part
    grad_stream, mlp_factors_a, extra_a = mlp_backward(
        grad_stream, mod_a, up_a_w, down_a_w, saved_a
    )
    grad_proj = (mod_a[2] * grad_stream).astype(jnp.bfloat16)
    grad_gate_a = jnp.sum(grad_stream * proj_a, 0)
    factors_oa = (att_a, grad_proj)
    grad_att = matmul_nt(grad_proj, out_a_w).astype(jnp.bfloat16)
    grad_q, grad_own, grad_far = attend_back(qkv_a, space_kv, grad_att, frame_windows)
    grad_kv = grad_own + from_partner(grad_far, "band", 0)
    grad_qkv = jnp.concatenate([grad_q, grad_kv.astype(jnp.bfloat16)], 1)
    factors_qkva = (in_a, grad_qkv)
    grad_part, grad_shift_a, grad_scale_a = back_a(matmul_nt(grad_qkv, qkv_a_w))
    grad_stream = grad_stream + grad_part
    grad_patch = matmul_tn(noisy_low.astype(jnp.float32), grad_stream, lax.Precision.HIGHEST)
    grad_bias = jnp.sum(grad_stream, 0)
    grad_modul = jnp.stack(
        [
            grad_shift_a,
            grad_scale_a,
            grad_gate_a,
            extra_a[0],
            extra_a[1],
            extra_a[2],
            grad_shift_b,
            grad_scale_b,
            grad_gate_b,
            extra_b[0],
            extra_b[1],
            extra_b[2],
        ]
    ).reshape(1, 12 * D)
    grad_small = jnp.concatenate(
        [grad_patch, grad_head, grad_bias[None], grad_gain_c[None], grad_gain_f[None]], 0
    )
    factors = mlp_factors_b + (
        (crossed, grad_cross),
        (cross_in, grad_query),
        factors_ob,
        factors_qkvb,
    )
    factors += mlp_factors_a + (factors_oa, factors_qkva)
    if wide_rows == 128 and deep_rows == 512:
        phases = (
            {"kind": 0, "first": 0, "lefts": (0, 1), "cols": (D, 10 * D + FF)},
            {"kind": 1, "first": 0, "lefts": (2, 3, 4, 5), "cols": (9 * D, 8 * D, 7 * D, 3 * D)},
            {"kind": 0, "first": 0, "lefts": (6, 7), "cols": (0, 10 * D)},
            {"kind": 1, "first": 2, "lefts": (8, 9), "cols": (6 * D, 0)},
        )
        used = 12 * D + grad_small.size
        vectors = jnp.concatenate(
            [grad_modul.reshape(-1), grad_small.reshape(-1), loss_part[None]]
        )
        vectors = jnp.pad(vectors, (0, 256 * 128 - vectors.shape[0])).reshape(256, 128)
        keyvals = grad_keyval.reshape(TEXT_PAD, band_count, kv_cols).transpose(1, 0, 2)
        wide_rest, deep_rest, squares, all_vectors, grad_w_ckv, kv_squares = reduce_gradients(
            phases,
            [f[0] for f in factors],
            [f[1] for f in factors],
            vectors,
            keyvals,
            all_text.reshape(clip_count * TEXT_PAD, deep_rows),
            10 * D + 2 * FF,
            2 * D,
        )
        all_vectors = all_vectors.reshape(clip_count, -1)
        all_grad_modul = all_vectors[:, : 12 * D]
        small_sum = jnp.sum(all_vectors[:, 12 * D : used], 0).reshape(grad_small.shape)
        loss_sum = jnp.sum(all_vectors[:, used])
        square_part = jnp.sum(squares) / (band_count // 2) + jnp.sum(kv_squares)
    else:
        summed = [sum_rows(*pair) for pair in factors]
        wide_rest = jnp.concatenate([summed[i] for i in (9, 5, 8, 4, 3, 2, 7, 1)], 1)
        deep_rest = jnp.concatenate([summed[6], summed[0]], 1)
        grad_keyval = lax.psum_scatter(grad_keyval, "band", scatter_dimension=1, tiled=True)
        grad_keyval = lax.all_gather(grad_keyval, "clip", axis=0, tiled=True)
        grad_w_ckv = matmul_tn(
            all_text.reshape(clip_count * TEXT_PAD, deep_rows).astype(jnp.float32),
            grad_keyval,
            lax.Precision.HIGHEST,
        )
        grad_w_ckv = lax.all_gather(grad_w_ckv, "band", axis=1, tiled=True)
        all_grad_modul = lax.all_gather(lax.psum(grad_modul, "band"), "clip", axis=0, tiled=True)
        loss_sum, small_sum = lax.psum((loss_part, grad_small), ("clip", "band"))
        square_part = sum(jnp.sum(x * x) for x in (wide_rest, deep_rest, grad_w_ckv)) / band_count
    grad_w_ada = matmul_tn(time_rows.astype(jnp.float32), all_grad_modul, lax.Precision.HIGHEST)
    wide_sum = jnp.concatenate([grad_w_ada, wide_rest], 1)
    deep_sum = jnp.concatenate([deep_rest[:, :D], grad_w_ckv, deep_rest[:, D:]], 1)
    square_part += jnp.sum(grad_w_ada * grad_w_ada) / band_count
    square_sum = total_over_devices(square_part)
    grad_norm = jnp.sqrt(square_sum + jnp.sum(small_sum * small_sum))
    factor = CLIP_MAX / jnp.maximum(grad_norm, CLIP_MAX)
    new_wide = adam_update(w_wide, m_wide, v_wide, wide_sum * factor, 0.15)
    new_deep = adam_update(w_deep, m_deep, v_deep, deep_sum * factor, 0.05)
    new_small = adam_update(w_small, m_small, v_small, small_sum * factor, 0.5)
    loss = loss_sum / global_count
    return (
        loss,
        grad_norm,
        new_wide[0],
        new_wide[1],
        new_wide[2],
        new_deep[0],
        new_deep[1],
        new_deep[2],
        new_small[0],
        new_small[1],
        new_small[2],
    )


def solution(mesh):
    in_specs = (
        P("clip", None, "band", None, None),
        P("clip", None, "band", None, None),
        P("clip"),
        P("clip"),
        P("clip", None),
        P("clip", None, None),
        P("clip", None),
        P("clip", None),
        P("clip", None),
        P("clip", None),
        P("clip", None),
        P("clip", None),
        P(),
        P(),
        P(),
    )
    out_specs = (
        P(),
        P(),
        P("clip", None),
        P("clip", None),
        P("clip", None),
        P("clip", None),
        P("clip", None),
        P("clip", None),
        P(),
        P(),
        P(),
    )
    return jax.shard_map(
        per_device, mesh=mesh, in_specs=in_specs, out_specs=out_specs, check_vma=False
    )
```

```python
from functools import partial
import math

import jax
import jax.numpy as jnp
from jax import lax
from jax.experimental import pallas as pl
from jax.experimental.pallas import tpu as pltpu
from jax.sharding import PartitionSpec as P

D = 1024
HEADS = 16
HEAD_DIM = 64
FF = 4096
CH = 8
SPACE = 16
WIN = 8
SHIFT = 4
TMAX = 1000
STEP = 10


EPS_NORM = 1e-06
CLIP_MAX = 0.001
BETA_ONE = 0.9
BETA_TWO = 0.95
ADAM_EPS = 1e-08
DECAY = 0.1


def shifted(value, axis, by):
    length = lax.axis_size(axis)
    return lax.ppermute(value, axis, [(i, (i + by) % length) for i in range(length)])


def matmul(left_op, right_op):
    return jnp.dot(left_op, right_op, preferred_element_type=jnp.float32)


def matmul_tn(left_op, right_op, precision=None):
    return lax.dot_general(
        left_op,
        right_op,
        (((0,), (0,)), ((), ())),
        precision=precision,
        preferred_element_type=jnp.float32,
    )


def matmul_nt(left_op, right_op):
    return lax.dot_general(
        left_op, right_op, (((1,), (1,)), ((), ())), preferred_element_type=jnp.float32
    )


def layer_norm(field_in):
    average = jnp.mean(field_in, -1, keepdims=True)
    centred = field_in - average
    return centred * lax.rsqrt(jnp.mean(centred * centred, -1, keepdims=True) + EPS_NORM)


def norm_modulated(field_in, shift_vec, scale_vec):
    return layer_norm(field_in) * (1.0 + scale_vec) + shift_vec


def norm_gained(field_in, gain_vec):
    return layer_norm(field_in) * gain_vec


def time_features(time_value):
    half_width = D // 2
    frequency = jnp.exp(-math.log(10000.0) * jnp.arange(half_width, dtype=jnp.float32) / half_width)
    angles = time_value[..., None] * frequency
    return jnp.concatenate([jnp.cos(angles), jnp.sin(angles)], -1)


def token_order(grid):
    frames, rows, cols, width = grid.shape
    halves = grid.reshape(frames, rows, cols // WIN, WIN, width).transpose(2, 0, 1, 3, 4)
    return halves.reshape(frames * rows * cols, width)


def with_rows(tokens, first_rows, run):
    width = tokens.shape[1]
    runs = tokens.reshape(-1, run, width)
    return jnp.concatenate([first_rows, runs[:, first_rows.shape[1] :]], 1).reshape(-1, width)


def first_rows(tokens, run, part):
    return tokens.reshape(-1, run, tokens.shape[1])[:, :part]


def attend_pieces(tokens, frames, keys):
    if keys == "frame":
        run = tokens // (2 * frames)
        return [((f * run, run), (tokens // 2 + f * run, run)) for f in range(frames)]
    if keys == "half":
        return [((half * (tokens // 2), tokens // 2),) for half in range(2)]
    return [((0, tokens),)]


def take(ref, runs):
    pieces = [ref[low : low + many, :] for low, many in runs]
    return pieces[0] if len(pieces) == 1 else jnp.concatenate(pieces, 0)


def put(ref, cols, runs, value):
    done = 0
    for low, many in runs:
        ref[low : low + many, cols] = value[done : done + many].astype(ref.dtype)
        done += many


def softmax_of(scores, axis, text_len):
    if text_len:
        place = lax.broadcasted_iota(jnp.int32, scores.shape, axis)
        scores = jnp.where(place < text_len, scores, -1e30)
    weight = jnp.exp(scores - jnp.max(scores, axis, keepdims=True))
    return weight * (1.0 / jnp.sum(weight, axis, keepdims=True))


def lanes_of(head, shape):
    lane = lax.broadcasted_iota(jnp.int32, shape, 1)
    return lane < HEAD_DIM if head == 0 else lane >= HEAD_DIM


def only(head, value):
    return jnp.where(lanes_of(head, value.shape), value, jnp.zeros_like(value))


def attention_gradients(queries, keys, values, grad_out, text_len):
    dq, dk, dv = [], [], []
    for head in range(2):
        probs = softmax_of(matmul_nt(keys, only(head, queries)), 0, text_len)
        dprobs = matmul_nt(values, only(head, grad_out))
        dv.append(matmul(probs.astype(jnp.bfloat16), grad_out))
        inner = jnp.sum(probs * dprobs, 0, keepdims=True)
        dscores = (probs * (dprobs - inner)).astype(jnp.bfloat16)
        dk.append(matmul(dscores, queries))
        dq.append(matmul_tn(dscores, keys))
    dq, dk, dv = (jnp.where(lanes_of(0, x[0].shape), *x) for x in (dq, dk, dv))
    return dq * HEAD_DIM ** (-0.5), dk, dv


def key_sets(key_refs, runs, text_len):
    if text_len:
        return key_refs[0][...]
    pieces = [take(ref, runs) for ref in key_refs]
    return pieces[0] if len(pieces) == 1 else jnp.concatenate(pieces, 0)


def attend_kernel(windows, text_len, sets, *refs):
    q_ref, k_refs, v_refs, out_ref = refs[0], refs[1 : 1 + sets], refs[1 + sets : 1 + 2 * sets], refs[-1]
    for runs in windows:
        queries = take(q_ref, runs) * HEAD_DIM ** (-0.5)
        keys, values = key_sets(k_refs, runs, text_len), key_sets(v_refs, runs, text_len)
        outs = []
        for head in range(2):
            probs = softmax_of(matmul_nt(only(head, queries), keys), 1, text_len)
            outs.append(matmul(probs.astype(jnp.bfloat16), values))
        put(out_ref, slice(None), runs, jnp.where(lanes_of(0, outs[0].shape), *outs))


def attend_back_kernel(windows, text_len, sets, *refs):
    q_ref, k_refs, v_refs = refs[0], refs[1 : 1 + sets], refs[1 + sets : 1 + 2 * sets]
    grad_ref = refs[1 + 2 * sets]
    dq_ref = refs[2 + 2 * sets]
    own_ref = refs[3 + 2 * sets] if text_len else None
    pair = pl.program_id(0)
    cols = [pl.ds(pl.multiple_of(i * D + pair * 2 * HEAD_DIM, 128), 2 * HEAD_DIM) for i in range(3)]
    merged = dq_ref.shape[1] == 3 * D
    for runs in windows:
        queries = take(q_ref, runs) * HEAD_DIM ** (-0.5)
        keys, values = key_sets(k_refs, runs, text_len), key_sets(v_refs, runs, text_len)
        grad_out = take(grad_ref, runs)
        dq, dk, dv = attention_gradients(queries, keys, values, grad_out, text_len)
        put(dq_ref, cols[0], runs, dq)
        if merged:
            put(dq_ref, cols[1], runs, dk)
            put(dq_ref, cols[2], runs, dv)
        else:
            own_ref[:, cols[0]] = dk
            own_ref[:, cols[1]] = dv


def pair_cols(which, pair):
    return pl.ds(pl.multiple_of(which * D + pair * 2 * HEAD_DIM, 128), 2 * HEAD_DIM)


def take_cols(ref, cols, runs):
    return jnp.concatenate([ref[low : low + many, cols] for low, many in runs], 0)


def attend_frames_kernel(windows, qkv_ref, out_ref, far_ref, send, recv):
    band = lax.axis_index("band")
    partner = (lax.axis_index("clip"), band + 1 - 2 * (band % 2))
    greet([partner])

    def copies(pair):
        return [
            pltpu.make_async_remote_copy(
                qkv_ref.at[:, pair_cols(1 + i, pair)],
                far_ref.at[:, pair_cols(i, pair)],
                send.at[pair, i],
                recv.at[pair, i],
                partner,
                MESH,
            )
            for i in range(2)
        ]

    @pl.loop(0, HEADS // 2)
    def _(pair):
        for copy in copies(pair):
            copy.start()

    @pl.loop(0, HEADS // 2)
    def _(pair):
        for copy in copies(pair):
            copy.wait_recv()
        for runs in windows:
            queries = take_cols(qkv_ref, pair_cols(0, pair), runs) * HEAD_DIM ** (-0.5)
            keys, values = (
                jnp.concatenate(
                    [
                        take_cols(qkv_ref, pair_cols(1 + i, pair), runs),
                        take_cols(far_ref, pair_cols(i, pair), runs),
                    ],
                    0,
                )
                for i in range(2)
            )
            outs = []
            for head in range(2):
                probs = softmax_of(matmul_nt(only(head, queries), keys), 1, 0)
                outs.append(matmul(probs.astype(jnp.bfloat16), values))
            put(out_ref, pair_cols(0, pair), runs, jnp.where(lanes_of(0, outs[0].shape), *outs))

    @pl.loop(0, HEADS // 2)
    def _(pair):
        for copy in copies(pair):
            copy.wait_send()


def attend_frames_back_kernel(
    windows, qkv_ref, far_ref, grad_ref, out_ref, own_buf, far_put, far_got, send, recv
):
    band = lax.axis_index("band")
    partner = (lax.axis_index("clip"), band + 1 - 2 * (band % 2))
    greet([partner])

    def copies(pair):
        return [
            pltpu.make_async_remote_copy(
                far_put.at[:, pair_cols(i, pair)],
                far_got.at[:, pair_cols(i, pair)],
                send.at[pair, i],
                recv.at[pair, i],
                partner,
                MESH,
            )
            for i in range(2)
        ]

    def merge(pair):
        for i, copy in enumerate(copies(pair)):
            copy.wait_recv()
            cols = pair_cols(i, pair)
            total = own_buf[:, cols] + far_got[:, cols]
            out_ref[:, pair_cols(1 + i, pair)] = total.astype(jnp.bfloat16)

    @pl.loop(0, HEADS // 2)
    def _(pair):
        for runs in windows:
            queries = take_cols(qkv_ref, pair_cols(0, pair), runs) * HEAD_DIM ** (-0.5)
            keys, values = (
                jnp.concatenate(
                    [
                        take_cols(qkv_ref, pair_cols(1 + i, pair), runs),
                        take_cols(far_ref, pair_cols(i, pair), runs),
                    ],
                    0,
                )
                for i in range(2)
            )
            grad_out = take_cols(grad_ref, pair_cols(0, pair), runs)
            dq, *dkv = attention_gradients(queries, keys, values, grad_out, 0)
            put(out_ref, pair_cols(0, pair), runs, dq)
            half = keys.shape[0] // 2
            for i, value in enumerate(dkv):
                put(own_buf, pair_cols(i, pair), runs, value[:half])
                put(far_put, pair_cols(i, pair), runs, value[half:])
        for copy in copies(pair):
            copy.start()

        @pl.when(pair >= 1)
        def _():
            merge(pair - 1)

    merge(HEADS // 2 - 1)

    @pl.loop(0, HEADS // 2)
    def _(pair):
        for copy in copies(pair):
            copy.wait_send()


def attend_frames(qkv, windows):
    tokens = qkv.shape[0]
    dma = pltpu.SemaphoreType.DMA((HEADS // 2, 2))
    return pl.pallas_call(
        partial(attend_frames_kernel, windows),
        out_shape=(
            jax.ShapeDtypeStruct((tokens, D), jnp.bfloat16),
            jax.ShapeDtypeStruct((tokens, 2 * D), jnp.bfloat16),
        ),
        in_specs=[IN_VMEM],
        out_specs=(IN_VMEM,) * 2,
        scratch_shapes=[dma, dma],
        compiler_params=pltpu.CompilerParams(
            collective_id=4, has_side_effects=True, vmem_limit_bytes=40 << 20
        ),
        cost_estimate=attention_cost(tokens, 256, 2),
    )(qkv)


def attend_frames_back(qkv, far_kv, grad_out, windows):
    tokens = qkv.shape[0]
    dma = pltpu.SemaphoreType.DMA((HEADS // 2, 2))
    return pl.pallas_call(
        partial(attend_frames_back_kernel, windows),
        out_shape=jax.ShapeDtypeStruct(qkv.shape, jnp.bfloat16),
        in_specs=[IN_VMEM] * 3,
        out_specs=IN_VMEM,
        scratch_shapes=[pltpu.VMEM((tokens, 2 * D), jnp.float32)] * 3 + [dma, dma],
        compiler_params=pltpu.CompilerParams(
            collective_id=5, has_side_effects=True, vmem_limit_bytes=50 << 20
        ),
        cost_estimate=attention_cost(tokens, 256, 5),
    )(qkv, far_kv, grad_out)


def head_cols(array, first):
    return array, pl.BlockSpec((array.shape[0], 2 * HEAD_DIM), lambda h: (0, first + h))


def attention_operands(queries, key_values):
    ins = [head_cols(queries, 0)]
    ins += [head_cols(array, first) for array, first, _ in key_values]
    return ins + [head_cols(array, second) for array, _, second in key_values]


def attention_cost(tokens, keys, products):
    flops = 2 * products * tokens * keys * D * 2
    return pl.CostEstimate(
        flops=flops, bytes_accessed=tokens * D * 2 * 8, transcendentals=tokens * keys * HEADS
    )


def attend(queries, key_values, windows, text_len=0):
    tokens = queries.shape[0]
    ins = attention_operands(queries, key_values)
    return pl.pallas_call(
        partial(attend_kernel, windows, text_len, len(key_values)),
        grid=(HEADS // 2,),
        in_specs=[spec for _, spec in ins],
        out_specs=pl.BlockSpec((tokens, 2 * HEAD_DIM), lambda h: (0, h)),
        out_shape=jax.ShapeDtypeStruct((tokens, D), jnp.bfloat16),
        compiler_params=pltpu.CompilerParams(vmem_limit_bytes=40 << 20),
        cost_estimate=attention_cost(tokens, 320, 2),
    )(*[array for array, _ in ins])


def attend_back(queries, key_values, grad_out, windows, text_len=0):
    tokens = queries.shape[0]
    ins = attention_operands(queries, key_values) + [head_cols(grad_out, 0)]
    sets = len(key_values)
    whole = lambda rows, cols: pl.BlockSpec((rows, cols), lambda h: (0, 0))
    if sets == 1 and not text_len:
        outs = [((tokens, 3 * D), jnp.bfloat16)]
    else:
        rows = key_values[0][0].shape[0]
        outs = [((tokens, D), jnp.bfloat16)] + [((rows, 2 * D), jnp.float32)] * sets
    return pl.pallas_call(
        partial(attend_back_kernel, windows, text_len, sets),
        grid=(HEADS // 2,),
        in_specs=[spec for _, spec in ins],
        out_specs=[whole(*shape) for shape, _ in outs],
        out_shape=[jax.ShapeDtypeStruct(*out) for out in outs],
        compiler_params=pltpu.CompilerParams(vmem_limit_bytes=50 << 20),
        cost_estimate=attention_cost(tokens, 320, 5),
    )(*[array for array, _ in ins])


def mlp_forward(stream, modul, up_weight, down_weight):
    mlp_val, norm_back = jax.vjp(norm_modulated, stream, modul[3], modul[4])
    mlp_in = mlp_val.astype(jnp.bfloat16)
    up_proj = matmul(mlp_in, up_weight)
    share = 0.5 + 0.5 * lax.erf(up_proj * math.sqrt(0.5))
    gelu_val = up_proj * share
    slope = share + up_proj * (jnp.exp(-0.5 * up_proj * up_proj) / math.sqrt(2.0 * math.pi))
    gelu_low = gelu_val.astype(jnp.bfloat16)
    down_proj = matmul(gelu_low, down_weight)
    return (stream + modul[5] * down_proj, (norm_back, mlp_in, slope, gelu_low, down_proj))


def mlp_backward(grad_stream, modul, up_weight, down_weight, saved):
    norm_back, mlp_in, slope, gelu_low, down_proj = saved
    grad_down = (modul[5] * grad_stream).astype(jnp.bfloat16)
    grad_gate = jnp.sum(grad_stream * down_proj, 0)
    grad_up = (slope * matmul_nt(grad_down, down_weight)).astype(jnp.bfloat16)
    grad_part, grad_shift, grad_scale = norm_back(matmul_nt(grad_up, up_weight))
    factors = ((gelu_low, grad_down), (mlp_in, grad_up))
    return (grad_stream + grad_part, factors, (grad_shift, grad_scale, grad_gate))


def adam_update(weight, first_mom, second_mom, grad_val, learn_rate):
    first_mom = BETA_ONE * first_mom + (1.0 - BETA_ONE) * grad_val
    second_mom = BETA_TWO * second_mom + (1.0 - BETA_TWO) * grad_val * grad_val
    first_hat = first_mom / (1.0 - BETA_ONE**STEP)
    second_hat = second_mom / (1.0 - BETA_TWO**STEP)
    weight = weight - learn_rate * (first_hat / (jnp.sqrt(second_hat) + ADAM_EPS) + DECAY * weight)
    return (weight, first_mom, second_mom)

MESH = pl.DeviceIdType.MESH
ANY = pl.BlockSpec(memory_space=pl.ANY)
IN_VMEM = pl.BlockSpec(memory_space=pltpu.VMEM)
TEXT_PAD = 80


def ring_place(clip, count):
    half = clip // 2
    odd = clip % 2
    return half + odd * (count - 1 - 2 * half)


def ring_clip(place, count):
    far = place // (count // 2)
    return (1 - far) * 2 * place + far * (2 * (count - 1 - place) + 1)


def greet(peers):
    barrier = pltpu.get_barrier_semaphore()
    for peer in peers:
        pl.semaphore_signal(barrier, inc=1, device_id=peer, device_id_type=MESH)
    pl.semaphore_wait(barrier, len(peers))


def exchange_kernel(count, facts_ref, facts_out, send, recv):
    me = lax.axis_index("clip")
    band = lax.axis_index("band")
    peers = [((me + step) % count, band) for step in range(1, count)]
    greet(peers)
    sent = [
        pltpu.make_async_remote_copy(
            facts_ref, facts_out.at[me], send.at[step], recv.at[step], peer, MESH
        )
        for step, peer in enumerate(peers)
    ]
    for copy in sent:
        copy.start()
    facts_out[me] = facts_ref[...]
    for copy in sent:
        copy.wait()


def exchange_facts(facts):
    count = lax.axis_size("clip")
    return pl.pallas_call(
        partial(exchange_kernel, count),
        out_shape=jax.ShapeDtypeStruct((count,) + facts.shape, facts.dtype),
        in_specs=[IN_VMEM],
        out_specs=IN_VMEM,
        scratch_shapes=[pltpu.SemaphoreType.DMA((count - 1,))] * 2,
        compiler_params=pltpu.CompilerParams(collective_id=0, has_side_effects=True),
    )(facts)


def gather_kernel(count, picks, sides, *refs):
    num = len(picks)
    packs, vec_ref, text_ref = refs[:2], refs[2], refs[3]
    full, (vec_out, text_out, kv_out) = refs[4 : 4 + num], refs[4 + num : 7 + num]
    refs = refs[7 + num :]
    wide, shards = refs[:num], refs[num : 2 * num]
    ring_send, ring_recv, pair_send, pair_recv, cross_send, cross_recv = refs[2 * num : 2 * num + 6]
    load_sem, own_sem, part_send, part_recv, part_own = refs[2 * num + 6 : 2 * num + 11]
    kv_wide, kv_part, kv_put, kv_got, kv_sum, kv_load, kv_send, kv_recv, band_send, band_recv = refs[
        2 * num + 11 :
    ]
    shapes = [(packs[pack].shape[0], cols) for pack, _, cols in picks]
    loads = [
        pltpu.make_async_copy(
            packs[pack].at[:, pl.ds(start, cols)], wide[group], load_sem.at[group]
        )
        for group, (pack, start, cols) in enumerate(picks)
    ]
    kv_width = kv_wide.shape[1]
    kv_first = D + lax.axis_index("band") * kv_width
    kv_weight = pltpu.make_async_copy(
        packs[1].at[:, pl.ds(pl.multiple_of(kv_first, 128), kv_width)], kv_wide, kv_load
    )
    for copy in loads + [kv_weight]:
        copy.start()
    me = lax.axis_index("clip")
    band = lax.axis_index("band")
    core = band % 2
    place = ring_place(me, count)
    onward = 1 - 2 * core
    following = (ring_clip((place + onward + count) % count, count), band)
    plane = band // 2
    partner = (me, band + 1 - 2 * core)
    mirror = (me, band + 2 - 4 * plane)
    peers = [((me + step) % count, band) for step in range(1, count)]
    band_count = 2 * D // kv_width
    band_peers = [(me, (band + step) % band_count) for step in range(1, band_count)]
    greet(peers + band_peers)

    def block(ref, group, owner):
        rows, cols = shapes[group]
        return ref.at[
            pl.ds(pl.multiple_of(owner * rows, rows), rows),
            pl.ds(pl.multiple_of(core * (cols // 2), 128), cols // 2),
        ]

    def ring_copy(group, step):
        owner = ring_clip((place - onward * step + 2 * count) % count, count)
        there = block(full[group], group, owner)
        return pltpu.make_async_remote_copy(
            there, there, ring_send.at[step, group], ring_recv.at[step, group], following, MESH
        )

    def handed(group, step, send, recv, peer):
        owner = ring_clip((place - onward * (step + 1) + 2 * count) % count, count)
        there = block(full[group], group, owner)
        return pltpu.make_async_remote_copy(
            there, there, send.at[step, group], recv.at[step, group], peer, MESH
        )

    def pair_copy(group, step):
        return handed(group, step, pair_send, pair_recv, partner)

    def cross_copy(group, step):
        return handed(group, step, cross_send, cross_recv, mirror)

    def in_ring(group):
        def decorate(body):
            if sides[group]:
                pl.when(plane == sides[group] - 1)(body)
            else:
                body()

        return decorate

    def off_ring(group, also=None):
        def decorate(body):
            if sides[group]:
                off = plane != sides[group] - 1
                pl.when(off if also is None else jnp.logical_and(off, also))(body)

        return decorate

    def ring_arrival(group, step, onto):
        ring_copy(group, step).wait_recv()
        if onto:
            ring_copy(group, step + 1).start()
        pair_copy(group, step).start()
        if sides[group]:
            cross_copy(group, step).start()

    def cross_arrival(group, step):
        cross_copy(group, step).wait_recv()
        pair_copy(group, step).start()

    def own_copy(group):
        rows, cols = shapes[group]
        return pltpu.make_async_copy(
            shards[group],
            full[group].at[pl.ds(pl.multiple_of(me * rows, rows), rows), :],
            own_sem.at[group],
        )

    parts = []
    for step, peer in enumerate(peers):
        for which, (src, dst) in enumerate(((vec_ref, vec_out), (text_ref, text_out))):
            parts.append(
                pltpu.make_async_remote_copy(
                    src.at[peer[0]],
                    dst.at[me],
                    part_send.at[which, step],
                    part_recv.at[which, step],
                    peer,
                    MESH,
                )
            )
    parts_own = [
        pltpu.make_async_copy(src.at[me], dst.at[me], part_own.at[which])
        for which, (src, dst) in enumerate(((vec_ref, vec_out), (text_ref, text_out)))
    ]
    for copy in parts_own + parts[::2]:
        copy.start()
    for group in range(num):
        rows, cols = shapes[group]
        loads[group].wait()
        shards[group][...] = wide[group][...].astype(jnp.bfloat16)
        own_copy(group).start()

        @in_ring(group)
        def _(group=group, rows=rows, cols=cols):
            pltpu.make_async_remote_copy(
                shards[group].at[:, pl.ds(pl.multiple_of(core * (cols // 2), 128), cols // 2)],
                block(full[group], group, me),
                ring_send.at[0, group],
                ring_recv.at[0, group],
                following,
                MESH,
            ).start()

    for copy in parts[1::2]:
        copy.start()

    def kv_copy(hop):
        return pltpu.make_async_remote_copy(
            kv_put.at[hop], kv_got.at[hop], kv_send.at[hop], kv_recv.at[hop], following, MESH
        )

    def kv_hop(hop):
        owner = ring_clip((place - onward * (hop + 1) + 2 * count) % count, count)
        total = kv_part[owner]
        if not isinstance(hop, int) or hop > 0:
            kv_copy(hop - 1).wait_recv()
            total = total + kv_got[hop - 1]
        kv_put[hop] = total
        kv_copy(hop).start()

    def band_copies():
        return [
            pltpu.make_async_remote_copy(
                kv_sum, kv_out.at[band], band_send.at[step], band_recv.at[step], peer, MESH
            )
            for step, peer in enumerate(band_peers)
        ]

    for copy in parts_own + parts:
        copy.wait()
    kv_weight.wait()
    weight = kv_wide[...].astype(jnp.bfloat16)
    for owner in range(count):
        kv_part[owner] = matmul(text_out[owner], weight)
    kv_hop(0)

    @pl.loop(1, count - 1)
    def _(step):
        for group in range(num):

            @in_ring(group)
            def _(group=group):
                ring_arrival(group, step - 1, True)

        kv_hop(step)
        for group in range(num):

            @off_ring(group, step >= 2)
            def _(group=group):
                cross_arrival(group, step - 2)

    for group in range(num):

        @in_ring(group)
        def _(group=group):
            ring_arrival(group, count - 2, False)

    for late in (count - 3, count - 2):
        for group in range(num):

            @off_ring(group)
            def _(group=group, late=late):
                cross_arrival(group, late)

    kv_copy(count - 2).wait_recv()
    kv_sum[...] = (kv_part[me] + kv_got[count - 2]).astype(jnp.bfloat16)
    kv_out[band] = kv_sum[...]
    for copy in band_copies():
        copy.start()
    for group in range(num):
        own_copy(group).wait()

    @pl.loop(0, count - 1)
    def _(step):
        for group in range(num):

            @in_ring(group)
            def _(group=group):
                ring_copy(group, step).wait_send()
                if sides[group]:
                    cross_copy(group, step).wait_send()

            pair_copy(group, step).wait()
        kv_copy(step).wait_send()

    for copy in band_copies():
        copy.wait()


def gather_quarters(shard):
    band_count = lax.axis_size("band")
    rows = shard.shape[0] // band_count
    own = lax.dynamic_slice_in_dim(shard, lax.axis_index("band") * rows, rows, 0)
    return lax.all_gather(own.astype(jnp.bfloat16), ("clip", "band"), axis=0, tiled=True)


def sum_rows(left, right):
    part = lax.psum_scatter(
        matmul_tn(left, right), ("clip", "band"), scatter_dimension=0, tiled=True
    )
    return lax.all_gather(part, "band", axis=0, tiled=True)


def gather_weights(packs, picks, sides, vectors, texts):
    count, band_count = lax.axis_size("clip"), lax.axis_size("band")
    num = len(picks)
    dma = pltpu.SemaphoreType.DMA
    shapes = [(packs[pack].shape[0], cols) for pack, _, cols in picks]
    kv_shape = (texts.shape[1], 2 * D // band_count)
    kv_all = pltpu.VMEM((count,) + kv_shape, jnp.float32)
    kv_hops = pltpu.VMEM((count - 1,) + kv_shape, jnp.float32)
    out = pl.pallas_call(
        partial(gather_kernel, count, picks, sides),
        out_shape=tuple(
            jax.ShapeDtypeStruct((count * rows, cols), jnp.bfloat16) for rows, cols in shapes
        )
        + tuple(jax.ShapeDtypeStruct(v.shape, v.dtype) for v in (vectors, texts))
        + (jax.ShapeDtypeStruct((band_count,) + kv_shape, jnp.bfloat16),),
        in_specs=[ANY] * 4,
        out_specs=(ANY,) * (num + 1) + (IN_VMEM,) * 2,
        scratch_shapes=[pltpu.VMEM(shape, jnp.float32) for shape in shapes]
        + [pltpu.VMEM(shape, jnp.bfloat16) for shape in shapes]
        + [dma((count - 1, num))] * 6
        + [dma((num,)), dma((num,)), dma((2, count - 1)), dma((2, count - 1)), dma((2,))]
        + [
            pltpu.VMEM((packs[1].shape[0], kv_shape[1]), jnp.float32),
            kv_all,
            kv_hops,
            kv_hops,
            pltpu.VMEM(kv_shape, jnp.bfloat16),
            dma,
            dma((count - 1,)),
            dma((count - 1,)),
            dma((band_count - 1,)),
            dma((band_count - 1,)),
        ],
        compiler_params=pltpu.CompilerParams(
            collective_id=1, has_side_effects=True, vmem_limit_bytes=50 << 20
        ),
        cost_estimate=pl.CostEstimate(flops=2 * 10**11, bytes_accessed=6 * 10**8, transcendentals=0),
    )(*packs, vectors, texts)
    return out[:num], out[num], out[num + 1], out[num + 2]


WIRE_MAX = 32767.0
WIRE_LEAST = 1e-30
UNIT = (128, 512)


def unit_parts(kind, first):
    if kind == 0:
        return ((0, 4, lambda u: u, lambda u: 0), (4, 4, lambda u: 4, lambda u: u - 3))
    if first:
        return ((2, 2, lambda u: u, lambda u: u), (4, 2, lambda u: 3, lambda u: u))
    return ((0, 3, lambda u: u, lambda u: u), (3, 3, lambda u: 3, lambda u: u))


def reduce_kernel(count, tokens, phases, *refs):
    num = sum(len(phase["lefts"]) for phase in phases)
    lefts, rights = refs[:num], refs[num : 2 * num]
    vec_ref, kv_ref, text_ref = refs[2 * num : 2 * num + 3]
    refs = refs[2 * num + 3 :]
    wide_out, deep_out, square_out, all_vec, kv_out, kv_square = refs[:6]
    left_far, right_far = refs[6 : 6 + num], refs[6 + num : 6 + 2 * num]
    scratch = refs[6 + 2 * num :]
    left_buf, right_buf, got_low, got_scale, put_low, put_scale, plane_put = (
        scratch[2 * i : 2 * i + 2] for i in range(7)
    )
    plane_got = scratch[14 : 14 + len(phases)]
    (
        square_buf,
        left_sem,
        right_sem,
        pair_send,
        pair_recv,
        half_send,
        half_recv,
        ring_send,
        ring_recv,
        credit,
        plane_send,
        plane_recv,
        out_sem,
        out_send,
        out_recv,
        last_put,
        last_put_scale,
        last_got,
        last_got_scale,
        push_send,
        push_recv,
        vec_got,
        kv_got,
        vec_sum,
        all_kv,
        text_buf,
        kv_grad,
        side_own,
        side_send,
        side_recv,
        vec_send,
        vec_recv,
        vec_pair_send,
        vec_pair_recv,
        kv_own,
        kv_send,
        kv_recv,
    ) = scratch[14 + len(phases) :]
    me = lax.axis_index("clip")
    band = lax.axis_index("band")
    core = band % 2
    plane = band // 2
    place = ring_place(me, count)
    onward = 1 - 2 * core
    following = (ring_clip((place + onward + count) % count, count), band)
    preceding = (ring_clip((place - onward + count) % count, count), band)
    partner = (me, band + 1 - 2 * core)
    mirror = (me, band + 2 - 4 * plane)
    band_count = vec_got.shape[0]
    band_peers = [(me, (band + step) % band_count) for step in range(1, band_count)]
    greet([following, preceding] + band_peers)

    def owner_at(step, way):
        return ring_clip((place - way * (step + 1) + 2 * count) % count, count)

    def left_blocks(at):
        phase = phases[at]
        if phase["kind"] == 0:
            return [(b, phase["lefts"][0], b, 4) for b in range(4)] + [(4, phase["lefts"][1], 0, 1)]
        first = phase["first"]
        return [(first + i, left, 0, 1) for i, left in enumerate(phase["lefts"])]

    def right_blocks(at):
        phase = phases[at]
        if phase["kind"] == 0:
            return [(0, phase["lefts"][0], 0)] + [(1 + i, phase["lefts"][1], i) for i in range(4)]
        first = phase["first"]
        return [(first + i, phase["lefts"][i], 0) for i in range(3 - first)] + [
            (3 + i, phase["lefts"][-1], i) for i in range(3)
        ]

    def left_cols(step, way, which, many):
        width = lefts_width // count if many == 1 else deep_width // count
        start = owner_at(step, way) * width + which * 128
        return pl.ds(pl.multiple_of(start, 128), 128)

    lefts_width = lefts[phases[1]["lefts"][0]].shape[1]
    deep_width = lefts[phases[0]["lefts"][0]].shape[1]

    def pair_left(at, step):
        out = []
        for block, operand, which, many in left_blocks(at):
            cols = left_cols(step, -onward, which, many)
            out.append(
                pltpu.make_async_remote_copy(
                    lefts[operand].at[:, cols],
                    left_far[operand].at[:, cols],
                    pair_send.at[at, block, step],
                    pair_recv.at[at, block, step],
                    partner,
                    MESH,
                )
            )
        return out

    def pair_right(at):
        out = []
        for i, operand in enumerate(phases[at]["lefts"]):
            half = rights[operand].shape[1] // 2
            out.append(
                pltpu.make_async_remote_copy(
                    rights[operand].at[:, pl.ds(pl.multiple_of((1 - core) * half, 128), half)],
                    right_far[operand],
                    half_send.at[operand],
                    half_recv.at[operand],
                    partner,
                    MESH,
                )
            )
        return out

    def load_left(at, step, slot, far):
        kind = phases[at]["kind"]
        out = []
        for block, operand, which, many in left_blocks(at):
            cols = left_cols(step, onward, which, many)
            source = left_far if far else lefts
            out.append(
                pltpu.make_async_copy(
                    source[operand].at[:, cols],
                    left_buf[kind].at[slot, block, pl.ds(far * tokens, tokens), :],
                    left_sem.at[kind, slot, block, far],
                )
            )
        return out

    def load_right(at, far):
        kind = phases[at]["kind"]
        out = []
        for block, operand, which in right_blocks(at):
            if far:
                source = right_far[operand].at[:, pl.ds(which * UNIT[1], UNIT[1])]
            else:
                half = rights[operand].shape[1] // 2
                start = pl.multiple_of(core * half + which * UNIT[1], 128)
                source = rights[operand].at[:, pl.ds(start, UNIT[1])]
            out.append(
                pltpu.make_async_copy(
                    source,
                    right_buf[kind].at[block, pl.ds(far * tokens, tokens), :],
                    right_sem.at[kind, block, far],
                )
            )
        return out

    def ring_copies(at, part, slot):
        kind = phases[at]["kind"]
        units = pl.ds(*unit_parts(kind, phases[at]["first"])[part][:2])
        return [
            pltpu.make_async_remote_copy(
                put.at[slot, units],
                got.at[slot, units],
                ring_send.at[kind, slot, part, i],
                ring_recv.at[kind, slot, part, i],
                following,
                MESH,
            )
            for i, (put, got) in enumerate(
                ((put_low[kind], got_low[kind]), (put_scale[kind], got_scale[kind]))
            )
        ]

    def plane_copies(at, part):
        kind = phases[at]["kind"]
        units = pl.ds(*unit_parts(kind, phases[at]["first"])[part][:2])
        pairs = ((plane_put[kind], plane_got[at]),)
        if at + 1 == len(phases):
            pairs = ((last_put, last_got), (last_put_scale, last_got_scale))
        return [
            pltpu.make_async_remote_copy(
                here.at[units],
                there.at[units],
                plane_send.at[at, part, i],
                plane_recv.at[at, part, i],
                mirror,
                MESH,
            )
            for i, (here, there) in enumerate(pairs)
        ]

    def push_right(block):
        operand, which = [entry[1:] for entry in right_blocks(0) if entry[0] == block][0]
        half = rights[operand].shape[1] // 2
        begin = pl.multiple_of((1 - core) * half + which * UNIT[1], 128)
        return pltpu.make_async_remote_copy(
            rights[operand].at[:, pl.ds(begin, UNIT[1])],
            right_buf[phases[0]["kind"]].at[block, pl.ds(tokens, tokens), :],
            push_send.at[block],
            push_recv.at[block],
            partner,
            MESH,
        )

    def out_copies(at, unit):
        phase = phases[at]
        if phase["kind"] == 0 and unit < 4:
            half = UNIT[1]
            rows = deep_out.shape[0] // 4
            there = deep_out.at[
                pl.ds(unit * rows, rows),
                pl.ds(pl.multiple_of(phase["cols"][0] + core * half, 128), half),
            ]
        else:
            which, col = (1, unit - 4) if phase["kind"] == 0 else (unit - phase["first"], 0)
            if phase["kind"] and unit >= 3:
                which, col = len(phase["lefts"]) - 1, unit - 3
            half = rights[phase["lefts"][which]].shape[1] // 2
            start = phase["cols"][which] + core * half + col * UNIT[1]
            there = wide_out.at[:, pl.ds(pl.multiple_of(start, 128), UNIT[1])]
        here = plane_got[at].at[unit]
        return (
            pltpu.make_async_copy(here, there, out_sem.at[at, unit]),
            pltpu.make_async_remote_copy(
                here, there, out_send.at[at, unit], out_recv.at[at, unit], partner, MESH
            ),
        )

    def product(kind, slot, left, right):
        return lax.dot_general(
            left_buf[kind][slot, left],
            right_buf[kind][right],
            (((0,), (0,)), ((), ())),
            preferred_element_type=jnp.float32,
        )

    def start(copies):
        for copy in copies:
            copy.start()

    def finish(copies):
        for copy in copies:
            copy.wait()

    def take_step(at, step, first, last):
        phase = phases[at]
        kind = phase["kind"]
        slot = step % 2
        before = (step + 1) % 2
        for far in range(2):
            finish(load_left(at, step, slot, far))

        def load_next():
            for copy in pair_left(at, step + 1):
                copy.wait_recv()
            for far in range(2):
                start(load_left(at, step + 1, before, far))

        opening = first and at == 0
        if not (last or opening):
            load_next()
        parts = unit_parts(kind, phase["first"])

        def encode(term):
            largest = jnp.maximum(jnp.max(jnp.abs(term), axis=0, keepdims=True), WIRE_LEAST)
            low = jnp.round(term * (WIRE_MAX / largest)).astype(jnp.int16)
            return low, largest * (1.0 / WIRE_MAX)

        for part, (low, many, left_of, right_of) in enumerate(parts):
            if opening:
                blocks = range(1) if part == 0 else range(1, 5)
                finish(load_right(0, 0)[blocks.start : blocks.stop])
                for block in blocks:
                    push_right(block).wait_recv()
            if not first:
                for copy in ring_copies(at, part, before):
                    copy.wait_recv()
            if not (first or last):

                @pl.when(step >= 2)
                def _(part=part):
                    for copy in ring_copies(at, part, slot):
                        copy.wait_send()
                    pl.semaphore_wait(credit.at[kind, part], 1)

            def settle(position, unit, term):
                if not first:
                    came = got_low[kind][before, position].astype(jnp.float32)
                    term = term + came * got_scale[kind][before, position]
                if last and at + 1 == len(phases):
                    last_put[unit], last_put_scale[unit] = encode(term)
                elif last:
                    plane_put[kind][unit] = term
                else:
                    low_part, scale_part = encode(term)
                    put_low[kind][slot, position] = low_part
                    put_scale[kind][slot, position] = scale_part

            @pl.loop(low, low + many)
            def _(unit, left_of=left_of, right_of=right_of):
                settle(unit, unit, product(kind, slot, left_of(unit), right_of(unit)))

            if last:
                start(plane_copies(at, part))
            else:
                start(ring_copies(at, part, slot))
            if not (first or last):

                @pl.when(step < count - 2)
                def _(part=part):
                    pl.semaphore_signal(
                        credit.at[kind, part], inc=1, device_id=preceding, device_id_type=MESH
                    )

        if opening:
            load_next()

    def close(at):
        kind = phases[at]["kind"]

        def add_square(total):
            square_buf[...] += jnp.sum((total * total).reshape(UNIT[0] // 8, 8, UNIT[1]), axis=0)

        for part, (low, many, _, _) in enumerate(unit_parts(kind, phases[at]["first"])):
            finish(plane_copies(at, part))

            @pl.loop(low, low + many)
            def _(unit):
                if at + 1 == len(phases):
                    total = last_put[unit].astype(jnp.float32) * last_put_scale[unit]
                    total += last_got[unit].astype(jnp.float32) * last_got_scale[unit]
                else:
                    total = plane_put[kind][unit] + plane_got[at][unit]
                plane_got[at][unit] = total
                add_square(total)

            for unit in range(low, low + many):
                start(out_copies(at, unit))

    half_rows = pl.ds(pl.multiple_of(core * (vec_sum.shape[0] // 2), 8), vec_sum.shape[0] // 2)
    side_local = [
        pltpu.make_async_copy(vec_ref, vec_got.at[band], side_own.at[0]),
        pltpu.make_async_copy(kv_ref.at[band], kv_got.at[band], side_own.at[1]),
        pltpu.make_async_copy(text_ref, text_buf, side_own.at[2]),
    ]
    side_remote = []
    for step, peer in enumerate(band_peers):
        side_remote += [
            pltpu.make_async_remote_copy(
                vec_ref, vec_got.at[band], side_send.at[0, step], side_recv.at[0, step], peer, MESH
            ),
            pltpu.make_async_remote_copy(
                kv_ref.at[peer[1]],
                kv_got.at[band],
                side_send.at[1, step],
                side_recv.at[1, step],
                peer,
                MESH,
            ),
        ]
    vec_own = pltpu.make_async_copy(vec_sum, all_vec.at[me], side_own.at[3])

    def vec_copies(step):
        owner = ring_clip((place - onward * step + 2 * count) % count, count)
        vec = all_vec.at[owner, half_rows]
        return [
            pltpu.make_async_remote_copy(
                here, there, vec_send.at[step, i], vec_recv.at[step, i], following, MESH
            )
            for i, (here, there) in enumerate(((vec, vec), (all_kv.at[owner], all_kv.at[owner])))
        ]

    def vec_first():
        vec = all_vec.at[me, half_rows]
        return [
            pltpu.make_async_remote_copy(
                here, there, vec_send.at[0, i], vec_recv.at[0, i], following, MESH
            )
            for i, (here, there) in enumerate(
                ((vec_sum.at[half_rows], vec), (all_kv.at[me], all_kv.at[me]))
            )
        ]

    def vec_pair(step):
        owner = ring_clip((place - onward * (step + 1) + 2 * count) % count, count)
        vec = all_vec.at[owner, half_rows]
        return pltpu.make_async_remote_copy(
            vec, vec, vec_pair_send.at[step], vec_pair_recv.at[step], partner, MESH
        )

    kv_width = kv_grad.shape[1]

    def kv_place(owner):
        return kv_out.at[:, pl.ds(pl.multiple_of(owner * kv_width, 128), kv_width)]

    def kv_copy(i):
        if i == 2:
            return pltpu.make_async_copy(kv_grad, kv_place(band), kv_own)
        peer = (partner, mirror)[i]
        return pltpu.make_async_remote_copy(
            kv_grad, kv_place(band), kv_send.at[i], kv_recv.at[i], peer, MESH
        )

    def kv_passed():
        there = kv_place(mirror[1])
        return pltpu.make_async_remote_copy(
            there, there, kv_send.at[2], kv_recv.at[2], partner, MESH
        )

    def sum_bands():
        finish(side_local + side_remote)
        vec_sum[...] = jnp.sum(vec_got[...], 0)
        all_kv[me] = jnp.sum(kv_got[...], 0)
        vec_own.start()
        start(vec_first())

    def pass_sums(step):
        for copy in vec_copies(step - 1):
            copy.wait_recv()
        start(vec_copies(step))
        vec_pair(step - 1).start()

    def multiply_text():
        for copy in vec_copies(count - 2):
            copy.wait_recv()
        vec_pair(count - 2).start()
        grads = all_kv[...].reshape(text_buf.shape[0], -1)
        total = jnp.zeros_like(kv_grad)
        for _ in range(3):
            part = grads.astype(jnp.bfloat16)
            grads = grads - part.astype(jnp.float32)
            total = total + matmul_tn(text_buf[...], part)
        kv_grad[...] = total
        kv_square[...] = jnp.sum((total * total).reshape(-1, 8, total.shape[1]), axis=0)
        start([kv_copy(i) for i in range(3)])

    square_buf[...] = jnp.zeros_like(square_buf)
    start(side_local + side_remote)
    start(load_right(0, 0))
    start(load_left(0, 0, 0, 0))
    push_right(0).start()
    start(pair_left(0, 0))
    for block in range(1, 5):
        push_right(block).start()

    @pl.loop(1, count)
    def _(step):
        start(pair_left(0, step))

    for copy in pair_left(0, 0):
        copy.wait_recv()
    start(load_left(0, 0, 0, 1))
    take_step(0, 0, True, False)
    for at in range(len(phases)):
        more = at + 1 < len(phases)
        if more:
            start(pair_right(at + 1))
            start(load_right(at + 1, 0))
            start(pair_left(at + 1, 0))
        if at == 1:
            sum_bands()

        @pl.loop(1, count - 1)
        def _(step, at=at, more=more):
            take_step(at, step, False, False)
            if at == 1:
                pass_sums(step)
            if more:
                start(pair_left(at + 1, step))

                @pl.when(step == count // 2)
                def _():
                    for copy in pair_right(at + 1):
                        copy.wait_recv()
                    start(load_right(at + 1, 1))
                    for copy in pair_left(at + 1, 0):
                        copy.wait_recv()
                    for far in range(2):
                        start(load_left(at + 1, 0, 0, far))

        if more:
            start(pair_left(at + 1, count - 1))
            for far in range(2):
                finish(load_right(at + 1, far))
            take_step(at + 1, 0, True, False)
        take_step(at, count - 1, False, True)
        if at == 1:
            multiply_text()
        for part in range(2):
            for slot in range(2):
                for copy in ring_copies(at, part, slot):
                    copy.wait_send()
        if at == 2:
            kv_copy(1).wait_recv()
            kv_passed().start()
        if at:
            close(at - 1)
    close(len(phases) - 1)
    vec_own.wait()
    kv_passed().wait()
    kv_copy(0).wait()
    kv_copy(1).wait_send()
    kv_copy(2).wait()

    @pl.loop(0, count - 1)
    def _(step):
        for copy in vec_copies(step):
            copy.wait_send()
        vec_pair(step).wait()

    square_out[...] = square_buf[...]
    for at, phase in enumerate(phases):
        for copy in pair_right(at) if at else [push_right(block) for block in range(5)]:
            copy.wait_send()

        @pl.loop(0, count)
        def _(step, at=at):
            for copy in pair_left(at, step):
                copy.wait_send()

        for unit in range(phase["first"], 8 if phase["kind"] == 0 else 6):
            finish(out_copies(at, unit))


def reduce_gradients(phases, lefts, rights, vectors, keyvals, text, wide_cols, deep_cols):
    count = lax.axis_size("clip")
    tokens = lefts[0].shape[0]
    wide_rows = lefts[1].shape[1] // count
    deep_rows = lefts[0].shape[1] // count
    band_count, _, kv_cols = keyvals.shape
    num = len(lefts)
    dma = pltpu.SemaphoreType.DMA
    units, lefts_of, rights_of = (8, 6), (5, 4), (5, 6)
    scratch = [pltpu.VMEM((2, lefts_of[k], 2 * tokens, 128), jnp.bfloat16) for k in range(2)]
    scratch += [pltpu.VMEM((rights_of[k], 2 * tokens, UNIT[1]), jnp.bfloat16) for k in range(2)]
    for _ in range(2):
        scratch += [pltpu.VMEM((2, units[k]) + UNIT, jnp.int16) for k in range(2)]
        scratch += [pltpu.VMEM((2, units[k], 1, UNIT[1]), jnp.float32) for k in range(2)]
    scratch += [pltpu.VMEM((units[k],) + UNIT, jnp.float32) for k in range(2)]
    scratch += [pltpu.VMEM((units[p["kind"]],) + UNIT, jnp.float32) for p in phases]
    scratch += [
        pltpu.VMEM((8, UNIT[1]), jnp.float32),
        dma((2, 2, 5, 2)),
        dma((2, 6, 2)),
        dma((len(phases), 5, count)),
        dma((len(phases), 5, count)),
        dma((num,)),
        dma((num,)),
        dma((2, 2, 2, 2)),
        dma((2, 2, 2, 2)),
        pltpu.SemaphoreType.REGULAR((2, 2)),
        dma((len(phases), 2, 2)),
        dma((len(phases), 2, 2)),
        dma((len(phases), 8)),
        dma((len(phases), 8)),
        dma((len(phases), 8)),
    ]
    for _ in range(2):
        scratch += [pltpu.VMEM((6,) + UNIT, jnp.int16), pltpu.VMEM((6, 1, UNIT[1]), jnp.float32)]
    scratch += [
        dma((5,)),
        dma((5,)),
        pltpu.VMEM((band_count,) + vectors.shape, jnp.float32),
        pltpu.VMEM(keyvals.shape, jnp.float32),
        pltpu.VMEM(vectors.shape, jnp.float32),
        pltpu.VMEM((count,) + keyvals.shape[1:], jnp.float32),
        pltpu.VMEM(text.shape, jnp.bfloat16),
        pltpu.VMEM((text.shape[1], kv_cols), jnp.float32),
        dma((4,)),
        dma((2, band_count - 1)),
        dma((2, band_count - 1)),
        dma((count - 1, 2)),
        dma((count - 1, 2)),
        dma((count - 1,)),
        dma((count - 1,)),
        dma,
        dma((3,)),
        dma((3,)),
    ]
    out = pl.pallas_call(
        partial(reduce_kernel, count, tokens, phases),
        out_shape=(
            jax.ShapeDtypeStruct((wide_rows, wide_cols), jnp.float32),
            jax.ShapeDtypeStruct((deep_rows, deep_cols), jnp.float32),
            jax.ShapeDtypeStruct((8, UNIT[1]), jnp.float32),
            jax.ShapeDtypeStruct((count,) + vectors.shape, jnp.float32),
            jax.ShapeDtypeStruct((deep_rows, band_count * kv_cols), jnp.float32),
            jax.ShapeDtypeStruct((8, kv_cols), jnp.float32),
        )
        + tuple(jax.ShapeDtypeStruct(x.shape, x.dtype) for x in lefts)
        + tuple(jax.ShapeDtypeStruct((tokens, x.shape[1] // 2), x.dtype) for x in rights),
        in_specs=[ANY] * (2 * num + 3),
        out_specs=(ANY, ANY, IN_VMEM, ANY, ANY, IN_VMEM) + (ANY,) * (2 * num),
        scratch_shapes=scratch,
        compiler_params=pltpu.CompilerParams(
            collective_id=2, has_side_effects=True, vmem_limit_bytes=58 << 20
        ),
        cost_estimate=pl.CostEstimate(flops=3 * 10**11, bytes_accessed=8 * 10**8, transcendentals=0),
    )(*lefts, *rights, vectors, keyvals, text)
    return out[:6]


def total_kernel(count, part_ref, out_ref, mid, band_got, clip_got, *sems):
    me = lax.axis_index("clip")
    band = lax.axis_index("band")
    band_count = band_got.shape[0]
    band_peers = [(me, (band + step) % band_count) for step in range(1, band_count)]
    clip_peers = [((me + step) % count, band) for step in range(1, count)]
    greet(band_peers + clip_peers)
    stages = (
        (part_ref, band_got, band, band_peers, mid, sems[:2]),
        (mid, clip_got, me, clip_peers, out_ref, sems[2:]),
    )
    for value, got, index, peers, result, (send, recv) in stages:
        copies = [
            pltpu.make_async_remote_copy(
                value, got.at[index], send.at[step], recv.at[step], peer, MESH
            )
            for step, peer in enumerate(peers)
        ]
        for copy in copies:
            copy.start()
        got[index] = value[...]
        for copy in copies:
            copy.wait()
        result[...] = jnp.sum(got[...], 0)


def total_over_devices(value):
    count, band_count = lax.axis_size("clip"), lax.axis_size("band")
    dma = pltpu.SemaphoreType.DMA
    tile = (8, 128)
    return pl.pallas_call(
        partial(total_kernel, count),
        out_shape=jax.ShapeDtypeStruct(tile, jnp.float32),
        in_specs=[IN_VMEM],
        out_specs=IN_VMEM,
        scratch_shapes=[
            pltpu.VMEM(tile, jnp.float32),
            pltpu.VMEM((band_count,) + tile, jnp.float32),
            pltpu.VMEM((count,) + tile, jnp.float32),
            dma((band_count - 1,)),
            dma((band_count - 1,)),
            dma((count - 1,)),
            dma((count - 1,)),
        ],
        compiler_params=pltpu.CompilerParams(collective_id=3, has_side_effects=True),
    )(jnp.broadcast_to(value, tile))[0, 0]


def per_device(
    latents,
    noise_field,
    timesteps,
    null_flags,
    frame_mask,
    context,
    w_wide,
    m_wide,
    v_wide,
    w_deep,
    m_deep,
    v_deep,
    w_small,
    m_small,
    v_small,
):
    clip_count = lax.axis_size("clip")
    band_count = lax.axis_size("band")
    clip_at = lax.axis_index("clip")
    band_at = lax.axis_index("band")
    wide_rows = w_wide.shape[0]
    deep_rows = w_deep.shape[0]
    text_len, text_dim = context.shape[1:]
    facts = jnp.pad(
        jnp.concatenate([timesteps, frame_mask[0]])[None],
        ((0, 7), (0, 127 - frame_mask.shape[1])),
    )
    kept_text = context[0] * (1 - null_flags[0]).astype(jnp.bfloat16)
    text_cols = jnp.pad(
        kept_text.reshape(text_len, clip_count, deep_rows).transpose(1, 0, 2),
        ((0, 0), (0, TEXT_PAD - text_len), (0, 0)),
    )
    all_facts = exchange_facts(facts)
    all_times = all_facts[:, 0, 0].astype(jnp.float32)
    all_time_low = jax.nn.silu(time_features(all_times)).astype(jnp.bfloat16)
    time_rows = lax.dynamic_slice(
        all_time_low, (0, clip_at * wide_rows), (clip_count, wide_rows)
    )
    part_modul = matmul(time_rows, w_wide[:, : 12 * D].astype(jnp.bfloat16))
    kv_cols = 2 * D // band_count
    up_b_w = gather_quarters(w_wide[:, 22 * D + FF :])
    gathered, all_modul, all_text, keyval = gather_weights(
        (w_wide, w_deep),
        (
            (0, 22 * D, FF),
            (1, 0, D),
            (0, 18 * D, D),
            (0, 19 * D, D),
            (0, 20 * D, D),
            (0, 21 * D, D),
            (0, 12 * D, 3 * D),
            (0, 15 * D, 3 * D),
        ),
        (1, 2, 1, 2, 1, 2, 0, 0),
        part_modul.reshape(clip_count, 12 * D // 128, 128),
        text_cols,
    )
    up_a_w, down_a_w, out_a_w, out_b_w, query_w, cross_out_w, qkv_a_w, qkv_b_w = gathered
    keyval = keyval.transpose(1, 0, 2).reshape(TEXT_PAD, 2 * D)
    late_down_b, all_modul = lax.optimization_barrier((w_deep[:, 3 * D :], all_modul))
    down_b_w = gather_quarters(late_down_b)
    small_low = w_small.astype(jnp.bfloat16)
    small_val = small_low.astype(jnp.float32)
    num_frames, num_rows, num_cols = (latents.shape[1], latents.shape[2], latents.shape[3])
    tok_count = num_frames * num_rows * num_cols
    all_mask = all_facts[:, 0, 1 : 1 + num_frames]
    global_count = jnp.sum(all_mask).astype(jnp.float32) * (num_rows * num_cols * CH * band_count)
    time_value = timesteps[0].astype(jnp.float32)
    noise_angle = 0.5 * math.pi * time_value / TMAX
    signal, spread = (jnp.cos(noise_angle), jnp.sin(noise_angle))
    clean_tok = token_order(latents[0])
    noise_tok = token_order(noise_field[0])
    run = num_rows * WIN
    part = SHIFT * WIN
    frame_windows = attend_pieces(tok_count, num_frames, "frame")
    half_windows = attend_pieces(tok_count, num_frames, "half")
    text_windows = attend_pieces(tok_count, num_frames, "text")
    noisy_low = (signal * clean_tok + spread * noise_tok).astype(jnp.bfloat16)
    target = signal * noise_tok - spread * clean_tok
    modulation = jnp.sum(all_modul, 0).reshape(12, D)
    mod_a, mod_b = (modulation[:6], modulation[6:])
    stream_zero = matmul(noisy_low, small_low[:CH]) + small_val[2 * CH]
    normed_a, back_a = jax.vjp(norm_modulated, stream_zero, mod_a[0], mod_a[1])
    in_a = normed_a.astype(jnp.bfloat16)
    qkv_a = matmul(in_a, qkv_a_w).astype(jnp.bfloat16)
    att_a, far_kv = attend_frames(qkv_a, frame_windows)
    proj_a = matmul(att_a, out_a_w)
    stream_one = stream_zero + mod_a[2] * proj_a
    stream_two, saved_a = mlp_forward(stream_one, mod_a, up_a_w, down_a_w)
    normed_b, back_b = jax.vjp(norm_modulated, stream_two, mod_b[0], mod_b[1])
    low_b = normed_b.astype(jnp.bfloat16)
    rolled = with_rows(low_b, shifted(first_rows(low_b, run, part), "band", -1), run)
    qkv_b = matmul(rolled, qkv_b_w).astype(jnp.bfloat16)
    win_kv = [(qkv_b, HEADS // 2, HEADS)]
    win_out = attend(qkv_b, win_kv, half_windows)
    att_b = with_rows(win_out, shifted(first_rows(win_out, run, part), "band", 1), run)
    proj_b = matmul(att_b, out_b_w)
    stream_three = stream_two + mod_b[2] * proj_b
    cross_val, cross_back = jax.vjp(norm_gained, stream_three, small_val[2 * CH + 1])
    cross_in = cross_val.astype(jnp.bfloat16)
    query_proj = matmul(cross_in, query_w).astype(jnp.bfloat16)
    text_kv = [(keyval, 0, HEADS // 2)]
    crossed = attend(query_proj, text_kv, text_windows, text_len)
    stream_four = stream_three + matmul(crossed, cross_out_w)
    stream_five, saved_b = mlp_forward(stream_four, mod_b, up_b_w, down_b_w)
    final_val, final_back = jax.vjp(norm_gained, stream_five, small_val[2 * CH + 2])
    final_low = final_val.astype(jnp.bfloat16)
    head_low = small_low[CH : 2 * CH]
    predicted = matmul_nt(final_low, head_low)
    weight_row = jnp.repeat(frame_mask[0].astype(jnp.float32), run)
    weight_row = jnp.tile(weight_row, num_cols // WIN)[:, None]
    pred_error = predicted - target
    loss_part = jnp.sum(weight_row * pred_error * pred_error)
    grad_pred = (weight_row * pred_error * (2.0 / global_count)).astype(jnp.bfloat16)
    grad_head = matmul_tn(grad_pred, final_low)
    grad_stream, grad_gain_f = final_back(matmul(grad_pred, head_low))
    grad_stream, mlp_factors_b, extra_b = mlp_backward(
        grad_stream, mod_b, up_b_w, down_b_w, saved_b
    )
    grad_cross = grad_stream.astype(jnp.bfloat16)
    grad_crossed = matmul_nt(grad_cross, cross_out_w).astype(jnp.bfloat16)
    grad_query, grad_keyval = attend_back(
        query_proj, text_kv, grad_crossed, text_windows, text_len
    )
    grad_part, grad_gain_c = cross_back(matmul_nt(grad_query, query_w))
    grad_stream = grad_stream + grad_part
    grad_proj = (mod_b[2] * grad_stream).astype(jnp.bfloat16)
    grad_gate_b = jnp.sum(grad_stream * proj_b, 0)
    factors_ob = (att_b, grad_proj)
    grad_att = matmul_nt(grad_proj, out_b_w).astype(jnp.bfloat16)
    grad_win = with_rows(grad_att, shifted(first_rows(grad_att, run, part), "band", -1), run)
    grad_qkv = attend_back(qkv_b, win_kv, grad_win, half_windows)[0]
    factors_qkvb = (rolled, grad_qkv)
    grad_in_roll = matmul_nt(grad_qkv, qkv_b_w)
    sent_back = shifted(first_rows(grad_in_roll, run, part), "band", 1)
    grad_normed = with_rows(grad_in_roll, sent_back, run)
    grad_part, grad_shift_b, grad_scale_b = back_b(grad_normed)
    grad_stream = grad_stream + grad_part
    grad_stream, mlp_factors_a, extra_a = mlp_backward(
        grad_stream, mod_a, up_a_w, down_a_w, saved_a
    )
    grad_proj = (mod_a[2] * grad_stream).astype(jnp.bfloat16)
    grad_gate_a = jnp.sum(grad_stream * proj_a, 0)
    factors_oa = (att_a, grad_proj)
    grad_att = matmul_nt(grad_proj, out_a_w).astype(jnp.bfloat16)
    grad_qkv = attend_frames_back(qkv_a, far_kv, grad_att, frame_windows)
    factors_qkva = (in_a, grad_qkv)
    grad_part, grad_shift_a, grad_scale_a = back_a(matmul_nt(grad_qkv, qkv_a_w))
    grad_stream = grad_stream + grad_part
    grad_patch = matmul_tn(noisy_low.astype(jnp.float32), grad_stream, lax.Precision.HIGHEST)
    grad_bias = jnp.sum(grad_stream, 0)
    grad_modul = jnp.stack(
        [
            grad_shift_a,
            grad_scale_a,
            grad_gate_a,
            extra_a[0],
            extra_a[1],
            extra_a[2],
            grad_shift_b,
            grad_scale_b,
            grad_gate_b,
            extra_b[0],
            extra_b[1],
            extra_b[2],
        ]
    ).reshape(1, 12 * D)
    grad_small = jnp.concatenate(
        [grad_patch, grad_head, grad_bias[None], grad_gain_c[None], grad_gain_f[None]], 0
    )
    factors = mlp_factors_b + (
        (crossed, grad_cross),
        (cross_in, grad_query),
        factors_ob,
        factors_qkvb,
    )
    factors += mlp_factors_a + (factors_oa, factors_qkva)
    if wide_rows == 128 and deep_rows == 512:
        phases = (
            {"kind": 0, "first": 0, "lefts": (0, 1), "cols": (D, 10 * D + FF)},
            {"kind": 1, "first": 0, "lefts": (2, 3, 4, 5), "cols": (9 * D, 8 * D, 7 * D, 3 * D)},
            {"kind": 0, "first": 0, "lefts": (6, 7), "cols": (0, 10 * D)},
            {"kind": 1, "first": 2, "lefts": (8, 9), "cols": (6 * D, 0)},
        )
        used = 12 * D + grad_small.size
        vectors = jnp.concatenate(
            [grad_modul.reshape(-1), grad_small.reshape(-1), loss_part[None]]
        )
        vectors = jnp.pad(vectors, (0, 256 * 128 - vectors.shape[0])).reshape(256, 128)
        keyvals = grad_keyval.reshape(TEXT_PAD, band_count, kv_cols).transpose(1, 0, 2)
        wide_rest, deep_rest, squares, all_vectors, grad_w_ckv, kv_squares = reduce_gradients(
            phases,
            [f[0] for f in factors],
            [f[1] for f in factors],
            vectors,
            keyvals,
            all_text.reshape(clip_count * TEXT_PAD, deep_rows),
            10 * D + 2 * FF,
            2 * D,
        )
        all_vectors = all_vectors.reshape(clip_count, -1)
        all_grad_modul = all_vectors[:, : 12 * D]
        small_sum = jnp.sum(all_vectors[:, 12 * D : used], 0).reshape(grad_small.shape)
        loss_sum = jnp.sum(all_vectors[:, used])
        square_part = jnp.sum(squares) / (band_count // 2) + jnp.sum(kv_squares)
    else:
        summed = [sum_rows(*pair) for pair in factors]
        wide_rest = jnp.concatenate([summed[i] for i in (9, 5, 8, 4, 3, 2, 7, 1)], 1)
        deep_rest = jnp.concatenate([summed[6], summed[0]], 1)
        grad_keyval = lax.psum_scatter(grad_keyval, "band", scatter_dimension=1, tiled=True)
        grad_keyval = lax.all_gather(grad_keyval, "clip", axis=0, tiled=True)
        grad_w_ckv = matmul_tn(
            all_text.reshape(clip_count * TEXT_PAD, deep_rows).astype(jnp.float32),
            grad_keyval,
            lax.Precision.HIGHEST,
        )
        grad_w_ckv = lax.all_gather(grad_w_ckv, "band", axis=1, tiled=True)
        all_grad_modul = lax.all_gather(lax.psum(grad_modul, "band"), "clip", axis=0, tiled=True)
        loss_sum, small_sum = lax.psum((loss_part, grad_small), ("clip", "band"))
        square_part = sum(jnp.sum(x * x) for x in (wide_rest, deep_rest, grad_w_ckv)) / band_count
    grad_w_ada = matmul_tn(time_rows.astype(jnp.float32), all_grad_modul, lax.Precision.HIGHEST)
    wide_sum = jnp.concatenate([grad_w_ada, wide_rest], 1)
    deep_sum = jnp.concatenate([deep_rest[:, :D], grad_w_ckv, deep_rest[:, D:]], 1)
    square_part += jnp.sum(grad_w_ada * grad_w_ada) / band_count
    square_sum = total_over_devices(square_part)
    grad_norm = jnp.sqrt(square_sum + jnp.sum(small_sum * small_sum))
    factor = CLIP_MAX / jnp.maximum(grad_norm, CLIP_MAX)
    new_wide = adam_update(w_wide, m_wide, v_wide, wide_sum * factor, 0.15)
    new_deep = adam_update(w_deep, m_deep, v_deep, deep_sum * factor, 0.05)
    new_small = adam_update(w_small, m_small, v_small, small_sum * factor, 0.5)
    loss = loss_sum / global_count
    return (
        loss,
        grad_norm,
        new_wide[0],
        new_wide[1],
        new_wide[2],
        new_deep[0],
        new_deep[1],
        new_deep[2],
        new_small[0],
        new_small[1],
        new_small[2],
    )


def solution(mesh):
    in_specs = (
        P("clip", None, "band", None, None),
        P("clip", None, "band", None, None),
        P("clip"),
        P("clip"),
        P("clip", None),
        P("clip", None, None),
        P("clip", None),
        P("clip", None),
        P("clip", None),
        P("clip", None),
        P("clip", None),
        P("clip", None),
        P(),
        P(),
        P(),
    )
    out_specs = (
        P(),
        P(),
        P("clip", None),
        P("clip", None),
        P("clip", None),
        P("clip", None),
        P("clip", None),
        P("clip", None),
        P(),
        P(),
        P(),
    )
    return jax.shard_map(
        per_device, mesh=mesh, in_specs=in_specs, out_specs=out_specs, check_vma=False
    )
```

```python
from functools import partial
import math

import jax
import jax.numpy as jnp
from jax import lax
from jax.experimental import pallas as pl
from jax.experimental.pallas import tpu as pltpu
from jax.sharding import PartitionSpec as P

D = 1024
HEADS = 16
HEAD_DIM = 64
FF = 4096
CH = 8
SPACE = 16
WIN = 8
SHIFT = 4
TMAX = 1000
STEP = 10


EPS_NORM = 1e-06
CLIP_MAX = 0.001
BETA_ONE = 0.9
BETA_TWO = 0.95
ADAM_EPS = 1e-08
DECAY = 0.1


def shifted(value, axis, by):
    length = lax.axis_size(axis)
    return lax.ppermute(value, axis, [(i, (i + by) % length) for i in range(length)])


def matmul(left_op, right_op):
    return jnp.dot(left_op, right_op, preferred_element_type=jnp.float32)


def matmul_tn(left_op, right_op, precision=None):
    return lax.dot_general(
        left_op,
        right_op,
        (((0,), (0,)), ((), ())),
        precision=precision,
        preferred_element_type=jnp.float32,
    )


def matmul_nt(left_op, right_op):
    return lax.dot_general(
        left_op, right_op, (((1,), (1,)), ((), ())), preferred_element_type=jnp.float32
    )


def layer_norm(field_in):
    average = jnp.mean(field_in, -1, keepdims=True)
    centred = field_in - average
    return centred * lax.rsqrt(jnp.mean(centred * centred, -1, keepdims=True) + EPS_NORM)


def norm_modulated(field_in, shift_vec, scale_vec):
    return layer_norm(field_in) * (1.0 + scale_vec) + shift_vec


def norm_gained(field_in, gain_vec):
    return layer_norm(field_in) * gain_vec


def time_features(time_value):
    half_width = D // 2
    frequency = jnp.exp(-math.log(10000.0) * jnp.arange(half_width, dtype=jnp.float32) / half_width)
    angles = time_value[..., None] * frequency
    return jnp.concatenate([jnp.cos(angles), jnp.sin(angles)], -1)


def token_order(grid):
    frames, rows, cols, width = grid.shape
    halves = grid.reshape(frames, rows, cols // WIN, WIN, width).transpose(2, 0, 1, 3, 4)
    return halves.reshape(frames * rows * cols, width)


def with_rows(tokens, first_rows, run):
    width = tokens.shape[1]
    runs = tokens.reshape(-1, run, width)
    return jnp.concatenate([first_rows, runs[:, first_rows.shape[1] :]], 1).reshape(-1, width)


def first_rows(tokens, run, part):
    return tokens.reshape(-1, run, tokens.shape[1])[:, :part]


def attend_pieces(tokens, frames, keys):
    if keys == "frame":
        run = tokens // (2 * frames)
        return [((f * run, run), (tokens // 2 + f * run, run)) for f in range(frames)]
    if keys == "half":
        return [((half * (tokens // 2), tokens // 2),) for half in range(2)]
    return [((0, tokens),)]


def take(ref, runs):
    pieces = [ref[low : low + many, :] for low, many in runs]
    return pieces[0] if len(pieces) == 1 else jnp.concatenate(pieces, 0)


def put(ref, cols, runs, value):
    done = 0
    for low, many in runs:
        ref[low : low + many, cols] = value[done : done + many].astype(ref.dtype)
        done += many


def softmax_of(scores, axis, text_len):
    if text_len:
        place = lax.broadcasted_iota(jnp.int32, scores.shape, axis)
        scores = jnp.where(place < text_len, scores, -1e30)
    weight = jnp.exp(scores - jnp.max(scores, axis, keepdims=True))
    return weight * (1.0 / jnp.sum(weight, axis, keepdims=True))


def lanes_of(head, shape):
    lane = lax.broadcasted_iota(jnp.int32, shape, 1)
    return lane < HEAD_DIM if head == 0 else lane >= HEAD_DIM


def only(head, value):
    return jnp.where(lanes_of(head, value.shape), value, jnp.zeros_like(value))


def attention_gradients(queries, keys, values, grad_out, text_len):
    queries, grad_out = stacked(queries), stacked(grad_out)
    probs = softmax_of(matmul_nt(keys, queries), 0, text_len)
    dprobs = matmul_nt(values, grad_out)
    dv = matmul(probs.astype(jnp.bfloat16), grad_out)
    inner = jnp.sum(probs * dprobs, 0, keepdims=True)
    dscores = (probs * (dprobs - inner)).astype(jnp.bfloat16)
    dk = matmul(dscores, queries)
    return unstacked(matmul_tn(dscores, keys)) * HEAD_DIM ** (-0.5), dk, dv


def attention_values(queries, keys, values, text_len):
    probs = softmax_of(matmul_nt(stacked(queries), keys), 1, text_len)
    return unstacked(matmul(probs.astype(jnp.bfloat16), values))


def stacked(rows):
    return jnp.concatenate([only(head, rows) for head in range(2)], 0)


def unstacked(rows):
    half = rows.shape[0] // 2
    return jnp.where(lanes_of(0, (half, rows.shape[1])), rows[:half], rows[half:])


def key_sets(key_refs, runs, text_len):
    if text_len:
        return key_refs[0][...]
    pieces = [take(ref, runs) for ref in key_refs]
    return pieces[0] if len(pieces) == 1 else jnp.concatenate(pieces, 0)


def attend_kernel(windows, text_len, sets, *refs):
    q_ref, k_refs, v_refs, out_ref = refs[0], refs[1 : 1 + sets], refs[1 + sets : 1 + 2 * sets], refs[-1]
    for runs in windows:
        queries = take(q_ref, runs) * HEAD_DIM ** (-0.5)
        keys, values = key_sets(k_refs, runs, text_len), key_sets(v_refs, runs, text_len)
        put(out_ref, slice(None), runs, attention_values(queries, keys, values, text_len))


def attend_back_kernel(windows, text_len, sets, *refs):
    q_ref, k_refs, v_refs = refs[0], refs[1 : 1 + sets], refs[1 + sets : 1 + 2 * sets]
    grad_ref = refs[1 + 2 * sets]
    dq_ref = refs[2 + 2 * sets]
    own_ref = refs[3 + 2 * sets] if text_len else None
    pair = pl.program_id(0)
    cols = [pl.ds(pl.multiple_of(i * D + pair * 2 * HEAD_DIM, 128), 2 * HEAD_DIM) for i in range(3)]
    merged = dq_ref.shape[1] == 3 * D
    for runs in windows:
        queries = take(q_ref, runs) * HEAD_DIM ** (-0.5)
        keys, values = key_sets(k_refs, runs, text_len), key_sets(v_refs, runs, text_len)
        grad_out = take(grad_ref, runs)
        dq, dk, dv = attention_gradients(queries, keys, values, grad_out, text_len)
        put(dq_ref, cols[0], runs, dq)
        if merged:
            put(dq_ref, cols[1], runs, dk)
            put(dq_ref, cols[2], runs, dv)
        else:
            own_ref[:, cols[0]] = dk
            own_ref[:, cols[1]] = dv


def pair_cols(which, pair):
    return pl.ds(pl.multiple_of(which * D + pair * 2 * HEAD_DIM, 128), 2 * HEAD_DIM)


def take_cols(ref, cols, runs):
    return jnp.concatenate([ref[low : low + many, cols] for low, many in runs], 0)


def attend_frames_kernel(windows, qkv_ref, out_ref, far_ref, send, recv):
    band = lax.axis_index("band")
    partner = (lax.axis_index("clip"), band + 1 - 2 * (band % 2))
    greet([partner])

    def copies(pair):
        return [
            pltpu.make_async_remote_copy(
                qkv_ref.at[:, pair_cols(1 + i, pair)],
                far_ref.at[:, pair_cols(i, pair)],
                send.at[pair, i],
                recv.at[pair, i],
                partner,
                MESH,
            )
            for i in range(2)
        ]

    @pl.loop(0, HEADS // 2)
    def _(pair):
        for copy in copies(pair):
            copy.start()

    @pl.loop(0, HEADS // 2)
    def _(pair):
        for copy in copies(pair):
            copy.wait_recv()
        for runs in windows:
            queries = take_cols(qkv_ref, pair_cols(0, pair), runs) * HEAD_DIM ** (-0.5)
            keys, values = (
                jnp.concatenate(
                    [
                        take_cols(qkv_ref, pair_cols(1 + i, pair), runs),
                        take_cols(far_ref, pair_cols(i, pair), runs),
                    ],
                    0,
                )
                for i in range(2)
            )
            put(
                out_ref, pair_cols(0, pair), runs, attention_values(queries, keys, values, 0)
            )

    @pl.loop(0, HEADS // 2)
    def _(pair):
        for copy in copies(pair):
            copy.wait_send()


def attend_frames_back_kernel(
    windows, qkv_ref, far_ref, grad_ref, out_ref, own_buf, far_put, far_got, send, recv
):
    band = lax.axis_index("band")
    partner = (lax.axis_index("clip"), band + 1 - 2 * (band % 2))
    greet([partner])

    def copies(pair):
        return [
            pltpu.make_async_remote_copy(
                far_put.at[:, pair_cols(i, pair)],
                far_got.at[:, pair_cols(i, pair)],
                send.at[pair, i],
                recv.at[pair, i],
                partner,
                MESH,
            )
            for i in range(2)
        ]

    def merge(pair):
        for i, copy in enumerate(copies(pair)):
            copy.wait_recv()
            cols = pair_cols(i, pair)
            total = own_buf[:, cols] + far_got[:, cols]
            out_ref[:, pair_cols(1 + i, pair)] = total.astype(jnp.bfloat16)

    @pl.loop(0, HEADS // 2)
    def _(pair):
        for runs in windows:
            queries = take_cols(qkv_ref, pair_cols(0, pair), runs) * HEAD_DIM ** (-0.5)
            keys, values = (
                jnp.concatenate(
                    [
                        take_cols(qkv_ref, pair_cols(1 + i, pair), runs),
                        take_cols(far_ref, pair_cols(i, pair), runs),
                    ],
                    0,
                )
                for i in range(2)
            )
            grad_out = take_cols(grad_ref, pair_cols(0, pair), runs)
            dq, *dkv = attention_gradients(queries, keys, values, grad_out, 0)
            put(out_ref, pair_cols(0, pair), runs, dq)
            half = keys.shape[0] // 2
            for i, value in enumerate(dkv):
                put(own_buf, pair_cols(i, pair), runs, value[:half])
                put(far_put, pair_cols(i, pair), runs, value[half:])
        for copy in copies(pair):
            copy.start()

        @pl.when(pair >= 1)
        def _():
            merge(pair - 1)

    merge(HEADS // 2 - 1)

    @pl.loop(0, HEADS // 2)
    def _(pair):
        for copy in copies(pair):
            copy.wait_send()


def attend_frames(qkv, windows):
    tokens = qkv.shape[0]
    dma = pltpu.SemaphoreType.DMA((HEADS // 2, 2))
    return pl.pallas_call(
        partial(attend_frames_kernel, windows),
        out_shape=(
            jax.ShapeDtypeStruct((tokens, D), jnp.bfloat16),
            jax.ShapeDtypeStruct((tokens, 2 * D), jnp.bfloat16),
        ),
        in_specs=[IN_VMEM],
        out_specs=(IN_VMEM,) * 2,
        scratch_shapes=[dma, dma],
        compiler_params=pltpu.CompilerParams(
            collective_id=4, has_side_effects=True, vmem_limit_bytes=40 << 20
        ),
        cost_estimate=attention_cost(tokens, 256, 2),
    )(qkv)


def attend_frames_back(qkv, far_kv, grad_out, windows):
    tokens = qkv.shape[0]
    dma = pltpu.SemaphoreType.DMA((HEADS // 2, 2))
    return pl.pallas_call(
        partial(attend_frames_back_kernel, windows),
        out_shape=jax.ShapeDtypeStruct(qkv.shape, jnp.bfloat16),
        in_specs=[IN_VMEM] * 3,
        out_specs=IN_VMEM,
        scratch_shapes=[pltpu.VMEM((tokens, 2 * D), jnp.float32)] * 3 + [dma, dma],
        compiler_params=pltpu.CompilerParams(
            collective_id=5, has_side_effects=True, vmem_limit_bytes=50 << 20
        ),
        cost_estimate=attention_cost(tokens, 256, 5),
    )(qkv, far_kv, grad_out)


def head_cols(array, first):
    return array, pl.BlockSpec((array.shape[0], 2 * HEAD_DIM), lambda h: (0, first + h))


def attention_operands(queries, key_values):
    ins = [head_cols(queries, 0)]
    ins += [head_cols(array, first) for array, first, _ in key_values]
    return ins + [head_cols(array, second) for array, _, second in key_values]


def attention_cost(tokens, keys, products):
    flops = 2 * products * tokens * keys * D * 2
    return pl.CostEstimate(
        flops=flops, bytes_accessed=tokens * D * 2 * 8, transcendentals=tokens * keys * HEADS
    )


def attend(queries, key_values, windows, text_len=0):
    tokens = queries.shape[0]
    ins = attention_operands(queries, key_values)
    return pl.pallas_call(
        partial(attend_kernel, windows, text_len, len(key_values)),
        grid=(HEADS // 2,),
        in_specs=[spec for _, spec in ins],
        out_specs=pl.BlockSpec((tokens, 2 * HEAD_DIM), lambda h: (0, h)),
        out_shape=jax.ShapeDtypeStruct((tokens, D), jnp.bfloat16),
        compiler_params=pltpu.CompilerParams(vmem_limit_bytes=40 << 20),
        cost_estimate=attention_cost(tokens, 320, 2),
    )(*[array for array, _ in ins])


def attend_back(queries, key_values, grad_out, windows, text_len=0):
    tokens = queries.shape[0]
    ins = attention_operands(queries, key_values) + [head_cols(grad_out, 0)]
    sets = len(key_values)
    whole = lambda rows, cols: pl.BlockSpec((rows, cols), lambda h: (0, 0))
    if sets == 1 and not text_len:
        outs = [((tokens, 3 * D), jnp.bfloat16)]
    else:
        rows = key_values[0][0].shape[0]
        outs = [((tokens, D), jnp.bfloat16)] + [((rows, 2 * D), jnp.float32)] * sets
    return pl.pallas_call(
        partial(attend_back_kernel, windows, text_len, sets),
        grid=(HEADS // 2,),
        in_specs=[spec for _, spec in ins],
        out_specs=[whole(*shape) for shape, _ in outs],
        out_shape=[jax.ShapeDtypeStruct(*out) for out in outs],
        compiler_params=pltpu.CompilerParams(vmem_limit_bytes=50 << 20),
        cost_estimate=attention_cost(tokens, 320, 5),
    )(*[array for array, _ in ins])


def mlp_forward(stream, modul, up_weight, down_weight):
    mlp_val, norm_back = jax.vjp(norm_modulated, stream, modul[3], modul[4])
    mlp_in = mlp_val.astype(jnp.bfloat16)
    up_proj = matmul(mlp_in, up_weight)
    share = 0.5 + 0.5 * lax.erf(up_proj * math.sqrt(0.5))
    gelu_val = up_proj * share
    slope = share + up_proj * (jnp.exp(-0.5 * up_proj * up_proj) / math.sqrt(2.0 * math.pi))
    gelu_low = gelu_val.astype(jnp.bfloat16)
    down_proj = matmul(gelu_low, down_weight)
    return (stream + modul[5] * down_proj, (norm_back, mlp_in, slope, gelu_low, down_proj))


def mlp_backward(grad_stream, modul, up_weight, down_weight, saved):
    norm_back, mlp_in, slope, gelu_low, down_proj = saved
    grad_down = (modul[5] * grad_stream).astype(jnp.bfloat16)
    grad_gate = jnp.sum(grad_stream * down_proj, 0)
    grad_up = (slope * matmul_nt(grad_down, down_weight)).astype(jnp.bfloat16)
    grad_part, grad_shift, grad_scale = norm_back(matmul_nt(grad_up, up_weight))
    factors = ((gelu_low, grad_down), (mlp_in, grad_up))
    return (grad_stream + grad_part, factors, (grad_shift, grad_scale, grad_gate))


def adam_update(weight, first_mom, second_mom, grad_val, learn_rate):
    first_mom = BETA_ONE * first_mom + (1.0 - BETA_ONE) * grad_val
    second_mom = BETA_TWO * second_mom + (1.0 - BETA_TWO) * grad_val * grad_val
    first_hat = first_mom / (1.0 - BETA_ONE**STEP)
    second_hat = second_mom / (1.0 - BETA_TWO**STEP)
    weight = weight - learn_rate * (first_hat / (jnp.sqrt(second_hat) + ADAM_EPS) + DECAY * weight)
    return (weight, first_mom, second_mom)

MESH = pl.DeviceIdType.MESH
ANY = pl.BlockSpec(memory_space=pl.ANY)
IN_VMEM = pl.BlockSpec(memory_space=pltpu.VMEM)
TEXT_PAD = 80


def ring_place(clip, count):
    half = clip // 2
    odd = clip % 2
    return half + odd * (count - 1 - 2 * half)


def ring_clip(place, count):
    far = place // (count // 2)
    return (1 - far) * 2 * place + far * (2 * (count - 1 - place) + 1)


def greet(peers):
    barrier = pltpu.get_barrier_semaphore()
    for peer in peers:
        pl.semaphore_signal(barrier, inc=1, device_id=peer, device_id_type=MESH)
    pl.semaphore_wait(barrier, len(peers))


def exchange_kernel(count, facts_ref, facts_out, send, recv):
    me = lax.axis_index("clip")
    band = lax.axis_index("band")
    peers = [((me + step) % count, band) for step in range(1, count)]
    greet(peers)
    sent = [
        pltpu.make_async_remote_copy(
            facts_ref, facts_out.at[me], send.at[step], recv.at[step], peer, MESH
        )
        for step, peer in enumerate(peers)
    ]
    for copy in sent:
        copy.start()
    facts_out[me] = facts_ref[...]
    for copy in sent:
        copy.wait()


def exchange_facts(facts):
    count = lax.axis_size("clip")
    return pl.pallas_call(
        partial(exchange_kernel, count),
        out_shape=jax.ShapeDtypeStruct((count,) + facts.shape, facts.dtype),
        in_specs=[IN_VMEM],
        out_specs=IN_VMEM,
        scratch_shapes=[pltpu.SemaphoreType.DMA((count - 1,))] * 2,
        compiler_params=pltpu.CompilerParams(collective_id=0, has_side_effects=True),
    )(facts)


def gather_kernel(count, picks, sides, *refs):
    num = len(picks)
    packs, vec_ref, text_ref = refs[:2], refs[2], refs[3]
    full, (vec_out, text_out, kv_out) = refs[4 : 4 + num], refs[4 + num : 7 + num]
    refs = refs[7 + num :]
    wide, shards = refs[:num], refs[num : 2 * num]
    ring_send, ring_recv, pair_send, pair_recv, cross_send, cross_recv = refs[2 * num : 2 * num + 6]
    load_sem, own_sem, part_send, part_recv, part_own = refs[2 * num + 6 : 2 * num + 11]
    kv_wide, kv_part, kv_put, kv_got, kv_sum, kv_load, kv_send, kv_recv, band_send, band_recv = refs[
        2 * num + 11 : 2 * num + 21
    ]
    share_send, share_recv = refs[2 * num + 21 :]
    shapes = [(packs[pack].shape[0], cols) for pack, _, cols in picks]
    loads = [
        pltpu.make_async_copy(
            packs[pack].at[:, pl.ds(start, cols)], wide[group], load_sem.at[group]
        )
        for group, (pack, start, cols) in enumerate(picks)
    ]
    kv_width = kv_wide.shape[1]
    kv_first = D + lax.axis_index("band") * kv_width
    kv_weight = pltpu.make_async_copy(
        packs[1].at[:, pl.ds(pl.multiple_of(kv_first, 128), kv_width)], kv_wide, kv_load
    )
    for copy in loads + [kv_weight]:
        copy.start()
    me = lax.axis_index("clip")
    band = lax.axis_index("band")
    core = band % 2
    place = ring_place(me, count)
    onward = 1 - 2 * core
    following = (ring_clip((place + onward + count) % count, count), band)
    plane = band // 2
    partner = (me, band + 1 - 2 * core)
    mirror = (me, band + 2 - 4 * plane)
    peers = [((me + step) % count, band) for step in range(1, count)]
    band_count = 2 * D // kv_width
    band_peers = [(me, (band + step) % band_count) for step in range(1, band_count)]
    greet(peers + band_peers)

    def block(ref, group, owner):
        rows, cols = shapes[group]
        return ref.at[
            pl.ds(pl.multiple_of(owner * rows, rows), rows),
            pl.ds(pl.multiple_of(core * (cols // 2), 128), cols // 2),
        ]

    def ring_copy(group, step):
        owner = ring_clip((place - onward * step + 2 * count) % count, count)
        there = block(full[group], group, owner)
        return pltpu.make_async_remote_copy(
            there, there, ring_send.at[step, group], ring_recv.at[step, group], following, MESH
        )

    def handed(group, step, send, recv, peer):
        owner = ring_clip((place - onward * (step + 1) + 2 * count) % count, count)
        there = block(full[group], group, owner)
        return pltpu.make_async_remote_copy(
            there, there, send.at[step, group], recv.at[step, group], peer, MESH
        )

    def pair_copy(group, step):
        return handed(group, step, pair_send, pair_recv, partner)

    def cross_copy(group, step):
        return handed(group, step, cross_send, cross_recv, mirror)

    def in_ring(group):
        def decorate(body):
            if sides[group]:
                pl.when(plane == sides[group] - 1)(body)
            else:
                body()

        return decorate

    def off_ring(group, also=None):
        def decorate(body):
            if sides[group]:
                off = plane != sides[group] - 1
                pl.when(off if also is None else jnp.logical_and(off, also))(body)

        return decorate

    def ring_arrival(group, step, onto):
        ring_copy(group, step).wait_recv()
        if onto:
            ring_copy(group, step + 1).start()
        pair_copy(group, step).start()
        if sides[group]:
            cross_copy(group, step).start()

    def cross_arrival(group, step):
        cross_copy(group, step).wait_recv()
        pair_copy(group, step).start()

    def own_copy(group):
        rows, cols = shapes[group]
        return pltpu.make_async_copy(
            shards[group],
            full[group].at[pl.ds(pl.multiple_of(me * rows, rows), rows), :],
            own_sem.at[group],
        )

    parts = []
    for step, peer in enumerate(peers):
        for which, (src, dst) in enumerate(((vec_ref, vec_out), (text_ref, text_out))):
            parts.append(
                pltpu.make_async_remote_copy(
                    src.at[peer[0], band],
                    dst.at[me, band],
                    part_send.at[which, step],
                    part_recv.at[which, step],
                    peer,
                    MESH,
                )
            )
    parts_own = [
        pltpu.make_async_copy(src.at[me, band], dst.at[me, band], part_own.at[which])
        for which, (src, dst) in enumerate(((vec_ref, vec_out), (text_ref, text_out)))
    ]
    for copy in parts_own + parts:
        copy.start()
    for group in range(num):
        rows, cols = shapes[group]
        loads[group].wait()
        shards[group][...] = wide[group][...].astype(jnp.bfloat16)
        own_copy(group).start()

        @in_ring(group)
        def _(group=group, rows=rows, cols=cols):
            pltpu.make_async_remote_copy(
                shards[group].at[:, pl.ds(pl.multiple_of(core * (cols // 2), 128), cols // 2)],
                block(full[group], group, me),
                ring_send.at[0, group],
                ring_recv.at[0, group],
                following,
                MESH,
            ).start()

    def kv_copy(hop):
        return pltpu.make_async_remote_copy(
            kv_put.at[hop], kv_got.at[hop], kv_send.at[hop], kv_recv.at[hop], following, MESH
        )

    def kv_hop(hop):
        owner = ring_clip((place - onward * (hop + 1) + 2 * count) % count, count)
        total = kv_part[owner]
        if not isinstance(hop, int) or hop > 0:
            kv_copy(hop - 1).wait_recv()
            total = total + kv_got[hop - 1]
        kv_put[hop] = total
        kv_copy(hop).start()

    def band_copies():
        return [
            pltpu.make_async_remote_copy(
                kv_sum, kv_out.at[band], band_send.at[step], band_recv.at[step], peer, MESH
            )
            for step, peer in enumerate(band_peers)
        ]

    for copy in parts_own + parts:
        copy.wait()
    shares = [
        pltpu.make_async_remote_copy(
            out.at[:, band],
            out.at[:, band],
            share_send.at[which, step],
            share_recv.at[which, step],
            peer,
            MESH,
        )
        for step, peer in enumerate(band_peers)
        for which, out in enumerate((vec_out, text_out))
    ]
    for copy in shares:
        copy.start()
    kv_weight.wait()
    weight = kv_wide[...].astype(jnp.bfloat16)
    depth = weight.shape[0] // band_count
    for copy in shares:
        copy.wait()
    for owner in range(count):
        kv_part[owner] = sum(
            matmul(text_out[owner, part], weight[part * depth : (part + 1) * depth])
            for part in range(band_count)
        )
    kv_hop(0)

    @pl.loop(1, count - 1)
    def _(step):
        for group in range(num):

            @in_ring(group)
            def _(group=group):
                ring_arrival(group, step - 1, True)

        kv_hop(step)
        for group in range(num):

            @off_ring(group, step >= 2)
            def _(group=group):
                cross_arrival(group, step - 2)

    for group in range(num):

        @in_ring(group)
        def _(group=group):
            ring_arrival(group, count - 2, False)

    for late in (count - 3, count - 2):
        for group in range(num):

            @off_ring(group)
            def _(group=group, late=late):
                cross_arrival(group, late)

    kv_copy(count - 2).wait_recv()
    kv_sum[...] = (kv_part[me] + kv_got[count - 2]).astype(jnp.bfloat16)
    kv_out[band] = kv_sum[...]
    for copy in band_copies():
        copy.start()
    for group in range(num):
        own_copy(group).wait()

    @pl.loop(0, count - 1)
    def _(step):
        for group in range(num):

            @in_ring(group)
            def _(group=group):
                ring_copy(group, step).wait_send()
                if sides[group]:
                    cross_copy(group, step).wait_send()

            pair_copy(group, step).wait()
        kv_copy(step).wait_send()

    for copy in band_copies():
        copy.wait()


def gather_quarters(shard):
    band_count = lax.axis_size("band")
    rows = shard.shape[0] // band_count
    own = lax.dynamic_slice_in_dim(shard, lax.axis_index("band") * rows, rows, 0)
    return lax.all_gather(own.astype(jnp.bfloat16), ("clip", "band"), axis=0, tiled=True)


def sum_rows(left, right):
    part = lax.psum_scatter(
        matmul_tn(left, right), ("clip", "band"), scatter_dimension=0, tiled=True
    )
    return lax.all_gather(part, "band", axis=0, tiled=True)


def gather_weights(packs, picks, sides, vectors, texts):
    count, band_count = lax.axis_size("clip"), lax.axis_size("band")
    num = len(picks)
    dma = pltpu.SemaphoreType.DMA
    shapes = [(packs[pack].shape[0], cols) for pack, _, cols in picks]
    kv_shape = (texts.shape[2], 2 * D // band_count)
    kv_all = pltpu.VMEM((count,) + kv_shape, jnp.float32)
    kv_hops = pltpu.VMEM((count - 1,) + kv_shape, jnp.float32)
    out = pl.pallas_call(
        partial(gather_kernel, count, picks, sides),
        out_shape=tuple(
            jax.ShapeDtypeStruct((count * rows, cols), jnp.bfloat16) for rows, cols in shapes
        )
        + tuple(jax.ShapeDtypeStruct(v.shape, v.dtype) for v in (vectors, texts))
        + (jax.ShapeDtypeStruct((band_count,) + kv_shape, jnp.bfloat16),),
        in_specs=[ANY] * 4,
        out_specs=(ANY,) * num + (IN_VMEM,) * 3,
        scratch_shapes=[pltpu.VMEM(shape, jnp.float32) for shape in shapes]
        + [pltpu.VMEM(shape, jnp.bfloat16) for shape in shapes]
        + [dma((count - 1, num))] * 6
        + [dma((num,)), dma((num,)), dma((2, count - 1)), dma((2, count - 1)), dma((2,))]
        + [
            pltpu.VMEM((packs[1].shape[0], kv_shape[1]), jnp.float32),
            kv_all,
            kv_hops,
            kv_hops,
            pltpu.VMEM(kv_shape, jnp.bfloat16),
            dma,
            dma((count - 1,)),
            dma((count - 1,)),
            dma((band_count - 1,)),
            dma((band_count - 1,)),
            dma((2, band_count - 1)),
            dma((2, band_count - 1)),
        ],
        compiler_params=pltpu.CompilerParams(
            collective_id=1, has_side_effects=True, vmem_limit_bytes=50 << 20
        ),
        cost_estimate=pl.CostEstimate(flops=2 * 10**11, bytes_accessed=6 * 10**8, transcendentals=0),
    )(*packs, vectors, texts)
    return out[:num], out[num], out[num + 1], out[num + 2]


WIRE_MAX = 32767.0
WIRE_LEAST = 1e-30
UNIT = (128, 512)


def unit_parts(kind, first):
    if kind == 0:
        return ((0, 4, lambda u: u, lambda u: 0), (4, 4, lambda u: 4, lambda u: u - 3))
    if first:
        return ((2, 2, lambda u: u, lambda u: u), (4, 2, lambda u: 3, lambda u: u))
    return ((0, 3, lambda u: u, lambda u: u), (3, 3, lambda u: 3, lambda u: u))


def reduce_kernel(count, tokens, phases, *refs):
    num = sum(len(phase["lefts"]) for phase in phases)
    lefts, rights = refs[:num], refs[num : 2 * num]
    vec_ref, kv_ref, text_ref = refs[2 * num : 2 * num + 3]
    refs = refs[2 * num + 3 :]
    wide_out, deep_out, square_out, all_vec, kv_out, kv_square = refs[:6]
    left_far, right_far = refs[6 : 6 + num], refs[6 + num : 6 + 2 * num]
    scratch = refs[6 + 2 * num :]
    left_buf, right_buf, got_low, got_scale, put_low, put_scale, plane_put = (
        scratch[2 * i : 2 * i + 2] for i in range(7)
    )
    plane_got = scratch[14 : 14 + len(phases)]
    (
        square_buf,
        left_sem,
        right_sem,
        pair_send,
        pair_recv,
        half_send,
        half_recv,
        ring_send,
        ring_recv,
        credit,
        plane_send,
        plane_recv,
        out_sem,
        out_send,
        out_recv,
        last_put,
        last_put_scale,
        last_got,
        last_got_scale,
        push_send,
        push_recv,
        vec_got,
        kv_got,
        vec_sum,
        all_kv,
        text_buf,
        kv_grad,
        side_own,
        side_send,
        side_recv,
        vec_send,
        vec_recv,
        vec_pair_send,
        vec_pair_recv,
        kv_own,
        kv_send,
        kv_recv,
    ) = scratch[14 + len(phases) :]
    me = lax.axis_index("clip")
    band = lax.axis_index("band")
    core = band % 2
    plane = band // 2
    place = ring_place(me, count)
    onward = 1 - 2 * core
    following = (ring_clip((place + onward + count) % count, count), band)
    preceding = (ring_clip((place - onward + count) % count, count), band)
    partner = (me, band + 1 - 2 * core)
    mirror = (me, band + 2 - 4 * plane)
    band_count = vec_got.shape[0]
    band_peers = [(me, (band + step) % band_count) for step in range(1, band_count)]
    greet([following, preceding] + band_peers)

    def owner_at(step, way):
        return ring_clip((place - way * (step + 1) + 2 * count) % count, count)

    def left_blocks(at):
        phase = phases[at]
        if phase["kind"] == 0:
            return [(b, phase["lefts"][0], b, 4) for b in range(4)] + [(4, phase["lefts"][1], 0, 1)]
        first = phase["first"]
        return [(first + i, left, 0, 1) for i, left in enumerate(phase["lefts"])]

    def right_blocks(at):
        phase = phases[at]
        if phase["kind"] == 0:
            return [(0, phase["lefts"][0], 0)] + [(1 + i, phase["lefts"][1], i) for i in range(4)]
        first = phase["first"]
        return [(first + i, phase["lefts"][i], 0) for i in range(3 - first)] + [
            (3 + i, phase["lefts"][-1], i) for i in range(3)
        ]

    def left_cols(step, way, which, many):
        width = lefts_width // count if many == 1 else deep_width // count
        start = owner_at(step, way) * width + which * 128
        return pl.ds(pl.multiple_of(start, 128), 128)

    lefts_width = lefts[phases[1]["lefts"][0]].shape[1]
    deep_width = lefts[phases[0]["lefts"][0]].shape[1]

    def pair_left(at, step):
        out = []
        for block, operand, which, many in left_blocks(at):
            cols = left_cols(step, -onward, which, many)
            out.append(
                pltpu.make_async_remote_copy(
                    lefts[operand].at[:, cols],
                    left_far[operand].at[:, cols],
                    pair_send.at[at, block, step],
                    pair_recv.at[at, block, step],
                    partner,
                    MESH,
                )
            )
        return out

    def pair_right(at):
        out = []
        for i, operand in enumerate(phases[at]["lefts"]):
            half = rights[operand].shape[1] // 2
            out.append(
                pltpu.make_async_remote_copy(
                    rights[operand].at[:, pl.ds(pl.multiple_of((1 - core) * half, 128), half)],
                    right_far[operand],
                    half_send.at[operand],
                    half_recv.at[operand],
                    partner,
                    MESH,
                )
            )
        return out

    def load_left(at, step, slot, far):
        kind = phases[at]["kind"]
        out = []
        for block, operand, which, many in left_blocks(at):
            cols = left_cols(step, onward, which, many)
            source = left_far if far else lefts
            out.append(
                pltpu.make_async_copy(
                    source[operand].at[:, cols],
                    left_buf[kind].at[slot, block, pl.ds(far * tokens, tokens), :],
                    left_sem.at[kind, slot, block, far],
                )
            )
        return out

    def load_right(at, far):
        kind = phases[at]["kind"]
        out = []
        for block, operand, which in right_blocks(at):
            if far:
                source = right_far[operand].at[:, pl.ds(which * UNIT[1], UNIT[1])]
            else:
                half = rights[operand].shape[1] // 2
                start = pl.multiple_of(core * half + which * UNIT[1], 128)
                source = rights[operand].at[:, pl.ds(start, UNIT[1])]
            out.append(
                pltpu.make_async_copy(
                    source,
                    right_buf[kind].at[block, pl.ds(far * tokens, tokens), :],
                    right_sem.at[kind, block, far],
                )
            )
        return out

    def ring_copies(at, part, slot):
        kind = phases[at]["kind"]
        units = pl.ds(*unit_parts(kind, phases[at]["first"])[part][:2])
        return [
            pltpu.make_async_remote_copy(
                put.at[slot, units],
                got.at[slot, units],
                ring_send.at[kind, slot, part, i],
                ring_recv.at[kind, slot, part, i],
                following,
                MESH,
            )
            for i, (put, got) in enumerate(
                ((put_low[kind], got_low[kind]), (put_scale[kind], got_scale[kind]))
            )
        ]

    def plane_copies(at, part):
        kind = phases[at]["kind"]
        units = pl.ds(*unit_parts(kind, phases[at]["first"])[part][:2])
        pairs = ((plane_put[kind], plane_got[at]),)
        if at + 1 == len(phases):
            pairs = ((last_put, last_got), (last_put_scale, last_got_scale))
        return [
            pltpu.make_async_remote_copy(
                here.at[units],
                there.at[units],
                plane_send.at[at, part, i],
                plane_recv.at[at, part, i],
                mirror,
                MESH,
            )
            for i, (here, there) in enumerate(pairs)
        ]

    def push_right(block):
        operand, which = [entry[1:] for entry in right_blocks(0) if entry[0] == block][0]
        half = rights[operand].shape[1] // 2
        begin = pl.multiple_of((1 - core) * half + which * UNIT[1], 128)
        return pltpu.make_async_remote_copy(
            rights[operand].at[:, pl.ds(begin, UNIT[1])],
            right_buf[phases[0]["kind"]].at[block, pl.ds(tokens, tokens), :],
            push_send.at[block],
            push_recv.at[block],
            partner,
            MESH,
        )

    def out_copies(at, unit):
        phase = phases[at]
        if phase["kind"] == 0 and unit < 4:
            half = UNIT[1]
            rows = deep_out.shape[0] // 4
            there = deep_out.at[
                pl.ds(unit * rows, rows),
                pl.ds(pl.multiple_of(phase["cols"][0] + core * half, 128), half),
            ]
        else:
            which, col = (1, unit - 4) if phase["kind"] == 0 else (unit - phase["first"], 0)
            if phase["kind"] and unit >= 3:
                which, col = len(phase["lefts"]) - 1, unit - 3
            half = rights[phase["lefts"][which]].shape[1] // 2
            start = phase["cols"][which] + core * half + col * UNIT[1]
            there = wide_out.at[:, pl.ds(pl.multiple_of(start, 128), UNIT[1])]
        here = plane_got[at].at[unit]
        return (
            pltpu.make_async_copy(here, there, out_sem.at[at, unit]),
            pltpu.make_async_remote_copy(
                here, there, out_send.at[at, unit], out_recv.at[at, unit], partner, MESH
            ),
        )

    def product(kind, slot, left, right):
        return lax.dot_general(
            left_buf[kind][slot, left],
            right_buf[kind][right],
            (((0,), (0,)), ((), ())),
            preferred_element_type=jnp.float32,
        )

    def start(copies):
        for copy in copies:
            copy.start()

    def finish(copies):
        for copy in copies:
            copy.wait()

    def take_step(at, step, first, last):
        phase = phases[at]
        kind = phase["kind"]
        slot = step % 2
        before = (step + 1) % 2
        for far in range(2):
            finish(load_left(at, step, slot, far))

        def load_next():
            for copy in pair_left(at, step + 1):
                copy.wait_recv()
            for far in range(2):
                start(load_left(at, step + 1, before, far))

        opening = first and at == 0
        if not (last or opening):
            load_next()
        parts = unit_parts(kind, phase["first"])

        def encode(term):
            largest = jnp.maximum(jnp.max(jnp.abs(term), axis=0, keepdims=True), WIRE_LEAST)
            low = jnp.round(term * (WIRE_MAX / largest)).astype(jnp.int16)
            return low, largest * (1.0 / WIRE_MAX)

        for part, (low, many, left_of, right_of) in enumerate(parts):
            if opening:
                blocks = range(1) if part == 0 else range(1, 5)
                finish(load_right(0, 0)[blocks.start : blocks.stop])
                for block in blocks:
                    push_right(block).wait_recv()
            if not first:
                for copy in ring_copies(at, part, before):
                    copy.wait_recv()
            if not (first or last):

                @pl.when(step >= 2)
                def _(part=part):
                    for copy in ring_copies(at, part, slot):
                        copy.wait_send()
                    pl.semaphore_wait(credit.at[kind, part], 1)

            def settle(position, unit, term):
                if not first:
                    came = got_low[kind][before, position].astype(jnp.float32)
                    term = term + came * got_scale[kind][before, position]
                if last and at + 1 == len(phases):
                    last_put[unit], last_put_scale[unit] = encode(term)
                elif last:
                    plane_put[kind][unit] = term
                else:
                    low_part, scale_part = encode(term)
                    put_low[kind][slot, position] = low_part
                    put_scale[kind][slot, position] = scale_part

            @pl.loop(low, low + many)
            def _(unit, left_of=left_of, right_of=right_of):
                settle(unit, unit, product(kind, slot, left_of(unit), right_of(unit)))

            if last:
                start(plane_copies(at, part))
            else:
                start(ring_copies(at, part, slot))
            if not (first or last):

                @pl.when(step < count - 2)
                def _(part=part):
                    pl.semaphore_signal(
                        credit.at[kind, part], inc=1, device_id=preceding, device_id_type=MESH
                    )

        if opening:
            load_next()

    def close(at):
        kind = phases[at]["kind"]

        def add_square(total):
            square_buf[...] += jnp.sum((total * total).reshape(UNIT[0] // 8, 8, UNIT[1]), axis=0)

        for part, (low, many, _, _) in enumerate(unit_parts(kind, phases[at]["first"])):
            finish(plane_copies(at, part))

            @pl.loop(low, low + many)
            def _(unit):
                if at + 1 == len(phases):
                    total = last_put[unit].astype(jnp.float32) * last_put_scale[unit]
                    total += last_got[unit].astype(jnp.float32) * last_got_scale[unit]
                else:
                    total = plane_put[kind][unit] + plane_got[at][unit]
                plane_got[at][unit] = total
                add_square(total)

            for unit in range(low, low + many):
                start(out_copies(at, unit))

    half_rows = pl.ds(pl.multiple_of(core * (vec_sum.shape[0] // 2), 8), vec_sum.shape[0] // 2)
    side_local = [
        pltpu.make_async_copy(vec_ref, vec_got.at[band], side_own.at[0]),
        pltpu.make_async_copy(kv_ref.at[band], kv_got.at[band], side_own.at[1]),
        pltpu.make_async_copy(text_ref, text_buf, side_own.at[2]),
    ]
    side_remote = []
    for step, peer in enumerate(band_peers):
        side_remote += [
            pltpu.make_async_remote_copy(
                vec_ref, vec_got.at[band], side_send.at[0, step], side_recv.at[0, step], peer, MESH
            ),
            pltpu.make_async_remote_copy(
                kv_ref.at[peer[1]],
                kv_got.at[band],
                side_send.at[1, step],
                side_recv.at[1, step],
                peer,
                MESH,
            ),
        ]
    vec_own = pltpu.make_async_copy(vec_sum, all_vec.at[me], side_own.at[3])

    def vec_copies(step):
        owner = ring_clip((place - onward * step + 2 * count) % count, count)
        vec = all_vec.at[owner, half_rows]
        return [
            pltpu.make_async_remote_copy(
                here, there, vec_send.at[step, i], vec_recv.at[step, i], following, MESH
            )
            for i, (here, there) in enumerate(((vec, vec), (all_kv.at[owner], all_kv.at[owner])))
        ]

    def vec_first():
        vec = all_vec.at[me, half_rows]
        return [
            pltpu.make_async_remote_copy(
                here, there, vec_send.at[0, i], vec_recv.at[0, i], following, MESH
            )
            for i, (here, there) in enumerate(
                ((vec_sum.at[half_rows], vec), (all_kv.at[me], all_kv.at[me]))
            )
        ]

    def vec_pair(step):
        owner = ring_clip((place - onward * (step + 1) + 2 * count) % count, count)
        vec = all_vec.at[owner, half_rows]
        return pltpu.make_async_remote_copy(
            vec, vec, vec_pair_send.at[step], vec_pair_recv.at[step], partner, MESH
        )

    kv_width = kv_grad.shape[1]

    def kv_place(owner):
        return kv_out.at[:, pl.ds(pl.multiple_of(owner * kv_width, 128), kv_width)]

    def kv_copy(i):
        if i == 2:
            return pltpu.make_async_copy(kv_grad, kv_place(band), kv_own)
        peer = (partner, mirror)[i]
        return pltpu.make_async_remote_copy(
            kv_grad, kv_place(band), kv_send.at[i], kv_recv.at[i], peer, MESH
        )

    def kv_passed():
        there = kv_place(mirror[1])
        return pltpu.make_async_remote_copy(
            there, there, kv_send.at[2], kv_recv.at[2], partner, MESH
        )

    def sum_bands():
        finish(side_local + side_remote)
        vec_sum[...] = jnp.sum(vec_got[...], 0)
        all_kv[me] = jnp.sum(kv_got[...], 0)
        vec_own.start()
        start(vec_first())

    def pass_sums(step):
        for copy in vec_copies(step - 1):
            copy.wait_recv()
        start(vec_copies(step))
        vec_pair(step - 1).start()

    def multiply_text():
        for copy in vec_copies(count - 2):
            copy.wait_recv()
        vec_pair(count - 2).start()
        grads = all_kv[...].reshape(text_buf.shape[0], -1)
        total = jnp.zeros_like(kv_grad)
        for _ in range(3):
            part = grads.astype(jnp.bfloat16)
            grads = grads - part.astype(jnp.float32)
            total = total + matmul_tn(text_buf[...], part)
        kv_grad[...] = total
        kv_square[...] = jnp.sum((total * total).reshape(-1, 8, total.shape[1]), axis=0)
        start([kv_copy(i) for i in range(3)])

    square_buf[...] = jnp.zeros_like(square_buf)
    start(side_local + side_remote)
    start(load_right(0, 0))
    start(load_left(0, 0, 0, 0))
    push_right(0).start()
    start(pair_left(0, 0))
    for block in range(1, 5):
        push_right(block).start()

    @pl.loop(1, count)
    def _(step):
        start(pair_left(0, step))

    for copy in pair_left(0, 0):
        copy.wait_recv()
    start(load_left(0, 0, 0, 1))
    take_step(0, 0, True, False)
    for at in range(len(phases)):
        more = at + 1 < len(phases)
        if more:
            start(pair_right(at + 1))
            start(load_right(at + 1, 0))
            start(pair_left(at + 1, 0))
        if at == 1:
            sum_bands()

        @pl.loop(1, count - 1)
        def _(step, at=at, more=more):
            take_step(at, step, False, False)
            if at == 1:
                pass_sums(step)
            if more:
                start(pair_left(at + 1, step))

                @pl.when(step == count // 2)
                def _():
                    for copy in pair_right(at + 1):
                        copy.wait_recv()
                    start(load_right(at + 1, 1))
                    for copy in pair_left(at + 1, 0):
                        copy.wait_recv()
                    for far in range(2):
                        start(load_left(at + 1, 0, 0, far))

        if more:
            start(pair_left(at + 1, count - 1))
            for far in range(2):
                finish(load_right(at + 1, far))
            take_step(at + 1, 0, True, False)
        take_step(at, count - 1, False, True)
        if at == 1:
            multiply_text()
        for part in range(2):
            for slot in range(2):
                for copy in ring_copies(at, part, slot):
                    copy.wait_send()
        if at == 2:
            kv_copy(1).wait_recv()
            kv_passed().start()
        if at:
            close(at - 1)
    close(len(phases) - 1)
    vec_own.wait()
    kv_passed().wait()
    kv_copy(0).wait()
    kv_copy(1).wait_send()
    kv_copy(2).wait()

    @pl.loop(0, count - 1)
    def _(step):
        for copy in vec_copies(step):
            copy.wait_send()
        vec_pair(step).wait()

    square_out[...] = square_buf[...]
    for at, phase in enumerate(phases):
        for copy in pair_right(at) if at else [push_right(block) for block in range(5)]:
            copy.wait_send()

        @pl.loop(0, count)
        def _(step, at=at):
            for copy in pair_left(at, step):
                copy.wait_send()

        for unit in range(phase["first"], 8 if phase["kind"] == 0 else 6):
            finish(out_copies(at, unit))


def reduce_gradients(phases, lefts, rights, vectors, keyvals, text, wide_cols, deep_cols):
    count = lax.axis_size("clip")
    tokens = lefts[0].shape[0]
    wide_rows = lefts[1].shape[1] // count
    deep_rows = lefts[0].shape[1] // count
    band_count, _, kv_cols = keyvals.shape
    num = len(lefts)
    dma = pltpu.SemaphoreType.DMA
    units, lefts_of, rights_of = (8, 6), (5, 4), (5, 6)
    scratch = [pltpu.VMEM((2, lefts_of[k], 2 * tokens, 128), jnp.bfloat16) for k in range(2)]
    scratch += [pltpu.VMEM((rights_of[k], 2 * tokens, UNIT[1]), jnp.bfloat16) for k in range(2)]
    for _ in range(2):
        scratch += [pltpu.VMEM((2, units[k]) + UNIT, jnp.int16) for k in range(2)]
        scratch += [pltpu.VMEM((2, units[k], 1, UNIT[1]), jnp.float32) for k in range(2)]
    scratch += [pltpu.VMEM((units[k],) + UNIT, jnp.float32) for k in range(2)]
    scratch += [pltpu.VMEM((units[p["kind"]],) + UNIT, jnp.float32) for p in phases]
    scratch += [
        pltpu.VMEM((8, UNIT[1]), jnp.float32),
        dma((2, 2, 5, 2)),
        dma((2, 6, 2)),
        dma((len(phases), 5, count)),
        dma((len(phases), 5, count)),
        dma((num,)),
        dma((num,)),
        dma((2, 2, 2, 2)),
        dma((2, 2, 2, 2)),
        pltpu.SemaphoreType.REGULAR((2, 2)),
        dma((len(phases), 2, 2)),
        dma((len(phases), 2, 2)),
        dma((len(phases), 8)),
        dma((len(phases), 8)),
        dma((len(phases), 8)),
    ]
    for _ in range(2):
        scratch += [pltpu.VMEM((6,) + UNIT, jnp.int16), pltpu.VMEM((6, 1, UNIT[1]), jnp.float32)]
    scratch += [
        dma((5,)),
        dma((5,)),
        pltpu.VMEM((band_count,) + vectors.shape, jnp.float32),
        pltpu.VMEM(keyvals.shape, jnp.float32),
        pltpu.VMEM(vectors.shape, jnp.float32),
        pltpu.VMEM((count,) + keyvals.shape[1:], jnp.float32),
        pltpu.VMEM(text.shape, jnp.bfloat16),
        pltpu.VMEM((text.shape[1], kv_cols), jnp.float32),
        dma((4,)),
        dma((2, band_count - 1)),
        dma((2, band_count - 1)),
        dma((count - 1, 2)),
        dma((count - 1, 2)),
        dma((count - 1,)),
        dma((count - 1,)),
        dma,
        dma((3,)),
        dma((3,)),
    ]
    out = pl.pallas_call(
        partial(reduce_kernel, count, tokens, phases),
        out_shape=(
            jax.ShapeDtypeStruct((wide_rows, wide_cols), jnp.float32),
            jax.ShapeDtypeStruct((deep_rows, deep_cols), jnp.float32),
            jax.ShapeDtypeStruct((8, UNIT[1]), jnp.float32),
            jax.ShapeDtypeStruct((count,) + vectors.shape, jnp.float32),
            jax.ShapeDtypeStruct((deep_rows, band_count * kv_cols), jnp.float32),
            jax.ShapeDtypeStruct((8, kv_cols), jnp.float32),
        )
        + tuple(jax.ShapeDtypeStruct(x.shape, x.dtype) for x in lefts)
        + tuple(jax.ShapeDtypeStruct((tokens, x.shape[1] // 2), x.dtype) for x in rights),
        in_specs=[ANY] * (2 * num + 3),
        out_specs=(ANY, ANY, IN_VMEM, ANY, ANY, IN_VMEM) + (ANY,) * (2 * num),
        scratch_shapes=scratch,
        compiler_params=pltpu.CompilerParams(
            collective_id=2, has_side_effects=True, vmem_limit_bytes=58 << 20
        ),
        cost_estimate=pl.CostEstimate(flops=3 * 10**11, bytes_accessed=8 * 10**8, transcendentals=0),
    )(*lefts, *rights, vectors, keyvals, text)
    return out[:6]


def total_kernel(count, part_ref, out_ref, mid, band_got, clip_got, *sems):
    me = lax.axis_index("clip")
    band = lax.axis_index("band")
    band_count = band_got.shape[0]
    band_peers = [(me, (band + step) % band_count) for step in range(1, band_count)]
    clip_peers = [((me + step) % count, band) for step in range(1, count)]
    greet(band_peers + clip_peers)
    stages = (
        (part_ref, band_got, band, band_peers, mid, sems[:2]),
        (mid, clip_got, me, clip_peers, out_ref, sems[2:]),
    )
    for value, got, index, peers, result, (send, recv) in stages:
        copies = [
            pltpu.make_async_remote_copy(
                value, got.at[index], send.at[step], recv.at[step], peer, MESH
            )
            for step, peer in enumerate(peers)
        ]
        for copy in copies:
            copy.start()
        got[index] = value[...]
        for copy in copies:
            copy.wait()
        result[...] = jnp.sum(got[...], 0)


def total_over_devices(value):
    count, band_count = lax.axis_size("clip"), lax.axis_size("band")
    dma = pltpu.SemaphoreType.DMA
    tile = (8, 128)
    return pl.pallas_call(
        partial(total_kernel, count),
        out_shape=jax.ShapeDtypeStruct(tile, jnp.float32),
        in_specs=[IN_VMEM],
        out_specs=IN_VMEM,
        scratch_shapes=[
            pltpu.VMEM(tile, jnp.float32),
            pltpu.VMEM((band_count,) + tile, jnp.float32),
            pltpu.VMEM((count,) + tile, jnp.float32),
            dma((band_count - 1,)),
            dma((band_count - 1,)),
            dma((count - 1,)),
            dma((count - 1,)),
        ],
        compiler_params=pltpu.CompilerParams(collective_id=3, has_side_effects=True),
    )(jnp.broadcast_to(value, tile))[0, 0]


def per_device(
    latents,
    noise_field,
    timesteps,
    null_flags,
    frame_mask,
    context,
    w_wide,
    m_wide,
    v_wide,
    w_deep,
    m_deep,
    v_deep,
    w_small,
    m_small,
    v_small,
):
    clip_count = lax.axis_size("clip")
    band_count = lax.axis_size("band")
    clip_at = lax.axis_index("clip")
    band_at = lax.axis_index("band")
    wide_rows = w_wide.shape[0]
    deep_rows = w_deep.shape[0]
    text_len, text_dim = context.shape[1:]
    facts = jnp.pad(
        jnp.concatenate([timesteps, frame_mask[0]])[None],
        ((0, 7), (0, 127 - frame_mask.shape[1])),
    )
    kept_text = context[0] * (1 - null_flags[0]).astype(jnp.bfloat16)
    text_cols = jnp.pad(
        kept_text.reshape(text_len, clip_count, band_count, -1).transpose(1, 2, 0, 3),
        ((0, 0), (0, 0), (0, TEXT_PAD - text_len), (0, 0)),
    )
    all_facts = exchange_facts(facts)
    all_times = all_facts[:, 0, 0].astype(jnp.float32)
    all_time_low = jax.nn.silu(time_features(all_times)).astype(jnp.bfloat16)
    time_rows = lax.dynamic_slice(
        all_time_low, (0, clip_at * wide_rows), (clip_count, wide_rows)
    )
    part_modul = matmul(time_rows, w_wide[:, : 12 * D].astype(jnp.bfloat16))
    kv_cols = 2 * D // band_count
    up_b_w = gather_quarters(w_wide[:, 22 * D + FF :])
    gathered, all_modul, all_text, keyval = gather_weights(
        (w_wide, w_deep),
        (
            (0, 22 * D, FF),
            (1, 0, D),
            (0, 18 * D, D),
            (0, 19 * D, D),
            (0, 20 * D, D),
            (0, 21 * D, D),
            (0, 12 * D, 3 * D),
            (0, 15 * D, 3 * D),
        ),
        (1, 2, 1, 2, 1, 2, 0, 0),
        part_modul.reshape(clip_count, band_count, -1, 128),
        text_cols,
    )
    up_a_w, down_a_w, out_a_w, out_b_w, query_w, cross_out_w, qkv_a_w, qkv_b_w = gathered
    all_text = all_text.transpose(0, 2, 1, 3)
    keyval = keyval.transpose(1, 0, 2).reshape(TEXT_PAD, 2 * D)
    late_down_b, all_modul = lax.optimization_barrier((w_deep[:, 3 * D :], all_modul))
    down_b_w = gather_quarters(late_down_b)
    small_low = w_small.astype(jnp.bfloat16)
    small_val = small_low.astype(jnp.float32)
    num_frames, num_rows, num_cols = (latents.shape[1], latents.shape[2], latents.shape[3])
    tok_count = num_frames * num_rows * num_cols
    all_mask = all_facts[:, 0, 1 : 1 + num_frames]
    global_count = jnp.sum(all_mask).astype(jnp.float32) * (num_rows * num_cols * CH * band_count)
    time_value = timesteps[0].astype(jnp.float32)
    noise_angle = 0.5 * math.pi * time_value / TMAX
    signal, spread = (jnp.cos(noise_angle), jnp.sin(noise_angle))
    clean_tok = token_order(latents[0])
    noise_tok = token_order(noise_field[0])
    run = num_rows * WIN
    part = SHIFT * WIN
    frame_windows = attend_pieces(tok_count, num_frames, "frame")
    half_windows = attend_pieces(tok_count, num_frames, "half")
    text_windows = attend_pieces(tok_count, num_frames, "text")
    noisy_low = (signal * clean_tok + spread * noise_tok).astype(jnp.bfloat16)
    target = signal * noise_tok - spread * clean_tok
    modulation = jnp.sum(all_modul, 0).reshape(12, D)
    mod_a, mod_b = (modulation[:6], modulation[6:])
    stream_zero = matmul(noisy_low, small_low[:CH]) + small_val[2 * CH]
    normed_a, back_a = jax.vjp(norm_modulated, stream_zero, mod_a[0], mod_a[1])
    in_a = normed_a.astype(jnp.bfloat16)
    qkv_a = matmul(in_a, qkv_a_w).astype(jnp.bfloat16)
    att_a, far_kv = attend_frames(qkv_a, frame_windows)
    proj_a = matmul(att_a, out_a_w)
    stream_one = stream_zero + mod_a[2] * proj_a
    stream_two, saved_a = mlp_forward(stream_one, mod_a, up_a_w, down_a_w)
    normed_b, back_b = jax.vjp(norm_modulated, stream_two, mod_b[0], mod_b[1])
    low_b = normed_b.astype(jnp.bfloat16)
    rolled = with_rows(low_b, shifted(first_rows(low_b, run, part), "band", -1), run)
    qkv_b = matmul(rolled, qkv_b_w).astype(jnp.bfloat16)
    win_kv = [(qkv_b, HEADS // 2, HEADS)]
    win_out = attend(qkv_b, win_kv, half_windows)
    att_b = with_rows(win_out, shifted(first_rows(win_out, run, part), "band", 1), run)
    proj_b = matmul(att_b, out_b_w)
    stream_three = stream_two + mod_b[2] * proj_b
    cross_val, cross_back = jax.vjp(norm_gained, stream_three, small_val[2 * CH + 1])
    cross_in = cross_val.astype(jnp.bfloat16)
    query_proj = matmul(cross_in, query_w).astype(jnp.bfloat16)
    text_kv = [(keyval, 0, HEADS // 2)]
    crossed = attend(query_proj, text_kv, text_windows, text_len)
    stream_four = stream_three + matmul(crossed, cross_out_w)
    stream_five, saved_b = mlp_forward(stream_four, mod_b, up_b_w, down_b_w)
    final_val, final_back = jax.vjp(norm_gained, stream_five, small_val[2 * CH + 2])
    final_low = final_val.astype(jnp.bfloat16)
    head_low = small_low[CH : 2 * CH]
    predicted = matmul_nt(final_low, head_low)
    weight_row = jnp.repeat(frame_mask[0].astype(jnp.float32), run)
    weight_row = jnp.tile(weight_row, num_cols // WIN)[:, None]
    pred_error = predicted - target
    loss_part = jnp.sum(weight_row * pred_error * pred_error)
    grad_pred = (weight_row * pred_error * (2.0 / global_count)).astype(jnp.bfloat16)
    grad_head = matmul_tn(grad_pred, final_low)
    grad_stream, grad_gain_f = final_back(matmul(grad_pred, head_low))
    grad_stream, mlp_factors_b, extra_b = mlp_backward(
        grad_stream, mod_b, up_b_w, down_b_w, saved_b
    )
    grad_cross = grad_stream.astype(jnp.bfloat16)
    grad_crossed = matmul_nt(grad_cross, cross_out_w).astype(jnp.bfloat16)
    grad_query, grad_keyval = attend_back(
        query_proj, text_kv, grad_crossed, text_windows, text_len
    )
    grad_part, grad_gain_c = cross_back(matmul_nt(grad_query, query_w))
    grad_stream = grad_stream + grad_part
    grad_proj = (mod_b[2] * grad_stream).astype(jnp.bfloat16)
    grad_gate_b = jnp.sum(grad_stream * proj_b, 0)
    factors_ob = (att_b, grad_proj)
    grad_att = matmul_nt(grad_proj, out_b_w).astype(jnp.bfloat16)
    grad_win = with_rows(grad_att, shifted(first_rows(grad_att, run, part), "band", -1), run)
    grad_qkv = attend_back(qkv_b, win_kv, grad_win, half_windows)[0]
    factors_qkvb = (rolled, grad_qkv)
    grad_in_roll = matmul_nt(grad_qkv, qkv_b_w)
    sent_back = shifted(first_rows(grad_in_roll, run, part), "band", 1)
    grad_normed = with_rows(grad_in_roll, sent_back, run)
    grad_part, grad_shift_b, grad_scale_b = back_b(grad_normed)
    grad_stream = grad_stream + grad_part
    grad_stream, mlp_factors_a, extra_a = mlp_backward(
        grad_stream, mod_a, up_a_w, down_a_w, saved_a
    )
    grad_proj = (mod_a[2] * grad_stream).astype(jnp.bfloat16)
    grad_gate_a = jnp.sum(grad_stream * proj_a, 0)
    factors_oa = (att_a, grad_proj)
    grad_att = matmul_nt(grad_proj, out_a_w).astype(jnp.bfloat16)
    grad_qkv = attend_frames_back(qkv_a, far_kv, grad_att, frame_windows)
    factors_qkva = (in_a, grad_qkv)
    grad_part, grad_shift_a, grad_scale_a = back_a(matmul_nt(grad_qkv, qkv_a_w))
    grad_stream = grad_stream + grad_part
    grad_patch = matmul_tn(noisy_low.astype(jnp.float32), grad_stream, lax.Precision.HIGHEST)
    grad_bias = jnp.sum(grad_stream, 0)
    grad_modul = jnp.stack(
        [
            grad_shift_a,
            grad_scale_a,
            grad_gate_a,
            extra_a[0],
            extra_a[1],
            extra_a[2],
            grad_shift_b,
            grad_scale_b,
            grad_gate_b,
            extra_b[0],
            extra_b[1],
            extra_b[2],
        ]
    ).reshape(1, 12 * D)
    grad_small = jnp.concatenate(
        [grad_patch, grad_head, grad_bias[None], grad_gain_c[None], grad_gain_f[None]], 0
    )
    factors = mlp_factors_b + (
        (crossed, grad_cross),
        (cross_in, grad_query),
        factors_ob,
        factors_qkvb,
    )
    factors += mlp_factors_a + (factors_oa, factors_qkva)
    if wide_rows == 128 and deep_rows == 512:
        phases = (
            {"kind": 0, "first": 0, "lefts": (0, 1), "cols": (D, 10 * D + FF)},
            {"kind": 1, "first": 0, "lefts": (2, 3, 4, 5), "cols": (9 * D, 8 * D, 7 * D, 3 * D)},
            {"kind": 0, "first": 0, "lefts": (6, 7), "cols": (0, 10 * D)},
            {"kind": 1, "first": 2, "lefts": (8, 9), "cols": (6 * D, 0)},
        )
        used = 12 * D + grad_small.size
        vectors = jnp.concatenate(
            [grad_modul.reshape(-1), grad_small.reshape(-1), loss_part[None]]
        )
        vectors = jnp.pad(vectors, (0, 256 * 128 - vectors.shape[0])).reshape(256, 128)
        keyvals = grad_keyval.reshape(TEXT_PAD, band_count, kv_cols).transpose(1, 0, 2)
        wide_rest, deep_rest, squares, all_vectors, grad_w_ckv, kv_squares = reduce_gradients(
            phases,
            [f[0] for f in factors],
            [f[1] for f in factors],
            vectors,
            keyvals,
            all_text.reshape(clip_count * TEXT_PAD, deep_rows),
            10 * D + 2 * FF,
            2 * D,
        )
        all_vectors = all_vectors.reshape(clip_count, -1)
        all_grad_modul = all_vectors[:, : 12 * D]
        small_sum = jnp.sum(all_vectors[:, 12 * D : used], 0).reshape(grad_small.shape)
        loss_sum = jnp.sum(all_vectors[:, used])
        square_part = jnp.sum(squares) / (band_count // 2) + jnp.sum(kv_squares)
    else:
        summed = [sum_rows(*pair) for pair in factors]
        wide_rest = jnp.concatenate([summed[i] for i in (9, 5, 8, 4, 3, 2, 7, 1)], 1)
        deep_rest = jnp.concatenate([summed[6], summed[0]], 1)
        grad_keyval = lax.psum_scatter(grad_keyval, "band", scatter_dimension=1, tiled=True)
        grad_keyval = lax.all_gather(grad_keyval, "clip", axis=0, tiled=True)
        grad_w_ckv = matmul_tn(
            all_text.reshape(clip_count * TEXT_PAD, deep_rows).astype(jnp.float32),
            grad_keyval,
            lax.Precision.HIGHEST,
        )
        grad_w_ckv = lax.all_gather(grad_w_ckv, "band", axis=1, tiled=True)
        all_grad_modul = lax.all_gather(lax.psum(grad_modul, "band"), "clip", axis=0, tiled=True)
        loss_sum, small_sum = lax.psum((loss_part, grad_small), ("clip", "band"))
        square_part = sum(jnp.sum(x * x) for x in (wide_rest, deep_rest, grad_w_ckv)) / band_count
    grad_w_ada = matmul_tn(time_rows.astype(jnp.float32), all_grad_modul, lax.Precision.HIGHEST)
    wide_sum = jnp.concatenate([grad_w_ada, wide_rest], 1)
    deep_sum = jnp.concatenate([deep_rest[:, :D], grad_w_ckv, deep_rest[:, D:]], 1)
    square_part += jnp.sum(grad_w_ada * grad_w_ada) / band_count
    square_sum = total_over_devices(square_part)
    grad_norm = jnp.sqrt(square_sum + jnp.sum(small_sum * small_sum))
    factor = CLIP_MAX / jnp.maximum(grad_norm, CLIP_MAX)
    new_wide = adam_update(w_wide, m_wide, v_wide, wide_sum * factor, 0.15)
    new_deep = adam_update(w_deep, m_deep, v_deep, deep_sum * factor, 0.05)
    new_small = adam_update(w_small, m_small, v_small, small_sum * factor, 0.5)
    loss = loss_sum / global_count
    return (
        loss,
        grad_norm,
        new_wide[0],
        new_wide[1],
        new_wide[2],
        new_deep[0],
        new_deep[1],
        new_deep[2],
        new_small[0],
        new_small[1],
        new_small[2],
    )


def solution(mesh):
    in_specs = (
        P("clip", None, "band", None, None),
        P("clip", None, "band", None, None),
        P("clip"),
        P("clip"),
        P("clip", None),
        P("clip", None, None),
        P("clip", None),
        P("clip", None),
        P("clip", None),
        P("clip", None),
        P("clip", None),
        P("clip", None),
        P(),
        P(),
        P(),
    )
    out_specs = (
        P(),
        P(),
        P("clip", None),
        P("clip", None),
        P("clip", None),
        P("clip", None),
        P("clip", None),
        P("clip", None),
        P(),
        P(),
        P(),
    )
    return jax.shard_map(
        per_device, mesh=mesh, in_specs=in_specs, out_specs=out_specs, check_vma=False
    )
```

```python
from functools import partial
import math

import jax
import jax.numpy as jnp
from jax import lax
from jax.experimental import pallas as pl
from jax.experimental.pallas import tpu as pltpu
from jax.sharding import PartitionSpec as P

D = 1024
HEADS = 16
HEAD_DIM = 64
FF = 4096
CH = 8
SPACE = 16
WIN = 8
SHIFT = 4
TMAX = 1000
STEP = 10


EPS_NORM = 1e-06
CLIP_MAX = 0.001
BETA_ONE = 0.9
BETA_TWO = 0.95
ADAM_EPS = 1e-08
DECAY = 0.1


def shifted(value, axis, by):
    length = lax.axis_size(axis)
    return lax.ppermute(value, axis, [(i, (i + by) % length) for i in range(length)])


def matmul(left_op, right_op):
    return jnp.dot(left_op, right_op, preferred_element_type=jnp.float32)


def matmul_tn(left_op, right_op, precision=None):
    return lax.dot_general(
        left_op,
        right_op,
        (((0,), (0,)), ((), ())),
        precision=precision,
        preferred_element_type=jnp.float32,
    )


def matmul_nt(left_op, right_op):
    return lax.dot_general(
        left_op, right_op, (((1,), (1,)), ((), ())), preferred_element_type=jnp.float32
    )


def layer_norm(field_in):
    average = jnp.mean(field_in, -1, keepdims=True)
    centred = field_in - average
    return centred * lax.rsqrt(jnp.mean(centred * centred, -1, keepdims=True) + EPS_NORM)


def norm_modulated(field_in, shift_vec, scale_vec):
    return layer_norm(field_in) * (1.0 + scale_vec) + shift_vec


def norm_gained(field_in, gain_vec):
    return layer_norm(field_in) * gain_vec


def time_features(time_value):
    half_width = D // 2
    frequency = jnp.exp(-math.log(10000.0) * jnp.arange(half_width, dtype=jnp.float32) / half_width)
    angles = time_value[..., None] * frequency
    return jnp.concatenate([jnp.cos(angles), jnp.sin(angles)], -1)


def token_order(grid):
    frames, rows, cols, width = grid.shape
    halves = grid.reshape(frames, rows, cols // WIN, WIN, width).transpose(2, 0, 1, 3, 4)
    return halves.reshape(frames * rows * cols, width)


def with_rows(tokens, first_rows, run):
    width = tokens.shape[1]
    runs = tokens.reshape(-1, run, width)
    return jnp.concatenate([first_rows, runs[:, first_rows.shape[1] :]], 1).reshape(-1, width)


def first_rows(tokens, run, part):
    return tokens.reshape(-1, run, tokens.shape[1])[:, :part]


def attend_pieces(tokens, frames, keys):
    if keys == "frame":
        run = tokens // (2 * frames)
        return [((f * run, run), (tokens // 2 + f * run, run)) for f in range(frames)]
    if keys == "half":
        return [((half * (tokens // 2), tokens // 2),) for half in range(2)]
    return [((0, tokens),)]


def take(ref, runs):
    pieces = [ref[low : low + many, :] for low, many in runs]
    return pieces[0] if len(pieces) == 1 else jnp.concatenate(pieces, 0)


def put(ref, cols, runs, value):
    done = 0
    for low, many in runs:
        ref[low : low + many, cols] = value[done : done + many].astype(ref.dtype)
        done += many


def softmax_of(scores, axis, text_len):
    if text_len:
        place = lax.broadcasted_iota(jnp.int32, scores.shape, axis)
        scores = jnp.where(place < text_len, scores, -1e30)
    weight = jnp.exp(scores - jnp.max(scores, axis, keepdims=True))
    return weight * (1.0 / jnp.sum(weight, axis, keepdims=True))


def lanes_of(head, shape):
    lane = lax.broadcasted_iota(jnp.int32, shape, 1)
    return lane < HEAD_DIM if head == 0 else lane >= HEAD_DIM


def only(head, value):
    return jnp.where(lanes_of(head, value.shape), value, jnp.zeros_like(value))


def attention_gradients(queries, keys, values, grad_out, text_len):
    queries, grad_out = stacked(queries), stacked(grad_out)
    probs = softmax_of(matmul_nt(keys, queries), 0, text_len)
    dprobs = matmul_nt(values, grad_out)
    dv = matmul(probs.astype(jnp.bfloat16), grad_out)
    inner = jnp.sum(probs * dprobs, 0, keepdims=True)
    dscores = (probs * (dprobs - inner)).astype(jnp.bfloat16)
    dk = matmul(dscores, queries)
    return unstacked(matmul_tn(dscores, keys)) * HEAD_DIM ** (-0.5), dk, dv


def attention_values(queries, keys, values, text_len):
    probs = softmax_of(matmul_nt(stacked(queries), keys), 1, text_len)
    return unstacked(matmul(probs.astype(jnp.bfloat16), values))


def stacked(rows):
    return jnp.concatenate([only(head, rows) for head in range(2)], 0)


def unstacked(rows):
    half = rows.shape[0] // 2
    return jnp.where(lanes_of(0, (half, rows.shape[1])), rows[:half], rows[half:])


def key_sets(key_refs, runs, text_len):
    if text_len:
        return key_refs[0][...]
    pieces = [take(ref, runs) for ref in key_refs]
    return pieces[0] if len(pieces) == 1 else jnp.concatenate(pieces, 0)


def attend_kernel(windows, text_len, sets, *refs):
    q_ref, k_refs, v_refs, out_ref = refs[0], refs[1 : 1 + sets], refs[1 + sets : 1 + 2 * sets], refs[-1]
    for runs in windows:
        queries = take(q_ref, runs) * HEAD_DIM ** (-0.5)
        keys, values = key_sets(k_refs, runs, text_len), key_sets(v_refs, runs, text_len)
        put(out_ref, slice(None), runs, attention_values(queries, keys, values, text_len))


def attend_back_kernel(windows, text_len, sets, *refs):
    q_ref, k_refs, v_refs = refs[0], refs[1 : 1 + sets], refs[1 + sets : 1 + 2 * sets]
    grad_ref = refs[1 + 2 * sets]
    dq_ref = refs[2 + 2 * sets]
    own_ref = refs[3 + 2 * sets] if text_len else None
    pair = pl.program_id(0)
    cols = [pl.ds(pl.multiple_of(i * D + pair * 2 * HEAD_DIM, 128), 2 * HEAD_DIM) for i in range(3)]
    merged = dq_ref.shape[1] == 3 * D
    for runs in windows:
        queries = take(q_ref, runs) * HEAD_DIM ** (-0.5)
        keys, values = key_sets(k_refs, runs, text_len), key_sets(v_refs, runs, text_len)
        grad_out = take(grad_ref, runs)
        dq, dk, dv = attention_gradients(queries, keys, values, grad_out, text_len)
        put(dq_ref, cols[0], runs, dq)
        if merged:
            put(dq_ref, cols[1], runs, dk)
            put(dq_ref, cols[2], runs, dv)
        else:
            own_ref[:, cols[0]] = dk
            own_ref[:, cols[1]] = dv


def pair_cols(which, pair):
    return pl.ds(pl.multiple_of(which * D + pair * 2 * HEAD_DIM, 128), 2 * HEAD_DIM)


def take_cols(ref, cols, runs):
    return jnp.concatenate([ref[low : low + many, cols] for low, many in runs], 0)


def attend_frames_kernel(windows, qkv_ref, out_ref, far_ref, send, recv):
    band = lax.axis_index("band")
    partner = (lax.axis_index("clip"), band + 1 - 2 * (band % 2))
    greet([partner])

    def copies(pair):
        return [
            pltpu.make_async_remote_copy(
                qkv_ref.at[:, pair_cols(1 + i, pair)],
                far_ref.at[:, pair_cols(i, pair)],
                send.at[pair, i],
                recv.at[pair, i],
                partner,
                MESH,
            )
            for i in range(2)
        ]

    @pl.loop(0, HEADS // 2)
    def _(pair):
        for copy in copies(pair):
            copy.start()

    @pl.loop(0, HEADS // 2)
    def _(pair):
        for copy in copies(pair):
            copy.wait_recv()
        for runs in windows:
            queries = take_cols(qkv_ref, pair_cols(0, pair), runs) * HEAD_DIM ** (-0.5)
            keys, values = (
                jnp.concatenate(
                    [
                        take_cols(qkv_ref, pair_cols(1 + i, pair), runs),
                        take_cols(far_ref, pair_cols(i, pair), runs),
                    ],
                    0,
                )
                for i in range(2)
            )
            put(
                out_ref, pair_cols(0, pair), runs, attention_values(queries, keys, values, 0)
            )

    @pl.loop(0, HEADS // 2)
    def _(pair):
        for copy in copies(pair):
            copy.wait_send()


def attend_frames_back_kernel(
    windows, qkv_ref, far_ref, grad_ref, out_ref, own_buf, far_put, far_got, send, recv
):
    band = lax.axis_index("band")
    partner = (lax.axis_index("clip"), band + 1 - 2 * (band % 2))
    greet([partner])

    def copies(pair):
        return [
            pltpu.make_async_remote_copy(
                far_put.at[:, pair_cols(i, pair)],
                far_got.at[:, pair_cols(i, pair)],
                send.at[pair, i],
                recv.at[pair, i],
                partner,
                MESH,
            )
            for i in range(2)
        ]

    def merge(pair):
        for i, copy in enumerate(copies(pair)):
            copy.wait_recv()
            cols = pair_cols(i, pair)
            total = own_buf[:, cols] + far_got[:, cols]
            out_ref[:, pair_cols(1 + i, pair)] = total.astype(jnp.bfloat16)

    @pl.loop(0, HEADS // 2)
    def _(pair):
        for runs in windows:
            queries = take_cols(qkv_ref, pair_cols(0, pair), runs) * HEAD_DIM ** (-0.5)
            keys, values = (
                jnp.concatenate(
                    [
                        take_cols(qkv_ref, pair_cols(1 + i, pair), runs),
                        take_cols(far_ref, pair_cols(i, pair), runs),
                    ],
                    0,
                )
                for i in range(2)
            )
            grad_out = take_cols(grad_ref, pair_cols(0, pair), runs)
            dq, *dkv = attention_gradients(queries, keys, values, grad_out, 0)
            put(out_ref, pair_cols(0, pair), runs, dq)
            half = keys.shape[0] // 2
            for i, value in enumerate(dkv):
                put(own_buf, pair_cols(i, pair), runs, value[:half])
                put(far_put, pair_cols(i, pair), runs, value[half:])
        for copy in copies(pair):
            copy.start()

        @pl.when(pair >= 1)
        def _():
            merge(pair - 1)

    merge(HEADS // 2 - 1)

    @pl.loop(0, HEADS // 2)
    def _(pair):
        for copy in copies(pair):
            copy.wait_send()


def attend_frames(qkv, windows):
    tokens = qkv.shape[0]
    dma = pltpu.SemaphoreType.DMA((HEADS // 2, 2))
    return pl.pallas_call(
        partial(attend_frames_kernel, windows),
        out_shape=(
            jax.ShapeDtypeStruct((tokens, D), jnp.bfloat16),
            jax.ShapeDtypeStruct((tokens, 2 * D), jnp.bfloat16),
        ),
        in_specs=[IN_VMEM],
        out_specs=(IN_VMEM,) * 2,
        scratch_shapes=[dma, dma],
        compiler_params=pltpu.CompilerParams(
            collective_id=4, has_side_effects=True, vmem_limit_bytes=40 << 20
        ),
        cost_estimate=attention_cost(tokens, 256, 2),
    )(qkv)


def attend_frames_back(qkv, far_kv, grad_out, windows):
    tokens = qkv.shape[0]
    dma = pltpu.SemaphoreType.DMA((HEADS // 2, 2))
    return pl.pallas_call(
        partial(attend_frames_back_kernel, windows),
        out_shape=jax.ShapeDtypeStruct(qkv.shape, jnp.bfloat16),
        in_specs=[IN_VMEM] * 3,
        out_specs=IN_VMEM,
        scratch_shapes=[pltpu.VMEM((tokens, 2 * D), jnp.float32)] * 3 + [dma, dma],
        compiler_params=pltpu.CompilerParams(
            collective_id=5, has_side_effects=True, vmem_limit_bytes=50 << 20
        ),
        cost_estimate=attention_cost(tokens, 256, 5),
    )(qkv, far_kv, grad_out)


def head_cols(array, first):
    return array, pl.BlockSpec((array.shape[0], 2 * HEAD_DIM), lambda h: (0, first + h))


def attention_operands(queries, key_values):
    ins = [head_cols(queries, 0)]
    ins += [head_cols(array, first) for array, first, _ in key_values]
    return ins + [head_cols(array, second) for array, _, second in key_values]


def attention_cost(tokens, keys, products):
    flops = 2 * products * tokens * keys * D * 2
    return pl.CostEstimate(
        flops=flops, bytes_accessed=tokens * D * 2 * 8, transcendentals=tokens * keys * HEADS
    )


def attend(queries, key_values, windows, text_len=0):
    tokens = queries.shape[0]
    ins = attention_operands(queries, key_values)
    return pl.pallas_call(
        partial(attend_kernel, windows, text_len, len(key_values)),
        grid=(HEADS // 2,),
        in_specs=[spec for _, spec in ins],
        out_specs=pl.BlockSpec((tokens, 2 * HEAD_DIM), lambda h: (0, h)),
        out_shape=jax.ShapeDtypeStruct((tokens, D), jnp.bfloat16),
        compiler_params=pltpu.CompilerParams(vmem_limit_bytes=40 << 20),
        cost_estimate=attention_cost(tokens, 320, 2),
    )(*[array for array, _ in ins])


def attend_back(queries, key_values, grad_out, windows, text_len=0):
    tokens = queries.shape[0]
    ins = attention_operands(queries, key_values) + [head_cols(grad_out, 0)]
    sets = len(key_values)
    whole = lambda rows, cols: pl.BlockSpec((rows, cols), lambda h: (0, 0))
    if sets == 1 and not text_len:
        outs = [((tokens, 3 * D), jnp.bfloat16)]
    else:
        rows = key_values[0][0].shape[0]
        outs = [((tokens, D), jnp.bfloat16)] + [((rows, 2 * D), jnp.float32)] * sets
    return pl.pallas_call(
        partial(attend_back_kernel, windows, text_len, sets),
        grid=(HEADS // 2,),
        in_specs=[spec for _, spec in ins],
        out_specs=[whole(*shape) for shape, _ in outs],
        out_shape=[jax.ShapeDtypeStruct(*out) for out in outs],
        compiler_params=pltpu.CompilerParams(vmem_limit_bytes=50 << 20),
        cost_estimate=attention_cost(tokens, 320, 5),
    )(*[array for array, _ in ins])


def mlp_forward(stream, modul, up_weight, down_weight):
    mlp_val, norm_back = jax.vjp(norm_modulated, stream, modul[3], modul[4])
    mlp_in = mlp_val.astype(jnp.bfloat16)
    up_proj = matmul(mlp_in, up_weight)
    share = 0.5 + 0.5 * lax.erf(up_proj * math.sqrt(0.5))
    gelu_val = up_proj * share
    slope = share + up_proj * (jnp.exp(-0.5 * up_proj * up_proj) / math.sqrt(2.0 * math.pi))
    gelu_low = gelu_val.astype(jnp.bfloat16)
    down_proj = matmul(gelu_low, down_weight)
    return (stream + modul[5] * down_proj, (norm_back, mlp_in, slope, gelu_low, down_proj))


def mlp_backward(grad_stream, modul, up_weight, down_weight, saved):
    norm_back, mlp_in, slope, gelu_low, down_proj = saved
    grad_down = (modul[5] * grad_stream).astype(jnp.bfloat16)
    grad_gate = jnp.sum(grad_stream * down_proj, 0)
    grad_up = (slope * matmul_nt(grad_down, down_weight)).astype(jnp.bfloat16)
    grad_part, grad_shift, grad_scale = norm_back(matmul_nt(grad_up, up_weight))
    factors = ((gelu_low, grad_down), (mlp_in, grad_up))
    return (grad_stream + grad_part, factors, (grad_shift, grad_scale, grad_gate))


def adam_update(weight, first_mom, second_mom, grad_val, learn_rate):
    first_mom = BETA_ONE * first_mom + (1.0 - BETA_ONE) * grad_val
    second_mom = BETA_TWO * second_mom + (1.0 - BETA_TWO) * grad_val * grad_val
    first_hat = first_mom / (1.0 - BETA_ONE**STEP)
    second_hat = second_mom / (1.0 - BETA_TWO**STEP)
    weight = weight - learn_rate * (first_hat / (jnp.sqrt(second_hat) + ADAM_EPS) + DECAY * weight)
    return (weight, first_mom, second_mom)

MESH = pl.DeviceIdType.MESH
ANY = pl.BlockSpec(memory_space=pl.ANY)
IN_VMEM = pl.BlockSpec(memory_space=pltpu.VMEM)
TEXT_PAD = 80


def ring_place(clip, count):
    half = clip // 2
    odd = clip % 2
    return half + odd * (count - 1 - 2 * half)


def ring_clip(place, count):
    far = place // (count // 2)
    return (1 - far) * 2 * place + far * (2 * (count - 1 - place) + 1)


def greet(peers):
    barrier = pltpu.get_barrier_semaphore()
    for peer in peers:
        pl.semaphore_signal(barrier, inc=1, device_id=peer, device_id_type=MESH)
    pl.semaphore_wait(barrier, len(peers))


def exchange_kernel(count, facts_ref, facts_out, send, recv):
    me = lax.axis_index("clip")
    band = lax.axis_index("band")
    peers = [((me + step) % count, band) for step in range(1, count)]
    greet(peers)
    sent = [
        pltpu.make_async_remote_copy(
            facts_ref, facts_out.at[me], send.at[step], recv.at[step], peer, MESH
        )
        for step, peer in enumerate(peers)
    ]
    for copy in sent:
        copy.start()
    facts_out[me] = facts_ref[...]
    for copy in sent:
        copy.wait()


def exchange_facts(facts):
    count = lax.axis_size("clip")
    return pl.pallas_call(
        partial(exchange_kernel, count),
        out_shape=jax.ShapeDtypeStruct((count,) + facts.shape, facts.dtype),
        in_specs=[IN_VMEM],
        out_specs=IN_VMEM,
        scratch_shapes=[pltpu.SemaphoreType.DMA((count - 1,))] * 2,
        compiler_params=pltpu.CompilerParams(collective_id=0, has_side_effects=True),
    )(facts)


def gather_kernel(count, picks, sides, *refs):
    num = len(picks)
    packs, vec_ref, text_ref = refs[:2], refs[2], refs[3]
    full, (vec_out, text_out, kv_out) = refs[4 : 4 + num], refs[4 + num : 7 + num]
    refs = refs[7 + num :]
    wide, shards = refs[:num], refs[num : 2 * num]
    ring_send, ring_recv, pair_send, pair_recv, cross_send, cross_recv = refs[2 * num : 2 * num + 6]
    load_sem, own_sem, part_send, part_recv, part_own = refs[2 * num + 6 : 2 * num + 11]
    kv_wide, kv_part, kv_put, kv_got, kv_sum, kv_load, kv_send, kv_recv, band_send, band_recv = refs[
        2 * num + 11 : 2 * num + 21
    ]
    share_send, share_recv = refs[2 * num + 21 :]
    shapes = [(packs[pack].shape[0], cols) for pack, _, cols in picks]
    loads = [
        pltpu.make_async_copy(
            packs[pack].at[:, pl.ds(start, cols)], wide[group], load_sem.at[group]
        )
        for group, (pack, start, cols) in enumerate(picks)
    ]
    kv_width = kv_wide.shape[1]
    kv_first = D + lax.axis_index("band") * kv_width
    kv_weight = pltpu.make_async_copy(
        packs[1].at[:, pl.ds(pl.multiple_of(kv_first, 128), kv_width)], kv_wide, kv_load
    )
    for copy in loads + [kv_weight]:
        copy.start()
    me = lax.axis_index("clip")
    band = lax.axis_index("band")
    core = band % 2
    place = ring_place(me, count)
    onward = 1 - 2 * core
    following = (ring_clip((place + onward + count) % count, count), band)
    plane = band // 2
    partner = (me, band + 1 - 2 * core)
    mirror = (me, band + 2 - 4 * plane)
    peers = [((me + step) % count, band) for step in range(1, count)]
    band_count = 2 * D // kv_width
    band_peers = [(me, (band + step) % band_count) for step in range(1, band_count)]
    greet(peers + band_peers)

    def block(ref, group, owner):
        rows, cols = shapes[group]
        return ref.at[
            pl.ds(pl.multiple_of(owner * rows, rows), rows),
            pl.ds(pl.multiple_of(core * (cols // 2), 128), cols // 2),
        ]

    def ring_copy(group, step):
        owner = ring_clip((place - onward * step + 2 * count) % count, count)
        there = block(full[group], group, owner)
        return pltpu.make_async_remote_copy(
            there, there, ring_send.at[step, group], ring_recv.at[step, group], following, MESH
        )

    def handed(group, step, send, recv, peer):
        owner = ring_clip((place - onward * (step + 1) + 2 * count) % count, count)
        there = block(full[group], group, owner)
        return pltpu.make_async_remote_copy(
            there, there, send.at[step, group], recv.at[step, group], peer, MESH
        )

    def pair_copy(group, step):
        return handed(group, step, pair_send, pair_recv, partner)

    def cross_copy(group, step):
        return handed(group, step, cross_send, cross_recv, mirror)

    def in_ring(group):
        def decorate(body):
            if sides[group]:
                pl.when(plane == sides[group] - 1)(body)
            else:
                body()

        return decorate

    def off_ring(group, also=None):
        def decorate(body):
            if sides[group]:
                off = plane != sides[group] - 1
                pl.when(off if also is None else jnp.logical_and(off, also))(body)

        return decorate

    def ring_arrival(group, step, onto):
        ring_copy(group, step).wait_recv()
        if onto:
            ring_copy(group, step + 1).start()
        pair_copy(group, step).start()
        if sides[group]:
            cross_copy(group, step).start()

    def cross_arrival(group, step):
        cross_copy(group, step).wait_recv()
        pair_copy(group, step).start()

    def own_copy(group):
        rows, cols = shapes[group]
        return pltpu.make_async_copy(
            shards[group],
            full[group].at[pl.ds(pl.multiple_of(me * rows, rows), rows), :],
            own_sem.at[group],
        )

    parts = []
    for step, peer in enumerate(peers):
        for which, (src, dst) in enumerate(((vec_ref, vec_out), (text_ref, text_out))):
            parts.append(
                pltpu.make_async_remote_copy(
                    src.at[peer[0], band],
                    dst.at[me, band],
                    part_send.at[which, step],
                    part_recv.at[which, step],
                    peer,
                    MESH,
                )
            )
    parts_own = [
        pltpu.make_async_copy(src.at[me, band], dst.at[me, band], part_own.at[which])
        for which, (src, dst) in enumerate(((vec_ref, vec_out), (text_ref, text_out)))
    ]
    for copy in parts_own + parts:
        copy.start()
    for group in range(num):
        rows, cols = shapes[group]
        loads[group].wait()
        shards[group][...] = wide[group][...].astype(jnp.bfloat16)
        own_copy(group).start()

        @in_ring(group)
        def _(group=group, rows=rows, cols=cols):
            pltpu.make_async_remote_copy(
                shards[group].at[:, pl.ds(pl.multiple_of(core * (cols // 2), 128), cols // 2)],
                block(full[group], group, me),
                ring_send.at[0, group],
                ring_recv.at[0, group],
                following,
                MESH,
            ).start()

    def kv_copy(hop):
        return pltpu.make_async_remote_copy(
            kv_put.at[hop], kv_got.at[hop], kv_send.at[hop], kv_recv.at[hop], following, MESH
        )

    def kv_hop(hop):
        owner = ring_clip((place - onward * (hop + 1) + 2 * count) % count, count)
        total = kv_part[owner]
        if not isinstance(hop, int) or hop > 0:
            kv_copy(hop - 1).wait_recv()
            total = total + kv_got[hop - 1]
        kv_put[hop] = total
        kv_copy(hop).start()

    def band_copies():
        return [
            pltpu.make_async_remote_copy(
                kv_sum, kv_out.at[band], band_send.at[step], band_recv.at[step], peer, MESH
            )
            for step, peer in enumerate(band_peers)
        ]

    for copy in parts_own + parts:
        copy.wait()
    shares = [
        pltpu.make_async_remote_copy(
            out.at[:, band],
            out.at[:, band],
            share_send.at[which, step],
            share_recv.at[which, step],
            peer,
            MESH,
        )
        for step, peer in enumerate(band_peers)
        for which, out in enumerate((vec_out, text_out))
    ]
    for copy in shares:
        copy.start()
    kv_weight.wait()
    weight = kv_wide[...].astype(jnp.bfloat16)
    depth = weight.shape[0] // band_count
    for copy in shares:
        copy.wait()
    for owner in range(count):
        kv_part[owner] = sum(
            matmul(text_out[owner, part], weight[part * depth : (part + 1) * depth])
            for part in range(band_count)
        )
    kv_hop(0)

    @pl.loop(1, count - 1)
    def _(step):
        for group in range(num):

            @in_ring(group)
            def _(group=group):
                ring_arrival(group, step - 1, True)

        kv_hop(step)
        for group in range(num):

            @off_ring(group, step >= 2)
            def _(group=group):
                cross_arrival(group, step - 2)

    for group in range(num):

        @in_ring(group)
        def _(group=group):
            ring_arrival(group, count - 2, False)

    for late in (count - 3, count - 2):
        for group in range(num):

            @off_ring(group)
            def _(group=group, late=late):
                cross_arrival(group, late)

    kv_copy(count - 2).wait_recv()
    kv_sum[...] = (kv_part[me] + kv_got[count - 2]).astype(jnp.bfloat16)
    kv_out[band] = kv_sum[...]
    for copy in band_copies():
        copy.start()
    for group in range(num):
        own_copy(group).wait()

    @pl.loop(0, count - 1)
    def _(step):
        for group in range(num):

            @in_ring(group)
            def _(group=group):
                ring_copy(group, step).wait_send()
                if sides[group]:
                    cross_copy(group, step).wait_send()

            pair_copy(group, step).wait()
        kv_copy(step).wait_send()

    for copy in band_copies():
        copy.wait()


def gather_quarters(shard):
    band_count = lax.axis_size("band")
    rows = shard.shape[0] // band_count
    own = lax.dynamic_slice_in_dim(shard, lax.axis_index("band") * rows, rows, 0)
    return lax.all_gather(own.astype(jnp.bfloat16), ("clip", "band"), axis=0, tiled=True)


def sum_rows(left, right):
    part = lax.psum_scatter(
        matmul_tn(left, right), ("clip", "band"), scatter_dimension=0, tiled=True
    )
    return lax.all_gather(part, "band", axis=0, tiled=True)


def gather_weights(packs, picks, sides, vectors, texts):
    count, band_count = lax.axis_size("clip"), lax.axis_size("band")
    num = len(picks)
    dma = pltpu.SemaphoreType.DMA
    shapes = [(packs[pack].shape[0], cols) for pack, _, cols in picks]
    kv_shape = (texts.shape[2], 2 * D // band_count)
    kv_all = pltpu.VMEM((count,) + kv_shape, jnp.float32)
    kv_hops = pltpu.VMEM((count - 1,) + kv_shape, jnp.float32)
    out = pl.pallas_call(
        partial(gather_kernel, count, picks, sides),
        out_shape=tuple(
            jax.ShapeDtypeStruct((count * rows, cols), jnp.bfloat16) for rows, cols in shapes
        )
        + tuple(jax.ShapeDtypeStruct(v.shape, v.dtype) for v in (vectors, texts))
        + (jax.ShapeDtypeStruct((band_count,) + kv_shape, jnp.bfloat16),),
        in_specs=[ANY] * 4,
        out_specs=(ANY,) * num + (IN_VMEM,) * 3,
        scratch_shapes=[pltpu.VMEM(shape, jnp.float32) for shape in shapes]
        + [pltpu.VMEM(shape, jnp.bfloat16) for shape in shapes]
        + [dma((count - 1, num))] * 6
        + [dma((num,)), dma((num,)), dma((2, count - 1)), dma((2, count - 1)), dma((2,))]
        + [
            pltpu.VMEM((packs[1].shape[0], kv_shape[1]), jnp.float32),
            kv_all,
            kv_hops,
            kv_hops,
            pltpu.VMEM(kv_shape, jnp.bfloat16),
            dma,
            dma((count - 1,)),
            dma((count - 1,)),
            dma((band_count - 1,)),
            dma((band_count - 1,)),
            dma((2, band_count - 1)),
            dma((2, band_count - 1)),
        ],
        compiler_params=pltpu.CompilerParams(
            collective_id=1, has_side_effects=True, vmem_limit_bytes=50 << 20
        ),
        cost_estimate=pl.CostEstimate(flops=2 * 10**11, bytes_accessed=6 * 10**8, transcendentals=0),
    )(*packs, vectors, texts)
    return out[:num], out[num], out[num + 1], out[num + 2]


WIRE_MAX = 32767.0
WIRE_LEAST = 1e-30
UNIT = (128, 512)


SPLIT = 2


def unit_parts(at, kind, first):
    if at == 0:
        return ((0, 4, lambda u: u, lambda u: 0), (4, SPLIT, lambda u: 4, lambda u: u - 3))
    if kind == 0:
        return ((0, 4, lambda u: u, lambda u: 0), (4, 4, lambda u: 4, lambda u: u - 3))
    if first:
        return ((2, 2, lambda u: u, lambda u: u), (4, 2, lambda u: 3, lambda u: u))
    return ((0, 3, lambda u: u, lambda u: u), (3, 3, lambda u: 3, lambda u: u))


def reduce_kernel(count, tokens, phases, *refs):
    num = sum(len(phase["lefts"]) for phase in phases)
    lefts, rights = refs[:num], refs[num : 2 * num]
    vec_ref, kv_ref, text_ref = refs[2 * num : 2 * num + 3]
    refs = refs[2 * num + 3 :]
    wide_out, deep_out, square_out, all_vec, kv_out, kv_square = refs[:6]
    left_far, right_far = refs[6 : 6 + num], refs[6 + num : 6 + 2 * num]
    scratch = refs[6 + 2 * num :]
    left_buf, right_buf, got_low, got_scale, put_low, put_scale, plane_put = (
        scratch[2 * i : 2 * i + 2] for i in range(7)
    )
    plane_got = scratch[14 : 14 + len(phases)]
    (
        square_buf,
        left_sem,
        right_sem,
        pair_send,
        pair_recv,
        half_send,
        half_recv,
        ring_send,
        ring_recv,
        credit,
        plane_send,
        plane_recv,
        out_sem,
        out_send,
        out_recv,
        last_put,
        last_put_scale,
        last_got,
        last_got_scale,
        push_send,
        push_recv,
        cross_put,
        cross_put_scale,
        cross_got,
        cross_got_scale,
        cross_send,
        cross_recv,
        cross_credit,
        vec_got,
        kv_got,
        vec_sum,
        all_kv,
        all_kv_scale,
        text_buf,
        kv_grad,
        side_own,
        side_send,
        side_recv,
        vec_send,
        vec_recv,
        vec_pair_send,
        vec_pair_recv,
        kv_own,
        kv_send,
        kv_recv,
    ) = scratch[14 + len(phases) :]
    me = lax.axis_index("clip")
    band = lax.axis_index("band")
    core = band % 2
    plane = band // 2
    place = ring_place(me, count)
    onward = 1 - 2 * core
    following = (ring_clip((place + onward + count) % count, count), band)
    preceding = (ring_clip((place - onward + count) % count, count), band)
    partner = (me, band + 1 - 2 * core)
    mirror = (me, band + 2 - 4 * plane)
    band_count = vec_got.shape[0]
    band_peers = [(me, (band + step) % band_count) for step in range(1, band_count)]
    greet([following, preceding] + band_peers)

    def owner_at(step, way):
        return ring_clip((place - way * (step + 1) + 2 * count) % count, count)

    def left_blocks(at):
        phase = phases[at]
        if phase["kind"] == 0:
            return [(b, phase["lefts"][0], b, 4) for b in range(4)] + [(4, phase["lefts"][1], 0, 1)]
        first = phase["first"]
        return [(first + i, left, 0, 1) for i, left in enumerate(phase["lefts"])]

    def right_blocks(at):
        phase = phases[at]
        if phase["kind"] == 0:
            return [(0, phase["lefts"][0], 0)] + [(1 + i, phase["lefts"][1], i) for i in range(4)]
        first = phase["first"]
        return [(first + i, phase["lefts"][i], 0) for i in range(3 - first)] + [
            (3 + i, phase["lefts"][-1], i) for i in range(3)
        ]

    def left_cols(step, way, which, many):
        width = lefts_width // count if many == 1 else deep_width // count
        start = owner_at(step, way) * width + which * 128
        return pl.ds(pl.multiple_of(start, 128), 128)

    lefts_width = lefts[phases[1]["lefts"][0]].shape[1]
    deep_width = lefts[phases[0]["lefts"][0]].shape[1]

    def pair_left(at, step):
        out = []
        for block, operand, which, many in left_blocks(at):
            cols = left_cols(step, -onward, which, many)
            out.append(
                pltpu.make_async_remote_copy(
                    lefts[operand].at[:, cols],
                    left_far[operand].at[:, cols],
                    pair_send.at[at, block, step],
                    pair_recv.at[at, block, step],
                    partner,
                    MESH,
                )
            )
        return out

    def pair_right(at):
        out = []
        for i, operand in enumerate(phases[at]["lefts"]):
            half = rights[operand].shape[1] // 2
            out.append(
                pltpu.make_async_remote_copy(
                    rights[operand].at[:, pl.ds(pl.multiple_of((1 - core) * half, 128), half)],
                    right_far[operand],
                    half_send.at[operand],
                    half_recv.at[operand],
                    partner,
                    MESH,
                )
            )
        return out

    def load_left(at, step, slot, far):
        kind = phases[at]["kind"]
        out = []
        for block, operand, which, many in left_blocks(at):
            cols = left_cols(step, onward, which, many)
            source = left_far if far else lefts
            out.append(
                pltpu.make_async_copy(
                    source[operand].at[:, cols],
                    left_buf[kind].at[slot, block, pl.ds(far * tokens, tokens), :],
                    left_sem.at[kind, slot, block, far],
                )
            )
        return out

    def load_right(at, far):
        kind = phases[at]["kind"]
        out = []
        for block, operand, which in right_blocks(at):
            if far:
                source = right_far[operand].at[:, pl.ds(which * UNIT[1], UNIT[1])]
            else:
                half = rights[operand].shape[1] // 2
                start = pl.multiple_of(core * half + which * UNIT[1], 128)
                source = rights[operand].at[:, pl.ds(start, UNIT[1])]
            out.append(
                pltpu.make_async_copy(
                    source,
                    right_buf[kind].at[block, pl.ds(far * tokens, tokens), :],
                    right_sem.at[kind, block, far],
                )
            )
        return out

    def ring_copies(at, part, slot):
        kind = phases[at]["kind"]
        units = pl.ds(*unit_parts(at, kind, phases[at]["first"])[part][:2])
        return [
            pltpu.make_async_remote_copy(
                put.at[slot, units],
                got.at[slot, units],
                ring_send.at[kind, slot, part, i],
                ring_recv.at[kind, slot, part, i],
                following,
                MESH,
            )
            for i, (put, got) in enumerate(
                ((put_low[kind], got_low[kind]), (put_scale[kind], got_scale[kind]))
            )
        ]

    def plane_copies(at, part):
        kind = phases[at]["kind"]
        units = pl.ds(*unit_parts(at, kind, phases[at]["first"])[part][:2])
        pairs = ((plane_put[kind], plane_got[at]),)
        if at + 1 == len(phases):
            pairs = ((last_put, last_got), (last_put_scale, last_got_scale))
        return [
            pltpu.make_async_remote_copy(
                here.at[units],
                there.at[units],
                plane_send.at[at, part, i],
                plane_recv.at[at, part, i],
                mirror,
                MESH,
            )
            for i, (here, there) in enumerate(pairs)
        ]

    def split_unit(pair, of_plane):
        return 4 + 2 * pair + of_plane

    def split_copy(pair, of_plane):
        unit = split_unit(pair, of_plane)
        return pltpu.make_async_remote_copy(
            plane_put[0].at[unit],
            plane_got[0].at[unit],
            plane_send.at[0, 1, pair],
            plane_recv.at[0, 1, pair],
            mirror,
            MESH,
        )

    def cross_copies(slot):
        return [
            pltpu.make_async_remote_copy(
                here.at[slot], there.at[slot], cross_send.at[slot, i], cross_recv.at[slot, i], mirror, MESH
            )
            for i, (here, there) in enumerate(
                ((cross_put, cross_got), (cross_put_scale, cross_got_scale))
            )
        ]

    def push_right(block):
        operand, which = [entry[1:] for entry in right_blocks(0) if entry[0] == block][0]
        half = rights[operand].shape[1] // 2
        begin = pl.multiple_of((1 - core) * half + which * UNIT[1], 128)
        return pltpu.make_async_remote_copy(
            rights[operand].at[:, pl.ds(begin, UNIT[1])],
            right_buf[phases[0]["kind"]].at[block, pl.ds(tokens, tokens), :],
            push_send.at[block],
            push_recv.at[block],
            partner,
            MESH,
        )

    def out_copies(at, unit):
        phase = phases[at]
        if phase["kind"] == 0 and unit < 4:
            half = UNIT[1]
            rows = deep_out.shape[0] // 4
            there = deep_out.at[
                pl.ds(unit * rows, rows),
                pl.ds(pl.multiple_of(phase["cols"][0] + core * half, 128), half),
            ]
        else:
            which, col = (1, unit - 4) if phase["kind"] == 0 else (unit - phase["first"], 0)
            if phase["kind"] and unit >= 3:
                which, col = len(phase["lefts"]) - 1, unit - 3
            half = rights[phase["lefts"][which]].shape[1] // 2
            start = phase["cols"][which] + core * half + col * UNIT[1]
            there = wide_out.at[:, pl.ds(pl.multiple_of(start, 128), UNIT[1])]
        here = plane_got[at].at[unit]
        return (
            pltpu.make_async_copy(here, there, out_sem.at[at, unit]),
            pltpu.make_async_remote_copy(
                here, there, out_send.at[at, unit], out_recv.at[at, unit], partner, MESH
            ),
        )

    def product(kind, slot, left, right):
        return lax.dot_general(
            left_buf[kind][slot, left],
            right_buf[kind][right],
            (((0,), (0,)), ((), ())),
            preferred_element_type=jnp.float32,
        )

    def start(copies):
        for copy in copies:
            copy.start()

    def finish(copies):
        for copy in copies:
            copy.wait()

    def encode(term):
        largest = jnp.maximum(jnp.max(jnp.abs(term), axis=0, keepdims=True), WIRE_LEAST)
        low = jnp.round(term * (WIRE_MAX / largest)).astype(jnp.int16)
        return low, largest * (1.0 / WIRE_MAX)

    def take_step(at, step, first, last):
        phase = phases[at]
        kind = phase["kind"]
        slot = step % 2
        before = (step + 1) % 2
        for far in range(2):
            finish(load_left(at, step, slot, far))

        def load_next():
            for copy in pair_left(at, step + 1):
                copy.wait_recv()
            for far in range(2):
                start(load_left(at, step + 1, before, far))

        opening = first and at == 0
        if not (last or opening):
            load_next()
        parts = unit_parts(at, kind, phase["first"])

        def send_theirs():
            def spend():
                for copy in cross_copies(slot):
                    copy.wait_send()
                pl.semaphore_wait(cross_credit, 1)

            if last:
                spend()
            elif not first:
                pl.when(step >= 2)(spend)
            for pair in range(SPLIT):
                unit = split_unit(pair, 1 - plane)
                term = product(kind, slot, parts[1][2](unit), parts[1][3](unit))
                cross_put[slot, pair], cross_put_scale[slot, pair] = encode(term)
            start(cross_copies(slot))

        if at == 0 and not opening:
            send_theirs()
        for part, (low, many, left_of, right_of) in enumerate(parts):
            if opening:
                blocks = range(1) if part == 0 else range(1, 5)
                finish(load_right(0, 0)[blocks.start : blocks.stop])
                for block in blocks:
                    push_right(block).wait_recv()
                if part:
                    send_theirs()
            if not first:
                for copy in ring_copies(at, part, before):
                    copy.wait_recv()
            if not (first or last):

                @pl.when(step >= 2)
                def _(part=part):
                    for copy in ring_copies(at, part, slot):
                        copy.wait_send()
                    pl.semaphore_wait(credit.at[kind, part], 1)

            def settle(position, unit, term):
                if not first:
                    came = got_low[kind][before, position].astype(jnp.float32)
                    term = term + came * got_scale[kind][before, position]
                if last and at + 1 == len(phases):
                    last_put[unit], last_put_scale[unit] = encode(term)
                elif last:
                    plane_put[kind][unit] = term
                else:
                    low_part, scale_part = encode(term)
                    put_low[kind][slot, position] = low_part
                    put_scale[kind][slot, position] = scale_part

            split = at == 0 and part == 1
            if split:
                for copy in cross_copies(slot):
                    copy.wait_recv()

            @pl.loop(low, low + many)
            def _(position, left_of=left_of, right_of=right_of):
                unit = split_unit(position - 4, plane) if split else position
                term = product(kind, slot, left_of(unit), right_of(unit))
                if split:
                    came = cross_got[slot, position - 4].astype(jnp.float32)
                    term = term + came * cross_got_scale[slot, position - 4]
                settle(position, unit, term)

            if split and not last:

                def credit_cross():
                    pl.semaphore_signal(
                        cross_credit, inc=1, device_id=mirror, device_id_type=MESH
                    )

                if first:
                    credit_cross()
                else:
                    pl.when(step < count - 2)(credit_cross)

            if last and split:
                start([split_copy(pair, plane) for pair in range(SPLIT)])
            elif last:
                start(plane_copies(at, part))
            else:
                start(ring_copies(at, part, slot))
            if not (first or last):

                @pl.when(step < count - 2)
                def _(part=part):
                    pl.semaphore_signal(
                        credit.at[kind, part], inc=1, device_id=preceding, device_id_type=MESH
                    )

        if opening:
            load_next()

    def close(at):
        kind = phases[at]["kind"]

        def add_square(total):
            square_buf[...] += jnp.sum((total * total).reshape(UNIT[0] // 8, 8, UNIT[1]), axis=0)

        for part, (low, many, _, _) in enumerate(unit_parts(at, kind, phases[at]["first"])):
            if at == 0 and part == 1:
                for pair in range(SPLIT):
                    split_copy(pair, plane).wait_send()
                    split_copy(pair, 1 - plane).wait_recv()
                    ours = split_unit(pair, plane)
                    plane_got[0][ours] = plane_put[0][ours]
                for unit in range(4, 8):
                    add_square(plane_got[0][unit])
                    start(out_copies(0, unit))
                continue
            finish(plane_copies(at, part))

            @pl.loop(low, low + many)
            def _(unit):
                if at + 1 == len(phases):
                    total = last_put[unit].astype(jnp.float32) * last_put_scale[unit]
                    total += last_got[unit].astype(jnp.float32) * last_got_scale[unit]
                else:
                    total = plane_put[kind][unit] + plane_got[at][unit]
                plane_got[at][unit] = total
                add_square(total)

            for unit in range(low, low + many):
                start(out_copies(at, unit))

    half_rows = pl.ds(pl.multiple_of(core * (vec_sum.shape[0] // 2), 8), vec_sum.shape[0] // 2)
    side_local = [
        pltpu.make_async_copy(vec_ref, vec_got.at[band], side_own.at[0]),
        pltpu.make_async_copy(kv_ref.at[band], kv_got.at[band], side_own.at[1]),
        pltpu.make_async_copy(text_ref, text_buf, side_own.at[2]),
    ]
    side_remote = []
    for step, peer in enumerate(band_peers):
        side_remote += [
            pltpu.make_async_remote_copy(
                vec_ref, vec_got.at[band], side_send.at[0, step], side_recv.at[0, step], peer, MESH
            ),
            pltpu.make_async_remote_copy(
                kv_ref.at[peer[1]],
                kv_got.at[band],
                side_send.at[1, step],
                side_recv.at[1, step],
                peer,
                MESH,
            ),
        ]
    vec_own = pltpu.make_async_copy(vec_sum, all_vec.at[me], side_own.at[3])

    def kv_parts(owner):
        return [(ref.at[owner], ref.at[owner]) for ref in (all_kv, all_kv_scale)]

    def vec_copies(step):
        owner = ring_clip((place - onward * step + 2 * count) % count, count)
        vec = all_vec.at[owner, half_rows]
        return [
            pltpu.make_async_remote_copy(
                here, there, vec_send.at[step, i], vec_recv.at[step, i], following, MESH
            )
            for i, (here, there) in enumerate([(vec, vec)] + kv_parts(owner))
        ]

    def vec_first():
        vec = all_vec.at[me, half_rows]
        return [
            pltpu.make_async_remote_copy(
                here, there, vec_send.at[0, i], vec_recv.at[0, i], following, MESH
            )
            for i, (here, there) in enumerate([(vec_sum.at[half_rows], vec)] + kv_parts(me))
        ]

    def vec_pair(step):
        owner = ring_clip((place - onward * (step + 1) + 2 * count) % count, count)
        vec = all_vec.at[owner, half_rows]
        return pltpu.make_async_remote_copy(
            vec, vec, vec_pair_send.at[step], vec_pair_recv.at[step], partner, MESH
        )

    kv_width = kv_grad.shape[1]

    def kv_place(owner):
        return kv_out.at[:, pl.ds(pl.multiple_of(owner * kv_width, 128), kv_width)]

    def kv_copy(i):
        if i == 2:
            return pltpu.make_async_copy(kv_grad, kv_place(band), kv_own)
        peer = (partner, mirror)[i]
        return pltpu.make_async_remote_copy(
            kv_grad, kv_place(band), kv_send.at[i], kv_recv.at[i], peer, MESH
        )

    def kv_passed():
        there = kv_place(mirror[1])
        return pltpu.make_async_remote_copy(
            there, there, kv_send.at[2], kv_recv.at[2], partner, MESH
        )

    def sum_bands():
        finish(side_local + side_remote)
        vec_sum[...] = jnp.sum(vec_got[...], 0)
        all_kv[me], all_kv_scale[me] = encode(jnp.sum(kv_got[...], 0))
        vec_own.start()
        start(vec_first())

    def pass_sums(step):
        for copy in vec_copies(step - 1):
            copy.wait_recv()
        start(vec_copies(step))
        vec_pair(step - 1).start()

    def multiply_text():
        for copy in vec_copies(count - 2):
            copy.wait_recv()
        vec_pair(count - 2).start()
        grads = all_kv[...].astype(jnp.float32) * all_kv_scale[...]
        grads = grads.reshape(text_buf.shape[0], -1)
        total = jnp.zeros_like(kv_grad)
        for _ in range(3):
            part = grads.astype(jnp.bfloat16)
            grads = grads - part.astype(jnp.float32)
            total = total + matmul_tn(text_buf[...], part)
        kv_grad[...] = total
        kv_square[...] = jnp.sum((total * total).reshape(-1, 8, total.shape[1]), axis=0)
        start([kv_copy(i) for i in range(3)])

    square_buf[...] = jnp.zeros_like(square_buf)
    start(side_local + side_remote)
    start(load_right(0, 0))
    start(load_left(0, 0, 0, 0))
    push_right(0).start()
    start(pair_left(0, 0))
    for block in range(1, 5):
        push_right(block).start()

    @pl.loop(1, count)
    def _(step):
        start(pair_left(0, step))

    for copy in pair_left(0, 0):
        copy.wait_recv()
    start(load_left(0, 0, 0, 1))
    take_step(0, 0, True, False)
    for at in range(len(phases)):
        more = at + 1 < len(phases)
        if more:
            start(pair_right(at + 1))
            start(load_right(at + 1, 0))
            start(pair_left(at + 1, 0))
        if at == 1:
            sum_bands()

        @pl.loop(1, count - 1)
        def _(step, at=at, more=more):
            take_step(at, step, False, False)
            if at == 1:
                pass_sums(step)
            if more:
                start(pair_left(at + 1, step))

                @pl.when(step == count // 2)
                def _():
                    for copy in pair_right(at + 1):
                        copy.wait_recv()
                    start(load_right(at + 1, 1))
                    for copy in pair_left(at + 1, 0):
                        copy.wait_recv()
                    for far in range(2):
                        start(load_left(at + 1, 0, 0, far))

        if more:
            start(pair_left(at + 1, count - 1))
            for far in range(2):
                finish(load_right(at + 1, far))
            take_step(at + 1, 0, True, False)
        take_step(at, count - 1, False, True)
        if at == 1:
            multiply_text()
        for slot in range(2):
            for part in range(2):
                for copy in ring_copies(at, part, slot):
                    copy.wait_send()
            if at == 0:
                for copy in cross_copies(slot):
                    copy.wait_send()
        if at == 2:
            kv_copy(1).wait_recv()
            kv_passed().start()
        if at:
            close(at - 1)
    close(len(phases) - 1)
    vec_own.wait()
    kv_passed().wait()
    kv_copy(0).wait()
    kv_copy(1).wait_send()
    kv_copy(2).wait()

    @pl.loop(0, count - 1)
    def _(step):
        for copy in vec_copies(step):
            copy.wait_send()
        vec_pair(step).wait()

    square_out[...] = square_buf[...]
    for at, phase in enumerate(phases):
        for copy in pair_right(at) if at else [push_right(block) for block in range(5)]:
            copy.wait_send()

        @pl.loop(0, count)
        def _(step, at=at):
            for copy in pair_left(at, step):
                copy.wait_send()

        for unit in range(phase["first"], 8 if phase["kind"] == 0 else 6):
            finish(out_copies(at, unit))


def reduce_gradients(phases, lefts, rights, vectors, keyvals, text, wide_cols, deep_cols):
    count = lax.axis_size("clip")
    tokens = lefts[0].shape[0]
    wide_rows = lefts[1].shape[1] // count
    deep_rows = lefts[0].shape[1] // count
    band_count, _, kv_cols = keyvals.shape
    num = len(lefts)
    dma = pltpu.SemaphoreType.DMA
    units, lefts_of, rights_of = (8, 6), (5, 4), (5, 6)
    scratch = [pltpu.VMEM((2, lefts_of[k], 2 * tokens, 128), jnp.bfloat16) for k in range(2)]
    scratch += [pltpu.VMEM((rights_of[k], 2 * tokens, UNIT[1]), jnp.bfloat16) for k in range(2)]
    for _ in range(2):
        scratch += [pltpu.VMEM((2, units[k]) + UNIT, jnp.int16) for k in range(2)]
        scratch += [pltpu.VMEM((2, units[k], 1, UNIT[1]), jnp.float32) for k in range(2)]
    scratch += [pltpu.VMEM((units[k],) + UNIT, jnp.float32) for k in range(2)]
    scratch += [pltpu.VMEM((units[p["kind"]],) + UNIT, jnp.float32) for p in phases]
    scratch += [
        pltpu.VMEM((8, UNIT[1]), jnp.float32),
        dma((2, 2, 5, 2)),
        dma((2, 6, 2)),
        dma((len(phases), 5, count)),
        dma((len(phases), 5, count)),
        dma((num,)),
        dma((num,)),
        dma((2, 2, 2, 2)),
        dma((2, 2, 2, 2)),
        pltpu.SemaphoreType.REGULAR((2, 2)),
        dma((len(phases), 2, 2)),
        dma((len(phases), 2, 2)),
        dma((len(phases), 8)),
        dma((len(phases), 8)),
        dma((len(phases), 8)),
    ]
    for _ in range(2):
        scratch += [pltpu.VMEM((6,) + UNIT, jnp.int16), pltpu.VMEM((6, 1, UNIT[1]), jnp.float32)]
    scratch += [
        dma((5,)),
        dma((5,)),
        *[
            pltpu.VMEM((2, SPLIT) + tile, kind)
            for _ in range(2)
            for tile, kind in ((UNIT, jnp.int16), ((1, UNIT[1]), jnp.float32))
        ],
        dma((2, 2)),
        dma((2, 2)),
        pltpu.SemaphoreType.REGULAR,
        pltpu.VMEM((band_count,) + vectors.shape, jnp.float32),
        pltpu.VMEM(keyvals.shape, jnp.float32),
        pltpu.VMEM(vectors.shape, jnp.float32),
        pltpu.VMEM((count,) + keyvals.shape[1:], jnp.int16),
        pltpu.VMEM((count, 1, kv_cols), jnp.float32),
        pltpu.VMEM(text.shape, jnp.bfloat16),
        pltpu.VMEM((text.shape[1], kv_cols), jnp.float32),
        dma((4,)),
        dma((2, band_count - 1)),
        dma((2, band_count - 1)),
        dma((count - 1, 3)),
        dma((count - 1, 3)),
        dma((count - 1,)),
        dma((count - 1,)),
        dma,
        dma((3,)),
        dma((3,)),
    ]
    out = pl.pallas_call(
        partial(reduce_kernel, count, tokens, phases),
        out_shape=(
            jax.ShapeDtypeStruct((wide_rows, wide_cols), jnp.float32),
            jax.ShapeDtypeStruct((deep_rows, deep_cols), jnp.float32),
            jax.ShapeDtypeStruct((8, UNIT[1]), jnp.float32),
            jax.ShapeDtypeStruct((count,) + vectors.shape, jnp.float32),
            jax.ShapeDtypeStruct((deep_rows, band_count * kv_cols), jnp.float32),
            jax.ShapeDtypeStruct((8, kv_cols), jnp.float32),
        )
        + tuple(jax.ShapeDtypeStruct(x.shape, x.dtype) for x in lefts)
        + tuple(jax.ShapeDtypeStruct((tokens, x.shape[1] // 2), x.dtype) for x in rights),
        in_specs=[ANY] * (2 * num + 3),
        out_specs=(ANY, ANY, IN_VMEM, ANY, ANY, IN_VMEM) + (ANY,) * (2 * num),
        scratch_shapes=scratch,
        compiler_params=pltpu.CompilerParams(
            collective_id=2, has_side_effects=True, vmem_limit_bytes=58 << 20
        ),
        cost_estimate=pl.CostEstimate(flops=3 * 10**11, bytes_accessed=8 * 10**8, transcendentals=0),
    )(*lefts, *rights, vectors, keyvals, text)
    return out[:6]


def total_kernel(count, part_ref, out_ref, mid, band_got, clip_got, *sems):
    me = lax.axis_index("clip")
    band = lax.axis_index("band")
    band_count = band_got.shape[0]
    band_peers = [(me, (band + step) % band_count) for step in range(1, band_count)]
    clip_peers = [((me + step) % count, band) for step in range(1, count)]
    greet(band_peers + clip_peers)
    stages = (
        (part_ref, band_got, band, band_peers, mid, sems[:2]),
        (mid, clip_got, me, clip_peers, out_ref, sems[2:]),
    )
    for value, got, index, peers, result, (send, recv) in stages:
        copies = [
            pltpu.make_async_remote_copy(
                value, got.at[index], send.at[step], recv.at[step], peer, MESH
            )
            for step, peer in enumerate(peers)
        ]
        for copy in copies:
            copy.start()
        got[index] = value[...]
        for copy in copies:
            copy.wait()
        result[...] = jnp.sum(got[...], 0)


def total_over_devices(value):
    count, band_count = lax.axis_size("clip"), lax.axis_size("band")
    dma = pltpu.SemaphoreType.DMA
    tile = (8, 128)
    return pl.pallas_call(
        partial(total_kernel, count),
        out_shape=jax.ShapeDtypeStruct(tile, jnp.float32),
        in_specs=[IN_VMEM],
        out_specs=IN_VMEM,
        scratch_shapes=[
            pltpu.VMEM(tile, jnp.float32),
            pltpu.VMEM((band_count,) + tile, jnp.float32),
            pltpu.VMEM((count,) + tile, jnp.float32),
            dma((band_count - 1,)),
            dma((band_count - 1,)),
            dma((count - 1,)),
            dma((count - 1,)),
        ],
        compiler_params=pltpu.CompilerParams(collective_id=3, has_side_effects=True),
    )(jnp.broadcast_to(value, tile))[0, 0]


def per_device(
    latents,
    noise_field,
    timesteps,
    null_flags,
    frame_mask,
    context,
    w_wide,
    m_wide,
    v_wide,
    w_deep,
    m_deep,
    v_deep,
    w_small,
    m_small,
    v_small,
):
    clip_count = lax.axis_size("clip")
    band_count = lax.axis_size("band")
    clip_at = lax.axis_index("clip")
    band_at = lax.axis_index("band")
    wide_rows = w_wide.shape[0]
    deep_rows = w_deep.shape[0]
    text_len, text_dim = context.shape[1:]
    facts = jnp.pad(
        jnp.concatenate([timesteps, frame_mask[0]])[None],
        ((0, 7), (0, 127 - frame_mask.shape[1])),
    )
    kept_text = context[0] * (1 - null_flags[0]).astype(jnp.bfloat16)
    text_cols = jnp.pad(
        kept_text.reshape(text_len, clip_count, band_count, -1).transpose(1, 2, 0, 3),
        ((0, 0), (0, 0), (0, TEXT_PAD - text_len), (0, 0)),
    )
    all_facts = exchange_facts(facts)
    all_times = all_facts[:, 0, 0].astype(jnp.float32)
    all_time_low = jax.nn.silu(time_features(all_times)).astype(jnp.bfloat16)
    time_rows = lax.dynamic_slice(
        all_time_low, (0, clip_at * wide_rows), (clip_count, wide_rows)
    )
    part_modul = matmul(time_rows, w_wide[:, : 12 * D].astype(jnp.bfloat16))
    kv_cols = 2 * D // band_count
    up_b_w = gather_quarters(w_wide[:, 22 * D + FF :])
    gathered, all_modul, all_text, keyval = gather_weights(
        (w_wide, w_deep),
        (
            (0, 22 * D, FF),
            (1, 0, D),
            (0, 20 * D, D),
            (0, 21 * D, D),
            (0, 18 * D, D),
            (0, 19 * D, D),
            (0, 12 * D, 3 * D),
            (0, 15 * D, 3 * D),
        ),
        (1, 2, 1, 2, 0, 0, 0, 0),
        part_modul.reshape(clip_count, band_count, -1, 128),
        text_cols,
    )
    up_a_w, down_a_w, query_w, cross_out_w, out_a_w, out_b_w, qkv_a_w, qkv_b_w = gathered
    all_text = all_text.transpose(0, 2, 1, 3)
    keyval = keyval.transpose(1, 0, 2).reshape(TEXT_PAD, 2 * D)
    late_down_b, all_modul = lax.optimization_barrier((w_deep[:, 3 * D :], all_modul))
    down_b_w = gather_quarters(late_down_b)
    small_low = w_small.astype(jnp.bfloat16)
    small_val = small_low.astype(jnp.float32)
    num_frames, num_rows, num_cols = (latents.shape[1], latents.shape[2], latents.shape[3])
    tok_count = num_frames * num_rows * num_cols
    all_mask = all_facts[:, 0, 1 : 1 + num_frames]
    global_count = jnp.sum(all_mask).astype(jnp.float32) * (num_rows * num_cols * CH * band_count)
    time_value = timesteps[0].astype(jnp.float32)
    noise_angle = 0.5 * math.pi * time_value / TMAX
    signal, spread = (jnp.cos(noise_angle), jnp.sin(noise_angle))
    clean_tok = token_order(latents[0])
    noise_tok = token_order(noise_field[0])
    run = num_rows * WIN
    part = SHIFT * WIN
    frame_windows = attend_pieces(tok_count, num_frames, "frame")
    half_windows = attend_pieces(tok_count, num_frames, "half")
    text_windows = attend_pieces(tok_count, num_frames, "text")
    noisy_low = (signal * clean_tok + spread * noise_tok).astype(jnp.bfloat16)
    target = signal * noise_tok - spread * clean_tok
    modulation = jnp.sum(all_modul, 0).reshape(12, D)
    mod_a, mod_b = (modulation[:6], modulation[6:])
    stream_zero = matmul(noisy_low, small_low[:CH]) + small_val[2 * CH]
    normed_a, back_a = jax.vjp(norm_modulated, stream_zero, mod_a[0], mod_a[1])
    in_a = normed_a.astype(jnp.bfloat16)
    qkv_a = matmul(in_a, qkv_a_w).astype(jnp.bfloat16)
    att_a, far_kv = attend_frames(qkv_a, frame_windows)
    proj_a = matmul(att_a, out_a_w)
    stream_one = stream_zero + mod_a[2] * proj_a
    stream_two, saved_a = mlp_forward(stream_one, mod_a, up_a_w, down_a_w)
    normed_b, back_b = jax.vjp(norm_modulated, stream_two, mod_b[0], mod_b[1])
    low_b = normed_b.astype(jnp.bfloat16)
    rolled = with_rows(low_b, shifted(first_rows(low_b, run, part), "band", -1), run)
    qkv_b = matmul(rolled, qkv_b_w).astype(jnp.bfloat16)
    win_kv = [(qkv_b, HEADS // 2, HEADS)]
    win_out = attend(qkv_b, win_kv, half_windows)
    att_b = with_rows(win_out, shifted(first_rows(win_out, run, part), "band", 1), run)
    proj_b = matmul(att_b, out_b_w)
    stream_three = stream_two + mod_b[2] * proj_b
    cross_val, cross_back = jax.vjp(norm_gained, stream_three, small_val[2 * CH + 1])
    cross_in = cross_val.astype(jnp.bfloat16)
    query_proj = matmul(cross_in, query_w).astype(jnp.bfloat16)
    text_kv = [(keyval, 0, HEADS // 2)]
    crossed = attend(query_proj, text_kv, text_windows, text_len)
    stream_four = stream_three + matmul(crossed, cross_out_w)
    stream_five, saved_b = mlp_forward(stream_four, mod_b, up_b_w, down_b_w)
    final_val, final_back = jax.vjp(norm_gained, stream_five, small_val[2 * CH + 2])
    final_low = final_val.astype(jnp.bfloat16)
    head_low = small_low[CH : 2 * CH]
    predicted = matmul_nt(final_low, head_low)
    weight_row = jnp.repeat(frame_mask[0].astype(jnp.float32), run)
    weight_row = jnp.tile(weight_row, num_cols // WIN)[:, None]
    pred_error = predicted - target
    loss_part = jnp.sum(weight_row * pred_error * pred_error)
    grad_pred = (weight_row * pred_error * (2.0 / global_count)).astype(jnp.bfloat16)
    grad_head = matmul_tn(grad_pred, final_low)
    grad_stream, grad_gain_f = final_back(matmul(grad_pred, head_low))
    grad_stream, mlp_factors_b, extra_b = mlp_backward(
        grad_stream, mod_b, up_b_w, down_b_w, saved_b
    )
    grad_cross = grad_stream.astype(jnp.bfloat16)
    grad_crossed = matmul_nt(grad_cross, cross_out_w).astype(jnp.bfloat16)
    grad_query, grad_keyval = attend_back(
        query_proj, text_kv, grad_crossed, text_windows, text_len
    )
    grad_part, grad_gain_c = cross_back(matmul_nt(grad_query, query_w))
    grad_stream = grad_stream + grad_part
    grad_proj = (mod_b[2] * grad_stream).astype(jnp.bfloat16)
    grad_gate_b = jnp.sum(grad_stream * proj_b, 0)
    factors_ob = (att_b, grad_proj)
    grad_att = matmul_nt(grad_proj, out_b_w).astype(jnp.bfloat16)
    grad_win = with_rows(grad_att, shifted(first_rows(grad_att, run, part), "band", -1), run)
    grad_qkv = attend_back(qkv_b, win_kv, grad_win, half_windows)[0]
    factors_qkvb = (rolled, grad_qkv)
    grad_in_roll = matmul_nt(grad_qkv, qkv_b_w)
    sent_back = shifted(first_rows(grad_in_roll, run, part), "band", 1)
    grad_normed = with_rows(grad_in_roll, sent_back, run)
    grad_part, grad_shift_b, grad_scale_b = back_b(grad_normed)
    grad_stream = grad_stream + grad_part
    grad_stream, mlp_factors_a, extra_a = mlp_backward(
        grad_stream, mod_a, up_a_w, down_a_w, saved_a
    )
    grad_proj = (mod_a[2] * grad_stream).astype(jnp.bfloat16)
    grad_gate_a = jnp.sum(grad_stream * proj_a, 0)
    factors_oa = (att_a, grad_proj)
    grad_att = matmul_nt(grad_proj, out_a_w).astype(jnp.bfloat16)
    grad_qkv = attend_frames_back(qkv_a, far_kv, grad_att, frame_windows)
    factors_qkva = (in_a, grad_qkv)
    grad_part, grad_shift_a, grad_scale_a = back_a(matmul_nt(grad_qkv, qkv_a_w))
    grad_stream = grad_stream + grad_part
    grad_patch = matmul_tn(noisy_low.astype(jnp.float32), grad_stream, lax.Precision.HIGHEST)
    grad_bias = jnp.sum(grad_stream, 0)
    grad_modul = jnp.stack(
        [
            grad_shift_a,
            grad_scale_a,
            grad_gate_a,
            extra_a[0],
            extra_a[1],
            extra_a[2],
            grad_shift_b,
            grad_scale_b,
            grad_gate_b,
            extra_b[0],
            extra_b[1],
            extra_b[2],
        ]
    ).reshape(1, 12 * D)
    grad_small = jnp.concatenate(
        [grad_patch, grad_head, grad_bias[None], grad_gain_c[None], grad_gain_f[None]], 0
    )
    factors = mlp_factors_b + (
        (crossed, grad_cross),
        (cross_in, grad_query),
        factors_ob,
        factors_qkvb,
    )
    factors += mlp_factors_a + (factors_oa, factors_qkva)
    if wide_rows == 128 and deep_rows == 512:
        phases = (
            {"kind": 0, "first": 0, "lefts": (0, 1), "cols": (D, 10 * D + FF)},
            {"kind": 1, "first": 0, "lefts": (2, 3, 4, 5), "cols": (9 * D, 8 * D, 7 * D, 3 * D)},
            {"kind": 0, "first": 0, "lefts": (6, 7), "cols": (0, 10 * D)},
            {"kind": 1, "first": 2, "lefts": (8, 9), "cols": (6 * D, 0)},
        )
        used = 12 * D + grad_small.size
        vectors = jnp.concatenate(
            [grad_modul.reshape(-1), grad_small.reshape(-1), loss_part[None]]
        )
        vectors = jnp.pad(vectors, (0, 256 * 128 - vectors.shape[0])).reshape(256, 128)
        keyvals = grad_keyval.reshape(TEXT_PAD, band_count, kv_cols).transpose(1, 0, 2)
        wide_rest, deep_rest, squares, all_vectors, grad_w_ckv, kv_squares = reduce_gradients(
            phases,
            [f[0] for f in factors],
            [f[1] for f in factors],
            vectors,
            keyvals,
            all_text.reshape(clip_count * TEXT_PAD, deep_rows),
            10 * D + 2 * FF,
            2 * D,
        )
        all_vectors = all_vectors.reshape(clip_count, -1)
        all_grad_modul = all_vectors[:, : 12 * D]
        small_sum = jnp.sum(all_vectors[:, 12 * D : used], 0).reshape(grad_small.shape)
        loss_sum = jnp.sum(all_vectors[:, used])
        square_part = jnp.sum(squares) / (band_count // 2) + jnp.sum(kv_squares)
    else:
        summed = [sum_rows(*pair) for pair in factors]
        wide_rest = jnp.concatenate([summed[i] for i in (9, 5, 8, 4, 3, 2, 7, 1)], 1)
        deep_rest = jnp.concatenate([summed[6], summed[0]], 1)
        grad_keyval = lax.psum_scatter(grad_keyval, "band", scatter_dimension=1, tiled=True)
        grad_keyval = lax.all_gather(grad_keyval, "clip", axis=0, tiled=True)
        grad_w_ckv = matmul_tn(
            all_text.reshape(clip_count * TEXT_PAD, deep_rows).astype(jnp.float32),
            grad_keyval,
            lax.Precision.HIGHEST,
        )
        grad_w_ckv = lax.all_gather(grad_w_ckv, "band", axis=1, tiled=True)
        all_grad_modul = lax.all_gather(lax.psum(grad_modul, "band"), "clip", axis=0, tiled=True)
        loss_sum, small_sum = lax.psum((loss_part, grad_small), ("clip", "band"))
        square_part = sum(jnp.sum(x * x) for x in (wide_rest, deep_rest, grad_w_ckv)) / band_count
    grad_w_ada = matmul_tn(time_rows.astype(jnp.float32), all_grad_modul, lax.Precision.HIGHEST)
    wide_sum = jnp.concatenate([grad_w_ada, wide_rest], 1)
    deep_sum = jnp.concatenate([deep_rest[:, :D], grad_w_ckv, deep_rest[:, D:]], 1)
    square_part += jnp.sum(grad_w_ada * grad_w_ada) / band_count
    square_sum = total_over_devices(square_part)
    grad_norm = jnp.sqrt(square_sum + jnp.sum(small_sum * small_sum))
    factor = CLIP_MAX / jnp.maximum(grad_norm, CLIP_MAX)
    new_wide = adam_update(w_wide, m_wide, v_wide, wide_sum * factor, 0.15)
    new_deep = adam_update(w_deep, m_deep, v_deep, deep_sum * factor, 0.05)
    new_small = adam_update(w_small, m_small, v_small, small_sum * factor, 0.5)
    loss = loss_sum / global_count
    return (
        loss,
        grad_norm,
        new_wide[0],
        new_wide[1],
        new_wide[2],
        new_deep[0],
        new_deep[1],
        new_deep[2],
        new_small[0],
        new_small[1],
        new_small[2],
    )


def solution(mesh):
    in_specs = (
        P("clip", None, "band", None, None),
        P("clip", None, "band", None, None),
        P("clip"),
        P("clip"),
        P("clip", None),
        P("clip", None, None),
        P("clip", None),
        P("clip", None),
        P("clip", None),
        P("clip", None),
        P("clip", None),
        P("clip", None),
        P(),
        P(),
        P(),
    )
    out_specs = (
        P(),
        P(),
        P("clip", None),
        P("clip", None),
        P("clip", None),
        P("clip", None),
        P("clip", None),
        P("clip", None),
        P(),
        P(),
        P(),
    )
    return jax.shard_map(
        per_device, mesh=mesh, in_specs=in_specs, out_specs=out_specs, check_vma=False
    )
```

```python
from functools import partial
import math

import jax
import jax.numpy as jnp
from jax import lax
from jax.experimental import pallas as pl
from jax.experimental.pallas import tpu as pltpu
from jax.sharding import PartitionSpec as P

D = 1024
HEADS = 16
HEAD_DIM = 64
FF = 4096
CH = 8
SPACE = 16
WIN = 8
SHIFT = 4
TMAX = 1000
STEP = 10


EPS_NORM = 1e-06
CLIP_MAX = 0.001
BETA_ONE = 0.9
BETA_TWO = 0.95
ADAM_EPS = 1e-08
DECAY = 0.1


def shifted(value, axis, by):
    length = lax.axis_size(axis)
    return lax.ppermute(value, axis, [(i, (i + by) % length) for i in range(length)])


def matmul(left_op, right_op):
    return jnp.dot(left_op, right_op, preferred_element_type=jnp.float32)


def matmul_tn(left_op, right_op, precision=None):
    return lax.dot_general(
        left_op,
        right_op,
        (((0,), (0,)), ((), ())),
        precision=precision,
        preferred_element_type=jnp.float32,
    )


def matmul_nt(left_op, right_op):
    return lax.dot_general(
        left_op, right_op, (((1,), (1,)), ((), ())), preferred_element_type=jnp.float32
    )


def layer_norm(field_in):
    average = jnp.mean(field_in, -1, keepdims=True)
    centred = field_in - average
    return centred * lax.rsqrt(jnp.mean(centred * centred, -1, keepdims=True) + EPS_NORM)


def norm_modulated(field_in, shift_vec, scale_vec):
    return layer_norm(field_in) * (1.0 + scale_vec) + shift_vec


def norm_gained(field_in, gain_vec):
    return layer_norm(field_in) * gain_vec


def time_features(time_value):
    half_width = D // 2
    frequency = jnp.exp(-math.log(10000.0) * jnp.arange(half_width, dtype=jnp.float32) / half_width)
    angles = time_value[..., None] * frequency
    return jnp.concatenate([jnp.cos(angles), jnp.sin(angles)], -1)


def token_order(grid):
    frames, rows, cols, width = grid.shape
    halves = grid.reshape(frames, rows, cols // WIN, WIN, width).transpose(2, 0, 1, 3, 4)
    return halves.reshape(frames * rows * cols, width)


def with_rows(tokens, first_rows, run):
    width = tokens.shape[1]
    runs = tokens.reshape(-1, run, width)
    return jnp.concatenate([first_rows, runs[:, first_rows.shape[1] :]], 1).reshape(-1, width)


def first_rows(tokens, run, part):
    return tokens.reshape(-1, run, tokens.shape[1])[:, :part]


def attend_pieces(tokens, frames, keys):
    if keys == "frame":
        run = tokens // (2 * frames)
        return [((f * run, run), (tokens // 2 + f * run, run)) for f in range(frames)]
    if keys == "half":
        return [((half * (tokens // 2), tokens // 2),) for half in range(2)]
    return [((0, tokens),)]


def take(ref, runs):
    pieces = [ref[low : low + many, :] for low, many in runs]
    return pieces[0] if len(pieces) == 1 else jnp.concatenate(pieces, 0)


def put(ref, cols, runs, value):
    done = 0
    for low, many in runs:
        ref[low : low + many, cols] = value[done : done + many].astype(ref.dtype)
        done += many


def softmax_of(scores, axis, text_len):
    if text_len:
        place = lax.broadcasted_iota(jnp.int32, scores.shape, axis)
        scores = jnp.where(place < text_len, scores, -1e30)
    weight = jnp.exp(scores - jnp.max(scores, axis, keepdims=True))
    return weight * (1.0 / jnp.sum(weight, axis, keepdims=True))


def lanes_of(head, shape):
    lane = lax.broadcasted_iota(jnp.int32, shape, 1)
    return lane < HEAD_DIM if head == 0 else lane >= HEAD_DIM


def only(head, value):
    return jnp.where(lanes_of(head, value.shape), value, jnp.zeros_like(value))


def attention_gradients(queries, keys, values, grad_out, text_len):
    queries, grad_out = stacked(queries), stacked(grad_out)
    probs = softmax_of(matmul_nt(keys, queries), 0, text_len)
    dprobs = matmul_nt(values, grad_out)
    dv = matmul(probs.astype(jnp.bfloat16), grad_out)
    inner = jnp.sum(probs * dprobs, 0, keepdims=True)
    dscores = (probs * (dprobs - inner)).astype(jnp.bfloat16)
    dk = matmul(dscores, queries)
    return unstacked(matmul_tn(dscores, keys)) * HEAD_DIM ** (-0.5), dk, dv


def attention_values(queries, keys, values, text_len):
    probs = softmax_of(matmul_nt(stacked(queries), keys), 1, text_len)
    return unstacked(matmul(probs.astype(jnp.bfloat16), values))


def stacked(rows):
    return jnp.concatenate([only(head, rows) for head in range(2)], 0)


def unstacked(rows):
    half = rows.shape[0] // 2
    return jnp.where(lanes_of(0, (half, rows.shape[1])), rows[:half], rows[half:])


def key_sets(key_refs, runs, text_len):
    if text_len:
        return key_refs[0][...]
    pieces = [take(ref, runs) for ref in key_refs]
    return pieces[0] if len(pieces) == 1 else jnp.concatenate(pieces, 0)


def attend_kernel(windows, text_len, sets, *refs):
    q_ref, k_refs, v_refs, out_ref = refs[0], refs[1 : 1 + sets], refs[1 + sets : 1 + 2 * sets], refs[-1]
    for runs in windows:
        queries = take(q_ref, runs) * HEAD_DIM ** (-0.5)
        keys, values = key_sets(k_refs, runs, text_len), key_sets(v_refs, runs, text_len)
        put(out_ref, slice(None), runs, attention_values(queries, keys, values, text_len))


def attend_back_kernel(windows, text_len, sets, *refs):
    q_ref, k_refs, v_refs = refs[0], refs[1 : 1 + sets], refs[1 + sets : 1 + 2 * sets]
    grad_ref = refs[1 + 2 * sets]
    dq_ref = refs[2 + 2 * sets]
    own_ref = refs[3 + 2 * sets] if text_len else None
    pair = pl.program_id(0)
    cols = [pl.ds(pl.multiple_of(i * D + pair * 2 * HEAD_DIM, 128), 2 * HEAD_DIM) for i in range(3)]
    merged = dq_ref.shape[1] == 3 * D
    for runs in windows:
        queries = take(q_ref, runs) * HEAD_DIM ** (-0.5)
        keys, values = key_sets(k_refs, runs, text_len), key_sets(v_refs, runs, text_len)
        grad_out = take(grad_ref, runs)
        dq, dk, dv = attention_gradients(queries, keys, values, grad_out, text_len)
        put(dq_ref, cols[0], runs, dq)
        if merged:
            put(dq_ref, cols[1], runs, dk)
            put(dq_ref, cols[2], runs, dv)
        else:
            own_ref[:, cols[0]] = dk
            own_ref[:, cols[1]] = dv


def pair_cols(which, pair):
    return pl.ds(pl.multiple_of(which * D + pair * 2 * HEAD_DIM, 128), 2 * HEAD_DIM)


def take_cols(ref, cols, runs):
    return jnp.concatenate([ref[low : low + many, cols] for low, many in runs], 0)


def attend_frames_kernel(windows, qkv_ref, out_ref, far_ref, send, recv):
    band = lax.axis_index("band")
    partner = (lax.axis_index("clip"), band + 1 - 2 * (band % 2))
    greet([partner])

    def copies(pair):
        return [
            pltpu.make_async_remote_copy(
                qkv_ref.at[:, pair_cols(1 + i, pair)],
                far_ref.at[:, pair_cols(i, pair)],
                send.at[pair, i],
                recv.at[pair, i],
                partner,
                MESH,
            )
            for i in range(2)
        ]

    @pl.loop(0, HEADS // 2)
    def _(pair):
        for copy in copies(pair):
            copy.start()

    @pl.loop(0, HEADS // 2)
    def _(pair):
        for copy in copies(pair):
            copy.wait_recv()
        for runs in windows:
            queries = take_cols(qkv_ref, pair_cols(0, pair), runs) * HEAD_DIM ** (-0.5)
            keys, values = (
                jnp.concatenate(
                    [
                        take_cols(qkv_ref, pair_cols(1 + i, pair), runs),
                        take_cols(far_ref, pair_cols(i, pair), runs),
                    ],
                    0,
                )
                for i in range(2)
            )
            put(
                out_ref, pair_cols(0, pair), runs, attention_values(queries, keys, values, 0)
            )

    @pl.loop(0, HEADS // 2)
    def _(pair):
        for copy in copies(pair):
            copy.wait_send()


def attend_frames_back_kernel(
    windows, qkv_ref, far_ref, grad_ref, out_ref, own_buf, far_put, far_got, send, recv
):
    band = lax.axis_index("band")
    partner = (lax.axis_index("clip"), band + 1 - 2 * (band % 2))
    greet([partner])

    def copies(pair):
        return [
            pltpu.make_async_remote_copy(
                far_put.at[:, pair_cols(i, pair)],
                far_got.at[:, pair_cols(i, pair)],
                send.at[pair, i],
                recv.at[pair, i],
                partner,
                MESH,
            )
            for i in range(2)
        ]

    def merge(pair):
        for i, copy in enumerate(copies(pair)):
            copy.wait_recv()
            cols = pair_cols(i, pair)
            total = own_buf[:, cols] + far_got[:, cols]
            out_ref[:, pair_cols(1 + i, pair)] = total.astype(jnp.bfloat16)

    @pl.loop(0, HEADS // 2)
    def _(pair):
        for runs in windows:
            queries = take_cols(qkv_ref, pair_cols(0, pair), runs) * HEAD_DIM ** (-0.5)
            keys, values = (
                jnp.concatenate(
                    [
                        take_cols(qkv_ref, pair_cols(1 + i, pair), runs),
                        take_cols(far_ref, pair_cols(i, pair), runs),
                    ],
                    0,
                )
                for i in range(2)
            )
            grad_out = take_cols(grad_ref, pair_cols(0, pair), runs)
            dq, *dkv = attention_gradients(queries, keys, values, grad_out, 0)
            put(out_ref, pair_cols(0, pair), runs, dq)
            half = keys.shape[0] // 2
            for i, value in enumerate(dkv):
                put(own_buf, pair_cols(i, pair), runs, value[:half])
                put(far_put, pair_cols(i, pair), runs, value[half:])
        for copy in copies(pair):
            copy.start()

        @pl.when(pair >= 1)
        def _():
            merge(pair - 1)

    merge(HEADS // 2 - 1)

    @pl.loop(0, HEADS // 2)
    def _(pair):
        for copy in copies(pair):
            copy.wait_send()


def attend_frames(qkv, windows):
    tokens = qkv.shape[0]
    dma = pltpu.SemaphoreType.DMA((HEADS // 2, 2))
    return pl.pallas_call(
        partial(attend_frames_kernel, windows),
        out_shape=(
            jax.ShapeDtypeStruct((tokens, D), jnp.bfloat16),
            jax.ShapeDtypeStruct((tokens, 2 * D), jnp.bfloat16),
        ),
        in_specs=[IN_VMEM],
        out_specs=(IN_VMEM,) * 2,
        scratch_shapes=[dma, dma],
        compiler_params=pltpu.CompilerParams(
            collective_id=4, has_side_effects=True, vmem_limit_bytes=40 << 20
        ),
        cost_estimate=attention_cost(tokens, 256, 2),
    )(qkv)


def attend_frames_back(qkv, far_kv, grad_out, windows):
    tokens = qkv.shape[0]
    dma = pltpu.SemaphoreType.DMA((HEADS // 2, 2))
    return pl.pallas_call(
        partial(attend_frames_back_kernel, windows),
        out_shape=jax.ShapeDtypeStruct(qkv.shape, jnp.bfloat16),
        in_specs=[IN_VMEM] * 3,
        out_specs=IN_VMEM,
        scratch_shapes=[pltpu.VMEM((tokens, 2 * D), jnp.float32)] * 3 + [dma, dma],
        compiler_params=pltpu.CompilerParams(
            collective_id=5, has_side_effects=True, vmem_limit_bytes=50 << 20
        ),
        cost_estimate=attention_cost(tokens, 256, 5),
    )(qkv, far_kv, grad_out)


def head_cols(array, first):
    return array, pl.BlockSpec((array.shape[0], 2 * HEAD_DIM), lambda h: (0, first + h))


def attention_operands(queries, key_values):
    ins = [head_cols(queries, 0)]
    ins += [head_cols(array, first) for array, first, _ in key_values]
    return ins + [head_cols(array, second) for array, _, second in key_values]


def attention_cost(tokens, keys, products):
    flops = 2 * products * tokens * keys * D * 2
    return pl.CostEstimate(
        flops=flops, bytes_accessed=tokens * D * 2 * 8, transcendentals=tokens * keys * HEADS
    )


def attend(queries, key_values, windows, text_len=0):
    tokens = queries.shape[0]
    ins = attention_operands(queries, key_values)
    return pl.pallas_call(
        partial(attend_kernel, windows, text_len, len(key_values)),
        grid=(HEADS // 2,),
        in_specs=[spec for _, spec in ins],
        out_specs=pl.BlockSpec((tokens, 2 * HEAD_DIM), lambda h: (0, h)),
        out_shape=jax.ShapeDtypeStruct((tokens, D), jnp.bfloat16),
        compiler_params=pltpu.CompilerParams(vmem_limit_bytes=40 << 20),
        cost_estimate=attention_cost(tokens, 320, 2),
    )(*[array for array, _ in ins])


def attend_back(queries, key_values, grad_out, windows, text_len=0):
    tokens = queries.shape[0]
    ins = attention_operands(queries, key_values) + [head_cols(grad_out, 0)]
    sets = len(key_values)
    whole = lambda rows, cols: pl.BlockSpec((rows, cols), lambda h: (0, 0))
    if sets == 1 and not text_len:
        outs = [((tokens, 3 * D), jnp.bfloat16)]
    else:
        rows = key_values[0][0].shape[0]
        outs = [((tokens, D), jnp.bfloat16)] + [((rows, 2 * D), jnp.float32)] * sets
    return pl.pallas_call(
        partial(attend_back_kernel, windows, text_len, sets),
        grid=(HEADS // 2,),
        in_specs=[spec for _, spec in ins],
        out_specs=[whole(*shape) for shape, _ in outs],
        out_shape=[jax.ShapeDtypeStruct(*out) for out in outs],
        compiler_params=pltpu.CompilerParams(vmem_limit_bytes=50 << 20),
        cost_estimate=attention_cost(tokens, 320, 5),
    )(*[array for array, _ in ins])


def mlp_forward(stream, modul, up_weight, down_weight):
    mlp_val, norm_back = jax.vjp(norm_modulated, stream, modul[3], modul[4])
    mlp_in = mlp_val.astype(jnp.bfloat16)
    up_proj = matmul(mlp_in, up_weight)
    share = 0.5 + 0.5 * lax.erf(up_proj * math.sqrt(0.5))
    gelu_val = up_proj * share
    slope = share + up_proj * (jnp.exp(-0.5 * up_proj * up_proj) / math.sqrt(2.0 * math.pi))
    gelu_low = gelu_val.astype(jnp.bfloat16)
    down_proj = matmul(gelu_low, down_weight)
    return (stream + modul[5] * down_proj, (norm_back, mlp_in, slope, gelu_low, down_proj))


def mlp_backward(grad_stream, modul, up_weight, down_weight, saved):
    norm_back, mlp_in, slope, gelu_low, down_proj = saved
    grad_down = (modul[5] * grad_stream).astype(jnp.bfloat16)
    grad_gate = jnp.sum(grad_stream * down_proj, 0)
    grad_up = (slope * matmul_nt(grad_down, down_weight)).astype(jnp.bfloat16)
    grad_part, grad_shift, grad_scale = norm_back(matmul_nt(grad_up, up_weight))
    factors = ((gelu_low, grad_down), (mlp_in, grad_up))
    return (grad_stream + grad_part, factors, (grad_shift, grad_scale, grad_gate))


def adam_update(weight, first_mom, second_mom, grad_val, learn_rate):
    first_mom = BETA_ONE * first_mom + (1.0 - BETA_ONE) * grad_val
    second_mom = BETA_TWO * second_mom + (1.0 - BETA_TWO) * grad_val * grad_val
    first_hat = first_mom / (1.0 - BETA_ONE**STEP)
    second_hat = second_mom / (1.0 - BETA_TWO**STEP)
    weight = weight - learn_rate * (first_hat / (jnp.sqrt(second_hat) + ADAM_EPS) + DECAY * weight)
    return (weight, first_mom, second_mom)

MESH = pl.DeviceIdType.MESH
ANY = pl.BlockSpec(memory_space=pl.ANY)
IN_VMEM = pl.BlockSpec(memory_space=pltpu.VMEM)
TEXT_PAD = 80


def ring_place(clip, count):
    half = clip // 2
    odd = clip % 2
    return half + odd * (count - 1 - 2 * half)


def ring_clip(place, count):
    far = place // (count // 2)
    return (1 - far) * 2 * place + far * (2 * (count - 1 - place) + 1)


def greet(peers):
    barrier = pltpu.get_barrier_semaphore()
    for peer in peers:
        pl.semaphore_signal(barrier, inc=1, device_id=peer, device_id_type=MESH)
    pl.semaphore_wait(barrier, len(peers))


def exchange_kernel(count, facts_ref, facts_out, send, recv):
    me = lax.axis_index("clip")
    band = lax.axis_index("band")
    peers = [((me + step) % count, band) for step in range(1, count)]
    greet(peers)
    sent = [
        pltpu.make_async_remote_copy(
            facts_ref, facts_out.at[me], send.at[step], recv.at[step], peer, MESH
        )
        for step, peer in enumerate(peers)
    ]
    for copy in sent:
        copy.start()
    facts_out[me] = facts_ref[...]
    for copy in sent:
        copy.wait()


def exchange_facts(facts):
    count = lax.axis_size("clip")
    return pl.pallas_call(
        partial(exchange_kernel, count),
        out_shape=jax.ShapeDtypeStruct((count,) + facts.shape, facts.dtype),
        in_specs=[IN_VMEM],
        out_specs=IN_VMEM,
        scratch_shapes=[pltpu.SemaphoreType.DMA((count - 1,))] * 2,
        compiler_params=pltpu.CompilerParams(collective_id=0, has_side_effects=True),
    )(facts)


def gather_kernel(count, picks, sides, *refs):
    num = len(picks)
    packs, vec_ref, text_ref = refs[:2], refs[2], refs[3]
    full, (vec_out, text_out, kv_out) = refs[4 : 4 + num], refs[4 + num : 7 + num]
    refs = refs[7 + num :]
    wide, shards = refs[:num], refs[num : 2 * num]
    ring_send, ring_recv, pair_send, pair_recv, cross_send, cross_recv = refs[2 * num : 2 * num + 6]
    load_sem, own_sem, part_send, part_recv, part_own = refs[2 * num + 6 : 2 * num + 11]
    kv_wide, kv_part, kv_put, kv_got, kv_sum, kv_load, kv_send, kv_recv, band_send, band_recv = refs[
        2 * num + 11 : 2 * num + 21
    ]
    share_send, share_recv = refs[2 * num + 21 :]
    shapes = [(packs[pack].shape[0], cols) for pack, _, cols in picks]
    loads = [
        pltpu.make_async_copy(
            packs[pack].at[:, pl.ds(start, cols)], wide[group], load_sem.at[group]
        )
        for group, (pack, start, cols) in enumerate(picks)
    ]
    kv_width = kv_wide.shape[1]
    kv_first = D + lax.axis_index("band") * kv_width
    kv_weight = pltpu.make_async_copy(
        packs[1].at[:, pl.ds(pl.multiple_of(kv_first, 128), kv_width)], kv_wide, kv_load
    )
    for copy in loads + [kv_weight]:
        copy.start()
    me = lax.axis_index("clip")
    band = lax.axis_index("band")
    core = band % 2
    place = ring_place(me, count)
    onward = 1 - 2 * core
    following = (ring_clip((place + onward + count) % count, count), band)
    plane = band // 2
    partner = (me, band + 1 - 2 * core)
    mirror = (me, band + 2 - 4 * plane)
    peers = [((me + step) % count, band) for step in range(1, count)]
    band_count = 2 * D // kv_width
    band_peers = [(me, (band + step) % band_count) for step in range(1, band_count)]
    greet(peers + band_peers)

    def block(ref, group, owner):
        rows, cols = shapes[group]
        return ref.at[
            pl.ds(pl.multiple_of(owner * rows, rows), rows),
            pl.ds(pl.multiple_of(core * (cols // 2), 128), cols // 2),
        ]

    def ring_copy(group, step):
        owner = ring_clip((place - onward * step + 2 * count) % count, count)
        there = block(full[group], group, owner)
        return pltpu.make_async_remote_copy(
            there, there, ring_send.at[step, group], ring_recv.at[step, group], following, MESH
        )

    def handed(group, step, send, recv, peer):
        owner = ring_clip((place - onward * (step + 1) + 2 * count) % count, count)
        there = block(full[group], group, owner)
        return pltpu.make_async_remote_copy(
            there, there, send.at[step, group], recv.at[step, group], peer, MESH
        )

    def pair_copy(group, step):
        return handed(group, step, pair_send, pair_recv, partner)

    def cross_copy(group, step):
        return handed(group, step, cross_send, cross_recv, mirror)

    def in_ring(group):
        def decorate(body):
            if sides[group]:
                pl.when(plane == sides[group] - 1)(body)
            else:
                body()

        return decorate

    def off_ring(group, also=None):
        def decorate(body):
            if sides[group]:
                off = plane != sides[group] - 1
                pl.when(off if also is None else jnp.logical_and(off, also))(body)

        return decorate

    def ring_arrival(group, step, onto):
        ring_copy(group, step).wait_recv()
        if onto:
            ring_copy(group, step + 1).start()
        pair_copy(group, step).start()
        if sides[group]:
            cross_copy(group, step).start()

    def cross_arrival(group, step):
        cross_copy(group, step).wait_recv()
        pair_copy(group, step).start()

    def own_copy(group):
        rows, cols = shapes[group]
        return pltpu.make_async_copy(
            shards[group],
            full[group].at[pl.ds(pl.multiple_of(me * rows, rows), rows), :],
            own_sem.at[group],
        )

    parts = []
    for step, peer in enumerate(peers):
        for which, (src, dst) in enumerate(((vec_ref, vec_out), (text_ref, text_out))):
            parts.append(
                pltpu.make_async_remote_copy(
                    src.at[peer[0], band],
                    dst.at[me, band],
                    part_send.at[which, step],
                    part_recv.at[which, step],
                    peer,
                    MESH,
                )
            )
    parts_own = [
        pltpu.make_async_copy(src.at[me, band], dst.at[me, band], part_own.at[which])
        for which, (src, dst) in enumerate(((vec_ref, vec_out), (text_ref, text_out)))
    ]
    for copy in parts_own + parts:
        copy.start()
    for group in range(num):
        rows, cols = shapes[group]
        loads[group].wait()
        shards[group][...] = wide[group][...].astype(jnp.bfloat16)
        own_copy(group).start()

        @in_ring(group)
        def _(group=group, rows=rows, cols=cols):
            pltpu.make_async_remote_copy(
                shards[group].at[:, pl.ds(pl.multiple_of(core * (cols // 2), 128), cols // 2)],
                block(full[group], group, me),
                ring_send.at[0, group],
                ring_recv.at[0, group],
                following,
                MESH,
            ).start()

    def kv_copy(hop):
        return pltpu.make_async_remote_copy(
            kv_put.at[hop], kv_got.at[hop], kv_send.at[hop], kv_recv.at[hop], following, MESH
        )

    def kv_hop(hop):
        owner = ring_clip((place - onward * (hop + 1) + 2 * count) % count, count)
        total = kv_part[owner]
        if not isinstance(hop, int) or hop > 0:
            kv_copy(hop - 1).wait_recv()
            total = total + kv_got[hop - 1]
        kv_put[hop] = total
        kv_copy(hop).start()

    def band_copies():
        return [
            pltpu.make_async_remote_copy(
                kv_sum, kv_out.at[band], band_send.at[step], band_recv.at[step], peer, MESH
            )
            for step, peer in enumerate(band_peers)
        ]

    shares = [
        pltpu.make_async_remote_copy(
            out.at[:, band],
            out.at[:, band],
            share_send.at[which, step],
            share_recv.at[which, step],
            peer,
            MESH,
        )
        for step, peer in enumerate(band_peers)
        for which, out in enumerate((vec_out, text_out))
    ]

    def share():
        for copy in parts_own + parts:
            copy.wait()
        for copy in shares:
            copy.start()

    def multiply():
        for copy in shares:
            copy.wait()
        kv_weight.wait()
        weight = kv_wide[...].astype(jnp.bfloat16)
        depth = weight.shape[0] // band_count
        for owner in range(count):
            kv_part[owner] = sum(
                matmul(text_out[owner, part], weight[part * depth : (part + 1) * depth])
                for part in range(band_count)
            )
        kv_hop(0)

    @pl.loop(1, count - 1)
    def _(step):
        for group in range(num):

            @in_ring(group)
            def _(group=group):
                ring_arrival(group, step - 1, True)

        pl.when(step == 1)(share)
        pl.when(step == 2)(multiply)

        @pl.when(step >= 3)
        def _():
            kv_hop(step - 2)
        for group in range(num):

            @off_ring(group, step >= 2)
            def _(group=group):
                cross_arrival(group, step - 2)

    for group in range(num):

        @in_ring(group)
        def _(group=group):
            ring_arrival(group, count - 2, False)

    kv_hop(count - 3)
    for late in (count - 3, count - 2):
        for group in range(num):

            @off_ring(group)
            def _(group=group, late=late):
                cross_arrival(group, late)

        if late == count - 3:
            kv_hop(count - 2)
    kv_copy(count - 2).wait_recv()
    kv_sum[...] = (kv_part[me] + kv_got[count - 2]).astype(jnp.bfloat16)
    kv_out[band] = kv_sum[...]
    for copy in band_copies():
        copy.start()
    for group in range(num):
        own_copy(group).wait()

    @pl.loop(0, count - 1)
    def _(step):
        for group in range(num):

            @in_ring(group)
            def _(group=group):
                ring_copy(group, step).wait_send()
                if sides[group]:
                    cross_copy(group, step).wait_send()

            pair_copy(group, step).wait()
        kv_copy(step).wait_send()

    for copy in band_copies():
        copy.wait()


def gather_quarters(shard):
    band_count = lax.axis_size("band")
    rows = shard.shape[0] // band_count
    own = lax.dynamic_slice_in_dim(shard, lax.axis_index("band") * rows, rows, 0)
    return lax.all_gather(own.astype(jnp.bfloat16), ("clip", "band"), axis=0, tiled=True)


def sum_rows(left, right):
    part = lax.psum_scatter(
        matmul_tn(left, right), ("clip", "band"), scatter_dimension=0, tiled=True
    )
    return lax.all_gather(part, "band", axis=0, tiled=True)


def gather_weights(packs, picks, sides, vectors, texts):
    count, band_count = lax.axis_size("clip"), lax.axis_size("band")
    num = len(picks)
    dma = pltpu.SemaphoreType.DMA
    shapes = [(packs[pack].shape[0], cols) for pack, _, cols in picks]
    kv_shape = (texts.shape[2], 2 * D // band_count)
    kv_all = pltpu.VMEM((count,) + kv_shape, jnp.float32)
    kv_hops = pltpu.VMEM((count - 1,) + kv_shape, jnp.float32)
    out = pl.pallas_call(
        partial(gather_kernel, count, picks, sides),
        out_shape=tuple(
            jax.ShapeDtypeStruct((count * rows, cols), jnp.bfloat16) for rows, cols in shapes
        )
        + tuple(jax.ShapeDtypeStruct(v.shape, v.dtype) for v in (vectors, texts))
        + (jax.ShapeDtypeStruct((band_count,) + kv_shape, jnp.bfloat16),),
        in_specs=[ANY] * 4,
        out_specs=(ANY,) * num + (IN_VMEM,) * 3,
        scratch_shapes=[pltpu.VMEM(shape, jnp.float32) for shape in shapes]
        + [pltpu.VMEM(shape, jnp.bfloat16) for shape in shapes]
        + [dma((count - 1, num))] * 6
        + [dma((num,)), dma((num,)), dma((2, count - 1)), dma((2, count - 1)), dma((2,))]
        + [
            pltpu.VMEM((packs[1].shape[0], kv_shape[1]), jnp.float32),
            kv_all,
            kv_hops,
            kv_hops,
            pltpu.VMEM(kv_shape, jnp.bfloat16),
            dma,
            dma((count - 1,)),
            dma((count - 1,)),
            dma((band_count - 1,)),
            dma((band_count - 1,)),
            dma((2, band_count - 1)),
            dma((2, band_count - 1)),
        ],
        compiler_params=pltpu.CompilerParams(
            collective_id=1, has_side_effects=True, vmem_limit_bytes=50 << 20
        ),
        cost_estimate=pl.CostEstimate(flops=2 * 10**11, bytes_accessed=6 * 10**8, transcendentals=0),
    )(*packs, vectors, texts)
    return out[:num], out[num], out[num + 1], out[num + 2]


WIRE_MAX = 32767.0
WIRE_LEAST = 1e-30
UNIT = (128, 512)


SPLIT = 2


def unit_parts(at, kind, first):
    if at == 0:
        return ((0, 4, lambda u: u, lambda u: 0), (4, SPLIT, lambda u: 4, lambda u: u - 3))
    if kind == 0:
        return ((0, 4, lambda u: u, lambda u: 0), (4, 4, lambda u: 4, lambda u: u - 3))
    if first:
        return ((2, 2, lambda u: u, lambda u: u), (4, 2, lambda u: 3, lambda u: u))
    return ((0, 3, lambda u: u, lambda u: u), (3, 3, lambda u: 3, lambda u: u))


def reduce_kernel(count, tokens, phases, *refs):
    num = sum(len(phase["lefts"]) for phase in phases)
    lefts, rights = refs[:num], refs[num : 2 * num]
    vec_ref, kv_ref, text_ref = refs[2 * num : 2 * num + 3]
    refs = refs[2 * num + 3 :]
    wide_out, deep_out, square_out, all_vec, kv_square = refs[:5]
    left_far, right_far = refs[5 : 5 + num], refs[5 + num : 5 + 2 * num]
    scratch = refs[5 + 2 * num :]
    left_buf, right_buf, got_low, got_scale, put_low, put_scale, plane_put = (
        scratch[2 * i : 2 * i + 2] for i in range(7)
    )
    plane_got = scratch[14 : 14 + len(phases)]
    (
        square_buf,
        left_sem,
        right_sem,
        pair_send,
        pair_recv,
        half_send,
        half_recv,
        ring_send,
        ring_recv,
        credit,
        plane_send,
        plane_recv,
        out_sem,
        out_send,
        out_recv,
        last_put,
        last_put_scale,
        last_got,
        last_got_scale,
        push_send,
        push_recv,
        cross_put,
        cross_put_scale,
        cross_got,
        cross_got_scale,
        cross_send,
        cross_recv,
        cross_credit,
        vec_got,
        kv_got,
        vec_sum,
        all_kv,
        all_kv_scale,
        text_buf,
        kv_grad,
        side_own,
        side_send,
        side_recv,
        vec_send,
        vec_recv,
        vec_pair_send,
        vec_pair_recv,
        kv_own,
        kv_send,
        kv_recv,
    ) = scratch[14 + len(phases) :]
    me = lax.axis_index("clip")
    band = lax.axis_index("band")
    core = band % 2
    plane = band // 2
    place = ring_place(me, count)
    onward = 1 - 2 * core
    following = (ring_clip((place + onward + count) % count, count), band)
    preceding = (ring_clip((place - onward + count) % count, count), band)
    partner = (me, band + 1 - 2 * core)
    mirror = (me, band + 2 - 4 * plane)
    band_count = vec_got.shape[0]
    band_peers = [(me, (band + step) % band_count) for step in range(1, band_count)]
    greet([following, preceding] + band_peers)

    def owner_at(step, way):
        return ring_clip((place - way * (step + 1) + 2 * count) % count, count)

    def left_blocks(at):
        phase = phases[at]
        if phase["kind"] == 0:
            return [(b, phase["lefts"][0], b, 4) for b in range(4)] + [(4, phase["lefts"][1], 0, 1)]
        first = phase["first"]
        return [(first + i, left, 0, 1) for i, left in enumerate(phase["lefts"])]

    def right_blocks(at):
        phase = phases[at]
        if phase["kind"] == 0:
            return [(0, phase["lefts"][0], 0)] + [(1 + i, phase["lefts"][1], i) for i in range(4)]
        first = phase["first"]
        return [(first + i, phase["lefts"][i], 0) for i in range(3 - first)] + [
            (3 + i, phase["lefts"][-1], i) for i in range(3)
        ]

    def left_cols(step, way, which, many):
        width = lefts_width // count if many == 1 else deep_width // count
        start = owner_at(step, way) * width + which * 128
        return pl.ds(pl.multiple_of(start, 128), 128)

    lefts_width = lefts[phases[1]["lefts"][0]].shape[1]
    deep_width = lefts[phases[0]["lefts"][0]].shape[1]

    def pair_left(at, step):
        out = []
        for block, operand, which, many in left_blocks(at):
            cols = left_cols(step, -onward, which, many)
            out.append(
                pltpu.make_async_remote_copy(
                    lefts[operand].at[:, cols],
                    left_far[operand].at[:, cols],
                    pair_send.at[at, block, step],
                    pair_recv.at[at, block, step],
                    partner,
                    MESH,
                )
            )
        return out

    def pair_right(at):
        out = []
        for i, operand in enumerate(phases[at]["lefts"]):
            half = rights[operand].shape[1] // 2
            out.append(
                pltpu.make_async_remote_copy(
                    rights[operand].at[:, pl.ds(pl.multiple_of((1 - core) * half, 128), half)],
                    right_far[operand],
                    half_send.at[operand],
                    half_recv.at[operand],
                    partner,
                    MESH,
                )
            )
        return out

    def load_left(at, step, slot, far):
        kind = phases[at]["kind"]
        out = []
        for block, operand, which, many in left_blocks(at):
            cols = left_cols(step, onward, which, many)
            source = left_far if far else lefts
            out.append(
                pltpu.make_async_copy(
                    source[operand].at[:, cols],
                    left_buf[kind].at[slot, block, pl.ds(far * tokens, tokens), :],
                    left_sem.at[kind, slot, block, far],
                )
            )
        return out

    def load_right(at, far):
        kind = phases[at]["kind"]
        out = []
        for block, operand, which in right_blocks(at):
            if far:
                source = right_far[operand].at[:, pl.ds(which * UNIT[1], UNIT[1])]
            else:
                half = rights[operand].shape[1] // 2
                start = pl.multiple_of(core * half + which * UNIT[1], 128)
                source = rights[operand].at[:, pl.ds(start, UNIT[1])]
            out.append(
                pltpu.make_async_copy(
                    source,
                    right_buf[kind].at[block, pl.ds(far * tokens, tokens), :],
                    right_sem.at[kind, block, far],
                )
            )
        return out

    def ring_copies(at, part, slot):
        kind = phases[at]["kind"]
        units = pl.ds(*unit_parts(at, kind, phases[at]["first"])[part][:2])
        return [
            pltpu.make_async_remote_copy(
                put.at[slot, units],
                got.at[slot, units],
                ring_send.at[kind, slot, part, i],
                ring_recv.at[kind, slot, part, i],
                following,
                MESH,
            )
            for i, (put, got) in enumerate(
                ((put_low[kind], got_low[kind]), (put_scale[kind], got_scale[kind]))
            )
        ]

    def plane_copies(at, part):
        kind = phases[at]["kind"]
        units = pl.ds(*unit_parts(at, kind, phases[at]["first"])[part][:2])
        pairs = ((plane_put[kind], plane_got[at]),)
        if at + 1 == len(phases):
            pairs = ((last_put, last_got), (last_put_scale, last_got_scale))
        return [
            pltpu.make_async_remote_copy(
                here.at[units],
                there.at[units],
                plane_send.at[at, part, i],
                plane_recv.at[at, part, i],
                mirror,
                MESH,
            )
            for i, (here, there) in enumerate(pairs)
        ]

    def split_unit(pair, of_plane):
        return 4 + 2 * pair + of_plane

    def split_copy(pair, of_plane):
        unit = split_unit(pair, of_plane)
        return pltpu.make_async_remote_copy(
            plane_put[0].at[unit],
            plane_got[0].at[unit],
            plane_send.at[0, 1, pair],
            plane_recv.at[0, 1, pair],
            mirror,
            MESH,
        )

    def cross_copies(slot):
        return [
            pltpu.make_async_remote_copy(
                here.at[slot], there.at[slot], cross_send.at[slot, i], cross_recv.at[slot, i], mirror, MESH
            )
            for i, (here, there) in enumerate(
                ((cross_put, cross_got), (cross_put_scale, cross_got_scale))
            )
        ]

    def push_right(block):
        operand, which = [entry[1:] for entry in right_blocks(0) if entry[0] == block][0]
        half = rights[operand].shape[1] // 2
        begin = pl.multiple_of((1 - core) * half + which * UNIT[1], 128)
        return pltpu.make_async_remote_copy(
            rights[operand].at[:, pl.ds(begin, UNIT[1])],
            right_buf[phases[0]["kind"]].at[block, pl.ds(tokens, tokens), :],
            push_send.at[block],
            push_recv.at[block],
            partner,
            MESH,
        )

    def out_copies(at, unit):
        phase = phases[at]
        if phase["kind"] == 0 and unit < 4:
            half = UNIT[1]
            rows = deep_out.shape[0] // 4
            there = deep_out.at[
                pl.ds(unit * rows, rows),
                pl.ds(pl.multiple_of(phase["cols"][0] + core * half, 128), half),
            ]
        else:
            which, col = (1, unit - 4) if phase["kind"] == 0 else (unit - phase["first"], 0)
            if phase["kind"] and unit >= 3:
                which, col = len(phase["lefts"]) - 1, unit - 3
            half = rights[phase["lefts"][which]].shape[1] // 2
            start = phase["cols"][which] + core * half + col * UNIT[1]
            there = wide_out.at[:, pl.ds(pl.multiple_of(start, 128), UNIT[1])]
        here = plane_got[at].at[unit]
        return (
            pltpu.make_async_copy(here, there, out_sem.at[at, unit]),
            pltpu.make_async_remote_copy(
                here, there, out_send.at[at, unit], out_recv.at[at, unit], partner, MESH
            ),
        )

    def product(kind, slot, left, right):
        return lax.dot_general(
            left_buf[kind][slot, left],
            right_buf[kind][right],
            (((0,), (0,)), ((), ())),
            preferred_element_type=jnp.float32,
        )

    def start(copies):
        for copy in copies:
            copy.start()

    def finish(copies):
        for copy in copies:
            copy.wait()

    def encode(term):
        largest = jnp.maximum(jnp.max(jnp.abs(term), axis=0, keepdims=True), WIRE_LEAST)
        low = jnp.round(term * (WIRE_MAX / largest)).astype(jnp.int16)
        return low, largest * (1.0 / WIRE_MAX)

    def take_step(at, step, first, last):
        phase = phases[at]
        kind = phase["kind"]
        slot = step % 2
        before = (step + 1) % 2
        for far in range(2):
            finish(load_left(at, step, slot, far))

        def load_next():
            for copy in pair_left(at, step + 1):
                copy.wait_recv()
            for far in range(2):
                start(load_left(at, step + 1, before, far))

        opening = first and at == 0
        if not (last or opening):
            load_next()
        parts = unit_parts(at, kind, phase["first"])

        def send_theirs():
            def spend():
                for copy in cross_copies(slot):
                    copy.wait_send()
                pl.semaphore_wait(cross_credit, 1)

            if last:
                spend()
            elif not first:
                pl.when(step >= 2)(spend)
            for pair in range(SPLIT):
                unit = split_unit(pair, 1 - plane)
                term = product(kind, slot, parts[1][2](unit), parts[1][3](unit))
                cross_put[slot, pair], cross_put_scale[slot, pair] = encode(term)
            start(cross_copies(slot))

        if at == 0 and not opening:
            send_theirs()
        for part, (low, many, left_of, right_of) in enumerate(parts):
            if opening:
                blocks = range(1) if part == 0 else range(1, 5)
                finish(load_right(0, 0)[blocks.start : blocks.stop])
                for block in blocks:
                    push_right(block).wait_recv()
                if part:
                    send_theirs()
            if not first:
                for copy in ring_copies(at, part, before):
                    copy.wait_recv()
            if not (first or last):

                @pl.when(step >= 2)
                def _(part=part):
                    for copy in ring_copies(at, part, slot):
                        copy.wait_send()
                    pl.semaphore_wait(credit.at[kind, part], 1)

            def settle(position, unit, term):
                if not first:
                    came = got_low[kind][before, position].astype(jnp.float32)
                    term = term + came * got_scale[kind][before, position]
                if last and at + 1 == len(phases):
                    last_put[unit], last_put_scale[unit] = encode(term)
                elif last:
                    plane_put[kind][unit] = term
                else:
                    low_part, scale_part = encode(term)
                    put_low[kind][slot, position] = low_part
                    put_scale[kind][slot, position] = scale_part

            split = at == 0 and part == 1
            if split:
                for copy in cross_copies(slot):
                    copy.wait_recv()

            @pl.loop(low, low + many)
            def _(position, left_of=left_of, right_of=right_of):
                unit = split_unit(position - 4, plane) if split else position
                term = product(kind, slot, left_of(unit), right_of(unit))
                if split:
                    came = cross_got[slot, position - 4].astype(jnp.float32)
                    term = term + came * cross_got_scale[slot, position - 4]
                settle(position, unit, term)

            if split and not last:

                def credit_cross():
                    pl.semaphore_signal(
                        cross_credit, inc=1, device_id=mirror, device_id_type=MESH
                    )

                if first:
                    credit_cross()
                else:
                    pl.when(step < count - 2)(credit_cross)

            if last and split:
                start([split_copy(pair, plane) for pair in range(SPLIT)])
            elif last:
                start(plane_copies(at, part))
            else:
                start(ring_copies(at, part, slot))
            if not (first or last):

                @pl.when(step < count - 2)
                def _(part=part):
                    pl.semaphore_signal(
                        credit.at[kind, part], inc=1, device_id=preceding, device_id_type=MESH
                    )

        if opening:
            load_next()

    def close(at):
        kind = phases[at]["kind"]

        def add_square(total):
            square_buf[...] += jnp.sum((total * total).reshape(UNIT[0] // 8, 8, UNIT[1]), axis=0)

        for part, (low, many, _, _) in enumerate(unit_parts(at, kind, phases[at]["first"])):
            if at == 0 and part == 1:
                for pair in range(SPLIT):
                    split_copy(pair, plane).wait_send()
                    split_copy(pair, 1 - plane).wait_recv()
                    ours = split_unit(pair, plane)
                    plane_got[0][ours] = plane_put[0][ours]
                for unit in range(4, 8):
                    add_square(plane_got[0][unit])
                    start(out_copies(0, unit))
                continue
            finish(plane_copies(at, part))

            @pl.loop(low, low + many)
            def _(unit):
                if at + 1 == len(phases):
                    total = last_put[unit].astype(jnp.float32) * last_put_scale[unit]
                    total += last_got[unit].astype(jnp.float32) * last_got_scale[unit]
                else:
                    total = plane_put[kind][unit] + plane_got[at][unit]
                plane_got[at][unit] = total
                add_square(total)

            for unit in range(low, low + many):
                start(out_copies(at, unit))

    half_rows = pl.ds(pl.multiple_of(core * (vec_sum.shape[0] // 2), 8), vec_sum.shape[0] // 2)
    side_local = [
        pltpu.make_async_copy(vec_ref, vec_got.at[band], side_own.at[0]),
        pltpu.make_async_copy(kv_ref.at[band], kv_got.at[band], side_own.at[1]),
        pltpu.make_async_copy(text_ref, text_buf, side_own.at[2]),
    ]
    side_remote = []
    for step, peer in enumerate(band_peers):
        side_remote += [
            pltpu.make_async_remote_copy(
                vec_ref, vec_got.at[band], side_send.at[0, step], side_recv.at[0, step], peer, MESH
            ),
            pltpu.make_async_remote_copy(
                kv_ref.at[peer[1]],
                kv_got.at[band],
                side_send.at[1, step],
                side_recv.at[1, step],
                peer,
                MESH,
            ),
        ]
    vec_own = pltpu.make_async_copy(vec_sum, all_vec.at[me], side_own.at[3])

    def kv_parts(owner):
        return [(ref.at[owner], ref.at[owner]) for ref in (all_kv, all_kv_scale)]

    def vec_copies(step):
        owner = ring_clip((place - onward * step + 2 * count) % count, count)
        vec = all_vec.at[owner, half_rows]
        return [
            pltpu.make_async_remote_copy(
                here, there, vec_send.at[step, i], vec_recv.at[step, i], following, MESH
            )
            for i, (here, there) in enumerate([(vec, vec)] + kv_parts(owner))
        ]

    def vec_first():
        vec = all_vec.at[me, half_rows]
        return [
            pltpu.make_async_remote_copy(
                here, there, vec_send.at[0, i], vec_recv.at[0, i], following, MESH
            )
            for i, (here, there) in enumerate([(vec_sum.at[half_rows], vec)] + kv_parts(me))
        ]

    def vec_pair(step):
        owner = ring_clip((place - onward * (step + 1) + 2 * count) % count, count)
        vec = all_vec.at[owner, half_rows]
        return pltpu.make_async_remote_copy(
            vec, vec, vec_pair_send.at[step], vec_pair_recv.at[step], partner, MESH
        )

    kv_width = kv_grad.shape[1]

    def kv_place(owner):
        return deep_out.at[:, pl.ds(pl.multiple_of(D + owner * kv_width, 128), kv_width)]

    def kv_copy(i):
        if i == 2:
            return pltpu.make_async_copy(kv_grad, kv_place(band), kv_own)
        peer = (partner, mirror)[i]
        return pltpu.make_async_remote_copy(
            kv_grad, kv_place(band), kv_send.at[i], kv_recv.at[i], peer, MESH
        )

    def kv_passed():
        there = kv_place(mirror[1])
        return pltpu.make_async_remote_copy(
            there, there, kv_send.at[2], kv_recv.at[2], partner, MESH
        )

    def sum_bands():
        finish(side_local + side_remote)
        vec_sum[...] = jnp.sum(vec_got[...], 0)
        all_kv[me], all_kv_scale[me] = encode(jnp.sum(kv_got[...], 0))
        vec_own.start()
        start(vec_first())

    def pass_sums(step):
        for copy in vec_copies(step - 1):
            copy.wait_recv()
        start(vec_copies(step))
        vec_pair(step - 1).start()

    def multiply_text():
        for copy in vec_copies(count - 2):
            copy.wait_recv()
        vec_pair(count - 2).start()
        grads = all_kv[...].astype(jnp.float32) * all_kv_scale[...]
        grads = grads.reshape(text_buf.shape[0], -1)
        total = jnp.zeros_like(kv_grad)
        for _ in range(3):
            part = grads.astype(jnp.bfloat16)
            grads = grads - part.astype(jnp.float32)
            total = total + matmul_tn(text_buf[...], part)
        kv_grad[...] = total
        kv_square[...] = jnp.sum((total * total).reshape(-1, 8, total.shape[1]), axis=0)
        start([kv_copy(i) for i in range(3)])

    square_buf[...] = jnp.zeros_like(square_buf)
    start(side_local + side_remote)
    start(load_right(0, 0))
    start(load_left(0, 0, 0, 0))
    push_right(0).start()
    start(pair_left(0, 0))
    for block in range(1, 5):
        push_right(block).start()

    @pl.loop(1, count)
    def _(step):
        start(pair_left(0, step))

    for copy in pair_left(0, 0):
        copy.wait_recv()
    start(load_left(0, 0, 0, 1))
    take_step(0, 0, True, False)
    for at in range(len(phases)):
        more = at + 1 < len(phases)
        if more:
            start(pair_right(at + 1))
            start(load_right(at + 1, 0))
            start(pair_left(at + 1, 0))
        if at == 1:
            sum_bands()

        @pl.loop(1, count - 1)
        def _(step, at=at, more=more):
            take_step(at, step, False, False)
            if at == 1:
                pass_sums(step)
            if more:
                start(pair_left(at + 1, step))

                @pl.when(step == count // 2)
                def _():
                    for copy in pair_right(at + 1):
                        copy.wait_recv()
                    start(load_right(at + 1, 1))
                    for copy in pair_left(at + 1, 0):
                        copy.wait_recv()
                    for far in range(2):
                        start(load_left(at + 1, 0, 0, far))

        if more:
            start(pair_left(at + 1, count - 1))
            for far in range(2):
                finish(load_right(at + 1, far))
            take_step(at + 1, 0, True, False)
        take_step(at, count - 1, False, True)
        if at == 1:
            multiply_text()
        for slot in range(2):
            for part in range(2):
                for copy in ring_copies(at, part, slot):
                    copy.wait_send()
            if at == 0:
                for copy in cross_copies(slot):
                    copy.wait_send()
        if at == 2:
            kv_copy(1).wait_recv()
            kv_passed().start()
        if at:
            close(at - 1)
    close(len(phases) - 1)
    vec_own.wait()
    kv_passed().wait()
    kv_copy(0).wait()
    kv_copy(1).wait_send()
    kv_copy(2).wait()

    @pl.loop(0, count - 1)
    def _(step):
        for copy in vec_copies(step):
            copy.wait_send()
        vec_pair(step).wait()

    square_out[...] = square_buf[...]
    for at, phase in enumerate(phases):
        for copy in pair_right(at) if at else [push_right(block) for block in range(5)]:
            copy.wait_send()

        @pl.loop(0, count)
        def _(step, at=at):
            for copy in pair_left(at, step):
                copy.wait_send()

        for unit in range(phase["first"], 8 if phase["kind"] == 0 else 6):
            finish(out_copies(at, unit))


def reduce_gradients(phases, lefts, rights, vectors, keyvals, text, wide_cols, deep_cols):
    count = lax.axis_size("clip")
    tokens = lefts[0].shape[0]
    wide_rows = lefts[1].shape[1] // count
    deep_rows = lefts[0].shape[1] // count
    band_count, _, kv_cols = keyvals.shape
    num = len(lefts)
    dma = pltpu.SemaphoreType.DMA
    units, lefts_of, rights_of = (8, 6), (5, 4), (5, 6)
    scratch = [pltpu.VMEM((2, lefts_of[k], 2 * tokens, 128), jnp.bfloat16) for k in range(2)]
    scratch += [pltpu.VMEM((rights_of[k], 2 * tokens, UNIT[1]), jnp.bfloat16) for k in range(2)]
    for _ in range(2):
        scratch += [pltpu.VMEM((2, units[k]) + UNIT, jnp.int16) for k in range(2)]
        scratch += [pltpu.VMEM((2, units[k], 1, UNIT[1]), jnp.float32) for k in range(2)]
    scratch += [pltpu.VMEM((units[k],) + UNIT, jnp.float32) for k in range(2)]
    scratch += [pltpu.VMEM((units[p["kind"]],) + UNIT, jnp.float32) for p in phases]
    scratch += [
        pltpu.VMEM((8, UNIT[1]), jnp.float32),
        dma((2, 2, 5, 2)),
        dma((2, 6, 2)),
        dma((len(phases), 5, count)),
        dma((len(phases), 5, count)),
        dma((num,)),
        dma((num,)),
        dma((2, 2, 2, 2)),
        dma((2, 2, 2, 2)),
        pltpu.SemaphoreType.REGULAR((2, 2)),
        dma((len(phases), 2, 2)),
        dma((len(phases), 2, 2)),
        dma((len(phases), 8)),
        dma((len(phases), 8)),
        dma((len(phases), 8)),
    ]
    for _ in range(2):
        scratch += [pltpu.VMEM((6,) + UNIT, jnp.int16), pltpu.VMEM((6, 1, UNIT[1]), jnp.float32)]
    scratch += [
        dma((5,)),
        dma((5,)),
        *[
            pltpu.VMEM((2, SPLIT) + tile, kind)
            for _ in range(2)
            for tile, kind in ((UNIT, jnp.int16), ((1, UNIT[1]), jnp.float32))
        ],
        dma((2, 2)),
        dma((2, 2)),
        pltpu.SemaphoreType.REGULAR,
        pltpu.VMEM((band_count,) + vectors.shape, jnp.float32),
        pltpu.VMEM(keyvals.shape, jnp.float32),
        pltpu.VMEM(vectors.shape, jnp.float32),
        pltpu.VMEM((count,) + keyvals.shape[1:], jnp.int16),
        pltpu.VMEM((count, 1, kv_cols), jnp.float32),
        pltpu.VMEM(text.shape, jnp.bfloat16),
        pltpu.VMEM((text.shape[1], kv_cols), jnp.float32),
        dma((4,)),
        dma((2, band_count - 1)),
        dma((2, band_count - 1)),
        dma((count - 1, 3)),
        dma((count - 1, 3)),
        dma((count - 1,)),
        dma((count - 1,)),
        dma,
        dma((3,)),
        dma((3,)),
    ]
    out = pl.pallas_call(
        partial(reduce_kernel, count, tokens, phases),
        out_shape=(
            jax.ShapeDtypeStruct((wide_rows, wide_cols), jnp.float32),
            jax.ShapeDtypeStruct((deep_rows, deep_cols), jnp.float32),
            jax.ShapeDtypeStruct((8, UNIT[1]), jnp.float32),
            jax.ShapeDtypeStruct((count,) + vectors.shape, jnp.float32),
            jax.ShapeDtypeStruct((8, kv_cols), jnp.float32),
        )
        + tuple(jax.ShapeDtypeStruct(x.shape, x.dtype) for x in lefts)
        + tuple(jax.ShapeDtypeStruct((tokens, x.shape[1] // 2), x.dtype) for x in rights),
        in_specs=[ANY] * (2 * num + 3),
        out_specs=(ANY, ANY, IN_VMEM, ANY, IN_VMEM) + (ANY,) * (2 * num),
        scratch_shapes=scratch,
        compiler_params=pltpu.CompilerParams(
            collective_id=2, has_side_effects=True, vmem_limit_bytes=58 << 20
        ),
        cost_estimate=pl.CostEstimate(flops=3 * 10**11, bytes_accessed=8 * 10**8, transcendentals=0),
    )(*lefts, *rights, vectors, keyvals, text)
    return out[:5]


def total_kernel(count, part_ref, out_ref, mid, band_got, clip_got, *sems):
    me = lax.axis_index("clip")
    band = lax.axis_index("band")
    band_count = band_got.shape[0]
    band_peers = [(me, (band + step) % band_count) for step in range(1, band_count)]
    clip_peers = [((me + step) % count, band) for step in range(1, count)]
    greet(band_peers + clip_peers)
    stages = (
        (part_ref, band_got, band, band_peers, mid, sems[:2]),
        (mid, clip_got, me, clip_peers, out_ref, sems[2:]),
    )
    for value, got, index, peers, result, (send, recv) in stages:
        copies = [
            pltpu.make_async_remote_copy(
                value, got.at[index], send.at[step], recv.at[step], peer, MESH
            )
            for step, peer in enumerate(peers)
        ]
        for copy in copies:
            copy.start()
        got[index] = value[...]
        for copy in copies:
            copy.wait()
        result[...] = jnp.sum(got[...], 0)


def total_over_devices(value):
    count, band_count = lax.axis_size("clip"), lax.axis_size("band")
    dma = pltpu.SemaphoreType.DMA
    tile = (8, 128)
    return pl.pallas_call(
        partial(total_kernel, count),
        out_shape=jax.ShapeDtypeStruct(tile, jnp.float32),
        in_specs=[IN_VMEM],
        out_specs=IN_VMEM,
        scratch_shapes=[
            pltpu.VMEM(tile, jnp.float32),
            pltpu.VMEM((band_count,) + tile, jnp.float32),
            pltpu.VMEM((count,) + tile, jnp.float32),
            dma((band_count - 1,)),
            dma((band_count - 1,)),
            dma((count - 1,)),
            dma((count - 1,)),
        ],
        compiler_params=pltpu.CompilerParams(collective_id=3, has_side_effects=True),
    )(jnp.broadcast_to(value, tile))[0, 0]


def per_device(
    latents,
    noise_field,
    timesteps,
    null_flags,
    frame_mask,
    context,
    w_wide,
    m_wide,
    v_wide,
    w_deep,
    m_deep,
    v_deep,
    w_small,
    m_small,
    v_small,
):
    clip_count = lax.axis_size("clip")
    band_count = lax.axis_size("band")
    clip_at = lax.axis_index("clip")
    band_at = lax.axis_index("band")
    wide_rows = w_wide.shape[0]
    deep_rows = w_deep.shape[0]
    text_len, text_dim = context.shape[1:]
    facts = jnp.pad(
        jnp.concatenate([timesteps, frame_mask[0]])[None],
        ((0, 7), (0, 127 - frame_mask.shape[1])),
    )
    kept_text = context[0] * (1 - null_flags[0]).astype(jnp.bfloat16)
    text_cols = jnp.pad(
        kept_text.reshape(text_len, clip_count, band_count, -1).transpose(1, 2, 0, 3),
        ((0, 0), (0, 0), (0, TEXT_PAD - text_len), (0, 0)),
    )
    all_facts = exchange_facts(facts)
    all_times = all_facts[:, 0, 0].astype(jnp.float32)
    all_time_low = jax.nn.silu(time_features(all_times)).astype(jnp.bfloat16)
    time_rows = lax.dynamic_slice(
        all_time_low, (0, clip_at * wide_rows), (clip_count, wide_rows)
    )
    part_modul = matmul(time_rows, w_wide[:, : 12 * D].astype(jnp.bfloat16))
    kv_cols = 2 * D // band_count
    up_b_w = gather_quarters(w_wide[:, 22 * D + FF :])
    gathered, all_modul, all_text, keyval = gather_weights(
        (w_wide, w_deep),
        (
            (0, 22 * D, FF),
            (1, 0, D),
            (0, 20 * D, D),
            (0, 21 * D, D),
            (0, 18 * D, D),
            (0, 19 * D, D),
            (0, 12 * D, 3 * D),
            (0, 15 * D, 3 * D),
        ),
        (1, 2, 1, 2, 1, 2, 0, 0),
        part_modul.reshape(clip_count, band_count, -1, 128),
        text_cols,
    )
    up_a_w, down_a_w, query_w, cross_out_w, out_a_w, out_b_w, qkv_a_w, qkv_b_w = gathered
    all_text = all_text.transpose(0, 2, 1, 3)
    keyval = keyval.transpose(1, 0, 2).reshape(TEXT_PAD, 2 * D)
    late_down_b, all_modul = lax.optimization_barrier((w_deep[:, 3 * D :], all_modul))
    down_b_w = gather_quarters(late_down_b)
    small_low = w_small.astype(jnp.bfloat16)
    small_val = small_low.astype(jnp.float32)
    num_frames, num_rows, num_cols = (latents.shape[1], latents.shape[2], latents.shape[3])
    tok_count = num_frames * num_rows * num_cols
    all_mask = all_facts[:, 0, 1 : 1 + num_frames]
    global_count = jnp.sum(all_mask).astype(jnp.float32) * (num_rows * num_cols * CH * band_count)
    time_value = timesteps[0].astype(jnp.float32)
    noise_angle = 0.5 * math.pi * time_value / TMAX
    signal, spread = (jnp.cos(noise_angle), jnp.sin(noise_angle))
    clean_tok = token_order(latents[0])
    noise_tok = token_order(noise_field[0])
    run = num_rows * WIN
    part = SHIFT * WIN
    frame_windows = attend_pieces(tok_count, num_frames, "frame")
    half_windows = attend_pieces(tok_count, num_frames, "half")
    text_windows = attend_pieces(tok_count, num_frames, "text")
    noisy_low = (signal * clean_tok + spread * noise_tok).astype(jnp.bfloat16)
    target = signal * noise_tok - spread * clean_tok
    modulation = jnp.sum(all_modul, 0).reshape(12, D)
    mod_a, mod_b = (modulation[:6], modulation[6:])
    stream_zero = matmul(noisy_low, small_low[:CH]) + small_val[2 * CH]
    normed_a, back_a = jax.vjp(norm_modulated, stream_zero, mod_a[0], mod_a[1])
    in_a = normed_a.astype(jnp.bfloat16)
    qkv_a = matmul(in_a, qkv_a_w).astype(jnp.bfloat16)
    att_a, far_kv = attend_frames(qkv_a, frame_windows)
    proj_a = matmul(att_a, out_a_w)
    stream_one = stream_zero + mod_a[2] * proj_a
    stream_two, saved_a = mlp_forward(stream_one, mod_a, up_a_w, down_a_w)
    normed_b, back_b = jax.vjp(norm_modulated, stream_two, mod_b[0], mod_b[1])
    low_b = normed_b.astype(jnp.bfloat16)
    rolled = with_rows(low_b, shifted(first_rows(low_b, run, part), "band", -1), run)
    qkv_b = matmul(rolled, qkv_b_w).astype(jnp.bfloat16)
    win_kv = [(qkv_b, HEADS // 2, HEADS)]
    win_out = attend(qkv_b, win_kv, half_windows)
    att_b = with_rows(win_out, shifted(first_rows(win_out, run, part), "band", 1), run)
    proj_b = matmul(att_b, out_b_w)
    stream_three = stream_two + mod_b[2] * proj_b
    cross_val, cross_back = jax.vjp(norm_gained, stream_three, small_val[2 * CH + 1])
    cross_in = cross_val.astype(jnp.bfloat16)
    query_proj = matmul(cross_in, query_w).astype(jnp.bfloat16)
    text_kv = [(keyval, 0, HEADS // 2)]
    crossed = attend(query_proj, text_kv, text_windows, text_len)
    stream_four = stream_three + matmul(crossed, cross_out_w)
    stream_five, saved_b = mlp_forward(stream_four, mod_b, up_b_w, down_b_w)
    final_val, final_back = jax.vjp(norm_gained, stream_five, small_val[2 * CH + 2])
    final_low = final_val.astype(jnp.bfloat16)
    head_low = small_low[CH : 2 * CH]
    predicted = matmul_nt(final_low, head_low)
    weight_row = jnp.repeat(frame_mask[0].astype(jnp.float32), run)
    weight_row = jnp.tile(weight_row, num_cols // WIN)[:, None]
    pred_error = predicted - target
    loss_part = jnp.sum(weight_row * pred_error * pred_error)
    grad_pred = (weight_row * pred_error * (2.0 / global_count)).astype(jnp.bfloat16)
    grad_head = matmul_tn(grad_pred, final_low)
    grad_stream, grad_gain_f = final_back(matmul(grad_pred, head_low))
    grad_stream, mlp_factors_b, extra_b = mlp_backward(
        grad_stream, mod_b, up_b_w, down_b_w, saved_b
    )
    grad_cross = grad_stream.astype(jnp.bfloat16)
    grad_crossed = matmul_nt(grad_cross, cross_out_w).astype(jnp.bfloat16)
    grad_query, grad_keyval = attend_back(
        query_proj, text_kv, grad_crossed, text_windows, text_len
    )
    grad_part, grad_gain_c = cross_back(matmul_nt(grad_query, query_w))
    grad_stream = grad_stream + grad_part
    grad_proj = (mod_b[2] * grad_stream).astype(jnp.bfloat16)
    grad_gate_b = jnp.sum(grad_stream * proj_b, 0)
    factors_ob = (att_b, grad_proj)
    grad_att = matmul_nt(grad_proj, out_b_w).astype(jnp.bfloat16)
    grad_win = with_rows(grad_att, shifted(first_rows(grad_att, run, part), "band", -1), run)
    grad_qkv = attend_back(qkv_b, win_kv, grad_win, half_windows)[0]
    factors_qkvb = (rolled, grad_qkv)
    grad_in_roll = matmul_nt(grad_qkv, qkv_b_w)
    sent_back = shifted(first_rows(grad_in_roll, run, part), "band", 1)
    grad_normed = with_rows(grad_in_roll, sent_back, run)
    grad_part, grad_shift_b, grad_scale_b = back_b(grad_normed)
    grad_stream = grad_stream + grad_part
    grad_stream, mlp_factors_a, extra_a = mlp_backward(
        grad_stream, mod_a, up_a_w, down_a_w, saved_a
    )
    grad_proj = (mod_a[2] * grad_stream).astype(jnp.bfloat16)
    grad_gate_a = jnp.sum(grad_stream * proj_a, 0)
    factors_oa = (att_a, grad_proj)
    grad_att = matmul_nt(grad_proj, out_a_w).astype(jnp.bfloat16)
    grad_qkv = attend_frames_back(qkv_a, far_kv, grad_att, frame_windows)
    factors_qkva = (in_a, grad_qkv)
    grad_part, grad_shift_a, grad_scale_a = back_a(matmul_nt(grad_qkv, qkv_a_w))
    grad_stream = grad_stream + grad_part
    grad_patch = matmul_tn(noisy_low.astype(jnp.float32), grad_stream, lax.Precision.HIGHEST)
    grad_bias = jnp.sum(grad_stream, 0)
    grad_modul = jnp.stack(
        [
            grad_shift_a,
            grad_scale_a,
            grad_gate_a,
            extra_a[0],
            extra_a[1],
            extra_a[2],
            grad_shift_b,
            grad_scale_b,
            grad_gate_b,
            extra_b[0],
            extra_b[1],
            extra_b[2],
        ]
    ).reshape(1, 12 * D)
    grad_small = jnp.concatenate(
        [grad_patch, grad_head, grad_bias[None], grad_gain_c[None], grad_gain_f[None]], 0
    )
    factors = mlp_factors_b + (
        (crossed, grad_cross),
        (cross_in, grad_query),
        factors_ob,
        factors_qkvb,
    )
    factors += mlp_factors_a + (factors_oa, factors_qkva)
    if wide_rows == 128 and deep_rows == 512:
        phases = (
            {"kind": 0, "first": 0, "lefts": (0, 1), "cols": (3 * D, 10 * D + FF)},
            {"kind": 1, "first": 0, "lefts": (2, 3, 4, 5), "cols": (9 * D, 8 * D, 7 * D, 3 * D)},
            {"kind": 0, "first": 0, "lefts": (6, 7), "cols": (0, 10 * D)},
            {"kind": 1, "first": 2, "lefts": (8, 9), "cols": (6 * D, 0)},
        )
        used = 12 * D + grad_small.size
        vectors = jnp.concatenate(
            [grad_modul.reshape(-1), grad_small.reshape(-1), loss_part[None]]
        )
        vectors = jnp.pad(vectors, (0, 256 * 128 - vectors.shape[0])).reshape(256, 128)
        keyvals = grad_keyval.reshape(TEXT_PAD, band_count, kv_cols).transpose(1, 0, 2)
        wide_rest, deep_sum, squares, all_vectors, kv_squares = reduce_gradients(
            phases,
            [f[0] for f in factors],
            [f[1] for f in factors],
            vectors,
            keyvals,
            all_text.reshape(clip_count * TEXT_PAD, deep_rows),
            10 * D + 2 * FF,
            4 * D,
        )
        all_vectors = all_vectors.reshape(clip_count, -1)
        all_grad_modul = all_vectors[:, : 12 * D]
        small_sum = jnp.sum(all_vectors[:, 12 * D : used], 0).reshape(grad_small.shape)
        loss_sum = jnp.sum(all_vectors[:, used])
        square_part = jnp.sum(squares) / (band_count // 2) + jnp.sum(kv_squares)
    else:
        summed = [sum_rows(*pair) for pair in factors]
        wide_rest = jnp.concatenate([summed[i] for i in (9, 5, 8, 4, 3, 2, 7, 1)], 1)
        grad_keyval = lax.psum_scatter(grad_keyval, "band", scatter_dimension=1, tiled=True)
        grad_keyval = lax.all_gather(grad_keyval, "clip", axis=0, tiled=True)
        grad_w_ckv = matmul_tn(
            all_text.reshape(clip_count * TEXT_PAD, deep_rows).astype(jnp.float32),
            grad_keyval,
            lax.Precision.HIGHEST,
        )
        grad_w_ckv = lax.all_gather(grad_w_ckv, "band", axis=1, tiled=True)
        all_grad_modul = lax.all_gather(lax.psum(grad_modul, "band"), "clip", axis=0, tiled=True)
        loss_sum, small_sum = lax.psum((loss_part, grad_small), ("clip", "band"))
        deep_sum = jnp.concatenate([summed[6], grad_w_ckv, summed[0]], 1)
        square_part = sum(jnp.sum(x * x) for x in (wide_rest, deep_sum)) / band_count
    grad_w_ada = matmul_tn(time_rows.astype(jnp.float32), all_grad_modul, lax.Precision.HIGHEST)
    wide_sum = jnp.concatenate([grad_w_ada, wide_rest], 1)
    square_part += jnp.sum(grad_w_ada * grad_w_ada) / band_count
    square_sum = total_over_devices(square_part)
    grad_norm = jnp.sqrt(square_sum + jnp.sum(small_sum * small_sum))
    factor = CLIP_MAX / jnp.maximum(grad_norm, CLIP_MAX)
    new_wide = adam_update(w_wide, m_wide, v_wide, wide_sum * factor, 0.15)
    new_deep = adam_update(w_deep, m_deep, v_deep, deep_sum * factor, 0.05)
    new_small = adam_update(w_small, m_small, v_small, small_sum * factor, 0.5)
    loss = loss_sum / global_count
    return (
        loss,
        grad_norm,
        new_wide[0],
        new_wide[1],
        new_wide[2],
        new_deep[0],
        new_deep[1],
        new_deep[2],
        new_small[0],
        new_small[1],
        new_small[2],
    )


def solution(mesh):
    in_specs = (
        P("clip", None, "band", None, None),
        P("clip", None, "band", None, None),
        P("clip"),
        P("clip"),
        P("clip", None),
        P("clip", None, None),
        P("clip", None),
        P("clip", None),
        P("clip", None),
        P("clip", None),
        P("clip", None),
        P("clip", None),
        P(),
        P(),
        P(),
    )
    out_specs = (
        P(),
        P(),
        P("clip", None),
        P("clip", None),
        P("clip", None),
        P("clip", None),
        P("clip", None),
        P("clip", None),
        P(),
        P(),
        P(),
    )
    return jax.shard_map(
        per_device, mesh=mesh, in_specs=in_specs, out_specs=out_specs, check_vma=False
    )
```

```python
from functools import partial
import math

import jax
import jax.numpy as jnp
from jax import lax
from jax.experimental import pallas as pl
from jax.experimental.pallas import tpu as pltpu
from jax.sharding import PartitionSpec as P

D = 1024
HEADS = 16
HEAD_DIM = 64
FF = 4096
CH = 8
SPACE = 16
WIN = 8
SHIFT = 4
TMAX = 1000
STEP = 10


EPS_NORM = 1e-06
CLIP_MAX = 0.001
BETA_ONE = 0.9
BETA_TWO = 0.95
ADAM_EPS = 1e-08
DECAY = 0.1


def shifted(value, axis, by):
    length = lax.axis_size(axis)
    return lax.ppermute(value, axis, [(i, (i + by) % length) for i in range(length)])


def matmul(left_op, right_op):
    return jnp.dot(left_op, right_op, preferred_element_type=jnp.float32)


def matmul_tn(left_op, right_op, precision=None):
    return lax.dot_general(
        left_op,
        right_op,
        (((0,), (0,)), ((), ())),
        precision=precision,
        preferred_element_type=jnp.float32,
    )


def matmul_nt(left_op, right_op):
    return lax.dot_general(
        left_op, right_op, (((1,), (1,)), ((), ())), preferred_element_type=jnp.float32
    )


def layer_norm(field_in):
    average = jnp.mean(field_in, -1, keepdims=True)
    centred = field_in - average
    return centred * lax.rsqrt(jnp.mean(centred * centred, -1, keepdims=True) + EPS_NORM)


def norm_modulated(field_in, shift_vec, scale_vec):
    return layer_norm(field_in) * (1.0 + scale_vec) + shift_vec


def norm_gained(field_in, gain_vec):
    return layer_norm(field_in) * gain_vec


def time_features(time_value):
    half_width = D // 2
    frequency = jnp.exp(-math.log(10000.0) * jnp.arange(half_width, dtype=jnp.float32) / half_width)
    angles = time_value[..., None] * frequency
    return jnp.concatenate([jnp.cos(angles), jnp.sin(angles)], -1)


def token_order(grid):
    frames, rows, cols, width = grid.shape
    halves = grid.reshape(frames, rows, cols // WIN, WIN, width).transpose(2, 0, 1, 3, 4)
    return halves.reshape(frames * rows * cols, width)


def with_rows(tokens, first_rows, run):
    width = tokens.shape[1]
    runs = tokens.reshape(-1, run, width)
    return jnp.concatenate([first_rows, runs[:, first_rows.shape[1] :]], 1).reshape(-1, width)


def first_rows(tokens, run, part):
    return tokens.reshape(-1, run, tokens.shape[1])[:, :part]


def attend_pieces(tokens, frames, keys):
    if keys == "frame":
        run = tokens // (2 * frames)
        return [((f * run, run), (tokens // 2 + f * run, run)) for f in range(frames)]
    if keys == "half":
        return [((half * (tokens // 2), tokens // 2),) for half in range(2)]
    return [((0, tokens),)]


def take(ref, runs):
    pieces = [ref[low : low + many, :] for low, many in runs]
    return pieces[0] if len(pieces) == 1 else jnp.concatenate(pieces, 0)


def put(ref, cols, runs, value):
    done = 0
    for low, many in runs:
        ref[low : low + many, cols] = value[done : done + many].astype(ref.dtype)
        done += many


def softmax_of(scores, axis, text_len):
    if text_len:
        place = lax.broadcasted_iota(jnp.int32, scores.shape, axis)
        scores = jnp.where(place < text_len, scores, -1e30)
    weight = jnp.exp(scores - jnp.max(scores, axis, keepdims=True))
    return weight * (1.0 / jnp.sum(weight, axis, keepdims=True))


def lanes_of(head, shape):
    lane = lax.broadcasted_iota(jnp.int32, shape, 1)
    return lane < HEAD_DIM if head == 0 else lane >= HEAD_DIM


def only(head, value):
    return jnp.where(lanes_of(head, value.shape), value, jnp.zeros_like(value))


def attention_gradients(queries, keys, values, grad_out, text_len):
    queries, grad_out = stacked(queries), stacked(grad_out)
    probs = softmax_of(matmul_nt(keys, queries), 0, text_len)
    dprobs = matmul_nt(values, grad_out)
    dv = matmul(probs.astype(jnp.bfloat16), grad_out)
    inner = jnp.sum(probs * dprobs, 0, keepdims=True)
    dscores = (probs * (dprobs - inner)).astype(jnp.bfloat16)
    dk = matmul(dscores, queries)
    return unstacked(matmul_tn(dscores, keys)) * HEAD_DIM ** (-0.5), dk, dv


def attention_values(queries, keys, values, text_len):
    probs = softmax_of(matmul_nt(stacked(queries), keys), 1, text_len)
    return unstacked(matmul(probs.astype(jnp.bfloat16), values))


def stacked(rows):
    return jnp.concatenate([only(head, rows) for head in range(2)], 0)


def unstacked(rows):
    half = rows.shape[0] // 2
    return jnp.where(lanes_of(0, (half, rows.shape[1])), rows[:half], rows[half:])


def key_sets(key_refs, runs, text_len):
    if text_len:
        return key_refs[0][...]
    pieces = [take(ref, runs) for ref in key_refs]
    return pieces[0] if len(pieces) == 1 else jnp.concatenate(pieces, 0)


def attend_kernel(windows, text_len, sets, *refs):
    q_ref, k_refs, v_refs, out_ref = refs[0], refs[1 : 1 + sets], refs[1 + sets : 1 + 2 * sets], refs[-1]
    for runs in windows:
        queries = take(q_ref, runs) * HEAD_DIM ** (-0.5)
        keys, values = key_sets(k_refs, runs, text_len), key_sets(v_refs, runs, text_len)
        put(out_ref, slice(None), runs, attention_values(queries, keys, values, text_len))


def attend_back_kernel(windows, text_len, sets, *refs):
    q_ref, k_refs, v_refs = refs[0], refs[1 : 1 + sets], refs[1 + sets : 1 + 2 * sets]
    grad_ref = refs[1 + 2 * sets]
    dq_ref = refs[2 + 2 * sets]
    own_ref = refs[3 + 2 * sets] if text_len else None
    pair = pl.program_id(0)
    cols = [pl.ds(pl.multiple_of(i * D + pair * 2 * HEAD_DIM, 128), 2 * HEAD_DIM) for i in range(3)]
    merged = dq_ref.shape[1] == 3 * D
    for runs in windows:
        queries = take(q_ref, runs) * HEAD_DIM ** (-0.5)
        keys, values = key_sets(k_refs, runs, text_len), key_sets(v_refs, runs, text_len)
        grad_out = take(grad_ref, runs)
        dq, dk, dv = attention_gradients(queries, keys, values, grad_out, text_len)
        put(dq_ref, cols[0], runs, dq)
        if merged:
            put(dq_ref, cols[1], runs, dk)
            put(dq_ref, cols[2], runs, dv)
        else:
            own_ref[:, cols[0]] = dk
            own_ref[:, cols[1]] = dv


def pair_cols(which, pair):
    return pl.ds(pl.multiple_of(which * D + pair * 2 * HEAD_DIM, 128), 2 * HEAD_DIM)


def take_cols(ref, cols, runs):
    return jnp.concatenate([ref[low : low + many, cols] for low, many in runs], 0)


def attend_frames_kernel(windows, qkv_ref, out_ref, far_ref, send, recv):
    band = lax.axis_index("band")
    partner = (lax.axis_index("clip"), band + 1 - 2 * (band % 2))
    greet([partner])

    def copies(pair):
        return [
            pltpu.make_async_remote_copy(
                qkv_ref.at[:, pair_cols(1 + i, pair)],
                far_ref.at[:, pair_cols(i, pair)],
                send.at[pair, i],
                recv.at[pair, i],
                partner,
                MESH,
            )
            for i in range(2)
        ]

    @pl.loop(0, HEADS // 2)
    def _(pair):
        for copy in copies(pair):
            copy.start()

    @pl.loop(0, HEADS // 2)
    def _(pair):
        for copy in copies(pair):
            copy.wait_recv()
        for runs in windows:
            queries = take_cols(qkv_ref, pair_cols(0, pair), runs) * HEAD_DIM ** (-0.5)
            keys, values = (
                jnp.concatenate(
                    [
                        take_cols(qkv_ref, pair_cols(1 + i, pair), runs),
                        take_cols(far_ref, pair_cols(i, pair), runs),
                    ],
                    0,
                )
                for i in range(2)
            )
            put(
                out_ref, pair_cols(0, pair), runs, attention_values(queries, keys, values, 0)
            )

    @pl.loop(0, HEADS // 2)
    def _(pair):
        for copy in copies(pair):
            copy.wait_send()


def attend_frames_back_kernel(
    windows, qkv_ref, far_ref, grad_ref, out_ref, own_buf, far_put, far_got, send, recv
):
    band = lax.axis_index("band")
    partner = (lax.axis_index("clip"), band + 1 - 2 * (band % 2))
    greet([partner])

    def copies(pair):
        return [
            pltpu.make_async_remote_copy(
                far_put.at[:, pair_cols(i, pair)],
                far_got.at[:, pair_cols(i, pair)],
                send.at[pair, i],
                recv.at[pair, i],
                partner,
                MESH,
            )
            for i in range(2)
        ]

    def merge(pair):
        for i, copy in enumerate(copies(pair)):
            copy.wait_recv()
            cols = pair_cols(i, pair)
            total = own_buf[:, cols] + far_got[:, cols]
            out_ref[:, pair_cols(1 + i, pair)] = total.astype(jnp.bfloat16)

    @pl.loop(0, HEADS // 2)
    def _(pair):
        for runs in windows:
            queries = take_cols(qkv_ref, pair_cols(0, pair), runs) * HEAD_DIM ** (-0.5)
            keys, values = (
                jnp.concatenate(
                    [
                        take_cols(qkv_ref, pair_cols(1 + i, pair), runs),
                        take_cols(far_ref, pair_cols(i, pair), runs),
                    ],
                    0,
                )
                for i in range(2)
            )
            grad_out = take_cols(grad_ref, pair_cols(0, pair), runs)
            dq, *dkv = attention_gradients(queries, keys, values, grad_out, 0)
            put(out_ref, pair_cols(0, pair), runs, dq)
            half = keys.shape[0] // 2
            for i, value in enumerate(dkv):
                put(own_buf, pair_cols(i, pair), runs, value[:half])
                put(far_put, pair_cols(i, pair), runs, value[half:])
        for copy in copies(pair):
            copy.start()

        @pl.when(pair >= 1)
        def _():
            merge(pair - 1)

    merge(HEADS // 2 - 1)

    @pl.loop(0, HEADS // 2)
    def _(pair):
        for copy in copies(pair):
            copy.wait_send()


def attend_frames(qkv, windows):
    tokens = qkv.shape[0]
    dma = pltpu.SemaphoreType.DMA((HEADS // 2, 2))
    return pl.pallas_call(
        partial(attend_frames_kernel, windows),
        out_shape=(
            jax.ShapeDtypeStruct((tokens, D), jnp.bfloat16),
            jax.ShapeDtypeStruct((tokens, 2 * D), jnp.bfloat16),
        ),
        in_specs=[IN_VMEM],
        out_specs=(IN_VMEM,) * 2,
        scratch_shapes=[dma, dma],
        compiler_params=pltpu.CompilerParams(
            collective_id=4, has_side_effects=True, vmem_limit_bytes=40 << 20
        ),
        cost_estimate=attention_cost(tokens, 256, 2),
    )(qkv)


def attend_frames_back(qkv, far_kv, grad_out, windows):
    tokens = qkv.shape[0]
    dma = pltpu.SemaphoreType.DMA((HEADS // 2, 2))
    return pl.pallas_call(
        partial(attend_frames_back_kernel, windows),
        out_shape=jax.ShapeDtypeStruct(qkv.shape, jnp.bfloat16),
        in_specs=[IN_VMEM] * 3,
        out_specs=IN_VMEM,
        scratch_shapes=[pltpu.VMEM((tokens, 2 * D), jnp.float32)] * 3 + [dma, dma],
        compiler_params=pltpu.CompilerParams(
            collective_id=5, has_side_effects=True, vmem_limit_bytes=50 << 20
        ),
        cost_estimate=attention_cost(tokens, 256, 5),
    )(qkv, far_kv, grad_out)


def head_cols(array, first):
    return array, pl.BlockSpec((array.shape[0], 2 * HEAD_DIM), lambda h: (0, first + h))


def attention_operands(queries, key_values):
    ins = [head_cols(queries, 0)]
    ins += [head_cols(array, first) for array, first, _ in key_values]
    return ins + [head_cols(array, second) for array, _, second in key_values]


def attention_cost(tokens, keys, products):
    flops = 2 * products * tokens * keys * D * 2
    return pl.CostEstimate(
        flops=flops, bytes_accessed=tokens * D * 2 * 8, transcendentals=tokens * keys * HEADS
    )


def attend(queries, key_values, windows, text_len=0):
    tokens = queries.shape[0]
    ins = attention_operands(queries, key_values)
    return pl.pallas_call(
        partial(attend_kernel, windows, text_len, len(key_values)),
        grid=(HEADS // 2,),
        in_specs=[spec for _, spec in ins],
        out_specs=pl.BlockSpec((tokens, 2 * HEAD_DIM), lambda h: (0, h)),
        out_shape=jax.ShapeDtypeStruct((tokens, D), jnp.bfloat16),
        compiler_params=pltpu.CompilerParams(vmem_limit_bytes=40 << 20),
        cost_estimate=attention_cost(tokens, 320, 2),
    )(*[array for array, _ in ins])


def attend_back(queries, key_values, grad_out, windows, text_len=0):
    tokens = queries.shape[0]
    ins = attention_operands(queries, key_values) + [head_cols(grad_out, 0)]
    sets = len(key_values)
    whole = lambda rows, cols: pl.BlockSpec((rows, cols), lambda h: (0, 0))
    if sets == 1 and not text_len:
        outs = [((tokens, 3 * D), jnp.bfloat16)]
    else:
        rows = key_values[0][0].shape[0]
        outs = [((tokens, D), jnp.bfloat16)] + [((rows, 2 * D), jnp.float32)] * sets
    return pl.pallas_call(
        partial(attend_back_kernel, windows, text_len, sets),
        grid=(HEADS // 2,),
        in_specs=[spec for _, spec in ins],
        out_specs=[whole(*shape) for shape, _ in outs],
        out_shape=[jax.ShapeDtypeStruct(*out) for out in outs],
        compiler_params=pltpu.CompilerParams(vmem_limit_bytes=50 << 20),
        cost_estimate=attention_cost(tokens, 320, 5),
    )(*[array for array, _ in ins])


def mlp_forward(stream, modul, up_weight, down_weight):
    mlp_val, norm_back = jax.vjp(norm_modulated, stream, modul[3], modul[4])
    mlp_in = mlp_val.astype(jnp.bfloat16)
    up_proj = matmul(mlp_in, up_weight)
    share = 0.5 + 0.5 * lax.erf(up_proj * math.sqrt(0.5))
    gelu_val = up_proj * share
    slope = share + up_proj * (jnp.exp(-0.5 * up_proj * up_proj) / math.sqrt(2.0 * math.pi))
    gelu_low = gelu_val.astype(jnp.bfloat16)
    down_proj = matmul(gelu_low, down_weight)
    return (stream + modul[5] * down_proj, (norm_back, mlp_in, slope, gelu_low, down_proj))


def mlp_backward(grad_stream, modul, up_weight, down_weight, saved):
    norm_back, mlp_in, slope, gelu_low, down_proj = saved
    grad_down = (modul[5] * grad_stream).astype(jnp.bfloat16)
    grad_gate = jnp.sum(grad_stream * down_proj, 0)
    grad_up = (slope * matmul_nt(grad_down, down_weight)).astype(jnp.bfloat16)
    grad_part, grad_shift, grad_scale = norm_back(matmul_nt(grad_up, up_weight))
    factors = ((gelu_low, grad_down), (mlp_in, grad_up))
    return (grad_stream + grad_part, factors, (grad_shift, grad_scale, grad_gate))


def adam_update(weight, first_mom, second_mom, grad_val, learn_rate):
    first_mom = BETA_ONE * first_mom + (1.0 - BETA_ONE) * grad_val
    second_mom = BETA_TWO * second_mom + (1.0 - BETA_TWO) * grad_val * grad_val
    first_hat = first_mom / (1.0 - BETA_ONE**STEP)
    second_hat = second_mom / (1.0 - BETA_TWO**STEP)
    weight = weight - learn_rate * (first_hat / (jnp.sqrt(second_hat) + ADAM_EPS) + DECAY * weight)
    return (weight, first_mom, second_mom)

MESH = pl.DeviceIdType.MESH
ANY = pl.BlockSpec(memory_space=pl.ANY)
IN_VMEM = pl.BlockSpec(memory_space=pltpu.VMEM)
TEXT_PAD = 80


def ring_place(clip, count):
    half = clip // 2
    odd = clip % 2
    return half + odd * (count - 1 - 2 * half)


def ring_clip(place, count):
    far = place // (count // 2)
    return (1 - far) * 2 * place + far * (2 * (count - 1 - place) + 1)


def greet(peers):
    barrier = pltpu.get_barrier_semaphore()
    for peer in peers:
        pl.semaphore_signal(barrier, inc=1, device_id=peer, device_id_type=MESH)
    pl.semaphore_wait(barrier, len(peers))


def exchange_kernel(count, facts_ref, facts_out, send, recv):
    me = lax.axis_index("clip")
    band = lax.axis_index("band")
    peers = [((me + step) % count, band) for step in range(1, count)]
    greet(peers)
    sent = [
        pltpu.make_async_remote_copy(
            facts_ref, facts_out.at[me], send.at[step], recv.at[step], peer, MESH
        )
        for step, peer in enumerate(peers)
    ]
    for copy in sent:
        copy.start()
    facts_out[me] = facts_ref[...]
    for copy in sent:
        copy.wait()


def exchange_facts(facts):
    count = lax.axis_size("clip")
    return pl.pallas_call(
        partial(exchange_kernel, count),
        out_shape=jax.ShapeDtypeStruct((count,) + facts.shape, facts.dtype),
        in_specs=[IN_VMEM],
        out_specs=IN_VMEM,
        scratch_shapes=[pltpu.SemaphoreType.DMA((count - 1,))] * 2,
        compiler_params=pltpu.CompilerParams(collective_id=0, has_side_effects=True),
    )(facts)


def gather_kernel(count, picks, sides, *refs):
    num = len(picks)
    packs, vec_ref, text_ref = refs[:2], refs[2], refs[3]
    full, (vec_out, text_out, kv_out) = refs[4 : 4 + num], refs[4 + num : 7 + num]
    refs = refs[7 + num :]
    wide, shards = refs[:num], refs[num : 2 * num]
    ring_send, ring_recv, pair_send, pair_recv, cross_send, cross_recv = refs[2 * num : 2 * num + 6]
    load_sem, own_sem, part_send, part_recv, part_own = refs[2 * num + 6 : 2 * num + 11]
    kv_wide, kv_part, kv_put, kv_got, kv_sum, kv_load, kv_send, kv_recv, band_send, band_recv = refs[
        2 * num + 11 : 2 * num + 21
    ]
    share_send, share_recv = refs[2 * num + 21 :]
    shapes = [(packs[pack].shape[0], cols) for pack, _, cols in picks]
    loads = [
        pltpu.make_async_copy(
            packs[pack].at[:, pl.ds(start, cols)], wide[group], load_sem.at[group]
        )
        for group, (pack, start, cols) in enumerate(picks)
    ]
    kv_width = kv_wide.shape[1]
    kv_first = D + lax.axis_index("band") * kv_width
    kv_weight = pltpu.make_async_copy(
        packs[1].at[:, pl.ds(pl.multiple_of(kv_first, 128), kv_width)], kv_wide, kv_load
    )
    for copy in loads + [kv_weight]:
        copy.start()
    me = lax.axis_index("clip")
    band = lax.axis_index("band")
    core = band % 2
    place = ring_place(me, count)
    onward = 1 - 2 * core
    following = (ring_clip((place + onward + count) % count, count), band)
    plane = band // 2
    partner = (me, band + 1 - 2 * core)
    mirror = (me, band + 2 - 4 * plane)
    peers = [((me + step) % count, band) for step in range(1, count)]
    band_count = 2 * D // kv_width
    band_peers = [(me, (band + step) % band_count) for step in range(1, band_count)]
    greet(peers + band_peers)

    def block(ref, group, owner):
        rows, cols = shapes[group]
        return ref.at[
            pl.ds(pl.multiple_of(owner * rows, rows), rows),
            pl.ds(pl.multiple_of(core * (cols // 2), 128), cols // 2),
        ]

    def ring_copy(group, step):
        owner = ring_clip((place - onward * step + 2 * count) % count, count)
        there = block(full[group], group, owner)
        return pltpu.make_async_remote_copy(
            there, there, ring_send.at[step, group], ring_recv.at[step, group], following, MESH
        )

    def handed(group, step, send, recv, peer):
        owner = ring_clip((place - onward * (step + 1) + 2 * count) % count, count)
        there = block(full[group], group, owner)
        return pltpu.make_async_remote_copy(
            there, there, send.at[step, group], recv.at[step, group], peer, MESH
        )

    def pair_copy(group, step):
        return handed(group, step, pair_send, pair_recv, partner)

    def cross_copy(group, step):
        return handed(group, step, cross_send, cross_recv, mirror)

    def in_ring(group):
        def decorate(body):
            if sides[group]:
                pl.when(plane == sides[group] - 1)(body)
            else:
                body()

        return decorate

    def off_ring(group, also=None):
        def decorate(body):
            if sides[group]:
                off = plane != sides[group] - 1
                pl.when(off if also is None else jnp.logical_and(off, also))(body)

        return decorate

    def ring_arrival(group, step, onto):
        ring_copy(group, step).wait_recv()
        if onto:
            ring_copy(group, step + 1).start()
        pair_copy(group, step).start()
        if sides[group]:
            cross_copy(group, step).start()

    def cross_arrival(group, step):
        cross_copy(group, step).wait_recv()
        pair_copy(group, step).start()

    def own_copy(group):
        rows, cols = shapes[group]
        return pltpu.make_async_copy(
            shards[group],
            full[group].at[pl.ds(pl.multiple_of(me * rows, rows), rows), :],
            own_sem.at[group],
        )

    parts = []
    for step, peer in enumerate(peers):
        for which, (src, dst) in enumerate(((vec_ref, vec_out), (text_ref, text_out))):
            parts.append(
                pltpu.make_async_remote_copy(
                    src.at[peer[0], band],
                    dst.at[me, band],
                    part_send.at[which, step],
                    part_recv.at[which, step],
                    peer,
                    MESH,
                )
            )
    parts_own = [
        pltpu.make_async_copy(src.at[me, band], dst.at[me, band], part_own.at[which])
        for which, (src, dst) in enumerate(((vec_ref, vec_out), (text_ref, text_out)))
    ]
    for copy in parts_own + parts:
        copy.start()
    for group in range(num):
        rows, cols = shapes[group]
        loads[group].wait()
        shards[group][...] = wide[group][...].astype(jnp.bfloat16)
        own_copy(group).start()

        @in_ring(group)
        def _(group=group, rows=rows, cols=cols):
            pltpu.make_async_remote_copy(
                shards[group].at[:, pl.ds(pl.multiple_of(core * (cols // 2), 128), cols // 2)],
                block(full[group], group, me),
                ring_send.at[0, group],
                ring_recv.at[0, group],
                following,
                MESH,
            ).start()

    def kv_copy(hop):
        return pltpu.make_async_remote_copy(
            kv_put.at[hop], kv_got.at[hop], kv_send.at[hop], kv_recv.at[hop], following, MESH
        )

    def kv_hop(hop):
        owner = ring_clip((place - onward * (hop + 1) + 2 * count) % count, count)
        total = kv_part[owner]
        if not isinstance(hop, int) or hop > 0:
            kv_copy(hop - 1).wait_recv()
            total = total + kv_got[hop - 1]
        kv_put[hop] = total
        kv_copy(hop).start()

    def band_copies():
        return [
            pltpu.make_async_remote_copy(
                kv_sum, kv_out.at[band], band_send.at[step], band_recv.at[step], peer, MESH
            )
            for step, peer in enumerate(band_peers)
        ]

    shares = [
        pltpu.make_async_remote_copy(
            out.at[:, band],
            out.at[:, band],
            share_send.at[which, step],
            share_recv.at[which, step],
            peer,
            MESH,
        )
        for step, peer in enumerate(band_peers)
        for which, out in enumerate((vec_out, text_out))
    ]

    def share():
        for copy in parts_own + parts:
            copy.wait()
        for copy in shares:
            copy.start()

    def multiply():
        for copy in shares:
            copy.wait()
        kv_weight.wait()
        weight = kv_wide[...].astype(jnp.bfloat16)
        depth = weight.shape[0] // band_count
        for owner in range(count):
            kv_part[owner] = sum(
                matmul(text_out[owner, part], weight[part * depth : (part + 1) * depth])
                for part in range(band_count)
            )
        kv_hop(0)

    @pl.loop(1, count - 1)
    def _(step):
        for group in range(num):

            @in_ring(group)
            def _(group=group):
                ring_arrival(group, step - 1, True)

        pl.when(step == 1)(share)
        pl.when(step == 2)(multiply)

        @pl.when(step >= 3)
        def _():
            kv_hop(step - 2)
        for group in range(num):

            @off_ring(group, step >= 2)
            def _(group=group):
                cross_arrival(group, step - 2)

    for group in range(num):

        @in_ring(group)
        def _(group=group):
            ring_arrival(group, count - 2, False)

    kv_hop(count - 3)
    for late in (count - 3, count - 2):
        for group in range(num):

            @off_ring(group)
            def _(group=group, late=late):
                cross_arrival(group, late)

        if late == count - 3:
            kv_hop(count - 2)
    kv_copy(count - 2).wait_recv()
    kv_sum[...] = (kv_part[me] + kv_got[count - 2]).astype(jnp.bfloat16)
    kv_out[band] = kv_sum[...]
    for copy in band_copies():
        copy.start()
    for group in range(num):
        own_copy(group).wait()

    @pl.loop(0, count - 1)
    def _(step):
        for group in range(num):

            @in_ring(group)
            def _(group=group):
                ring_copy(group, step).wait_send()
                if sides[group]:
                    cross_copy(group, step).wait_send()

            pair_copy(group, step).wait()
        kv_copy(step).wait_send()

    for copy in band_copies():
        copy.wait()


def own_quarter(shard):
    rows = shard.shape[0] // lax.axis_size("band")
    own = lax.dynamic_slice_in_dim(shard, lax.axis_index("band") * rows, rows, 0)
    return own.astype(jnp.bfloat16)


def sum_rows(left, right):
    part = lax.psum_scatter(
        matmul_tn(left, right), ("clip", "band"), scatter_dimension=0, tiled=True
    )
    return lax.all_gather(part, "band", axis=0, tiled=True)


def gather_weights(packs, picks, sides, vectors, texts):
    count, band_count = lax.axis_size("clip"), lax.axis_size("band")
    num = len(picks)
    dma = pltpu.SemaphoreType.DMA
    shapes = [(packs[pack].shape[0], cols) for pack, _, cols in picks]
    kv_shape = (texts.shape[2], 2 * D // band_count)
    kv_all = pltpu.VMEM((count,) + kv_shape, jnp.float32)
    kv_hops = pltpu.VMEM((count - 1,) + kv_shape, jnp.float32)
    out = pl.pallas_call(
        partial(gather_kernel, count, picks, sides),
        out_shape=tuple(
            jax.ShapeDtypeStruct((count * rows, cols), jnp.bfloat16) for rows, cols in shapes
        )
        + tuple(jax.ShapeDtypeStruct(v.shape, v.dtype) for v in (vectors, texts))
        + (jax.ShapeDtypeStruct((band_count,) + kv_shape, jnp.bfloat16),),
        in_specs=[ANY] * 4,
        out_specs=(ANY,) * num + (IN_VMEM,) * 3,
        scratch_shapes=[pltpu.VMEM(shape, jnp.float32) for shape in shapes]
        + [pltpu.VMEM(shape, jnp.bfloat16) for shape in shapes]
        + [dma((count - 1, num))] * 6
        + [dma((num,)), dma((num,)), dma((2, count - 1)), dma((2, count - 1)), dma((2,))]
        + [
            pltpu.VMEM((packs[1].shape[0], kv_shape[1]), jnp.float32),
            kv_all,
            kv_hops,
            kv_hops,
            pltpu.VMEM(kv_shape, jnp.bfloat16),
            dma,
            dma((count - 1,)),
            dma((count - 1,)),
            dma((band_count - 1,)),
            dma((band_count - 1,)),
            dma((2, band_count - 1)),
            dma((2, band_count - 1)),
        ],
        compiler_params=pltpu.CompilerParams(
            collective_id=1, has_side_effects=True, vmem_limit_bytes=50 << 20
        ),
        cost_estimate=pl.CostEstimate(flops=2 * 10**11, bytes_accessed=6 * 10**8, transcendentals=0),
    )(*packs, vectors, texts)
    return out[:num], out[num], out[num + 1], out[num + 2]


WIRE_MAX = 32767.0
WIRE_LEAST = 1e-30
UNIT = (128, 512)


SPLIT = 2


def unit_parts(at, kind, first):
    if at == 0:
        return ((0, 4, lambda u: u, lambda u: 0), (4, SPLIT, lambda u: 4, lambda u: u - 3))
    if kind == 0:
        return ((0, 4, lambda u: u, lambda u: 0), (4, 4, lambda u: 4, lambda u: u - 3))
    if first:
        return ((2, 2, lambda u: u, lambda u: u), (4, 2, lambda u: 3, lambda u: u))
    return ((0, 3, lambda u: u, lambda u: u), (3, 3, lambda u: 3, lambda u: u))


def reduce_kernel(count, tokens, phases, *refs):
    num = sum(len(phase["lefts"]) for phase in phases)
    lefts, rights = refs[:num], refs[num : 2 * num]
    vec_ref, kv_ref, text_ref = refs[2 * num : 2 * num + 3]
    refs = refs[2 * num + 3 :]
    wide_out, deep_out, square_out, all_vec, kv_square = refs[:5]
    left_far, right_far = refs[5 : 5 + num], refs[5 + num : 5 + 2 * num]
    scratch = refs[5 + 2 * num :]
    left_buf, right_buf, got_low, got_scale, put_low, put_scale, plane_put = (
        scratch[2 * i : 2 * i + 2] for i in range(7)
    )
    plane_got = scratch[14 : 14 + len(phases)]
    (
        square_buf,
        left_sem,
        right_sem,
        pair_send,
        pair_recv,
        half_send,
        half_recv,
        ring_send,
        ring_recv,
        credit,
        plane_send,
        plane_recv,
        out_sem,
        out_send,
        out_recv,
        last_put,
        last_put_scale,
        last_got,
        last_got_scale,
        late_put,
        late_put_scale,
        late_got,
        late_got_scale,
        push_send,
        push_recv,
        cross_put,
        cross_put_scale,
        cross_got,
        cross_got_scale,
        cross_send,
        cross_recv,
        cross_credit,
        vec_got,
        kv_got,
        vec_sum,
        all_kv,
        all_kv_scale,
        text_buf,
        kv_grad,
        side_own,
        side_send,
        side_recv,
        vec_send,
        vec_recv,
        vec_pair_send,
        vec_pair_recv,
        kv_own,
        kv_send,
        kv_recv,
    ) = scratch[14 + len(phases) :]
    me = lax.axis_index("clip")
    band = lax.axis_index("band")
    core = band % 2
    plane = band // 2
    place = ring_place(me, count)
    onward = 1 - 2 * core
    following = (ring_clip((place + onward + count) % count, count), band)
    preceding = (ring_clip((place - onward + count) % count, count), band)
    partner = (me, band + 1 - 2 * core)
    mirror = (me, band + 2 - 4 * plane)
    band_count = vec_got.shape[0]
    band_peers = [(me, (band + step) % band_count) for step in range(1, band_count)]
    greet([following, preceding] + band_peers)

    def owner_at(step, way):
        return ring_clip((place - way * (step + 1) + 2 * count) % count, count)

    def left_blocks(at):
        phase = phases[at]
        if phase["kind"] == 0:
            return [(b, phase["lefts"][0], b, 4) for b in range(4)] + [(4, phase["lefts"][1], 0, 1)]
        first = phase["first"]
        return [(first + i, left, 0, 1) for i, left in enumerate(phase["lefts"])]

    def right_blocks(at):
        phase = phases[at]
        if phase["kind"] == 0:
            return [(0, phase["lefts"][0], 0)] + [(1 + i, phase["lefts"][1], i) for i in range(4)]
        first = phase["first"]
        return [(first + i, phase["lefts"][i], 0) for i in range(3 - first)] + [
            (3 + i, phase["lefts"][-1], i) for i in range(3)
        ]

    def left_cols(step, way, which, many):
        width = lefts_width // count if many == 1 else deep_width // count
        start = owner_at(step, way) * width + which * 128
        return pl.ds(pl.multiple_of(start, 128), 128)

    lefts_width = lefts[phases[1]["lefts"][0]].shape[1]
    deep_width = lefts[phases[0]["lefts"][0]].shape[1]

    def pair_left(at, step):
        out = []
        for block, operand, which, many in left_blocks(at):
            cols = left_cols(step, -onward, which, many)
            out.append(
                pltpu.make_async_remote_copy(
                    lefts[operand].at[:, cols],
                    left_far[operand].at[:, cols],
                    pair_send.at[at, block, step],
                    pair_recv.at[at, block, step],
                    partner,
                    MESH,
                )
            )
        return out

    def pair_right(at):
        out = []
        for i, operand in enumerate(phases[at]["lefts"]):
            half = rights[operand].shape[1] // 2
            out.append(
                pltpu.make_async_remote_copy(
                    rights[operand].at[:, pl.ds(pl.multiple_of((1 - core) * half, 128), half)],
                    right_far[operand],
                    half_send.at[operand],
                    half_recv.at[operand],
                    partner,
                    MESH,
                )
            )
        return out

    def load_left(at, step, slot, far):
        kind = phases[at]["kind"]
        out = []
        for block, operand, which, many in left_blocks(at):
            cols = left_cols(step, onward, which, many)
            source = left_far if far else lefts
            out.append(
                pltpu.make_async_copy(
                    source[operand].at[:, cols],
                    left_buf[kind].at[slot, block, pl.ds(far * tokens, tokens), :],
                    left_sem.at[kind, slot, block, far],
                )
            )
        return out

    def load_right(at, far):
        kind = phases[at]["kind"]
        out = []
        for block, operand, which in right_blocks(at):
            if far:
                source = right_far[operand].at[:, pl.ds(which * UNIT[1], UNIT[1])]
            else:
                half = rights[operand].shape[1] // 2
                start = pl.multiple_of(core * half + which * UNIT[1], 128)
                source = rights[operand].at[:, pl.ds(start, UNIT[1])]
            out.append(
                pltpu.make_async_copy(
                    source,
                    right_buf[kind].at[block, pl.ds(far * tokens, tokens), :],
                    right_sem.at[kind, block, far],
                )
            )
        return out

    def ring_copies(at, part, slot):
        kind = phases[at]["kind"]
        units = pl.ds(*unit_parts(at, kind, phases[at]["first"])[part][:2])
        return [
            pltpu.make_async_remote_copy(
                put.at[slot, units],
                got.at[slot, units],
                ring_send.at[kind, slot, part, i],
                ring_recv.at[kind, slot, part, i],
                following,
                MESH,
            )
            for i, (put, got) in enumerate(
                ((put_low[kind], got_low[kind]), (put_scale[kind], got_scale[kind]))
            )
        ]

    def plane_copies(at, part):
        kind = phases[at]["kind"]
        units = pl.ds(*unit_parts(at, kind, phases[at]["first"])[part][:2])
        pairs = ((plane_put[kind], plane_got[at]),)
        if at in coded:
            pairs = (coded[at][::2], coded[at][1::2])
        return [
            pltpu.make_async_remote_copy(
                here.at[units],
                there.at[units],
                plane_send.at[at, part, i],
                plane_recv.at[at, part, i],
                mirror,
                MESH,
            )
            for i, (here, there) in enumerate(pairs)
        ]

    coded = {
        len(phases) - 2: (late_put, late_put_scale, late_got, late_got_scale),
        len(phases) - 1: (last_put, last_put_scale, last_got, last_got_scale),
    }

    def split_unit(pair, of_plane):
        return 4 + 2 * pair + of_plane

    def split_copy(pair, of_plane):
        unit = split_unit(pair, of_plane)
        return pltpu.make_async_remote_copy(
            plane_put[0].at[unit],
            plane_got[0].at[unit],
            plane_send.at[0, 1, pair],
            plane_recv.at[0, 1, pair],
            mirror,
            MESH,
        )

    def cross_copies(slot):
        return [
            pltpu.make_async_remote_copy(
                here.at[slot], there.at[slot], cross_send.at[slot, i], cross_recv.at[slot, i], mirror, MESH
            )
            for i, (here, there) in enumerate(
                ((cross_put, cross_got), (cross_put_scale, cross_got_scale))
            )
        ]

    def push_right(block):
        operand, which = [entry[1:] for entry in right_blocks(0) if entry[0] == block][0]
        half = rights[operand].shape[1] // 2
        begin = pl.multiple_of((1 - core) * half + which * UNIT[1], 128)
        return pltpu.make_async_remote_copy(
            rights[operand].at[:, pl.ds(begin, UNIT[1])],
            right_buf[phases[0]["kind"]].at[block, pl.ds(tokens, tokens), :],
            push_send.at[block],
            push_recv.at[block],
            partner,
            MESH,
        )

    def out_copies(at, unit):
        phase = phases[at]
        if phase["kind"] == 0 and unit < 4:
            half = UNIT[1]
            rows = deep_out.shape[0] // 4
            there = deep_out.at[
                pl.ds(unit * rows, rows),
                pl.ds(pl.multiple_of(phase["cols"][0] + core * half, 128), half),
            ]
        else:
            which, col = (1, unit - 4) if phase["kind"] == 0 else (unit - phase["first"], 0)
            if phase["kind"] and unit >= 3:
                which, col = len(phase["lefts"]) - 1, unit - 3
            half = rights[phase["lefts"][which]].shape[1] // 2
            start = phase["cols"][which] + core * half + col * UNIT[1]
            there = wide_out.at[:, pl.ds(pl.multiple_of(start, 128), UNIT[1])]
        here = plane_got[at].at[unit]
        return (
            pltpu.make_async_copy(here, there, out_sem.at[at, unit]),
            pltpu.make_async_remote_copy(
                here, there, out_send.at[at, unit], out_recv.at[at, unit], partner, MESH
            ),
        )

    def product(kind, slot, left, right):
        return lax.dot_general(
            left_buf[kind][slot, left],
            right_buf[kind][right],
            (((0,), (0,)), ((), ())),
            preferred_element_type=jnp.float32,
        )

    def start(copies):
        for copy in copies:
            copy.start()

    def finish(copies):
        for copy in copies:
            copy.wait()

    def encode(term):
        largest = jnp.maximum(jnp.max(jnp.abs(term), axis=0, keepdims=True), WIRE_LEAST)
        low = jnp.round(term * (WIRE_MAX / largest)).astype(jnp.int16)
        return low, largest * (1.0 / WIRE_MAX)

    def take_step(at, step, first, last):
        phase = phases[at]
        kind = phase["kind"]
        slot = step % 2
        before = (step + 1) % 2
        for far in range(2):
            finish(load_left(at, step, slot, far))

        def load_next():
            for copy in pair_left(at, step + 1):
                copy.wait_recv()
            for far in range(2):
                start(load_left(at, step + 1, before, far))

        opening = first and at == 0
        if not (last or opening):
            load_next()
        parts = unit_parts(at, kind, phase["first"])

        def send_theirs():
            def spend():
                for copy in cross_copies(slot):
                    copy.wait_send()
                pl.semaphore_wait(cross_credit, 1)

            if last:
                spend()
            elif not first:
                pl.when(step >= 2)(spend)
            for pair in range(SPLIT):
                unit = split_unit(pair, 1 - plane)
                term = product(kind, slot, parts[1][2](unit), parts[1][3](unit))
                cross_put[slot, pair], cross_put_scale[slot, pair] = encode(term)
            start(cross_copies(slot))

        if at == 0 and not opening:
            send_theirs()
        for part, (low, many, left_of, right_of) in enumerate(parts):
            if opening:
                blocks = range(1) if part == 0 else range(1, 5)
                finish(load_right(0, 0)[blocks.start : blocks.stop])
                for block in blocks:
                    push_right(block).wait_recv()
                if part:
                    send_theirs()
            if not first:
                for copy in ring_copies(at, part, before):
                    copy.wait_recv()
            if not (first or last):

                @pl.when(step >= 2)
                def _(part=part):
                    for copy in ring_copies(at, part, slot):
                        copy.wait_send()
                    pl.semaphore_wait(credit.at[kind, part], 1)

            def settle(position, unit, term):
                if not first:
                    came = got_low[kind][before, position].astype(jnp.float32)
                    term = term + came * got_scale[kind][before, position]
                if last and at in coded:
                    coded[at][0][unit], coded[at][1][unit] = encode(term)
                elif last:
                    plane_put[kind][unit] = term
                else:
                    low_part, scale_part = encode(term)
                    put_low[kind][slot, position] = low_part
                    put_scale[kind][slot, position] = scale_part

            split = at == 0 and part == 1
            if split:
                for copy in cross_copies(slot):
                    copy.wait_recv()

            @pl.loop(low, low + many)
            def _(position, left_of=left_of, right_of=right_of):
                unit = split_unit(position - 4, plane) if split else position
                term = product(kind, slot, left_of(unit), right_of(unit))
                if split:
                    came = cross_got[slot, position - 4].astype(jnp.float32)
                    term = term + came * cross_got_scale[slot, position - 4]
                settle(position, unit, term)

            if split and not last:

                def credit_cross():
                    pl.semaphore_signal(
                        cross_credit, inc=1, device_id=mirror, device_id_type=MESH
                    )

                if first:
                    credit_cross()
                else:
                    pl.when(step < count - 2)(credit_cross)

            if last and split:
                start([split_copy(pair, plane) for pair in range(SPLIT)])
            elif last:
                start(plane_copies(at, part))
            else:
                start(ring_copies(at, part, slot))
            if not (first or last):

                @pl.when(step < count - 2)
                def _(part=part):
                    pl.semaphore_signal(
                        credit.at[kind, part], inc=1, device_id=preceding, device_id_type=MESH
                    )

        if opening:
            load_next()

    def close(at):
        kind = phases[at]["kind"]

        def add_square(total):
            square_buf[...] += jnp.sum((total * total).reshape(UNIT[0] // 8, 8, UNIT[1]), axis=0)

        for part, (low, many, _, _) in enumerate(unit_parts(at, kind, phases[at]["first"])):
            if at == 0 and part == 1:
                for pair in range(SPLIT):
                    split_copy(pair, plane).wait_send()
                    split_copy(pair, 1 - plane).wait_recv()
                    ours = split_unit(pair, plane)
                    plane_got[0][ours] = plane_put[0][ours]
                for unit in range(4, 8):
                    add_square(plane_got[0][unit])
                    start(out_copies(0, unit))
                continue
            finish(plane_copies(at, part))

            @pl.loop(low, low + many)
            def _(unit):
                if at in coded:
                    here, here_scale, there, there_scale = coded[at]
                    total = here[unit].astype(jnp.float32) * here_scale[unit]
                    total += there[unit].astype(jnp.float32) * there_scale[unit]
                else:
                    total = plane_put[kind][unit] + plane_got[at][unit]
                plane_got[at][unit] = total
                add_square(total)

            for unit in range(low, low + many):
                start(out_copies(at, unit))

    half_rows = pl.ds(pl.multiple_of(core * (vec_sum.shape[0] // 2), 8), vec_sum.shape[0] // 2)
    side_local = [
        pltpu.make_async_copy(vec_ref, vec_got.at[band], side_own.at[0]),
        pltpu.make_async_copy(kv_ref.at[band], kv_got.at[band], side_own.at[1]),
        pltpu.make_async_copy(text_ref, text_buf, side_own.at[2]),
    ]
    side_remote = []
    for step, peer in enumerate(band_peers):
        side_remote += [
            pltpu.make_async_remote_copy(
                vec_ref, vec_got.at[band], side_send.at[0, step], side_recv.at[0, step], peer, MESH
            ),
            pltpu.make_async_remote_copy(
                kv_ref.at[peer[1]],
                kv_got.at[band],
                side_send.at[1, step],
                side_recv.at[1, step],
                peer,
                MESH,
            ),
        ]
    vec_own = pltpu.make_async_copy(vec_sum, all_vec.at[me], side_own.at[3])

    def kv_parts(owner):
        return [(ref.at[owner], ref.at[owner]) for ref in (all_kv, all_kv_scale)]

    def vec_copies(step):
        owner = ring_clip((place - onward * step + 2 * count) % count, count)
        vec = all_vec.at[owner, half_rows]
        return [
            pltpu.make_async_remote_copy(
                here, there, vec_send.at[step, i], vec_recv.at[step, i], following, MESH
            )
            for i, (here, there) in enumerate([(vec, vec)] + kv_parts(owner))
        ]

    def vec_first():
        vec = all_vec.at[me, half_rows]
        return [
            pltpu.make_async_remote_copy(
                here, there, vec_send.at[0, i], vec_recv.at[0, i], following, MESH
            )
            for i, (here, there) in enumerate([(vec_sum.at[half_rows], vec)] + kv_parts(me))
        ]

    def vec_pair(step):
        owner = ring_clip((place - onward * (step + 1) + 2 * count) % count, count)
        vec = all_vec.at[owner, half_rows]
        return pltpu.make_async_remote_copy(
            vec, vec, vec_pair_send.at[step], vec_pair_recv.at[step], partner, MESH
        )

    kv_width = kv_grad.shape[1]

    def kv_place(owner):
        return deep_out.at[:, pl.ds(pl.multiple_of(D + owner * kv_width, 128), kv_width)]

    def kv_copy(i):
        if i == 2:
            return pltpu.make_async_copy(kv_grad, kv_place(band), kv_own)
        peer = (partner, mirror)[i]
        return pltpu.make_async_remote_copy(
            kv_grad, kv_place(band), kv_send.at[i], kv_recv.at[i], peer, MESH
        )

    def kv_passed():
        there = kv_place(mirror[1])
        return pltpu.make_async_remote_copy(
            there, there, kv_send.at[2], kv_recv.at[2], partner, MESH
        )

    def sum_bands():
        finish(side_local + side_remote)
        vec_sum[...] = jnp.sum(vec_got[...], 0)
        all_kv[me], all_kv_scale[me] = encode(jnp.sum(kv_got[...], 0))
        vec_own.start()
        start(vec_first())

    def pass_sums(step):
        for copy in vec_copies(step - 1):
            copy.wait_recv()
        start(vec_copies(step))
        vec_pair(step - 1).start()

    def multiply_text():
        for copy in vec_copies(count - 2):
            copy.wait_recv()
        vec_pair(count - 2).start()
        grads = all_kv[...].astype(jnp.float32) * all_kv_scale[...]
        grads = grads.reshape(text_buf.shape[0], -1)
        total = jnp.zeros_like(kv_grad)
        for _ in range(3):
            part = grads.astype(jnp.bfloat16)
            grads = grads - part.astype(jnp.float32)
            total = total + matmul_tn(text_buf[...], part)
        kv_grad[...] = total
        kv_square[...] = jnp.sum((total * total).reshape(-1, 8, total.shape[1]), axis=0)
        start([kv_copy(i) for i in range(3)])

    square_buf[...] = jnp.zeros_like(square_buf)
    start(side_local + side_remote)
    start(load_right(0, 0))
    start(load_left(0, 0, 0, 0))
    push_right(0).start()
    start(pair_left(0, 0))
    for block in range(1, 5):
        push_right(block).start()

    @pl.loop(1, count)
    def _(step):
        start(pair_left(0, step))

    for copy in pair_left(0, 0):
        copy.wait_recv()
    start(load_left(0, 0, 0, 1))
    take_step(0, 0, True, False)
    for at in range(len(phases)):
        more = at + 1 < len(phases)
        if more:
            start(pair_right(at + 1))
            start(load_right(at + 1, 0))
            start(pair_left(at + 1, 0))
        if at == 1:
            sum_bands()

        @pl.loop(1, count - 1)
        def _(step, at=at, more=more):
            take_step(at, step, False, False)
            if at == 1:
                pass_sums(step)
            if more:
                start(pair_left(at + 1, step))

                @pl.when(step == count // 2)
                def _():
                    for copy in pair_right(at + 1):
                        copy.wait_recv()
                    start(load_right(at + 1, 1))
                    for copy in pair_left(at + 1, 0):
                        copy.wait_recv()
                    for far in range(2):
                        start(load_left(at + 1, 0, 0, far))

        if more:
            start(pair_left(at + 1, count - 1))
            for far in range(2):
                finish(load_right(at + 1, far))
            take_step(at + 1, 0, True, False)
        take_step(at, count - 1, False, True)
        if at == 1:
            multiply_text()
        for slot in range(2):
            for part in range(2):
                for copy in ring_copies(at, part, slot):
                    copy.wait_send()
            if at == 0:
                for copy in cross_copies(slot):
                    copy.wait_send()
        if at == 2:
            kv_copy(1).wait_recv()
            kv_passed().start()
        if at:
            close(at - 1)
    close(len(phases) - 1)
    vec_own.wait()
    kv_passed().wait()
    kv_copy(0).wait()
    kv_copy(1).wait_send()
    kv_copy(2).wait()

    @pl.loop(0, count - 1)
    def _(step):
        for copy in vec_copies(step):
            copy.wait_send()
        vec_pair(step).wait()

    square_out[...] = square_buf[...]
    for at, phase in enumerate(phases):
        for copy in pair_right(at) if at else [push_right(block) for block in range(5)]:
            copy.wait_send()

        @pl.loop(0, count)
        def _(step, at=at):
            for copy in pair_left(at, step):
                copy.wait_send()

        for unit in range(phase["first"], 8 if phase["kind"] == 0 else 6):
            finish(out_copies(at, unit))


def reduce_gradients(phases, lefts, rights, vectors, keyvals, text, wide_cols, deep_cols):
    count = lax.axis_size("clip")
    tokens = lefts[0].shape[0]
    wide_rows = lefts[1].shape[1] // count
    deep_rows = lefts[0].shape[1] // count
    band_count, _, kv_cols = keyvals.shape
    num = len(lefts)
    dma = pltpu.SemaphoreType.DMA
    units, lefts_of, rights_of = (8, 6), (5, 4), (5, 6)
    scratch = [pltpu.VMEM((2, lefts_of[k], 2 * tokens, 128), jnp.bfloat16) for k in range(2)]
    scratch += [pltpu.VMEM((rights_of[k], 2 * tokens, UNIT[1]), jnp.bfloat16) for k in range(2)]
    for _ in range(2):
        scratch += [pltpu.VMEM((2, units[k]) + UNIT, jnp.int16) for k in range(2)]
        scratch += [pltpu.VMEM((2, units[k], 1, UNIT[1]), jnp.float32) for k in range(2)]
    scratch += [pltpu.VMEM((units[k],) + UNIT, jnp.float32) for k in range(2)]
    scratch += [pltpu.VMEM((units[p["kind"]],) + UNIT, jnp.float32) for p in phases]
    scratch += [
        pltpu.VMEM((8, UNIT[1]), jnp.float32),
        dma((2, 2, 5, 2)),
        dma((2, 6, 2)),
        dma((len(phases), 5, count)),
        dma((len(phases), 5, count)),
        dma((num,)),
        dma((num,)),
        dma((2, 2, 2, 2)),
        dma((2, 2, 2, 2)),
        pltpu.SemaphoreType.REGULAR((2, 2)),
        dma((len(phases), 2, 2)),
        dma((len(phases), 2, 2)),
        dma((len(phases), 8)),
        dma((len(phases), 8)),
        dma((len(phases), 8)),
    ]
    for many in (6, 6, 8, 8):
        scratch += [pltpu.VMEM((many,) + UNIT, jnp.int16)]
        scratch += [pltpu.VMEM((many, 1, UNIT[1]), jnp.float32)]
    scratch += [
        dma((5,)),
        dma((5,)),
        *[
            pltpu.VMEM((2, SPLIT) + tile, kind)
            for _ in range(2)
            for tile, kind in ((UNIT, jnp.int16), ((1, UNIT[1]), jnp.float32))
        ],
        dma((2, 2)),
        dma((2, 2)),
        pltpu.SemaphoreType.REGULAR,
        pltpu.VMEM((band_count,) + vectors.shape, jnp.float32),
        pltpu.VMEM(keyvals.shape, jnp.float32),
        pltpu.VMEM(vectors.shape, jnp.float32),
        pltpu.VMEM((count,) + keyvals.shape[1:], jnp.int16),
        pltpu.VMEM((count, 1, kv_cols), jnp.float32),
        pltpu.VMEM(text.shape, jnp.bfloat16),
        pltpu.VMEM((text.shape[1], kv_cols), jnp.float32),
        dma((4,)),
        dma((2, band_count - 1)),
        dma((2, band_count - 1)),
        dma((count - 1, 3)),
        dma((count - 1, 3)),
        dma((count - 1,)),
        dma((count - 1,)),
        dma,
        dma((3,)),
        dma((3,)),
    ]
    out = pl.pallas_call(
        partial(reduce_kernel, count, tokens, phases),
        out_shape=(
            jax.ShapeDtypeStruct((wide_rows, wide_cols), jnp.float32),
            jax.ShapeDtypeStruct((deep_rows, deep_cols), jnp.float32),
            jax.ShapeDtypeStruct((8, UNIT[1]), jnp.float32),
            jax.ShapeDtypeStruct((count,) + vectors.shape, jnp.float32),
            jax.ShapeDtypeStruct((8, kv_cols), jnp.float32),
        )
        + tuple(jax.ShapeDtypeStruct(x.shape, x.dtype) for x in lefts)
        + tuple(jax.ShapeDtypeStruct((tokens, x.shape[1] // 2), x.dtype) for x in rights),
        in_specs=[ANY] * (2 * num + 3),
        out_specs=(ANY, ANY, IN_VMEM, ANY, IN_VMEM) + (ANY,) * (2 * num),
        scratch_shapes=scratch,
        compiler_params=pltpu.CompilerParams(
            collective_id=2, has_side_effects=True, vmem_limit_bytes=58 << 20
        ),
        cost_estimate=pl.CostEstimate(flops=3 * 10**11, bytes_accessed=8 * 10**8, transcendentals=0),
    )(*lefts, *rights, vectors, keyvals, text)
    return out[:5]


def total_kernel(count, part_ref, out_ref, mid, band_got, clip_got, *sems):
    me = lax.axis_index("clip")
    band = lax.axis_index("band")
    band_count = band_got.shape[0]
    band_peers = [(me, (band + step) % band_count) for step in range(1, band_count)]
    clip_peers = [((me + step) % count, band) for step in range(1, count)]
    greet(band_peers + clip_peers)
    stages = (
        (part_ref, band_got, band, band_peers, mid, sems[:2]),
        (mid, clip_got, me, clip_peers, out_ref, sems[2:]),
    )
    for value, got, index, peers, result, (send, recv) in stages:
        copies = [
            pltpu.make_async_remote_copy(
                value, got.at[index], send.at[step], recv.at[step], peer, MESH
            )
            for step, peer in enumerate(peers)
        ]
        for copy in copies:
            copy.start()
        got[index] = value[...]
        for copy in copies:
            copy.wait()
        result[...] = jnp.sum(got[...], 0)


def total_over_devices(value):
    count, band_count = lax.axis_size("clip"), lax.axis_size("band")
    dma = pltpu.SemaphoreType.DMA
    tile = (8, 128)
    return pl.pallas_call(
        partial(total_kernel, count),
        out_shape=jax.ShapeDtypeStruct(tile, jnp.float32),
        in_specs=[IN_VMEM],
        out_specs=IN_VMEM,
        scratch_shapes=[
            pltpu.VMEM(tile, jnp.float32),
            pltpu.VMEM((band_count,) + tile, jnp.float32),
            pltpu.VMEM((count,) + tile, jnp.float32),
            dma((band_count - 1,)),
            dma((band_count - 1,)),
            dma((count - 1,)),
            dma((count - 1,)),
        ],
        compiler_params=pltpu.CompilerParams(collective_id=3, has_side_effects=True),
    )(jnp.broadcast_to(value, tile))[0, 0]


def per_device(
    latents,
    noise_field,
    timesteps,
    null_flags,
    frame_mask,
    context,
    w_wide,
    m_wide,
    v_wide,
    w_deep,
    m_deep,
    v_deep,
    w_small,
    m_small,
    v_small,
):
    clip_count = lax.axis_size("clip")
    band_count = lax.axis_size("band")
    clip_at = lax.axis_index("clip")
    band_at = lax.axis_index("band")
    wide_rows = w_wide.shape[0]
    deep_rows = w_deep.shape[0]
    text_len, text_dim = context.shape[1:]
    facts = jnp.pad(
        jnp.concatenate([timesteps, frame_mask[0]])[None],
        ((0, 7), (0, 127 - frame_mask.shape[1])),
    )
    kept_text = context[0] * (1 - null_flags[0]).astype(jnp.bfloat16)
    text_cols = jnp.pad(
        kept_text.reshape(text_len, clip_count, band_count, -1).transpose(1, 2, 0, 3),
        ((0, 0), (0, 0), (0, TEXT_PAD - text_len), (0, 0)),
    )
    all_facts = exchange_facts(facts)
    all_times = all_facts[:, 0, 0].astype(jnp.float32)
    all_time_low = jax.nn.silu(time_features(all_times)).astype(jnp.bfloat16)
    time_rows = lax.dynamic_slice(
        all_time_low, (0, clip_at * wide_rows), (clip_count, wide_rows)
    )
    part_modul = matmul(time_rows, w_wide[:, : 12 * D].astype(jnp.bfloat16))
    kv_cols = 2 * D // band_count
    gathered, all_modul, all_text, keyval = gather_weights(
        (w_wide, w_deep),
        (
            (0, 22 * D, FF),
            (1, 0, D),
            (0, 20 * D, D),
            (0, 21 * D, D),
            (0, 18 * D, D),
            (0, 19 * D, D),
            (0, 12 * D, 3 * D),
            (0, 15 * D, 3 * D),
        ),
        (1, 2, 1, 2, 1, 2, 0, 0),
        part_modul.reshape(clip_count, band_count, -1, 128),
        text_cols,
    )
    up_a_w, down_a_w, query_w, cross_out_w, out_a_w, out_b_w, qkv_a_w, qkv_b_w = gathered
    all_text = all_text.transpose(0, 2, 1, 3)
    keyval = keyval.transpose(1, 0, 2).reshape(TEXT_PAD, 2 * D)
    late_up_b, late_down_b, all_modul = lax.optimization_barrier(
        (own_quarter(w_wide[:, 22 * D + FF :]), own_quarter(w_deep[:, 3 * D :]), all_modul)
    )
    up_b_w = lax.all_gather(late_up_b, ("clip", "band"), axis=0, tiled=True)
    down_b_w = lax.all_gather(late_down_b, ("clip", "band"), axis=0, tiled=True)
    small_low = w_small.astype(jnp.bfloat16)
    small_val = small_low.astype(jnp.float32)
    num_frames, num_rows, num_cols = (latents.shape[1], latents.shape[2], latents.shape[3])
    tok_count = num_frames * num_rows * num_cols
    all_mask = all_facts[:, 0, 1 : 1 + num_frames]
    global_count = jnp.sum(all_mask).astype(jnp.float32) * (num_rows * num_cols * CH * band_count)
    time_value = timesteps[0].astype(jnp.float32)
    noise_angle = 0.5 * math.pi * time_value / TMAX
    signal, spread = (jnp.cos(noise_angle), jnp.sin(noise_angle))
    clean_tok = token_order(latents[0])
    noise_tok = token_order(noise_field[0])
    run = num_rows * WIN
    part = SHIFT * WIN
    frame_windows = attend_pieces(tok_count, num_frames, "frame")
    half_windows = attend_pieces(tok_count, num_frames, "half")
    text_windows = attend_pieces(tok_count, num_frames, "text")
    noisy_low = (signal * clean_tok + spread * noise_tok).astype(jnp.bfloat16)
    target = signal * noise_tok - spread * clean_tok
    modulation = jnp.sum(all_modul, 0).reshape(12, D)
    mod_a, mod_b = (modulation[:6], modulation[6:])
    stream_zero = matmul(noisy_low, small_low[:CH]) + small_val[2 * CH]
    normed_a, back_a = jax.vjp(norm_modulated, stream_zero, mod_a[0], mod_a[1])
    in_a = normed_a.astype(jnp.bfloat16)
    qkv_a = matmul(in_a, qkv_a_w).astype(jnp.bfloat16)
    att_a, far_kv = attend_frames(qkv_a, frame_windows)
    proj_a = matmul(att_a, out_a_w)
    stream_one = stream_zero + mod_a[2] * proj_a
    stream_two, saved_a = mlp_forward(stream_one, mod_a, up_a_w, down_a_w)
    normed_b, back_b = jax.vjp(norm_modulated, stream_two, mod_b[0], mod_b[1])
    low_b = normed_b.astype(jnp.bfloat16)
    rolled = with_rows(low_b, shifted(first_rows(low_b, run, part), "band", -1), run)
    qkv_b = matmul(rolled, qkv_b_w).astype(jnp.bfloat16)
    win_kv = [(qkv_b, HEADS // 2, HEADS)]
    win_out = attend(qkv_b, win_kv, half_windows)
    att_b = with_rows(win_out, shifted(first_rows(win_out, run, part), "band", 1), run)
    proj_b = matmul(att_b, out_b_w)
    stream_three = stream_two + mod_b[2] * proj_b
    cross_val, cross_back = jax.vjp(norm_gained, stream_three, small_val[2 * CH + 1])
    cross_in = cross_val.astype(jnp.bfloat16)
    query_proj = matmul(cross_in, query_w).astype(jnp.bfloat16)
    text_kv = [(keyval, 0, HEADS // 2)]
    crossed = attend(query_proj, text_kv, text_windows, text_len)
    stream_four = stream_three + matmul(crossed, cross_out_w)
    stream_five, saved_b = mlp_forward(stream_four, mod_b, up_b_w, down_b_w)
    final_val, final_back = jax.vjp(norm_gained, stream_five, small_val[2 * CH + 2])
    final_low = final_val.astype(jnp.bfloat16)
    head_low = small_low[CH : 2 * CH]
    predicted = matmul_nt(final_low, head_low)
    weight_row = jnp.repeat(frame_mask[0].astype(jnp.float32), run)
    weight_row = jnp.tile(weight_row, num_cols // WIN)[:, None]
    pred_error = predicted - target
    loss_part = jnp.sum(weight_row * pred_error * pred_error)
    grad_pred = (weight_row * pred_error * (2.0 / global_count)).astype(jnp.bfloat16)
    grad_head = matmul_tn(grad_pred, final_low)
    grad_stream, grad_gain_f = final_back(matmul(grad_pred, head_low))
    grad_stream, mlp_factors_b, extra_b = mlp_backward(
        grad_stream, mod_b, up_b_w, down_b_w, saved_b
    )
    grad_cross = grad_stream.astype(jnp.bfloat16)
    grad_crossed = matmul_nt(grad_cross, cross_out_w).astype(jnp.bfloat16)
    grad_query, grad_keyval = attend_back(
        query_proj, text_kv, grad_crossed, text_windows, text_len
    )
    grad_part, grad_gain_c = cross_back(matmul_nt(grad_query, query_w))
    grad_stream = grad_stream + grad_part
    grad_proj = (mod_b[2] * grad_stream).astype(jnp.bfloat16)
    grad_gate_b = jnp.sum(grad_stream * proj_b, 0)
    factors_ob = (att_b, grad_proj)
    grad_att = matmul_nt(grad_proj, out_b_w).astype(jnp.bfloat16)
    grad_win = with_rows(grad_att, shifted(first_rows(grad_att, run, part), "band", -1), run)
    grad_qkv = attend_back(qkv_b, win_kv, grad_win, half_windows)[0]
    factors_qkvb = (rolled, grad_qkv)
    grad_in_roll = matmul_nt(grad_qkv, qkv_b_w)
    sent_back = shifted(first_rows(grad_in_roll, run, part), "band", 1)
    grad_normed = with_rows(grad_in_roll, sent_back, run)
    grad_part, grad_shift_b, grad_scale_b = back_b(grad_normed)
    grad_stream = grad_stream + grad_part
    grad_stream, mlp_factors_a, extra_a = mlp_backward(
        grad_stream, mod_a, up_a_w, down_a_w, saved_a
    )
    grad_proj = (mod_a[2] * grad_stream).astype(jnp.bfloat16)
    grad_gate_a = jnp.sum(grad_stream * proj_a, 0)
    factors_oa = (att_a, grad_proj)
    grad_att = matmul_nt(grad_proj, out_a_w).astype(jnp.bfloat16)
    grad_qkv = attend_frames_back(qkv_a, far_kv, grad_att, frame_windows)
    factors_qkva = (in_a, grad_qkv)
    grad_part, grad_shift_a, grad_scale_a = back_a(matmul_nt(grad_qkv, qkv_a_w))
    grad_stream = grad_stream + grad_part
    grad_patch = matmul_tn(noisy_low.astype(jnp.float32), grad_stream, lax.Precision.HIGHEST)
    grad_bias = jnp.sum(grad_stream, 0)
    grad_modul = jnp.stack(
        [
            grad_shift_a,
            grad_scale_a,
            grad_gate_a,
            extra_a[0],
            extra_a[1],
            extra_a[2],
            grad_shift_b,
            grad_scale_b,
            grad_gate_b,
            extra_b[0],
            extra_b[1],
            extra_b[2],
        ]
    ).reshape(1, 12 * D)
    grad_small = jnp.concatenate(
        [grad_patch, grad_head, grad_bias[None], grad_gain_c[None], grad_gain_f[None]], 0
    )
    factors = mlp_factors_b + (
        (crossed, grad_cross),
        (cross_in, grad_query),
        factors_ob,
        factors_qkvb,
    )
    factors += mlp_factors_a + (factors_oa, factors_qkva)
    if wide_rows == 128 and deep_rows == 512:
        phases = (
            {"kind": 0, "first": 0, "lefts": (0, 1), "cols": (3 * D, 10 * D + FF)},
            {"kind": 1, "first": 0, "lefts": (2, 3, 4, 5), "cols": (9 * D, 8 * D, 7 * D, 3 * D)},
            {"kind": 0, "first": 0, "lefts": (6, 7), "cols": (0, 10 * D)},
            {"kind": 1, "first": 2, "lefts": (8, 9), "cols": (6 * D, 0)},
        )
        used = 12 * D + grad_small.size
        vectors = jnp.concatenate(
            [grad_modul.reshape(-1), grad_small.reshape(-1), loss_part[None]]
        )
        vectors = jnp.pad(vectors, (0, 256 * 128 - vectors.shape[0])).reshape(256, 128)
        keyvals = grad_keyval.reshape(TEXT_PAD, band_count, kv_cols).transpose(1, 0, 2)
        wide_rest, deep_sum, squares, all_vectors, kv_squares = reduce_gradients(
            phases,
            [f[0] for f in factors],
            [f[1] for f in factors],
            vectors,
            keyvals,
            all_text.reshape(clip_count * TEXT_PAD, deep_rows),
            10 * D + 2 * FF,
            4 * D,
        )
        all_vectors = all_vectors.reshape(clip_count, -1)
        all_grad_modul = all_vectors[:, : 12 * D]
        small_sum = jnp.sum(all_vectors[:, 12 * D : used], 0).reshape(grad_small.shape)
        loss_sum = jnp.sum(all_vectors[:, used])
        square_part = jnp.sum(squares) / (band_count // 2) + jnp.sum(kv_squares)
    else:
        summed = [sum_rows(*pair) for pair in factors]
        wide_rest = jnp.concatenate([summed[i] for i in (9, 5, 8, 4, 3, 2, 7, 1)], 1)
        grad_keyval = lax.psum_scatter(grad_keyval, "band", scatter_dimension=1, tiled=True)
        grad_keyval = lax.all_gather(grad_keyval, "clip", axis=0, tiled=True)
        grad_w_ckv = matmul_tn(
            all_text.reshape(clip_count * TEXT_PAD, deep_rows).astype(jnp.float32),
            grad_keyval,
            lax.Precision.HIGHEST,
        )
        grad_w_ckv = lax.all_gather(grad_w_ckv, "band", axis=1, tiled=True)
        all_grad_modul = lax.all_gather(lax.psum(grad_modul, "band"), "clip", axis=0, tiled=True)
        loss_sum, small_sum = lax.psum((loss_part, grad_small), ("clip", "band"))
        deep_sum = jnp.concatenate([summed[6], grad_w_ckv, summed[0]], 1)
        square_part = sum(jnp.sum(x * x) for x in (wide_rest, deep_sum)) / band_count
    grad_w_ada = matmul_tn(time_rows.astype(jnp.float32), all_grad_modul, lax.Precision.HIGHEST)
    wide_sum = jnp.concatenate([grad_w_ada, wide_rest], 1)
    square_part += jnp.sum(grad_w_ada * grad_w_ada) / band_count
    square_sum = total_over_devices(square_part)
    grad_norm = jnp.sqrt(square_sum + jnp.sum(small_sum * small_sum))
    factor = CLIP_MAX / jnp.maximum(grad_norm, CLIP_MAX)
    new_wide = adam_update(w_wide, m_wide, v_wide, wide_sum * factor, 0.15)
    new_deep = adam_update(w_deep, m_deep, v_deep, deep_sum * factor, 0.05)
    new_small = adam_update(w_small, m_small, v_small, small_sum * factor, 0.5)
    loss = loss_sum / global_count
    return (
        loss,
        grad_norm,
        new_wide[0],
        new_wide[1],
        new_wide[2],
        new_deep[0],
        new_deep[1],
        new_deep[2],
        new_small[0],
        new_small[1],
        new_small[2],
    )


def solution(mesh):
    in_specs = (
        P("clip", None, "band", None, None),
        P("clip", None, "band", None, None),
        P("clip"),
        P("clip"),
        P("clip", None),
        P("clip", None, None),
        P("clip", None),
        P("clip", None),
        P("clip", None),
        P("clip", None),
        P("clip", None),
        P("clip", None),
        P(),
        P(),
        P(),
    )
    out_specs = (
        P(),
        P(),
        P("clip", None),
        P("clip", None),
        P("clip", None),
        P("clip", None),
        P("clip", None),
        P("clip", None),
        P(),
        P(),
        P(),
    )
    return jax.shard_map(
        per_device, mesh=mesh, in_specs=in_specs, out_specs=out_specs, check_vma=False
    )
```

```python
from functools import partial
import math

import jax
import jax.numpy as jnp
from jax import lax
from jax.experimental import pallas as pl
from jax.experimental.pallas import tpu as pltpu
from jax.sharding import PartitionSpec as P

D = 1024
HEADS = 16
HEAD_DIM = 64
FF = 4096
CH = 8
SPACE = 16
WIN = 8
SHIFT = 4
TMAX = 1000
STEP = 10


EPS_NORM = 1e-06
CLIP_MAX = 0.001
BETA_ONE = 0.9
BETA_TWO = 0.95
ADAM_EPS = 1e-08
DECAY = 0.1


def shifted(value, axis, by):
    length = lax.axis_size(axis)
    return lax.ppermute(value, axis, [(i, (i + by) % length) for i in range(length)])


def matmul(left_op, right_op):
    return jnp.dot(left_op, right_op, preferred_element_type=jnp.float32)


def matmul_tn(left_op, right_op, precision=None):
    return lax.dot_general(
        left_op,
        right_op,
        (((0,), (0,)), ((), ())),
        precision=precision,
        preferred_element_type=jnp.float32,
    )


def matmul_nt(left_op, right_op):
    return lax.dot_general(
        left_op, right_op, (((1,), (1,)), ((), ())), preferred_element_type=jnp.float32
    )


def layer_norm(field_in):
    average = jnp.mean(field_in, -1, keepdims=True)
    centred = field_in - average
    return centred * lax.rsqrt(jnp.mean(centred * centred, -1, keepdims=True) + EPS_NORM)


def norm_modulated(field_in, shift_vec, scale_vec):
    return layer_norm(field_in) * (1.0 + scale_vec) + shift_vec


def norm_gained(field_in, gain_vec):
    return layer_norm(field_in) * gain_vec


def time_features(time_value):
    half_width = D // 2
    frequency = jnp.exp(-math.log(10000.0) * jnp.arange(half_width, dtype=jnp.float32) / half_width)
    angles = time_value[..., None] * frequency
    return jnp.concatenate([jnp.cos(angles), jnp.sin(angles)], -1)


def token_order(grid):
    frames, rows, cols, width = grid.shape
    halves = grid.reshape(frames, rows, cols // WIN, WIN, width).transpose(2, 0, 1, 3, 4)
    return halves.reshape(frames * rows * cols, width)


def with_rows(tokens, first_rows, run):
    width = tokens.shape[1]
    runs = tokens.reshape(-1, run, width)
    return jnp.concatenate([first_rows, runs[:, first_rows.shape[1] :]], 1).reshape(-1, width)


def first_rows(tokens, run, part):
    return tokens.reshape(-1, run, tokens.shape[1])[:, :part]


def attend_pieces(tokens, frames, keys):
    if keys == "frame":
        run = tokens // (2 * frames)
        return [((f * run, run), (tokens // 2 + f * run, run)) for f in range(frames)]
    if keys == "half":
        return [((half * (tokens // 2), tokens // 2),) for half in range(2)]
    return [((0, tokens),)]


def take(ref, runs):
    pieces = [ref[low : low + many, :] for low, many in runs]
    return pieces[0] if len(pieces) == 1 else jnp.concatenate(pieces, 0)


def put(ref, cols, runs, value):
    done = 0
    for low, many in runs:
        ref[low : low + many, cols] = value[done : done + many].astype(ref.dtype)
        done += many


def softmax_of(scores, axis, text_len):
    if text_len:
        place = lax.broadcasted_iota(jnp.int32, scores.shape, axis)
        scores = jnp.where(place < text_len, scores, -1e30)
    weight = jnp.exp(scores - jnp.max(scores, axis, keepdims=True))
    return weight * (1.0 / jnp.sum(weight, axis, keepdims=True))


def lanes_of(head, shape):
    lane = lax.broadcasted_iota(jnp.int32, shape, 1)
    return lane < HEAD_DIM if head == 0 else lane >= HEAD_DIM


def only(head, value):
    return jnp.where(lanes_of(head, value.shape), value, jnp.zeros_like(value))


def attention_gradients(queries, keys, values, grad_out, text_len):
    queries, grad_out = stacked(queries), stacked(grad_out)
    probs = softmax_of(matmul_nt(keys, queries), 0, text_len)
    dprobs = matmul_nt(values, grad_out)
    dv = matmul(probs.astype(jnp.bfloat16), grad_out)
    inner = jnp.sum(probs * dprobs, 0, keepdims=True)
    dscores = (probs * (dprobs - inner)).astype(jnp.bfloat16)
    dk = matmul(dscores, queries)
    return unstacked(matmul_tn(dscores, keys)) * HEAD_DIM ** (-0.5), dk, dv


def attention_values(queries, keys, values, text_len):
    probs = softmax_of(matmul_nt(stacked(queries), keys), 1, text_len)
    return unstacked(matmul(probs.astype(jnp.bfloat16), values))


def stacked(rows):
    return jnp.concatenate([only(head, rows) for head in range(2)], 0)


def unstacked(rows):
    half = rows.shape[0] // 2
    return jnp.where(lanes_of(0, (half, rows.shape[1])), rows[:half], rows[half:])


def key_sets(key_refs, runs, text_len):
    if text_len:
        return key_refs[0][...]
    pieces = [take(ref, runs) for ref in key_refs]
    return pieces[0] if len(pieces) == 1 else jnp.concatenate(pieces, 0)


def attend_kernel(windows, text_len, sets, *refs):
    q_ref, k_refs, v_refs, out_ref = refs[0], refs[1 : 1 + sets], refs[1 + sets : 1 + 2 * sets], refs[-1]
    for runs in windows:
        queries = take(q_ref, runs) * HEAD_DIM ** (-0.5)
        keys, values = key_sets(k_refs, runs, text_len), key_sets(v_refs, runs, text_len)
        put(out_ref, slice(None), runs, attention_values(queries, keys, values, text_len))


def attend_back_kernel(windows, text_len, sets, *refs):
    q_ref, k_refs, v_refs = refs[0], refs[1 : 1 + sets], refs[1 + sets : 1 + 2 * sets]
    grad_ref = refs[1 + 2 * sets]
    dq_ref = refs[2 + 2 * sets]
    own_ref = refs[3 + 2 * sets] if text_len else None
    pair = pl.program_id(0)
    cols = [pl.ds(pl.multiple_of(i * D + pair * 2 * HEAD_DIM, 128), 2 * HEAD_DIM) for i in range(3)]
    merged = dq_ref.shape[1] == 3 * D
    for runs in windows:
        queries = take(q_ref, runs) * HEAD_DIM ** (-0.5)
        keys, values = key_sets(k_refs, runs, text_len), key_sets(v_refs, runs, text_len)
        grad_out = take(grad_ref, runs)
        dq, dk, dv = attention_gradients(queries, keys, values, grad_out, text_len)
        put(dq_ref, cols[0], runs, dq)
        if merged:
            put(dq_ref, cols[1], runs, dk)
            put(dq_ref, cols[2], runs, dv)
        else:
            own_ref[:, cols[0]] = dk
            own_ref[:, cols[1]] = dv


def pair_cols(which, pair):
    return pl.ds(pl.multiple_of(which * D + pair * 2 * HEAD_DIM, 128), 2 * HEAD_DIM)


def take_cols(ref, cols, runs):
    return jnp.concatenate([ref[low : low + many, cols] for low, many in runs], 0)


def attend_frames_kernel(windows, qkv_ref, out_ref, far_ref, send, recv):
    band = lax.axis_index("band")
    partner = (lax.axis_index("clip"), band + 1 - 2 * (band % 2))
    greet([partner])

    def copies(pair):
        return [
            pltpu.make_async_remote_copy(
                qkv_ref.at[:, pair_cols(1 + i, pair)],
                far_ref.at[:, pair_cols(i, pair)],
                send.at[pair, i],
                recv.at[pair, i],
                partner,
                MESH,
            )
            for i in range(2)
        ]

    @pl.loop(0, HEADS // 2)
    def _(pair):
        for copy in copies(pair):
            copy.start()

    @pl.loop(0, HEADS // 2)
    def _(pair):
        for copy in copies(pair):
            copy.wait_recv()
        for runs in windows:
            queries = take_cols(qkv_ref, pair_cols(0, pair), runs) * HEAD_DIM ** (-0.5)
            keys, values = (
                jnp.concatenate(
                    [
                        take_cols(qkv_ref, pair_cols(1 + i, pair), runs),
                        take_cols(far_ref, pair_cols(i, pair), runs),
                    ],
                    0,
                )
                for i in range(2)
            )
            put(
                out_ref, pair_cols(0, pair), runs, attention_values(queries, keys, values, 0)
            )

    @pl.loop(0, HEADS // 2)
    def _(pair):
        for copy in copies(pair):
            copy.wait_send()


def attend_frames_back_kernel(
    windows, qkv_ref, far_ref, grad_ref, out_ref, own_buf, far_put, far_got, send, recv
):
    band = lax.axis_index("band")
    partner = (lax.axis_index("clip"), band + 1 - 2 * (band % 2))
    greet([partner])

    def copies(pair):
        return [
            pltpu.make_async_remote_copy(
                far_put.at[:, pair_cols(i, pair)],
                far_got.at[:, pair_cols(i, pair)],
                send.at[pair, i],
                recv.at[pair, i],
                partner,
                MESH,
            )
            for i in range(2)
        ]

    def merge(pair):
        for i, copy in enumerate(copies(pair)):
            copy.wait_recv()
            cols = pair_cols(i, pair)
            total = own_buf[:, cols] + far_got[:, cols]
            out_ref[:, pair_cols(1 + i, pair)] = total.astype(jnp.bfloat16)

    @pl.loop(0, HEADS // 2)
    def _(pair):
        for runs in windows:
            queries = take_cols(qkv_ref, pair_cols(0, pair), runs) * HEAD_DIM ** (-0.5)
            keys, values = (
                jnp.concatenate(
                    [
                        take_cols(qkv_ref, pair_cols(1 + i, pair), runs),
                        take_cols(far_ref, pair_cols(i, pair), runs),
                    ],
                    0,
                )
                for i in range(2)
            )
            grad_out = take_cols(grad_ref, pair_cols(0, pair), runs)
            dq, *dkv = attention_gradients(queries, keys, values, grad_out, 0)
            put(out_ref, pair_cols(0, pair), runs, dq)
            half = keys.shape[0] // 2
            for i, value in enumerate(dkv):
                put(own_buf, pair_cols(i, pair), runs, value[:half])
                put(far_put, pair_cols(i, pair), runs, value[half:])
        for copy in copies(pair):
            copy.start()

        @pl.when(pair >= 1)
        def _():
            merge(pair - 1)

    merge(HEADS // 2 - 1)

    @pl.loop(0, HEADS // 2)
    def _(pair):
        for copy in copies(pair):
            copy.wait_send()


def next_bands():
    clip, band, count = lax.axis_index("clip"), lax.axis_index("band"), lax.axis_size("band")
    return (clip, (band + 1) % count), (clip, (band + count - 1) % count)


def half_window(qkv_ref, half, pair):
    tokens = qkv_ref.shape[0] // 2
    rows = pl.ds(half * tokens, tokens)
    queries, keys, values = (qkv_ref[rows, pair_cols(i, pair)] for i in range(3))
    return queries * HEAD_DIM ** (-0.5), keys, values


def attend_halves_kernel(part, qkv_ref, out_ref, put_buf, send, recv):
    following, preceding = next_bands()
    greet([following, preceding])
    runs, run = out_ref.shape[:2]

    def copy(pair):
        cols = pair_cols(0, pair)
        return pltpu.make_async_remote_copy(
            put_buf.at[:, :, cols],
            out_ref.at[:, pl.ds(0, part), cols],
            send.at[pair],
            recv.at[pair],
            following,
            MESH,
        )

    @pl.loop(0, HEADS // 2)
    def _(pair):
        for half in range(2):
            values = attention_values(*half_window(qkv_ref, half, pair), 0).astype(jnp.bfloat16)
            values = values.reshape(runs // 2, run, 2 * HEAD_DIM)
            low = half * (runs // 2)
            put_buf[low : low + runs // 2, :, pair_cols(0, pair)] = values[:, :part]
            out_ref[low : low + runs // 2, part:, pair_cols(0, pair)] = values[:, part:]
        copy(pair).start()

    @pl.loop(0, HEADS // 2)
    def _(pair):
        copy(pair).wait()


def attend_halves_back_kernel(part, qkv_ref, grad_ref, out_ref, got_buf, send, recv):
    following, preceding = next_bands()
    greet([following, preceding])
    runs, run = grad_ref.shape[:2]

    def copy(pair):
        cols = pair_cols(0, pair)
        return pltpu.make_async_remote_copy(
            grad_ref.at[:, pl.ds(0, part), cols],
            got_buf.at[:, :, cols],
            send.at[pair],
            recv.at[pair],
            preceding,
            MESH,
        )

    @pl.loop(0, HEADS // 2)
    def _(pair):
        copy(pair).start()

    @pl.loop(0, HEADS // 2)
    def _(pair):
        copy(pair).wait_recv()
        for half in range(2):
            low = half * (runs // 2)
            pieces = (
                got_buf[low : low + runs // 2, :, pair_cols(0, pair)],
                grad_ref[low : low + runs // 2, part:, pair_cols(0, pair)],
            )
            grad_out = jnp.concatenate(pieces, 1).reshape(-1, 2 * HEAD_DIM)
            parts = attention_gradients(*half_window(qkv_ref, half, pair), grad_out, 0)
            rows = pl.ds(low * run, grad_out.shape[0])
            for i, value in enumerate(parts):
                out_ref[rows, pair_cols(i, pair)] = value.astype(jnp.bfloat16)

    @pl.loop(0, HEADS // 2)
    def _(pair):
        copy(pair).wait_send()


def attend_halves(qkv, run, part):
    tokens = qkv.shape[0]
    dma = pltpu.SemaphoreType.DMA((HEADS // 2,))
    return pl.pallas_call(
        partial(attend_halves_kernel, part),
        out_shape=jax.ShapeDtypeStruct((tokens // run, run, D), jnp.bfloat16),
        in_specs=[IN_VMEM],
        out_specs=IN_VMEM,
        scratch_shapes=[pltpu.VMEM((tokens // run, part, D), jnp.bfloat16), dma, dma],
        compiler_params=pltpu.CompilerParams(
            collective_id=6, has_side_effects=True, vmem_limit_bytes=40 << 20
        ),
        cost_estimate=attention_cost(tokens, 320, 2),
    )(qkv).reshape(tokens, D)


def attend_halves_back(qkv, grad_out, run, part):
    tokens = qkv.shape[0]
    dma = pltpu.SemaphoreType.DMA((HEADS // 2,))
    return pl.pallas_call(
        partial(attend_halves_back_kernel, part),
        out_shape=jax.ShapeDtypeStruct(qkv.shape, jnp.bfloat16),
        in_specs=[IN_VMEM] * 2,
        out_specs=IN_VMEM,
        scratch_shapes=[pltpu.VMEM((tokens // run, part, D), jnp.bfloat16), dma, dma],
        compiler_params=pltpu.CompilerParams(
            collective_id=7, has_side_effects=True, vmem_limit_bytes=50 << 20
        ),
        cost_estimate=attention_cost(tokens, 320, 5),
    )(qkv, grad_out.reshape(tokens // run, run, D))


def attend_frames(qkv, windows):
    tokens = qkv.shape[0]
    dma = pltpu.SemaphoreType.DMA((HEADS // 2, 2))
    return pl.pallas_call(
        partial(attend_frames_kernel, windows),
        out_shape=(
            jax.ShapeDtypeStruct((tokens, D), jnp.bfloat16),
            jax.ShapeDtypeStruct((tokens, 2 * D), jnp.bfloat16),
        ),
        in_specs=[IN_VMEM],
        out_specs=(IN_VMEM,) * 2,
        scratch_shapes=[dma, dma],
        compiler_params=pltpu.CompilerParams(
            collective_id=4, has_side_effects=True, vmem_limit_bytes=40 << 20
        ),
        cost_estimate=attention_cost(tokens, 256, 2),
    )(qkv)


def attend_frames_back(qkv, far_kv, grad_out, windows):
    tokens = qkv.shape[0]
    dma = pltpu.SemaphoreType.DMA((HEADS // 2, 2))
    return pl.pallas_call(
        partial(attend_frames_back_kernel, windows),
        out_shape=jax.ShapeDtypeStruct(qkv.shape, jnp.bfloat16),
        in_specs=[IN_VMEM] * 3,
        out_specs=IN_VMEM,
        scratch_shapes=[pltpu.VMEM((tokens, 2 * D), jnp.float32)] * 3 + [dma, dma],
        compiler_params=pltpu.CompilerParams(
            collective_id=5, has_side_effects=True, vmem_limit_bytes=50 << 20
        ),
        cost_estimate=attention_cost(tokens, 256, 5),
    )(qkv, far_kv, grad_out)


def head_cols(array, first):
    return array, pl.BlockSpec((array.shape[0], 2 * HEAD_DIM), lambda h: (0, first + h))


def attention_operands(queries, key_values):
    ins = [head_cols(queries, 0)]
    ins += [head_cols(array, first) for array, first, _ in key_values]
    return ins + [head_cols(array, second) for array, _, second in key_values]


def attention_cost(tokens, keys, products):
    flops = 2 * products * tokens * keys * D * 2
    return pl.CostEstimate(
        flops=flops, bytes_accessed=tokens * D * 2 * 8, transcendentals=tokens * keys * HEADS
    )


def attend(queries, key_values, windows, text_len=0):
    tokens = queries.shape[0]
    ins = attention_operands(queries, key_values)
    return pl.pallas_call(
        partial(attend_kernel, windows, text_len, len(key_values)),
        grid=(HEADS // 2,),
        in_specs=[spec for _, spec in ins],
        out_specs=pl.BlockSpec((tokens, 2 * HEAD_DIM), lambda h: (0, h)),
        out_shape=jax.ShapeDtypeStruct((tokens, D), jnp.bfloat16),
        compiler_params=pltpu.CompilerParams(vmem_limit_bytes=40 << 20),
        cost_estimate=attention_cost(tokens, 320, 2),
    )(*[array for array, _ in ins])


def attend_back(queries, key_values, grad_out, windows, text_len=0):
    tokens = queries.shape[0]
    ins = attention_operands(queries, key_values) + [head_cols(grad_out, 0)]
    sets = len(key_values)
    whole = lambda rows, cols: pl.BlockSpec((rows, cols), lambda h: (0, 0))
    if sets == 1 and not text_len:
        outs = [((tokens, 3 * D), jnp.bfloat16)]
    else:
        rows = key_values[0][0].shape[0]
        outs = [((tokens, D), jnp.bfloat16)] + [((rows, 2 * D), jnp.float32)] * sets
    return pl.pallas_call(
        partial(attend_back_kernel, windows, text_len, sets),
        grid=(HEADS // 2,),
        in_specs=[spec for _, spec in ins],
        out_specs=[whole(*shape) for shape, _ in outs],
        out_shape=[jax.ShapeDtypeStruct(*out) for out in outs],
        compiler_params=pltpu.CompilerParams(vmem_limit_bytes=50 << 20),
        cost_estimate=attention_cost(tokens, 320, 5),
    )(*[array for array, _ in ins])


def mlp_forward(stream, modul, up_weight, down_weight):
    mlp_val, norm_back = jax.vjp(norm_modulated, stream, modul[3], modul[4])
    mlp_in = mlp_val.astype(jnp.bfloat16)
    up_proj = matmul(mlp_in, up_weight)
    share = 0.5 + 0.5 * lax.erf(up_proj * math.sqrt(0.5))
    gelu_val = up_proj * share
    slope = share + up_proj * (jnp.exp(-0.5 * up_proj * up_proj) / math.sqrt(2.0 * math.pi))
    gelu_low = gelu_val.astype(jnp.bfloat16)
    down_proj = matmul(gelu_low, down_weight)
    return (stream + modul[5] * down_proj, (norm_back, mlp_in, slope, gelu_low, down_proj))


def mlp_backward(grad_stream, modul, up_weight, down_weight, saved):
    norm_back, mlp_in, slope, gelu_low, down_proj = saved
    grad_down = (modul[5] * grad_stream).astype(jnp.bfloat16)
    grad_gate = jnp.sum(grad_stream * down_proj, 0)
    grad_up = (slope * matmul_nt(grad_down, down_weight)).astype(jnp.bfloat16)
    grad_part, grad_shift, grad_scale = norm_back(matmul_nt(grad_up, up_weight))
    factors = ((gelu_low, grad_down), (mlp_in, grad_up))
    return (grad_stream + grad_part, factors, (grad_shift, grad_scale, grad_gate))


def adam_update(weight, first_mom, second_mom, grad_val, learn_rate):
    first_mom = BETA_ONE * first_mom + (1.0 - BETA_ONE) * grad_val
    second_mom = BETA_TWO * second_mom + (1.0 - BETA_TWO) * grad_val * grad_val
    first_hat = first_mom / (1.0 - BETA_ONE**STEP)
    second_hat = second_mom / (1.0 - BETA_TWO**STEP)
    weight = weight - learn_rate * (first_hat / (jnp.sqrt(second_hat) + ADAM_EPS) + DECAY * weight)
    return (weight, first_mom, second_mom)

MESH = pl.DeviceIdType.MESH
ANY = pl.BlockSpec(memory_space=pl.ANY)
IN_VMEM = pl.BlockSpec(memory_space=pltpu.VMEM)
TEXT_PAD = 80


def ring_place(clip, count):
    half = clip // 2
    odd = clip % 2
    return half + odd * (count - 1 - 2 * half)


def ring_clip(place, count):
    far = place // (count // 2)
    return (1 - far) * 2 * place + far * (2 * (count - 1 - place) + 1)


def greet(peers):
    barrier = pltpu.get_barrier_semaphore()
    for peer in peers:
        pl.semaphore_signal(barrier, inc=1, device_id=peer, device_id_type=MESH)
    pl.semaphore_wait(barrier, len(peers))


def exchange_kernel(count, facts_ref, facts_out, send, recv):
    me = lax.axis_index("clip")
    band = lax.axis_index("band")
    peers = [((me + step) % count, band) for step in range(1, count)]
    greet(peers)
    sent = [
        pltpu.make_async_remote_copy(
            facts_ref, facts_out.at[me], send.at[step], recv.at[step], peer, MESH
        )
        for step, peer in enumerate(peers)
    ]
    for copy in sent:
        copy.start()
    facts_out[me] = facts_ref[...]
    for copy in sent:
        copy.wait()


def exchange_facts(facts):
    count = lax.axis_size("clip")
    return pl.pallas_call(
        partial(exchange_kernel, count),
        out_shape=jax.ShapeDtypeStruct((count,) + facts.shape, facts.dtype),
        in_specs=[IN_VMEM],
        out_specs=IN_VMEM,
        scratch_shapes=[pltpu.SemaphoreType.DMA((count - 1,))] * 2,
        compiler_params=pltpu.CompilerParams(collective_id=0, has_side_effects=True),
    )(facts)


def gather_kernel(count, picks, sides, *refs):
    num = len(picks)
    packs, vec_ref, text_ref = refs[:2], refs[2], refs[3]
    full, (vec_out, text_out, kv_out) = refs[4 : 4 + num], refs[4 + num : 7 + num]
    refs = refs[7 + num :]
    wide, shards = refs[:num], refs[num : 2 * num]
    ring_send, ring_recv, pair_send, pair_recv, cross_send, cross_recv = refs[2 * num : 2 * num + 6]
    load_sem, own_sem, part_send, part_recv, part_own = refs[2 * num + 6 : 2 * num + 11]
    kv_wide, kv_part, kv_put, kv_got, kv_sum, kv_load, kv_send, kv_recv, band_send, band_recv = refs[
        2 * num + 11 : 2 * num + 21
    ]
    share_send, share_recv = refs[2 * num + 21 :]
    shapes = [(packs[pack].shape[0], cols) for pack, _, cols in picks]
    loads = [
        pltpu.make_async_copy(
            packs[pack].at[:, pl.ds(start, cols)], wide[group], load_sem.at[group]
        )
        for group, (pack, start, cols) in enumerate(picks)
    ]
    kv_width = kv_wide.shape[1]
    kv_first = D + lax.axis_index("band") * kv_width
    kv_weight = pltpu.make_async_copy(
        packs[1].at[:, pl.ds(pl.multiple_of(kv_first, 128), kv_width)], kv_wide, kv_load
    )
    for copy in loads + [kv_weight]:
        copy.start()
    me = lax.axis_index("clip")
    band = lax.axis_index("band")
    core = band % 2
    place = ring_place(me, count)
    onward = 1 - 2 * core
    following = (ring_clip((place + onward + count) % count, count), band)
    plane = band // 2
    partner = (me, band + 1 - 2 * core)
    mirror = (me, band + 2 - 4 * plane)
    peers = [((me + step) % count, band) for step in range(1, count)]
    band_count = 2 * D // kv_width
    band_peers = [(me, (band + step) % band_count) for step in range(1, band_count)]
    greet(peers + band_peers)

    def block(ref, group, owner):
        rows, cols = shapes[group]
        return ref.at[
            pl.ds(pl.multiple_of(owner * rows, rows), rows),
            pl.ds(pl.multiple_of(core * (cols // 2), 128), cols // 2),
        ]

    def ring_copy(group, step):
        owner = ring_clip((place - onward * step + 2 * count) % count, count)
        there = block(full[group], group, owner)
        return pltpu.make_async_remote_copy(
            there, there, ring_send.at[step, group], ring_recv.at[step, group], following, MESH
        )

    def handed(group, step, send, recv, peer):
        owner = ring_clip((place - onward * (step + 1) + 2 * count) % count, count)
        there = block(full[group], group, owner)
        return pltpu.make_async_remote_copy(
            there, there, send.at[step, group], recv.at[step, group], peer, MESH
        )

    def pair_copy(group, step):
        return handed(group, step, pair_send, pair_recv, partner)

    def cross_copy(group, step):
        return handed(group, step, cross_send, cross_recv, mirror)

    def in_ring(group):
        def decorate(body):
            if sides[group]:
                pl.when(plane == sides[group] - 1)(body)
            else:
                body()

        return decorate

    def off_ring(group, also=None):
        def decorate(body):
            if sides[group]:
                off = plane != sides[group] - 1
                pl.when(off if also is None else jnp.logical_and(off, also))(body)

        return decorate

    def ring_arrival(group, step, onto):
        ring_copy(group, step).wait_recv()
        if onto:
            ring_copy(group, step + 1).start()
        pair_copy(group, step).start()
        if sides[group]:
            cross_copy(group, step).start()

    def cross_arrival(group, step):
        cross_copy(group, step).wait_recv()
        pair_copy(group, step).start()

    def own_copy(group):
        rows, cols = shapes[group]
        return pltpu.make_async_copy(
            shards[group],
            full[group].at[pl.ds(pl.multiple_of(me * rows, rows), rows), :],
            own_sem.at[group],
        )

    parts = []
    for step, peer in enumerate(peers):
        for which, (src, dst) in enumerate(((vec_ref, vec_out), (text_ref, text_out))):
            parts.append(
                pltpu.make_async_remote_copy(
                    src.at[peer[0], band],
                    dst.at[me, band],
                    part_send.at[which, step],
                    part_recv.at[which, step],
                    peer,
                    MESH,
                )
            )
    parts_own = [
        pltpu.make_async_copy(src.at[me, band], dst.at[me, band], part_own.at[which])
        for which, (src, dst) in enumerate(((vec_ref, vec_out), (text_ref, text_out)))
    ]
    for copy in parts_own + parts:
        copy.start()
    for group in range(num):
        rows, cols = shapes[group]
        loads[group].wait()
        shards[group][...] = wide[group][...].astype(jnp.bfloat16)
        own_copy(group).start()

        @in_ring(group)
        def _(group=group, rows=rows, cols=cols):
            pltpu.make_async_remote_copy(
                shards[group].at[:, pl.ds(pl.multiple_of(core * (cols // 2), 128), cols // 2)],
                block(full[group], group, me),
                ring_send.at[0, group],
                ring_recv.at[0, group],
                following,
                MESH,
            ).start()

    def kv_copy(hop):
        return pltpu.make_async_remote_copy(
            kv_put.at[hop], kv_got.at[hop], kv_send.at[hop], kv_recv.at[hop], following, MESH
        )

    def kv_hop(hop):
        owner = ring_clip((place - onward * (hop + 1) + 2 * count) % count, count)
        total = kv_part[owner]
        if not isinstance(hop, int) or hop > 0:
            kv_copy(hop - 1).wait_recv()
            total = total + kv_got[hop - 1]
        kv_put[hop] = total
        kv_copy(hop).start()

    def band_copies():
        return [
            pltpu.make_async_remote_copy(
                kv_sum, kv_out.at[band], band_send.at[step], band_recv.at[step], peer, MESH
            )
            for step, peer in enumerate(band_peers)
        ]

    shares = [
        pltpu.make_async_remote_copy(
            out.at[:, band],
            out.at[:, band],
            share_send.at[which, step],
            share_recv.at[which, step],
            peer,
            MESH,
        )
        for step, peer in enumerate(band_peers)
        for which, out in enumerate((vec_out, text_out))
    ]

    def share():
        for copy in parts_own + parts:
            copy.wait()
        for copy in shares:
            copy.start()

    def multiply():
        for copy in shares:
            copy.wait()
        kv_weight.wait()
        weight = kv_wide[...].astype(jnp.bfloat16)
        depth = weight.shape[0] // band_count
        for owner in range(count):
            kv_part[owner] = sum(
                matmul(text_out[owner, part], weight[part * depth : (part + 1) * depth])
                for part in range(band_count)
            )
        kv_hop(0)

    @pl.loop(1, count - 1)
    def _(step):
        for group in range(num):

            @in_ring(group)
            def _(group=group):
                ring_arrival(group, step - 1, True)

        pl.when(step == 1)(share)
        pl.when(step == 2)(multiply)

        @pl.when(step >= 3)
        def _():
            kv_hop(step - 2)
        for group in range(num):

            @off_ring(group, step >= 2)
            def _(group=group):
                cross_arrival(group, step - 2)

    for group in range(num):

        @in_ring(group)
        def _(group=group):
            ring_arrival(group, count - 2, False)

    kv_hop(count - 3)
    for late in (count - 3, count - 2):
        for group in range(num):

            @off_ring(group)
            def _(group=group, late=late):
                cross_arrival(group, late)

        if late == count - 3:
            kv_hop(count - 2)
    kv_copy(count - 2).wait_recv()
    kv_sum[...] = (kv_part[me] + kv_got[count - 2]).astype(jnp.bfloat16)
    kv_out[band] = kv_sum[...]
    for copy in band_copies():
        copy.start()
    for group in range(num):
        own_copy(group).wait()

    @pl.loop(0, count - 1)
    def _(step):
        for group in range(num):

            @in_ring(group)
            def _(group=group):
                ring_copy(group, step).wait_send()
                if sides[group]:
                    cross_copy(group, step).wait_send()

            pair_copy(group, step).wait()
        kv_copy(step).wait_send()

    for copy in band_copies():
        copy.wait()


def own_quarter(shard):
    rows = shard.shape[0] // lax.axis_size("band")
    own = lax.dynamic_slice_in_dim(shard, lax.axis_index("band") * rows, rows, 0)
    return own.astype(jnp.bfloat16)


def sum_rows(left, right):
    part = lax.psum_scatter(
        matmul_tn(left, right), ("clip", "band"), scatter_dimension=0, tiled=True
    )
    return lax.all_gather(part, "band", axis=0, tiled=True)


def gather_weights(packs, picks, sides, vectors, texts):
    count, band_count = lax.axis_size("clip"), lax.axis_size("band")
    num = len(picks)
    dma = pltpu.SemaphoreType.DMA
    shapes = [(packs[pack].shape[0], cols) for pack, _, cols in picks]
    kv_shape = (texts.shape[2], 2 * D // band_count)
    kv_all = pltpu.VMEM((count,) + kv_shape, jnp.float32)
    kv_hops = pltpu.VMEM((count - 1,) + kv_shape, jnp.float32)
    out = pl.pallas_call(
        partial(gather_kernel, count, picks, sides),
        out_shape=tuple(
            jax.ShapeDtypeStruct((count * rows, cols), jnp.bfloat16) for rows, cols in shapes
        )
        + tuple(jax.ShapeDtypeStruct(v.shape, v.dtype) for v in (vectors, texts))
        + (jax.ShapeDtypeStruct((band_count,) + kv_shape, jnp.bfloat16),),
        in_specs=[ANY] * 4,
        out_specs=(ANY,) * num + (IN_VMEM,) * 3,
        scratch_shapes=[pltpu.VMEM(shape, jnp.float32) for shape in shapes]
        + [pltpu.VMEM(shape, jnp.bfloat16) for shape in shapes]
        + [dma((count - 1, num))] * 6
        + [dma((num,)), dma((num,)), dma((2, count - 1)), dma((2, count - 1)), dma((2,))]
        + [
            pltpu.VMEM((packs[1].shape[0], kv_shape[1]), jnp.float32),
            kv_all,
            kv_hops,
            kv_hops,
            pltpu.VMEM(kv_shape, jnp.bfloat16),
            dma,
            dma((count - 1,)),
            dma((count - 1,)),
            dma((band_count - 1,)),
            dma((band_count - 1,)),
            dma((2, band_count - 1)),
            dma((2, band_count - 1)),
        ],
        compiler_params=pltpu.CompilerParams(
            collective_id=1, has_side_effects=True, vmem_limit_bytes=50 << 20
        ),
        cost_estimate=pl.CostEstimate(flops=2 * 10**11, bytes_accessed=6 * 10**8, transcendentals=0),
    )(*packs, vectors, texts)
    return out[:num], out[num], out[num + 1], out[num + 2]


WIRE_MAX = 32767.0
WIRE_LEAST = 1e-30
UNIT = (128, 512)


SPLIT = 2


def unit_parts(at, kind, first):
    if at == 0:
        return ((0, 4, lambda u: u, lambda u: 0), (4, SPLIT, lambda u: 4, lambda u: u - 3))
    if kind == 0:
        return ((0, 4, lambda u: u, lambda u: 0), (4, 4, lambda u: 4, lambda u: u - 3))
    if first:
        return ((2, 2, lambda u: u, lambda u: u), (4, 2, lambda u: 3, lambda u: u))
    return ((0, 3, lambda u: u, lambda u: u), (3, 3, lambda u: 3, lambda u: u))


def reduce_kernel(count, tokens, phases, *refs):
    num = sum(len(phase["lefts"]) for phase in phases)
    lefts, rights = refs[:num], refs[num : 2 * num]
    vec_ref, kv_ref, text_ref = refs[2 * num : 2 * num + 3]
    refs = refs[2 * num + 3 :]
    wide_out, deep_out, square_out, all_vec, kv_square = refs[:5]
    left_far, right_far = refs[5 : 5 + num], refs[5 + num : 5 + 2 * num]
    scratch = refs[5 + 2 * num :]
    left_buf, right_buf, got_low, got_scale, put_low, put_scale, plane_put = (
        scratch[2 * i : 2 * i + 2] for i in range(7)
    )
    plane_got = scratch[14 : 14 + len(phases)]
    (
        square_buf,
        left_sem,
        right_sem,
        pair_send,
        pair_recv,
        half_send,
        half_recv,
        ring_send,
        ring_recv,
        credit,
        plane_send,
        plane_recv,
        out_sem,
        out_send,
        out_recv,
        last_put,
        last_put_scale,
        last_got,
        last_got_scale,
        late_put,
        late_put_scale,
        late_got,
        late_got_scale,
        push_send,
        push_recv,
        cross_put,
        cross_put_scale,
        cross_got,
        cross_got_scale,
        cross_send,
        cross_recv,
        cross_credit,
        vec_got,
        kv_got,
        vec_sum,
        all_kv,
        all_kv_scale,
        text_buf,
        kv_grad,
        side_own,
        side_send,
        side_recv,
        vec_send,
        vec_recv,
        vec_pair_send,
        vec_pair_recv,
        kv_own,
        kv_send,
        kv_recv,
    ) = scratch[14 + len(phases) :]
    me = lax.axis_index("clip")
    band = lax.axis_index("band")
    core = band % 2
    plane = band // 2
    place = ring_place(me, count)
    onward = 1 - 2 * core
    following = (ring_clip((place + onward + count) % count, count), band)
    preceding = (ring_clip((place - onward + count) % count, count), band)
    partner = (me, band + 1 - 2 * core)
    mirror = (me, band + 2 - 4 * plane)
    band_count = vec_got.shape[0]
    band_peers = [(me, (band + step) % band_count) for step in range(1, band_count)]
    greet([following, preceding] + band_peers)

    def owner_at(step, way):
        return ring_clip((place - way * (step + 1) + 2 * count) % count, count)

    def left_blocks(at):
        phase = phases[at]
        if phase["kind"] == 0:
            return [(b, phase["lefts"][0], b, 4) for b in range(4)] + [(4, phase["lefts"][1], 0, 1)]
        first = phase["first"]
        return [(first + i, left, 0, 1) for i, left in enumerate(phase["lefts"])]

    def right_blocks(at):
        phase = phases[at]
        if phase["kind"] == 0:
            return [(0, phase["lefts"][0], 0)] + [(1 + i, phase["lefts"][1], i) for i in range(4)]
        first = phase["first"]
        return [(first + i, phase["lefts"][i], 0) for i in range(3 - first)] + [
            (3 + i, phase["lefts"][-1], i) for i in range(3)
        ]

    def left_cols(step, way, which, many):
        width = lefts_width // count if many == 1 else deep_width // count
        start = owner_at(step, way) * width + which * 128
        return pl.ds(pl.multiple_of(start, 128), 128)

    lefts_width = lefts[phases[1]["lefts"][0]].shape[1]
    deep_width = lefts[phases[0]["lefts"][0]].shape[1]

    def pair_left(at, step):
        out = []
        for block, operand, which, many in left_blocks(at):
            cols = left_cols(step, -onward, which, many)
            out.append(
                pltpu.make_async_remote_copy(
                    lefts[operand].at[:, cols],
                    left_far[operand].at[:, cols],
                    pair_send.at[at, block, step],
                    pair_recv.at[at, block, step],
                    partner,
                    MESH,
                )
            )
        return out

    def pair_right(at):
        out = []
        for i, operand in enumerate(phases[at]["lefts"]):
            half = rights[operand].shape[1] // 2
            out.append(
                pltpu.make_async_remote_copy(
                    rights[operand].at[:, pl.ds(pl.multiple_of((1 - core) * half, 128), half)],
                    right_far[operand],
                    half_send.at[operand],
                    half_recv.at[operand],
                    partner,
                    MESH,
                )
            )
        return out

    def load_left(at, step, slot, far):
        kind = phases[at]["kind"]
        out = []
        for block, operand, which, many in left_blocks(at):
            cols = left_cols(step, onward, which, many)
            source = left_far if far else lefts
            out.append(
                pltpu.make_async_copy(
                    source[operand].at[:, cols],
                    left_buf[kind].at[slot, block, pl.ds(far * tokens, tokens), :],
                    left_sem.at[kind, slot, block, far],
                )
            )
        return out

    def load_right(at, far):
        kind = phases[at]["kind"]
        out = []
        for block, operand, which in right_blocks(at):
            if far:
                source = right_far[operand].at[:, pl.ds(which * UNIT[1], UNIT[1])]
            else:
                half = rights[operand].shape[1] // 2
                start = pl.multiple_of(core * half + which * UNIT[1], 128)
                source = rights[operand].at[:, pl.ds(start, UNIT[1])]
            out.append(
                pltpu.make_async_copy(
                    source,
                    right_buf[kind].at[block, pl.ds(far * tokens, tokens), :],
                    right_sem.at[kind, block, far],
                )
            )
        return out

    def ring_copies(at, part, slot):
        kind = phases[at]["kind"]
        units = pl.ds(*unit_parts(at, kind, phases[at]["first"])[part][:2])
        return [
            pltpu.make_async_remote_copy(
                put.at[slot, units],
                got.at[slot, units],
                ring_send.at[kind, slot, part, i],
                ring_recv.at[kind, slot, part, i],
                following,
                MESH,
            )
            for i, (put, got) in enumerate(
                ((put_low[kind], got_low[kind]), (put_scale[kind], got_scale[kind]))
            )
        ]

    def plane_copies(at, part):
        kind = phases[at]["kind"]
        units = pl.ds(*unit_parts(at, kind, phases[at]["first"])[part][:2])
        pairs = ((plane_put[kind], plane_got[at]),)
        if at in coded:
            pairs = (coded[at][::2], coded[at][1::2])
        return [
            pltpu.make_async_remote_copy(
                here.at[units],
                there.at[units],
                plane_send.at[at, part, i],
                plane_recv.at[at, part, i],
                mirror,
                MESH,
            )
            for i, (here, there) in enumerate(pairs)
        ]

    coded = {
        len(phases) - 2: (late_put, late_put_scale, late_got, late_got_scale),
        len(phases) - 1: (last_put, last_put_scale, last_got, last_got_scale),
    }

    def split_unit(pair, of_plane):
        return 4 + 2 * pair + of_plane

    def split_copy(pair, of_plane):
        unit = split_unit(pair, of_plane)
        return pltpu.make_async_remote_copy(
            plane_put[0].at[unit],
            plane_got[0].at[unit],
            plane_send.at[0, 1, pair],
            plane_recv.at[0, 1, pair],
            mirror,
            MESH,
        )

    def cross_copies(slot):
        return [
            pltpu.make_async_remote_copy(
                here.at[slot], there.at[slot], cross_send.at[slot, i], cross_recv.at[slot, i], mirror, MESH
            )
            for i, (here, there) in enumerate(
                ((cross_put, cross_got), (cross_put_scale, cross_got_scale))
            )
        ]

    def push_right(block):
        operand, which = [entry[1:] for entry in right_blocks(0) if entry[0] == block][0]
        half = rights[operand].shape[1] // 2
        begin = pl.multiple_of((1 - core) * half + which * UNIT[1], 128)
        return pltpu.make_async_remote_copy(
            rights[operand].at[:, pl.ds(begin, UNIT[1])],
            right_buf[phases[0]["kind"]].at[block, pl.ds(tokens, tokens), :],
            push_send.at[block],
            push_recv.at[block],
            partner,
            MESH,
        )

    def out_copies(at, unit):
        phase = phases[at]
        if phase["kind"] == 0 and unit < 4:
            half = UNIT[1]
            rows = deep_out.shape[0] // 4
            there = deep_out.at[
                pl.ds(unit * rows, rows),
                pl.ds(pl.multiple_of(phase["cols"][0] + core * half, 128), half),
            ]
        else:
            which, col = (1, unit - 4) if phase["kind"] == 0 else (unit - phase["first"], 0)
            if phase["kind"] and unit >= 3:
                which, col = len(phase["lefts"]) - 1, unit - 3
            half = rights[phase["lefts"][which]].shape[1] // 2
            start = phase["cols"][which] + core * half + col * UNIT[1]
            there = wide_out.at[:, pl.ds(pl.multiple_of(start, 128), UNIT[1])]
        here = plane_got[at].at[unit]
        return (
            pltpu.make_async_copy(here, there, out_sem.at[at, unit]),
            pltpu.make_async_remote_copy(
                here, there, out_send.at[at, unit], out_recv.at[at, unit], partner, MESH
            ),
        )

    def product(kind, slot, left, right):
        return lax.dot_general(
            left_buf[kind][slot, left],
            right_buf[kind][right],
            (((0,), (0,)), ((), ())),
            preferred_element_type=jnp.float32,
        )

    def start(copies):
        for copy in copies:
            copy.start()

    def finish(copies):
        for copy in copies:
            copy.wait()

    def encode(term):
        largest = jnp.maximum(jnp.max(jnp.abs(term), axis=0, keepdims=True), WIRE_LEAST)
        low = jnp.round(term * (WIRE_MAX / largest)).astype(jnp.int16)
        return low, largest * (1.0 / WIRE_MAX)

    def take_step(at, step, first, last):
        phase = phases[at]
        kind = phase["kind"]
        slot = step % 2
        before = (step + 1) % 2
        for far in range(2):
            finish(load_left(at, step, slot, far))

        def load_next():
            for copy in pair_left(at, step + 1):
                copy.wait_recv()
            for far in range(2):
                start(load_left(at, step + 1, before, far))

        opening = first and at == 0
        if not (last or opening):
            load_next()
        parts = unit_parts(at, kind, phase["first"])

        def send_theirs():
            def spend():
                for copy in cross_copies(slot):
                    copy.wait_send()
                pl.semaphore_wait(cross_credit, 1)

            if last:
                spend()
            elif not first:
                pl.when(step >= 2)(spend)
            for pair in range(SPLIT):
                unit = split_unit(pair, 1 - plane)
                term = product(kind, slot, parts[1][2](unit), parts[1][3](unit))
                cross_put[slot, pair], cross_put_scale[slot, pair] = encode(term)
            start(cross_copies(slot))

        if at == 0 and not opening:
            send_theirs()
        for part, (low, many, left_of, right_of) in enumerate(parts):
            if opening:
                blocks = range(1) if part == 0 else range(1, 5)
                finish(load_right(0, 0)[blocks.start : blocks.stop])
                for block in blocks:
                    push_right(block).wait_recv()
                if part:
                    send_theirs()
            if not first:
                for copy in ring_copies(at, part, before):
                    copy.wait_recv()
            if not (first or last):

                @pl.when(step >= 2)
                def _(part=part):
                    for copy in ring_copies(at, part, slot):
                        copy.wait_send()
                    pl.semaphore_wait(credit.at[kind, part], 1)

            def settle(position, unit, term):
                if not first:
                    came = got_low[kind][before, position].astype(jnp.float32)
                    term = term + came * got_scale[kind][before, position]
                if last and at in coded:
                    coded[at][0][unit], coded[at][1][unit] = encode(term)
                elif last:
                    plane_put[kind][unit] = term
                else:
                    low_part, scale_part = encode(term)
                    put_low[kind][slot, position] = low_part
                    put_scale[kind][slot, position] = scale_part

            split = at == 0 and part == 1
            if split:
                for copy in cross_copies(slot):
                    copy.wait_recv()

            @pl.loop(low, low + many)
            def _(position, left_of=left_of, right_of=right_of):
                unit = split_unit(position - 4, plane) if split else position
                term = product(kind, slot, left_of(unit), right_of(unit))
                if split:
                    came = cross_got[slot, position - 4].astype(jnp.float32)
                    term = term + came * cross_got_scale[slot, position - 4]
                settle(position, unit, term)

            if split and not last:

                def credit_cross():
                    pl.semaphore_signal(
                        cross_credit, inc=1, device_id=mirror, device_id_type=MESH
                    )

                if first:
                    credit_cross()
                else:
                    pl.when(step < count - 2)(credit_cross)

            if last and split:
                start([split_copy(pair, plane) for pair in range(SPLIT)])
            elif last:
                start(plane_copies(at, part))
            else:
                start(ring_copies(at, part, slot))
            if not (first or last):

                @pl.when(step < count - 2)
                def _(part=part):
                    pl.semaphore_signal(
                        credit.at[kind, part], inc=1, device_id=preceding, device_id_type=MESH
                    )

        if opening:
            load_next()

    def close(at):
        kind = phases[at]["kind"]

        def add_square(total):
            square_buf[...] += jnp.sum((total * total).reshape(UNIT[0] // 8, 8, UNIT[1]), axis=0)

        for part, (low, many, _, _) in enumerate(unit_parts(at, kind, phases[at]["first"])):
            if at == 0 and part == 1:
                for pair in range(SPLIT):
                    split_copy(pair, plane).wait_send()
                    split_copy(pair, 1 - plane).wait_recv()
                    ours = split_unit(pair, plane)
                    plane_got[0][ours] = plane_put[0][ours]
                for unit in range(4, 8):
                    add_square(plane_got[0][unit])
                    start(out_copies(0, unit))
                continue
            finish(plane_copies(at, part))

            @pl.loop(low, low + many)
            def _(unit):
                if at in coded:
                    here, here_scale, there, there_scale = coded[at]
                    total = here[unit].astype(jnp.float32) * here_scale[unit]
                    total += there[unit].astype(jnp.float32) * there_scale[unit]
                else:
                    total = plane_put[kind][unit] + plane_got[at][unit]
                plane_got[at][unit] = total
                add_square(total)

            for unit in range(low, low + many):
                start(out_copies(at, unit))

    half_rows = pl.ds(pl.multiple_of(core * (vec_sum.shape[0] // 2), 8), vec_sum.shape[0] // 2)
    side_local = [
        pltpu.make_async_copy(vec_ref, vec_got.at[band], side_own.at[0]),
        pltpu.make_async_copy(kv_ref.at[band], kv_got.at[band], side_own.at[1]),
        pltpu.make_async_copy(text_ref, text_buf, side_own.at[2]),
    ]
    side_remote = []
    for step, peer in enumerate(band_peers):
        side_remote += [
            pltpu.make_async_remote_copy(
                vec_ref, vec_got.at[band], side_send.at[0, step], side_recv.at[0, step], peer, MESH
            ),
            pltpu.make_async_remote_copy(
                kv_ref.at[peer[1]],
                kv_got.at[band],
                side_send.at[1, step],
                side_recv.at[1, step],
                peer,
                MESH,
            ),
        ]
    vec_own = pltpu.make_async_copy(vec_sum, all_vec.at[me], side_own.at[3])

    def kv_parts(owner):
        return [(ref.at[owner], ref.at[owner]) for ref in (all_kv, all_kv_scale)]

    def vec_copies(step):
        owner = ring_clip((place - onward * step + 2 * count) % count, count)
        vec = all_vec.at[owner, half_rows]
        return [
            pltpu.make_async_remote_copy(
                here, there, vec_send.at[step, i], vec_recv.at[step, i], following, MESH
            )
            for i, (here, there) in enumerate([(vec, vec)] + kv_parts(owner))
        ]

    def vec_first():
        vec = all_vec.at[me, half_rows]
        return [
            pltpu.make_async_remote_copy(
                here, there, vec_send.at[0, i], vec_recv.at[0, i], following, MESH
            )
            for i, (here, there) in enumerate([(vec_sum.at[half_rows], vec)] + kv_parts(me))
        ]

    def vec_pair(step):
        owner = ring_clip((place - onward * (step + 1) + 2 * count) % count, count)
        vec = all_vec.at[owner, half_rows]
        return pltpu.make_async_remote_copy(
            vec, vec, vec_pair_send.at[step], vec_pair_recv.at[step], partner, MESH
        )

    kv_width = kv_grad.shape[1]

    def kv_place(owner):
        return deep_out.at[:, pl.ds(pl.multiple_of(D + owner * kv_width, 128), kv_width)]

    def kv_copy(i):
        if i == 2:
            return pltpu.make_async_copy(kv_grad, kv_place(band), kv_own)
        peer = (partner, mirror)[i]
        return pltpu.make_async_remote_copy(
            kv_grad, kv_place(band), kv_send.at[i], kv_recv.at[i], peer, MESH
        )

    def kv_passed():
        there = kv_place(mirror[1])
        return pltpu.make_async_remote_copy(
            there, there, kv_send.at[2], kv_recv.at[2], partner, MESH
        )

    def sum_bands():
        finish(side_local + side_remote)
        vec_sum[...] = jnp.sum(vec_got[...], 0)
        all_kv[me], all_kv_scale[me] = encode(jnp.sum(kv_got[...], 0))
        vec_own.start()
        start(vec_first())

    def pass_sums(step):
        for copy in vec_copies(step - 1):
            copy.wait_recv()
        start(vec_copies(step))
        vec_pair(step - 1).start()

    def multiply_text():
        for copy in vec_copies(count - 2):
            copy.wait_recv()
        vec_pair(count - 2).start()
        grads = all_kv[...].astype(jnp.float32) * all_kv_scale[...]
        grads = grads.reshape(text_buf.shape[0], -1)
        total = jnp.zeros_like(kv_grad)
        for _ in range(3):
            part = grads.astype(jnp.bfloat16)
            grads = grads - part.astype(jnp.float32)
            total = total + matmul_tn(text_buf[...], part)
        kv_grad[...] = total
        kv_square[...] = jnp.sum((total * total).reshape(-1, 8, total.shape[1]), axis=0)
        start([kv_copy(i) for i in range(3)])

    square_buf[...] = jnp.zeros_like(square_buf)
    start(side_local + side_remote)
    start(load_right(0, 0))
    start(load_left(0, 0, 0, 0))
    push_right(0).start()
    start(pair_left(0, 0))
    for block in range(1, 5):
        push_right(block).start()

    @pl.loop(1, count)
    def _(step):
        start(pair_left(0, step))

    for copy in pair_left(0, 0):
        copy.wait_recv()
    start(load_left(0, 0, 0, 1))
    take_step(0, 0, True, False)
    for at in range(len(phases)):
        more = at + 1 < len(phases)
        if more:
            start(pair_right(at + 1))
            start(load_right(at + 1, 0))
            start(pair_left(at + 1, 0))
        if at == 1:
            sum_bands()

        @pl.loop(1, count - 1)
        def _(step, at=at, more=more):
            take_step(at, step, False, False)
            if at == 1:
                pass_sums(step)
            if more:
                start(pair_left(at + 1, step))

                @pl.when(step == count // 2)
                def _():
                    for copy in pair_right(at + 1):
                        copy.wait_recv()
                    start(load_right(at + 1, 1))
                    for copy in pair_left(at + 1, 0):
                        copy.wait_recv()
                    for far in range(2):
                        start(load_left(at + 1, 0, 0, far))

        if more:
            start(pair_left(at + 1, count - 1))
            for far in range(2):
                finish(load_right(at + 1, far))
            take_step(at + 1, 0, True, False)
        take_step(at, count - 1, False, True)
        if at == 1:
            multiply_text()
        for slot in range(2):
            for part in range(2):
                for copy in ring_copies(at, part, slot):
                    copy.wait_send()
            if at == 0:
                for copy in cross_copies(slot):
                    copy.wait_send()
        if at == 2:
            kv_copy(1).wait_recv()
            kv_passed().start()
        if at:
            close(at - 1)
    close(len(phases) - 1)
    vec_own.wait()
    kv_passed().wait()
    kv_copy(0).wait()
    kv_copy(1).wait_send()
    kv_copy(2).wait()

    @pl.loop(0, count - 1)
    def _(step):
        for copy in vec_copies(step):
            copy.wait_send()
        vec_pair(step).wait()

    square_out[...] = square_buf[...]
    for at, phase in enumerate(phases):
        for copy in pair_right(at) if at else [push_right(block) for block in range(5)]:
            copy.wait_send()

        @pl.loop(0, count)
        def _(step, at=at):
            for copy in pair_left(at, step):
                copy.wait_send()

        for unit in range(phase["first"], 8 if phase["kind"] == 0 else 6):
            finish(out_copies(at, unit))


def reduce_gradients(phases, lefts, rights, vectors, keyvals, text, wide_cols, deep_cols):
    count = lax.axis_size("clip")
    tokens = lefts[0].shape[0]
    wide_rows = lefts[1].shape[1] // count
    deep_rows = lefts[0].shape[1] // count
    band_count, _, kv_cols = keyvals.shape
    num = len(lefts)
    dma = pltpu.SemaphoreType.DMA
    units, lefts_of, rights_of = (8, 6), (5, 4), (5, 6)
    scratch = [pltpu.VMEM((2, lefts_of[k], 2 * tokens, 128), jnp.bfloat16) for k in range(2)]
    scratch += [pltpu.VMEM((rights_of[k], 2 * tokens, UNIT[1]), jnp.bfloat16) for k in range(2)]
    for _ in range(2):
        scratch += [pltpu.VMEM((2, units[k]) + UNIT, jnp.int16) for k in range(2)]
        scratch += [pltpu.VMEM((2, units[k], 1, UNIT[1]), jnp.float32) for k in range(2)]
    scratch += [pltpu.VMEM((units[k],) + UNIT, jnp.float32) for k in range(2)]
    scratch += [pltpu.VMEM((units[p["kind"]],) + UNIT, jnp.float32) for p in phases]
    scratch += [
        pltpu.VMEM((8, UNIT[1]), jnp.float32),
        dma((2, 2, 5, 2)),
        dma((2, 6, 2)),
        dma((len(phases), 5, count)),
        dma((len(phases), 5, count)),
        dma((num,)),
        dma((num,)),
        dma((2, 2, 2, 2)),
        dma((2, 2, 2, 2)),
        pltpu.SemaphoreType.REGULAR((2, 2)),
        dma((len(phases), 2, 2)),
        dma((len(phases), 2, 2)),
        dma((len(phases), 8)),
        dma((len(phases), 8)),
        dma((len(phases), 8)),
    ]
    for many in (6, 6, 8, 8):
        scratch += [pltpu.VMEM((many,) + UNIT, jnp.int16)]
        scratch += [pltpu.VMEM((many, 1, UNIT[1]), jnp.float32)]
    scratch += [
        dma((5,)),
        dma((5,)),
        *[
            pltpu.VMEM((2, SPLIT) + tile, kind)
            for _ in range(2)
            for tile, kind in ((UNIT, jnp.int16), ((1, UNIT[1]), jnp.float32))
        ],
        dma((2, 2)),
        dma((2, 2)),
        pltpu.SemaphoreType.REGULAR,
        pltpu.VMEM((band_count,) + vectors.shape, jnp.float32),
        pltpu.VMEM(keyvals.shape, jnp.float32),
        pltpu.VMEM(vectors.shape, jnp.float32),
        pltpu.VMEM((count,) + keyvals.shape[1:], jnp.int16),
        pltpu.VMEM((count, 1, kv_cols), jnp.float32),
        pltpu.VMEM(text.shape, jnp.bfloat16),
        pltpu.VMEM((text.shape[1], kv_cols), jnp.float32),
        dma((4,)),
        dma((2, band_count - 1)),
        dma((2, band_count - 1)),
        dma((count - 1, 3)),
        dma((count - 1, 3)),
        dma((count - 1,)),
        dma((count - 1,)),
        dma,
        dma((3,)),
        dma((3,)),
    ]
    out = pl.pallas_call(
        partial(reduce_kernel, count, tokens, phases),
        out_shape=(
            jax.ShapeDtypeStruct((wide_rows, wide_cols), jnp.float32),
            jax.ShapeDtypeStruct((deep_rows, deep_cols), jnp.float32),
            jax.ShapeDtypeStruct((8, UNIT[1]), jnp.float32),
            jax.ShapeDtypeStruct((count,) + vectors.shape, jnp.float32),
            jax.ShapeDtypeStruct((8, kv_cols), jnp.float32),
        )
        + tuple(jax.ShapeDtypeStruct(x.shape, x.dtype) for x in lefts)
        + tuple(jax.ShapeDtypeStruct((tokens, x.shape[1] // 2), x.dtype) for x in rights),
        in_specs=[ANY] * (2 * num + 3),
        out_specs=(ANY, ANY, IN_VMEM, ANY, IN_VMEM) + (ANY,) * (2 * num),
        scratch_shapes=scratch,
        compiler_params=pltpu.CompilerParams(
            collective_id=2, has_side_effects=True, vmem_limit_bytes=58 << 20
        ),
        cost_estimate=pl.CostEstimate(flops=3 * 10**11, bytes_accessed=8 * 10**8, transcendentals=0),
    )(*lefts, *rights, vectors, keyvals, text)
    return out[:5]


def total_kernel(count, part_ref, out_ref, mid, band_got, clip_got, *sems):
    me = lax.axis_index("clip")
    band = lax.axis_index("band")
    band_count = band_got.shape[0]
    band_peers = [(me, (band + step) % band_count) for step in range(1, band_count)]
    clip_peers = [((me + step) % count, band) for step in range(1, count)]
    greet(band_peers + clip_peers)
    stages = (
        (part_ref, band_got, band, band_peers, mid, sems[:2]),
        (mid, clip_got, me, clip_peers, out_ref, sems[2:]),
    )
    for value, got, index, peers, result, (send, recv) in stages:
        copies = [
            pltpu.make_async_remote_copy(
                value, got.at[index], send.at[step], recv.at[step], peer, MESH
            )
            for step, peer in enumerate(peers)
        ]
        for copy in copies:
            copy.start()
        got[index] = value[...]
        for copy in copies:
            copy.wait()
        result[...] = jnp.sum(got[...], 0)


def total_over_devices(value):
    count, band_count = lax.axis_size("clip"), lax.axis_size("band")
    dma = pltpu.SemaphoreType.DMA
    tile = (8, 128)
    return pl.pallas_call(
        partial(total_kernel, count),
        out_shape=jax.ShapeDtypeStruct(tile, jnp.float32),
        in_specs=[IN_VMEM],
        out_specs=IN_VMEM,
        scratch_shapes=[
            pltpu.VMEM(tile, jnp.float32),
            pltpu.VMEM((band_count,) + tile, jnp.float32),
            pltpu.VMEM((count,) + tile, jnp.float32),
            dma((band_count - 1,)),
            dma((band_count - 1,)),
            dma((count - 1,)),
            dma((count - 1,)),
        ],
        compiler_params=pltpu.CompilerParams(collective_id=3, has_side_effects=True),
    )(jnp.broadcast_to(value, tile))[0, 0]


def per_device(
    latents,
    noise_field,
    timesteps,
    null_flags,
    frame_mask,
    context,
    w_wide,
    m_wide,
    v_wide,
    w_deep,
    m_deep,
    v_deep,
    w_small,
    m_small,
    v_small,
):
    clip_count = lax.axis_size("clip")
    band_count = lax.axis_size("band")
    clip_at = lax.axis_index("clip")
    band_at = lax.axis_index("band")
    wide_rows = w_wide.shape[0]
    deep_rows = w_deep.shape[0]
    text_len, text_dim = context.shape[1:]
    facts = jnp.pad(
        jnp.concatenate([timesteps, frame_mask[0]])[None],
        ((0, 7), (0, 127 - frame_mask.shape[1])),
    )
    kept_text = context[0] * (1 - null_flags[0]).astype(jnp.bfloat16)
    text_cols = jnp.pad(
        kept_text.reshape(text_len, clip_count, band_count, -1).transpose(1, 2, 0, 3),
        ((0, 0), (0, 0), (0, TEXT_PAD - text_len), (0, 0)),
    )
    all_facts = exchange_facts(facts)
    all_times = all_facts[:, 0, 0].astype(jnp.float32)
    all_time_low = jax.nn.silu(time_features(all_times)).astype(jnp.bfloat16)
    time_rows = lax.dynamic_slice(
        all_time_low, (0, clip_at * wide_rows), (clip_count, wide_rows)
    )
    part_modul = matmul(time_rows, w_wide[:, : 12 * D].astype(jnp.bfloat16))
    kv_cols = 2 * D // band_count
    gathered, all_modul, all_text, keyval = gather_weights(
        (w_wide, w_deep),
        (
            (0, 22 * D, FF),
            (1, 0, D),
            (0, 20 * D, D),
            (0, 21 * D, D),
            (0, 18 * D, D),
            (0, 19 * D, D),
            (0, 12 * D, 3 * D),
            (0, 15 * D, 3 * D),
        ),
        (1, 2, 1, 2, 1, 2, 0, 0),
        part_modul.reshape(clip_count, band_count, -1, 128),
        text_cols,
    )
    up_a_w, down_a_w, query_w, cross_out_w, out_a_w, out_b_w, qkv_a_w, qkv_b_w = gathered
    all_text = all_text.transpose(0, 2, 1, 3)
    keyval = keyval.transpose(1, 0, 2).reshape(TEXT_PAD, 2 * D)
    late_up_b, late_down_b, all_modul = lax.optimization_barrier(
        (own_quarter(w_wide[:, 22 * D + FF :]), own_quarter(w_deep[:, 3 * D :]), all_modul)
    )
    up_b_w = lax.all_gather(late_up_b, ("clip", "band"), axis=0, tiled=True)
    down_b_w = lax.all_gather(late_down_b, ("clip", "band"), axis=0, tiled=True)
    small_low = w_small.astype(jnp.bfloat16)
    small_val = small_low.astype(jnp.float32)
    num_frames, num_rows, num_cols = (latents.shape[1], latents.shape[2], latents.shape[3])
    tok_count = num_frames * num_rows * num_cols
    all_mask = all_facts[:, 0, 1 : 1 + num_frames]
    global_count = jnp.sum(all_mask).astype(jnp.float32) * (num_rows * num_cols * CH * band_count)
    time_value = timesteps[0].astype(jnp.float32)
    noise_angle = 0.5 * math.pi * time_value / TMAX
    signal, spread = (jnp.cos(noise_angle), jnp.sin(noise_angle))
    clean_tok = token_order(latents[0])
    noise_tok = token_order(noise_field[0])
    run = num_rows * WIN
    part = SHIFT * WIN
    frame_windows = attend_pieces(tok_count, num_frames, "frame")
    text_windows = attend_pieces(tok_count, num_frames, "text")
    noisy_low = (signal * clean_tok + spread * noise_tok).astype(jnp.bfloat16)
    target = signal * noise_tok - spread * clean_tok
    modulation = jnp.sum(all_modul, 0).reshape(12, D)
    mod_a, mod_b = (modulation[:6], modulation[6:])
    stream_zero = matmul(noisy_low, small_low[:CH]) + small_val[2 * CH]
    normed_a, back_a = jax.vjp(norm_modulated, stream_zero, mod_a[0], mod_a[1])
    in_a = normed_a.astype(jnp.bfloat16)
    qkv_a = matmul(in_a, qkv_a_w).astype(jnp.bfloat16)
    att_a, far_kv = attend_frames(qkv_a, frame_windows)
    proj_a = matmul(att_a, out_a_w)
    stream_one = stream_zero + mod_a[2] * proj_a
    stream_two, saved_a = mlp_forward(stream_one, mod_a, up_a_w, down_a_w)
    normed_b, back_b = jax.vjp(norm_modulated, stream_two, mod_b[0], mod_b[1])
    low_b = normed_b.astype(jnp.bfloat16)
    rolled = with_rows(low_b, shifted(first_rows(low_b, run, part), "band", -1), run)
    qkv_b = matmul(rolled, qkv_b_w).astype(jnp.bfloat16)
    att_b = attend_halves(qkv_b, run, part)
    proj_b = matmul(att_b, out_b_w)
    stream_three = stream_two + mod_b[2] * proj_b
    cross_val, cross_back = jax.vjp(norm_gained, stream_three, small_val[2 * CH + 1])
    cross_in = cross_val.astype(jnp.bfloat16)
    query_proj = matmul(cross_in, query_w).astype(jnp.bfloat16)
    text_kv = [(keyval, 0, HEADS // 2)]
    crossed = attend(query_proj, text_kv, text_windows, text_len)
    stream_four = stream_three + matmul(crossed, cross_out_w)
    stream_five, saved_b = mlp_forward(stream_four, mod_b, up_b_w, down_b_w)
    final_val, final_back = jax.vjp(norm_gained, stream_five, small_val[2 * CH + 2])
    final_low = final_val.astype(jnp.bfloat16)
    head_low = small_low[CH : 2 * CH]
    predicted = matmul_nt(final_low, head_low)
    weight_row = jnp.repeat(frame_mask[0].astype(jnp.float32), run)
    weight_row = jnp.tile(weight_row, num_cols // WIN)[:, None]
    pred_error = predicted - target
    loss_part = jnp.sum(weight_row * pred_error * pred_error)
    grad_pred = (weight_row * pred_error * (2.0 / global_count)).astype(jnp.bfloat16)
    grad_head = matmul_tn(grad_pred, final_low)
    grad_stream, grad_gain_f = final_back(matmul(grad_pred, head_low))
    grad_stream, mlp_factors_b, extra_b = mlp_backward(
        grad_stream, mod_b, up_b_w, down_b_w, saved_b
    )
    grad_cross = grad_stream.astype(jnp.bfloat16)
    grad_crossed = matmul_nt(grad_cross, cross_out_w).astype(jnp.bfloat16)
    grad_query, grad_keyval = attend_back(
        query_proj, text_kv, grad_crossed, text_windows, text_len
    )
    grad_part, grad_gain_c = cross_back(matmul_nt(grad_query, query_w))
    grad_stream = grad_stream + grad_part
    grad_proj = (mod_b[2] * grad_stream).astype(jnp.bfloat16)
    grad_gate_b = jnp.sum(grad_stream * proj_b, 0)
    factors_ob = (att_b, grad_proj)
    grad_att = matmul_nt(grad_proj, out_b_w).astype(jnp.bfloat16)
    grad_qkv = attend_halves_back(qkv_b, grad_att, run, part)
    factors_qkvb = (rolled, grad_qkv)
    grad_in_roll = matmul_nt(grad_qkv, qkv_b_w)
    sent_back = shifted(first_rows(grad_in_roll, run, part), "band", 1)
    grad_normed = with_rows(grad_in_roll, sent_back, run)
    grad_part, grad_shift_b, grad_scale_b = back_b(grad_normed)
    grad_stream = grad_stream + grad_part
    grad_stream, mlp_factors_a, extra_a = mlp_backward(
        grad_stream, mod_a, up_a_w, down_a_w, saved_a
    )
    grad_proj = (mod_a[2] * grad_stream).astype(jnp.bfloat16)
    grad_gate_a = jnp.sum(grad_stream * proj_a, 0)
    factors_oa = (att_a, grad_proj)
    grad_att = matmul_nt(grad_proj, out_a_w).astype(jnp.bfloat16)
    grad_qkv = attend_frames_back(qkv_a, far_kv, grad_att, frame_windows)
    factors_qkva = (in_a, grad_qkv)
    grad_part, grad_shift_a, grad_scale_a = back_a(matmul_nt(grad_qkv, qkv_a_w))
    grad_stream = grad_stream + grad_part
    grad_patch = matmul_tn(noisy_low.astype(jnp.float32), grad_stream, lax.Precision.HIGHEST)
    grad_bias = jnp.sum(grad_stream, 0)
    grad_modul = jnp.stack(
        [
            grad_shift_a,
            grad_scale_a,
            grad_gate_a,
            extra_a[0],
            extra_a[1],
            extra_a[2],
            grad_shift_b,
            grad_scale_b,
            grad_gate_b,
            extra_b[0],
            extra_b[1],
            extra_b[2],
        ]
    ).reshape(1, 12 * D)
    grad_small = jnp.concatenate(
        [grad_patch, grad_head, grad_bias[None], grad_gain_c[None], grad_gain_f[None]], 0
    )
    factors = mlp_factors_b + (
        (crossed, grad_cross),
        (cross_in, grad_query),
        factors_ob,
        factors_qkvb,
    )
    factors += mlp_factors_a + (factors_oa, factors_qkva)
    if wide_rows == 128 and deep_rows == 512:
        phases = (
            {"kind": 0, "first": 0, "lefts": (0, 1), "cols": (3 * D, 10 * D + FF)},
            {"kind": 1, "first": 0, "lefts": (2, 3, 4, 5), "cols": (9 * D, 8 * D, 7 * D, 3 * D)},
            {"kind": 0, "first": 0, "lefts": (6, 7), "cols": (0, 10 * D)},
            {"kind": 1, "first": 2, "lefts": (8, 9), "cols": (6 * D, 0)},
        )
        used = 12 * D + grad_small.size
        vectors = jnp.concatenate(
            [grad_modul.reshape(-1), grad_small.reshape(-1), loss_part[None]]
        )
        vectors = jnp.pad(vectors, (0, 256 * 128 - vectors.shape[0])).reshape(256, 128)
        keyvals = grad_keyval.reshape(TEXT_PAD, band_count, kv_cols).transpose(1, 0, 2)
        wide_rest, deep_sum, squares, all_vectors, kv_squares = reduce_gradients(
            phases,
            [f[0] for f in factors],
            [f[1] for f in factors],
            vectors,
            keyvals,
            all_text.reshape(clip_count * TEXT_PAD, deep_rows),
            10 * D + 2 * FF,
            4 * D,
        )
        all_vectors = all_vectors.reshape(clip_count, -1)
        all_grad_modul = all_vectors[:, : 12 * D]
        small_sum = jnp.sum(all_vectors[:, 12 * D : used], 0).reshape(grad_small.shape)
        loss_sum = jnp.sum(all_vectors[:, used])
        square_part = jnp.sum(squares) / (band_count // 2) + jnp.sum(kv_squares)
    else:
        summed = [sum_rows(*pair) for pair in factors]
        wide_rest = jnp.concatenate([summed[i] for i in (9, 5, 8, 4, 3, 2, 7, 1)], 1)
        grad_keyval = lax.psum_scatter(grad_keyval, "band", scatter_dimension=1, tiled=True)
        grad_keyval = lax.all_gather(grad_keyval, "clip", axis=0, tiled=True)
        grad_w_ckv = matmul_tn(
            all_text.reshape(clip_count * TEXT_PAD, deep_rows).astype(jnp.float32),
            grad_keyval,
            lax.Precision.HIGHEST,
        )
        grad_w_ckv = lax.all_gather(grad_w_ckv, "band", axis=1, tiled=True)
        all_grad_modul = lax.all_gather(lax.psum(grad_modul, "band"), "clip", axis=0, tiled=True)
        loss_sum, small_sum = lax.psum((loss_part, grad_small), ("clip", "band"))
        deep_sum = jnp.concatenate([summed[6], grad_w_ckv, summed[0]], 1)
        square_part = sum(jnp.sum(x * x) for x in (wide_rest, deep_sum)) / band_count
    grad_w_ada = matmul_tn(time_rows.astype(jnp.float32), all_grad_modul, lax.Precision.HIGHEST)
    wide_sum = jnp.concatenate([grad_w_ada, wide_rest], 1)
    square_part += jnp.sum(grad_w_ada * grad_w_ada) / band_count
    square_sum = total_over_devices(square_part)
    grad_norm = jnp.sqrt(square_sum + jnp.sum(small_sum * small_sum))
    factor = CLIP_MAX / jnp.maximum(grad_norm, CLIP_MAX)
    new_wide = adam_update(w_wide, m_wide, v_wide, wide_sum * factor, 0.15)
    new_deep = adam_update(w_deep, m_deep, v_deep, deep_sum * factor, 0.05)
    new_small = adam_update(w_small, m_small, v_small, small_sum * factor, 0.5)
    loss = loss_sum / global_count
    return (
        loss,
        grad_norm,
        new_wide[0],
        new_wide[1],
        new_wide[2],
        new_deep[0],
        new_deep[1],
        new_deep[2],
        new_small[0],
        new_small[1],
        new_small[2],
    )


def solution(mesh):
    in_specs = (
        P("clip", None, "band", None, None),
        P("clip", None, "band", None, None),
        P("clip"),
        P("clip"),
        P("clip", None),
        P("clip", None, None),
        P("clip", None),
        P("clip", None),
        P("clip", None),
        P("clip", None),
        P("clip", None),
        P("clip", None),
        P(),
        P(),
        P(),
    )
    out_specs = (
        P(),
        P(),
        P("clip", None),
        P("clip", None),
        P("clip", None),
        P("clip", None),
        P("clip", None),
        P("clip", None),
        P(),
        P(),
        P(),
    )
    return jax.shard_map(
        per_device, mesh=mesh, in_specs=in_specs, out_specs=out_specs, check_vma=False
    )
```

```python
from functools import partial
import math

import jax
import jax.numpy as jnp
from jax import lax
from jax.experimental import pallas as pl
from jax.experimental.pallas import tpu as pltpu
from jax.sharding import PartitionSpec as P

D = 1024
HEADS = 16
HEAD_DIM = 64
FF = 4096
CH = 8
SPACE = 16
WIN = 8
SHIFT = 4
TMAX = 1000
STEP = 10


EPS_NORM = 1e-06
CLIP_MAX = 0.001
BETA_ONE = 0.9
BETA_TWO = 0.95
ADAM_EPS = 1e-08
DECAY = 0.1


def shifted(value, axis, by):
    length = lax.axis_size(axis)
    return lax.ppermute(value, axis, [(i, (i + by) % length) for i in range(length)])


def matmul(left_op, right_op):
    return jnp.dot(left_op, right_op, preferred_element_type=jnp.float32)


def matmul_tn(left_op, right_op, precision=None):
    return lax.dot_general(
        left_op,
        right_op,
        (((0,), (0,)), ((), ())),
        precision=precision,
        preferred_element_type=jnp.float32,
    )


def matmul_nt(left_op, right_op):
    return lax.dot_general(
        left_op, right_op, (((1,), (1,)), ((), ())), preferred_element_type=jnp.float32
    )


def layer_norm(field_in):
    average = jnp.mean(field_in, -1, keepdims=True)
    centred = field_in - average
    return centred * lax.rsqrt(jnp.mean(centred * centred, -1, keepdims=True) + EPS_NORM)


def norm_modulated(field_in, shift_vec, scale_vec):
    return layer_norm(field_in) * (1.0 + scale_vec) + shift_vec


def norm_gained(field_in, gain_vec):
    return layer_norm(field_in) * gain_vec


def time_features(time_value):
    half_width = D // 2
    frequency = jnp.exp(-math.log(10000.0) * jnp.arange(half_width, dtype=jnp.float32) / half_width)
    angles = time_value[..., None] * frequency
    return jnp.concatenate([jnp.cos(angles), jnp.sin(angles)], -1)


def token_order(grid):
    frames, rows, cols, width = grid.shape
    halves = grid.reshape(frames, rows, cols // WIN, WIN, width).transpose(2, 0, 1, 3, 4)
    return halves.reshape(frames * rows * cols, width)


def with_rows(tokens, first_rows, run):
    width = tokens.shape[1]
    runs = tokens.reshape(-1, run, width)
    return jnp.concatenate([first_rows, runs[:, first_rows.shape[1] :]], 1).reshape(-1, width)


def first_rows(tokens, run, part):
    return tokens.reshape(-1, run, tokens.shape[1])[:, :part]


def attend_pieces(tokens, frames, keys):
    if keys == "frame":
        run = tokens // (2 * frames)
        return [((f * run, run), (tokens // 2 + f * run, run)) for f in range(frames)]
    if keys == "half":
        return [((half * (tokens // 2), tokens // 2),) for half in range(2)]
    return [((0, tokens),)]


def take(ref, runs):
    pieces = [ref[low : low + many, :] for low, many in runs]
    return pieces[0] if len(pieces) == 1 else jnp.concatenate(pieces, 0)


def put(ref, cols, runs, value):
    done = 0
    for low, many in runs:
        ref[low : low + many, cols] = value[done : done + many].astype(ref.dtype)
        done += many


def softmax_of(scores, axis, text_len):
    if text_len:
        place = lax.broadcasted_iota(jnp.int32, scores.shape, axis)
        scores = jnp.where(place < text_len, scores, -1e30)
    weight = jnp.exp(scores - jnp.max(scores, axis, keepdims=True))
    return weight * (1.0 / jnp.sum(weight, axis, keepdims=True))


def lanes_of(head, shape):
    lane = lax.broadcasted_iota(jnp.int32, shape, 1)
    return lane < HEAD_DIM if head == 0 else lane >= HEAD_DIM


def only(head, value):
    return jnp.where(lanes_of(head, value.shape), value, jnp.zeros_like(value))


def attention_gradients(queries, keys, values, grad_out, text_len):
    queries, grad_out = stacked(queries), stacked(grad_out)
    probs = softmax_of(matmul_nt(keys, queries), 0, text_len)
    dprobs = matmul_nt(values, grad_out)
    dv = matmul(probs.astype(jnp.bfloat16), grad_out)
    inner = jnp.sum(probs * dprobs, 0, keepdims=True)
    dscores = (probs * (dprobs - inner)).astype(jnp.bfloat16)
    dk = matmul(dscores, queries)
    return unstacked(matmul_tn(dscores, keys)) * HEAD_DIM ** (-0.5), dk, dv


def attention_values(queries, keys, values, text_len):
    probs = softmax_of(matmul_nt(stacked(queries), keys), 1, text_len)
    return unstacked(matmul(probs.astype(jnp.bfloat16), values))


def stacked(rows):
    return jnp.concatenate([only(head, rows) for head in range(2)], 0)


def unstacked(rows):
    half = rows.shape[0] // 2
    return jnp.where(lanes_of(0, (half, rows.shape[1])), rows[:half], rows[half:])


def key_sets(key_refs, runs, text_len):
    if text_len:
        return key_refs[0][...]
    pieces = [take(ref, runs) for ref in key_refs]
    return pieces[0] if len(pieces) == 1 else jnp.concatenate(pieces, 0)


def attend_kernel(windows, text_len, sets, *refs):
    q_ref, k_refs, v_refs, out_ref = refs[0], refs[1 : 1 + sets], refs[1 + sets : 1 + 2 * sets], refs[-1]
    for runs in windows:
        queries = take(q_ref, runs) * HEAD_DIM ** (-0.5)
        keys, values = key_sets(k_refs, runs, text_len), key_sets(v_refs, runs, text_len)
        put(out_ref, slice(None), runs, attention_values(queries, keys, values, text_len))


def attend_back_kernel(windows, text_len, sets, *refs):
    q_ref, k_refs, v_refs = refs[0], refs[1 : 1 + sets], refs[1 + sets : 1 + 2 * sets]
    grad_ref = refs[1 + 2 * sets]
    dq_ref = refs[2 + 2 * sets]
    own_ref = refs[3 + 2 * sets] if text_len else None
    pair = pl.program_id(0)
    cols = [pl.ds(pl.multiple_of(i * D + pair * 2 * HEAD_DIM, 128), 2 * HEAD_DIM) for i in range(3)]
    merged = dq_ref.shape[1] == 3 * D
    for runs in windows:
        queries = take(q_ref, runs) * HEAD_DIM ** (-0.5)
        keys, values = key_sets(k_refs, runs, text_len), key_sets(v_refs, runs, text_len)
        grad_out = take(grad_ref, runs)
        dq, dk, dv = attention_gradients(queries, keys, values, grad_out, text_len)
        put(dq_ref, cols[0], runs, dq)
        if merged:
            put(dq_ref, cols[1], runs, dk)
            put(dq_ref, cols[2], runs, dv)
        else:
            own_ref[:, cols[0]] = dk
            own_ref[:, cols[1]] = dv


def pair_cols(which, pair):
    return pl.ds(pl.multiple_of(which * D + pair * 2 * HEAD_DIM, 128), 2 * HEAD_DIM)


def take_cols(ref, cols, runs):
    return jnp.concatenate([ref[low : low + many, cols] for low, many in runs], 0)


def attend_frames_kernel(windows, qkv_ref, out_ref, far_ref, send, recv):
    band = lax.axis_index("band")
    partner = (lax.axis_index("clip"), band + 1 - 2 * (band % 2))
    greet([partner])

    def copies(pair):
        return [
            pltpu.make_async_remote_copy(
                qkv_ref.at[:, pair_cols(1 + i, pair)],
                far_ref.at[:, pair_cols(i, pair)],
                send.at[pair, i],
                recv.at[pair, i],
                partner,
                MESH,
            )
            for i in range(2)
        ]

    @pl.loop(0, HEADS // 2)
    def _(pair):
        for copy in copies(pair):
            copy.start()

    @pl.loop(0, HEADS // 2)
    def _(pair):
        for copy in copies(pair):
            copy.wait_recv()
        for runs in windows:
            queries = take_cols(qkv_ref, pair_cols(0, pair), runs) * HEAD_DIM ** (-0.5)
            keys, values = (
                jnp.concatenate(
                    [
                        take_cols(qkv_ref, pair_cols(1 + i, pair), runs),
                        take_cols(far_ref, pair_cols(i, pair), runs),
                    ],
                    0,
                )
                for i in range(2)
            )
            put(
                out_ref, pair_cols(0, pair), runs, attention_values(queries, keys, values, 0)
            )

    @pl.loop(0, HEADS // 2)
    def _(pair):
        for copy in copies(pair):
            copy.wait_send()


def attend_frames_back_kernel(
    windows, qkv_ref, far_ref, grad_ref, out_ref, own_buf, far_put, far_got, send, recv
):
    band = lax.axis_index("band")
    partner = (lax.axis_index("clip"), band + 1 - 2 * (band % 2))
    greet([partner])

    def copies(pair):
        return [
            pltpu.make_async_remote_copy(
                far_put.at[:, pair_cols(i, pair)],
                far_got.at[:, pair_cols(i, pair)],
                send.at[pair, i],
                recv.at[pair, i],
                partner,
                MESH,
            )
            for i in range(2)
        ]

    def merge(pair):
        for i, copy in enumerate(copies(pair)):
            copy.wait_recv()
            cols = pair_cols(i, pair)
            total = own_buf[:, cols] + far_got[:, cols]
            out_ref[:, pair_cols(1 + i, pair)] = total.astype(jnp.bfloat16)

    @pl.loop(0, HEADS // 2)
    def _(pair):
        for runs in windows:
            queries = take_cols(qkv_ref, pair_cols(0, pair), runs) * HEAD_DIM ** (-0.5)
            keys, values = (
                jnp.concatenate(
                    [
                        take_cols(qkv_ref, pair_cols(1 + i, pair), runs),
                        take_cols(far_ref, pair_cols(i, pair), runs),
                    ],
                    0,
                )
                for i in range(2)
            )
            grad_out = take_cols(grad_ref, pair_cols(0, pair), runs)
            dq, *dkv = attention_gradients(queries, keys, values, grad_out, 0)
            put(out_ref, pair_cols(0, pair), runs, dq)
            half = keys.shape[0] // 2
            for i, value in enumerate(dkv):
                put(own_buf, pair_cols(i, pair), runs, value[:half])
                put(far_put, pair_cols(i, pair), runs, value[half:])
        for copy in copies(pair):
            copy.start()

        @pl.when(pair >= 1)
        def _():
            merge(pair - 1)

    merge(HEADS // 2 - 1)

    @pl.loop(0, HEADS // 2)
    def _(pair):
        for copy in copies(pair):
            copy.wait_send()


def next_bands():
    clip, band, count = lax.axis_index("clip"), lax.axis_index("band"), lax.axis_size("band")
    return (clip, (band + 1) % count), (clip, (band + count - 1) % count)


def half_window(qkv_ref, half, pair):
    tokens = qkv_ref.shape[0] // 2
    rows = pl.ds(half * tokens, tokens)
    queries, keys, values = (qkv_ref[rows, pair_cols(i, pair)] for i in range(3))
    return queries * HEAD_DIM ** (-0.5), keys, values


def attend_halves_kernel(part, qkv_ref, out_ref, put_buf, send, recv):
    following, preceding = next_bands()
    greet([following, preceding])
    runs, run = out_ref.shape[:2]

    def copy(pair):
        cols = pair_cols(0, pair)
        return pltpu.make_async_remote_copy(
            put_buf.at[:, :, cols],
            out_ref.at[:, pl.ds(0, part), cols],
            send.at[pair],
            recv.at[pair],
            following,
            MESH,
        )

    @pl.loop(0, HEADS // 2)
    def _(pair):
        for half in range(2):
            values = attention_values(*half_window(qkv_ref, half, pair), 0).astype(jnp.bfloat16)
            values = values.reshape(runs // 2, run, 2 * HEAD_DIM)
            low = half * (runs // 2)
            put_buf[low : low + runs // 2, :, pair_cols(0, pair)] = values[:, :part]
            out_ref[low : low + runs // 2, part:, pair_cols(0, pair)] = values[:, part:]
        copy(pair).start()

    @pl.loop(0, HEADS // 2)
    def _(pair):
        copy(pair).wait()


def attend_halves_back_kernel(part, qkv_ref, grad_ref, out_ref, got_buf, send, recv):
    following, preceding = next_bands()
    greet([following, preceding])
    runs, run = grad_ref.shape[:2]

    def copy(pair):
        cols = pair_cols(0, pair)
        return pltpu.make_async_remote_copy(
            grad_ref.at[:, pl.ds(0, part), cols],
            got_buf.at[:, :, cols],
            send.at[pair],
            recv.at[pair],
            preceding,
            MESH,
        )

    @pl.loop(0, HEADS // 2)
    def _(pair):
        copy(pair).start()

    @pl.loop(0, HEADS // 2)
    def _(pair):
        copy(pair).wait_recv()
        for half in range(2):
            low = half * (runs // 2)
            pieces = (
                got_buf[low : low + runs // 2, :, pair_cols(0, pair)],
                grad_ref[low : low + runs // 2, part:, pair_cols(0, pair)],
            )
            grad_out = jnp.concatenate(pieces, 1).reshape(-1, 2 * HEAD_DIM)
            parts = attention_gradients(*half_window(qkv_ref, half, pair), grad_out, 0)
            rows = pl.ds(low * run, grad_out.shape[0])
            for i, value in enumerate(parts):
                out_ref[rows, pair_cols(i, pair)] = value.astype(jnp.bfloat16)

    @pl.loop(0, HEADS // 2)
    def _(pair):
        copy(pair).wait_send()


def attend_halves(qkv, run, part):
    tokens = qkv.shape[0]
    dma = pltpu.SemaphoreType.DMA((HEADS // 2,))
    return pl.pallas_call(
        partial(attend_halves_kernel, part),
        out_shape=jax.ShapeDtypeStruct((tokens // run, run, D), jnp.bfloat16),
        in_specs=[IN_VMEM],
        out_specs=IN_VMEM,
        scratch_shapes=[pltpu.VMEM((tokens // run, part, D), jnp.bfloat16), dma, dma],
        compiler_params=pltpu.CompilerParams(
            collective_id=6, has_side_effects=True, vmem_limit_bytes=40 << 20
        ),
        cost_estimate=attention_cost(tokens, 320, 2),
    )(qkv).reshape(tokens, D)


def attend_halves_back(qkv, grad_out, run, part):
    tokens = qkv.shape[0]
    dma = pltpu.SemaphoreType.DMA((HEADS // 2,))
    return pl.pallas_call(
        partial(attend_halves_back_kernel, part),
        out_shape=jax.ShapeDtypeStruct(qkv.shape, jnp.bfloat16),
        in_specs=[IN_VMEM] * 2,
        out_specs=IN_VMEM,
        scratch_shapes=[pltpu.VMEM((tokens // run, part, D), jnp.bfloat16), dma, dma],
        compiler_params=pltpu.CompilerParams(
            collective_id=7, has_side_effects=True, vmem_limit_bytes=50 << 20
        ),
        cost_estimate=attention_cost(tokens, 320, 5),
    )(qkv, grad_out.reshape(tokens // run, run, D))


def attend_frames(qkv, windows):
    tokens = qkv.shape[0]
    dma = pltpu.SemaphoreType.DMA((HEADS // 2, 2))
    return pl.pallas_call(
        partial(attend_frames_kernel, windows),
        out_shape=(
            jax.ShapeDtypeStruct((tokens, D), jnp.bfloat16),
            jax.ShapeDtypeStruct((tokens, 2 * D), jnp.bfloat16),
        ),
        in_specs=[IN_VMEM],
        out_specs=(IN_VMEM,) * 2,
        scratch_shapes=[dma, dma],
        compiler_params=pltpu.CompilerParams(
            collective_id=4, has_side_effects=True, vmem_limit_bytes=40 << 20
        ),
        cost_estimate=attention_cost(tokens, 256, 2),
    )(qkv)


def attend_frames_back(qkv, far_kv, grad_out, windows):
    tokens = qkv.shape[0]
    dma = pltpu.SemaphoreType.DMA((HEADS // 2, 2))
    return pl.pallas_call(
        partial(attend_frames_back_kernel, windows),
        out_shape=jax.ShapeDtypeStruct(qkv.shape, jnp.bfloat16),
        in_specs=[IN_VMEM] * 3,
        out_specs=IN_VMEM,
        scratch_shapes=[pltpu.VMEM((tokens, 2 * D), jnp.float32)] * 3 + [dma, dma],
        compiler_params=pltpu.CompilerParams(
            collective_id=5, has_side_effects=True, vmem_limit_bytes=50 << 20
        ),
        cost_estimate=attention_cost(tokens, 256, 5),
    )(qkv, far_kv, grad_out)


def head_cols(array, first):
    return array, pl.BlockSpec((array.shape[0], 2 * HEAD_DIM), lambda h: (0, first + h))


def attention_operands(queries, key_values):
    ins = [head_cols(queries, 0)]
    ins += [head_cols(array, first) for array, first, _ in key_values]
    return ins + [head_cols(array, second) for array, _, second in key_values]


def attention_cost(tokens, keys, products):
    flops = 2 * products * tokens * keys * D * 2
    return pl.CostEstimate(
        flops=flops, bytes_accessed=tokens * D * 2 * 8, transcendentals=tokens * keys * HEADS
    )


def attend(queries, key_values, windows, text_len=0):
    tokens = queries.shape[0]
    ins = attention_operands(queries, key_values)
    return pl.pallas_call(
        partial(attend_kernel, windows, text_len, len(key_values)),
        grid=(HEADS // 2,),
        in_specs=[spec for _, spec in ins],
        out_specs=pl.BlockSpec((tokens, 2 * HEAD_DIM), lambda h: (0, h)),
        out_shape=jax.ShapeDtypeStruct((tokens, D), jnp.bfloat16),
        compiler_params=pltpu.CompilerParams(vmem_limit_bytes=40 << 20),
        cost_estimate=attention_cost(tokens, 320, 2),
    )(*[array for array, _ in ins])


def attend_back(queries, key_values, grad_out, windows, text_len=0):
    tokens = queries.shape[0]
    ins = attention_operands(queries, key_values) + [head_cols(grad_out, 0)]
    sets = len(key_values)
    whole = lambda rows, cols: pl.BlockSpec((rows, cols), lambda h: (0, 0))
    if sets == 1 and not text_len:
        outs = [((tokens, 3 * D), jnp.bfloat16)]
    else:
        rows = key_values[0][0].shape[0]
        outs = [((tokens, D), jnp.bfloat16)] + [((rows, 2 * D), jnp.float32)] * sets
    return pl.pallas_call(
        partial(attend_back_kernel, windows, text_len, sets),
        grid=(HEADS // 2,),
        in_specs=[spec for _, spec in ins],
        out_specs=[whole(*shape) for shape, _ in outs],
        out_shape=[jax.ShapeDtypeStruct(*out) for out in outs],
        compiler_params=pltpu.CompilerParams(vmem_limit_bytes=50 << 20),
        cost_estimate=attention_cost(tokens, 320, 5),
    )(*[array for array, _ in ins])


def mlp_forward(stream, modul, up_weight, down_weight):
    mlp_val, norm_back = jax.vjp(norm_modulated, stream, modul[3], modul[4])
    mlp_in = mlp_val.astype(jnp.bfloat16)
    up_proj = matmul(mlp_in, up_weight)
    share = 0.5 + 0.5 * lax.erf(up_proj * math.sqrt(0.5))
    gelu_val = up_proj * share
    slope = share + up_proj * (jnp.exp(-0.5 * up_proj * up_proj) / math.sqrt(2.0 * math.pi))
    gelu_low = gelu_val.astype(jnp.bfloat16)
    down_proj = matmul(gelu_low, down_weight)
    return (stream + modul[5] * down_proj, (norm_back, mlp_in, slope, gelu_low, down_proj))


def mlp_backward(grad_stream, modul, up_weight, down_weight, saved):
    norm_back, mlp_in, slope, gelu_low, down_proj = saved
    grad_down = (modul[5] * grad_stream).astype(jnp.bfloat16)
    grad_gate = jnp.sum(grad_stream * down_proj, 0)
    grad_up = (slope * matmul_nt(grad_down, down_weight)).astype(jnp.bfloat16)
    grad_part, grad_shift, grad_scale = norm_back(matmul_nt(grad_up, up_weight))
    factors = ((gelu_low, grad_down), (mlp_in, grad_up))
    return (grad_stream + grad_part, factors, (grad_shift, grad_scale, grad_gate))


def adam_update(weight, first_mom, second_mom, grad_val, learn_rate):
    first_mom = BETA_ONE * first_mom + (1.0 - BETA_ONE) * grad_val
    second_mom = BETA_TWO * second_mom + (1.0 - BETA_TWO) * grad_val * grad_val
    first_hat = first_mom / (1.0 - BETA_ONE**STEP)
    second_hat = second_mom / (1.0 - BETA_TWO**STEP)
    weight = weight - learn_rate * (first_hat / (jnp.sqrt(second_hat) + ADAM_EPS) + DECAY * weight)
    return (weight, first_mom, second_mom)

MESH = pl.DeviceIdType.MESH
ANY = pl.BlockSpec(memory_space=pl.ANY)
IN_VMEM = pl.BlockSpec(memory_space=pltpu.VMEM)
TEXT_PAD = 80


def ring_place(clip, count):
    half = clip // 2
    odd = clip % 2
    return half + odd * (count - 1 - 2 * half)


def ring_clip(place, count):
    far = place // (count // 2)
    return (1 - far) * 2 * place + far * (2 * (count - 1 - place) + 1)


def greet(peers):
    barrier = pltpu.get_barrier_semaphore()
    for peer in peers:
        pl.semaphore_signal(barrier, inc=1, device_id=peer, device_id_type=MESH)
    pl.semaphore_wait(barrier, len(peers))


def exchange_kernel(count, facts_ref, facts_out, send, recv):
    me = lax.axis_index("clip")
    band = lax.axis_index("band")
    peers = [((me + step) % count, band) for step in range(1, count)]
    greet(peers)
    sent = [
        pltpu.make_async_remote_copy(
            facts_ref, facts_out.at[me], send.at[step], recv.at[step], peer, MESH
        )
        for step, peer in enumerate(peers)
    ]
    for copy in sent:
        copy.start()
    facts_out[me] = facts_ref[...]
    for copy in sent:
        copy.wait()


def exchange_facts(facts):
    count = lax.axis_size("clip")
    return pl.pallas_call(
        partial(exchange_kernel, count),
        out_shape=jax.ShapeDtypeStruct((count,) + facts.shape, facts.dtype),
        in_specs=[IN_VMEM],
        out_specs=IN_VMEM,
        scratch_shapes=[pltpu.SemaphoreType.DMA((count - 1,))] * 2,
        compiler_params=pltpu.CompilerParams(collective_id=0, has_side_effects=True),
    )(facts)


def gather_kernel(count, picks, sides, *refs):
    num = len(picks)
    packs, vec_ref, text_ref = refs[:2], refs[2], refs[3]
    full, (vec_out, text_out, kv_out) = refs[4 : 4 + num], refs[4 + num : 7 + num]
    refs = refs[7 + num :]
    wide, shards = refs[:num], refs[num : 2 * num]
    ring_send, ring_recv, pair_send, pair_recv, cross_send, cross_recv = refs[2 * num : 2 * num + 6]
    load_sem, own_sem, part_send, part_recv, part_own = refs[2 * num + 6 : 2 * num + 11]
    kv_wide, kv_part, kv_put, kv_got, kv_sum, kv_load, kv_send, kv_recv, band_send, band_recv = refs[
        2 * num + 11 : 2 * num + 21
    ]
    share_send, share_recv = refs[2 * num + 21 :]
    shapes = [(packs[pack].shape[0], cols) for pack, _, cols in picks]
    loads = [
        pltpu.make_async_copy(
            packs[pack].at[:, pl.ds(start, cols)], wide[group], load_sem.at[group]
        )
        for group, (pack, start, cols) in enumerate(picks)
    ]
    kv_width = kv_wide.shape[1]
    kv_first = D + lax.axis_index("band") * kv_width
    kv_weight = pltpu.make_async_copy(
        packs[1].at[:, pl.ds(pl.multiple_of(kv_first, 128), kv_width)], kv_wide, kv_load
    )
    for copy in loads + [kv_weight]:
        copy.start()
    me = lax.axis_index("clip")
    band = lax.axis_index("band")
    core = band % 2
    place = ring_place(me, count)
    onward = 1 - 2 * core
    following = (ring_clip((place + onward + count) % count, count), band)
    plane = band // 2
    partner = (me, band + 1 - 2 * core)
    mirror = (me, band + 2 - 4 * plane)
    peers = [((me + step) % count, band) for step in range(1, count)]
    band_count = 2 * D // kv_width
    band_peers = [(me, (band + step) % band_count) for step in range(1, band_count)]
    greet(peers + band_peers)

    def block(ref, group, owner):
        rows, cols = shapes[group]
        return ref.at[
            pl.ds(pl.multiple_of(owner * rows, rows), rows),
            pl.ds(pl.multiple_of(core * (cols // 2), 128), cols // 2),
        ]

    def ring_copy(group, step):
        owner = ring_clip((place - onward * step + 2 * count) % count, count)
        there = block(full[group], group, owner)
        return pltpu.make_async_remote_copy(
            there, there, ring_send.at[step, group], ring_recv.at[step, group], following, MESH
        )

    def handed(group, step, send, recv, peer):
        owner = ring_clip((place - onward * (step + 1) + 2 * count) % count, count)
        there = block(full[group], group, owner)
        return pltpu.make_async_remote_copy(
            there, there, send.at[step, group], recv.at[step, group], peer, MESH
        )

    def pair_copy(group, step):
        return handed(group, step, pair_send, pair_recv, partner)

    def cross_copy(group, step):
        return handed(group, step, cross_send, cross_recv, mirror)

    def in_ring(group):
        def decorate(body):
            if sides[group]:
                pl.when(plane == sides[group] - 1)(body)
            else:
                body()

        return decorate

    def off_ring(group, also=None):
        def decorate(body):
            if sides[group]:
                off = plane != sides[group] - 1
                pl.when(off if also is None else jnp.logical_and(off, also))(body)

        return decorate

    def ring_arrival(group, step, onto):
        ring_copy(group, step).wait_recv()
        if onto:
            ring_copy(group, step + 1).start()
        pair_copy(group, step).start()
        if sides[group]:
            cross_copy(group, step).start()

    def cross_arrival(group, step):
        cross_copy(group, step).wait_recv()
        pair_copy(group, step).start()

    def own_copy(group):
        rows, cols = shapes[group]
        return pltpu.make_async_copy(
            shards[group],
            full[group].at[pl.ds(pl.multiple_of(me * rows, rows), rows), :],
            own_sem.at[group],
        )

    parts = []
    for step, peer in enumerate(peers):
        for which, (src, dst) in enumerate(((vec_ref, vec_out), (text_ref, text_out))):
            parts.append(
                pltpu.make_async_remote_copy(
                    src.at[peer[0], band],
                    dst.at[me, band],
                    part_send.at[which, step],
                    part_recv.at[which, step],
                    peer,
                    MESH,
                )
            )
    parts_own = [
        pltpu.make_async_copy(src.at[me, band], dst.at[me, band], part_own.at[which])
        for which, (src, dst) in enumerate(((vec_ref, vec_out), (text_ref, text_out)))
    ]
    for copy in parts_own + parts:
        copy.start()
    for group in range(num):
        rows, cols = shapes[group]
        loads[group].wait()
        shards[group][...] = wide[group][...].astype(jnp.bfloat16)
        own_copy(group).start()

        @in_ring(group)
        def _(group=group, rows=rows, cols=cols):
            pltpu.make_async_remote_copy(
                shards[group].at[:, pl.ds(pl.multiple_of(core * (cols // 2), 128), cols // 2)],
                block(full[group], group, me),
                ring_send.at[0, group],
                ring_recv.at[0, group],
                following,
                MESH,
            ).start()

    def kv_copy(hop):
        return pltpu.make_async_remote_copy(
            kv_put.at[hop], kv_got.at[hop], kv_send.at[hop], kv_recv.at[hop], following, MESH
        )

    def kv_hop(hop):
        owner = ring_clip((place - onward * (hop + 1) + 2 * count) % count, count)
        total = kv_part[owner]
        if not isinstance(hop, int) or hop > 0:
            kv_copy(hop - 1).wait_recv()
            total = total + kv_got[hop - 1]
        kv_put[hop] = total
        kv_copy(hop).start()

    def band_copies():
        return [
            pltpu.make_async_remote_copy(
                kv_sum, kv_out.at[band], band_send.at[step], band_recv.at[step], peer, MESH
            )
            for step, peer in enumerate(band_peers)
        ]

    shares = [
        pltpu.make_async_remote_copy(
            out.at[:, band],
            out.at[:, band],
            share_send.at[which, step],
            share_recv.at[which, step],
            peer,
            MESH,
        )
        for step, peer in enumerate(band_peers)
        for which, out in enumerate((vec_out, text_out))
    ]

    def share():
        for copy in parts_own + parts:
            copy.wait()
        for copy in shares:
            copy.start()

    def multiply():
        for copy in shares:
            copy.wait()
        kv_weight.wait()
        weight = kv_wide[...].astype(jnp.bfloat16)
        depth = weight.shape[0] // band_count
        for owner in range(count):
            kv_part[owner] = sum(
                matmul(text_out[owner, part], weight[part * depth : (part + 1) * depth])
                for part in range(band_count)
            )
        kv_hop(0)

    @pl.loop(1, count - 1)
    def _(step):
        for group in range(num):

            @in_ring(group)
            def _(group=group):
                ring_arrival(group, step - 1, True)

        pl.when(step == 1)(share)
        pl.when(step == 2)(multiply)

        @pl.when(step >= 3)
        def _():
            kv_hop(step - 2)
        for group in range(num):

            @off_ring(group, step >= 2)
            def _(group=group):
                cross_arrival(group, step - 2)

    for group in range(num):

        @in_ring(group)
        def _(group=group):
            ring_arrival(group, count - 2, False)

    kv_hop(count - 3)
    for late in (count - 3, count - 2):
        for group in range(num):

            @off_ring(group)
            def _(group=group, late=late):
                cross_arrival(group, late)

        if late == count - 3:
            kv_hop(count - 2)
    kv_copy(count - 2).wait_recv()
    kv_sum[...] = (kv_part[me] + kv_got[count - 2]).astype(jnp.bfloat16)
    kv_out[band] = kv_sum[...]
    for copy in band_copies():
        copy.start()
    for group in range(num):
        own_copy(group).wait()

    @pl.loop(0, count - 1)
    def _(step):
        for group in range(num):

            @in_ring(group)
            def _(group=group):
                ring_copy(group, step).wait_send()
                if sides[group]:
                    cross_copy(group, step).wait_send()

            pair_copy(group, step).wait()
        kv_copy(step).wait_send()

    for copy in band_copies():
        copy.wait()


def own_quarter(shard):
    rows = shard.shape[0] // lax.axis_size("band")
    own = lax.dynamic_slice_in_dim(shard, lax.axis_index("band") * rows, rows, 0)
    return own.astype(jnp.bfloat16)


def sum_rows(left, right):
    part = lax.psum_scatter(
        matmul_tn(left, right), ("clip", "band"), scatter_dimension=0, tiled=True
    )
    return lax.all_gather(part, "band", axis=0, tiled=True)


def gather_weights(packs, picks, sides, vectors, texts):
    count, band_count = lax.axis_size("clip"), lax.axis_size("band")
    num = len(picks)
    dma = pltpu.SemaphoreType.DMA
    shapes = [(packs[pack].shape[0], cols) for pack, _, cols in picks]
    kv_shape = (texts.shape[2], 2 * D // band_count)
    kv_all = pltpu.VMEM((count,) + kv_shape, jnp.float32)
    kv_hops = pltpu.VMEM((count - 1,) + kv_shape, jnp.float32)
    out = pl.pallas_call(
        partial(gather_kernel, count, picks, sides),
        out_shape=tuple(
            jax.ShapeDtypeStruct((count * rows, cols), jnp.bfloat16) for rows, cols in shapes
        )
        + tuple(jax.ShapeDtypeStruct(v.shape, v.dtype) for v in (vectors, texts))
        + (jax.ShapeDtypeStruct((band_count,) + kv_shape, jnp.bfloat16),),
        in_specs=[ANY] * 4,
        out_specs=(ANY,) * num + (IN_VMEM,) * 3,
        scratch_shapes=[pltpu.VMEM(shape, jnp.float32) for shape in shapes]
        + [pltpu.VMEM(shape, jnp.bfloat16) for shape in shapes]
        + [dma((count - 1, num))] * 6
        + [dma((num,)), dma((num,)), dma((2, count - 1)), dma((2, count - 1)), dma((2,))]
        + [
            pltpu.VMEM((packs[1].shape[0], kv_shape[1]), jnp.float32),
            kv_all,
            kv_hops,
            kv_hops,
            pltpu.VMEM(kv_shape, jnp.bfloat16),
            dma,
            dma((count - 1,)),
            dma((count - 1,)),
            dma((band_count - 1,)),
            dma((band_count - 1,)),
            dma((2, band_count - 1)),
            dma((2, band_count - 1)),
        ],
        compiler_params=pltpu.CompilerParams(
            collective_id=1, has_side_effects=True, vmem_limit_bytes=50 << 20
        ),
        cost_estimate=pl.CostEstimate(flops=2 * 10**11, bytes_accessed=6 * 10**8, transcendentals=0),
    )(*packs, vectors, texts)
    return out[:num], out[num], out[num + 1], out[num + 2]


WIRE_MAX = 32767.0
WIRE_LEAST = 1e-30
UNIT = (128, 512)


SPLIT = 2


def unit_parts(at, kind, first):
    if at == 0:
        return ((0, 4, lambda u: u, lambda u: 0), (4, SPLIT, lambda u: 4, lambda u: u - 3))
    if kind == 0:
        return ((0, 4, lambda u: u, lambda u: 0), (4, 4, lambda u: 4, lambda u: u - 3))
    if first:
        return ((2, 2, lambda u: u, lambda u: u), (4, 2, lambda u: 3, lambda u: u))
    return ((0, 3, lambda u: u, lambda u: u), (3, 3, lambda u: 3, lambda u: u))


def reduce_kernel(count, tokens, phases, *refs):
    num = sum(len(phase["lefts"]) for phase in phases)
    lefts, rights = refs[:num], refs[num : 2 * num]
    vec_ref, kv_ref, text_ref = refs[2 * num : 2 * num + 3]
    refs = refs[2 * num + 3 :]
    wide_out, deep_out, square_out, all_vec, kv_square = refs[:5]
    left_far, right_far = refs[5 : 5 + num], refs[5 + num : 5 + 2 * num]
    scratch = refs[5 + 2 * num :]
    left_buf, right_buf, got_low, got_scale, put_low, put_scale, plane_put = (
        scratch[2 * i : 2 * i + 2] for i in range(7)
    )
    plane_got = scratch[14 : 14 + len(phases)]
    (
        square_buf,
        left_sem,
        right_sem,
        pair_send,
        pair_recv,
        half_send,
        half_recv,
        ring_send,
        ring_recv,
        credit,
        plane_send,
        plane_recv,
        out_sem,
        out_send,
        out_recv,
        last_put,
        last_put_scale,
        last_got,
        last_got_scale,
        late_put,
        late_put_scale,
        late_got,
        late_got_scale,
        push_send,
        push_recv,
        cross_put,
        cross_put_scale,
        cross_got,
        cross_got_scale,
        cross_send,
        cross_recv,
        cross_credit,
        vec_got,
        kv_got,
        vec_sum,
        all_kv,
        all_kv_scale,
        text_buf,
        kv_grad,
        side_own,
        side_send,
        side_recv,
        vec_send,
        vec_recv,
        vec_pair_send,
        vec_pair_recv,
        kv_own,
        kv_send,
        kv_recv,
    ) = scratch[14 + len(phases) :]
    me = lax.axis_index("clip")
    band = lax.axis_index("band")
    core = band % 2
    plane = band // 2
    place = ring_place(me, count)
    onward = 1 - 2 * core
    following = (ring_clip((place + onward + count) % count, count), band)
    preceding = (ring_clip((place - onward + count) % count, count), band)
    partner = (me, band + 1 - 2 * core)
    mirror = (me, band + 2 - 4 * plane)
    band_count = vec_got.shape[0]
    band_peers = [(me, (band + step) % band_count) for step in range(1, band_count)]
    greet([following, preceding] + band_peers)

    def owner_at(step, way):
        return ring_clip((place - way * (step + 1) + 2 * count) % count, count)

    def left_blocks(at):
        phase = phases[at]
        if phase["kind"] == 0:
            return [(b, phase["lefts"][0], b, 4) for b in range(4)] + [(4, phase["lefts"][1], 0, 1)]
        first = phase["first"]
        return [(first + i, left, 0, 1) for i, left in enumerate(phase["lefts"])]

    def right_blocks(at):
        phase = phases[at]
        if phase["kind"] == 0:
            return [(0, phase["lefts"][0], 0)] + [(1 + i, phase["lefts"][1], i) for i in range(4)]
        first = phase["first"]
        return [(first + i, phase["lefts"][i], 0) for i in range(3 - first)] + [
            (3 + i, phase["lefts"][-1], i) for i in range(3)
        ]

    def left_cols(step, way, which, many):
        width = lefts_width // count if many == 1 else deep_width // count
        start = owner_at(step, way) * width + which * 128
        return pl.ds(pl.multiple_of(start, 128), 128)

    lefts_width = lefts[phases[1]["lefts"][0]].shape[1]
    deep_width = lefts[phases[0]["lefts"][0]].shape[1]

    def pair_left(at, step):
        out = []
        for block, operand, which, many in left_blocks(at):
            cols = left_cols(step, -onward, which, many)
            out.append(
                pltpu.make_async_remote_copy(
                    lefts[operand].at[:, cols],
                    left_far[operand].at[:, cols],
                    pair_send.at[at, block, step],
                    pair_recv.at[at, block, step],
                    partner,
                    MESH,
                )
            )
        return out

    def pair_right(at):
        out = []
        for i, operand in enumerate(phases[at]["lefts"]):
            half = rights[operand].shape[1] // 2
            out.append(
                pltpu.make_async_remote_copy(
                    rights[operand].at[:, pl.ds(pl.multiple_of((1 - core) * half, 128), half)],
                    right_far[operand],
                    half_send.at[operand],
                    half_recv.at[operand],
                    partner,
                    MESH,
                )
            )
        return out

    def load_left(at, step, slot, far):
        kind = phases[at]["kind"]
        out = []
        for block, operand, which, many in left_blocks(at):
            cols = left_cols(step, onward, which, many)
            source = left_far if far else lefts
            out.append(
                pltpu.make_async_copy(
                    source[operand].at[:, cols],
                    left_buf[kind].at[slot, block, pl.ds(far * tokens, tokens), :],
                    left_sem.at[kind, slot, block, far],
                )
            )
        return out

    def load_right(at, far):
        kind = phases[at]["kind"]
        out = []
        for block, operand, which in right_blocks(at):
            if far:
                source = right_far[operand].at[:, pl.ds(which * UNIT[1], UNIT[1])]
            else:
                half = rights[operand].shape[1] // 2
                start = pl.multiple_of(core * half + which * UNIT[1], 128)
                source = rights[operand].at[:, pl.ds(start, UNIT[1])]
            out.append(
                pltpu.make_async_copy(
                    source,
                    right_buf[kind].at[block, pl.ds(far * tokens, tokens), :],
                    right_sem.at[kind, block, far],
                )
            )
        return out

    def ring_copies(at, part, slot):
        kind = phases[at]["kind"]
        units = pl.ds(*unit_parts(at, kind, phases[at]["first"])[part][:2])
        return [
            pltpu.make_async_remote_copy(
                put.at[slot, units],
                got.at[slot, units],
                ring_send.at[kind, slot, part, i],
                ring_recv.at[kind, slot, part, i],
                following,
                MESH,
            )
            for i, (put, got) in enumerate(
                ((put_low[kind], got_low[kind]), (put_scale[kind], got_scale[kind]))
            )
        ]

    def plane_copies(at, part):
        kind = phases[at]["kind"]
        units = pl.ds(*unit_parts(at, kind, phases[at]["first"])[part][:2])
        pairs = ((plane_put[kind], plane_got[at]),)
        if at in coded:
            pairs = (coded[at][::2], coded[at][1::2])
        return [
            pltpu.make_async_remote_copy(
                here.at[units],
                there.at[units],
                plane_send.at[at, part, i],
                plane_recv.at[at, part, i],
                mirror,
                MESH,
            )
            for i, (here, there) in enumerate(pairs)
        ]

    coded = {
        len(phases) - 2: (late_put, late_put_scale, late_got, late_got_scale),
        len(phases) - 1: (last_put, last_put_scale, last_got, last_got_scale),
    }

    def split_unit(pair, of_plane):
        return 4 + 2 * pair + of_plane

    def split_copy(pair, of_plane):
        unit = split_unit(pair, of_plane)
        return pltpu.make_async_remote_copy(
            plane_put[0].at[unit],
            plane_got[0].at[unit],
            plane_send.at[0, 1, pair],
            plane_recv.at[0, 1, pair],
            mirror,
            MESH,
        )

    def cross_copies(slot):
        return [
            pltpu.make_async_remote_copy(
                here.at[slot], there.at[slot], cross_send.at[slot, i], cross_recv.at[slot, i], mirror, MESH
            )
            for i, (here, there) in enumerate(
                ((cross_put, cross_got), (cross_put_scale, cross_got_scale))
            )
        ]

    def push_right(block):
        operand, which = [entry[1:] for entry in right_blocks(0) if entry[0] == block][0]
        half = rights[operand].shape[1] // 2
        begin = pl.multiple_of((1 - core) * half + which * UNIT[1], 128)
        return pltpu.make_async_remote_copy(
            rights[operand].at[:, pl.ds(begin, UNIT[1])],
            right_buf[phases[0]["kind"]].at[block, pl.ds(tokens, tokens), :],
            push_send.at[block],
            push_recv.at[block],
            partner,
            MESH,
        )

    def out_copies(at, unit):
        phase = phases[at]
        if phase["kind"] == 0 and unit < 4:
            half = UNIT[1]
            rows = deep_out.shape[0] // 4
            there = deep_out.at[
                pl.ds(unit * rows, rows),
                pl.ds(pl.multiple_of(phase["cols"][0] + core * half, 128), half),
            ]
        else:
            which, col = (1, unit - 4) if phase["kind"] == 0 else (unit - phase["first"], 0)
            if phase["kind"] and unit >= 3:
                which, col = len(phase["lefts"]) - 1, unit - 3
            half = rights[phase["lefts"][which]].shape[1] // 2
            start = phase["cols"][which] + core * half + col * UNIT[1]
            there = wide_out.at[:, pl.ds(pl.multiple_of(start, 128), UNIT[1])]
        here = plane_got[at].at[unit]
        return (
            pltpu.make_async_copy(here, there, out_sem.at[at, unit]),
            pltpu.make_async_remote_copy(
                here, there, out_send.at[at, unit], out_recv.at[at, unit], partner, MESH
            ),
        )

    def product(kind, slot, left, right):
        return lax.dot_general(
            left_buf[kind][slot, left],
            right_buf[kind][right],
            (((0,), (0,)), ((), ())),
            preferred_element_type=jnp.float32,
        )

    def start(copies):
        for copy in copies:
            copy.start()

    def finish(copies):
        for copy in copies:
            copy.wait()

    def encode(term):
        largest = jnp.maximum(jnp.max(jnp.abs(term), axis=0, keepdims=True), WIRE_LEAST)
        low = jnp.round(term * (WIRE_MAX / largest)).astype(jnp.int16)
        return low, largest * (1.0 / WIRE_MAX)

    def take_step(at, step, first, last):
        phase = phases[at]
        kind = phase["kind"]
        slot = step % 2
        before = (step + 1) % 2
        for far in range(2):
            finish(load_left(at, step, slot, far))

        def load_next():
            for copy in pair_left(at, step + 1):
                copy.wait_recv()
            for far in range(2):
                start(load_left(at, step + 1, before, far))

        opening = first and at == 0
        if not (last or opening):
            load_next()
        parts = unit_parts(at, kind, phase["first"])

        def send_theirs():
            def spend():
                for copy in cross_copies(slot):
                    copy.wait_send()
                pl.semaphore_wait(cross_credit, 1)

            if last:
                spend()
            elif not first:
                pl.when(step >= 2)(spend)
            for pair in range(SPLIT):
                unit = split_unit(pair, 1 - plane)
                term = product(kind, slot, parts[1][2](unit), parts[1][3](unit))
                cross_put[slot, pair], cross_put_scale[slot, pair] = encode(term)
            start(cross_copies(slot))

        if at == 0 and not opening:
            send_theirs()
        for part, (low, many, left_of, right_of) in enumerate(parts):
            if opening:
                blocks = range(1) if part == 0 else range(1, 5)
                finish(load_right(0, 0)[blocks.start : blocks.stop])
                for block in blocks:
                    push_right(block).wait_recv()
                if part:
                    send_theirs()
            if not first:
                for copy in ring_copies(at, part, before):
                    copy.wait_recv()
            if not (first or last):

                @pl.when(step >= 2)
                def _(part=part):
                    for copy in ring_copies(at, part, slot):
                        copy.wait_send()
                    pl.semaphore_wait(credit.at[kind, part], 1)

            def settle(position, unit, term):
                if not first:
                    came = got_low[kind][before, position].astype(jnp.float32)
                    term = term + came * got_scale[kind][before, position]
                if last and at in coded:
                    coded[at][0][unit], coded[at][1][unit] = encode(term)
                elif last:
                    plane_put[kind][unit] = term
                else:
                    low_part, scale_part = encode(term)
                    put_low[kind][slot, position] = low_part
                    put_scale[kind][slot, position] = scale_part

            split = at == 0 and part == 1
            if split:
                for copy in cross_copies(slot):
                    copy.wait_recv()

            @pl.loop(low, low + many)
            def _(position, left_of=left_of, right_of=right_of):
                unit = split_unit(position - 4, plane) if split else position
                term = product(kind, slot, left_of(unit), right_of(unit))
                if split:
                    came = cross_got[slot, position - 4].astype(jnp.float32)
                    term = term + came * cross_got_scale[slot, position - 4]
                settle(position, unit, term)

            if split and not last:

                def credit_cross():
                    pl.semaphore_signal(
                        cross_credit, inc=1, device_id=mirror, device_id_type=MESH
                    )

                if first:
                    credit_cross()
                else:
                    pl.when(step < count - 2)(credit_cross)

            if last and split:
                start([split_copy(pair, plane) for pair in range(SPLIT)])
            elif last:
                start(plane_copies(at, part))
            else:
                start(ring_copies(at, part, slot))
            if not (first or last):

                @pl.when(step < count - 2)
                def _(part=part):
                    pl.semaphore_signal(
                        credit.at[kind, part], inc=1, device_id=preceding, device_id_type=MESH
                    )

        if opening:
            load_next()

    def close(at):
        kind = phases[at]["kind"]

        def add_square(total):
            square_buf[...] += jnp.sum((total * total).reshape(UNIT[0] // 8, 8, UNIT[1]), axis=0)

        for part, (low, many, _, _) in enumerate(unit_parts(at, kind, phases[at]["first"])):
            if at == 0 and part == 1:
                for pair in range(SPLIT):
                    split_copy(pair, plane).wait_send()
                    split_copy(pair, 1 - plane).wait_recv()
                    ours = split_unit(pair, plane)
                    plane_got[0][ours] = plane_put[0][ours]
                for unit in range(4, 8):
                    add_square(plane_got[0][unit])
                    start(out_copies(0, unit))
                continue
            finish(plane_copies(at, part))

            @pl.loop(low, low + many)
            def _(unit):
                if at in coded:
                    here, here_scale, there, there_scale = coded[at]
                    total = here[unit].astype(jnp.float32) * here_scale[unit]
                    total += there[unit].astype(jnp.float32) * there_scale[unit]
                else:
                    total = plane_put[kind][unit] + plane_got[at][unit]
                plane_got[at][unit] = total
                add_square(total)

            for unit in range(low, low + many):
                start(out_copies(at, unit))

    half_rows = pl.ds(pl.multiple_of(core * (vec_sum.shape[0] // 2), 8), vec_sum.shape[0] // 2)
    side_local = [
        pltpu.make_async_copy(vec_ref, vec_got.at[band], side_own.at[0]),
        pltpu.make_async_copy(kv_ref.at[band], kv_got.at[band], side_own.at[1]),
        pltpu.make_async_copy(text_ref, text_buf, side_own.at[2]),
    ]
    side_remote = []
    for step, peer in enumerate(band_peers):
        side_remote += [
            pltpu.make_async_remote_copy(
                vec_ref, vec_got.at[band], side_send.at[0, step], side_recv.at[0, step], peer, MESH
            ),
            pltpu.make_async_remote_copy(
                kv_ref.at[peer[1]],
                kv_got.at[band],
                side_send.at[1, step],
                side_recv.at[1, step],
                peer,
                MESH,
            ),
        ]
    vec_own = pltpu.make_async_copy(vec_sum, all_vec.at[me], side_own.at[3])

    def kv_parts(owner):
        return [(ref.at[owner], ref.at[owner]) for ref in (all_kv, all_kv_scale)]

    def vec_copies(step):
        owner = ring_clip((place - onward * step + 2 * count) % count, count)
        vec = all_vec.at[owner, half_rows]
        return [
            pltpu.make_async_remote_copy(
                here, there, vec_send.at[step, i], vec_recv.at[step, i], following, MESH
            )
            for i, (here, there) in enumerate([(vec, vec)] + kv_parts(owner))
        ]

    def vec_first():
        vec = all_vec.at[me, half_rows]
        return [
            pltpu.make_async_remote_copy(
                here, there, vec_send.at[0, i], vec_recv.at[0, i], following, MESH
            )
            for i, (here, there) in enumerate([(vec_sum.at[half_rows], vec)] + kv_parts(me))
        ]

    def vec_pair(step):
        owner = ring_clip((place - onward * (step + 1) + 2 * count) % count, count)
        vec = all_vec.at[owner, half_rows]
        return pltpu.make_async_remote_copy(
            vec, vec, vec_pair_send.at[step], vec_pair_recv.at[step], partner, MESH
        )

    kv_width = kv_grad.shape[1]

    def kv_place(owner):
        return deep_out.at[:, pl.ds(pl.multiple_of(D + owner * kv_width, 128), kv_width)]

    def kv_copy(i):
        if i == 2:
            return pltpu.make_async_copy(kv_grad, kv_place(band), kv_own)
        peer = (partner, mirror)[i]
        return pltpu.make_async_remote_copy(
            kv_grad, kv_place(band), kv_send.at[i], kv_recv.at[i], peer, MESH
        )

    def kv_passed():
        there = kv_place(mirror[1])
        return pltpu.make_async_remote_copy(
            there, there, kv_send.at[2], kv_recv.at[2], partner, MESH
        )

    def sum_bands():
        finish(side_local + side_remote)
        vec_sum[...] = jnp.sum(vec_got[...], 0)
        all_kv[me], all_kv_scale[me] = encode(jnp.sum(kv_got[...], 0))
        vec_own.start()
        start(vec_first())

    def pass_sums(step):
        for copy in vec_copies(step - 1):
            copy.wait_recv()
        start(vec_copies(step))
        vec_pair(step - 1).start()

    def multiply_text():
        for copy in vec_copies(count - 2):
            copy.wait_recv()
        vec_pair(count - 2).start()
        grads = all_kv[...].astype(jnp.float32) * all_kv_scale[...]
        grads = grads.reshape(text_buf.shape[0], -1)
        total = jnp.zeros_like(kv_grad)
        for _ in range(3):
            part = grads.astype(jnp.bfloat16)
            grads = grads - part.astype(jnp.float32)
            total = total + matmul_tn(text_buf[...], part)
        kv_grad[...] = total
        kv_square[...] = jnp.sum((total * total).reshape(-1, 8, total.shape[1]), axis=0)
        start([kv_copy(i) for i in range(3)])

    square_buf[...] = jnp.zeros_like(square_buf)
    start(side_local + side_remote)
    start(load_right(0, 0))
    start(load_left(0, 0, 0, 0))
    push_right(0).start()
    start(pair_left(0, 0))
    for block in range(1, 5):
        push_right(block).start()

    @pl.loop(1, count)
    def _(step):
        start(pair_left(0, step))

    for copy in pair_left(0, 0):
        copy.wait_recv()
    start(load_left(0, 0, 0, 1))
    take_step(0, 0, True, False)
    for at in range(len(phases)):
        more = at + 1 < len(phases)
        if more:
            start(pair_right(at + 1))
            start(load_right(at + 1, 0))
            start(pair_left(at + 1, 0))
        if at == 1:
            sum_bands()

        @pl.loop(1, count - 1)
        def _(step, at=at, more=more):
            take_step(at, step, False, False)
            if at == 1:
                pass_sums(step)
            if more:
                start(pair_left(at + 1, step))

                @pl.when(step == count // 2)
                def _():
                    for copy in pair_right(at + 1):
                        copy.wait_recv()
                    start(load_right(at + 1, 1))
                    for copy in pair_left(at + 1, 0):
                        copy.wait_recv()
                    for far in range(2):
                        start(load_left(at + 1, 0, 0, far))

        if more:
            start(pair_left(at + 1, count - 1))
            for far in range(2):
                finish(load_right(at + 1, far))
            take_step(at + 1, 0, True, False)
        take_step(at, count - 1, False, True)
        if at == 1:
            multiply_text()
        for slot in range(2):
            for part in range(2):
                for copy in ring_copies(at, part, slot):
                    copy.wait_send()
            if at == 0:
                for copy in cross_copies(slot):
                    copy.wait_send()
        if at == 2:
            kv_copy(1).wait_recv()
            kv_passed().start()
        if at:
            close(at - 1)
    close(len(phases) - 1)
    vec_own.wait()
    kv_passed().wait()
    kv_copy(0).wait()
    kv_copy(1).wait_send()
    kv_copy(2).wait()

    @pl.loop(0, count - 1)
    def _(step):
        for copy in vec_copies(step):
            copy.wait_send()
        vec_pair(step).wait()

    square_out[...] = square_buf[...]
    for at, phase in enumerate(phases):
        for copy in pair_right(at) if at else [push_right(block) for block in range(5)]:
            copy.wait_send()

        @pl.loop(0, count)
        def _(step, at=at):
            for copy in pair_left(at, step):
                copy.wait_send()

        for unit in range(phase["first"], 8 if phase["kind"] == 0 else 6):
            finish(out_copies(at, unit))


def reduce_gradients(phases, lefts, rights, vectors, keyvals, text, wide_cols, deep_cols):
    count = lax.axis_size("clip")
    tokens = lefts[0].shape[0]
    wide_rows = lefts[1].shape[1] // count
    deep_rows = lefts[0].shape[1] // count
    band_count, _, kv_cols = keyvals.shape
    num = len(lefts)
    dma = pltpu.SemaphoreType.DMA
    units, lefts_of, rights_of = (8, 6), (5, 4), (5, 6)
    scratch = [pltpu.VMEM((2, lefts_of[k], 2 * tokens, 128), jnp.bfloat16) for k in range(2)]
    scratch += [pltpu.VMEM((rights_of[k], 2 * tokens, UNIT[1]), jnp.bfloat16) for k in range(2)]
    for _ in range(2):
        scratch += [pltpu.VMEM((2, units[k]) + UNIT, jnp.int16) for k in range(2)]
        scratch += [pltpu.VMEM((2, units[k], 1, UNIT[1]), jnp.float32) for k in range(2)]
    scratch += [pltpu.VMEM((units[k],) + UNIT, jnp.float32) for k in range(2)]
    scratch += [pltpu.VMEM((units[p["kind"]],) + UNIT, jnp.float32) for p in phases]
    scratch += [
        pltpu.VMEM((8, UNIT[1]), jnp.float32),
        dma((2, 2, 5, 2)),
        dma((2, 6, 2)),
        dma((len(phases), 5, count)),
        dma((len(phases), 5, count)),
        dma((num,)),
        dma((num,)),
        dma((2, 2, 2, 2)),
        dma((2, 2, 2, 2)),
        pltpu.SemaphoreType.REGULAR((2, 2)),
        dma((len(phases), 2, 2)),
        dma((len(phases), 2, 2)),
        dma((len(phases), 8)),
        dma((len(phases), 8)),
        dma((len(phases), 8)),
    ]
    for many in (6, 6, 8, 8):
        scratch += [pltpu.VMEM((many,) + UNIT, jnp.int16)]
        scratch += [pltpu.VMEM((many, 1, UNIT[1]), jnp.float32)]
    scratch += [
        dma((5,)),
        dma((5,)),
        *[
            pltpu.VMEM((2, SPLIT) + tile, kind)
            for _ in range(2)
            for tile, kind in ((UNIT, jnp.int16), ((1, UNIT[1]), jnp.float32))
        ],
        dma((2, 2)),
        dma((2, 2)),
        pltpu.SemaphoreType.REGULAR,
        pltpu.VMEM((band_count,) + vectors.shape, jnp.float32),
        pltpu.VMEM(keyvals.shape, jnp.float32),
        pltpu.VMEM(vectors.shape, jnp.float32),
        pltpu.VMEM((count,) + keyvals.shape[1:], jnp.int16),
        pltpu.VMEM((count, 1, kv_cols), jnp.float32),
        pltpu.VMEM(text.shape, jnp.bfloat16),
        pltpu.VMEM((text.shape[1], kv_cols), jnp.float32),
        dma((4,)),
        dma((2, band_count - 1)),
        dma((2, band_count - 1)),
        dma((count - 1, 3)),
        dma((count - 1, 3)),
        dma((count - 1,)),
        dma((count - 1,)),
        dma,
        dma((3,)),
        dma((3,)),
    ]
    out = pl.pallas_call(
        partial(reduce_kernel, count, tokens, phases),
        out_shape=(
            jax.ShapeDtypeStruct((wide_rows, wide_cols), jnp.float32),
            jax.ShapeDtypeStruct((deep_rows, deep_cols), jnp.float32),
            jax.ShapeDtypeStruct((8, UNIT[1]), jnp.float32),
            jax.ShapeDtypeStruct((count,) + vectors.shape, jnp.float32),
            jax.ShapeDtypeStruct((8, kv_cols), jnp.float32),
        )
        + tuple(jax.ShapeDtypeStruct(x.shape, x.dtype) for x in lefts)
        + tuple(jax.ShapeDtypeStruct((tokens, x.shape[1] // 2), x.dtype) for x in rights),
        in_specs=[ANY] * (2 * num + 3),
        out_specs=(ANY, ANY, IN_VMEM, ANY, IN_VMEM) + (ANY,) * (2 * num),
        scratch_shapes=scratch,
        compiler_params=pltpu.CompilerParams(
            collective_id=2, has_side_effects=True, vmem_limit_bytes=58 << 20
        ),
        cost_estimate=pl.CostEstimate(flops=3 * 10**11, bytes_accessed=8 * 10**8, transcendentals=0),
    )(*lefts, *rights, vectors, keyvals, text)
    return out[:5]


def total_kernel(count, part_ref, out_ref, mid, band_got, clip_got, *sems):
    me = lax.axis_index("clip")
    band = lax.axis_index("band")
    band_count = band_got.shape[0]
    band_peers = [(me, (band + step) % band_count) for step in range(1, band_count)]
    clip_peers = [((me + step) % count, band) for step in range(1, count)]
    greet(band_peers + clip_peers)
    stages = (
        (part_ref, band_got, band, band_peers, mid, sems[:2]),
        (mid, clip_got, me, clip_peers, out_ref, sems[2:]),
    )
    for value, got, index, peers, result, (send, recv) in stages:
        copies = [
            pltpu.make_async_remote_copy(
                value, got.at[index], send.at[step], recv.at[step], peer, MESH
            )
            for step, peer in enumerate(peers)
        ]
        for copy in copies:
            copy.start()
        got[index] = value[...]
        for copy in copies:
            copy.wait()
        result[...] = jnp.sum(got[...], 0)


def total_over_devices(value):
    count, band_count = lax.axis_size("clip"), lax.axis_size("band")
    dma = pltpu.SemaphoreType.DMA
    tile = (8, 128)
    return pl.pallas_call(
        partial(total_kernel, count),
        out_shape=jax.ShapeDtypeStruct(tile, jnp.float32),
        in_specs=[IN_VMEM],
        out_specs=IN_VMEM,
        scratch_shapes=[
            pltpu.VMEM(tile, jnp.float32),
            pltpu.VMEM((band_count,) + tile, jnp.float32),
            pltpu.VMEM((count,) + tile, jnp.float32),
            dma((band_count - 1,)),
            dma((band_count - 1,)),
            dma((count - 1,)),
            dma((count - 1,)),
        ],
        compiler_params=pltpu.CompilerParams(collective_id=3, has_side_effects=True),
    )(jnp.broadcast_to(value, tile))[0, 0]


def per_device(
    latents,
    noise_field,
    timesteps,
    null_flags,
    frame_mask,
    context,
    w_wide,
    m_wide,
    v_wide,
    w_deep,
    m_deep,
    v_deep,
    w_small,
    m_small,
    v_small,
):
    clip_count = lax.axis_size("clip")
    band_count = lax.axis_size("band")
    clip_at = lax.axis_index("clip")
    band_at = lax.axis_index("band")
    wide_rows = w_wide.shape[0]
    deep_rows = w_deep.shape[0]
    text_len, text_dim = context.shape[1:]
    facts = jnp.pad(
        jnp.concatenate([timesteps, frame_mask[0]])[None],
        ((0, 7), (0, 127 - frame_mask.shape[1])),
    )
    kept_text = context[0] * (1 - null_flags[0]).astype(jnp.bfloat16)
    text_cols = jnp.pad(
        kept_text.reshape(text_len, clip_count, band_count, -1).transpose(1, 2, 0, 3),
        ((0, 0), (0, 0), (0, TEXT_PAD - text_len), (0, 0)),
    )
    all_facts = exchange_facts(facts)
    all_times = all_facts[:, 0, 0].astype(jnp.float32)
    all_time_low = jax.nn.silu(time_features(all_times)).astype(jnp.bfloat16)
    time_rows = lax.dynamic_slice(
        all_time_low, (0, clip_at * wide_rows), (clip_count, wide_rows)
    )
    part_modul = matmul(time_rows, w_wide[:, : 12 * D].astype(jnp.bfloat16))
    kv_cols = 2 * D // band_count
    gathered, all_modul, all_text, keyval = gather_weights(
        (w_wide, w_deep),
        (
            (0, 22 * D, FF),
            (0, 12 * D, 3 * D),
            (0, 15 * D, 3 * D),
            (0, 18 * D, D),
            (0, 19 * D, D),
            (1, 0, D),
            (0, 22 * D + FF, FF),
        ),
        (1, 2, 2, 1, 1, 0, 0),
        part_modul.reshape(clip_count, band_count, -1, 128),
        text_cols,
    )
    up_a_w, qkv_a_w, qkv_b_w, out_a_w, out_b_w, down_a_w, up_b_w = gathered
    all_text = all_text.transpose(0, 2, 1, 3)
    keyval = keyval.transpose(1, 0, 2).reshape(TEXT_PAD, 2 * D)
    late_cross, late_down_b, all_modul = lax.optimization_barrier(
        (own_quarter(w_wide[:, 20 * D : 22 * D]), own_quarter(w_deep[:, 3 * D :]), all_modul)
    )
    cross_w = lax.all_gather(late_cross, ("clip", "band"), axis=0, tiled=True)
    query_w, cross_out_w = (cross_w[:, :D], cross_w[:, D:])
    down_b_w = lax.all_gather(late_down_b, ("clip", "band"), axis=0, tiled=True)
    small_low = w_small.astype(jnp.bfloat16)
    small_val = small_low.astype(jnp.float32)
    num_frames, num_rows, num_cols = (latents.shape[1], latents.shape[2], latents.shape[3])
    tok_count = num_frames * num_rows * num_cols
    all_mask = all_facts[:, 0, 1 : 1 + num_frames]
    global_count = jnp.sum(all_mask).astype(jnp.float32) * (num_rows * num_cols * CH * band_count)
    time_value = timesteps[0].astype(jnp.float32)
    noise_angle = 0.5 * math.pi * time_value / TMAX
    signal, spread = (jnp.cos(noise_angle), jnp.sin(noise_angle))
    clean_tok = token_order(latents[0])
    noise_tok = token_order(noise_field[0])
    run = num_rows * WIN
    part = SHIFT * WIN
    frame_windows = attend_pieces(tok_count, num_frames, "frame")
    text_windows = attend_pieces(tok_count, num_frames, "text")
    noisy_low = (signal * clean_tok + spread * noise_tok).astype(jnp.bfloat16)
    target = signal * noise_tok - spread * clean_tok
    modulation = jnp.sum(all_modul, 0).reshape(12, D)
    mod_a, mod_b = (modulation[:6], modulation[6:])
    stream_zero = matmul(noisy_low, small_low[:CH]) + small_val[2 * CH]
    normed_a, back_a = jax.vjp(norm_modulated, stream_zero, mod_a[0], mod_a[1])
    in_a = normed_a.astype(jnp.bfloat16)
    qkv_a = matmul(in_a, qkv_a_w).astype(jnp.bfloat16)
    att_a, far_kv = attend_frames(qkv_a, frame_windows)
    proj_a = matmul(att_a, out_a_w)
    stream_one = stream_zero + mod_a[2] * proj_a
    stream_two, saved_a = mlp_forward(stream_one, mod_a, up_a_w, down_a_w)
    normed_b, back_b = jax.vjp(norm_modulated, stream_two, mod_b[0], mod_b[1])
    low_b = normed_b.astype(jnp.bfloat16)
    rolled = with_rows(low_b, shifted(first_rows(low_b, run, part), "band", -1), run)
    qkv_b = matmul(rolled, qkv_b_w).astype(jnp.bfloat16)
    att_b = attend_halves(qkv_b, run, part)
    proj_b = matmul(att_b, out_b_w)
    stream_three = stream_two + mod_b[2] * proj_b
    cross_val, cross_back = jax.vjp(norm_gained, stream_three, small_val[2 * CH + 1])
    cross_in = cross_val.astype(jnp.bfloat16)
    query_proj = matmul(cross_in, query_w).astype(jnp.bfloat16)
    text_kv = [(keyval, 0, HEADS // 2)]
    crossed = attend(query_proj, text_kv, text_windows, text_len)
    stream_four = stream_three + matmul(crossed, cross_out_w)
    stream_five, saved_b = mlp_forward(stream_four, mod_b, up_b_w, down_b_w)
    final_val, final_back = jax.vjp(norm_gained, stream_five, small_val[2 * CH + 2])
    final_low = final_val.astype(jnp.bfloat16)
    head_low = small_low[CH : 2 * CH]
    predicted = matmul_nt(final_low, head_low)
    weight_row = jnp.repeat(frame_mask[0].astype(jnp.float32), run)
    weight_row = jnp.tile(weight_row, num_cols // WIN)[:, None]
    pred_error = predicted - target
    loss_part = jnp.sum(weight_row * pred_error * pred_error)
    grad_pred = (weight_row * pred_error * (2.0 / global_count)).astype(jnp.bfloat16)
    grad_head = matmul_tn(grad_pred, final_low)
    grad_stream, grad_gain_f = final_back(matmul(grad_pred, head_low))
    grad_stream, mlp_factors_b, extra_b = mlp_backward(
        grad_stream, mod_b, up_b_w, down_b_w, saved_b
    )
    grad_cross = grad_stream.astype(jnp.bfloat16)
    grad_crossed = matmul_nt(grad_cross, cross_out_w).astype(jnp.bfloat16)
    grad_query, grad_keyval = attend_back(
        query_proj, text_kv, grad_crossed, text_windows, text_len
    )
    grad_part, grad_gain_c = cross_back(matmul_nt(grad_query, query_w))
    grad_stream = grad_stream + grad_part
    grad_proj = (mod_b[2] * grad_stream).astype(jnp.bfloat16)
    grad_gate_b = jnp.sum(grad_stream * proj_b, 0)
    factors_ob = (att_b, grad_proj)
    grad_att = matmul_nt(grad_proj, out_b_w).astype(jnp.bfloat16)
    grad_qkv = attend_halves_back(qkv_b, grad_att, run, part)
    factors_qkvb = (rolled, grad_qkv)
    grad_in_roll = matmul_nt(grad_qkv, qkv_b_w)
    sent_back = shifted(first_rows(grad_in_roll, run, part), "band", 1)
    grad_normed = with_rows(grad_in_roll, sent_back, run)
    grad_part, grad_shift_b, grad_scale_b = back_b(grad_normed)
    grad_stream = grad_stream + grad_part
    grad_stream, mlp_factors_a, extra_a = mlp_backward(
        grad_stream, mod_a, up_a_w, down_a_w, saved_a
    )
    grad_proj = (mod_a[2] * grad_stream).astype(jnp.bfloat16)
    grad_gate_a = jnp.sum(grad_stream * proj_a, 0)
    factors_oa = (att_a, grad_proj)
    grad_att = matmul_nt(grad_proj, out_a_w).astype(jnp.bfloat16)
    grad_qkv = attend_frames_back(qkv_a, far_kv, grad_att, frame_windows)
    factors_qkva = (in_a, grad_qkv)
    grad_part, grad_shift_a, grad_scale_a = back_a(matmul_nt(grad_qkv, qkv_a_w))
    grad_stream = grad_stream + grad_part
    grad_patch = matmul_tn(noisy_low.astype(jnp.float32), grad_stream, lax.Precision.HIGHEST)
    grad_bias = jnp.sum(grad_stream, 0)
    grad_modul = jnp.stack(
        [
            grad_shift_a,
            grad_scale_a,
            grad_gate_a,
            extra_a[0],
            extra_a[1],
            extra_a[2],
            grad_shift_b,
            grad_scale_b,
            grad_gate_b,
            extra_b[0],
            extra_b[1],
            extra_b[2],
        ]
    ).reshape(1, 12 * D)
    grad_small = jnp.concatenate(
        [grad_patch, grad_head, grad_bias[None], grad_gain_c[None], grad_gain_f[None]], 0
    )
    factors = mlp_factors_b + (
        (crossed, grad_cross),
        (cross_in, grad_query),
        factors_ob,
        factors_qkvb,
    )
    factors += mlp_factors_a + (factors_oa, factors_qkva)
    if wide_rows == 128 and deep_rows == 512:
        phases = (
            {"kind": 0, "first": 0, "lefts": (0, 1), "cols": (3 * D, 10 * D + FF)},
            {"kind": 1, "first": 0, "lefts": (2, 3, 4, 5), "cols": (9 * D, 8 * D, 7 * D, 3 * D)},
            {"kind": 0, "first": 0, "lefts": (6, 7), "cols": (0, 10 * D)},
            {"kind": 1, "first": 2, "lefts": (8, 9), "cols": (6 * D, 0)},
        )
        used = 12 * D + grad_small.size
        vectors = jnp.concatenate(
            [grad_modul.reshape(-1), grad_small.reshape(-1), loss_part[None]]
        )
        vectors = jnp.pad(vectors, (0, 256 * 128 - vectors.shape[0])).reshape(256, 128)
        keyvals = grad_keyval.reshape(TEXT_PAD, band_count, kv_cols).transpose(1, 0, 2)
        wide_rest, deep_sum, squares, all_vectors, kv_squares = reduce_gradients(
            phases,
            [f[0] for f in factors],
            [f[1] for f in factors],
            vectors,
            keyvals,
            all_text.reshape(clip_count * TEXT_PAD, deep_rows),
            10 * D + 2 * FF,
            4 * D,
        )
        all_vectors = all_vectors.reshape(clip_count, -1)
        all_grad_modul = all_vectors[:, : 12 * D]
        small_sum = jnp.sum(all_vectors[:, 12 * D : used], 0).reshape(grad_small.shape)
        loss_sum = jnp.sum(all_vectors[:, used])
        square_part = jnp.sum(squares) / (band_count // 2) + jnp.sum(kv_squares)
    else:
        summed = [sum_rows(*pair) for pair in factors]
        wide_rest = jnp.concatenate([summed[i] for i in (9, 5, 8, 4, 3, 2, 7, 1)], 1)
        grad_keyval = lax.psum_scatter(grad_keyval, "band", scatter_dimension=1, tiled=True)
        grad_keyval = lax.all_gather(grad_keyval, "clip", axis=0, tiled=True)
        grad_w_ckv = matmul_tn(
            all_text.reshape(clip_count * TEXT_PAD, deep_rows).astype(jnp.float32),
            grad_keyval,
            lax.Precision.HIGHEST,
        )
        grad_w_ckv = lax.all_gather(grad_w_ckv, "band", axis=1, tiled=True)
        all_grad_modul = lax.all_gather(lax.psum(grad_modul, "band"), "clip", axis=0, tiled=True)
        loss_sum, small_sum = lax.psum((loss_part, grad_small), ("clip", "band"))
        deep_sum = jnp.concatenate([summed[6], grad_w_ckv, summed[0]], 1)
        square_part = sum(jnp.sum(x * x) for x in (wide_rest, deep_sum)) / band_count
    grad_w_ada = matmul_tn(time_rows.astype(jnp.float32), all_grad_modul, lax.Precision.HIGHEST)
    wide_sum = jnp.concatenate([grad_w_ada, wide_rest], 1)
    square_part += jnp.sum(grad_w_ada * grad_w_ada) / band_count
    square_sum = total_over_devices(square_part)
    grad_norm = jnp.sqrt(square_sum + jnp.sum(small_sum * small_sum))
    factor = CLIP_MAX / jnp.maximum(grad_norm, CLIP_MAX)
    new_wide = adam_update(w_wide, m_wide, v_wide, wide_sum * factor, 0.15)
    new_deep = adam_update(w_deep, m_deep, v_deep, deep_sum * factor, 0.05)
    new_small = adam_update(w_small, m_small, v_small, small_sum * factor, 0.5)
    loss = loss_sum / global_count
    return (
        loss,
        grad_norm,
        new_wide[0],
        new_wide[1],
        new_wide[2],
        new_deep[0],
        new_deep[1],
        new_deep[2],
        new_small[0],
        new_small[1],
        new_small[2],
    )


def solution(mesh):
    in_specs = (
        P("clip", None, "band", None, None),
        P("clip", None, "band", None, None),
        P("clip"),
        P("clip"),
        P("clip", None),
        P("clip", None, None),
        P("clip", None),
        P("clip", None),
        P("clip", None),
        P("clip", None),
        P("clip", None),
        P("clip", None),
        P(),
        P(),
        P(),
    )
    out_specs = (
        P(),
        P(),
        P("clip", None),
        P("clip", None),
        P("clip", None),
        P("clip", None),
        P("clip", None),
        P("clip", None),
        P(),
        P(),
        P(),
    )
    return jax.shard_map(
        per_device, mesh=mesh, in_specs=in_specs, out_specs=out_specs, check_vma=False
    )
```
